32 devices in a mesh: dp: 4 (over y, x), seq: 8 (over z, core).
Axes of the slice: x: 2, y: 2, z: 4, core: 2. Of those that a mesh axis runs over, the one named last changes fastest.
Arguments:
- layer_input: bfloat16 [2, 4, 1024, 1024], P(None, 'dp', 'seq'), may hold values from -6 to 6
- first_gain: float32 [1024], replicated, may hold values from 0.5 to 1.5
- query_weight: bfloat16 [1024, 1024], replicated, may hold values from -0.75 to 0.75
- key_weight: bfloat16 [1024, 512], replicated, may hold values from -0.75 to 0.75
- value_weight: bfloat16 [1024, 512], replicated, may hold values from -0.1875 to 0.1875
- output_weight: bfloat16 [1024, 1024], replicated, may hold values from -2 to 2
- second_gain: float32 [1024], replicated, may hold values from 0.5 to 1.5
- gate_weight: bfloat16 [16, 1024, 512], P('seq'), may hold values from -0.1875 to 0.1875
- up_weight: bfloat16 [16, 1024, 512], P('seq'), may hold values from -0.1875 to 0.1875
- down_weight: bfloat16 [16, 512, 1024], P('seq'), may hold values from -3 to 3
- expert_ids: int32 [2, 4, 1024, 8], P(None, 'dp'), may hold values from 0 to 15, all different within a row; in each aligned block of 128 rows (0 to 127, 128 to 255, ..., all dimensions but the last counted through in order) at most 128 rows name the same one
- gate_values: bfloat16 [2, 4, 1024, 8], P(None, 'dp'), may hold values from 0.059814453 to 0.19921875
- positions: int32 [2, 4, 1024], P(None, 'dp', 'seq'), may hold values from 0 to 3069, as said below
- cotangent: bfloat16 [2, 4, 1024, 1024], P(None, 'dp', 'seq'), may hold values from -6 to 6
Outputs:
- layer_output: bfloat16 [2, 4, 1024, 1024], P(None, 'dp', 'seq')
- input_grad: float32 [2, 4, 1024, 1024], P(None, 'dp', 'seq')
- first_gain_grad: float32 [1024], replicated
- query_weight_grad: float32 [1024, 1024], replicated
- key_weight_grad: float32 [1024, 512], replicated
- value_weight_grad: float32 [1024, 512], replicated
- output_weight_grad: float32 [1024, 1024], replicated
- second_gain_grad: float32 [1024], replicated
- gate_weight_grad: float32 [16, 1024, 512], P('seq')
- up_weight_grad: float32 [16, 1024, 512], P('seq')
- down_weight_grad: float32 [16, 512, 1024], P('seq')
The draws below stay inside these ranges and needn't reach their ends.
Inputs may be any that keep to these rules, and one draw needn't show every extreme that they name: `expert_ids`: each row names 8 different experts. Within each aligned block of 128 rows (the tokens of one device), no expert is named by more than 128 rows, a bound that some block reaches. Within each sequence the positions start at 0 and rise by 1 to 3 from each token to the next; in every draw some sequence rises by 3 at every token.
All inputs are finite; a program needn't handle non-finite values.
Results may differ from the reference program's by a relative error of at most 0.02.
Values may be sent and summed in bfloat16 or wider, within the bound.
No kernel may reach another device: no remote copies, remote signals or barrier semaphores. Data moves between devices by JAX's collectives and lax.ppermute only.
A program may use at most 256 MiB of HBM per device.

```python
import math
import jax
import jax.numpy as jnp
import numpy as np
from jax import lax

D = 1024
HEADS = 16
KV_HEADS = 8
HEAD_DIM = 64
FF = 512
TOP = 8
EXPERTS = 16
BLOCK = 128
LENGTH = 1024
SEQS = 4
MICRO = 2
MOST = 128
N_SEQ = 8


def draw_positions(key, part):
    step_key = jax.random.fold_in(key, 11)
    pick_key = jax.random.fold_in(key, 12)
    increments = jax.random.randint(step_key, (MICRO, SEQS, LENGTH), 1, 4).astype(jnp.int32)
    chosen = jax.random.randint(pick_key, (), 0, MICRO * SEQS).astype(jnp.int32)
    sequence_number = jnp.arange(MICRO * SEQS, dtype=jnp.int32).reshape(MICRO, SEQS, 1)
    increments = jnp.where(sequence_number == chosen, 3, increments).astype(jnp.int32)
    return (jnp.cumsum(increments, axis=-1, dtype=jnp.int32) - increments).astype(jnp.int32)


def shard_levels(own_key, dims, cuts, smallest, largest):
    def one(axis_at, blocks):
        steps = jax.random.uniform(jax.random.fold_in(jax.random.fold_in(own_key, 6), axis_at), (blocks,), jnp.float32, smallest / len(cuts), largest / len(cuts))
        return jnp.repeat(jnp.exp(steps), dims[axis_at] // blocks).reshape((-1,) + (1,) * (len(dims) - axis_at - 1))

    factor_of = one(*cuts[0])
    for cut in cuts[1:]:
        factor_of = factor_of * one(*cut)
    return factor_of


def shared_out(stream_key, own, number, rows, count, top, limit, skew):
    ranking = jax.random.permutation(stream_key, count)
    heavy_load, common = load_shares(count, rows * top, limit, skew, True), load_shares(count, rows * top, limit, skew, False)
    places = jnp.arange(count)

    def named(sizes, offset_by):
        used = int((sizes > 0).sum())
        fixed = max(1, used // 4)
        passed = fixed + (places - fixed + offset_by * (used - fixed)) % max(1, count - fixed)
        return jnp.zeros((count,), jnp.int32).at[ranking[jnp.where(places < fixed, places, passed)]].set(jnp.asarray(sizes, jnp.int32))

    sizes = jnp.where(number % 4 == 0, named(heavy_load, number // 4), named(common, number - number // 4 - 1))
    mixed = jax.random.permutation(jax.random.fold_in(own, 3), count)
    donor, sink = mixed[0:count // 2 * 2:2], mixed[1:count // 2 * 2:2]
    margin = jnp.minimum(sizes[donor] - 1, limit - sizes[sink]) // 2
    margin = jnp.where((donor == ranking[0]) | (sink == ranking[0]) | (sizes[sink] == 0), 0, jnp.maximum(margin, 0))
    passed = jax.random.randint(jax.random.fold_in(own, 4), (count // 2,), 0, 1 << 20) % (margin + 1)
    sizes = sizes.at[donor].add(-passed).at[sink].add(passed)
    labels = jnp.searchsorted(jnp.cumsum(sizes), jnp.arange(rows * top), side="right").astype(jnp.int32)
    table = labels.reshape(top, rows).T
    table = table[jax.random.permutation(jax.random.fold_in(own, 1), rows)]
    offset_by = jax.random.randint(jax.random.fold_in(own, 2), (rows, 1), 0, top)
    return jnp.take_along_axis(table, (jnp.arange(top)[None, :] + offset_by) % top, axis=1)


def load_shares(amount, total, limit, lean, full):
    portions = [(1 << 20) // math.isqrt(standing ** lean) + 1 for standing in range(1, amount + 1)]
    largest = limit if full else min(limit, max(-(-total // amount), total * portions[0] // sum(portions)))
    least = 1 if total - largest >= amount - 1 else 0
    holding, spare = [largest] + [least] * (amount - 1), total - largest - least * (amount - 1)
    while spare > 0:
        free = [i for i in range(1, amount) if holding[i] < largest] or [i for i in range(1, amount) if holding[i] < limit]
        mass, budget = sum([portions[i] for i in free]), spare
        for i in free:
            addition = min(limit - holding[i], max(1, budget * portions[i] // mass), spare)
            holding[i] = holding[i] + addition
            spare = spare - addition
    return np.array(holding)


def noise(own_key, dims, width, limit, pieces=(), kind=jnp.bfloat16):
    values = width * jax.random.normal(own_key, dims, jnp.float32)
    if pieces:
        values = values * shard_levels(own_key, dims, pieces, -0.22, 0.18)
    return jnp.clip(values, -limit, limit).astype(kind)


def setup_inputs(seed: int = 0) -> dict:
    key_list = jax.random.split(jax.random.key(seed), 15)
    layer_input = noise(key_list[0], (MICRO, SEQS, LENGTH, D), 1.0, 6.0, ((1, 4), (2, 8)))
    first_gain = jnp.clip(1.0 + 0.1 * jax.random.normal(key_list[1], (D,), jnp.float32), 0.5, 1.5)
    query_weight = noise(key_list[2], (D, HEADS * HEAD_DIM), (max(D // 16, 1)) ** -0.5, 0.75)
    key_weight = noise(key_list[3], (D, KV_HEADS * HEAD_DIM), (max(D // 16, 1)) ** -0.5, 0.75)
    value_weight = noise(key_list[4], (D, KV_HEADS * HEAD_DIM), D ** -0.5, 0.1875)
    output_weight = noise(key_list[5], (HEADS * HEAD_DIM, D), (max(D // 128, 1)) ** -0.5, 2.0)
    second_gain = jnp.clip(1.0 + 0.1 * jax.random.normal(key_list[6], (D,), jnp.float32), 0.5, 1.5)
    gate_weight = noise(key_list[7], (EXPERTS, D, FF), D ** -0.5, 0.1875, ((0, 8),))
    up_weight = noise(key_list[8], (EXPERTS, D, FF), D ** -0.5, 0.1875, ((0, 8),))
    down_weight = noise(key_list[9], (EXPERTS, FF, D), (max(FF // 128, 1)) ** -0.5, 3.0, ((0, 8),))
    expert_ids_keys = jax.random.split(jax.random.fold_in(key_list[10], 1), MICRO * SEQS * LENGTH // BLOCK)
    expert_ids_turns = jax.random.permutation(jax.random.fold_in(key_list[10], 3), MICRO * SEQS * LENGTH // BLOCK)
    expert_ids = jax.vmap(lambda own, number: shared_out(jax.random.fold_in(key_list[10], 2), own, number, BLOCK, EXPERTS, TOP, MOST, 2))(expert_ids_keys, expert_ids_turns).reshape((MICRO, SEQS, LENGTH, TOP))
    gate_values = jnp.clip(jnp.exp(math.log(0.19921875) - 1.2031561 * jax.random.uniform(key_list[11], (MICRO, SEQS, LENGTH, TOP), jnp.float32) ** shard_levels(key_list[11], (MICRO, SEQS, LENGTH, TOP), ((1, 4),), -0.2, 0.2)), 0.059814453, 0.19921875).astype(jnp.bfloat16)
    positions = draw_positions(jax.random.fold_in(key_list[14], 71), 0)
    cotangent = noise(key_list[13], (MICRO, SEQS, LENGTH, D), 1.0, 6.0, ((1, 4), (2, 8)))
    return {"layer_input": layer_input, "first_gain": first_gain, "query_weight": query_weight, "key_weight": key_weight, "value_weight": value_weight, "output_weight": output_weight, "second_gain": second_gain, "gate_weight": gate_weight, "up_weight": up_weight, "down_weight": down_weight, "expert_ids": expert_ids, "gate_values": gate_values, "positions": positions, "cotangent": cotangent}


@jax.custom_vjp
def low(v):
    return lax.optimization_barrier(v.astype(jnp.bfloat16)).astype(jnp.float32)

@jax.custom_vjp
def low_back(v):
    return v

def low_keep(v):
    return (low(v), None)

def low_pass(kept, grad):
    return (grad,)

def back_keep(v):
    return (v, None)

def back_low(kept, grad):
    return (low(grad),)
low.defvjp(low_keep, low_pass)
low_back.defvjp(back_keep, back_low)
highest = lax.Precision.HIGHEST
rope_theta = 10000.0
attention_scale = 0.015625
residual_scale = 0.22
norm_eps = 1e-06
masked_score = -1e+30

def rms_scale(values, norm_gain):
    return values * lax.rsqrt(lax.optimization_barrier(jnp.mean(values * values, axis=-1, keepdims=True)) + norm_eps) * norm_gain

def rotate(values, positions):
    half_dim = values.shape[-1] // 2
    exponent = jnp.arange(half_dim, dtype=jnp.float32) * (-2.0 / values.shape[-1])
    angles = positions.astype(jnp.float32)[:, None] * (rope_theta ** exponent)[None, :]
    cosine = jnp.cos(angles)[:, None, :]
    sine_part = jnp.sin(angles)[:, None, :]
    first_half = values[..., :half_dim]
    second_half = values[..., half_dim:]
    return jnp.concatenate([first_half * cosine - second_half * sine_part, second_half * cosine + first_half * sine_part], axis=-1)

def slot_table(route_ids, route_gates, chosen, block_count, capacity):
    rows_all = route_ids.shape[0]
    per_block = rows_all // block_count
    matches = route_ids[:, None, :] == chosen[None, :, None]
    member = lax.optimization_barrier(jnp.sum(matches.astype(jnp.int32), axis=-1, dtype=jnp.int32))
    weight_of = lax.optimization_barrier(jnp.sum(jnp.where(matches, route_gates[:, None, :], 0.0), axis=-1))
    member = member.reshape(block_count, per_block, -1)
    rank_in = jnp.cumsum(member, axis=1, dtype=jnp.int32) - member
    slot_of = jnp.where(member > 0, rank_in, capacity)
    one_hot = slot_of[..., None] == jnp.arange(capacity, dtype=jnp.int32)
    row_number = jnp.arange(rows_all, dtype=jnp.int32).reshape(block_count, per_block)
    picked = lax.optimization_barrier(jnp.sum(jnp.where(one_hot, row_number[:, :, None, None], 0), axis=1, dtype=jnp.int32))
    filled = jnp.any(one_hot, axis=1)
    slot_rows = jnp.where(filled, picked, rows_all).astype(jnp.int32)
    slot_gates = lax.optimization_barrier(jnp.sum(jnp.where(one_hot, weight_of.reshape(block_count, per_block, -1)[..., None], 0.0), axis=1))
    return (slot_rows, slot_gates)

def attention(queries, key_rows, value_rows):
    group_size = HEADS // KV_HEADS
    query_span = min(512, LENGTH)
    blocks = queries.reshape(LENGTH // query_span, query_span, KV_HEADS, group_size, HEAD_DIM)
    key_index = jnp.arange(LENGTH, dtype=jnp.int32)

    def one_block(block_in):
        query_block, block_number = block_in
        scores = jnp.einsum('qkgd,skd->kgqs', query_block, key_rows, precision=highest) * attention_scale
        scores = low_back(scores)
        query_index = block_number * query_span + jnp.arange(query_span, dtype=jnp.int32)
        allowed = key_index[None, :] <= query_index[:, None]
        scores = jnp.where(allowed, scores, masked_score)
        row_max = lax.optimization_barrier(jnp.max(scores, axis=-1, keepdims=True))
        weights = jnp.exp(scores - row_max)
        probability = low(weights / lax.optimization_barrier(jnp.sum(weights, axis=-1, keepdims=True)))
        return jnp.einsum('kgqs,skd->qkgd', probability, value_rows, precision=highest)
    numbers = jnp.arange(LENGTH // query_span, dtype=jnp.int32)
    mixed_out = lax.map(jax.checkpoint(one_block), (blocks, numbers))
    return mixed_out.reshape(LENGTH, HEADS * HEAD_DIM)

def expert_apply(normed, slot_rows, slot_gates, gate_weight, up_weight, down_weight):
    flat_rows = jnp.transpose(slot_rows, (1, 0, 2)).reshape(EXPERTS, -1)
    flat_gates = jnp.transpose(slot_gates, (1, 0, 2)).reshape(EXPERTS, -1)
    taken = jnp.take(normed, flat_rows, axis=0, mode='fill', fill_value=0.0)
    gate_pre = low_back(jnp.einsum('ecd,edf->ecf', taken, gate_weight, precision=highest))
    up_pre = low_back(jnp.einsum('ecd,edf->ecf', taken, up_weight, precision=highest))
    hidden = low(jax.nn.silu(gate_pre) * up_pre)
    produced = low_back(jnp.einsum('ecf,efd->ecd', hidden, down_weight, precision=highest))
    weighted = flat_gates[:, :, None] * produced
    return jnp.zeros_like(normed).at[flat_rows.reshape(-1)].add(weighted.reshape(-1, normed.shape[-1]), mode='drop')

def forward(layer_in, first_gain, query_weight, key_weight, value_weight, output_weight, second_gain, gate_weight, up_weight, down_weight, slot_rows, slot_gates, positions):
    normed_first = low(rms_scale(layer_in, first_gain))
    query_raw = low_back(jnp.dot(normed_first, query_weight, precision=highest)).reshape(LENGTH, HEADS, HEAD_DIM)
    queries = low(rotate(query_raw, positions))
    key_raw = low_back(jnp.dot(normed_first, key_weight, precision=highest)).reshape(LENGTH, KV_HEADS, HEAD_DIM)
    key_rows = low(rotate(key_raw, positions))
    value_rows = low(low_back(jnp.dot(normed_first, value_weight, precision=highest))).reshape(LENGTH, KV_HEADS, HEAD_DIM)
    mixed = low(low_back(attention(queries, key_rows, value_rows)))
    projected = low_back(jnp.dot(mixed, output_weight, precision=highest))
    middle = layer_in + residual_scale * projected
    normed_second = low(rms_scale(middle, second_gain))
    return middle + residual_scale * expert_apply(normed_second, slot_rows, slot_gates, gate_weight, up_weight, down_weight)

def reference(layer_input, first_gain, query_weight, key_weight, value_weight, output_weight, second_gain, gate_weight, up_weight, down_weight, expert_ids, gate_values, positions, cotangent):
    params = (first_gain.astype(jnp.float32), query_weight.astype(jnp.float32), key_weight.astype(jnp.float32), value_weight.astype(jnp.float32), output_weight.astype(jnp.float32), second_gain.astype(jnp.float32), gate_weight.astype(jnp.float32), up_weight.astype(jnp.float32), down_weight.astype(jnp.float32))
    seq_count = MICRO * SEQS
    inputs_flat = layer_input.reshape(seq_count, LENGTH, D)
    cot_flat = cotangent.reshape(seq_count, LENGTH, D)
    ids_flat = expert_ids.reshape(seq_count, LENGTH, TOP)
    gates_flat = gate_values.reshape(seq_count, LENGTH, TOP)
    pos_flat = positions.reshape(seq_count, LENGTH)
    every_expert = jnp.arange(EXPERTS, dtype=jnp.int32)

    def one_sequence(sums, item):
        seq_in, seq_cot, seq_ids, seq_gates, seq_pos = item
        slot_rows, slot_gates = slot_table(seq_ids, seq_gates.astype(jnp.float32), every_expert, N_SEQ, MOST)

        def apply_layer(layer_in, *weights):
            return forward(layer_in, *weights, slot_rows, slot_gates, seq_pos)
        result, pullback = jax.vjp(apply_layer, seq_in.astype(jnp.float32), *params)
        grads = pullback(seq_cot.astype(jnp.float32))
        sums = tuple((running + increment for running, increment in zip(sums, grads[1:])))
        return (sums, (result.astype(jnp.bfloat16), grads[0]))
    start_sums = tuple((jnp.zeros_like(weight) for weight in params))
    sums, (outputs, input_grads) = lax.scan(one_sequence, start_sums, (inputs_flat, cot_flat, ids_flat, gates_flat, pos_flat))
    return (outputs.reshape(MICRO, SEQS, LENGTH, D), input_grads.reshape(MICRO, SEQS, LENGTH, D), sums[0], sums[1], sums[2], sums[3], sums[4], sums[5], sums[6], sums[7], sums[8])
```

```python
from functools import partial

import jax
import jax.numpy as jnp
from jax import lax
from jax.experimental import pallas as pl
from jax.experimental.pallas import tpu as pltpu
from jax.sharding import PartitionSpec as P

HEAD_DIM = 64

rope_theta = 10000.0
attention_scale = 0.015625
residual_scale = 0.22
norm_eps = 1e-06
masked_score = -1e30

f32 = jnp.float32
bf16 = jnp.bfloat16
NT = (((1,), (1,)), ((), ()))
TN = (((0,), (0,)), ((), ()))


def dot(a, b):
    return jnp.dot(a, b, preferred_element_type=f32)


def dot_nt(a, b):
    return lax.dot_general(a, b, NT, preferred_element_type=f32)


def params(mib, *semantics):
    return pltpu.CompilerParams(
        vmem_limit_bytes=mib * 1024 * 1024, dimension_semantics=semantics or None
    )


def cost(flops, nbytes, trans=0):
    return pl.CostEstimate(
        flops=int(flops), bytes_accessed=int(nbytes), transcendentals=int(trans)
    )


def whole(shape):
    return pl.BlockSpec(shape, lambda *_: (0,) * len(shape))


def rope_tables(positions, width):
    half = HEAD_DIM // 2
    exponent = jnp.arange(half, dtype=f32) * (-2.0 / HEAD_DIM)
    angles = positions.astype(f32)[:, None] * (rope_theta**exponent)[None, :]
    cosine, sine = jnp.cos(angles), jnp.sin(angles)
    copies = width // HEAD_DIM
    cos_row = jnp.concatenate([cosine, cosine] * copies, axis=1)
    sin_row = jnp.concatenate([-sine, sine] * copies, axis=1)
    return cos_row, sin_row


def partner(values):
    width = values.shape[1]
    half = HEAD_DIM // 2
    lane = lax.broadcasted_iota(jnp.int32, values.shape, 1)
    ahead = pltpu.roll(values, width - half, 1)
    behind = pltpu.roll(values, half, 1)
    return jnp.where(lane % HEAD_DIM < half, ahead, behind)


def pre_kernel(x_ref, gain_ref, cos_ref, sin_ref, wq_ref, wk_ref, wv_ref, send_ref, low_ref, kv_ref):
    group = pl.program_id(0)
    pair = 2 * HEAD_DIM

    @pl.when(group == 0)
    def _():
        x = x_ref[...].astype(f32)
        scale = lax.rsqrt(jnp.mean(x * x, axis=-1, keepdims=True) + norm_eps)
        low = (x * scale * gain_ref[...]).astype(bf16)
        low_ref[...] = low
        keys = dot(low, wk_ref[...])
        vals = dot(low, wv_ref[...])
        for at in range(keys.shape[1] // pair):
            k = keys[:, at * pair : (at + 1) * pair]
            v = vals[:, at * pair : (at + 1) * pair]
            k = k * cos_ref[...] + partner(k) * sin_ref[...]
            lane = lax.broadcasted_iota(jnp.int32, k.shape, 1)
            first = lane < HEAD_DIM
            kv_ref[2 * at] = jnp.where(first, k, pltpu.roll(v, HEAD_DIM, 1)).astype(bf16)
            kv_ref[2 * at + 1] = jnp.where(first, pltpu.roll(k, HEAD_DIM, 1), v).astype(bf16)

    q = dot(low_ref[...], wq_ref[...])
    q = (q * cos_ref[...] + partner(q) * sin_ref[...]) * attention_scale
    send_ref[0, :, :pair] = q.astype(bf16)
    send_ref[0, :, pair:] = kv_ref[group]


def pre_call(x, gain, cos_row, sin_row, wq, wk, wv):
    rows, features = x.shape
    groups = wk.shape[1] // HEAD_DIM
    pair = wq.shape[1] // groups
    return pl.pallas_call(
        pre_kernel,
        grid=(groups,),
        in_specs=[
            whole((rows, features)),
            whole((1, features)),
            whole((rows, pair)),
            whole((rows, pair)),
            pl.BlockSpec((features, pair), lambda g: (0, g)),
            whole(wk.shape),
            whole(wv.shape),
        ],
        out_specs=[
            pl.BlockSpec((1, rows, 2 * pair), lambda g: (g, 0, 0)),
            whole((rows, features)),
        ],
        out_shape=[
            jax.ShapeDtypeStruct((groups, rows, 2 * pair), bf16),
            jax.ShapeDtypeStruct((rows, features), bf16),
        ],
        scratch_shapes=[pltpu.VMEM((groups, rows, pair), bf16)],
        compiler_params=params(40, "arbitrary"),
        cost_estimate=cost(4 * rows * features * features, 6e6),
        name="norm_qkv_rope",
    )(x, gain, cos_row, sin_row, wq, wk, wv)


def split_heads(block, first):
    wide = block.astype(f32)
    lane = lax.broadcasted_iota(jnp.int32, wide.shape, 1)
    turned = pltpu.roll(wide, HEAD_DIM, 1)
    if first:
        parts = [jnp.where(lane < HEAD_DIM, wide, 0.0), jnp.where(lane < HEAD_DIM, turned, 0.0)]
    else:
        parts = [jnp.where(lane >= HEAD_DIM, turned, 0.0), jnp.where(lane >= HEAD_DIM, wide, 0.0)]
    return jnp.concatenate(parts, axis=0).astype(bf16)


def join_heads(turned):
    rows = turned.shape[1] // 2
    return jnp.transpose(jnp.concatenate([turned[:, :rows], turned[:, rows:]], axis=0))


def scores_of(kv, q2, rows):
    scores = dot_nt(kv, q2)
    count = scores.shape[0]
    own = scores[count - rows :]
    key_at = lax.broadcasted_iota(jnp.int32, own.shape, 0)
    query_at = lax.broadcasted_iota(jnp.int32, own.shape, 1) % rows
    own = jnp.where(key_at <= query_at, own, masked_score)
    if count == rows:
        return own
    return jnp.concatenate([scores[: count - rows], own], axis=0)


def attend_kernel(qkv_ref, out_ref):
    blocks, _, rows, width = qkv_ref.shape
    pair = width // 2
    kv = qkv_ref[:, 0, :, pair:].reshape(blocks * rows, pair)
    kv_t = jnp.transpose(kv)
    for at in range(blocks):
        count = (at + 1) * rows
        q2 = split_heads(qkv_ref[at, 0, :, :pair], True)
        scores = scores_of(kv[:count], q2, rows)
        top = jnp.max(scores, axis=0, keepdims=True)
        weights = jnp.exp(scores - top)
        total = jnp.sum(weights, axis=0, keepdims=True)
        out_t = dot(kv_t[:, :count], weights.astype(bf16))
        out_ref[at, 0] = join_heads(out_t[HEAD_DIM:] / total).astype(bf16)


def attend_call(qkv):
    blocks, micro, rows, width = qkv.shape
    pair = width // 2
    length = blocks * rows
    return pl.pallas_call(
        attend_kernel,
        grid=(micro,),
        in_specs=[pl.BlockSpec((blocks, 1, rows, width), lambda m: (0, m, 0, 0))],
        out_specs=pl.BlockSpec((blocks, 1, rows, pair), lambda m: (0, m, 0, 0)),
        out_shape=jax.ShapeDtypeStruct((blocks, micro, rows, pair), bf16),
        compiler_params=params(48, "arbitrary"),
        cost_estimate=cost(
            micro * length * length * 512, 3 * qkv.size, micro * length * length
        ),
        name="attention_forward",
    )(qkv)


def attend_back_kernel(qkv_ref, grad_ref, cos_ref, sin_ref, out_ref, dkv_ref):
    blocks, _, rows, width = qkv_ref.shape
    pair = width // 2
    kv = qkv_ref[:, 0, :, pair:].reshape(blocks * rows, pair)
    kv_t = jnp.transpose(kv)
    dkv_ref[...] = jnp.zeros_like(dkv_ref)
    for at in range(blocks):
        count = (at + 1) * rows
        q2 = split_heads(qkv_ref[at, 0, :, :pair], True)
        g2 = split_heads(grad_ref[at, 0], False)
        scores = scores_of(kv[:count], q2, rows)
        top = jnp.max(scores, axis=0, keepdims=True)
        weights = jnp.exp(scores - top)
        total = jnp.sum(weights, axis=0, keepdims=True)
        prob = weights * (1.0 / total)
        prob_grad = dot_nt(kv[:count], g2)
        delta = jnp.sum(prob * prob_grad, axis=0, keepdims=True)
        score_grad = (prob * (prob_grad - delta)).astype(bf16)
        dkv_ref[:count] += dot(score_grad, q2) + dot(prob.astype(bf16), g2)
        dq_t = dot(kv_t[:, :count], score_grad)
        dq = join_heads(dq_t[:HEAD_DIM] * attention_scale)
        dq = dq * cos_ref[at, 0] - partner(dq) * sin_ref[at, 0]
        out_ref[at, 0, :, :pair] = dq.astype(bf16)
    for at in range(blocks):
        dkv = dkv_ref[at * rows : (at + 1) * rows]
        lane = lax.broadcasted_iota(jnp.int32, dkv.shape, 1)
        turned = dkv * cos_ref[at, 0] - partner(dkv) * sin_ref[at, 0]
        out_ref[at, 0, :, pair:] = jnp.where(lane < HEAD_DIM, turned, dkv).astype(bf16)


def attend_back_call(qkv, grads, cos_all, sin_all):
    blocks, micro, rows, width = qkv.shape
    pair = width // 2
    length = blocks * rows
    spec = lambda lanes: pl.BlockSpec((blocks, 1, rows, lanes), lambda m: (0, m, 0, 0))
    return pl.pallas_call(
        attend_back_kernel,
        grid=(micro,),
        in_specs=[spec(width), spec(pair), spec(pair), spec(pair)],
        out_specs=spec(width),
        out_shape=jax.ShapeDtypeStruct(qkv.shape, bf16),
        scratch_shapes=[pltpu.VMEM((length, pair), f32)],
        compiler_params=params(56, "arbitrary"),
        cost_estimate=cost(
            micro * length * length * 1280, 10 * qkv.size, micro * length * length
        ),
        name="attention_backward",
    )(qkv, grads, cos_all, sin_all)


def post_kernel(mix_ref, wo_ref, x_ref, gain_ref, mixed_ref, middle_ref, low_ref):
    mixed = jnp.concatenate([mix_ref[g] for g in range(mix_ref.shape[0])], axis=1)
    mixed_ref[...] = mixed
    middle = x_ref[...].astype(f32) + residual_scale * dot(mixed, wo_ref[...])
    middle_ref[...] = middle
    scale = lax.rsqrt(jnp.mean(middle * middle, axis=-1, keepdims=True) + norm_eps)
    low_ref[...] = (middle * scale * gain_ref[...]).astype(bf16)


def post_call(mix, wo, x, gain):
    rows, features = x.shape
    return pl.pallas_call(
        post_kernel,
        out_shape=[
            jax.ShapeDtypeStruct((rows, wo.shape[0]), bf16),
            jax.ShapeDtypeStruct((rows, features), f32),
            jax.ShapeDtypeStruct((rows, features), bf16),
        ],
        compiler_params=params(32),
        cost_estimate=cost(2 * rows * wo.size, 5e6),
        name="project_norm",
    )(mix, wo, x, gain)


def expert_kernel(x_ref, cot_ref, w_ref, wg_ref, wu_ref, wd_ref, dx_ref, h_ref, dg_ref, du_ref):
    x = x_ref[0]
    cot = residual_scale * cot_ref[0].astype(f32)
    weight = w_ref[...]
    total = None
    for e in range(wg_ref.shape[0]):
        gate = dot(x, wg_ref[e])
        up = dot(x, wu_ref[e])
        slot_grad = (weight[:, e : e + 1] * cot).astype(bf16)
        hidden_grad = dot_nt(slot_grad, wd_ref[e])
        sig = 1.0 / (1.0 + jnp.exp(-gate))
        silu = gate * sig
        h_ref[e] = (silu * up).astype(bf16)
        gate_grad = (hidden_grad * up * (sig * (1.0 + gate * (1.0 - sig)))).astype(bf16)
        up_grad = (hidden_grad * silu).astype(bf16)
        dg_ref[e] = gate_grad
        du_ref[e] = up_grad
        term = dot_nt(gate_grad, wg_ref[e]) + dot_nt(up_grad, wu_ref[e])
        total = term if total is None else total + term
    dx_ref[...] = total.astype(bf16)


def expert_call(x, cot, weight, wg, wu, wd):
    blocks, rows, features = x.shape
    count, _, hidden = wg.shape
    tokens = blocks * rows
    inner = jax.ShapeDtypeStruct((count, tokens, hidden), bf16)
    inner_spec = pl.BlockSpec((count, rows, hidden), lambda s: (0, s, 0))
    return pl.pallas_call(
        expert_kernel,
        grid=(blocks,),
        in_specs=[
            pl.BlockSpec((1, rows, features), lambda s: (s, 0, 0)),
            pl.BlockSpec((1, rows, features), lambda s: (s, 0, 0)),
            pl.BlockSpec((rows, count), lambda s: (s, 0)),
            whole(wg.shape),
            whole(wu.shape),
            whole(wd.shape),
        ],
        out_specs=[
            pl.BlockSpec((rows, features), lambda s: (s, 0)),
            inner_spec,
            inner_spec,
            inner_spec,
        ],
        out_shape=[jax.ShapeDtypeStruct((tokens, features), bf16), inner, inner, inner],
        compiler_params=params(48, "arbitrary"),
        cost_estimate=cost(10 * tokens * wg.size, 4e7, tokens * hidden * count),
        name="expert_gradients",
    )(x, cot, weight, wg, wu, wd)


def turn_kernel(sg_ref, middle_ref, gain_ref, cot_ref, wo_ref, mg_ref, proj_ref, dmid_ref, dgain_ref):
    grad = sg_ref[...].astype(f32)
    middle = middle_ref[...]
    scale = lax.rsqrt(jnp.mean(middle * middle, axis=-1, keepdims=True) + norm_eps)
    unit = middle * scale
    dgain_ref[...] = jnp.sum(grad * unit, axis=0, keepdims=True)
    w = gain_ref[...] * grad
    dmid = cot_ref[...].astype(f32) + scale * (w - unit * jnp.mean(w * unit, axis=-1, keepdims=True))
    dmid_ref[...] = dmid
    proj = (residual_scale * dmid).astype(bf16)
    proj_ref[...] = proj
    mixed_grad = dot_nt(proj, wo_ref[...]).astype(bf16)
    groups, _, pair = mg_ref.shape
    for g in range(groups):
        mg_ref[g] = mixed_grad[:, g * pair : (g + 1) * pair]


def turn_call(sg, middle, gain, cot, wo, groups):
    rows, features = middle.shape
    pair = wo.shape[0] // groups
    return pl.pallas_call(
        turn_kernel,
        out_shape=[
            jax.ShapeDtypeStruct((groups, rows, pair), bf16),
            jax.ShapeDtypeStruct((rows, features), bf16),
            jax.ShapeDtypeStruct((rows, features), f32),
            jax.ShapeDtypeStruct((1, features), f32),
        ],
        compiler_params=params(32),
        cost_estimate=cost(2 * rows * wo.size, 6e6),
        name="norm_back_project_back",
    )(sg, middle, gain, cot, wo)


def last_kernel(d_ref, wq_ref, wk_ref, wv_ref, x_ref, gain_ref, dmid_ref, out_ref):
    groups, rows, width = d_ref.shape
    pair = width // 2
    dq = jnp.concatenate([d_ref[g, :, :pair] for g in range(groups)], axis=1)
    grad = dot_nt(dq, wq_ref[...])
    keys, vals = [], []
    for at in range(groups // 2):
        a = d_ref[2 * at, :, pair:].astype(f32)
        b = d_ref[2 * at + 1, :, pair:].astype(f32)
        lane = lax.broadcasted_iota(jnp.int32, a.shape, 1)
        keys.append(jnp.where(lane < HEAD_DIM, a, pltpu.roll(b, HEAD_DIM, 1)).astype(bf16))
        vals.append(jnp.where(lane < HEAD_DIM, pltpu.roll(a, HEAD_DIM, 1), b).astype(bf16))
    grad = grad + dot_nt(jnp.concatenate(keys, axis=1), wk_ref[...])
    grad = grad + dot_nt(jnp.concatenate(vals, axis=1), wv_ref[...])
    x = x_ref[...].astype(f32)
    scale = lax.rsqrt(jnp.mean(x * x, axis=-1, keepdims=True) + norm_eps)
    unit = x * scale
    w = gain_ref[...] * grad
    out_ref[...] = dmid_ref[...] + scale * (w - unit * jnp.mean(w * unit, axis=-1, keepdims=True))


def last_call(d, wq, wk, wv, x, gain, dmid):
    rows, features = x.shape
    return pl.pallas_call(
        last_kernel,
        out_shape=jax.ShapeDtypeStruct((rows, features), f32),
        compiler_params=params(40),
        cost_estimate=cost(4 * rows * features * features, 8e6),
        name="input_gradient",
    )(d, wq, wk, wv, x, gain, dmid)


def body(
    layer_input,
    first_gain,
    query_weight,
    key_weight,
    value_weight,
    output_weight,
    second_gain,
    gate_weight,
    up_weight,
    down_weight,
    expert_ids,
    gate_values,
    positions,
    cotangent,
):
    micro, _, per_device, features = layer_input.shape
    devices = lax.axis_size("seq")
    replicas = lax.axis_size("dp")
    seq_place = lax.axis_index("seq")
    rows = micro * per_device
    local_experts = gate_weight.shape[0]
    groups = key_weight.shape[1] // HEAD_DIM
    pair = query_weight.shape[1] // groups
    copies = devices // groups

    def spread(blocks):
        if copies > 1:
            blocks = jnp.repeat(blocks, copies, axis=0)
        return lax.all_to_all(blocks, "seq", 0, 0, tiled=True)

    def unspread(blocks):
        return lax.all_to_all(blocks, "seq", 0, 0, tiled=True)[::copies]

    x = layer_input.reshape(rows, features)
    cot = cotangent.reshape(rows, features)
    gain_one = first_gain.reshape(1, features)
    gain_two = second_gain.reshape(1, features)
    pos = positions.reshape(rows)
    pos_all = lax.all_to_all(
        jnp.broadcast_to(pos[None, :], (devices, rows)), "seq", 0, 0, tiled=True
    )
    cos_row, sin_row = rope_tables(pos, pair)

    send, first_low = pre_call(
        x, gain_one, cos_row, sin_row, query_weight, key_weight, value_weight
    )
    qkv = spread(send)
    cot_all = lax.all_gather(cot, "seq", axis=0)
    qkv = qkv.reshape(devices, micro, per_device, 2 * pair)
    mix = attend_call(qkv)
    mix = unspread(mix.reshape(devices, rows, pair))
    mixed, middle, second_low = post_call(mix, output_weight, x, gain_two)
    second_all = lax.all_gather(second_low, "seq", axis=0)

    mine = seq_place * local_experts + jnp.arange(local_experts, dtype=jnp.int32)
    ids = expert_ids[:, 0]
    gates = gate_values[:, 0].astype(f32)
    routed = jnp.sum(
        jnp.where(ids[..., None] == mine, gates[..., None], 0.0), axis=2
    )
    routed = routed.reshape(micro, devices, per_device, local_experts)
    routed = jnp.transpose(routed, (1, 0, 2, 3)).reshape(devices * rows, local_experts)

    dx, hidden, gate_low, up_low = expert_call(
        second_all, cot_all, routed, gate_weight, up_weight, down_weight
    )
    second_grad = lax.psum_scatter(dx, "seq", scatter_dimension=0, tiled=True)

    tokens = second_all.reshape(devices * rows, features)
    cot_tokens = cot_all.reshape(devices * rows, features)
    slot_grad = (routed.T[..., None] * (residual_scale * cot_tokens.astype(f32))[None]).astype(bf16)
    gate_term = jnp.einsum("td,etf->edf", tokens, gate_low, preferred_element_type=f32)
    up_term = jnp.einsum("td,etf->edf", tokens, up_low, preferred_element_type=f32)
    down_term = jnp.einsum("etf,etd->efd", hidden, slot_grad, preferred_element_type=f32)
    expert_sums = lax.psum(
        (gate_term.astype(bf16), up_term.astype(bf16), down_term.astype(bf16)), "dp"
    )
    produced = jnp.einsum("etf,efd->etd", hidden, down_weight, preferred_element_type=f32)
    moe_all = jnp.sum(routed.T[..., None] * produced, axis=0).astype(bf16)
    moe = lax.psum_scatter(moe_all, "seq", scatter_dimension=0, tiled=True)
    layer_output = (middle + residual_scale * moe.astype(f32)).astype(bf16)

    mg_send, proj, middle_grad, gain_two_part = turn_call(
        second_grad, middle, gain_two, cot, output_weight, groups
    )
    mg = spread(mg_send)
    output_part = lax.dot_general(mixed, proj, TN, preferred_element_type=f32).astype(bf16)
    dense = jnp.concatenate(
        [output_part, jnp.broadcast_to(gain_two_part.astype(bf16), (16, features))], axis=0
    )
    dense = lax.psum(dense, ("dp", "seq"))
    output_weight_grad = dense[: output_part.shape[0]].astype(f32)
    second_gain_grad = dense[output_part.shape[0]].astype(f32)

    cos_all, sin_all = rope_tables(pos_all.reshape(-1), pair)
    table_shape = (devices, micro, per_device, pair)
    dqkv = attend_back_call(
        qkv,
        mg.reshape(devices, micro, per_device, pair),
        cos_all.reshape(table_shape),
        sin_all.reshape(table_shape),
    )
    d_all = dqkv.reshape(devices * rows, 2 * pair)
    first_all = lax.all_gather(first_low, "seq", axis=0).reshape(devices * rows, features)
    part = lax.dot_general(first_all, d_all, TN, preferred_element_type=f32).astype(bf16)
    part = part.reshape(replicas, features // replicas, 2 * pair)
    part = lax.all_to_all(part, "dp", 0, 0, tiled=True)
    part = jnp.sum(part.astype(f32), axis=0).astype(bf16)
    wide = lax.all_gather(part, ("dp", "seq"), axis=0)
    wide = wide.reshape(replicas, devices, features // replicas, 2 * pair)[:, ::copies].astype(f32)
    wide = jnp.transpose(wide, (0, 2, 1, 3)).reshape(features, groups, 2 * pair)
    query_weight_grad = wide[..., :pair].reshape(query_weight.shape)
    key_weight_grad = wide[..., pair : pair + HEAD_DIM].reshape(key_weight.shape)
    value_weight_grad = wide[..., pair + HEAD_DIM :].reshape(value_weight.shape)
    first_gain_grad = (
        jnp.sum(query_weight_grad * query_weight.astype(f32), axis=1)
        + jnp.sum(key_weight_grad * key_weight.astype(f32), axis=1)
        + jnp.sum(value_weight_grad * value_weight.astype(f32), axis=1)
    ) / first_gain

    back = unspread(dqkv.reshape(devices, rows, 2 * pair))
    input_grad = last_call(
        back, query_weight, key_weight, value_weight, x, gain_one, middle_grad
    )
    return (
        layer_output.reshape(layer_input.shape),
        input_grad.reshape(layer_input.shape),
        first_gain_grad,
        query_weight_grad,
        key_weight_grad,
        value_weight_grad,
        output_weight_grad,
        second_gain_grad,
        expert_sums[0].astype(f32),
        expert_sums[1].astype(f32),
        expert_sums[2].astype(f32),
    )


def solution(mesh):
    return jax.shard_map(
        body,
        mesh=mesh,
        in_specs=(
            P(None, "dp", "seq", None),
            P(),
            P(),
            P(),
            P(),
            P(),
            P(),
            P("seq", None, None),
            P("seq", None, None),
            P("seq", None, None),
            P(None, "dp", None, None),
            P(None, "dp", None, None),
            P(None, "dp", "seq"),
            P(None, "dp", "seq", None),
        ),
        out_specs=(
            P(None, "dp", "seq", None),
            P(None, "dp", "seq", None),
            P(),
            P(),
            P(),
            P(),
            P(),
            P(),
            P("seq", None, None),
            P("seq", None, None),
            P("seq", None, None),
        ),
        check_vma=False,
    )
```

```python
from functools import partial

import jax
import jax.numpy as jnp
from jax import lax
from jax.experimental import pallas as pl
from jax.experimental.pallas import tpu as pltpu
from jax.sharding import PartitionSpec as P

HEAD_DIM = 64

rope_theta = 10000.0
attention_scale = 0.015625
residual_scale = 0.22
norm_eps = 1e-06
masked_score = -1e30

f32 = jnp.float32
bf16 = jnp.bfloat16
NT = (((1,), (1,)), ((), ()))
TN = (((0,), (0,)), ((), ()))


def dot(a, b):
    return jnp.dot(a, b, preferred_element_type=f32)


def dot_nt(a, b):
    return lax.dot_general(a, b, NT, preferred_element_type=f32)


def params(mib, *semantics):
    return pltpu.CompilerParams(
        vmem_limit_bytes=mib * 1024 * 1024, dimension_semantics=semantics or None
    )


def cost(flops, nbytes, trans=0):
    return pl.CostEstimate(
        flops=int(flops), bytes_accessed=int(nbytes), transcendentals=int(trans)
    )


def whole(shape):
    return pl.BlockSpec(shape, lambda *_: (0,) * len(shape))


def rope_tables(positions, width):
    half = HEAD_DIM // 2
    exponent = jnp.arange(half, dtype=f32) * (-2.0 / HEAD_DIM)
    angles = positions.astype(f32)[:, None] * (rope_theta**exponent)[None, :]
    cosine, sine = jnp.cos(angles), jnp.sin(angles)
    copies = width // HEAD_DIM
    cos_row = jnp.concatenate([cosine, cosine] * copies, axis=1)
    sin_row = jnp.concatenate([-sine, sine] * copies, axis=1)
    return cos_row, sin_row


def partner(values):
    width = values.shape[1]
    half = HEAD_DIM // 2
    lane = lax.broadcasted_iota(jnp.int32, values.shape, 1)
    ahead = pltpu.roll(values, width - half, 1)
    behind = pltpu.roll(values, half, 1)
    return jnp.where(lane % HEAD_DIM < half, ahead, behind)


def qkv_kernel(place_ref, x_ref, gain_ref, cos_ref, sin_ref, wq_ref, wk_ref, wv_ref, qkv_ref, low_ref):
    pair = 2 * HEAD_DIM
    x = x_ref[0].astype(f32)
    scale = lax.rsqrt(jnp.mean(x * x, axis=-1, keepdims=True) + norm_eps)
    low = (x * scale * gain_ref[...]).astype(bf16)
    low_ref[0] = low
    cosine, sine = cos_ref[...], sin_ref[...]
    q = dot(low, wq_ref[...])
    q = (q * cosine + partner(q) * sine) * attention_scale
    qkv_ref[0, :, :pair] = q.astype(bf16)
    k = dot(low, wk_ref[...])
    v = dot(low, wv_ref[...])
    second = place_ref[0] % 2
    k = k * cosine + partner(k) * sine
    k = jnp.where(second == 0, k, pltpu.roll(k, HEAD_DIM, 1))
    v = jnp.where(second == 0, pltpu.roll(v, HEAD_DIM, 1), v)
    lane = lax.broadcasted_iota(jnp.int32, k.shape, 1)
    qkv_ref[0, :, pair:] = jnp.where(lane < HEAD_DIM, k, v).astype(bf16)


def qkv_call(group, x_all, gain, cos_all, sin_all, wq, wk, wv):
    blocks, rows, features = x_all.shape
    pair = 2 * HEAD_DIM
    return pl.pallas_call(
        qkv_kernel,
        grid_spec=pltpu.PrefetchScalarGridSpec(
            num_scalar_prefetch=1,
            grid=(blocks,),
            in_specs=[
                pl.BlockSpec((1, rows, features), lambda s, place: (s, 0, 0)),
                pl.BlockSpec((1, features), lambda s, place: (0, 0)),
                pl.BlockSpec((rows, pair), lambda s, place: (s, 0)),
                pl.BlockSpec((rows, pair), lambda s, place: (s, 0)),
                pl.BlockSpec((features, pair), lambda s, place: (0, place[0])),
                pl.BlockSpec((features, pair), lambda s, place: (0, place[0] // 2)),
                pl.BlockSpec((features, pair), lambda s, place: (0, place[0] // 2)),
            ],
            out_specs=[
                pl.BlockSpec((1, rows, 2 * pair), lambda s, place: (s, 0, 0)),
                pl.BlockSpec((1, rows, features), lambda s, place: (s, 0, 0)),
            ],
        ),
        out_shape=[
            jax.ShapeDtypeStruct((blocks, rows, 2 * pair), bf16),
            jax.ShapeDtypeStruct((blocks, rows, features), bf16),
        ],
        compiler_params=params(32, "arbitrary"),
        cost_estimate=cost(6 * blocks * rows * features * pair, 14e6),
        name="norm_qkv_rope",
    )(group, x_all, gain, cos_all, sin_all, wq, wk, wv)


def split_heads(block, first):
    wide = block.astype(f32)
    lane = lax.broadcasted_iota(jnp.int32, wide.shape, 1)
    turned = pltpu.roll(wide, HEAD_DIM, 1)
    if first:
        parts = [jnp.where(lane < HEAD_DIM, wide, 0.0), jnp.where(lane < HEAD_DIM, turned, 0.0)]
    else:
        parts = [jnp.where(lane >= HEAD_DIM, turned, 0.0), jnp.where(lane >= HEAD_DIM, wide, 0.0)]
    return jnp.concatenate(parts, axis=0).astype(bf16)


def join_heads(turned):
    rows = turned.shape[1] // 2
    return jnp.transpose(jnp.concatenate([turned[:, :rows], turned[:, rows:]], axis=0))


def scores_of(kv, q2, rows):
    scores = dot_nt(kv, q2)
    count = scores.shape[0]
    own = scores[count - rows :]
    key_at = lax.broadcasted_iota(jnp.int32, own.shape, 0)
    query_at = lax.broadcasted_iota(jnp.int32, own.shape, 1) % rows
    own = jnp.where(key_at <= query_at, own, masked_score)
    if count == rows:
        return own
    return jnp.concatenate([scores[: count - rows], own], axis=0)


def attend_kernel(qkv_ref, out_ref):
    blocks, _, rows, width = qkv_ref.shape
    pair = width // 2
    kv = qkv_ref[:, 0, :, pair:].reshape(blocks * rows, pair)
    kv_t = jnp.transpose(kv)
    for at in range(blocks):
        count = (at + 1) * rows
        q2 = split_heads(qkv_ref[at, 0, :, :pair], True)
        scores = scores_of(kv[:count], q2, rows)
        top = jnp.max(scores, axis=0, keepdims=True)
        weights = jnp.exp(scores - top)
        total = jnp.sum(weights, axis=0, keepdims=True)
        out_t = dot(kv_t[:, :count], weights.astype(bf16))
        out_ref[at, 0] = join_heads(out_t[HEAD_DIM:] / total).astype(bf16)


def attend_call(qkv):
    blocks, micro, rows, width = qkv.shape
    pair = width // 2
    length = blocks * rows
    return pl.pallas_call(
        attend_kernel,
        grid=(micro,),
        in_specs=[pl.BlockSpec((blocks, 1, rows, width), lambda m: (0, m, 0, 0))],
        out_specs=pl.BlockSpec((blocks, 1, rows, pair), lambda m: (0, m, 0, 0)),
        out_shape=jax.ShapeDtypeStruct((blocks, micro, rows, pair), bf16),
        compiler_params=params(48, "arbitrary"),
        cost_estimate=cost(
            micro * length * length * 512, 3 * qkv.size, micro * length * length
        ),
        name="attention_forward",
    )(qkv)


def attend_back_kernel(qkv_ref, grad_ref, cos_ref, sin_ref, out_ref, dkv_ref):
    blocks, _, rows, width = qkv_ref.shape
    pair = width // 2
    kv = qkv_ref[:, 0, :, pair:].reshape(blocks * rows, pair)
    kv_t = jnp.transpose(kv)
    dkv_ref[...] = jnp.zeros_like(dkv_ref)
    for at in range(blocks):
        count = (at + 1) * rows
        q2 = split_heads(qkv_ref[at, 0, :, :pair], True)
        g2 = split_heads(grad_ref[at, 0], False)
        scores = scores_of(kv[:count], q2, rows)
        top = jnp.max(scores, axis=0, keepdims=True)
        weights = jnp.exp(scores - top)
        total = jnp.sum(weights, axis=0, keepdims=True)
        prob = weights * (1.0 / total)
        prob_grad = dot_nt(kv[:count], g2)
        delta = jnp.sum(prob * prob_grad, axis=0, keepdims=True)
        score_grad = (prob * (prob_grad - delta)).astype(bf16)
        dkv_ref[:count] += dot(score_grad, q2) + dot(prob.astype(bf16), g2)
        dq_t = dot(kv_t[:, :count], score_grad)
        dq = join_heads(dq_t[:HEAD_DIM] * attention_scale)
        dq = dq * cos_ref[at, 0] - partner(dq) * sin_ref[at, 0]
        out_ref[at, 0, :, :pair] = dq.astype(bf16)
    for at in range(blocks):
        dkv = dkv_ref[at * rows : (at + 1) * rows]
        lane = lax.broadcasted_iota(jnp.int32, dkv.shape, 1)
        turned = dkv * cos_ref[at, 0] - partner(dkv) * sin_ref[at, 0]
        out_ref[at, 0, :, pair:] = jnp.where(lane < HEAD_DIM, turned, dkv).astype(bf16)


def attend_back_call(qkv, grads, cos_all, sin_all):
    blocks, micro, rows, width = qkv.shape
    pair = width // 2
    length = blocks * rows
    spec = lambda lanes: pl.BlockSpec((blocks, 1, rows, lanes), lambda m: (0, m, 0, 0))
    return pl.pallas_call(
        attend_back_kernel,
        grid=(micro,),
        in_specs=[spec(width), spec(pair), spec(pair), spec(pair)],
        out_specs=spec(width),
        out_shape=jax.ShapeDtypeStruct(qkv.shape, bf16),
        scratch_shapes=[pltpu.VMEM((length, pair), f32)],
        compiler_params=params(56, "arbitrary"),
        cost_estimate=cost(
            micro * length * length * 1280, 10 * qkv.size, micro * length * length
        ),
        name="attention_backward",
    )(qkv, grads, cos_all, sin_all)


def post_kernel(mix_ref, wo_ref, x_ref, gain_ref, mixed_ref, middle_ref, low_ref):
    mixed = jnp.concatenate([mix_ref[g] for g in range(mix_ref.shape[0])], axis=1)
    mixed_ref[...] = mixed
    middle = x_ref[...].astype(f32) + residual_scale * dot(mixed, wo_ref[...])
    middle_ref[...] = middle
    scale = lax.rsqrt(jnp.mean(middle * middle, axis=-1, keepdims=True) + norm_eps)
    low_ref[...] = (middle * scale * gain_ref[...]).astype(bf16)


def post_call(mix, wo, x, gain):
    rows, features = x.shape
    return pl.pallas_call(
        post_kernel,
        out_shape=[
            jax.ShapeDtypeStruct((rows, wo.shape[0]), bf16),
            jax.ShapeDtypeStruct((rows, features), f32),
            jax.ShapeDtypeStruct((rows, features), bf16),
        ],
        compiler_params=params(32),
        cost_estimate=cost(2 * rows * wo.size, 5e6),
        name="project_norm",
    )(mix, wo, x, gain)


def expert_kernel(
    x_ref, cot_ref, w_ref, wg_ref, wu_ref, wd_ref, dx_ref, h_ref, dg_ref, du_ref, sg_ref
):
    x = x_ref[0]
    cot = residual_scale * cot_ref[0].astype(f32)
    weight = w_ref[...]
    total = None
    for e in range(wg_ref.shape[0]):
        gate = dot(x, wg_ref[e])
        up = dot(x, wu_ref[e])
        slot_grad = (weight[:, e : e + 1] * cot).astype(bf16)
        sg_ref[e] = slot_grad
        hidden_grad = dot_nt(slot_grad, wd_ref[e])
        sig = 1.0 / (1.0 + jnp.exp(-gate))
        silu = gate * sig
        h_ref[e] = (silu * up).astype(bf16)
        gate_grad = (hidden_grad * up * (sig * (1.0 + gate * (1.0 - sig)))).astype(bf16)
        up_grad = (hidden_grad * silu).astype(bf16)
        dg_ref[e] = gate_grad
        du_ref[e] = up_grad
        term = dot_nt(gate_grad, wg_ref[e]) + dot_nt(up_grad, wu_ref[e])
        total = term if total is None else total + term
    dx_ref[...] = total.astype(bf16)


def expert_call(x, cot, weight, wg, wu, wd):
    blocks, rows, features = x.shape
    count, _, hidden = wg.shape
    tokens = blocks * rows
    inner = jax.ShapeDtypeStruct((count, tokens, hidden), bf16)
    inner_spec = pl.BlockSpec((count, rows, hidden), lambda s: (0, s, 0))
    return pl.pallas_call(
        expert_kernel,
        grid=(blocks,),
        in_specs=[
            pl.BlockSpec((1, rows, features), lambda s: (s, 0, 0)),
            pl.BlockSpec((1, rows, features), lambda s: (s, 0, 0)),
            pl.BlockSpec((rows, count), lambda s: (s, 0)),
            whole(wg.shape),
            whole(wu.shape),
            whole(wd.shape),
        ],
        out_specs=[
            pl.BlockSpec((rows, features), lambda s: (s, 0)),
            inner_spec,
            inner_spec,
            inner_spec,
            pl.BlockSpec((count, rows, features), lambda s: (0, s, 0)),
        ],
        out_shape=[
            jax.ShapeDtypeStruct((tokens, features), bf16),
            inner,
            inner,
            inner,
            jax.ShapeDtypeStruct((count, tokens, features), bf16),
        ],
        compiler_params=params(48, "arbitrary"),
        cost_estimate=cost(10 * tokens * wg.size, 4e7, tokens * hidden * count),
        name="expert_gradients",
    )(x, cot, weight, wg, wu, wd)


def moe_kernel(h_ref, w_ref, wd_ref, out_ref):
    weight = w_ref[...]
    total = None
    for e in range(wd_ref.shape[0]):
        term = weight[:, e : e + 1] * dot(h_ref[e], wd_ref[e])
        total = term if total is None else total + term
    out_ref[...] = total.astype(bf16)


def moe_call(hidden, weight, wd):
    count, tokens, inner = hidden.shape
    features = wd.shape[2]
    rows = 256
    return pl.pallas_call(
        moe_kernel,
        grid=(tokens // rows,),
        in_specs=[
            pl.BlockSpec((count, rows, inner), lambda s: (0, s, 0)),
            pl.BlockSpec((rows, count), lambda s: (s, 0)),
            whole(wd.shape),
        ],
        out_specs=pl.BlockSpec((rows, features), lambda s: (s, 0)),
        out_shape=jax.ShapeDtypeStruct((tokens, features), bf16),
        compiler_params=params(32, "arbitrary"),
        cost_estimate=cost(2 * tokens * wd.size, 1.1e7),
        name="expert_outputs",
    )(hidden, weight, wd)


def turn_kernel(sg_ref, middle_ref, gain_ref, cot_ref, wo_ref, mg_ref, proj_ref, dmid_ref, dgain_ref):
    grad = sg_ref[...].astype(f32)
    middle = middle_ref[...]
    scale = lax.rsqrt(jnp.mean(middle * middle, axis=-1, keepdims=True) + norm_eps)
    unit = middle * scale
    dgain_ref[...] = jnp.sum(grad * unit, axis=0, keepdims=True)
    w = gain_ref[...] * grad
    dmid = cot_ref[...].astype(f32) + scale * (w - unit * jnp.mean(w * unit, axis=-1, keepdims=True))
    dmid_ref[...] = dmid
    proj = (residual_scale * dmid).astype(bf16)
    proj_ref[...] = proj
    mixed_grad = dot_nt(proj, wo_ref[...]).astype(bf16)
    groups, _, pair = mg_ref.shape
    for g in range(groups):
        mg_ref[g] = mixed_grad[:, g * pair : (g + 1) * pair]


def turn_call(sg, middle, gain, cot, wo, groups):
    rows, features = middle.shape
    pair = wo.shape[0] // groups
    return pl.pallas_call(
        turn_kernel,
        out_shape=[
            jax.ShapeDtypeStruct((groups, rows, pair), bf16),
            jax.ShapeDtypeStruct((rows, features), bf16),
            jax.ShapeDtypeStruct((rows, features), f32),
            jax.ShapeDtypeStruct((1, features), f32),
        ],
        compiler_params=params(32),
        cost_estimate=cost(2 * rows * wo.size, 6e6),
        name="norm_back_project_back",
    )(sg, middle, gain, cot, wo)


def output_weight_kernel(mixed_ref, proj_ref, dgain_ref, out_ref):
    held, each, features = out_ref.shape
    rows = mixed_ref.shape[1] // held
    part = lax.dot_general(mixed_ref[...], proj_ref[...], TN, preferred_element_type=f32)
    extra = jnp.broadcast_to(dgain_ref[...], (each - rows, features)).astype(bf16)
    for at in range(held):
        out_ref[at, :rows] = part[at * rows : (at + 1) * rows].astype(bf16)
        out_ref[at, rows:] = extra


def output_weight_call(mixed, proj, dgain, parts):
    rows, width = mixed.shape
    features = proj.shape[1]
    each = width // parts
    lanes = max(each, 2 * HEAD_DIM)
    held = lanes // each
    return pl.pallas_call(
        output_weight_kernel,
        grid=(parts // held,),
        in_specs=[
            pl.BlockSpec((rows, lanes), lambda s: (0, s)),
            whole((rows, features)),
            whole((1, features)),
        ],
        out_specs=pl.BlockSpec((held, each + 16, features), lambda s: (s, 0, 0)),
        out_shape=jax.ShapeDtypeStruct((parts, each + 16, features), bf16),
        compiler_params=params(32, "arbitrary"),
        cost_estimate=cost(2 * rows * width * features, 4e6),
        name="output_weight_part",
    )(mixed, proj, dgain)


def weights_out_kernel(wide_ref, wq_ref, wk_ref, wv_ref, gain_ref, dq_ref, dk_ref, dv_ref, dg_ref):
    groups, rows, width = wide_ref.shape
    pair = width // 2
    total = jnp.zeros((rows, pair), f32)
    for g in range(groups):
        part = wide_ref[g, :, :pair].astype(f32)
        at = slice(g * pair, (g + 1) * pair)
        dq_ref[:, at] = part
        total += part * wq_ref[:, at].astype(f32)
    for g in range(groups // 2):
        a = wide_ref[2 * g, :, pair:].astype(f32)
        b = wide_ref[2 * g + 1, :, pair:].astype(f32)
        lane = lax.broadcasted_iota(jnp.int32, a.shape, 1)
        at = slice(g * pair, (g + 1) * pair)
        k = jnp.where(lane < HEAD_DIM, a, pltpu.roll(b, HEAD_DIM, 1))
        v = jnp.where(lane < HEAD_DIM, pltpu.roll(a, HEAD_DIM, 1), b)
        dk_ref[:, at] = k
        dv_ref[:, at] = v
        total += k * wk_ref[:, at].astype(f32) + v * wv_ref[:, at].astype(f32)
    dg_ref[...] = jnp.sum(jnp.transpose(total), axis=0, keepdims=True) / gain_ref[...]


def weights_out_call(wide, wq, wk, wv, gain):
    chunks, groups, rows, width = wide.shape
    features = chunks * rows
    by_rows = lambda w: pl.BlockSpec((rows, w.shape[1]), lambda c: (c, 0))
    return pl.pallas_call(
        weights_out_kernel,
        grid=(chunks,),
        in_specs=[
            pl.BlockSpec((None, groups, rows, width), lambda c: (c, 0, 0, 0)),
            by_rows(wq),
            by_rows(wk),
            by_rows(wv),
            pl.BlockSpec((1, rows), lambda c: (0, c)),
        ],
        out_specs=[
            by_rows(wq),
            by_rows(wk),
            by_rows(wv),
            pl.BlockSpec((1, rows), lambda c: (0, c)),
        ],
        out_shape=[
            jax.ShapeDtypeStruct(wq.shape, f32),
            jax.ShapeDtypeStruct(wk.shape, f32),
            jax.ShapeDtypeStruct(wv.shape, f32),
            jax.ShapeDtypeStruct((1, features), f32),
        ],
        compiler_params=params(32, "arbitrary"),
        cost_estimate=cost(2 * wq.size, 1.6e7),
        name="attention_weights_out",
    )(wide, wq, wk, wv, gain)


def last_kernel(d_ref, wq_ref, wk_ref, wv_ref, x_ref, gain_ref, dmid_ref, out_ref):
    groups, rows, width = d_ref.shape
    pair = width // 2
    dq = jnp.concatenate([d_ref[g, :, :pair] for g in range(groups)], axis=1)
    grad = dot_nt(dq, wq_ref[...])
    keys, vals = [], []
    for at in range(groups // 2):
        a = d_ref[2 * at, :, pair:].astype(f32)
        b = d_ref[2 * at + 1, :, pair:].astype(f32)
        lane = lax.broadcasted_iota(jnp.int32, a.shape, 1)
        keys.append(jnp.where(lane < HEAD_DIM, a, pltpu.roll(b, HEAD_DIM, 1)).astype(bf16))
        vals.append(jnp.where(lane < HEAD_DIM, pltpu.roll(a, HEAD_DIM, 1), b).astype(bf16))
    grad = grad + dot_nt(jnp.concatenate(keys, axis=1), wk_ref[...])
    grad = grad + dot_nt(jnp.concatenate(vals, axis=1), wv_ref[...])
    x = x_ref[...].astype(f32)
    scale = lax.rsqrt(jnp.mean(x * x, axis=-1, keepdims=True) + norm_eps)
    unit = x * scale
    w = gain_ref[...] * grad
    out_ref[...] = dmid_ref[...] + scale * (w - unit * jnp.mean(w * unit, axis=-1, keepdims=True))


def last_call(d, wq, wk, wv, x, gain, dmid):
    rows, features = x.shape
    return pl.pallas_call(
        last_kernel,
        out_shape=jax.ShapeDtypeStruct((rows, features), f32),
        compiler_params=params(40),
        cost_estimate=cost(4 * rows * features * features, 8e6),
        name="input_gradient",
    )(d, wq, wk, wv, x, gain, dmid)


def swap(values, axis, bit):
    return lax.ppermute(values, axis, [(i, i ^ bit) for i in range(lax.axis_size(axis))])


def half_sum(values, axis, bit):
    half = values.shape[0] // 2
    upper = (lax.axis_index(axis) & bit) > 0
    low, high = values[:half], values[half:]
    came = swap(jnp.where(upper, low, high), axis, bit)
    return (jnp.where(upper, high, low).astype(f32) + came.astype(f32)).astype(bf16)


def join_halves(values, axis, bit):
    came = swap(values, axis, bit)
    upper = (lax.axis_index(axis) & bit) > 0
    return jnp.concatenate(
        [jnp.where(upper, came, values), jnp.where(upper, values, came)], axis=0
    )


def sum_over(values, axis, bits):
    shape = values.shape
    values = values.reshape(-1, shape[-1])
    for bit in bits:
        values = half_sum(values, axis, bit)
    for bit in bits[::-1]:
        values = join_halves(values, axis, bit)
    return values.reshape(shape)


def body(
    layer_input,
    first_gain,
    query_weight,
    key_weight,
    value_weight,
    output_weight,
    second_gain,
    gate_weight,
    up_weight,
    down_weight,
    expert_ids,
    gate_values,
    positions,
    cotangent,
):
    micro, _, per_device, features = layer_input.shape
    devices = lax.axis_size("seq")
    replicas = lax.axis_size("dp")
    seq_place = lax.axis_index("seq")
    rows = micro * per_device
    local_experts = gate_weight.shape[0]
    groups = key_weight.shape[1] // HEAD_DIM
    pair = query_weight.shape[1] // groups
    copies = devices // groups

    dp_bits = [1 << i for i in range(replicas.bit_length() - 1)]

    def spread(blocks):
        if copies > 1:
            blocks = jnp.repeat(blocks, copies, axis=0)
        return lax.all_to_all(blocks, "seq", 0, 0, tiled=True)

    def unspread(blocks):
        return lax.all_to_all(blocks, "seq", 0, 0, tiled=True)[::copies]

    x = layer_input.reshape(rows, features)
    cot = cotangent.reshape(rows, features)
    gain_one = first_gain.reshape(1, features)
    gain_two = second_gain.reshape(1, features)
    x_all = lax.all_gather(x, "seq", axis=0)
    pos_all = lax.all_to_all(
        jnp.broadcast_to(positions.reshape(1, rows), (devices, rows)), "seq", 0, 0, tiled=True
    )
    cos_all, sin_all = rope_tables(pos_all.reshape(-1), pair)
    x_all, cot_then = lax.optimization_barrier((x_all, cot))
    cot_all = lax.all_gather(cot_then, "seq", axis=0)

    group = (seq_place // copies).astype(jnp.int32).reshape(1)
    qkv, first_all = qkv_call(
        group, x_all, gain_one, cos_all, sin_all, query_weight, key_weight, value_weight
    )
    qkv = qkv.reshape(devices, micro, per_device, 2 * pair)
    mix = attend_call(qkv)
    mix = unspread(mix.reshape(devices, rows, pair))
    mixed, middle, second_low = post_call(mix, output_weight, x, gain_two)
    second_all = lax.all_gather(second_low, "seq", axis=0)

    mine = seq_place * local_experts + jnp.arange(local_experts, dtype=jnp.int32)
    ids = expert_ids[:, 0]
    gates = gate_values[:, 0].astype(f32)
    routed = jnp.sum(
        jnp.where(ids[..., None] == mine, gates[..., None], 0.0), axis=2
    )
    routed = routed.reshape(micro, devices, per_device, local_experts)
    routed = jnp.transpose(routed, (1, 0, 2, 3)).reshape(devices * rows, local_experts)

    dx, hidden, gate_low, up_low, slot_grad = expert_call(
        second_all, cot_all, routed, gate_weight, up_weight, down_weight
    )
    second_grad = lax.psum_scatter(dx, "seq", scatter_dimension=0, tiled=True)

    tokens = second_all.reshape(devices * rows, features)
    gate_term = jnp.einsum("td,etf->edf", tokens, gate_low, preferred_element_type=f32)
    up_term = jnp.einsum("td,etf->edf", tokens, up_low, preferred_element_type=f32)
    down_term = jnp.einsum("etf,etd->efd", hidden, slot_grad, preferred_element_type=f32)
    moe_all = moe_call(hidden, routed, down_weight)
    gate_sum = sum_over(gate_term.astype(bf16), "dp", dp_bits)
    up_sum = sum_over(up_term.astype(bf16), "dp", dp_bits[::-1])
    down_low = down_term.astype(bf16)
    cut = local_experts // 2
    down_sum = jnp.concatenate(
        [
            sum_over(down_low[:cut], "dp", dp_bits),
            sum_over(down_low[cut:], "dp", dp_bits[::-1]),
        ],
        axis=0,
    )

    mg_send, proj, middle_grad, gain_two_part = turn_call(
        second_grad, middle, gain_two, cot, output_weight, groups
    )
    mg = spread(mg_send)
    dense = output_weight_call(mixed, proj, gain_two_part, devices)
    mg, dense, moe_all = lax.optimization_barrier((mg, dense, moe_all))
    dense = lax.psum_scatter(dense, "seq", scatter_dimension=0)
    moe = lax.psum_scatter(moe_all, "seq", scatter_dimension=0, tiled=True)
    layer_output = (middle + residual_scale * moe.astype(f32)).astype(bf16)
    for bit in dp_bits:
        dense = (dense.astype(f32) + swap(dense, "dp", bit).astype(f32)).astype(bf16)
    dense = lax.all_gather(dense, "seq", axis=0).astype(f32)
    each = output_weight.shape[0] // devices
    output_weight_grad = dense[:, :each].reshape(output_weight.shape)
    second_gain_grad = dense[0, each]

    table_shape = (devices, micro, per_device, pair)
    dqkv = attend_back_call(
        qkv,
        mg.reshape(devices, micro, per_device, pair),
        cos_all.reshape(table_shape),
        sin_all.reshape(table_shape),
    )
    d_all = dqkv.reshape(devices * rows, 2 * pair)
    first_tokens = first_all.reshape(devices * rows, features)
    part = lax.dot_general(first_tokens, d_all, TN, preferred_element_type=f32).astype(bf16)
    for bit in dp_bits[::-1]:
        part = half_sum(part, "dp", bit)
    wide = lax.all_gather(part, ("dp", "seq"), axis=0)
    wide = wide.reshape(replicas, devices, features // replicas, 2 * pair)[:, ::copies]
    query_weight_grad, key_weight_grad, value_weight_grad, first_gain_grad = weights_out_call(
        wide, query_weight, key_weight, value_weight, gain_one
    )

    back = unspread(dqkv.reshape(devices, rows, 2 * pair))
    input_grad = last_call(
        back, query_weight, key_weight, value_weight, x, gain_one, middle_grad
    )
    return (
        layer_output.reshape(layer_input.shape),
        input_grad.reshape(layer_input.shape),
        first_gain_grad.reshape(features),
        query_weight_grad,
        key_weight_grad,
        value_weight_grad,
        output_weight_grad,
        second_gain_grad,
        gate_sum.astype(f32),
        up_sum.astype(f32),
        down_sum.astype(f32),
    )


def solution(mesh):
    return jax.shard_map(
        body,
        mesh=mesh,
        in_specs=(
            P(None, "dp", "seq", None),
            P(),
            P(),
            P(),
            P(),
            P(),
            P(),
            P("seq", None, None),
            P("seq", None, None),
            P("seq", None, None),
            P(None, "dp", None, None),
            P(None, "dp", None, None),
            P(None, "dp", "seq"),
            P(None, "dp", "seq", None),
        ),
        out_specs=(
            P(None, "dp", "seq", None),
            P(None, "dp", "seq", None),
            P(),
            P(),
            P(),
            P(),
            P(),
            P(),
            P("seq", None, None),
            P("seq", None, None),
            P("seq", None, None),
        ),
        check_vma=False,
    )
```

```python
from functools import partial

import jax
import jax.numpy as jnp
from jax import lax
from jax.experimental import pallas as pl
from jax.experimental.pallas import tpu as pltpu
from jax.sharding import PartitionSpec as P

HEAD_DIM = 64

rope_theta = 10000.0
attention_scale = 0.015625
residual_scale = 0.22
norm_eps = 1e-06
masked_score = -1e30

f32 = jnp.float32
bf16 = jnp.bfloat16
NT = (((1,), (1,)), ((), ()))
TN = (((0,), (0,)), ((), ()))


def dot(a, b):
    return jnp.dot(a, b, preferred_element_type=f32)


def dot_nt(a, b):
    return lax.dot_general(a, b, NT, preferred_element_type=f32)


def params(mib, *semantics):
    return pltpu.CompilerParams(
        vmem_limit_bytes=mib * 1024 * 1024, dimension_semantics=semantics or None
    )


def cost(flops, nbytes, trans=0):
    return pl.CostEstimate(
        flops=int(flops), bytes_accessed=int(nbytes), transcendentals=int(trans)
    )


def whole(shape):
    return pl.BlockSpec(shape, lambda *_: (0,) * len(shape))


def rope_tables(positions, width):
    half = HEAD_DIM // 2
    exponent = jnp.arange(half, dtype=f32) * (-2.0 / HEAD_DIM)
    angles = positions.astype(f32)[:, None] * (rope_theta**exponent)[None, :]
    cosine, sine = jnp.cos(angles), jnp.sin(angles)
    copies = width // HEAD_DIM
    cos_row = jnp.concatenate([cosine, cosine] * copies, axis=1)
    sin_row = jnp.concatenate([-sine, sine] * copies, axis=1)
    return cos_row, sin_row


def partner(values):
    width = values.shape[1]
    half = HEAD_DIM // 2
    lane = lax.broadcasted_iota(jnp.int32, values.shape, 1)
    ahead = pltpu.roll(values, width - half, 1)
    behind = pltpu.roll(values, half, 1)
    return jnp.where(lane % HEAD_DIM < half, ahead, behind)


def qkv_kernel(place_ref, x_ref, gain_ref, cos_ref, sin_ref, wq_ref, wk_ref, wv_ref, qkv_ref, low_ref):
    pair = 2 * HEAD_DIM
    x = x_ref[0].astype(f32)
    scale = lax.rsqrt(jnp.mean(x * x, axis=-1, keepdims=True) + norm_eps)
    low = (x * scale * gain_ref[...]).astype(bf16)
    low_ref[0] = low
    cosine, sine = cos_ref[...], sin_ref[...]
    q = dot(low, wq_ref[...])
    q = (q * cosine + partner(q) * sine) * attention_scale
    qkv_ref[0, :, :pair] = q.astype(bf16)
    k = dot(low, wk_ref[...])
    v = dot(low, wv_ref[...])
    second = place_ref[0] % 2
    k = k * cosine + partner(k) * sine
    k = jnp.where(second == 0, k, pltpu.roll(k, HEAD_DIM, 1))
    v = jnp.where(second == 0, pltpu.roll(v, HEAD_DIM, 1), v)
    lane = lax.broadcasted_iota(jnp.int32, k.shape, 1)
    qkv_ref[0, :, pair:] = jnp.where(lane < HEAD_DIM, k, v).astype(bf16)


def qkv_call(group, x_all, gain, cos_all, sin_all, wq, wk, wv):
    blocks, rows, features = x_all.shape
    pair = 2 * HEAD_DIM
    return pl.pallas_call(
        qkv_kernel,
        grid_spec=pltpu.PrefetchScalarGridSpec(
            num_scalar_prefetch=1,
            grid=(blocks,),
            in_specs=[
                pl.BlockSpec((1, rows, features), lambda s, place: (s, 0, 0)),
                pl.BlockSpec((1, features), lambda s, place: (0, 0)),
                pl.BlockSpec((rows, pair), lambda s, place: (s, 0)),
                pl.BlockSpec((rows, pair), lambda s, place: (s, 0)),
                pl.BlockSpec((features, pair), lambda s, place: (0, place[0])),
                pl.BlockSpec((features, pair), lambda s, place: (0, place[0] // 2)),
                pl.BlockSpec((features, pair), lambda s, place: (0, place[0] // 2)),
            ],
            out_specs=[
                pl.BlockSpec((1, rows, 2 * pair), lambda s, place: (s, 0, 0)),
                pl.BlockSpec((1, rows, features), lambda s, place: (s, 0, 0)),
            ],
        ),
        out_shape=[
            jax.ShapeDtypeStruct((blocks, rows, 2 * pair), bf16),
            jax.ShapeDtypeStruct((blocks, rows, features), bf16),
        ],
        compiler_params=params(32, "arbitrary"),
        cost_estimate=cost(6 * blocks * rows * features * pair, 14e6),
        name="norm_qkv_rope",
    )(group, x_all, gain, cos_all, sin_all, wq, wk, wv)


def split_heads(block, first):
    wide = block.astype(f32)
    lane = lax.broadcasted_iota(jnp.int32, wide.shape, 1)
    turned = pltpu.roll(wide, HEAD_DIM, 1)
    if first:
        parts = [jnp.where(lane < HEAD_DIM, wide, 0.0), jnp.where(lane < HEAD_DIM, turned, 0.0)]
    else:
        parts = [jnp.where(lane >= HEAD_DIM, turned, 0.0), jnp.where(lane >= HEAD_DIM, wide, 0.0)]
    return jnp.concatenate(parts, axis=0).astype(bf16)


def join_heads(turned):
    rows = turned.shape[1] // 2
    return jnp.transpose(jnp.concatenate([turned[:, :rows], turned[:, rows:]], axis=0))


def scores_of(kv, q2, rows):
    scores = dot_nt(kv, q2)
    count = scores.shape[0]
    own = scores[count - rows :]
    key_at = lax.broadcasted_iota(jnp.int32, own.shape, 0)
    query_at = lax.broadcasted_iota(jnp.int32, own.shape, 1) % rows
    own = jnp.where(key_at <= query_at, own, masked_score)
    if count == rows:
        return own
    return jnp.concatenate([scores[: count - rows], own], axis=0)


def attend_kernel(qkv_ref, out_ref):
    blocks, _, rows, width = qkv_ref.shape
    pair = width // 2
    kv = qkv_ref[:, 0, :, pair:].reshape(blocks * rows, pair)
    kv_t = jnp.transpose(kv)
    for at in range(blocks):
        count = (at + 1) * rows
        q2 = split_heads(qkv_ref[at, 0, :, :pair], True)
        scores = scores_of(kv[:count], q2, rows)
        top = jnp.max(scores, axis=0, keepdims=True)
        weights = jnp.exp(scores - top)
        total = jnp.sum(weights, axis=0, keepdims=True)
        out_t = dot(kv_t[:, :count], weights.astype(bf16))
        out_ref[at, 0] = join_heads(out_t[HEAD_DIM:] / total).astype(bf16)


def attend_call(qkv):
    blocks, micro, rows, width = qkv.shape
    pair = width // 2
    length = blocks * rows
    return pl.pallas_call(
        attend_kernel,
        grid=(micro,),
        in_specs=[pl.BlockSpec((blocks, 1, rows, width), lambda m: (0, m, 0, 0))],
        out_specs=pl.BlockSpec((blocks, 1, rows, pair), lambda m: (0, m, 0, 0)),
        out_shape=jax.ShapeDtypeStruct((blocks, micro, rows, pair), bf16),
        compiler_params=params(48, "arbitrary"),
        cost_estimate=cost(
            micro * length * length * 512, 3 * qkv.size, micro * length * length
        ),
        name="attention_forward",
    )(qkv)


def attend_back_kernel(qkv_ref, grad_ref, cos_ref, sin_ref, out_ref, dkv_ref):
    blocks, _, rows, width = qkv_ref.shape
    pair = width // 2
    kv = qkv_ref[:, 0, :, pair:].reshape(blocks * rows, pair)
    kv_t = jnp.transpose(kv)
    dkv_ref[...] = jnp.zeros_like(dkv_ref)
    for at in range(blocks):
        count = (at + 1) * rows
        q2 = split_heads(qkv_ref[at, 0, :, :pair], True)
        g2 = split_heads(grad_ref[at, 0], False)
        scores = scores_of(kv[:count], q2, rows)
        top = jnp.max(scores, axis=0, keepdims=True)
        weights = jnp.exp(scores - top)
        total = jnp.sum(weights, axis=0, keepdims=True)
        prob = weights * (1.0 / total)
        prob_grad = dot_nt(kv[:count], g2)
        delta = jnp.sum(prob * prob_grad, axis=0, keepdims=True)
        score_grad = (prob * (prob_grad - delta)).astype(bf16)
        dkv_ref[:count] += dot(score_grad, q2) + dot(prob.astype(bf16), g2)
        dq_t = dot(kv_t[:, :count], score_grad)
        dq = join_heads(dq_t[:HEAD_DIM] * attention_scale)
        dq = dq * cos_ref[at, 0] - partner(dq) * sin_ref[at, 0]
        out_ref[at, 0, :, :pair] = dq.astype(bf16)
    for at in range(blocks):
        dkv = dkv_ref[at * rows : (at + 1) * rows]
        lane = lax.broadcasted_iota(jnp.int32, dkv.shape, 1)
        turned = dkv * cos_ref[at, 0] - partner(dkv) * sin_ref[at, 0]
        out_ref[at, 0, :, pair:] = jnp.where(lane < HEAD_DIM, turned, dkv).astype(bf16)


def attend_back_call(qkv, grads, cos_all, sin_all):
    blocks, micro, rows, width = qkv.shape
    pair = width // 2
    length = blocks * rows
    spec = lambda lanes: pl.BlockSpec((blocks, 1, rows, lanes), lambda m: (0, m, 0, 0))
    return pl.pallas_call(
        attend_back_kernel,
        grid=(micro,),
        in_specs=[spec(width), spec(pair), spec(pair), spec(pair)],
        out_specs=spec(width),
        out_shape=jax.ShapeDtypeStruct(qkv.shape, bf16),
        scratch_shapes=[pltpu.VMEM((length, pair), f32)],
        compiler_params=params(56, "arbitrary"),
        cost_estimate=cost(
            micro * length * length * 1280, 10 * qkv.size, micro * length * length
        ),
        name="attention_backward",
    )(qkv, grads, cos_all, sin_all)


def post_kernel(mix_ref, wo_ref, x_ref, gain_ref, mixed_ref, middle_ref, low_ref):
    mixed = jnp.concatenate([mix_ref[g] for g in range(mix_ref.shape[0])], axis=1)
    mixed_ref[...] = mixed
    middle = x_ref[...].astype(f32) + residual_scale * dot(mixed, wo_ref[...])
    middle_ref[...] = middle
    scale = lax.rsqrt(jnp.mean(middle * middle, axis=-1, keepdims=True) + norm_eps)
    low_ref[...] = (middle * scale * gain_ref[...]).astype(bf16)


def post_call(mix, wo, x, gain):
    rows, features = x.shape
    return pl.pallas_call(
        post_kernel,
        out_shape=[
            jax.ShapeDtypeStruct((rows, wo.shape[0]), bf16),
            jax.ShapeDtypeStruct((rows, features), f32),
            jax.ShapeDtypeStruct((rows, features), bf16),
        ],
        compiler_params=params(32),
        cost_estimate=cost(2 * rows * wo.size, 5e6),
        name="project_norm",
    )(mix, wo, x, gain)


def expert_kernel(place_ref, a_ref, b_ref, cot_ref, w_ref, wg_ref, wu_ref, wd_ref, *refs):
    dx_ref, moe_ref, x_ref, h_ref, dg_ref, du_ref, sg_ref = refs[-7:]
    step = pl.program_id(0)

    @pl.when(step == 0)
    def _():
        x_ref[...] = a_ref[...]

    @pl.when(step == 1)
    def _():
        x_ref[...] = b_ref[...]

    x = x_ref[...]
    cot = residual_scale * cot_ref[0].astype(f32)
    weight = w_ref[...]
    total, made = None, None
    for e in range(wg_ref.shape[0]):
        gate = dot(x, wg_ref[e])
        up = dot(x, wu_ref[e])
        slot_grad = (weight[:, e : e + 1] * cot).astype(bf16)
        sg_ref[e] = slot_grad
        hidden_grad = dot_nt(slot_grad, wd_ref[e])
        sig = 1.0 / (1.0 + jnp.exp(-gate))
        silu = gate * sig
        hidden = (silu * up).astype(bf16)
        h_ref[e] = hidden
        gate_grad = (hidden_grad * up * (sig * (1.0 + gate * (1.0 - sig)))).astype(bf16)
        up_grad = (hidden_grad * silu).astype(bf16)
        dg_ref[e] = gate_grad
        du_ref[e] = up_grad
        term = dot_nt(gate_grad, wg_ref[e]) + dot_nt(up_grad, wu_ref[e])
        out = weight[:, e : e + 1] * dot(hidden, wd_ref[e])
        total = term if total is None else total + term
        made = out if made is None else made + out
    dx_ref[0] = total.astype(bf16)
    moe_ref[0] = made.astype(bf16)


def expert_call(at, place, own, other, cot_all, weight, wg, wu, wd, kept):
    blocks, rows, features = cot_all.shape
    count, _, hidden = wg.shape
    tokens = blocks * rows
    inner = jax.ShapeDtypeStruct((count, tokens, hidden), bf16)
    inner_spec = pl.BlockSpec((count, rows, hidden), lambda s, place: (0, 2 * at + s, 0))
    fixed = lambda shape: pl.BlockSpec(shape, lambda s, place: (0,) * len(shape))
    any_spec = pl.BlockSpec(memory_space=pl.ANY)
    first = 8
    return pl.pallas_call(
        expert_kernel,
        grid_spec=pltpu.PrefetchScalarGridSpec(
            num_scalar_prefetch=1,
            grid=(2,),
            in_specs=[
                fixed((rows, features)),
                fixed((rows, features)),
                pl.BlockSpec((1, rows, features), lambda s, place: (place[s], 0, 0)),
                pl.BlockSpec((rows, count), lambda s, place: (place[s], 0)),
                fixed(wg.shape),
                fixed(wu.shape),
                fixed(wd.shape),
            ]
            + [any_spec] * len(kept),
            out_specs=[
                pl.BlockSpec((1, rows, features), lambda s, place: (s, 0, 0)),
                pl.BlockSpec((1, rows, features), lambda s, place: (place[s], 0, 0)),
                pl.BlockSpec((rows, features), lambda s, place: (2 * at + s, 0)),
                inner_spec,
                inner_spec,
                inner_spec,
                pl.BlockSpec((count, rows, features), lambda s, place: (0, 2 * at + s, 0)),
            ],
        ),
        out_shape=[
            jax.ShapeDtypeStruct((2, rows, features), bf16),
            jax.ShapeDtypeStruct((blocks, rows, features), bf16),
            jax.ShapeDtypeStruct((tokens, features), bf16),
            inner,
            inner,
            inner,
            jax.ShapeDtypeStruct((count, tokens, features), bf16),
        ],
        input_output_aliases={first + i: 1 + i for i in range(len(kept))},
        compiler_params=params(48, "arbitrary"),
        cost_estimate=cost(24 * rows * wg.size, 2e7, 2 * rows * hidden * count),
        name="experts",
    )(place, own, other, cot_all, weight, wg, wu, wd, *kept)


def turn_kernel(sg_ref, middle_ref, gain_ref, cot_ref, wo_ref, mg_ref, proj_ref, dmid_ref, dgain_ref):
    grad = sg_ref[...].astype(f32)
    middle = middle_ref[...]
    scale = lax.rsqrt(jnp.mean(middle * middle, axis=-1, keepdims=True) + norm_eps)
    unit = middle * scale
    dgain_ref[...] = jnp.sum(grad * unit, axis=0, keepdims=True)
    w = gain_ref[...] * grad
    dmid = cot_ref[...].astype(f32) + scale * (w - unit * jnp.mean(w * unit, axis=-1, keepdims=True))
    dmid_ref[...] = dmid
    proj = (residual_scale * dmid).astype(bf16)
    proj_ref[...] = proj
    mixed_grad = dot_nt(proj, wo_ref[...]).astype(bf16)
    groups, _, pair = mg_ref.shape
    for g in range(groups):
        mg_ref[g] = mixed_grad[:, g * pair : (g + 1) * pair]


def turn_call(sg, middle, gain, cot, wo, groups):
    rows, features = middle.shape
    pair = wo.shape[0] // groups
    return pl.pallas_call(
        turn_kernel,
        out_shape=[
            jax.ShapeDtypeStruct((groups, rows, pair), bf16),
            jax.ShapeDtypeStruct((rows, features), bf16),
            jax.ShapeDtypeStruct((rows, features), f32),
            jax.ShapeDtypeStruct((1, features), f32),
        ],
        compiler_params=params(32),
        cost_estimate=cost(2 * rows * wo.size, 6e6),
        name="norm_back_project_back",
    )(sg, middle, gain, cot, wo)


def output_weight_kernel(mixed_ref, proj_ref, dgain_ref, out_ref):
    held, each, features = out_ref.shape
    rows = mixed_ref.shape[1] // held
    part = lax.dot_general(mixed_ref[...], proj_ref[...], TN, preferred_element_type=f32)
    extra = jnp.broadcast_to(dgain_ref[...], (each - rows, features)).astype(bf16)
    for at in range(held):
        out_ref[at, :rows] = part[at * rows : (at + 1) * rows].astype(bf16)
        out_ref[at, rows:] = extra


def output_weight_call(mixed, proj, dgain, parts):
    rows, width = mixed.shape
    features = proj.shape[1]
    each = width // parts
    lanes = max(each, 2 * HEAD_DIM)
    held = lanes // each
    return pl.pallas_call(
        output_weight_kernel,
        grid=(parts // held,),
        in_specs=[
            pl.BlockSpec((rows, lanes), lambda s: (0, s)),
            whole((rows, features)),
            whole((1, features)),
        ],
        out_specs=pl.BlockSpec((held, each + 16, features), lambda s: (s, 0, 0)),
        out_shape=jax.ShapeDtypeStruct((parts, each + 16, features), bf16),
        compiler_params=params(32, "arbitrary"),
        cost_estimate=cost(2 * rows * width * features, 4e6),
        name="output_weight_part",
    )(mixed, proj, dgain)


def weights_out_kernel(wide_ref, wq_ref, wk_ref, wv_ref, gain_ref, dq_ref, dk_ref, dv_ref, dg_ref):
    groups, rows, width = wide_ref.shape
    pair = width // 2
    total = jnp.zeros((rows, pair), f32)
    for g in range(groups):
        part = wide_ref[g, :, :pair].astype(f32)
        at = slice(g * pair, (g + 1) * pair)
        dq_ref[:, at] = part
        total += part * wq_ref[:, at].astype(f32)
    for g in range(groups // 2):
        a = wide_ref[2 * g, :, pair:].astype(f32)
        b = wide_ref[2 * g + 1, :, pair:].astype(f32)
        lane = lax.broadcasted_iota(jnp.int32, a.shape, 1)
        at = slice(g * pair, (g + 1) * pair)
        k = jnp.where(lane < HEAD_DIM, a, pltpu.roll(b, HEAD_DIM, 1))
        v = jnp.where(lane < HEAD_DIM, pltpu.roll(a, HEAD_DIM, 1), b)
        dk_ref[:, at] = k
        dv_ref[:, at] = v
        total += k * wk_ref[:, at].astype(f32) + v * wv_ref[:, at].astype(f32)
    dg_ref[...] = jnp.sum(jnp.transpose(total), axis=0, keepdims=True) / gain_ref[...]


def weights_out_call(wide, wq, wk, wv, gain):
    chunks, groups, rows, width = wide.shape
    features = chunks * rows
    by_rows = lambda w: pl.BlockSpec((rows, w.shape[1]), lambda c: (c, 0))
    return pl.pallas_call(
        weights_out_kernel,
        grid=(chunks,),
        in_specs=[
            pl.BlockSpec((None, groups, rows, width), lambda c: (c, 0, 0, 0)),
            by_rows(wq),
            by_rows(wk),
            by_rows(wv),
            pl.BlockSpec((1, rows), lambda c: (0, c)),
        ],
        out_specs=[
            by_rows(wq),
            by_rows(wk),
            by_rows(wv),
            pl.BlockSpec((1, rows), lambda c: (0, c)),
        ],
        out_shape=[
            jax.ShapeDtypeStruct(wq.shape, f32),
            jax.ShapeDtypeStruct(wk.shape, f32),
            jax.ShapeDtypeStruct(wv.shape, f32),
            jax.ShapeDtypeStruct((1, features), f32),
        ],
        compiler_params=params(32, "arbitrary"),
        cost_estimate=cost(2 * wq.size, 1.6e7),
        name="attention_weights_out",
    )(wide, wq, wk, wv, gain)


def last_kernel(d_ref, wq_ref, wk_ref, wv_ref, x_ref, gain_ref, dmid_ref, out_ref):
    groups, rows, width = d_ref.shape
    pair = width // 2
    dq = jnp.concatenate([d_ref[g, :, :pair] for g in range(groups)], axis=1)
    grad = dot_nt(dq, wq_ref[...])
    keys, vals = [], []
    for at in range(groups // 2):
        a = d_ref[2 * at, :, pair:].astype(f32)
        b = d_ref[2 * at + 1, :, pair:].astype(f32)
        lane = lax.broadcasted_iota(jnp.int32, a.shape, 1)
        keys.append(jnp.where(lane < HEAD_DIM, a, pltpu.roll(b, HEAD_DIM, 1)).astype(bf16))
        vals.append(jnp.where(lane < HEAD_DIM, pltpu.roll(a, HEAD_DIM, 1), b).astype(bf16))
    grad = grad + dot_nt(jnp.concatenate(keys, axis=1), wk_ref[...])
    grad = grad + dot_nt(jnp.concatenate(vals, axis=1), wv_ref[...])
    x = x_ref[...].astype(f32)
    scale = lax.rsqrt(jnp.mean(x * x, axis=-1, keepdims=True) + norm_eps)
    unit = x * scale
    w = gain_ref[...] * grad
    out_ref[...] = dmid_ref[...] + scale * (w - unit * jnp.mean(w * unit, axis=-1, keepdims=True))


def last_call(d, wq, wk, wv, x, gain, dmid):
    rows, features = x.shape
    return pl.pallas_call(
        last_kernel,
        out_shape=jax.ShapeDtypeStruct((rows, features), f32),
        compiler_params=params(40),
        cost_estimate=cost(4 * rows * features * features, 8e6),
        name="input_gradient",
    )(d, wq, wk, wv, x, gain, dmid)


def swap(values, axis, bit):
    return lax.ppermute(values, axis, [(i, i ^ bit) for i in range(lax.axis_size(axis))])


def half_sum(values, axis, bit):
    half = values.shape[0] // 2
    upper = (lax.axis_index(axis) & bit) > 0
    low, high = values[:half], values[half:]
    came = swap(jnp.where(upper, low, high), axis, bit)
    return (jnp.where(upper, high, low).astype(f32) + came.astype(f32)).astype(bf16)


def join_halves(values, axis, bit):
    came = swap(values, axis, bit)
    upper = (lax.axis_index(axis) & bit) > 0
    return jnp.concatenate(
        [jnp.where(upper, came, values), jnp.where(upper, values, came)], axis=0
    )


def body(
    layer_input,
    first_gain,
    query_weight,
    key_weight,
    value_weight,
    output_weight,
    second_gain,
    gate_weight,
    up_weight,
    down_weight,
    expert_ids,
    gate_values,
    positions,
    cotangent,
):
    micro, _, per_device, features = layer_input.shape
    devices = lax.axis_size("seq")
    replicas = lax.axis_size("dp")
    seq_place = lax.axis_index("seq")
    rows = micro * per_device
    local_experts = gate_weight.shape[0]
    groups = key_weight.shape[1] // HEAD_DIM
    pair = query_weight.shape[1] // groups
    copies = devices // groups

    dp_bits = [1 << i for i in range(replicas.bit_length() - 1)]

    def spread(blocks):
        if copies > 1:
            blocks = jnp.repeat(blocks, copies, axis=0)
        return lax.all_to_all(blocks, "seq", 0, 0, tiled=True)

    def unspread(blocks):
        return lax.all_to_all(blocks, "seq", 0, 0, tiled=True)[::copies]

    x = layer_input.reshape(rows, features)
    cot = cotangent.reshape(rows, features)
    gain_one = first_gain.reshape(1, features)
    gain_two = second_gain.reshape(1, features)
    pos_all = lax.all_to_all(
        jnp.broadcast_to(positions.reshape(1, rows), (devices, rows)), "seq", 0, 0, tiled=True
    )
    x_then, pos_all = lax.optimization_barrier((x, pos_all))
    x_all = lax.all_gather(x_then, "seq", axis=0)
    cos_all, sin_all = rope_tables(pos_all.reshape(-1), pair)
    mine = seq_place * local_experts + jnp.arange(local_experts, dtype=jnp.int32)
    ids = expert_ids[:, 0]
    gates = gate_values[:, 0].astype(f32)
    routed = jnp.sum(
        jnp.where(ids[..., None] == mine, gates[..., None], 0.0), axis=2
    )
    routed = routed.reshape(micro, devices, per_device, local_experts)
    routed = jnp.transpose(routed, (1, 0, 2, 3)).reshape(devices * rows, local_experts)
    cos_all, sin_all, routed = lax.optimization_barrier((cos_all, sin_all, routed))
    x_all, cot_then, cos_all, sin_all, routed = lax.optimization_barrier(
        (x_all, cot, cos_all, sin_all, routed)
    )
    cot_all = lax.all_gather(cot_then, "seq", axis=0)

    group = (seq_place // copies).astype(jnp.int32).reshape(1)
    qkv, first_all = qkv_call(
        group, x_all, gain_one, cos_all, sin_all, query_weight, key_weight, value_weight
    )
    qkv = qkv.reshape(devices, micro, per_device, 2 * pair)
    mix = attend_call(qkv)
    mix = unspread(mix.reshape(devices, rows, pair))
    mixed, middle, second_low = post_call(mix, output_weight, x, gain_two)

    chips = devices // 2
    chip, core = seq_place // 2, seq_place % 2
    onward = [(i, (i + 2) % devices) for i in range(devices)]
    held, kept, running = second_low, (), None
    for hop in range(chips):
        following = lax.ppermute(held, "seq", onward) if hop < chips - 1 else None
        other = swap(held, "seq", 1)
        source = 2 * ((chip - hop) % chips)
        place = jnp.stack([source + core, source + 1 - core]).astype(jnp.int32)
        dx, *kept = expert_call(
            hop, place, held, other, cot_all, routed, gate_weight, up_weight, down_weight, kept
        )
        if following is not None:
            following, dx = lax.optimization_barrier((following, dx))
        part = dx[0].astype(f32) + swap(dx[1], "seq", 1).astype(f32)
        if hop == 0:
            own_part = part
        else:
            if running is not None:
                part = part + running.astype(f32)
            part = part.astype(bf16)
            if following is not None:
                part, following = lax.optimization_barrier((part, following))
            running = lax.ppermute(part, "seq", onward)
        held = following
    second_grad = (own_part + running.astype(f32)).astype(bf16)
    moe_all, tokens, hidden, gate_low, up_low, slot_grad = kept

    gate_term = jnp.einsum("td,etf->edf", tokens, gate_low, preferred_element_type=f32)
    up_term = jnp.einsum("td,etf->edf", tokens, up_low, preferred_element_type=f32)
    down_term = jnp.einsum("etf,etd->efd", hidden, slot_grad, preferred_element_type=f32)
    gate_term, up_term, down_low, second_grad = lax.optimization_barrier(
        (gate_term.astype(bf16), up_term.astype(bf16), down_term.astype(bf16), second_grad)
    )
    cut = local_experts // 2
    sums = [
        (gate_term.reshape(-1, gate_term.shape[-1]), dp_bits),
        (up_term.reshape(-1, up_term.shape[-1]), dp_bits[::-1]),
        (down_low[:cut].reshape(-1, features), dp_bits),
        (down_low[cut:].reshape(-1, features), dp_bits[::-1]),
    ]
    pieces = [half_sum(values, "dp", bits[0]) for values, bits in sums]

    mg_send, proj, middle_grad, gain_two_part = turn_call(
        second_grad, middle, gain_two, cot, output_weight, groups
    )
    mg = spread(mg_send)
    dense = output_weight_call(mixed, proj, gain_two_part, devices)
    mg, dense, moe_all, *pieces = lax.optimization_barrier((mg, dense, moe_all, *pieces))
    for at in range(1, len(dp_bits)):
        pieces = [half_sum(p, "dp", bits[at]) for p, (_, bits) in zip(pieces, sums)]
    dense = lax.psum_scatter(dense, "seq", scatter_dimension=0)
    moe = lax.psum_scatter(moe_all, "seq", scatter_dimension=0)
    layer_output = (middle + residual_scale * moe.astype(f32)).astype(bf16)
    for bit in dp_bits:
        dense = (dense.astype(f32) + swap(dense, "dp", bit).astype(f32)).astype(bf16)
    dense = lax.all_gather(dense, "seq", axis=0).astype(f32)
    each = output_weight.shape[0] // devices
    output_weight_grad = dense[:, :each].reshape(output_weight.shape)
    second_gain_grad = dense[0, each]

    table_shape = (devices, micro, per_device, pair)
    dqkv = attend_back_call(
        qkv,
        mg.reshape(devices, micro, per_device, pair),
        cos_all.reshape(table_shape),
        sin_all.reshape(table_shape),
    )
    dqkv, *pieces = lax.optimization_barrier((dqkv, *pieces))
    for at in range(len(dp_bits))[::-1]:
        pieces = [join_halves(p, "dp", bits[at]) for p, (_, bits) in zip(pieces, sums)]
    gate_sum, up_sum = pieces[0].reshape(gate_term.shape), pieces[1].reshape(up_term.shape)
    down_sum = jnp.concatenate(pieces[2:], axis=0).reshape(down_low.shape)
    d_all = dqkv.reshape(devices * rows, 2 * pair)
    first_tokens = first_all.reshape(devices * rows, features)
    part = lax.dot_general(first_tokens, d_all, TN, preferred_element_type=f32).astype(bf16)
    for bit in dp_bits[::-1]:
        part = half_sum(part, "dp", bit)
    wide = lax.all_gather(part, ("dp", "seq"), axis=0)
    wide = wide.reshape(replicas, devices, features // replicas, 2 * pair)[:, ::copies]
    query_weight_grad, key_weight_grad, value_weight_grad, first_gain_grad = weights_out_call(
        wide, query_weight, key_weight, value_weight, gain_one
    )

    back = unspread(dqkv.reshape(devices, rows, 2 * pair))
    input_grad = last_call(
        back, query_weight, key_weight, value_weight, x, gain_one, middle_grad
    )
    return (
        layer_output.reshape(layer_input.shape),
        input_grad.reshape(layer_input.shape),
        first_gain_grad.reshape(features),
        query_weight_grad,
        key_weight_grad,
        value_weight_grad,
        output_weight_grad,
        second_gain_grad,
        gate_sum.astype(f32),
        up_sum.astype(f32),
        down_sum.astype(f32),
    )


def solution(mesh):
    return jax.shard_map(
        body,
        mesh=mesh,
        in_specs=(
            P(None, "dp", "seq", None),
            P(),
            P(),
            P(),
            P(),
            P(),
            P(),
            P("seq", None, None),
            P("seq", None, None),
            P("seq", None, None),
            P(None, "dp", None, None),
            P(None, "dp", None, None),
            P(None, "dp", "seq"),
            P(None, "dp", "seq", None),
        ),
        out_specs=(
            P(None, "dp", "seq", None),
            P(None, "dp", "seq", None),
            P(),
            P(),
            P(),
            P(),
            P(),
            P(),
            P("seq", None, None),
            P("seq", None, None),
            P("seq", None, None),
        ),
        check_vma=False,
    )
```

```python
from functools import partial

import jax
import jax.numpy as jnp
from jax import lax
from jax.experimental import pallas as pl
from jax.experimental.pallas import tpu as pltpu
from jax.sharding import PartitionSpec as P

HEAD_DIM = 64

rope_theta = 10000.0
attention_scale = 0.015625
residual_scale = 0.22
norm_eps = 1e-06
masked_score = -1e30

f32 = jnp.float32
bf16 = jnp.bfloat16
NT = (((1,), (1,)), ((), ()))
TN = (((0,), (0,)), ((), ()))


def dot(a, b):
    return jnp.dot(a, b, preferred_element_type=f32)


def dot_nt(a, b):
    return lax.dot_general(a, b, NT, preferred_element_type=f32)


def params(mib, *semantics):
    return pltpu.CompilerParams(
        vmem_limit_bytes=mib * 1024 * 1024, dimension_semantics=semantics or None
    )


def cost(flops, nbytes, trans=0):
    return pl.CostEstimate(
        flops=int(flops / 8), bytes_accessed=int(nbytes / 8), transcendentals=int(trans / 8)
    )


def whole(shape):
    return pl.BlockSpec(shape, lambda *_: (0,) * len(shape))


def rope_tables(positions, width):
    half = HEAD_DIM // 2
    exponent = jnp.arange(half, dtype=f32) * (-2.0 / HEAD_DIM)
    angles = positions.astype(f32)[:, None] * (rope_theta**exponent)[None, :]
    cosine, sine = jnp.cos(angles), jnp.sin(angles)
    copies = width // HEAD_DIM
    cos_row = jnp.concatenate([cosine, cosine] * copies, axis=1)
    sin_row = jnp.concatenate([-sine, sine] * copies, axis=1)
    return cos_row, sin_row


def partner(values):
    width = values.shape[1]
    half = HEAD_DIM // 2
    lane = lax.broadcasted_iota(jnp.int32, values.shape, 1)
    ahead = pltpu.roll(values, width - half, 1)
    behind = pltpu.roll(values, half, 1)
    return jnp.where(lane % HEAD_DIM < half, ahead, behind)


def qkv_kernel(place_ref, x_ref, gain_ref, cos_ref, sin_ref, wq_ref, wk_ref, wv_ref, qkv_ref, low_ref):
    pair = 2 * HEAD_DIM
    x = x_ref[0].astype(f32)
    scale = lax.rsqrt(jnp.mean(x * x, axis=-1, keepdims=True) + norm_eps)
    low = (x * scale * gain_ref[...]).astype(bf16)
    low_ref[0] = low
    cosine, sine = cos_ref[...], sin_ref[...]
    q = dot(low, wq_ref[...])
    q = (q * cosine + partner(q) * sine) * attention_scale
    qkv_ref[0, :, :pair] = q.astype(bf16)
    k = dot(low, wk_ref[...])
    v = dot(low, wv_ref[...])
    second = place_ref[0] % 2
    k = k * cosine + partner(k) * sine
    k = jnp.where(second == 0, k, pltpu.roll(k, HEAD_DIM, 1))
    v = jnp.where(second == 0, pltpu.roll(v, HEAD_DIM, 1), v)
    lane = lax.broadcasted_iota(jnp.int32, k.shape, 1)
    qkv_ref[0, :, pair:] = jnp.where(lane < HEAD_DIM, k, v).astype(bf16)


def qkv_call(group, x_all, gain, cos_all, sin_all, wq, wk, wv):
    blocks, rows, features = x_all.shape
    pair = 2 * HEAD_DIM
    return pl.pallas_call(
        qkv_kernel,
        grid_spec=pltpu.PrefetchScalarGridSpec(
            num_scalar_prefetch=1,
            grid=(blocks,),
            in_specs=[
                pl.BlockSpec((1, rows, features), lambda s, place: (s, 0, 0)),
                pl.BlockSpec((1, features), lambda s, place: (0, 0)),
                pl.BlockSpec((rows, pair), lambda s, place: (s, 0)),
                pl.BlockSpec((rows, pair), lambda s, place: (s, 0)),
                pl.BlockSpec((features, pair), lambda s, place: (0, place[0])),
                pl.BlockSpec((features, pair), lambda s, place: (0, place[0] // 2)),
                pl.BlockSpec((features, pair), lambda s, place: (0, place[0] // 2)),
            ],
            out_specs=[
                pl.BlockSpec((1, rows, 2 * pair), lambda s, place: (s, 0, 0)),
                pl.BlockSpec((1, rows, features), lambda s, place: (s, 0, 0)),
            ],
        ),
        out_shape=[
            jax.ShapeDtypeStruct((blocks, rows, 2 * pair), bf16),
            jax.ShapeDtypeStruct((blocks, rows, features), bf16),
        ],
        compiler_params=params(58, "arbitrary"),
        cost_estimate=cost(6 * blocks * rows * features * pair, 14e6),
        name="norm_qkv_rope",
    )(group, x_all, gain, cos_all, sin_all, wq, wk, wv)


def split_heads(block, first):
    wide = block.astype(f32)
    lane = lax.broadcasted_iota(jnp.int32, wide.shape, 1)
    turned = pltpu.roll(wide, HEAD_DIM, 1)
    if first:
        parts = [jnp.where(lane < HEAD_DIM, wide, 0.0), jnp.where(lane < HEAD_DIM, turned, 0.0)]
    else:
        parts = [jnp.where(lane >= HEAD_DIM, turned, 0.0), jnp.where(lane >= HEAD_DIM, wide, 0.0)]
    return jnp.concatenate(parts, axis=0).astype(bf16)


def join_heads(turned):
    rows = turned.shape[1] // 2
    return jnp.transpose(jnp.concatenate([turned[:, :rows], turned[:, rows:]], axis=0))


def scores_of(kv, q2, rows):
    scores = dot_nt(kv, q2)
    count = scores.shape[0]
    own = scores[count - rows :]
    key_at = lax.broadcasted_iota(jnp.int32, own.shape, 0)
    query_at = lax.broadcasted_iota(jnp.int32, own.shape, 1) % rows
    own = jnp.where(key_at <= query_at, own, masked_score)
    if count == rows:
        return own
    return jnp.concatenate([scores[: count - rows], own], axis=0)


def attend_kernel(qkv_ref, out_ref):
    blocks, _, rows, width = qkv_ref.shape
    pair = width // 2
    kv = qkv_ref[:, 0, :, pair:].reshape(blocks * rows, pair)
    kv_t = jnp.transpose(kv)
    for at in range(blocks):
        count = (at + 1) * rows
        q2 = split_heads(qkv_ref[at, 0, :, :pair], True)
        scores = scores_of(kv[:count], q2, rows)
        top = jnp.max(scores, axis=0, keepdims=True)
        weights = jnp.exp(scores - top)
        total = jnp.sum(weights, axis=0, keepdims=True)
        out_t = dot(kv_t[:, :count], weights.astype(bf16))
        out_ref[at, 0] = join_heads(out_t[HEAD_DIM:] / total).astype(bf16)


def attend_call(qkv):
    blocks, micro, rows, width = qkv.shape
    pair = width // 2
    length = blocks * rows
    return pl.pallas_call(
        attend_kernel,
        grid=(micro,),
        in_specs=[pl.BlockSpec((blocks, 1, rows, width), lambda m: (0, m, 0, 0))],
        out_specs=pl.BlockSpec((blocks, 1, rows, pair), lambda m: (0, m, 0, 0)),
        out_shape=jax.ShapeDtypeStruct((blocks, micro, rows, pair), bf16),
        compiler_params=params(48, "arbitrary"),
        cost_estimate=cost(
            micro * length * length * 512, 3 * qkv.size, micro * length * length
        ),
        name="attention_forward",
    )(qkv)


def attend_back_kernel(qkv_ref, grad_ref, cos_ref, sin_ref, out_ref, dkv_ref):
    blocks, _, rows, width = qkv_ref.shape
    pair = width // 2
    kv = qkv_ref[:, 0, :, pair:].reshape(blocks * rows, pair)
    kv_t = jnp.transpose(kv)
    dkv_ref[...] = jnp.zeros_like(dkv_ref)
    for at in range(blocks):
        count = (at + 1) * rows
        q2 = split_heads(qkv_ref[at, 0, :, :pair], True)
        g2 = split_heads(grad_ref[at, 0], False)
        scores = scores_of(kv[:count], q2, rows)
        top = jnp.max(scores, axis=0, keepdims=True)
        weights = jnp.exp(scores - top)
        total = jnp.sum(weights, axis=0, keepdims=True)
        prob = weights * (1.0 / total)
        prob_grad = dot_nt(kv[:count], g2)
        delta = jnp.sum(prob * prob_grad, axis=0, keepdims=True)
        score_grad = (prob * (prob_grad - delta)).astype(bf16)
        dkv_ref[:count] += dot(score_grad, q2) + dot(prob.astype(bf16), g2)
        dq_t = dot(kv_t[:, :count], score_grad)
        dq = join_heads(dq_t[:HEAD_DIM] * attention_scale)
        dq = dq * cos_ref[at, 0] - partner(dq) * sin_ref[at, 0]
        out_ref[at, 0, :, :pair] = dq.astype(bf16)
    for at in range(blocks):
        dkv = dkv_ref[at * rows : (at + 1) * rows]
        lane = lax.broadcasted_iota(jnp.int32, dkv.shape, 1)
        turned = dkv * cos_ref[at, 0] - partner(dkv) * sin_ref[at, 0]
        out_ref[at, 0, :, pair:] = jnp.where(lane < HEAD_DIM, turned, dkv).astype(bf16)


def attend_back_call(qkv, grads, cos_all, sin_all):
    blocks, micro, rows, width = qkv.shape
    pair = width // 2
    length = blocks * rows
    spec = lambda lanes: pl.BlockSpec((blocks, 1, rows, lanes), lambda m: (0, m, 0, 0))
    return pl.pallas_call(
        attend_back_kernel,
        grid=(micro,),
        in_specs=[spec(width), spec(pair), spec(pair), spec(pair)],
        out_specs=spec(width),
        out_shape=jax.ShapeDtypeStruct(qkv.shape, bf16),
        scratch_shapes=[pltpu.VMEM((length, pair), f32)],
        compiler_params=params(56, "arbitrary"),
        cost_estimate=cost(
            micro * length * length * 1280, 10 * qkv.size, micro * length * length
        ),
        name="attention_backward",
    )(qkv, grads, cos_all, sin_all)


def post_kernel(mix_ref, wo_ref, x_ref, gain_ref, mixed_ref, middle_ref, low_ref):
    mixed = jnp.concatenate([mix_ref[g] for g in range(mix_ref.shape[0])], axis=1)
    mixed_ref[...] = mixed
    middle = x_ref[...].astype(f32) + residual_scale * dot(mixed, wo_ref[...])
    middle_ref[...] = middle
    scale = lax.rsqrt(jnp.mean(middle * middle, axis=-1, keepdims=True) + norm_eps)
    low_ref[...] = (middle * scale * gain_ref[...]).astype(bf16)


def post_call(mix, wo, x, gain):
    rows, features = x.shape
    return pl.pallas_call(
        post_kernel,
        out_shape=[
            jax.ShapeDtypeStruct((rows, wo.shape[0]), bf16),
            jax.ShapeDtypeStruct((rows, features), f32),
            jax.ShapeDtypeStruct((rows, features), bf16),
        ],
        compiler_params=params(32),
        cost_estimate=cost(2 * rows * wo.size, 5e6),
        name="project_norm",
    )(mix, wo, x, gain)


def expert_kernel(place_ref, a_ref, b_ref, cot_ref, w_ref, wg_ref, wu_ref, wd_ref, *refs):
    dx_ref, x_ref, ha_ref, hb_ref, dg_ref, du_ref, sa_ref, sb_ref = refs[-8:]
    step = pl.program_id(0)
    first, second = place_ref[2], place_ref[3]
    half = sa_ref.shape[2]

    @pl.when(step == 0)
    def _():
        x_ref[...] = a_ref[...]

    @pl.when(step == 1)
    def _():
        x_ref[...] = b_ref[...]

    x = x_ref[...]
    cot = residual_scale * cot_ref[0].astype(f32)
    weight = w_ref[...]
    total = None
    for e in range(wg_ref.shape[0]):
        gate = dot(x, wg_ref[e])
        up = dot(x, wu_ref[e])
        slot_grad = (weight[:, e : e + 1] * cot).astype(bf16)
        to_a, to_b = jnp.bitwise_xor(first, e), jnp.bitwise_xor(second, e)
        sa_ref[to_a] = slot_grad[:, :half]
        sb_ref[to_b] = slot_grad[:, half:]
        hidden_grad = dot_nt(slot_grad, wd_ref[e])
        sig = 1.0 / (1.0 + jnp.exp(-gate))
        silu = gate * sig
        hidden = (silu * up).astype(bf16)
        ha_ref[to_a] = hidden
        hb_ref[to_b] = hidden
        gate_grad = (hidden_grad * up * (sig * (1.0 + gate * (1.0 - sig)))).astype(bf16)
        up_grad = (hidden_grad * silu).astype(bf16)
        dg_ref[to_a] = gate_grad
        du_ref[to_b] = up_grad
        term = dot_nt(gate_grad, wg_ref[e]) + dot_nt(up_grad, wu_ref[e])
        total = term if total is None else total + term
    dx_ref[0] = total.astype(bf16)


def expert_call(at, place, own, other, cot_all, weight, wg, wu, wd, kept):
    blocks, rows, features = cot_all.shape
    count, _, hidden = wg.shape
    tokens = blocks * rows
    inner = jax.ShapeDtypeStruct((count, tokens, hidden), bf16)
    outer = jax.ShapeDtypeStruct((count, tokens, features // 2), bf16)
    inner_spec = pl.BlockSpec((count, rows, hidden), lambda s, place: (0, 2 * at + s, 0))
    outer_spec = pl.BlockSpec((count, rows, features // 2), lambda s, place: (0, 2 * at + s, 0))
    fixed = lambda shape: pl.BlockSpec(shape, lambda s, place: (0,) * len(shape))
    any_spec = pl.BlockSpec(memory_space=pl.ANY)
    first = 8
    return pl.pallas_call(
        expert_kernel,
        grid_spec=pltpu.PrefetchScalarGridSpec(
            num_scalar_prefetch=1,
            grid=(2,),
            in_specs=[
                fixed((rows, features)),
                fixed((rows, features)),
                pl.BlockSpec((1, rows, features), lambda s, place: (place[s], 0, 0)),
                pl.BlockSpec((rows, count), lambda s, place: (place[s], 0)),
                fixed(wg.shape),
                fixed(wu.shape),
                fixed(wd.shape),
            ]
            + [any_spec] * len(kept),
            out_specs=[
                pl.BlockSpec((1, rows, features), lambda s, place: (s, 0, 0)),
                pl.BlockSpec((rows, features), lambda s, place: (2 * at + s, 0)),
            ]
            + [inner_spec] * 4
            + [outer_spec] * 2,
        ),
        out_shape=[
            jax.ShapeDtypeStruct((2, rows, features), bf16),
            jax.ShapeDtypeStruct((tokens, features), bf16),
            inner,
            inner,
            inner,
            inner,
            outer,
            outer,
        ],
        input_output_aliases={first + i: 1 + i for i in range(len(kept))},
        compiler_params=params(48, "arbitrary"),
        cost_estimate=cost(20 * rows * wg.size, 2e7, 2 * rows * hidden * count),
        name="experts",
    )(place, own, other, cot_all, weight, wg, wu, wd, *kept)


def expert_out_kernel(at_ref, a_ref, b_ref, gate_ref, up_ref, down_ref):
    rows = gate_ref.shape[1]
    half = down_ref.shape[2] // 2
    gate_ref[0] = a_ref[:rows].astype(f32)
    up_ref[0] = b_ref[:rows].astype(f32)
    down_ref[0, :, :half] = a_ref[rows:].astype(f32)
    down_ref[0, :, half:] = b_ref[rows:].astype(f32)


def expert_out_call(at, a, b, gate_shape, down_shape):
    parts, held, width = a.shape
    count = gate_shape[0]
    per = parts // count
    gate_rows, down_rows = gate_shape[1] // per, down_shape[1] // per
    taken = lambda which: pl.BlockSpec(
        (None, held, width), lambda r, at: (jnp.bitwise_xor(r, at[which]), 0, 0)
    )
    place = lambda r, at: (lax.div(r, per), lax.rem(r, per), 0)
    return pl.pallas_call(
        expert_out_kernel,
        grid_spec=pltpu.PrefetchScalarGridSpec(
            num_scalar_prefetch=1,
            grid=(parts,),
            in_specs=[taken(0), taken(1)],
            out_specs=[
                pl.BlockSpec((1, gate_rows, gate_shape[2]), place),
                pl.BlockSpec((1, gate_rows, gate_shape[2]), place),
                pl.BlockSpec((1, down_rows, down_shape[2]), place),
            ],
        ),
        out_shape=[
            jax.ShapeDtypeStruct(gate_shape, f32),
            jax.ShapeDtypeStruct(gate_shape, f32),
            jax.ShapeDtypeStruct(down_shape, f32),
        ],
        compiler_params=params(40, "arbitrary"),
        cost_estimate=cost(0, 2e7),
        name="expert_weights_out",
    )(at, a, b)


def moe_kernel(place_ref, h_ref, w_ref, wd_ref, out_ref):
    weight = w_ref[...]
    total = None
    first = place_ref[pl.num_programs(0)]
    for e in range(wd_ref.shape[0]):
        term = weight[:, e : e + 1] * dot(h_ref[jnp.bitwise_xor(first, e)], wd_ref[e])
        total = term if total is None else total + term
    out_ref[0] = total.astype(bf16)


def moe_call(place, hidden, weight, wd, blocks):
    count, tokens, inner = hidden.shape
    features = wd.shape[2]
    rows = tokens // blocks
    return pl.pallas_call(
        moe_kernel,
        grid_spec=pltpu.PrefetchScalarGridSpec(
            num_scalar_prefetch=1,
            grid=(blocks,),
            in_specs=[
                pl.BlockSpec((count, rows, inner), lambda s, place: (0, s, 0)),
                pl.BlockSpec((rows, count), lambda s, place: (place[s], 0)),
                pl.BlockSpec(wd.shape, lambda s, place: (0, 0, 0)),
            ],
            out_specs=pl.BlockSpec((1, rows, features), lambda s, place: (place[s], 0, 0)),
        ),
        out_shape=jax.ShapeDtypeStruct((blocks, rows, features), bf16),
        compiler_params=params(32, "arbitrary"),
        cost_estimate=cost(2 * tokens * wd.size, 1.1e7),
        name="expert_outputs",
    )(place, hidden, weight, wd)


def turn_kernel(sg_ref, middle_ref, gain_ref, cot_ref, wo_ref, mg_ref, proj_ref, dmid_ref, dgain_ref):
    grad = sg_ref[...].astype(f32)
    middle = middle_ref[...]
    scale = lax.rsqrt(jnp.mean(middle * middle, axis=-1, keepdims=True) + norm_eps)
    unit = middle * scale
    dgain_ref[...] = jnp.sum(grad * unit, axis=0, keepdims=True)
    w = gain_ref[...] * grad
    dmid = cot_ref[...].astype(f32) + scale * (w - unit * jnp.mean(w * unit, axis=-1, keepdims=True))
    dmid_ref[...] = dmid
    proj = (residual_scale * dmid).astype(bf16)
    proj_ref[...] = proj
    mixed_grad = dot_nt(proj, wo_ref[...]).astype(bf16)
    groups, _, pair = mg_ref.shape
    for g in range(groups):
        mg_ref[g] = mixed_grad[:, g * pair : (g + 1) * pair]


def turn_call(sg, middle, gain, cot, wo, groups):
    rows, features = middle.shape
    pair = wo.shape[0] // groups
    return pl.pallas_call(
        turn_kernel,
        out_shape=[
            jax.ShapeDtypeStruct((groups, rows, pair), bf16),
            jax.ShapeDtypeStruct((rows, features), bf16),
            jax.ShapeDtypeStruct((rows, features), f32),
            jax.ShapeDtypeStruct((1, features), f32),
        ],
        compiler_params=params(32),
        cost_estimate=cost(2 * rows * wo.size, 6e6),
        name="norm_back_project_back",
    )(sg, middle, gain, cot, wo)


def output_weight_kernel(mixed_ref, proj_ref, dgain_ref, out_ref):
    held, each, features = out_ref.shape
    rows = mixed_ref.shape[1] // held
    part = lax.dot_general(mixed_ref[...], proj_ref[...], TN, preferred_element_type=f32)
    extra = jnp.broadcast_to(dgain_ref[...], (each - rows, features)).astype(bf16)
    for at in range(held):
        out_ref[at, :rows] = part[at * rows : (at + 1) * rows].astype(bf16)
        out_ref[at, rows:] = extra


def output_weight_call(mixed, proj, dgain, parts):
    rows, width = mixed.shape
    features = proj.shape[1]
    each = width // parts
    lanes = max(each, 2 * HEAD_DIM)
    held = lanes // each
    return pl.pallas_call(
        output_weight_kernel,
        grid=(parts // held,),
        in_specs=[
            pl.BlockSpec((rows, lanes), lambda s: (0, s)),
            whole((rows, features)),
            whole((1, features)),
        ],
        out_specs=pl.BlockSpec((held, each + 16, features), lambda s: (s, 0, 0)),
        out_shape=jax.ShapeDtypeStruct((parts, each + 16, features), bf16),
        compiler_params=params(32, "arbitrary"),
        cost_estimate=cost(2 * rows * width * features, 4e6),
        name="output_weight_part",
    )(mixed, proj, dgain)


def dense_out_kernel(
    at_ref, own_ref, other_ref, wq_ref, wk_ref, wv_ref, gain_ref, dq_ref, dk_ref, dv_ref, dg_ref, wo_ref
):
    chips, _, width = own_ref.shape
    rows = dq_ref.shape[0]
    pair = width // 2
    chip, core = at_ref[2], at_ref[3]
    total = jnp.zeros((rows, pair), f32)
    for k in range(chips):
        source = lax.rem(chip - k + chips, chips)
        a = jnp.where(core == 0, own_ref[k], other_ref[k]).astype(f32)
        b = jnp.where(core == 0, other_ref[k], own_ref[k]).astype(f32)
        q = jnp.concatenate([a[:rows, :pair], b[:rows, :pair]], axis=1)
        cols = pl.ds(pl.multiple_of(source * width, width), width)
        dq_ref[:, cols] = q
        made = q * wq_ref[:, cols].astype(f32)
        total += made[:, :pair] + made[:, pair:]
        a_kv, b_kv = a[:rows, pair:], b[:rows, pair:]
        lane = lax.broadcasted_iota(jnp.int32, a_kv.shape, 1)
        key = jnp.where(lane < HEAD_DIM, a_kv, pltpu.roll(b_kv, HEAD_DIM, 1))
        val = jnp.where(lane < HEAD_DIM, pltpu.roll(a_kv, HEAD_DIM, 1), b_kv)
        cols = pl.ds(pl.multiple_of(source * pair, pair), pair)
        dk_ref[:, cols] = key
        dv_ref[:, cols] = val
        total += key * wk_ref[:, cols].astype(f32) + val * wv_ref[:, cols].astype(f32)
        wo_ref[2 * source, 0] = a[rows:]
        wo_ref[2 * source + 1, 0] = b[rows:]
    dg_ref[...] = jnp.sum(jnp.transpose(total), axis=0, keepdims=True) / gain_ref[...]


def dense_out_call(at, own, other, wq, wk, wv, gain, wo_shape):
    streams, parts, chips, held, width = own.shape
    features = wq.shape[0]
    groups = 2 * chips
    rows = features // (streams * parts)
    block_cols = wo_shape[1] // width
    per_block = streams * parts // block_cols
    wo_rows = wo_shape[0] // groups // per_block
    by_rows = lambda w: pl.BlockSpec((rows, w.shape[1]), lambda s, r, at: (s * parts + r, 0))
    taken = pl.BlockSpec(
        (None, None, chips, held, width), lambda s, r, at: (s, jnp.bitwise_xor(r, at[s]), 0, 0, 0)
    )
    gain_spec = pl.BlockSpec((1, rows), lambda s, r, at: (0, s * parts + r))
    outs = pl.pallas_call(
        dense_out_kernel,
        grid_spec=pltpu.PrefetchScalarGridSpec(
            num_scalar_prefetch=1,
            grid=(streams, parts),
            in_specs=[taken, taken, by_rows(wq), by_rows(wk), by_rows(wv), gain_spec],
            out_specs=[
                by_rows(wq),
                by_rows(wk),
                by_rows(wv),
                gain_spec,
                pl.BlockSpec(
                    (groups, 1, wo_rows, width),
                    lambda s, r, at: (
                        0,
                        lax.rem(s * parts + r, per_block),
                        0,
                        lax.div(s * parts + r, per_block),
                    ),
                ),
            ],
        ),
        out_shape=[
            jax.ShapeDtypeStruct(wq.shape, f32),
            jax.ShapeDtypeStruct(wk.shape, f32),
            jax.ShapeDtypeStruct(wv.shape, f32),
            jax.ShapeDtypeStruct((1, features), f32),
            jax.ShapeDtypeStruct((groups, per_block, wo_rows, wo_shape[1]), f32),
        ],
        compiler_params=params(48, "arbitrary", "arbitrary"),
        cost_estimate=cost(2 * wq.size, 2.4e7),
        name="dense_weights_out",
    )(at, own, other, wq, wk, wv, gain)
    return (*outs[:4], outs[4].reshape(wo_shape))


def weights_out_kernel(wide_ref, wq_ref, wk_ref, wv_ref, gain_ref, dq_ref, dk_ref, dv_ref, dg_ref):
    groups, rows, width = wide_ref.shape
    pair = width // 2
    total = jnp.zeros((rows, pair), f32)
    for g in range(groups):
        part = wide_ref[g, :, :pair].astype(f32)
        at = slice(g * pair, (g + 1) * pair)
        dq_ref[:, at] = part
        total += part * wq_ref[:, at].astype(f32)
    for g in range(groups // 2):
        a = wide_ref[2 * g, :, pair:].astype(f32)
        b = wide_ref[2 * g + 1, :, pair:].astype(f32)
        lane = lax.broadcasted_iota(jnp.int32, a.shape, 1)
        at = slice(g * pair, (g + 1) * pair)
        k = jnp.where(lane < HEAD_DIM, a, pltpu.roll(b, HEAD_DIM, 1))
        v = jnp.where(lane < HEAD_DIM, pltpu.roll(a, HEAD_DIM, 1), b)
        dk_ref[:, at] = k
        dv_ref[:, at] = v
        total += k * wk_ref[:, at].astype(f32) + v * wv_ref[:, at].astype(f32)
    dg_ref[...] = jnp.sum(jnp.transpose(total), axis=0, keepdims=True) / gain_ref[...]


def weights_out_call(wide, wq, wk, wv, gain):
    chunks, groups, rows, width = wide.shape
    features = chunks * rows
    by_rows = lambda w: pl.BlockSpec((rows, w.shape[1]), lambda c: (c, 0))
    return pl.pallas_call(
        weights_out_kernel,
        grid=(chunks,),
        in_specs=[
            pl.BlockSpec((None, groups, rows, width), lambda c: (c, 0, 0, 0)),
            by_rows(wq),
            by_rows(wk),
            by_rows(wv),
            pl.BlockSpec((1, rows), lambda c: (0, c)),
        ],
        out_specs=[
            by_rows(wq),
            by_rows(wk),
            by_rows(wv),
            pl.BlockSpec((1, rows), lambda c: (0, c)),
        ],
        out_shape=[
            jax.ShapeDtypeStruct(wq.shape, f32),
            jax.ShapeDtypeStruct(wk.shape, f32),
            jax.ShapeDtypeStruct(wv.shape, f32),
            jax.ShapeDtypeStruct((1, features), f32),
        ],
        compiler_params=params(32, "arbitrary"),
        cost_estimate=cost(2 * wq.size, 1.6e7),
        name="attention_weights_out",
    )(wide, wq, wk, wv, gain)


def last_kernel(d_ref, wq_ref, wk_ref, wv_ref, x_ref, gain_ref, dmid_ref, out_ref):
    groups, rows, width = d_ref.shape
    pair = width // 2
    dq = jnp.concatenate([d_ref[g, :, :pair] for g in range(groups)], axis=1)
    grad = dot_nt(dq, wq_ref[...])
    keys, vals = [], []
    for at in range(groups // 2):
        a = d_ref[2 * at, :, pair:].astype(f32)
        b = d_ref[2 * at + 1, :, pair:].astype(f32)
        lane = lax.broadcasted_iota(jnp.int32, a.shape, 1)
        keys.append(jnp.where(lane < HEAD_DIM, a, pltpu.roll(b, HEAD_DIM, 1)).astype(bf16))
        vals.append(jnp.where(lane < HEAD_DIM, pltpu.roll(a, HEAD_DIM, 1), b).astype(bf16))
    grad = grad + dot_nt(jnp.concatenate(keys, axis=1), wk_ref[...])
    grad = grad + dot_nt(jnp.concatenate(vals, axis=1), wv_ref[...])
    x = x_ref[...].astype(f32)
    scale = lax.rsqrt(jnp.mean(x * x, axis=-1, keepdims=True) + norm_eps)
    unit = x * scale
    w = gain_ref[...] * grad
    out_ref[...] = dmid_ref[...] + scale * (w - unit * jnp.mean(w * unit, axis=-1, keepdims=True))


def last_call(d, wq, wk, wv, x, gain, dmid):
    rows, features = x.shape
    return pl.pallas_call(
        last_kernel,
        out_shape=jax.ShapeDtypeStruct((rows, features), f32),
        compiler_params=params(40),
        cost_estimate=cost(4 * rows * features * features, 8e6),
        name="input_gradient",
    )(d, wq, wk, wv, x, gain, dmid)


def swap(values, axis, bit):
    return lax.ppermute(values, axis, [(i, i ^ bit) for i in range(lax.axis_size(axis))])


def half_sum(values, axis, bit):
    half = values.shape[0] // 2
    upper = ((lax.axis_index(axis) & bit) > 0).astype(jnp.int32)
    came = swap(lax.dynamic_slice_in_dim(values, (1 - upper) * half, half), axis, bit)
    mine = lax.dynamic_slice_in_dim(values, upper * half, half)
    return (mine.astype(f32) + came.astype(f32)).astype(bf16)


def join_parts(stream, axis, bits):
    shape = stream.shape
    for bit in bits[::-1]:
        stream = jnp.stack([stream, swap(stream, axis, bit)])
    return stream.reshape(-1, *shape)


def body(
    layer_input,
    first_gain,
    query_weight,
    key_weight,
    value_weight,
    output_weight,
    second_gain,
    gate_weight,
    up_weight,
    down_weight,
    expert_ids,
    gate_values,
    positions,
    cotangent,
):
    micro, _, per_device, features = layer_input.shape
    devices = lax.axis_size("seq")
    replicas = lax.axis_size("dp")
    seq_place = lax.axis_index("seq")
    rows = micro * per_device
    local_experts = gate_weight.shape[0]
    groups = key_weight.shape[1] // HEAD_DIM
    pair = query_weight.shape[1] // groups
    copies = devices // groups

    dp_bits = [1 << i for i in range(replicas.bit_length() - 1)]

    def spread(blocks):
        if copies > 1:
            blocks = jnp.repeat(blocks, copies, axis=0)
        return lax.all_to_all(blocks, "seq", 0, 0, tiled=True)

    def unspread(blocks):
        return lax.all_to_all(blocks, "seq", 0, 0, tiled=True)[::copies]

    x = layer_input.reshape(rows, features)
    cot = cotangent.reshape(rows, features)
    gain_one = first_gain.reshape(1, features)
    gain_two = second_gain.reshape(1, features)
    pos_all = lax.all_to_all(
        jnp.broadcast_to(positions.reshape(1, rows), (devices, rows)), "seq", 0, 0, tiled=True
    )
    x_all = lax.all_gather(x, "seq", axis=0)
    cos_all, sin_all = rope_tables(pos_all.reshape(-1), pair)
    mine = seq_place * local_experts + jnp.arange(local_experts, dtype=jnp.int32)
    ids = expert_ids[:, 0]
    gates = gate_values[:, 0].astype(f32)
    routed = jnp.sum(
        jnp.where(ids[..., None] == mine, gates[..., None], 0.0), axis=2
    )
    routed = routed.reshape(micro, devices, per_device, local_experts)
    routed = jnp.transpose(routed, (1, 0, 2, 3)).reshape(devices * rows, local_experts)
    cos_all, sin_all, routed = lax.optimization_barrier((cos_all, sin_all, routed))
    x_all, cot_then, cos_all, sin_all, routed = lax.optimization_barrier(
        (x_all, cot, cos_all, sin_all, routed)
    )
    cot_all = lax.all_gather(cot_then, "seq", axis=0)

    group = (seq_place // copies).astype(jnp.int32).reshape(1)
    qkv, first_all = qkv_call(
        group, x_all, gain_one, cos_all, sin_all, query_weight, key_weight, value_weight
    )
    qkv = qkv.reshape(devices, micro, per_device, 2 * pair)
    mix = attend_call(qkv)
    mix = unspread(mix.reshape(devices, rows, pair))
    mixed, middle, second_low = post_call(mix, output_weight, x, gain_two)

    chips = devices // 2
    chip, core = seq_place // 2, seq_place % 2
    onward = [(i, (i + 2) % devices) for i in range(devices)]
    dp_place = lax.axis_index("dp")
    first_bit = dp_place & 1
    last_bit = dp_place >> (len(dp_bits) - 1)
    held, kept, running, places = second_low, (), None, []
    for hop in range(chips):
        following = lax.ppermute(held, "seq", onward) if hop < chips - 1 else None
        other = swap(held, "seq", 1)
        source = 2 * ((chip - hop) % chips)
        place = jnp.stack([source + core, source + 1 - core, 1 - first_bit, 1 - last_bit])
        place = place.astype(jnp.int32)
        places.append(place[:2])
        dx, *kept = expert_call(
            hop, place, held, other, cot_all, routed, gate_weight, up_weight, down_weight, kept
        )
        if following is not None:
            following, dx = lax.optimization_barrier((following, dx))
        part = dx[0].astype(f32) + swap(dx[1], "seq", 1).astype(f32)
        if hop == 0:
            own_part = part
        else:
            if running is not None:
                part = part + running.astype(f32)
            part = part.astype(bf16)
            if following is not None:
                part, following = lax.optimization_barrier((part, following))
            else:
                part, kept = lax.optimization_barrier((part, kept))
            running = lax.ppermute(part, "seq", onward)
        held = following
    second_grad = (own_part + running.astype(f32)).astype(bf16)
    tokens, hidden_a, hidden_b, gate_low, up_low, slot_a, slot_b = kept

    def weight_parts(at, tokens, hidden_a, hidden_b, gate_low, up_low, slot_a, slot_b):
        pairs = (
            (tokens, gate_low[at]),
            (tokens, up_low[at]),
            (hidden_a[at], slot_a[at]),
            (hidden_b[at], slot_b[at]),
        )
        return [
            lax.dot_general(a, b, TN, preferred_element_type=f32).astype(bf16) for a, b in pairs
        ]

    leaving = weight_parts(0, *kept)
    leaving, second_grad = lax.optimization_barrier((leaving, second_grad))
    part_bits = (dp_bits[0], dp_bits[-1], dp_bits[0], dp_bits[-1])
    came = [swap(values, "dp", bit) for values, bit in zip(leaving, part_bits)]

    mg_send, proj, middle_grad, gain_two_part = turn_call(
        second_grad, middle, gain_two, cot, output_weight, groups
    )
    mg = spread(mg_send)
    mixed, kept, proj, _ = lax.optimization_barrier((mixed, kept, proj, mg_send))
    staying = weight_parts(1, *kept)
    moe_place = jnp.concatenate(places + [(1 - first_bit).astype(jnp.int32).reshape(1)])
    moe_all = moe_call(moe_place, kept[1], routed, down_weight, devices)
    dense = output_weight_call(mixed, proj, gain_two_part, devices)
    mg, dense, moe_all, came, staying = lax.optimization_barrier(
        (mg, dense, moe_all, came, staying)
    )
    summed = [
        (a.astype(f32) + b.astype(f32)).astype(bf16).reshape(replicas // 2, -1, b.shape[-1])
        for a, b in zip(came, staying)
    ]
    streams = [
        jnp.concatenate([summed[0], summed[2]], axis=1),
        jnp.concatenate([summed[1], summed[3]], axis=1),
    ]
    stream_bits = (dp_bits, dp_bits[::-1])
    for at in range(1, len(dp_bits)):
        streams = [half_sum(v, "dp", bits[at]) for v, bits in zip(streams, stream_bits)]
    dense = lax.psum_scatter(dense, "seq", scatter_dimension=0)
    moe_all, _ = lax.optimization_barrier((moe_all, mg))
    moe = lax.psum_scatter(moe_all, "seq", scatter_dimension=0)
    layer_output = (middle + residual_scale * moe.astype(f32)).astype(bf16)
    table_shape = (devices, micro, per_device, pair)
    dqkv = attend_back_call(
        qkv,
        mg.reshape(devices, micro, per_device, pair),
        cos_all.reshape(table_shape),
        sin_all.reshape(table_shape),
    )
    dqkv, streams = lax.optimization_barrier((dqkv, streams))
    turned = sum(((dp_place >> i) & 1) << (len(dp_bits) - 1 - i) for i in range(len(dp_bits)))
    part_at = jnp.stack([turned, dp_place]).astype(jnp.int32)
    expert_parts = [
        join_parts(v[0], "dp", bits[-1:]) for v, bits in zip(streams, stream_bits)
    ]
    d_all = dqkv.reshape(devices * rows, 2 * pair)
    first_tokens = first_all.reshape(devices * rows, features)
    part = lax.dot_general(first_tokens, d_all, TN, preferred_element_type=f32).astype(bf16)
    back = unspread(dqkv.reshape(devices, rows, 2 * pair))
    dense = dense.reshape(dense.shape[-2], features)
    each = output_weight.shape[0] // devices
    gain_row, dense = dense[each:], dense[:each]
    for bit in dp_bits:
        gain_row = (gain_row.astype(f32) + swap(gain_row, "dp", bit).astype(f32)).astype(bf16)
    second_gain_grad = gain_row[0].astype(f32)
    if copies == 1:
        pieces_all = 2 * replicas
        width = 2 * pair
        per_block = pieces_all * width // features
        dense = dense.reshape(per_block, each // per_block, features // width, width)
        dense = jnp.transpose(dense, (2, 0, 1, 3)).reshape(pieces_all, each // per_block, width)
        joint = jnp.concatenate([part.reshape(pieces_all, -1, width), dense], axis=1)
        depth = joint.shape[1]
        streams = []
        for at, bits in enumerate(stream_bits):
            stream = joint[at * replicas : (at + 1) * replicas].reshape(replicas * depth, width)
            for bit in bits:
                stream = half_sum(stream, "dp", bit)
            streams.append(stream)
        own = jnp.stack(streams)
        backward = [(i, (i - 2) % devices) for i in range(devices)]
        round_ring = {0: own}
        for k in range(1, chips // 2 + 1):
            round_ring[k] = lax.ppermute(round_ring[k - 1], "seq", onward)
            if chips - k > k:
                round_ring[chips - k] = lax.ppermute(
                    round_ring[(chips - k + 1) % chips], "seq", backward
                )
        held = jnp.stack([round_ring[k] for k in range(chips)])
        held, expert_parts = lax.optimization_barrier((held, expert_parts))
        full = [join_parts(held[:, at], "dp", b[-1:]) for at, b in enumerate(stream_bits)]
        full, expert_parts = lax.optimization_barrier((full, expert_parts))
        full = [
            join_parts(v, "dp", b[:-1]).reshape(-1, *held[:, 0].shape)
            for v, b in zip(full, stream_bits)
        ]
        full, back = lax.optimization_barrier((jnp.stack(full), back))
        other = swap(full, "seq", 1)
        where_at = jnp.stack([turned, dp_place, chip, core]).astype(jnp.int32)
        (
            query_weight_grad,
            key_weight_grad,
            value_weight_grad,
            first_gain_grad,
            output_weight_grad,
        ) = dense_out_call(
            where_at, full, other, query_weight, key_weight, value_weight, gain_one, output_weight.shape
        )
    else:
        for bit in dp_bits:
            dense = (dense.astype(f32) + swap(dense, "dp", bit).astype(f32)).astype(bf16)
        dense = lax.all_gather(dense, "seq", axis=0).astype(f32)
        output_weight_grad = dense.reshape(output_weight.shape)
        for bit in dp_bits[::-1]:
            part = half_sum(part, "dp", bit)
        wide = lax.all_gather(part, ("dp", "seq"), axis=0)
        wide = wide.reshape(replicas, devices, features // replicas, 2 * pair)[:, ::copies]
        query_weight_grad, key_weight_grad, value_weight_grad, first_gain_grad = weights_out_call(
            wide, query_weight, key_weight, value_weight, gain_one
        )

    expert_parts = [
        join_parts(v, "dp", bits[:-1]).reshape(-1, *v.shape[-2:])
        for v, bits in zip(expert_parts, stream_bits)
    ]
    gate_sum, up_sum, down_sum = expert_out_call(
        part_at, *expert_parts, gate_weight.shape, down_weight.shape
    )
    input_grad = last_call(
        back, query_weight, key_weight, value_weight, x, gain_one, middle_grad
    )
    return (
        layer_output.reshape(layer_input.shape),
        input_grad.reshape(layer_input.shape),
        first_gain_grad.reshape(features),
        query_weight_grad,
        key_weight_grad,
        value_weight_grad,
        output_weight_grad,
        second_gain_grad,
        gate_sum,
        up_sum,
        down_sum,
    )


def solution(mesh):
    return jax.shard_map(
        body,
        mesh=mesh,
        in_specs=(
            P(None, "dp", "seq", None),
            P(),
            P(),
            P(),
            P(),
            P(),
            P(),
            P("seq", None, None),
            P("seq", None, None),
            P("seq", None, None),
            P(None, "dp", None, None),
            P(None, "dp", None, None),
            P(None, "dp", "seq"),
            P(None, "dp", "seq", None),
        ),
        out_specs=(
            P(None, "dp", "seq", None),
            P(None, "dp", "seq", None),
            P(),
            P(),
            P(),
            P(),
            P(),
            P(),
            P("seq", None, None),
            P("seq", None, None),
            P("seq", None, None),
        ),
        check_vma=False,
    )
```

```python
from functools import partial

import jax
import jax.numpy as jnp
from jax import lax
from jax.experimental import pallas as pl
from jax.experimental.pallas import tpu as pltpu
from jax.sharding import PartitionSpec as P

HEAD_DIM = 64

rope_theta = 10000.0
attention_scale = 0.015625
residual_scale = 0.22
norm_eps = 1e-06
masked_score = -1e30

f32 = jnp.float32
bf16 = jnp.bfloat16
NT = (((1,), (1,)), ((), ()))
TN = (((0,), (0,)), ((), ()))


def dot(a, b):
    return jnp.dot(a, b, preferred_element_type=f32)


def dot_nt(a, b):
    return lax.dot_general(a, b, NT, preferred_element_type=f32)


def params(mib, *semantics):
    return pltpu.CompilerParams(
        vmem_limit_bytes=mib * 1024 * 1024, dimension_semantics=semantics or None
    )


def cost(flops, nbytes, trans=0):
    return pl.CostEstimate(
        flops=int(flops / 8), bytes_accessed=int(nbytes / 8), transcendentals=int(trans / 8)
    )


def whole(shape):
    return pl.BlockSpec(shape, lambda *_: (0,) * len(shape))


def rope_tables(positions, width):
    half = HEAD_DIM // 2
    exponent = jnp.arange(half, dtype=f32) * (-2.0 / HEAD_DIM)
    angles = positions.astype(f32)[:, None] * (rope_theta**exponent)[None, :]
    cosine, sine = jnp.cos(angles), jnp.sin(angles)
    copies = width // HEAD_DIM
    cos_row = jnp.concatenate([cosine, cosine] * copies, axis=1)
    sin_row = jnp.concatenate([-sine, sine] * copies, axis=1)
    return cos_row, sin_row


def partner(values):
    width = values.shape[1]
    half = HEAD_DIM // 2
    lane = lax.broadcasted_iota(jnp.int32, values.shape, 1)
    ahead = pltpu.roll(values, width - half, 1)
    behind = pltpu.roll(values, half, 1)
    return jnp.where(lane % HEAD_DIM < half, ahead, behind)


def qkv_kernel(x_ref, gain_ref, cos_ref, sin_ref, w_ref, qkv_ref, low_ref):
    pair = 2 * HEAD_DIM
    x = x_ref[0].astype(f32)
    scale = lax.rsqrt(jnp.mean(x * x, axis=-1, keepdims=True) + norm_eps)
    low = (x * scale * gain_ref[...]).astype(bf16)
    low_ref[0] = low
    cosine, sine = cos_ref[...], sin_ref[...]
    made = dot(low, w_ref[...])
    q, kv = made[:, :pair], made[:, pair:]
    q = (q * cosine + partner(q) * sine) * attention_scale
    qkv_ref[0, :, :pair] = q.astype(bf16)
    lane = lax.broadcasted_iota(jnp.int32, kv.shape, 1)
    turned = kv * cosine + partner(kv) * sine
    qkv_ref[0, :, pair:] = jnp.where(lane < HEAD_DIM, turned, kv).astype(bf16)


def qkv_call(x_all, gain, cos_all, sin_all, w_own):
    blocks, rows, features = x_all.shape
    pair = 2 * HEAD_DIM
    return pl.pallas_call(
        qkv_kernel,
        grid=(blocks,),
        in_specs=[
            pl.BlockSpec((1, rows, features), lambda s: (s, 0, 0)),
            whole((1, features)),
            pl.BlockSpec((rows, pair), lambda s: (s, 0)),
            pl.BlockSpec((rows, pair), lambda s: (s, 0)),
            whole(w_own.shape),
        ],
        out_specs=[
            pl.BlockSpec((1, rows, 2 * pair), lambda s: (s, 0, 0)),
            pl.BlockSpec((1, rows, features), lambda s: (s, 0, 0)),
        ],
        out_shape=[
            jax.ShapeDtypeStruct((blocks, rows, 2 * pair), bf16),
            jax.ShapeDtypeStruct((blocks, rows, features), bf16),
        ],
        compiler_params=params(58, "arbitrary"),
        cost_estimate=cost(4 * blocks * rows * features * pair, 14e6),
        name="norm_qkv_rope",
    )(x_all, gain, cos_all, sin_all, w_own)


def split_heads(block, first):
    wide = block.astype(f32)
    lane = lax.broadcasted_iota(jnp.int32, wide.shape, 1)
    turned = pltpu.roll(wide, HEAD_DIM, 1)
    if first:
        parts = [jnp.where(lane < HEAD_DIM, wide, 0.0), jnp.where(lane < HEAD_DIM, turned, 0.0)]
    else:
        parts = [jnp.where(lane >= HEAD_DIM, turned, 0.0), jnp.where(lane >= HEAD_DIM, wide, 0.0)]
    return jnp.concatenate(parts, axis=0).astype(bf16)


def join_heads(turned):
    rows = turned.shape[1] // 2
    return jnp.transpose(jnp.concatenate([turned[:, :rows], turned[:, rows:]], axis=0))


def scores_of(kv, q2, rows):
    scores = dot_nt(kv, q2)
    count = scores.shape[0]
    own = scores[count - rows :]
    key_at = lax.broadcasted_iota(jnp.int32, own.shape, 0)
    query_at = lax.broadcasted_iota(jnp.int32, own.shape, 1) % rows
    own = jnp.where(key_at <= query_at, own, masked_score)
    if count == rows:
        return own
    return jnp.concatenate([scores[: count - rows], own], axis=0)


def attend_kernel(qkv_ref, out_ref):
    blocks, _, rows, width = qkv_ref.shape
    pair = width // 2
    kv = qkv_ref[:, 0, :, pair:].reshape(blocks * rows, pair)
    kv_t = jnp.transpose(kv)
    for at in range(blocks):
        count = (at + 1) * rows
        q2 = split_heads(qkv_ref[at, 0, :, :pair], True)
        scores = scores_of(kv[:count], q2, rows)
        top = jnp.max(scores, axis=0, keepdims=True)
        weights = jnp.exp(scores - top)
        total = jnp.sum(weights, axis=0, keepdims=True)
        out_t = dot(kv_t[:, :count], weights.astype(bf16))
        out_ref[at, 0] = join_heads(out_t[HEAD_DIM:] / total).astype(bf16)


def attend_call(qkv):
    blocks, micro, rows, width = qkv.shape
    pair = width // 2
    length = blocks * rows
    return pl.pallas_call(
        attend_kernel,
        grid=(micro,),
        in_specs=[pl.BlockSpec((blocks, 1, rows, width), lambda m: (0, m, 0, 0))],
        out_specs=pl.BlockSpec((blocks, 1, rows, pair), lambda m: (0, m, 0, 0)),
        out_shape=jax.ShapeDtypeStruct((blocks, micro, rows, pair), bf16),
        compiler_params=params(48, "arbitrary"),
        cost_estimate=cost(
            micro * length * length * 512, 3 * qkv.size, micro * length * length
        ),
        name="attention_forward",
    )(qkv)


def attend_back_kernel(qkv_ref, grad_ref, cos_ref, sin_ref, out_ref, dkv_ref):
    blocks, _, rows, width = qkv_ref.shape
    pair = width // 2
    kv = qkv_ref[:, 0, :, pair:].reshape(blocks * rows, pair)
    kv_t = jnp.transpose(kv)
    dkv_ref[...] = jnp.zeros_like(dkv_ref)
    for at in range(blocks):
        count = (at + 1) * rows
        q2 = split_heads(qkv_ref[at, 0, :, :pair], True)
        g2 = split_heads(grad_ref[at, 0], False)
        scores = scores_of(kv[:count], q2, rows)
        top = jnp.max(scores, axis=0, keepdims=True)
        weights = jnp.exp(scores - top)
        total = jnp.sum(weights, axis=0, keepdims=True)
        prob = weights * (1.0 / total)
        prob_grad = dot_nt(kv[:count], g2)
        delta = jnp.sum(prob * prob_grad, axis=0, keepdims=True)
        score_grad = (prob * (prob_grad - delta)).astype(bf16)
        dkv_ref[:count] += dot(score_grad, q2) + dot(prob.astype(bf16), g2)
        dq_t = dot(kv_t[:, :count], score_grad)
        dq = join_heads(dq_t[:HEAD_DIM] * attention_scale)
        dq = dq * cos_ref[at, 0] - partner(dq) * sin_ref[at, 0]
        out_ref[at, 0, :, :pair] = dq.astype(bf16)
    for at in range(blocks):
        dkv = dkv_ref[at * rows : (at + 1) * rows]
        lane = lax.broadcasted_iota(jnp.int32, dkv.shape, 1)
        turned = dkv * cos_ref[at, 0] - partner(dkv) * sin_ref[at, 0]
        out_ref[at, 0, :, pair:] = jnp.where(lane < HEAD_DIM, turned, dkv).astype(bf16)


def attend_back_call(qkv, grads, cos_all, sin_all):
    blocks, micro, rows, width = qkv.shape
    pair = width // 2
    length = blocks * rows
    spec = lambda lanes: pl.BlockSpec((blocks, 1, rows, lanes), lambda m: (0, m, 0, 0))
    return pl.pallas_call(
        attend_back_kernel,
        grid=(micro,),
        in_specs=[spec(width), spec(pair), spec(pair), spec(pair)],
        out_specs=spec(width),
        out_shape=jax.ShapeDtypeStruct(qkv.shape, bf16),
        scratch_shapes=[pltpu.VMEM((length, pair), f32)],
        compiler_params=params(56, "arbitrary"),
        cost_estimate=cost(
            micro * length * length * 1280, 10 * qkv.size, micro * length * length
        ),
        name="attention_backward",
    )(qkv, grads, cos_all, sin_all)


def post_kernel(mix_ref, wo_ref, x_ref, gain_ref, mixed_ref, middle_ref, low_ref):
    mixed = jnp.concatenate([mix_ref[g] for g in range(mix_ref.shape[0])], axis=1)
    mixed_ref[...] = mixed
    middle = x_ref[...].astype(f32) + residual_scale * dot(mixed, wo_ref[...])
    middle_ref[...] = middle
    scale = lax.rsqrt(jnp.mean(middle * middle, axis=-1, keepdims=True) + norm_eps)
    low_ref[...] = (middle * scale * gain_ref[...]).astype(bf16)


def post_call(mix, wo, x, gain):
    rows, features = x.shape
    return pl.pallas_call(
        post_kernel,
        out_shape=[
            jax.ShapeDtypeStruct((rows, wo.shape[0]), bf16),
            jax.ShapeDtypeStruct((rows, features), f32),
            jax.ShapeDtypeStruct((rows, features), bf16),
        ],
        compiler_params=params(32),
        cost_estimate=cost(2 * rows * wo.size, 5e6),
        name="project_norm",
    )(mix, wo, x, gain)


def expert_kernel(place_ref, a_ref, b_ref, cot_ref, w_ref, wg_ref, wu_ref, wd_ref, *refs):
    dx_ref, x_ref, ha_ref, hb_ref, dg_ref, du_ref, sa_ref, sb_ref = refs[-8:]
    step = pl.program_id(0)
    first, second = place_ref[2], place_ref[3]
    half = sa_ref.shape[2]

    @pl.when(step == 0)
    def _():
        x_ref[...] = a_ref[...]

    @pl.when(step == 1)
    def _():
        x_ref[...] = b_ref[...]

    x = x_ref[...]
    cot = residual_scale * cot_ref[0].astype(f32)
    weight = w_ref[...]
    total = None
    for e in range(wg_ref.shape[0]):
        gate = dot(x, wg_ref[e])
        up = dot(x, wu_ref[e])
        slot_grad = (weight[:, e : e + 1] * cot).astype(bf16)
        to_a, to_b = jnp.bitwise_xor(first, e), jnp.bitwise_xor(second, e)
        sa_ref[to_a] = slot_grad[:, :half]
        sb_ref[to_b] = slot_grad[:, half:]
        hidden_grad = dot_nt(slot_grad, wd_ref[e])
        sig = 1.0 / (1.0 + jnp.exp(-gate))
        silu = gate * sig
        hidden = (silu * up).astype(bf16)
        ha_ref[to_a] = hidden
        hb_ref[to_b] = hidden
        gate_grad = (hidden_grad * up * (sig * (1.0 + gate * (1.0 - sig)))).astype(bf16)
        up_grad = (hidden_grad * silu).astype(bf16)
        dg_ref[to_a] = gate_grad
        du_ref[to_b] = up_grad
        term = dot_nt(gate_grad, wg_ref[e]) + dot_nt(up_grad, wu_ref[e])
        total = term if total is None else total + term
    dx_ref[0] = total.astype(bf16)


def expert_call(at, place, own, other, cot_all, weight, wg, wu, wd, kept):
    blocks, rows, features = cot_all.shape
    count, _, hidden = wg.shape
    tokens = blocks * rows
    inner = jax.ShapeDtypeStruct((count, tokens, hidden), bf16)
    outer = jax.ShapeDtypeStruct((count, tokens, features // 2), bf16)
    inner_spec = pl.BlockSpec((count, rows, hidden), lambda s, place: (0, 2 * at + s, 0))
    outer_spec = pl.BlockSpec((count, rows, features // 2), lambda s, place: (0, 2 * at + s, 0))
    fixed = lambda shape: pl.BlockSpec(shape, lambda s, place: (0,) * len(shape))
    any_spec = pl.BlockSpec(memory_space=pl.ANY)
    first = 8
    return pl.pallas_call(
        expert_kernel,
        grid_spec=pltpu.PrefetchScalarGridSpec(
            num_scalar_prefetch=1,
            grid=(2,),
            in_specs=[
                fixed((rows, features)),
                fixed((rows, features)),
                pl.BlockSpec((1, rows, features), lambda s, place: (place[s], 0, 0)),
                pl.BlockSpec((rows, count), lambda s, place: (place[s], 0)),
                fixed(wg.shape),
                fixed(wu.shape),
                fixed(wd.shape),
            ]
            + [any_spec] * len(kept),
            out_specs=[
                pl.BlockSpec((1, rows, features), lambda s, place: (s, 0, 0)),
                pl.BlockSpec((rows, features), lambda s, place: (2 * at + s, 0)),
            ]
            + [inner_spec] * 4
            + [outer_spec] * 2,
        ),
        out_shape=[
            jax.ShapeDtypeStruct((2, rows, features), bf16),
            jax.ShapeDtypeStruct((tokens, features), bf16),
            inner,
            inner,
            inner,
            inner,
            outer,
            outer,
        ],
        input_output_aliases={first + i: 1 + i for i in range(len(kept))},
        compiler_params=params(48, "arbitrary"),
        cost_estimate=cost(20 * rows * wg.size, 2e7, 2 * rows * hidden * count),
        name="experts",
    )(place, own, other, cot_all, weight, wg, wu, wd, *kept)


def part_sum_kernel(at_ref, *refs):
    inputs, outs = refs[:16], refs[16:]
    at = 0
    for out in outs:
        gate_came, gate_here, down_came, down_here = inputs[at : at + 4]
        rows = gate_came.shape[0]
        out[0, :rows] = (gate_came[...].astype(f32) + gate_here[...].astype(f32)).astype(bf16)
        out[0, rows:] = (down_came[...].astype(f32) + down_here[...].astype(f32)).astype(bf16)
        at += 4


def part_sum_call(at, per, came, here):
    gate_rows, down_rows = came[0].shape[0] // per, came[2].shape[0] // per
    width = came[0].shape[1]
    steps = per // 2
    specs, args, out_specs, out_shapes = [], [], [], []
    for stream in range(2):
        for sent in range(2):
            for which, rows in ((stream, gate_rows), (stream + 2, down_rows)):
                spec = pl.BlockSpec(
                    (rows, width),
                    lambda s, at, sent=sent, stream=stream: (
                        jnp.bitwise_xor(s + sent * steps, at[stream]),
                        0,
                    ),
                )
                specs += [spec, spec]
                args += [came[which], here[which]]
            out_specs.append(
                pl.BlockSpec((1, gate_rows + down_rows, width), lambda s, at: (s, 0, 0))
            )
            out_shapes.append(
                jax.ShapeDtypeStruct((steps, gate_rows + down_rows, width), bf16)
            )
    return pl.pallas_call(
        part_sum_kernel,
        grid_spec=pltpu.PrefetchScalarGridSpec(
            num_scalar_prefetch=1, grid=(steps,), in_specs=specs, out_specs=out_specs
        ),
        out_shape=out_shapes,
        compiler_params=params(48, "arbitrary"),
        cost_estimate=cost(0, 9e6),
        name="expert_part_sum",
    )(at, *args)


def joint_kernel(at_ref, keep_part_ref, keep_wo_ref, send_part_ref, send_wo_ref, keep_ref, send_ref):
    rows = keep_part_ref.shape[0]
    for part_ref, wo_ref, out_ref in (
        (keep_part_ref, keep_wo_ref, keep_ref),
        (send_part_ref, send_wo_ref, send_ref),
    ):
        out_ref[0, 0, :rows] = part_ref[...].astype(bf16)
        out_ref[0, 0, rows:] = wo_ref[...]


def joint_call(at, part, dense, parts):
    features, width = part.shape
    pieces = 2 * parts
    rows = features // pieces
    block_cols = dense.shape[1] // width
    per_block = pieces // block_cols
    wo_rows = dense.shape[0] // per_block
    steps = parts // 2

    def piece(sent):
        return lambda s, p, at: s * parts + jnp.bitwise_xor(p + sent * steps, at[s])

    specs = []
    for sent in range(2):
        at_piece = piece(sent)
        specs.append(
            pl.BlockSpec((rows, width), lambda s, p, at, f=at_piece: (f(s, p, at), 0))
        )
        specs.append(
            pl.BlockSpec(
                (wo_rows, width),
                lambda s, p, at, f=at_piece: (
                    lax.rem(f(s, p, at), per_block),
                    lax.div(f(s, p, at), per_block),
                ),
            )
        )
    out_spec = pl.BlockSpec((1, 1, rows + wo_rows, width), lambda s, p, at: (s, p, 0, 0))
    out_shape = jax.ShapeDtypeStruct((2, steps, rows + wo_rows, width), bf16)
    return pl.pallas_call(
        joint_kernel,
        grid_spec=pltpu.PrefetchScalarGridSpec(
            num_scalar_prefetch=1, grid=(2, steps), in_specs=specs, out_specs=[out_spec] * 2
        ),
        out_shape=[out_shape] * 2,
        compiler_params=params(32, "arbitrary", "arbitrary"),
        cost_estimate=cost(0, 2e6),
        name="dense_pieces",
    )(at, part, dense, part, dense)


def expert_out_kernel(at_ref, a_ref, b_ref, gate_ref, up_ref, down_ref):
    rows = gate_ref.shape[1]
    half = down_ref.shape[2] // 2
    gate_ref[0] = a_ref[:rows].astype(f32)
    up_ref[0] = b_ref[:rows].astype(f32)
    down_ref[0, :, :half] = a_ref[rows:].astype(f32)
    down_ref[0, :, half:] = b_ref[rows:].astype(f32)


def expert_out_call(at, a, b, gate_shape, down_shape):
    parts, held, width = a.shape
    count = gate_shape[0]
    per = parts // count
    gate_rows, down_rows = gate_shape[1] // per, down_shape[1] // per
    taken = lambda which: pl.BlockSpec(
        (None, held, width), lambda r, at: (jnp.bitwise_xor(r, at[which]), 0, 0)
    )
    place = lambda r, at: (lax.div(r, per), lax.rem(r, per), 0)
    return pl.pallas_call(
        expert_out_kernel,
        grid_spec=pltpu.PrefetchScalarGridSpec(
            num_scalar_prefetch=1,
            grid=(parts,),
            in_specs=[taken(0), taken(1)],
            out_specs=[
                pl.BlockSpec((1, gate_rows, gate_shape[2]), place),
                pl.BlockSpec((1, gate_rows, gate_shape[2]), place),
                pl.BlockSpec((1, down_rows, down_shape[2]), place),
            ],
        ),
        out_shape=[
            jax.ShapeDtypeStruct(gate_shape, f32),
            jax.ShapeDtypeStruct(gate_shape, f32),
            jax.ShapeDtypeStruct(down_shape, f32),
        ],
        compiler_params=params(40, "arbitrary"),
        cost_estimate=cost(0, 2e7),
        name="expert_weights_out",
    )(at, a, b)


def moe_kernel(place_ref, h_ref, w_ref, wd_ref, out_ref):
    weight = w_ref[...]
    total = None
    first = place_ref[pl.num_programs(0)]
    for e in range(wd_ref.shape[0]):
        term = weight[:, e : e + 1] * dot(h_ref[jnp.bitwise_xor(first, e)], wd_ref[e])
        total = term if total is None else total + term
    out_ref[0] = total.astype(bf16)


def moe_call(place, hidden, weight, wd, blocks):
    count, tokens, inner = hidden.shape
    features = wd.shape[2]
    rows = tokens // blocks
    return pl.pallas_call(
        moe_kernel,
        grid_spec=pltpu.PrefetchScalarGridSpec(
            num_scalar_prefetch=1,
            grid=(blocks,),
            in_specs=[
                pl.BlockSpec((count, rows, inner), lambda s, place: (0, s, 0)),
                pl.BlockSpec((rows, count), lambda s, place: (place[s], 0)),
                pl.BlockSpec(wd.shape, lambda s, place: (0, 0, 0)),
            ],
            out_specs=pl.BlockSpec((1, rows, features), lambda s, place: (place[s], 0, 0)),
        ),
        out_shape=jax.ShapeDtypeStruct((blocks, rows, features), bf16),
        compiler_params=params(32, "arbitrary"),
        cost_estimate=cost(2 * tokens * wd.size, 1.1e7),
        name="expert_outputs",
    )(place, hidden, weight, wd)


def turn_kernel(sg_ref, middle_ref, gain_ref, cot_ref, wo_ref, mg_ref, proj_ref, dmid_ref, dgain_ref):
    grad = sg_ref[...].astype(f32)
    middle = middle_ref[...]
    scale = lax.rsqrt(jnp.mean(middle * middle, axis=-1, keepdims=True) + norm_eps)
    unit = middle * scale
    dgain_ref[...] = jnp.sum(grad * unit, axis=0, keepdims=True)
    w = gain_ref[...] * grad
    dmid = cot_ref[...].astype(f32) + scale * (w - unit * jnp.mean(w * unit, axis=-1, keepdims=True))
    dmid_ref[...] = dmid
    proj = (residual_scale * dmid).astype(bf16)
    proj_ref[...] = proj
    mixed_grad = dot_nt(proj, wo_ref[...]).astype(bf16)
    groups, _, pair = mg_ref.shape
    for g in range(groups):
        mg_ref[g] = mixed_grad[:, g * pair : (g + 1) * pair]


def turn_call(sg, middle, gain, cot, wo, groups):
    rows, features = middle.shape
    pair = wo.shape[0] // groups
    return pl.pallas_call(
        turn_kernel,
        out_shape=[
            jax.ShapeDtypeStruct((groups, rows, pair), bf16),
            jax.ShapeDtypeStruct((rows, features), bf16),
            jax.ShapeDtypeStruct((rows, features), f32),
            jax.ShapeDtypeStruct((1, features), f32),
        ],
        compiler_params=params(32),
        cost_estimate=cost(2 * rows * wo.size, 6e6),
        name="norm_back_project_back",
    )(sg, middle, gain, cot, wo)


def output_weight_kernel(mixed_ref, proj_ref, dgain_ref, out_ref):
    held, each, features = out_ref.shape
    rows = mixed_ref.shape[1] // held
    part = lax.dot_general(mixed_ref[...], proj_ref[...], TN, preferred_element_type=f32)
    extra = jnp.broadcast_to(dgain_ref[...], (each - rows, features)).astype(bf16)
    for at in range(held):
        out_ref[at, :rows] = part[at * rows : (at + 1) * rows].astype(bf16)
        out_ref[at, rows:] = extra


def output_weight_call(mixed, proj, dgain, parts):
    rows, width = mixed.shape
    features = proj.shape[1]
    each = width // parts
    lanes = max(each, 2 * HEAD_DIM)
    held = lanes // each
    return pl.pallas_call(
        output_weight_kernel,
        grid=(parts // held,),
        in_specs=[
            pl.BlockSpec((rows, lanes), lambda s: (0, s)),
            whole((rows, features)),
            whole((1, features)),
        ],
        out_specs=pl.BlockSpec((held, each + 16, features), lambda s: (s, 0, 0)),
        out_shape=jax.ShapeDtypeStruct((parts, each + 16, features), bf16),
        compiler_params=params(32, "arbitrary"),
        cost_estimate=cost(2 * rows * width * features, 4e6),
        name="output_weight_part",
    )(mixed, proj, dgain)


def dense_out_kernel(
    at_ref, own_ref, other_ref, wq_ref, wk_ref, wv_ref, gain_ref, dq_ref, dk_ref, dv_ref, dg_ref, wo_ref
):
    chips, _, width = own_ref.shape
    rows = dq_ref.shape[0]
    pair = width // 2
    chip, core = at_ref[2], at_ref[3]
    total = jnp.zeros((rows, pair), f32)
    for k in range(chips):
        source = lax.rem(chip - k + chips, chips)
        a = jnp.where(core == 0, own_ref[k], other_ref[k]).astype(f32)
        b = jnp.where(core == 0, other_ref[k], own_ref[k]).astype(f32)
        q = jnp.concatenate([a[:rows, :pair], b[:rows, :pair]], axis=1)
        cols = pl.ds(pl.multiple_of(source * width, width), width)
        dq_ref[:, cols] = q
        made = q * wq_ref[:, cols].astype(f32)
        total += made[:, :pair] + made[:, pair:]
        a_kv, b_kv = a[:rows, pair:], b[:rows, pair:]
        lane = lax.broadcasted_iota(jnp.int32, a_kv.shape, 1)
        key = jnp.where(lane < HEAD_DIM, a_kv, pltpu.roll(b_kv, HEAD_DIM, 1))
        val = jnp.where(lane < HEAD_DIM, pltpu.roll(a_kv, HEAD_DIM, 1), b_kv)
        cols = pl.ds(pl.multiple_of(source * pair, pair), pair)
        dk_ref[:, cols] = key
        dv_ref[:, cols] = val
        total += key * wk_ref[:, cols].astype(f32) + val * wv_ref[:, cols].astype(f32)
        wo_ref[2 * source, 0] = a[rows:]
        wo_ref[2 * source + 1, 0] = b[rows:]
    dg_ref[...] = jnp.sum(jnp.transpose(total), axis=0, keepdims=True) / gain_ref[...]


def dense_out_call(at, own, other, wq, wk, wv, gain, wo_shape):
    streams, parts, chips, held, width = own.shape
    features = wq.shape[0]
    groups = 2 * chips
    rows = features // (streams * parts)
    block_cols = wo_shape[1] // width
    per_block = streams * parts // block_cols
    wo_rows = wo_shape[0] // groups // per_block
    by_rows = lambda w: pl.BlockSpec((rows, w.shape[1]), lambda s, r, at: (s * parts + r, 0))
    taken = pl.BlockSpec(
        (None, None, chips, held, width), lambda s, r, at: (s, jnp.bitwise_xor(r, at[s]), 0, 0, 0)
    )
    gain_spec = pl.BlockSpec((1, rows), lambda s, r, at: (0, s * parts + r))
    outs = pl.pallas_call(
        dense_out_kernel,
        grid_spec=pltpu.PrefetchScalarGridSpec(
            num_scalar_prefetch=1,
            grid=(streams, parts),
            in_specs=[taken, taken, by_rows(wq), by_rows(wk), by_rows(wv), gain_spec],
            out_specs=[
                by_rows(wq),
                by_rows(wk),
                by_rows(wv),
                gain_spec,
                pl.BlockSpec(
                    (groups, 1, wo_rows, width),
                    lambda s, r, at: (
                        0,
                        lax.rem(s * parts + r, per_block),
                        0,
                        lax.div(s * parts + r, per_block),
                    ),
                ),
            ],
        ),
        out_shape=[
            jax.ShapeDtypeStruct(wq.shape, f32),
            jax.ShapeDtypeStruct(wk.shape, f32),
            jax.ShapeDtypeStruct(wv.shape, f32),
            jax.ShapeDtypeStruct((1, features), f32),
            jax.ShapeDtypeStruct((groups, per_block, wo_rows, wo_shape[1]), f32),
        ],
        compiler_params=params(48, "arbitrary", "arbitrary"),
        cost_estimate=cost(2 * wq.size, 2.4e7),
        name="dense_weights_out",
    )(at, own, other, wq, wk, wv, gain)
    return (*outs[:4], outs[4].reshape(wo_shape))


def weights_out_kernel(wide_ref, wq_ref, wk_ref, wv_ref, gain_ref, dq_ref, dk_ref, dv_ref, dg_ref):
    groups, rows, width = wide_ref.shape
    pair = width // 2
    total = jnp.zeros((rows, pair), f32)
    for g in range(groups):
        part = wide_ref[g, :, :pair].astype(f32)
        at = slice(g * pair, (g + 1) * pair)
        dq_ref[:, at] = part
        total += part * wq_ref[:, at].astype(f32)
    for g in range(groups // 2):
        a = wide_ref[2 * g, :, pair:].astype(f32)
        b = wide_ref[2 * g + 1, :, pair:].astype(f32)
        lane = lax.broadcasted_iota(jnp.int32, a.shape, 1)
        at = slice(g * pair, (g + 1) * pair)
        k = jnp.where(lane < HEAD_DIM, a, pltpu.roll(b, HEAD_DIM, 1))
        v = jnp.where(lane < HEAD_DIM, pltpu.roll(a, HEAD_DIM, 1), b)
        dk_ref[:, at] = k
        dv_ref[:, at] = v
        total += k * wk_ref[:, at].astype(f32) + v * wv_ref[:, at].astype(f32)
    dg_ref[...] = jnp.sum(jnp.transpose(total), axis=0, keepdims=True) / gain_ref[...]


def weights_out_call(wide, wq, wk, wv, gain):
    chunks, groups, rows, width = wide.shape
    features = chunks * rows
    by_rows = lambda w: pl.BlockSpec((rows, w.shape[1]), lambda c: (c, 0))
    return pl.pallas_call(
        weights_out_kernel,
        grid=(chunks,),
        in_specs=[
            pl.BlockSpec((None, groups, rows, width), lambda c: (c, 0, 0, 0)),
            by_rows(wq),
            by_rows(wk),
            by_rows(wv),
            pl.BlockSpec((1, rows), lambda c: (0, c)),
        ],
        out_specs=[
            by_rows(wq),
            by_rows(wk),
            by_rows(wv),
            pl.BlockSpec((1, rows), lambda c: (0, c)),
        ],
        out_shape=[
            jax.ShapeDtypeStruct(wq.shape, f32),
            jax.ShapeDtypeStruct(wk.shape, f32),
            jax.ShapeDtypeStruct(wv.shape, f32),
            jax.ShapeDtypeStruct((1, features), f32),
        ],
        compiler_params=params(32, "arbitrary"),
        cost_estimate=cost(2 * wq.size, 1.6e7),
        name="attention_weights_out",
    )(wide, wq, wk, wv, gain)


def last_kernel(d_ref, wq_ref, wk_ref, wv_ref, x_ref, gain_ref, dmid_ref, out_ref):
    groups, rows, width = d_ref.shape
    pair = width // 2
    dq = jnp.concatenate([d_ref[g, :, :pair] for g in range(groups)], axis=1)
    grad = dot_nt(dq, wq_ref[...])
    keys, vals = [], []
    for at in range(groups // 2):
        a = d_ref[2 * at, :, pair:].astype(f32)
        b = d_ref[2 * at + 1, :, pair:].astype(f32)
        lane = lax.broadcasted_iota(jnp.int32, a.shape, 1)
        keys.append(jnp.where(lane < HEAD_DIM, a, pltpu.roll(b, HEAD_DIM, 1)).astype(bf16))
        vals.append(jnp.where(lane < HEAD_DIM, pltpu.roll(a, HEAD_DIM, 1), b).astype(bf16))
    grad = grad + dot_nt(jnp.concatenate(keys, axis=1), wk_ref[...])
    grad = grad + dot_nt(jnp.concatenate(vals, axis=1), wv_ref[...])
    x = x_ref[...].astype(f32)
    scale = lax.rsqrt(jnp.mean(x * x, axis=-1, keepdims=True) + norm_eps)
    unit = x * scale
    w = gain_ref[...] * grad
    out_ref[...] = dmid_ref[...] + scale * (w - unit * jnp.mean(w * unit, axis=-1, keepdims=True))


def last_call(d, wq, wk, wv, x, gain, dmid):
    rows, features = x.shape
    return pl.pallas_call(
        last_kernel,
        out_shape=jax.ShapeDtypeStruct((rows, features), f32),
        compiler_params=params(40),
        cost_estimate=cost(4 * rows * features * features, 8e6),
        name="input_gradient",
    )(d, wq, wk, wv, x, gain, dmid)


def swap(values, axis, bit):
    return lax.ppermute(values, axis, [(i, i ^ bit) for i in range(lax.axis_size(axis))])


def half_sum(values, axis, bit):
    half = values.shape[0] // 2
    upper = ((lax.axis_index(axis) & bit) > 0).astype(jnp.int32)
    came = swap(lax.dynamic_slice_in_dim(values, (1 - upper) * half, half), axis, bit)
    mine = lax.dynamic_slice_in_dim(values, upper * half, half)
    return (mine.astype(f32) + came.astype(f32)).astype(bf16)


def relative_sum(kept, sent, axis, bits):
    while True:
        kept = (kept.astype(f32) + swap(sent, axis, bits[0]).astype(f32)).astype(bf16)
        bits = bits[1:]
        if not bits:
            return kept
        half = kept.shape[0] // 2
        kept, sent = kept[:half], kept[half:]


def join_parts(stream, axis, bits):
    shape = stream.shape
    for bit in bits[::-1]:
        stream = jnp.stack([stream, swap(stream, axis, bit)])
    return stream.reshape(-1, *shape)


def body(
    layer_input,
    first_gain,
    query_weight,
    key_weight,
    value_weight,
    output_weight,
    second_gain,
    gate_weight,
    up_weight,
    down_weight,
    expert_ids,
    gate_values,
    positions,
    cotangent,
):
    micro, _, per_device, features = layer_input.shape
    devices = lax.axis_size("seq")
    replicas = lax.axis_size("dp")
    seq_place = lax.axis_index("seq")
    rows = micro * per_device
    local_experts = gate_weight.shape[0]
    groups = key_weight.shape[1] // HEAD_DIM
    pair = query_weight.shape[1] // groups
    copies = devices // groups

    dp_bits = [1 << i for i in range(replicas.bit_length() - 1)]

    def spread(blocks):
        if copies > 1:
            blocks = jnp.repeat(blocks, copies, axis=0)
        return lax.all_to_all(blocks, "seq", 0, 0, tiled=True)

    def unspread(blocks):
        return lax.all_to_all(blocks, "seq", 0, 0, tiled=True)[::copies]

    x = layer_input.reshape(rows, features)
    cot = cotangent.reshape(rows, features)
    gain_one = first_gain.reshape(1, features)
    gain_two = second_gain.reshape(1, features)
    pos_all = lax.all_to_all(
        jnp.broadcast_to(positions.reshape(1, rows), (devices, rows)), "seq", 0, 0, tiled=True
    )
    x_all = lax.all_gather(x, "seq", axis=0)
    cos_all, sin_all = rope_tables(pos_all.reshape(-1), pair)
    mine = seq_place * local_experts + jnp.arange(local_experts, dtype=jnp.int32)
    ids = expert_ids[:, 0]
    gates = gate_values[:, 0].astype(f32)
    routed = jnp.sum(
        jnp.where(ids[..., None] == mine, gates[..., None], 0.0), axis=2
    )
    routed = routed.reshape(micro, devices, per_device, local_experts)
    routed = jnp.transpose(routed, (1, 0, 2, 3)).reshape(devices * rows, local_experts)
    group = seq_place // copies
    w_own = jnp.concatenate(
        [
            lax.dynamic_slice_in_dim(query_weight, group * pair, pair, axis=1),
            lax.dynamic_slice_in_dim(key_weight, group * HEAD_DIM, HEAD_DIM, axis=1),
            lax.dynamic_slice_in_dim(value_weight, group * HEAD_DIM, HEAD_DIM, axis=1),
        ],
        axis=1,
    )
    cos_all, sin_all, routed, w_own = lax.optimization_barrier((cos_all, sin_all, routed, w_own))
    x_all, cot_then, cos_all, sin_all, routed, w_own = lax.optimization_barrier(
        (x_all, cot, cos_all, sin_all, routed, w_own)
    )
    cot_all = lax.all_gather(cot_then, "seq", axis=0)

    qkv, first_all = qkv_call(x_all, gain_one, cos_all, sin_all, w_own)
    qkv = qkv.reshape(devices, micro, per_device, 2 * pair)
    mix = attend_call(qkv)
    mix = unspread(mix.reshape(devices, rows, pair))
    mixed, middle, second_low = post_call(mix, output_weight, x, gain_two)

    chips = devices // 2
    chip, core = seq_place // 2, seq_place % 2
    onward = [(i, (i + 2) % devices) for i in range(devices)]
    dp_place = lax.axis_index("dp")
    first_bit = dp_place & 1
    last_bit = dp_place >> (len(dp_bits) - 1)
    held, kept, running, places = second_low, (), None, []
    for hop in range(chips):
        following = lax.ppermute(held, "seq", onward) if hop < chips - 1 else None
        other = swap(held, "seq", 1)
        source = 2 * ((chip - hop) % chips)
        place = jnp.stack([source + core, source + 1 - core, 1 - first_bit, 1 - last_bit])
        place = place.astype(jnp.int32)
        places.append(place[:2])
        dx, *kept = expert_call(
            hop, place, held, other, cot_all, routed, gate_weight, up_weight, down_weight, kept
        )
        if following is not None:
            following, dx = lax.optimization_barrier((following, dx))
        part = dx[0].astype(f32) + swap(dx[1], "seq", 1).astype(f32)
        if hop == 0:
            own_part = part
        else:
            if running is not None:
                part = part + running.astype(f32)
            part = part.astype(bf16)
            if following is not None:
                part, following = lax.optimization_barrier((part, following))
            else:
                part, kept = lax.optimization_barrier((part, kept))
            running = lax.ppermute(part, "seq", onward)
        held = following
    second_grad = (own_part + running.astype(f32)).astype(bf16)
    tokens, hidden_a, hidden_b, gate_low, up_low, slot_a, slot_b = kept

    def weight_parts(at, tokens, hidden_a, hidden_b, gate_low, up_low, slot_a, slot_b):
        pairs = (
            (tokens, gate_low[at]),
            (tokens, up_low[at]),
            (hidden_a[at], slot_a[at]),
            (hidden_b[at], slot_b[at]),
        )
        return [
            lax.dot_general(a, b, TN, preferred_element_type=f32).astype(bf16) for a, b in pairs
        ]

    leaving = weight_parts(0, *kept)
    part_bits = (dp_bits[0], dp_bits[-1], dp_bits[0], dp_bits[-1])
    stream_bits = (dp_bits, dp_bits[::-1])
    came = [swap(values, "dp", bit) for values, bit in zip(leaving, part_bits)]
    leaving, second_grad = lax.optimization_barrier((leaving, second_grad))

    mg_send, proj, middle_grad, gain_two_part = turn_call(
        second_grad, middle, gain_two, cot, output_weight, groups
    )
    mg = spread(mg_send)
    mixed, kept, proj, _ = lax.optimization_barrier((mixed, kept, proj, mg_send))
    dense = output_weight_call(mixed, proj, gain_two_part, devices)
    dense_own, kept = lax.optimization_barrier((dense, kept))
    staying = weight_parts(1, *kept)
    turned = sum(((dp_place >> i) & 1) << (len(dp_bits) - 1 - i) for i in range(len(dp_bits)))
    part_at = jnp.stack([turned, dp_place]).astype(jnp.int32)
    low_at = jnp.bitwise_and(part_at, replicas // 2 - 1)
    keep_a, send_a, keep_b, send_b = part_sum_call(low_at, replicas // 2, came, staying)
    mg, keep_a, send_a, keep_b, send_b = lax.optimization_barrier(
        (mg, keep_a, send_a, keep_b, send_b)
    )
    streams = [
        relative_sum(keep_a, send_a, "dp", stream_bits[0][1:]),
        relative_sum(keep_b, send_b, "dp", stream_bits[1][1:]),
    ]
    dense = dense_own
    dense = lax.psum_scatter(dense, "seq", scatter_dimension=0)
    table_shape = (devices, micro, per_device, pair)
    dqkv = attend_back_call(
        qkv,
        mg.reshape(devices, micro, per_device, pair),
        cos_all.reshape(table_shape),
        sin_all.reshape(table_shape),
    )
    dqkv, streams = lax.optimization_barrier((dqkv, streams))
    expert_parts = [
        join_parts(v[0], "dp", bits[-1:]) for v, bits in zip(streams, stream_bits)
    ]
    back = unspread(dqkv.reshape(devices, rows, 2 * pair))
    d_all = dqkv.reshape(devices * rows, 2 * pair)
    first_tokens = first_all.reshape(devices * rows, features)
    part = lax.dot_general(first_tokens, d_all, TN, preferred_element_type=f32)
    dense = dense.reshape(dense.shape[-2], features)
    each = output_weight.shape[0] // devices
    gain_row, dense = dense[each:], dense[:each]
    if copies == 1:
        width = 2 * pair
        kept_pieces, sent_pieces = joint_call(part_at, part, dense, replicas)
        own = [
            relative_sum(kept_pieces[at], sent_pieces[at], "dp", bits)
            for at, bits in enumerate(stream_bits)
        ]
        own = jnp.concatenate(own, axis=0)
        own, expert_parts = lax.optimization_barrier((own, expert_parts))
    else:
        sent_pieces = part
    kept, sent_pieces = lax.optimization_barrier((kept, sent_pieces))
    moe_place = jnp.concatenate(places + [(1 - first_bit).astype(jnp.int32).reshape(1)])
    moe_all = moe_call(moe_place, kept[1], routed, down_weight, devices)
    moe = lax.psum_scatter(moe_all, "seq", scatter_dimension=0)
    layer_output = (middle + residual_scale * moe.astype(f32)).astype(bf16)
    for bit in dp_bits:
        gain_row = (gain_row.astype(f32) + swap(gain_row, "dp", bit).astype(f32)).astype(bf16)
    expert_parts = [
        join_parts(v, "dp", bits[:-1]).reshape(-1, *v.shape[-2:])
        for v, bits in zip(expert_parts, stream_bits)
    ]
    input_grad = last_call(
        back, query_weight, key_weight, value_weight, x, gain_one, middle_grad
    )
    if copies == 1:
        backward = [(i, (i - 2) % devices) for i in range(devices)]
        round_ring = {0: own}
        for k in range(1, chips // 2 + 1):
            round_ring[k] = lax.ppermute(round_ring[k - 1], "seq", onward)
            if chips - k > k:
                round_ring[chips - k] = lax.ppermute(
                    round_ring[(chips - k + 1) % chips], "seq", backward
                )
        held = jnp.stack([round_ring[k] for k in range(chips)])
        held, expert_parts, input_grad, gain_row = lax.optimization_barrier(
            (held, expert_parts, input_grad, gain_row)
        )
        gate_sum, up_sum, down_sum = expert_out_call(
            part_at, *expert_parts, gate_weight.shape, down_weight.shape
        )
        full = [join_parts(held[:, at], "dp", b) for at, b in enumerate(stream_bits)]
        full, gate_sum, up_sum, down_sum = lax.optimization_barrier(
            (jnp.stack(full), gate_sum, up_sum, down_sum)
        )
        other = swap(full, "seq", 1)
        where_at = jnp.stack([turned, dp_place, chip, core]).astype(jnp.int32)
        (
            query_weight_grad,
            key_weight_grad,
            value_weight_grad,
            first_gain_grad,
            output_weight_grad,
        ) = dense_out_call(
            where_at, full, other, query_weight, key_weight, value_weight, gain_one, output_weight.shape
        )
    else:
        gate_sum, up_sum, down_sum = expert_out_call(
            part_at, *expert_parts, gate_weight.shape, down_weight.shape
        )
        for bit in dp_bits:
            dense = (dense.astype(f32) + swap(dense, "dp", bit).astype(f32)).astype(bf16)
        dense = lax.all_gather(dense, "seq", axis=0).astype(f32)
        output_weight_grad = dense.reshape(output_weight.shape)
        part = part.astype(bf16)
        for bit in dp_bits[::-1]:
            part = half_sum(part, "dp", bit)
        wide = lax.all_gather(part, ("dp", "seq"), axis=0)
        wide = wide.reshape(replicas, devices, features // replicas, 2 * pair)[:, ::copies]
        query_weight_grad, key_weight_grad, value_weight_grad, first_gain_grad = weights_out_call(
            wide, query_weight, key_weight, value_weight, gain_one
        )
    second_gain_grad = gain_row[0].astype(f32)
    return (
        layer_output.reshape(layer_input.shape),
        input_grad.reshape(layer_input.shape),
        first_gain_grad.reshape(features),
        query_weight_grad,
        key_weight_grad,
        value_weight_grad,
        output_weight_grad,
        second_gain_grad,
        gate_sum,
        up_sum,
        down_sum,
    )


def solution(mesh):
    return jax.shard_map(
        body,
        mesh=mesh,
        in_specs=(
            P(None, "dp", "seq", None),
            P(),
            P(),
            P(),
            P(),
            P(),
            P(),
            P("seq", None, None),
            P("seq", None, None),
            P("seq", None, None),
            P(None, "dp", None, None),
            P(None, "dp", None, None),
            P(None, "dp", "seq"),
            P(None, "dp", "seq", None),
        ),
        out_specs=(
            P(None, "dp", "seq", None),
            P(None, "dp", "seq", None),
            P(),
            P(),
            P(),
            P(),
            P(),
            P(),
            P("seq", None, None),
            P("seq", None, None),
            P("seq", None, None),
        ),
        check_vma=False,
    )
```

```python
from functools import partial

import jax
import jax.numpy as jnp
from jax import lax
from jax.experimental import pallas as pl
from jax.experimental.pallas import tpu as pltpu
from jax.sharding import PartitionSpec as P

HEAD_DIM = 64

rope_theta = 10000.0
attention_scale = 0.015625
residual_scale = 0.22
norm_eps = 1e-06
masked_score = -1e30

f32 = jnp.float32
bf16 = jnp.bfloat16
NT = (((1,), (1,)), ((), ()))
TN = (((0,), (0,)), ((), ()))


def dot(a, b):
    return jnp.dot(a, b, preferred_element_type=f32)


def dot_nt(a, b):
    return lax.dot_general(a, b, NT, preferred_element_type=f32)


def params(mib, *semantics):
    return pltpu.CompilerParams(
        vmem_limit_bytes=mib * 1024 * 1024, dimension_semantics=semantics or None
    )


def cost(flops, nbytes, trans=0):
    return pl.CostEstimate(
        flops=int(flops / 8), bytes_accessed=int(nbytes / 8), transcendentals=int(trans / 8)
    )


def whole(shape):
    return pl.BlockSpec(shape, lambda *_: (0,) * len(shape))


def rope_tables(positions, width):
    half = HEAD_DIM // 2
    exponent = jnp.arange(half, dtype=f32) * (-2.0 / HEAD_DIM)
    angles = positions.astype(f32)[:, None] * (rope_theta**exponent)[None, :]
    cosine, sine = jnp.cos(angles), jnp.sin(angles)
    copies = width // HEAD_DIM
    cos_row = jnp.concatenate([cosine, cosine] * copies, axis=1)
    sin_row = jnp.concatenate([-sine, sine] * copies, axis=1)
    return cos_row, sin_row


def partner(values):
    width = values.shape[1]
    half = HEAD_DIM // 2
    lane = lax.broadcasted_iota(jnp.int32, values.shape, 1)
    ahead = pltpu.roll(values, width - half, 1)
    behind = pltpu.roll(values, half, 1)
    return jnp.where(lane % HEAD_DIM < half, ahead, behind)


def qkv_kernel(x_ref, gain_ref, cos_ref, sin_ref, w_ref, qkv_ref, low_ref):
    pair = 2 * HEAD_DIM
    x = x_ref[0].astype(f32)
    scale = lax.rsqrt(jnp.mean(x * x, axis=-1, keepdims=True) + norm_eps)
    low = (x * scale * gain_ref[...]).astype(bf16)
    low_ref[0] = low
    cosine, sine = cos_ref[...], sin_ref[...]
    made = dot(low, w_ref[...])
    q, kv = made[:, :pair], made[:, pair:]
    q = (q * cosine + partner(q) * sine) * attention_scale
    qkv_ref[0, :, :pair] = q.astype(bf16)
    lane = lax.broadcasted_iota(jnp.int32, kv.shape, 1)
    turned = kv * cosine + partner(kv) * sine
    qkv_ref[0, :, pair:] = jnp.where(lane < HEAD_DIM, turned, kv).astype(bf16)


def qkv_call(x_all, gain, cos_all, sin_all, w_own):
    blocks, rows, features = x_all.shape
    pair = 2 * HEAD_DIM
    return pl.pallas_call(
        qkv_kernel,
        grid=(blocks,),
        in_specs=[
            pl.BlockSpec((1, rows, features), lambda s: (s, 0, 0)),
            whole((1, features)),
            pl.BlockSpec((rows, pair), lambda s: (s, 0)),
            pl.BlockSpec((rows, pair), lambda s: (s, 0)),
            whole(w_own.shape),
        ],
        out_specs=[
            pl.BlockSpec((1, rows, 2 * pair), lambda s: (s, 0, 0)),
            pl.BlockSpec((1, rows, features), lambda s: (s, 0, 0)),
        ],
        out_shape=[
            jax.ShapeDtypeStruct((blocks, rows, 2 * pair), bf16),
            jax.ShapeDtypeStruct((blocks, rows, features), bf16),
        ],
        compiler_params=params(58, "arbitrary"),
        cost_estimate=cost(4 * blocks * rows * features * pair, 14e6),
        name="norm_qkv_rope",
    )(x_all, gain, cos_all, sin_all, w_own)


def split_heads(block, first):
    wide = block.astype(f32)
    lane = lax.broadcasted_iota(jnp.int32, wide.shape, 1)
    turned = pltpu.roll(wide, HEAD_DIM, 1)
    if first:
        parts = [jnp.where(lane < HEAD_DIM, wide, 0.0), jnp.where(lane < HEAD_DIM, turned, 0.0)]
    else:
        parts = [jnp.where(lane >= HEAD_DIM, turned, 0.0), jnp.where(lane >= HEAD_DIM, wide, 0.0)]
    return jnp.concatenate(parts, axis=0).astype(bf16)


def join_heads(turned):
    rows = turned.shape[1] // 2
    return jnp.transpose(jnp.concatenate([turned[:, :rows], turned[:, rows:]], axis=0))


def scores_of(kv, q2, rows):
    scores = dot_nt(kv, q2)
    count = scores.shape[0]
    own = scores[count - rows :]
    key_at = lax.broadcasted_iota(jnp.int32, own.shape, 0)
    query_at = lax.broadcasted_iota(jnp.int32, own.shape, 1) % rows
    own = jnp.where(key_at <= query_at, own, masked_score)
    if count == rows:
        return own
    return jnp.concatenate([scores[: count - rows], own], axis=0)


def attend_kernel(qkv_ref, out_ref):
    blocks, _, rows, width = qkv_ref.shape
    pair = width // 2
    kv = qkv_ref[:, 0, :, pair:].reshape(blocks * rows, pair)
    kv_t = jnp.transpose(kv)
    for at in range(blocks):
        count = (at + 1) * rows
        q2 = split_heads(qkv_ref[at, 0, :, :pair], True)
        scores = scores_of(kv[:count], q2, rows)
        top = jnp.max(scores, axis=0, keepdims=True)
        weights = jnp.exp(scores - top)
        total = jnp.sum(weights, axis=0, keepdims=True)
        out_t = dot(kv_t[:, :count], weights.astype(bf16))
        out_ref[at, 0] = join_heads(out_t[HEAD_DIM:] / total).astype(bf16)


def attend_call(qkv):
    blocks, micro, rows, width = qkv.shape
    pair = width // 2
    length = blocks * rows
    return pl.pallas_call(
        attend_kernel,
        grid=(micro,),
        in_specs=[pl.BlockSpec((blocks, 1, rows, width), lambda m: (0, m, 0, 0))],
        out_specs=pl.BlockSpec((blocks, 1, rows, pair), lambda m: (0, m, 0, 0)),
        out_shape=jax.ShapeDtypeStruct((blocks, micro, rows, pair), bf16),
        compiler_params=params(48, "arbitrary"),
        cost_estimate=cost(
            micro * length * length * 512, 3 * qkv.size, micro * length * length
        ),
        name="attention_forward",
    )(qkv)


def attend_back_kernel(qkv_ref, grad_ref, cos_ref, sin_ref, out_ref, dkv_ref):
    blocks, _, rows, width = qkv_ref.shape
    pair = width // 2
    kv = qkv_ref[:, 0, :, pair:].reshape(blocks * rows, pair)
    kv_t = jnp.transpose(kv)
    dkv_ref[...] = jnp.zeros_like(dkv_ref)
    for at in range(blocks):
        count = (at + 1) * rows
        q2 = split_heads(qkv_ref[at, 0, :, :pair], True)
        g2 = split_heads(grad_ref[at, 0], False)
        scores = scores_of(kv[:count], q2, rows)
        top = jnp.max(scores, axis=0, keepdims=True)
        weights = jnp.exp(scores - top)
        total = jnp.sum(weights, axis=0, keepdims=True)
        prob = weights * (1.0 / total)
        prob_grad = dot_nt(kv[:count], g2)
        delta = jnp.sum(prob * prob_grad, axis=0, keepdims=True)
        score_grad = (prob * (prob_grad - delta)).astype(bf16)
        dkv_ref[:count] += dot(score_grad, q2) + dot(prob.astype(bf16), g2)
        dq_t = dot(kv_t[:, :count], score_grad)
        dq = join_heads(dq_t[:HEAD_DIM] * attention_scale)
        dq = dq * cos_ref[at, 0] - partner(dq) * sin_ref[at, 0]
        out_ref[at, 0, :, :pair] = dq.astype(bf16)
    for at in range(blocks):
        dkv = dkv_ref[at * rows : (at + 1) * rows]
        lane = lax.broadcasted_iota(jnp.int32, dkv.shape, 1)
        turned = dkv * cos_ref[at, 0] - partner(dkv) * sin_ref[at, 0]
        out_ref[at, 0, :, pair:] = jnp.where(lane < HEAD_DIM, turned, dkv).astype(bf16)


def attend_back_call(qkv, grads, cos_all, sin_all):
    blocks, micro, rows, width = qkv.shape
    pair = width // 2
    length = blocks * rows
    spec = lambda lanes: pl.BlockSpec((blocks, 1, rows, lanes), lambda m: (0, m, 0, 0))
    return pl.pallas_call(
        attend_back_kernel,
        grid=(micro,),
        in_specs=[spec(width), spec(pair), spec(pair), spec(pair)],
        out_specs=spec(width),
        out_shape=jax.ShapeDtypeStruct(qkv.shape, bf16),
        scratch_shapes=[pltpu.VMEM((length, pair), f32)],
        compiler_params=params(56, "arbitrary"),
        cost_estimate=cost(
            micro * length * length * 1280, 10 * qkv.size, micro * length * length
        ),
        name="attention_backward",
    )(qkv, grads, cos_all, sin_all)


def post_kernel(mix_ref, wo_ref, x_ref, gain_ref, mixed_ref, middle_ref, low_ref):
    mixed = jnp.concatenate([mix_ref[g] for g in range(mix_ref.shape[0])], axis=1)
    mixed_ref[...] = mixed
    middle = x_ref[...].astype(f32) + residual_scale * dot(mixed, wo_ref[...])
    middle_ref[...] = middle
    scale = lax.rsqrt(jnp.mean(middle * middle, axis=-1, keepdims=True) + norm_eps)
    low_ref[...] = (middle * scale * gain_ref[...]).astype(bf16)


def post_call(mix, wo, x, gain):
    rows, features = x.shape
    return pl.pallas_call(
        post_kernel,
        out_shape=[
            jax.ShapeDtypeStruct((rows, wo.shape[0]), bf16),
            jax.ShapeDtypeStruct((rows, features), f32),
            jax.ShapeDtypeStruct((rows, features), bf16),
        ],
        compiler_params=params(32),
        cost_estimate=cost(2 * rows * wo.size, 5e6),
        name="project_norm",
    )(mix, wo, x, gain)


def expert_kernel(place_ref, a_ref, b_ref, cot_ref, w_ref, wg_ref, wu_ref, wd_ref, *refs):
    dx_ref, x_ref, ha_ref, hb_ref, dg_ref, du_ref, sa_ref, sb_ref = refs[-8:]
    step = pl.program_id(0)
    first, second = place_ref[2], place_ref[3]
    half = sa_ref.shape[2]

    @pl.when(step == 0)
    def _():
        x_ref[...] = a_ref[...]

    @pl.when(step == 1)
    def _():
        x_ref[...] = b_ref[...]

    x = x_ref[...]
    cot = residual_scale * cot_ref[0].astype(f32)
    weight = w_ref[...]
    total = None
    for e in range(wg_ref.shape[0]):
        gate = dot(x, wg_ref[e])
        up = dot(x, wu_ref[e])
        slot_grad = (weight[:, e : e + 1] * cot).astype(bf16)
        to_a, to_b = jnp.bitwise_xor(first, e), jnp.bitwise_xor(second, e)
        sa_ref[to_a] = slot_grad[:, :half]
        sb_ref[to_b] = slot_grad[:, half:]
        hidden_grad = dot_nt(slot_grad, wd_ref[e])
        sig = 1.0 / (1.0 + jnp.exp(-gate))
        silu = gate * sig
        hidden = (silu * up).astype(bf16)
        ha_ref[to_a] = hidden
        hb_ref[to_b] = hidden
        gate_grad = (hidden_grad * up * (sig * (1.0 + gate * (1.0 - sig)))).astype(bf16)
        up_grad = (hidden_grad * silu).astype(bf16)
        dg_ref[to_a] = gate_grad
        du_ref[to_b] = up_grad
        term = dot_nt(gate_grad, wg_ref[e]) + dot_nt(up_grad, wu_ref[e])
        total = term if total is None else total + term
    dx_ref[0] = total.astype(bf16)


def expert_call(at, place, own, other, cot_all, weight, wg, wu, wd, kept):
    blocks, rows, features = cot_all.shape
    count, _, hidden = wg.shape
    tokens = blocks * rows
    inner = jax.ShapeDtypeStruct((count, tokens, hidden), bf16)
    outer = jax.ShapeDtypeStruct((count, tokens, features // 2), bf16)
    inner_spec = pl.BlockSpec((count, rows, hidden), lambda s, place: (0, 2 * at + s, 0))
    outer_spec = pl.BlockSpec((count, rows, features // 2), lambda s, place: (0, 2 * at + s, 0))
    fixed = lambda shape: pl.BlockSpec(shape, lambda s, place: (0,) * len(shape))
    any_spec = pl.BlockSpec(memory_space=pl.ANY)
    first = 8
    return pl.pallas_call(
        expert_kernel,
        grid_spec=pltpu.PrefetchScalarGridSpec(
            num_scalar_prefetch=1,
            grid=(2,),
            in_specs=[
                fixed((rows, features)),
                fixed((rows, features)),
                pl.BlockSpec((1, rows, features), lambda s, place: (place[s], 0, 0)),
                pl.BlockSpec((rows, count), lambda s, place: (place[s], 0)),
                fixed(wg.shape),
                fixed(wu.shape),
                fixed(wd.shape),
            ]
            + [any_spec] * len(kept),
            out_specs=[
                pl.BlockSpec((1, rows, features), lambda s, place: (s, 0, 0)),
                pl.BlockSpec((rows, features), lambda s, place: (2 * at + s, 0)),
            ]
            + [inner_spec] * 4
            + [outer_spec] * 2,
        ),
        out_shape=[
            jax.ShapeDtypeStruct((2, rows, features), bf16),
            jax.ShapeDtypeStruct((tokens, features), bf16),
            inner,
            inner,
            inner,
            inner,
            outer,
            outer,
        ],
        input_output_aliases={first + i: 1 + i for i in range(len(kept))},
        compiler_params=params(48, "arbitrary"),
        cost_estimate=cost(20 * rows * wg.size, 2e7, 2 * rows * hidden * count),
        name="experts",
    )(place, own, other, cot_all, weight, wg, wu, wd, *kept)


def part_sum_kernel(at_ref, *refs):
    inputs, outs = refs[:16], refs[16:]
    at = 0
    for out in outs:
        gate_came, gate_here, down_came, down_here = inputs[at : at + 4]
        rows = gate_came.shape[0]
        out[0, :rows] = (gate_came[...].astype(f32) + gate_here[...].astype(f32)).astype(bf16)
        out[0, rows:] = (down_came[...].astype(f32) + down_here[...].astype(f32)).astype(bf16)
        at += 4


def part_sum_call(at, per, came, here):
    gate_rows, down_rows = came[0].shape[0] // per, came[2].shape[0] // per
    width = came[0].shape[1]
    steps = per // 2
    specs, args, out_specs, out_shapes = [], [], [], []
    for stream in range(2):
        for sent in range(2):
            for which, rows in ((stream, gate_rows), (stream + 2, down_rows)):
                spec = pl.BlockSpec(
                    (rows, width),
                    lambda s, at, sent=sent, stream=stream: (
                        jnp.bitwise_xor(s + sent * steps, at[stream]),
                        0,
                    ),
                )
                specs += [spec, spec]
                args += [came[which], here[which]]
            out_specs.append(
                pl.BlockSpec((1, gate_rows + down_rows, width), lambda s, at: (s, 0, 0))
            )
            out_shapes.append(
                jax.ShapeDtypeStruct((steps, gate_rows + down_rows, width), bf16)
            )
    return pl.pallas_call(
        part_sum_kernel,
        grid_spec=pltpu.PrefetchScalarGridSpec(
            num_scalar_prefetch=1, grid=(steps,), in_specs=specs, out_specs=out_specs
        ),
        out_shape=out_shapes,
        compiler_params=params(48, "arbitrary"),
        cost_estimate=cost(0, 9e6),
        name="expert_part_sum",
    )(at, *args)


def joint_kernel(at_ref, *refs):
    for (part_ref, wo_ref, gain_ref), out_ref in ((refs[:3], refs[6]), (refs[3:6], refs[7])):
        rows = part_ref.shape[0]
        upto = rows + wo_ref.shape[0]
        out_ref[0, 0, :rows] = part_ref[...].astype(bf16)
        out_ref[0, 0, rows:upto] = wo_ref[...]
        out_ref[0, 0, upto:] = gain_ref[...]


def joint_call(at, part, dense, parts):
    features, width = part.shape
    pieces = 2 * parts
    rows = features // pieces
    block_cols = dense.shape[1] // width
    per_block = pieces // block_cols
    extra = 16
    wo_rows = (dense.shape[0] - extra) // per_block
    last = dense.shape[0] // extra - 1
    steps = parts // 2

    def piece(sent):
        return lambda s, p, at: s * parts + jnp.bitwise_xor(p + sent * steps, at[s])

    specs = []
    for sent in range(2):
        at_piece = piece(sent)
        specs.append(
            pl.BlockSpec((rows, width), lambda s, p, at, f=at_piece: (f(s, p, at), 0))
        )
        specs.append(
            pl.BlockSpec(
                (wo_rows, width),
                lambda s, p, at, f=at_piece: (
                    lax.rem(f(s, p, at), per_block),
                    lax.div(f(s, p, at), per_block),
                ),
            )
        )
        specs.append(
            pl.BlockSpec(
                (extra, width), lambda s, p, at, f=at_piece: (last, lax.div(f(s, p, at), per_block))
            )
        )
    out_spec = pl.BlockSpec((1, 1, rows + wo_rows + extra, width), lambda s, p, at: (s, p, 0, 0))
    out_shape = jax.ShapeDtypeStruct((2, steps, rows + wo_rows + extra, width), bf16)
    return pl.pallas_call(
        joint_kernel,
        grid_spec=pltpu.PrefetchScalarGridSpec(
            num_scalar_prefetch=1, grid=(2, steps), in_specs=specs, out_specs=[out_spec] * 2
        ),
        out_shape=[out_shape] * 2,
        compiler_params=params(32, "arbitrary", "arbitrary"),
        cost_estimate=cost(0, 2e6),
        name="dense_pieces",
    )(at, part, dense, dense, part, dense, dense)


def expert_out_kernel(at_ref, a_ref, b_ref, gate_ref, up_ref, down_ref):
    rows = gate_ref.shape[1]
    half = down_ref.shape[2] // 2
    gate_ref[0] = a_ref[:rows].astype(f32)
    up_ref[0] = b_ref[:rows].astype(f32)
    down_ref[0, :, :half] = a_ref[rows:].astype(f32)
    down_ref[0, :, half:] = b_ref[rows:].astype(f32)


def expert_out_call(at, a, b, gate_shape, down_shape):
    parts, held, width = a.shape
    count = gate_shape[0]
    per = parts // count
    gate_rows, down_rows = gate_shape[1] // per, down_shape[1] // per
    taken = lambda which: pl.BlockSpec(
        (None, held, width), lambda r, at: (jnp.bitwise_xor(r, at[which]), 0, 0)
    )
    place = lambda r, at: (lax.div(r, per), lax.rem(r, per), 0)
    return pl.pallas_call(
        expert_out_kernel,
        grid_spec=pltpu.PrefetchScalarGridSpec(
            num_scalar_prefetch=1,
            grid=(parts,),
            in_specs=[taken(0), taken(1)],
            out_specs=[
                pl.BlockSpec((1, gate_rows, gate_shape[2]), place),
                pl.BlockSpec((1, gate_rows, gate_shape[2]), place),
                pl.BlockSpec((1, down_rows, down_shape[2]), place),
            ],
        ),
        out_shape=[
            jax.ShapeDtypeStruct(gate_shape, f32),
            jax.ShapeDtypeStruct(gate_shape, f32),
            jax.ShapeDtypeStruct(down_shape, f32),
        ],
        compiler_params=params(40, "arbitrary"),
        cost_estimate=cost(0, 2e7),
        name="expert_weights_out",
    )(at, a, b)


def moe_kernel(place_ref, h_ref, w_ref, wd_ref, out_ref):
    weight = w_ref[...]
    total = None
    first = place_ref[pl.num_programs(0)]
    for e in range(wd_ref.shape[0]):
        term = weight[:, e : e + 1] * dot(h_ref[jnp.bitwise_xor(first, e)], wd_ref[e])
        total = term if total is None else total + term
    out_ref[0] = total.astype(bf16)


def moe_call(place, hidden, weight, wd, blocks):
    count, tokens, inner = hidden.shape
    features = wd.shape[2]
    rows = tokens // blocks
    return pl.pallas_call(
        moe_kernel,
        grid_spec=pltpu.PrefetchScalarGridSpec(
            num_scalar_prefetch=1,
            grid=(blocks,),
            in_specs=[
                pl.BlockSpec((count, rows, inner), lambda s, place: (0, s, 0)),
                pl.BlockSpec((rows, count), lambda s, place: (place[s], 0)),
                pl.BlockSpec(wd.shape, lambda s, place: (0, 0, 0)),
            ],
            out_specs=pl.BlockSpec((1, rows, features), lambda s, place: (place[s], 0, 0)),
        ),
        out_shape=jax.ShapeDtypeStruct((blocks, rows, features), bf16),
        compiler_params=params(32, "arbitrary"),
        cost_estimate=cost(2 * tokens * wd.size, 1.1e7),
        name="expert_outputs",
    )(place, hidden, weight, wd)


def turn_kernel(sg_ref, middle_ref, gain_ref, cot_ref, wo_ref, mg_ref, proj_ref, dmid_ref, dgain_ref):
    grad = sg_ref[...].astype(f32)
    middle = middle_ref[...]
    scale = lax.rsqrt(jnp.mean(middle * middle, axis=-1, keepdims=True) + norm_eps)
    unit = middle * scale
    dgain_ref[...] = jnp.sum(grad * unit, axis=0, keepdims=True)
    w = gain_ref[...] * grad
    dmid = cot_ref[...].astype(f32) + scale * (w - unit * jnp.mean(w * unit, axis=-1, keepdims=True))
    dmid_ref[...] = dmid
    proj = (residual_scale * dmid).astype(bf16)
    proj_ref[...] = proj
    mixed_grad = dot_nt(proj, wo_ref[...]).astype(bf16)
    groups, _, pair = mg_ref.shape
    for g in range(groups):
        mg_ref[g] = mixed_grad[:, g * pair : (g + 1) * pair]


def turn_call(sg, middle, gain, cot, wo, groups):
    rows, features = middle.shape
    pair = wo.shape[0] // groups
    return pl.pallas_call(
        turn_kernel,
        out_shape=[
            jax.ShapeDtypeStruct((groups, rows, pair), bf16),
            jax.ShapeDtypeStruct((rows, features), bf16),
            jax.ShapeDtypeStruct((rows, features), f32),
            jax.ShapeDtypeStruct((1, features), f32),
        ],
        compiler_params=params(32),
        cost_estimate=cost(2 * rows * wo.size, 6e6),
        name="norm_back_project_back",
    )(sg, middle, gain, cot, wo)


def output_weight_kernel(mixed_ref, proj_ref, dgain_ref, out_ref):
    held, each, features = out_ref.shape
    rows = mixed_ref.shape[1] // held
    part = lax.dot_general(mixed_ref[...], proj_ref[...], TN, preferred_element_type=f32)
    extra = jnp.broadcast_to(dgain_ref[...], (each - rows, features)).astype(bf16)
    for at in range(held):
        out_ref[at, :rows] = part[at * rows : (at + 1) * rows].astype(bf16)
        out_ref[at, rows:] = extra


def output_weight_call(mixed, proj, dgain, parts):
    rows, width = mixed.shape
    features = proj.shape[1]
    each = width // parts
    lanes = max(each, 2 * HEAD_DIM)
    held = lanes // each
    return pl.pallas_call(
        output_weight_kernel,
        grid=(parts // held,),
        in_specs=[
            pl.BlockSpec((rows, lanes), lambda s: (0, s)),
            whole((rows, features)),
            whole((1, features)),
        ],
        out_specs=pl.BlockSpec((held, each + 16, features), lambda s: (s, 0, 0)),
        out_shape=jax.ShapeDtypeStruct((parts, each + 16, features), bf16),
        compiler_params=params(32, "arbitrary"),
        cost_estimate=cost(2 * rows * width * features, 4e6),
        name="output_weight_part",
    )(mixed, proj, dgain)


def dense_out_kernel(
    at_ref, own_ref, other_ref, wq_ref, wk_ref, wv_ref, gain_ref, dq_ref, dk_ref, dv_ref, dg_ref, wo_ref, dg2_ref
):
    chips, _, width = own_ref.shape
    rows = dq_ref.shape[0]
    pair = width // 2
    chip, core = at_ref[2], at_ref[3]
    total = jnp.zeros((rows, pair), f32)
    for k in range(chips):
        source = lax.rem(chip - k + chips, chips)
        a = jnp.where(core == 0, own_ref[k], other_ref[k]).astype(f32)
        b = jnp.where(core == 0, other_ref[k], own_ref[k]).astype(f32)
        q = jnp.concatenate([a[:rows, :pair], b[:rows, :pair]], axis=1)
        cols = pl.ds(pl.multiple_of(source * width, width), width)
        dq_ref[:, cols] = q
        made = q * wq_ref[:, cols].astype(f32)
        total += made[:, :pair] + made[:, pair:]
        a_kv, b_kv = a[:rows, pair:], b[:rows, pair:]
        lane = lax.broadcasted_iota(jnp.int32, a_kv.shape, 1)
        key = jnp.where(lane < HEAD_DIM, a_kv, pltpu.roll(b_kv, HEAD_DIM, 1))
        val = jnp.where(lane < HEAD_DIM, pltpu.roll(a_kv, HEAD_DIM, 1), b_kv)
        cols = pl.ds(pl.multiple_of(source * pair, pair), pair)
        dk_ref[:, cols] = key
        dv_ref[:, cols] = val
        total += key * wk_ref[:, cols].astype(f32) + val * wv_ref[:, cols].astype(f32)
        wo_ref[2 * source, 0] = a[rows : rows + wo_ref.shape[2]]
        wo_ref[2 * source + 1, 0] = b[rows : rows + wo_ref.shape[2]]
        if k == 0:
            dg2_ref[...] = a[rows + wo_ref.shape[2] :][:1]
    dg_ref[...] = jnp.sum(jnp.transpose(total), axis=0, keepdims=True) / gain_ref[...]


def dense_out_call(at, own, other, wq, wk, wv, gain, wo_shape):
    streams, parts, chips, held, width = own.shape
    features = wq.shape[0]
    groups = 2 * chips
    rows = features // (streams * parts)
    block_cols = wo_shape[1] // width
    per_block = streams * parts // block_cols
    wo_rows = wo_shape[0] // groups // per_block
    by_rows = lambda w: pl.BlockSpec((rows, w.shape[1]), lambda s, r, at: (s * parts + r, 0))
    taken = pl.BlockSpec(
        (None, None, chips, held, width), lambda s, r, at: (s, jnp.bitwise_xor(r, at[s]), 0, 0, 0)
    )
    gain_spec = pl.BlockSpec((1, rows), lambda s, r, at: (0, s * parts + r))
    outs = pl.pallas_call(
        dense_out_kernel,
        grid_spec=pltpu.PrefetchScalarGridSpec(
            num_scalar_prefetch=1,
            grid=(streams, parts),
            in_specs=[taken, taken, by_rows(wq), by_rows(wk), by_rows(wv), gain_spec],
            out_specs=[
                by_rows(wq),
                by_rows(wk),
                by_rows(wv),
                gain_spec,
                pl.BlockSpec(
                    (groups, 1, wo_rows, width),
                    lambda s, r, at: (
                        0,
                        lax.rem(s * parts + r, per_block),
                        0,
                        lax.div(s * parts + r, per_block),
                    ),
                ),
                pl.BlockSpec((1, width), lambda s, r, at: (0, lax.div(s * parts + r, per_block))),
            ],
        ),
        out_shape=[
            jax.ShapeDtypeStruct(wq.shape, f32),
            jax.ShapeDtypeStruct(wk.shape, f32),
            jax.ShapeDtypeStruct(wv.shape, f32),
            jax.ShapeDtypeStruct((1, features), f32),
            jax.ShapeDtypeStruct((groups, per_block, wo_rows, wo_shape[1]), f32),
            jax.ShapeDtypeStruct((1, wo_shape[1]), f32),
        ],
        compiler_params=params(48, "arbitrary", "arbitrary"),
        cost_estimate=cost(2 * wq.size, 2.4e7),
        name="dense_weights_out",
    )(at, own, other, wq, wk, wv, gain)
    return (*outs[:4], outs[4].reshape(wo_shape), outs[5])


def weights_out_kernel(wide_ref, wq_ref, wk_ref, wv_ref, gain_ref, dq_ref, dk_ref, dv_ref, dg_ref):
    groups, rows, width = wide_ref.shape
    pair = width // 2
    total = jnp.zeros((rows, pair), f32)
    for g in range(groups):
        part = wide_ref[g, :, :pair].astype(f32)
        at = slice(g * pair, (g + 1) * pair)
        dq_ref[:, at] = part
        total += part * wq_ref[:, at].astype(f32)
    for g in range(groups // 2):
        a = wide_ref[2 * g, :, pair:].astype(f32)
        b = wide_ref[2 * g + 1, :, pair:].astype(f32)
        lane = lax.broadcasted_iota(jnp.int32, a.shape, 1)
        at = slice(g * pair, (g + 1) * pair)
        k = jnp.where(lane < HEAD_DIM, a, pltpu.roll(b, HEAD_DIM, 1))
        v = jnp.where(lane < HEAD_DIM, pltpu.roll(a, HEAD_DIM, 1), b)
        dk_ref[:, at] = k
        dv_ref[:, at] = v
        total += k * wk_ref[:, at].astype(f32) + v * wv_ref[:, at].astype(f32)
    dg_ref[...] = jnp.sum(jnp.transpose(total), axis=0, keepdims=True) / gain_ref[...]


def weights_out_call(wide, wq, wk, wv, gain):
    chunks, groups, rows, width = wide.shape
    features = chunks * rows
    by_rows = lambda w: pl.BlockSpec((rows, w.shape[1]), lambda c: (c, 0))
    return pl.pallas_call(
        weights_out_kernel,
        grid=(chunks,),
        in_specs=[
            pl.BlockSpec((None, groups, rows, width), lambda c: (c, 0, 0, 0)),
            by_rows(wq),
            by_rows(wk),
            by_rows(wv),
            pl.BlockSpec((1, rows), lambda c: (0, c)),
        ],
        out_specs=[
            by_rows(wq),
            by_rows(wk),
            by_rows(wv),
            pl.BlockSpec((1, rows), lambda c: (0, c)),
        ],
        out_shape=[
            jax.ShapeDtypeStruct(wq.shape, f32),
            jax.ShapeDtypeStruct(wk.shape, f32),
            jax.ShapeDtypeStruct(wv.shape, f32),
            jax.ShapeDtypeStruct((1, features), f32),
        ],
        compiler_params=params(32, "arbitrary"),
        cost_estimate=cost(2 * wq.size, 1.6e7),
        name="attention_weights_out",
    )(wide, wq, wk, wv, gain)


def last_kernel(d_ref, wq_ref, wk_ref, wv_ref, x_ref, gain_ref, dmid_ref, out_ref):
    groups, rows, width = d_ref.shape
    pair = width // 2
    dq = jnp.concatenate([d_ref[g, :, :pair] for g in range(groups)], axis=1)
    grad = dot_nt(dq, wq_ref[...])
    keys, vals = [], []
    for at in range(groups // 2):
        a = d_ref[2 * at, :, pair:].astype(f32)
        b = d_ref[2 * at + 1, :, pair:].astype(f32)
        lane = lax.broadcasted_iota(jnp.int32, a.shape, 1)
        keys.append(jnp.where(lane < HEAD_DIM, a, pltpu.roll(b, HEAD_DIM, 1)).astype(bf16))
        vals.append(jnp.where(lane < HEAD_DIM, pltpu.roll(a, HEAD_DIM, 1), b).astype(bf16))
    grad = grad + dot_nt(jnp.concatenate(keys, axis=1), wk_ref[...])
    grad = grad + dot_nt(jnp.concatenate(vals, axis=1), wv_ref[...])
    x = x_ref[...].astype(f32)
    scale = lax.rsqrt(jnp.mean(x * x, axis=-1, keepdims=True) + norm_eps)
    unit = x * scale
    w = gain_ref[...] * grad
    out_ref[...] = dmid_ref[...] + scale * (w - unit * jnp.mean(w * unit, axis=-1, keepdims=True))


def last_call(d, wq, wk, wv, x, gain, dmid):
    rows, features = x.shape
    return pl.pallas_call(
        last_kernel,
        out_shape=jax.ShapeDtypeStruct((rows, features), f32),
        compiler_params=params(40),
        cost_estimate=cost(4 * rows * features * features, 8e6),
        name="input_gradient",
    )(d, wq, wk, wv, x, gain, dmid)


def swap(values, axis, bit):
    return lax.ppermute(values, axis, [(i, i ^ bit) for i in range(lax.axis_size(axis))])


def half_sum(values, axis, bit):
    half = values.shape[0] // 2
    upper = ((lax.axis_index(axis) & bit) > 0).astype(jnp.int32)
    came = swap(lax.dynamic_slice_in_dim(values, (1 - upper) * half, half), axis, bit)
    mine = lax.dynamic_slice_in_dim(values, upper * half, half)
    return (mine.astype(f32) + came.astype(f32)).astype(bf16)


def relative_sum(kept, sent, axis, bits):
    while True:
        kept = (kept.astype(f32) + swap(sent, axis, bits[0]).astype(f32)).astype(bf16)
        bits = bits[1:]
        if not bits:
            return kept
        half = kept.shape[0] // 2
        kept, sent = kept[:half], kept[half:]


def join_parts(stream, axis, bits):
    shape = stream.shape
    for bit in bits[::-1]:
        stream = jnp.stack([stream, swap(stream, axis, bit)])
    return stream.reshape(-1, *shape)


def body(
    layer_input,
    first_gain,
    query_weight,
    key_weight,
    value_weight,
    output_weight,
    second_gain,
    gate_weight,
    up_weight,
    down_weight,
    expert_ids,
    gate_values,
    positions,
    cotangent,
):
    micro, _, per_device, features = layer_input.shape
    devices = lax.axis_size("seq")
    replicas = lax.axis_size("dp")
    seq_place = lax.axis_index("seq")
    rows = micro * per_device
    local_experts = gate_weight.shape[0]
    groups = key_weight.shape[1] // HEAD_DIM
    pair = query_weight.shape[1] // groups
    copies = devices // groups

    dp_bits = [1 << i for i in range(replicas.bit_length() - 1)]

    def spread(blocks):
        if copies > 1:
            blocks = jnp.repeat(blocks, copies, axis=0)
        return lax.all_to_all(blocks, "seq", 0, 0, tiled=True)

    def unspread(blocks):
        return lax.all_to_all(blocks, "seq", 0, 0, tiled=True)[::copies]

    x = layer_input.reshape(rows, features)
    cot = cotangent.reshape(rows, features)
    gain_one = first_gain.reshape(1, features)
    gain_two = second_gain.reshape(1, features)
    pos_all = lax.all_to_all(
        jnp.broadcast_to(positions.reshape(1, rows), (devices, rows)), "seq", 0, 0, tiled=True
    )
    x_all = lax.all_gather(x, "seq", axis=0)
    cos_all, sin_all = rope_tables(pos_all.reshape(-1), pair)
    mine = seq_place * local_experts + jnp.arange(local_experts, dtype=jnp.int32)
    ids = expert_ids[:, 0]
    gates = gate_values[:, 0].astype(f32)
    routed = jnp.sum(
        jnp.where(ids[..., None] == mine, gates[..., None], 0.0), axis=2
    )
    routed = routed.reshape(micro, devices, per_device, local_experts)
    routed = jnp.transpose(routed, (1, 0, 2, 3)).reshape(devices * rows, local_experts)
    group = seq_place // copies
    w_own = jnp.concatenate(
        [
            lax.dynamic_slice_in_dim(query_weight, group * pair, pair, axis=1),
            lax.dynamic_slice_in_dim(key_weight, group * HEAD_DIM, HEAD_DIM, axis=1),
            lax.dynamic_slice_in_dim(value_weight, group * HEAD_DIM, HEAD_DIM, axis=1),
        ],
        axis=1,
    )
    cos_all, sin_all, routed, w_own = lax.optimization_barrier((cos_all, sin_all, routed, w_own))
    x_all, cot_then, cos_all, sin_all, routed, w_own = lax.optimization_barrier(
        (x_all, cot, cos_all, sin_all, routed, w_own)
    )
    cot_all = lax.all_gather(cot_then, "seq", axis=0)

    qkv, first_all = qkv_call(x_all, gain_one, cos_all, sin_all, w_own)
    qkv = qkv.reshape(devices, micro, per_device, 2 * pair)
    mix = attend_call(qkv)
    mix = unspread(mix.reshape(devices, rows, pair))
    mixed, middle, second_low = post_call(mix, output_weight, x, gain_two)

    chips = devices // 2
    chip, core = seq_place // 2, seq_place % 2
    onward = [(i, (i + 2) % devices) for i in range(devices)]
    dp_place = lax.axis_index("dp")
    first_bit = dp_place & 1
    last_bit = dp_place >> (len(dp_bits) - 1)
    held, kept, running, places = second_low, (), None, []
    for hop in range(chips):
        following = lax.ppermute(held, "seq", onward) if hop < chips - 1 else None
        other = swap(held, "seq", 1)
        source = 2 * ((chip - hop) % chips)
        place = jnp.stack([source + core, source + 1 - core, 1 - first_bit, 1 - last_bit])
        place = place.astype(jnp.int32)
        places.append(place[:2])
        dx, *kept = expert_call(
            hop, place, held, other, cot_all, routed, gate_weight, up_weight, down_weight, kept
        )
        if following is not None:
            following, dx = lax.optimization_barrier((following, dx))
        part = dx[0].astype(f32) + swap(dx[1], "seq", 1).astype(f32)
        if hop == 0:
            own_part = part
        else:
            if running is not None:
                part = part + running.astype(f32)
            part = part.astype(bf16)
            if following is not None:
                part, following = lax.optimization_barrier((part, following))
            else:
                part, kept = lax.optimization_barrier((part, kept))
            running = lax.ppermute(part, "seq", onward)
        held = following
    second_grad = (own_part + running.astype(f32)).astype(bf16)
    tokens, hidden_a, hidden_b, gate_low, up_low, slot_a, slot_b = kept

    def weight_parts(at, tokens, hidden_a, hidden_b, gate_low, up_low, slot_a, slot_b):
        pairs = (
            (tokens, gate_low[at]),
            (tokens, up_low[at]),
            (hidden_a[at], slot_a[at]),
            (hidden_b[at], slot_b[at]),
        )
        return [
            lax.dot_general(a, b, TN, preferred_element_type=f32).astype(bf16) for a, b in pairs
        ]

    leaving = weight_parts(0, *kept)
    part_bits = (dp_bits[0], dp_bits[-1], dp_bits[0], dp_bits[-1])
    stream_bits = (dp_bits, dp_bits[::-1])
    came = [swap(values, "dp", bit) for values, bit in zip(leaving, part_bits)]
    leaving, second_grad = lax.optimization_barrier((leaving, second_grad))

    mg_send, proj, middle_grad, gain_two_part = turn_call(
        second_grad, middle, gain_two, cot, output_weight, groups
    )
    mg = spread(mg_send)
    kept, _ = lax.optimization_barrier((kept, mg_send))
    mixed, proj, came[2:] = lax.optimization_barrier((mixed, proj, came[2:]))
    dense = output_weight_call(mixed, proj, gain_two_part, devices)
    dense_own = dense
    staying = weight_parts(1, *kept)
    turned = sum(((dp_place >> i) & 1) << (len(dp_bits) - 1 - i) for i in range(len(dp_bits)))
    part_at = jnp.stack([turned, dp_place]).astype(jnp.int32)
    low_at = jnp.bitwise_and(part_at, replicas // 2 - 1)
    keep_a, send_a, keep_b, send_b = part_sum_call(low_at, replicas // 2, came, staying)
    mg, keep_a, send_a, keep_b, send_b = lax.optimization_barrier(
        (mg, keep_a, send_a, keep_b, send_b)
    )
    streams = [
        relative_sum(keep_a, send_a, "dp", stream_bits[0][1:]),
        relative_sum(keep_b, send_b, "dp", stream_bits[1][1:]),
    ]
    dense = dense_own
    dense = lax.psum_scatter(dense, "seq", scatter_dimension=0)
    table_shape = (devices, micro, per_device, pair)
    dqkv = attend_back_call(
        qkv,
        mg.reshape(devices, micro, per_device, pair),
        cos_all.reshape(table_shape),
        sin_all.reshape(table_shape),
    )
    dqkv, streams = lax.optimization_barrier((dqkv, streams))
    expert_parts = [
        join_parts(v[0], "dp", bits[-1:]) for v, bits in zip(streams, stream_bits)
    ]
    back = unspread(dqkv.reshape(devices, rows, 2 * pair))
    d_all = dqkv.reshape(devices * rows, 2 * pair)
    first_tokens = first_all.reshape(devices * rows, features)
    part = lax.dot_general(first_tokens, d_all, TN, preferred_element_type=f32)
    dense = dense.reshape(dense.shape[-2], features)
    each = output_weight.shape[0] // devices
    if copies == 1:
        width = 2 * pair
        kept_pieces, sent_pieces = joint_call(part_at, part, dense, replicas)
        kept, sent_pieces = lax.optimization_barrier((kept, sent_pieces))
        moe_place = jnp.concatenate(places + [(1 - first_bit).astype(jnp.int32).reshape(1)])
        moe_all = moe_call(moe_place, kept[1], routed, down_weight, devices)
        moe = lax.psum_scatter(moe_all, "seq", scatter_dimension=0)
        layer_output = (middle + residual_scale * moe.astype(f32)).astype(bf16)
        own = [
            relative_sum(kept_pieces[at], sent_pieces[at], "dp", bits)
            for at, bits in enumerate(stream_bits)
        ]
        own = jnp.concatenate(own, axis=0)
        backward = [(i, (i - 2) % devices) for i in range(devices)]
        round_ring = {0: own}
        for k in range(1, chips // 2 + 1):
            round_ring[k] = lax.ppermute(round_ring[k - 1], "seq", onward)
            if chips - k > k:
                round_ring[chips - k] = lax.ppermute(
                    round_ring[(chips - k + 1) % chips], "seq", backward
                )
            if k == 1:
                round_ring[1], expert_parts = lax.optimization_barrier(
                    (round_ring[1], expert_parts)
                )
        held = jnp.stack([round_ring[k] for k in range(chips)])
    expert_parts = [
        join_parts(v, "dp", bits[:-1]).reshape(-1, *v.shape[-2:])
        for v, bits in zip(expert_parts, stream_bits)
    ]
    input_grad = last_call(
        back, query_weight, key_weight, value_weight, x, gain_one, middle_grad
    )
    if copies == 1:
        held, expert_parts, input_grad = lax.optimization_barrier((held, expert_parts, input_grad))
        gate_sum, up_sum, down_sum = expert_out_call(
            part_at, *expert_parts, gate_weight.shape, down_weight.shape
        )
        full = [join_parts(held[:, at], "dp", b) for at, b in enumerate(stream_bits)]
        full, gate_sum, up_sum, down_sum, layer_output = lax.optimization_barrier(
            (jnp.stack(full), gate_sum, up_sum, down_sum, layer_output)
        )
        other = swap(full, "seq", 1)
        where_at = jnp.stack([turned, dp_place, chip, core]).astype(jnp.int32)
        (
            query_weight_grad,
            key_weight_grad,
            value_weight_grad,
            first_gain_grad,
            output_weight_grad,
            second_gain_grad,
        ) = dense_out_call(
            where_at, full, other, query_weight, key_weight, value_weight, gain_one, output_weight.shape
        )
    else:
        gate_sum, up_sum, down_sum = expert_out_call(
            part_at, *expert_parts, gate_weight.shape, down_weight.shape
        )
        for bit in dp_bits:
            dense = (dense.astype(f32) + swap(dense, "dp", bit).astype(f32)).astype(bf16)
        dense = lax.all_gather(dense, "seq", axis=0).astype(f32)
        output_weight_grad = dense[:, :each].reshape(output_weight.shape)
        moe_place = jnp.concatenate(places + [(1 - first_bit).astype(jnp.int32).reshape(1)])
        moe_all = moe_call(moe_place, kept[1], routed, down_weight, devices)
        moe = lax.psum_scatter(moe_all, "seq", scatter_dimension=0)
        layer_output = (middle + residual_scale * moe.astype(f32)).astype(bf16)
        second_gain_grad = dense[0, each]
        part = part.astype(bf16)
        for bit in dp_bits[::-1]:
            part = half_sum(part, "dp", bit)
        wide = lax.all_gather(part, ("dp", "seq"), axis=0)
        wide = wide.reshape(replicas, devices, features // replicas, 2 * pair)[:, ::copies]
        query_weight_grad, key_weight_grad, value_weight_grad, first_gain_grad = weights_out_call(
            wide, query_weight, key_weight, value_weight, gain_one
        )
    second_gain_grad = second_gain_grad.reshape(features)
    return (
        layer_output.reshape(layer_input.shape),
        input_grad.reshape(layer_input.shape),
        first_gain_grad.reshape(features),
        query_weight_grad,
        key_weight_grad,
        value_weight_grad,
        output_weight_grad,
        second_gain_grad,
        gate_sum,
        up_sum,
        down_sum,
    )


def solution(mesh):
    return jax.shard_map(
        body,
        mesh=mesh,
        in_specs=(
            P(None, "dp", "seq", None),
            P(),
            P(),
            P(),
            P(),
            P(),
            P(),
            P("seq", None, None),
            P("seq", None, None),
            P("seq", None, None),
            P(None, "dp", None, None),
            P(None, "dp", None, None),
            P(None, "dp", "seq"),
            P(None, "dp", "seq", None),
        ),
        out_specs=(
            P(None, "dp", "seq", None),
            P(None, "dp", "seq", None),
            P(),
            P(),
            P(),
            P(),
            P(),
            P(),
            P("seq", None, None),
            P("seq", None, None),
            P("seq", None, None),
        ),
        check_vma=False,
    )
```

```python
from functools import partial

import jax
import jax.numpy as jnp
from jax import lax
from jax.experimental import pallas as pl
from jax.experimental.pallas import tpu as pltpu
from jax.sharding import PartitionSpec as P

HEAD_DIM = 64

rope_theta = 10000.0
attention_scale = 0.015625
residual_scale = 0.22
norm_eps = 1e-06
masked_score = -1e30

f32 = jnp.float32
bf16 = jnp.bfloat16
NT = (((1,), (1,)), ((), ()))
TN = (((0,), (0,)), ((), ()))


def dot(a, b):
    return jnp.dot(a, b, preferred_element_type=f32)


def dot_nt(a, b):
    return lax.dot_general(a, b, NT, preferred_element_type=f32)


def params(mib, *semantics):
    return pltpu.CompilerParams(
        vmem_limit_bytes=mib * 1024 * 1024, dimension_semantics=semantics or None
    )


def cost(flops, nbytes, trans=0):
    return pl.CostEstimate(
        flops=int(flops / 8), bytes_accessed=int(nbytes / 8), transcendentals=int(trans / 8)
    )


def whole(shape):
    return pl.BlockSpec(shape, lambda *_: (0,) * len(shape))


def rope_tables(positions, width):
    half = HEAD_DIM // 2
    exponent = jnp.arange(half, dtype=f32) * (-2.0 / HEAD_DIM)
    angles = positions.astype(f32)[:, None] * (rope_theta**exponent)[None, :]
    cosine, sine = jnp.cos(angles), jnp.sin(angles)
    copies = width // HEAD_DIM
    cos_row = jnp.concatenate([cosine, cosine] * copies, axis=1)
    sin_row = jnp.concatenate([-sine, sine] * copies, axis=1)
    return cos_row, sin_row


def partner(values):
    width = values.shape[1]
    half = HEAD_DIM // 2
    lane = lax.broadcasted_iota(jnp.int32, values.shape, 1)
    ahead = pltpu.roll(values, width - half, 1)
    behind = pltpu.roll(values, half, 1)
    return jnp.where(lane % HEAD_DIM < half, ahead, behind)


def qkv_kernel(x_ref, gain_ref, cos_ref, sin_ref, w_ref, qkv_ref, low_ref):
    pair = 2 * HEAD_DIM
    x = x_ref[0].astype(f32)
    scale = lax.rsqrt(jnp.mean(x * x, axis=-1, keepdims=True) + norm_eps)
    low = (x * scale * gain_ref[...]).astype(bf16)
    low_ref[0] = low
    cosine, sine = cos_ref[...], sin_ref[...]
    made = dot(low, w_ref[...])
    q, kv = made[:, :pair], made[:, pair:]
    q = (q * cosine + partner(q) * sine) * attention_scale
    qkv_ref[0, :, :pair] = q.astype(bf16)
    lane = lax.broadcasted_iota(jnp.int32, kv.shape, 1)
    turned = kv * cosine + partner(kv) * sine
    qkv_ref[0, :, pair:] = jnp.where(lane < HEAD_DIM, turned, kv).astype(bf16)


def qkv_call(x_all, gain, cos_all, sin_all, w_own):
    blocks, rows, features = x_all.shape
    pair = 2 * HEAD_DIM
    return pl.pallas_call(
        qkv_kernel,
        grid=(blocks,),
        in_specs=[
            pl.BlockSpec((1, rows, features), lambda s: (s, 0, 0)),
            whole((1, features)),
            pl.BlockSpec((rows, pair), lambda s: (s, 0)),
            pl.BlockSpec((rows, pair), lambda s: (s, 0)),
            whole(w_own.shape),
        ],
        out_specs=[
            pl.BlockSpec((1, rows, 2 * pair), lambda s: (s, 0, 0)),
            pl.BlockSpec((1, rows, features), lambda s: (s, 0, 0)),
        ],
        out_shape=[
            jax.ShapeDtypeStruct((blocks, rows, 2 * pair), bf16),
            jax.ShapeDtypeStruct((blocks, rows, features), bf16),
        ],
        compiler_params=params(58, "arbitrary"),
        cost_estimate=cost(4 * blocks * rows * features * pair, 14e6),
        name="norm_qkv_rope",
    )(x_all, gain, cos_all, sin_all, w_own)


def split_heads(block, first):
    wide = block.astype(f32)
    lane = lax.broadcasted_iota(jnp.int32, wide.shape, 1)
    turned = pltpu.roll(wide, HEAD_DIM, 1)
    if first:
        parts = [jnp.where(lane < HEAD_DIM, wide, 0.0), jnp.where(lane < HEAD_DIM, turned, 0.0)]
    else:
        parts = [jnp.where(lane >= HEAD_DIM, turned, 0.0), jnp.where(lane >= HEAD_DIM, wide, 0.0)]
    return jnp.concatenate(parts, axis=0).astype(bf16)


def join_heads(turned):
    rows = turned.shape[1] // 2
    return jnp.transpose(jnp.concatenate([turned[:, :rows], turned[:, rows:]], axis=0))


def scores_of(kv, q2, rows):
    scores = dot_nt(kv, q2)
    count = scores.shape[0]
    own = scores[count - rows :]
    key_at = lax.broadcasted_iota(jnp.int32, own.shape, 0)
    query_at = lax.broadcasted_iota(jnp.int32, own.shape, 1) % rows
    own = jnp.where(key_at <= query_at, own, masked_score)
    if count == rows:
        return own
    return jnp.concatenate([scores[: count - rows], own], axis=0)


def attend_kernel(qkv_ref, out_ref):
    blocks, _, rows, width = qkv_ref.shape
    pair = width // 2
    kv = qkv_ref[:, 0, :, pair:].reshape(blocks * rows, pair)
    kv_t = jnp.transpose(kv)
    for at in range(blocks):
        count = (at + 1) * rows
        q2 = split_heads(qkv_ref[at, 0, :, :pair], True)
        scores = scores_of(kv[:count], q2, rows)
        top = jnp.max(scores, axis=0, keepdims=True)
        weights = jnp.exp(scores - top)
        total = jnp.sum(weights, axis=0, keepdims=True)
        out_t = dot(kv_t[:, :count], weights.astype(bf16))
        out_ref[at, 0] = join_heads(out_t[HEAD_DIM:] / total).astype(bf16)


def attend_call(qkv):
    blocks, micro, rows, width = qkv.shape
    pair = width // 2
    length = blocks * rows
    return pl.pallas_call(
        attend_kernel,
        grid=(micro,),
        in_specs=[pl.BlockSpec((blocks, 1, rows, width), lambda m: (0, m, 0, 0))],
        out_specs=pl.BlockSpec((blocks, 1, rows, pair), lambda m: (0, m, 0, 0)),
        out_shape=jax.ShapeDtypeStruct((blocks, micro, rows, pair), bf16),
        compiler_params=params(48, "arbitrary"),
        cost_estimate=cost(
            micro * length * length * 512, 3 * qkv.size, micro * length * length
        ),
        name="attention_forward",
    )(qkv)


def attend_back_kernel(qkv_ref, grad_ref, cos_ref, sin_ref, out_ref, dkv_ref):
    blocks, _, rows, width = qkv_ref.shape
    pair = width // 2
    kv = qkv_ref[:, 0, :, pair:].reshape(blocks * rows, pair)
    kv_t = jnp.transpose(kv)
    dkv_ref[...] = jnp.zeros_like(dkv_ref)
    for at in range(blocks):
        count = (at + 1) * rows
        q2 = split_heads(qkv_ref[at, 0, :, :pair], True)
        g2 = split_heads(grad_ref[at, 0], False)
        scores = scores_of(kv[:count], q2, rows)
        top = jnp.max(scores, axis=0, keepdims=True)
        weights = jnp.exp(scores - top)
        total = jnp.sum(weights, axis=0, keepdims=True)
        prob = weights * (1.0 / total)
        prob_grad = dot_nt(kv[:count], g2)
        delta = jnp.sum(prob * prob_grad, axis=0, keepdims=True)
        score_grad = (prob * (prob_grad - delta)).astype(bf16)
        dkv_ref[:count] += dot(score_grad, q2) + dot(prob.astype(bf16), g2)
        dq_t = dot(kv_t[:, :count], score_grad)
        dq = join_heads(dq_t[:HEAD_DIM] * attention_scale)
        dq = dq * cos_ref[at, 0] - partner(dq) * sin_ref[at, 0]
        out_ref[at, 0, :, :pair] = dq.astype(bf16)
    for at in range(blocks):
        dkv = dkv_ref[at * rows : (at + 1) * rows]
        lane = lax.broadcasted_iota(jnp.int32, dkv.shape, 1)
        turned = dkv * cos_ref[at, 0] - partner(dkv) * sin_ref[at, 0]
        out_ref[at, 0, :, pair:] = jnp.where(lane < HEAD_DIM, turned, dkv).astype(bf16)


def attend_back_call(qkv, grads, cos_all, sin_all):
    blocks, micro, rows, width = qkv.shape
    pair = width // 2
    length = blocks * rows
    spec = lambda lanes: pl.BlockSpec((blocks, 1, rows, lanes), lambda m: (0, m, 0, 0))
    return pl.pallas_call(
        attend_back_kernel,
        grid=(micro,),
        in_specs=[spec(width), spec(pair), spec(pair), spec(pair)],
        out_specs=spec(width),
        out_shape=jax.ShapeDtypeStruct(qkv.shape, bf16),
        scratch_shapes=[pltpu.VMEM((length, pair), f32)],
        compiler_params=params(56, "arbitrary"),
        cost_estimate=cost(
            micro * length * length * 1280, 10 * qkv.size, micro * length * length
        ),
        name="attention_backward",
    )(qkv, grads, cos_all, sin_all)


def post_kernel(mix_ref, wo_ref, x_ref, gain_ref, mixed_ref, middle_ref, low_ref):
    mixed = jnp.concatenate([mix_ref[g] for g in range(mix_ref.shape[0])], axis=1)
    mixed_ref[...] = mixed
    middle = x_ref[...].astype(f32) + residual_scale * dot(mixed, wo_ref[...])
    middle_ref[...] = middle
    scale = lax.rsqrt(jnp.mean(middle * middle, axis=-1, keepdims=True) + norm_eps)
    low_ref[...] = (middle * scale * gain_ref[...]).astype(bf16)


def post_call(mix, wo, x, gain):
    rows, features = x.shape
    return pl.pallas_call(
        post_kernel,
        out_shape=[
            jax.ShapeDtypeStruct((rows, wo.shape[0]), bf16),
            jax.ShapeDtypeStruct((rows, features), f32),
            jax.ShapeDtypeStruct((rows, features), bf16),
        ],
        compiler_params=params(32),
        cost_estimate=cost(2 * rows * wo.size, 5e6),
        name="project_norm",
    )(mix, wo, x, gain)


def expert_kernel(place_ref, a_ref, b_ref, cot_ref, w_ref, wg_ref, wu_ref, wd_ref, *refs):
    dx_ref, x_ref, ha_ref, hb_ref, dg_ref, du_ref, sa_ref, sb_ref = refs[-8:]
    step = pl.program_id(0)
    first, second = place_ref[2], place_ref[3]
    half = sa_ref.shape[2]

    @pl.when(step == 0)
    def _():
        x_ref[...] = a_ref[...]

    @pl.when(step == 1)
    def _():
        x_ref[...] = b_ref[...]

    x = x_ref[...]
    cot = residual_scale * cot_ref[0].astype(f32)
    weight = w_ref[...]
    total = None
    for e in range(wg_ref.shape[0]):
        gate = dot(x, wg_ref[e])
        up = dot(x, wu_ref[e])
        slot_grad = (weight[:, e : e + 1] * cot).astype(bf16)
        to_a, to_b = jnp.bitwise_xor(first, e), jnp.bitwise_xor(second, e)
        sa_ref[to_a] = slot_grad[:, :half]
        sb_ref[to_b] = slot_grad[:, half:]
        hidden_grad = dot_nt(slot_grad, wd_ref[e])
        sig = 1.0 / (1.0 + jnp.exp(-gate))
        silu = gate * sig
        hidden = (silu * up).astype(bf16)
        ha_ref[to_a] = hidden
        hb_ref[to_b] = hidden
        gate_grad = (hidden_grad * up * (sig * (1.0 + gate * (1.0 - sig)))).astype(bf16)
        up_grad = (hidden_grad * silu).astype(bf16)
        dg_ref[to_a] = gate_grad
        du_ref[to_b] = up_grad
        term = dot_nt(gate_grad, wg_ref[e]) + dot_nt(up_grad, wu_ref[e])
        total = term if total is None else total + term
    dx_ref[0] = total.astype(bf16)


def expert_call(at, place, own, other, cot_all, weight, wg, wu, wd, kept):
    blocks, rows, features = cot_all.shape
    count, _, hidden = wg.shape
    tokens = blocks * rows
    inner = jax.ShapeDtypeStruct((count, tokens, hidden), bf16)
    outer = jax.ShapeDtypeStruct((count, tokens, features // 2), bf16)
    inner_spec = pl.BlockSpec((count, rows, hidden), lambda s, place: (0, 2 * at + s, 0))
    outer_spec = pl.BlockSpec((count, rows, features // 2), lambda s, place: (0, 2 * at + s, 0))
    fixed = lambda shape: pl.BlockSpec(shape, lambda s, place: (0,) * len(shape))
    any_spec = pl.BlockSpec(memory_space=pl.ANY)
    first = 8
    return pl.pallas_call(
        expert_kernel,
        grid_spec=pltpu.PrefetchScalarGridSpec(
            num_scalar_prefetch=1,
            grid=(2,),
            in_specs=[
                fixed((rows, features)),
                fixed((rows, features)),
                pl.BlockSpec((1, rows, features), lambda s, place: (place[s], 0, 0)),
                pl.BlockSpec((rows, count), lambda s, place: (place[s], 0)),
                fixed(wg.shape),
                fixed(wu.shape),
                fixed(wd.shape),
            ]
            + [any_spec] * len(kept),
            out_specs=[
                pl.BlockSpec((1, rows, features), lambda s, place: (s, 0, 0)),
                pl.BlockSpec((rows, features), lambda s, place: (2 * at + s, 0)),
            ]
            + [inner_spec] * 4
            + [outer_spec] * 2,
        ),
        out_shape=[
            jax.ShapeDtypeStruct((2, rows, features), bf16),
            jax.ShapeDtypeStruct((tokens, features), bf16),
            inner,
            inner,
            inner,
            inner,
            outer,
            outer,
        ],
        input_output_aliases={first + i: 1 + i for i in range(len(kept))},
        compiler_params=params(48, "arbitrary"),
        cost_estimate=cost(20 * rows * wg.size, 2e7, 2 * rows * hidden * count),
        name="experts",
    )(place, own, other, cot_all, weight, wg, wu, wd, *kept)


def part_sum_kernel(at_ref, *refs):
    inputs, outs = refs[:16], refs[16:]
    at = 0
    for out in outs:
        gate_came, gate_here, down_came, down_here = inputs[at : at + 4]
        rows = gate_came.shape[0]
        out[0, :rows] = (gate_came[...].astype(f32) + gate_here[...].astype(f32)).astype(bf16)
        out[0, rows:] = (down_came[...].astype(f32) + down_here[...].astype(f32)).astype(bf16)
        at += 4


def part_sum_call(at, per, came, here):
    gate_rows, down_rows = came[0].shape[0] // per, came[2].shape[0] // per
    width = came[0].shape[1]
    steps = per // 2
    specs, args, out_specs, out_shapes = [], [], [], []
    for stream in range(2):
        for sent in range(2):
            for which, rows in ((stream, gate_rows), (stream + 2, down_rows)):
                spec = pl.BlockSpec(
                    (rows, width),
                    lambda s, at, sent=sent, stream=stream: (
                        jnp.bitwise_xor(s + sent * steps, at[stream]),
                        0,
                    ),
                )
                specs += [spec, spec]
                args += [came[which], here[which]]
            out_specs.append(
                pl.BlockSpec((1, gate_rows + down_rows, width), lambda s, at: (s, 0, 0))
            )
            out_shapes.append(
                jax.ShapeDtypeStruct((steps, gate_rows + down_rows, width), bf16)
            )
    return pl.pallas_call(
        part_sum_kernel,
        grid_spec=pltpu.PrefetchScalarGridSpec(
            num_scalar_prefetch=1, grid=(steps,), in_specs=specs, out_specs=out_specs
        ),
        out_shape=out_shapes,
        compiler_params=params(48, "arbitrary"),
        cost_estimate=cost(0, 9e6),
        name="expert_part_sum",
    )(at, *args)


def joint_kernel(at_ref, *refs):
    for (part_ref, wo_ref, gain_ref), out_ref in ((refs[:3], refs[6]), (refs[3:6], refs[7])):
        rows = part_ref.shape[0]
        upto = rows + wo_ref.shape[0]
        out_ref[0, 0, :rows] = part_ref[...].astype(bf16)
        out_ref[0, 0, rows:upto] = wo_ref[...]
        out_ref[0, 0, upto:] = gain_ref[...]


def joint_call(at, part, dense, parts):
    features, width = part.shape
    pieces = 2 * parts
    rows = features // pieces
    block_cols = dense.shape[1] // width
    per_block = pieces // block_cols
    extra = 16
    wo_rows = (dense.shape[0] - extra) // per_block
    last = dense.shape[0] // extra - 1
    steps = parts // 2

    def piece(sent):
        return lambda s, p, at: s * parts + jnp.bitwise_xor(p + sent * steps, at[s])

    specs = []
    for sent in range(2):
        at_piece = piece(sent)
        specs.append(
            pl.BlockSpec((rows, width), lambda s, p, at, f=at_piece: (f(s, p, at), 0))
        )
        specs.append(
            pl.BlockSpec(
                (wo_rows, width),
                lambda s, p, at, f=at_piece: (
                    lax.rem(f(s, p, at), per_block),
                    lax.div(f(s, p, at), per_block),
                ),
            )
        )
        specs.append(
            pl.BlockSpec(
                (extra, width), lambda s, p, at, f=at_piece: (last, lax.div(f(s, p, at), per_block))
            )
        )
    out_spec = pl.BlockSpec((1, 1, rows + wo_rows + extra, width), lambda s, p, at: (s, p, 0, 0))
    out_shape = jax.ShapeDtypeStruct((2, steps, rows + wo_rows + extra, width), bf16)
    return pl.pallas_call(
        joint_kernel,
        grid_spec=pltpu.PrefetchScalarGridSpec(
            num_scalar_prefetch=1, grid=(2, steps), in_specs=specs, out_specs=[out_spec] * 2
        ),
        out_shape=[out_shape] * 2,
        compiler_params=params(32, "arbitrary", "arbitrary"),
        cost_estimate=cost(0, 2e6),
        name="dense_pieces",
    )(at, part, dense, dense, part, dense, dense)


def expert_out_kernel(at_ref, *refs):
    pieces, (gate_ref, up_ref, down_ref) = refs[:-3], refs[-3:]
    parts = len(pieces) // 2
    step = pl.program_id(0)
    rows = gate_ref.shape[1]
    half = down_ref.shape[2] // 2
    for which in range(parts):

        @pl.when(jnp.bitwise_xor(step, at_ref[0]) == which)
        def _():
            a_ref = pieces[which]
            gate_ref[0] = a_ref[:rows].astype(f32)
            down_ref[0, :, :half] = a_ref[rows:].astype(f32)

        @pl.when(jnp.bitwise_xor(step, at_ref[1]) == which)
        def _():
            b_ref = pieces[parts + which]
            up_ref[0] = b_ref[:rows].astype(f32)
            down_ref[0, :, half:] = b_ref[rows:].astype(f32)


def expert_out_call(at, a, b, gate_shape, down_shape):
    parts = len(a)
    held, width = a[0].shape
    count = gate_shape[0]
    per = parts // count
    gate_rows, down_rows = gate_shape[1] // per, down_shape[1] // per
    place = lambda r, at: (lax.div(r, per), lax.rem(r, per), 0)
    return pl.pallas_call(
        expert_out_kernel,
        grid_spec=pltpu.PrefetchScalarGridSpec(
            num_scalar_prefetch=1,
            grid=(parts,),
            in_specs=[pl.BlockSpec((held, width), lambda r, at: (0, 0))] * (2 * parts),
            out_specs=[
                pl.BlockSpec((1, gate_rows, gate_shape[2]), place),
                pl.BlockSpec((1, gate_rows, gate_shape[2]), place),
                pl.BlockSpec((1, down_rows, down_shape[2]), place),
            ],
        ),
        out_shape=[
            jax.ShapeDtypeStruct(gate_shape, f32),
            jax.ShapeDtypeStruct(gate_shape, f32),
            jax.ShapeDtypeStruct(down_shape, f32),
        ],
        compiler_params=params(40, "arbitrary"),
        cost_estimate=cost(0, 2e7),
        name="expert_weights_out",
    )(at, *a, *b)


def moe_kernel(place_ref, h_ref, w_ref, wd_ref, out_ref):
    weight = w_ref[...]
    total = None
    first = place_ref[pl.num_programs(0)]
    for e in range(wd_ref.shape[0]):
        term = weight[:, e : e + 1] * dot(h_ref[jnp.bitwise_xor(first, e)], wd_ref[e])
        total = term if total is None else total + term
    out_ref[0] = total.astype(bf16)


def moe_call(place, hidden, weight, wd, blocks):
    count, tokens, inner = hidden.shape
    features = wd.shape[2]
    rows = tokens // blocks
    return pl.pallas_call(
        moe_kernel,
        grid_spec=pltpu.PrefetchScalarGridSpec(
            num_scalar_prefetch=1,
            grid=(blocks,),
            in_specs=[
                pl.BlockSpec((count, rows, inner), lambda s, place: (0, s, 0)),
                pl.BlockSpec((rows, count), lambda s, place: (place[s], 0)),
                pl.BlockSpec(wd.shape, lambda s, place: (0, 0, 0)),
            ],
            out_specs=pl.BlockSpec((1, rows, features), lambda s, place: (place[s], 0, 0)),
        ),
        out_shape=jax.ShapeDtypeStruct((blocks, rows, features), bf16),
        compiler_params=params(32, "arbitrary"),
        cost_estimate=cost(2 * tokens * wd.size, 1.1e7),
        name="expert_outputs",
    )(place, hidden, weight, wd)


def turn_kernel(sg_ref, middle_ref, gain_ref, cot_ref, wo_ref, mg_ref, proj_ref, dmid_ref, dgain_ref):
    grad = sg_ref[...].astype(f32)
    middle = middle_ref[...]
    scale = lax.rsqrt(jnp.mean(middle * middle, axis=-1, keepdims=True) + norm_eps)
    unit = middle * scale
    dgain_ref[...] = jnp.sum(grad * unit, axis=0, keepdims=True)
    w = gain_ref[...] * grad
    dmid = cot_ref[...].astype(f32) + scale * (w - unit * jnp.mean(w * unit, axis=-1, keepdims=True))
    dmid_ref[...] = dmid
    proj = (residual_scale * dmid).astype(bf16)
    proj_ref[...] = proj
    mixed_grad = dot_nt(proj, wo_ref[...]).astype(bf16)
    groups, _, pair = mg_ref.shape
    for g in range(groups):
        mg_ref[g] = mixed_grad[:, g * pair : (g + 1) * pair]


def turn_call(sg, middle, gain, cot, wo, groups):
    rows, features = middle.shape
    pair = wo.shape[0] // groups
    return pl.pallas_call(
        turn_kernel,
        out_shape=[
            jax.ShapeDtypeStruct((groups, rows, pair), bf16),
            jax.ShapeDtypeStruct((rows, features), bf16),
            jax.ShapeDtypeStruct((rows, features), f32),
            jax.ShapeDtypeStruct((1, features), f32),
        ],
        compiler_params=params(32),
        cost_estimate=cost(2 * rows * wo.size, 6e6),
        name="norm_back_project_back",
    )(sg, middle, gain, cot, wo)


def output_weight_kernel(mixed_ref, proj_ref, dgain_ref, out_ref):
    held, each, features = out_ref.shape
    rows = mixed_ref.shape[1] // held
    part = lax.dot_general(mixed_ref[...], proj_ref[...], TN, preferred_element_type=f32)
    extra = jnp.broadcast_to(dgain_ref[...], (each - rows, features)).astype(bf16)
    for at in range(held):
        out_ref[at, :rows] = part[at * rows : (at + 1) * rows].astype(bf16)
        out_ref[at, rows:] = extra


def output_weight_call(mixed, proj, dgain, parts):
    rows, width = mixed.shape
    features = proj.shape[1]
    each = width // parts
    lanes = max(each, 2 * HEAD_DIM)
    held = lanes // each
    return pl.pallas_call(
        output_weight_kernel,
        grid=(parts // held,),
        in_specs=[
            pl.BlockSpec((rows, lanes), lambda s: (0, s)),
            whole((rows, features)),
            whole((1, features)),
        ],
        out_specs=pl.BlockSpec((held, each + 16, features), lambda s: (s, 0, 0)),
        out_shape=jax.ShapeDtypeStruct((parts, each + 16, features), bf16),
        compiler_params=params(32, "arbitrary"),
        cost_estimate=cost(2 * rows * width * features, 4e6),
        name="output_weight_part",
    )(mixed, proj, dgain)


def dense_out_kernel(
    at_ref, own_ref, other_ref, wq_ref, wk_ref, wv_ref, gain_ref, dq_ref, dk_ref, dv_ref, dg_ref, wo_ref, dg2_ref
):
    chips, _, width = own_ref.shape
    rows = dq_ref.shape[0]
    pair = width // 2
    chip, core = at_ref[2], at_ref[3]
    total = jnp.zeros((rows, pair), f32)
    for k in range(chips):
        source = lax.rem(chip - k + chips, chips)
        a = jnp.where(core == 0, own_ref[k], other_ref[k]).astype(f32)
        b = jnp.where(core == 0, other_ref[k], own_ref[k]).astype(f32)
        q = jnp.concatenate([a[:rows, :pair], b[:rows, :pair]], axis=1)
        cols = pl.ds(pl.multiple_of(source * width, width), width)
        dq_ref[:, cols] = q
        made = q * wq_ref[:, cols].astype(f32)
        total += made[:, :pair] + made[:, pair:]
        a_kv, b_kv = a[:rows, pair:], b[:rows, pair:]
        lane = lax.broadcasted_iota(jnp.int32, a_kv.shape, 1)
        key = jnp.where(lane < HEAD_DIM, a_kv, pltpu.roll(b_kv, HEAD_DIM, 1))
        val = jnp.where(lane < HEAD_DIM, pltpu.roll(a_kv, HEAD_DIM, 1), b_kv)
        cols = pl.ds(pl.multiple_of(source * pair, pair), pair)
        dk_ref[:, cols] = key
        dv_ref[:, cols] = val
        total += key * wk_ref[:, cols].astype(f32) + val * wv_ref[:, cols].astype(f32)
        wo_ref[2 * source, 0] = a[rows : rows + wo_ref.shape[2]]
        wo_ref[2 * source + 1, 0] = b[rows : rows + wo_ref.shape[2]]
        if k == 0:
            dg2_ref[...] = a[rows + wo_ref.shape[2] :][:1]
    dg_ref[...] = jnp.sum(jnp.transpose(total), axis=0, keepdims=True) / gain_ref[...]


def dense_out_call(at, own, other, wq, wk, wv, gain, wo_shape):
    streams, parts, chips, held, width = own.shape
    features = wq.shape[0]
    groups = 2 * chips
    rows = features // (streams * parts)
    block_cols = wo_shape[1] // width
    per_block = streams * parts // block_cols
    wo_rows = wo_shape[0] // groups // per_block
    by_rows = lambda w: pl.BlockSpec((rows, w.shape[1]), lambda s, r, at: (s * parts + r, 0))
    taken = pl.BlockSpec(
        (None, None, chips, held, width), lambda s, r, at: (s, jnp.bitwise_xor(r, at[s]), 0, 0, 0)
    )
    gain_spec = pl.BlockSpec((1, rows), lambda s, r, at: (0, s * parts + r))
    outs = pl.pallas_call(
        dense_out_kernel,
        grid_spec=pltpu.PrefetchScalarGridSpec(
            num_scalar_prefetch=1,
            grid=(streams, parts),
            in_specs=[taken, taken, by_rows(wq), by_rows(wk), by_rows(wv), gain_spec],
            out_specs=[
                by_rows(wq),
                by_rows(wk),
                by_rows(wv),
                gain_spec,
                pl.BlockSpec(
                    (groups, 1, wo_rows, width),
                    lambda s, r, at: (
                        0,
                        lax.rem(s * parts + r, per_block),
                        0,
                        lax.div(s * parts + r, per_block),
                    ),
                ),
                pl.BlockSpec((1, width), lambda s, r, at: (0, lax.div(s * parts + r, per_block))),
            ],
        ),
        out_shape=[
            jax.ShapeDtypeStruct(wq.shape, f32),
            jax.ShapeDtypeStruct(wk.shape, f32),
            jax.ShapeDtypeStruct(wv.shape, f32),
            jax.ShapeDtypeStruct((1, features), f32),
            jax.ShapeDtypeStruct((groups, per_block, wo_rows, wo_shape[1]), f32),
            jax.ShapeDtypeStruct((1, wo_shape[1]), f32),
        ],
        compiler_params=params(48, "arbitrary", "arbitrary"),
        cost_estimate=cost(2 * wq.size, 2.4e7),
        name="dense_weights_out",
    )(at, own, other, wq, wk, wv, gain)
    return (*outs[:4], outs[4].reshape(wo_shape), outs[5])


def weights_out_kernel(wide_ref, wq_ref, wk_ref, wv_ref, gain_ref, dq_ref, dk_ref, dv_ref, dg_ref):
    groups, rows, width = wide_ref.shape
    pair = width // 2
    total = jnp.zeros((rows, pair), f32)
    for g in range(groups):
        part = wide_ref[g, :, :pair].astype(f32)
        at = slice(g * pair, (g + 1) * pair)
        dq_ref[:, at] = part
        total += part * wq_ref[:, at].astype(f32)
    for g in range(groups // 2):
        a = wide_ref[2 * g, :, pair:].astype(f32)
        b = wide_ref[2 * g + 1, :, pair:].astype(f32)
        lane = lax.broadcasted_iota(jnp.int32, a.shape, 1)
        at = slice(g * pair, (g + 1) * pair)
        k = jnp.where(lane < HEAD_DIM, a, pltpu.roll(b, HEAD_DIM, 1))
        v = jnp.where(lane < HEAD_DIM, pltpu.roll(a, HEAD_DIM, 1), b)
        dk_ref[:, at] = k
        dv_ref[:, at] = v
        total += k * wk_ref[:, at].astype(f32) + v * wv_ref[:, at].astype(f32)
    dg_ref[...] = jnp.sum(jnp.transpose(total), axis=0, keepdims=True) / gain_ref[...]


def weights_out_call(wide, wq, wk, wv, gain):
    chunks, groups, rows, width = wide.shape
    features = chunks * rows
    by_rows = lambda w: pl.BlockSpec((rows, w.shape[1]), lambda c: (c, 0))
    return pl.pallas_call(
        weights_out_kernel,
        grid=(chunks,),
        in_specs=[
            pl.BlockSpec((None, groups, rows, width), lambda c: (c, 0, 0, 0)),
            by_rows(wq),
            by_rows(wk),
            by_rows(wv),
            pl.BlockSpec((1, rows), lambda c: (0, c)),
        ],
        out_specs=[
            by_rows(wq),
            by_rows(wk),
            by_rows(wv),
            pl.BlockSpec((1, rows), lambda c: (0, c)),
        ],
        out_shape=[
            jax.ShapeDtypeStruct(wq.shape, f32),
            jax.ShapeDtypeStruct(wk.shape, f32),
            jax.ShapeDtypeStruct(wv.shape, f32),
            jax.ShapeDtypeStruct((1, features), f32),
        ],
        compiler_params=params(32, "arbitrary"),
        cost_estimate=cost(2 * wq.size, 1.6e7),
        name="attention_weights_out",
    )(wide, wq, wk, wv, gain)


def last_kernel(d_ref, wq_ref, wk_ref, wv_ref, x_ref, gain_ref, dmid_ref, out_ref):
    groups, rows, width = d_ref.shape
    pair = width // 2
    dq = jnp.concatenate([d_ref[g, :, :pair] for g in range(groups)], axis=1)
    grad = dot_nt(dq, wq_ref[...])
    keys, vals = [], []
    for at in range(groups // 2):
        a = d_ref[2 * at, :, pair:].astype(f32)
        b = d_ref[2 * at + 1, :, pair:].astype(f32)
        lane = lax.broadcasted_iota(jnp.int32, a.shape, 1)
        keys.append(jnp.where(lane < HEAD_DIM, a, pltpu.roll(b, HEAD_DIM, 1)).astype(bf16))
        vals.append(jnp.where(lane < HEAD_DIM, pltpu.roll(a, HEAD_DIM, 1), b).astype(bf16))
    grad = grad + dot_nt(jnp.concatenate(keys, axis=1), wk_ref[...])
    grad = grad + dot_nt(jnp.concatenate(vals, axis=1), wv_ref[...])
    x = x_ref[...].astype(f32)
    scale = lax.rsqrt(jnp.mean(x * x, axis=-1, keepdims=True) + norm_eps)
    unit = x * scale
    w = gain_ref[...] * grad
    out_ref[...] = dmid_ref[...] + scale * (w - unit * jnp.mean(w * unit, axis=-1, keepdims=True))


def last_call(d, wq, wk, wv, x, gain, dmid):
    rows, features = x.shape
    return pl.pallas_call(
        last_kernel,
        out_shape=jax.ShapeDtypeStruct((rows, features), f32),
        compiler_params=params(40),
        cost_estimate=cost(4 * rows * features * features, 8e6),
        name="input_gradient",
    )(d, wq, wk, wv, x, gain, dmid)


def swap(values, axis, bit):
    return lax.ppermute(values, axis, [(i, i ^ bit) for i in range(lax.axis_size(axis))])


def half_sum(values, axis, bit):
    half = values.shape[0] // 2
    upper = ((lax.axis_index(axis) & bit) > 0).astype(jnp.int32)
    came = swap(lax.dynamic_slice_in_dim(values, (1 - upper) * half, half), axis, bit)
    mine = lax.dynamic_slice_in_dim(values, upper * half, half)
    return (mine.astype(f32) + came.astype(f32)).astype(bf16)


def relative_sum(kept, sent, axis, bits):
    while True:
        kept = (kept.astype(f32) + swap(sent, axis, bits[0]).astype(f32)).astype(bf16)
        bits = bits[1:]
        if not bits:
            return kept
        half = kept.shape[0] // 2
        kept, sent = kept[:half], kept[half:]


def join_parts(stream, axis, bits):
    shape = stream.shape
    for bit in bits[::-1]:
        stream = jnp.stack([stream, swap(stream, axis, bit)])
    return stream.reshape(-1, *shape)


def body(
    layer_input,
    first_gain,
    query_weight,
    key_weight,
    value_weight,
    output_weight,
    second_gain,
    gate_weight,
    up_weight,
    down_weight,
    expert_ids,
    gate_values,
    positions,
    cotangent,
):
    micro, _, per_device, features = layer_input.shape
    devices = lax.axis_size("seq")
    replicas = lax.axis_size("dp")
    seq_place = lax.axis_index("seq")
    rows = micro * per_device
    local_experts = gate_weight.shape[0]
    groups = key_weight.shape[1] // HEAD_DIM
    pair = query_weight.shape[1] // groups
    copies = devices // groups

    dp_bits = [1 << i for i in range(replicas.bit_length() - 1)]

    def spread(blocks):
        if copies > 1:
            blocks = jnp.repeat(blocks, copies, axis=0)
        return lax.all_to_all(blocks, "seq", 0, 0, tiled=True)

    def unspread(blocks):
        return lax.all_to_all(blocks, "seq", 0, 0, tiled=True)[::copies]

    x = layer_input.reshape(rows, features)
    cot = cotangent.reshape(rows, features)
    gain_one = first_gain.reshape(1, features)
    gain_two = second_gain.reshape(1, features)
    pos_all = lax.all_to_all(
        jnp.broadcast_to(positions.reshape(1, rows), (devices, rows)), "seq", 0, 0, tiled=True
    )
    x_all = lax.all_gather(x, "seq", axis=0)
    cos_all, sin_all = rope_tables(pos_all.reshape(-1), pair)
    mine = seq_place * local_experts + jnp.arange(local_experts, dtype=jnp.int32)
    ids = expert_ids[:, 0]
    gates = gate_values[:, 0].astype(f32)
    routed = jnp.sum(
        jnp.where(ids[..., None] == mine, gates[..., None], 0.0), axis=2
    )
    routed = routed.reshape(micro, devices, per_device, local_experts)
    routed = jnp.transpose(routed, (1, 0, 2, 3)).reshape(devices * rows, local_experts)
    group = seq_place // copies
    w_own = jnp.concatenate(
        [
            lax.dynamic_slice_in_dim(query_weight, group * pair, pair, axis=1),
            lax.dynamic_slice_in_dim(key_weight, group * HEAD_DIM, HEAD_DIM, axis=1),
            lax.dynamic_slice_in_dim(value_weight, group * HEAD_DIM, HEAD_DIM, axis=1),
        ],
        axis=1,
    )
    cos_all, sin_all, routed, w_own = lax.optimization_barrier((cos_all, sin_all, routed, w_own))
    x_all, cot_then, cos_all, sin_all, routed, w_own = lax.optimization_barrier(
        (x_all, cot, cos_all, sin_all, routed, w_own)
    )
    cot_all = lax.all_gather(cot_then, "seq", axis=0)

    qkv, first_all = qkv_call(x_all, gain_one, cos_all, sin_all, w_own)
    qkv = qkv.reshape(devices, micro, per_device, 2 * pair)
    mix = attend_call(qkv)
    mix = unspread(mix.reshape(devices, rows, pair))
    mixed, middle, second_low = post_call(mix, output_weight, x, gain_two)

    chips = devices // 2
    chip, core = seq_place // 2, seq_place % 2
    onward = [(i, (i + 2) % devices) for i in range(devices)]
    dp_place = lax.axis_index("dp")
    first_bit = dp_place & 1
    last_bit = dp_place >> (len(dp_bits) - 1)
    held, kept, running, places = second_low, (), None, []
    for hop in range(chips):
        following = lax.ppermute(held, "seq", onward) if hop < chips - 1 else None
        other = swap(held, "seq", 1)
        source = 2 * ((chip - hop) % chips)
        place = jnp.stack([source + core, source + 1 - core, 1 - first_bit, 1 - last_bit])
        place = place.astype(jnp.int32)
        places.append(place[:2])
        dx, *kept = expert_call(
            hop, place, held, other, cot_all, routed, gate_weight, up_weight, down_weight, kept
        )
        if following is not None:
            following, dx = lax.optimization_barrier((following, dx))
        part = dx[0].astype(f32) + swap(dx[1], "seq", 1).astype(f32)
        if hop == 0:
            own_part = part
        else:
            if running is not None:
                part = part + running.astype(f32)
            part = part.astype(bf16)
            if following is not None:
                part, following = lax.optimization_barrier((part, following))
            else:
                part, kept = lax.optimization_barrier((part, kept))
            running = lax.ppermute(part, "seq", onward)
        held = following
    second_grad = (own_part + running.astype(f32)).astype(bf16)
    tokens, hidden_a, hidden_b, gate_low, up_low, slot_a, slot_b = kept

    def weight_parts(at, tokens, hidden_a, hidden_b, gate_low, up_low, slot_a, slot_b):
        pairs = (
            (tokens, gate_low[at]),
            (tokens, up_low[at]),
            (hidden_a[at], slot_a[at]),
            (hidden_b[at], slot_b[at]),
        )
        return [
            lax.dot_general(a, b, TN, preferred_element_type=f32).astype(bf16) for a, b in pairs
        ]

    leaving = weight_parts(0, *kept)
    part_bits = (dp_bits[0], dp_bits[-1], dp_bits[0], dp_bits[-1])
    stream_bits = (dp_bits, dp_bits[::-1])
    came = [swap(values, "dp", bit) for values, bit in zip(leaving, part_bits)]
    leaving, second_grad = lax.optimization_barrier((leaving, second_grad))

    mg_send, proj, middle_grad, gain_two_part = turn_call(
        second_grad, middle, gain_two, cot, output_weight, groups
    )
    mg = spread(mg_send)
    kept, _ = lax.optimization_barrier((kept, mg_send))
    mixed, proj, came[2:] = lax.optimization_barrier((mixed, proj, came[2:]))
    dense = output_weight_call(mixed, proj, gain_two_part, devices)
    dense_own = dense
    staying = weight_parts(1, *kept)
    turned = sum(((dp_place >> i) & 1) << (len(dp_bits) - 1 - i) for i in range(len(dp_bits)))
    part_at = jnp.stack([turned, dp_place]).astype(jnp.int32)
    low_at = jnp.bitwise_and(part_at, replicas // 2 - 1)
    keep_a, send_a, keep_b, send_b = part_sum_call(low_at, replicas // 2, came, staying)
    mg, keep_a, send_a, keep_b, send_b = lax.optimization_barrier(
        (mg, keep_a, send_a, keep_b, send_b)
    )
    streams = [
        relative_sum(keep_a, send_a, "dp", stream_bits[0][1:]),
        relative_sum(keep_b, send_b, "dp", stream_bits[1][1:]),
    ]
    dense = dense_own
    dense = lax.psum_scatter(dense, "seq", scatter_dimension=0)
    table_shape = (devices, micro, per_device, pair)
    dqkv = attend_back_call(
        qkv,
        mg.reshape(devices, micro, per_device, pair),
        cos_all.reshape(table_shape),
        sin_all.reshape(table_shape),
    )
    dqkv, streams = lax.optimization_barrier((dqkv, streams))
    near = [
        [v[0], swap(v[0], "dp", bits[-1])] for v, bits in zip(streams, stream_bits)
    ]
    far = [[swap(v[0], "dp", bits[-2])] for v, bits in zip(streams, stream_bits)]
    back = unspread(dqkv.reshape(devices, rows, 2 * pair))
    d_all = dqkv.reshape(devices * rows, 2 * pair)
    first_tokens = first_all.reshape(devices * rows, features)
    part = lax.dot_general(first_tokens, d_all, TN, preferred_element_type=f32)
    dense = dense.reshape(dense.shape[-2], features)
    each = output_weight.shape[0] // devices
    if copies == 1:
        width = 2 * pair
        kept_pieces, sent_pieces = joint_call(part_at, part, dense, replicas)
        own = [
            relative_sum(kept_pieces[at], sent_pieces[at], "dp", bits)
            for at, bits in enumerate(stream_bits)
        ]
        own = jnp.concatenate(own, axis=0)
        kept, own = lax.optimization_barrier((kept, own))
        moe_place = jnp.concatenate(places + [(1 - first_bit).astype(jnp.int32).reshape(1)])
        moe_all = moe_call(moe_place, kept[1], routed, down_weight, devices)
        own, back, near = lax.optimization_barrier((own, back, near))
        backward = [(i, (i - 2) % devices) for i in range(devices)]
        round_ring = {0: own}
        for k in range(1, chips // 2 + 1):
            round_ring[k] = lax.ppermute(round_ring[k - 1], "seq", onward)
            if chips - k > k:
                round_ring[chips - k] = lax.ppermute(
                    round_ring[(chips - k + 1) % chips], "seq", backward
                )
        held = jnp.stack([round_ring[k] for k in range(chips)])
        held, moe_all, far = lax.optimization_barrier((held, moe_all, far))
        moe = lax.psum_scatter(moe_all, "seq", scatter_dimension=0)
        layer_output = (middle + residual_scale * moe.astype(f32)).astype(bf16)
    expert_pieces = []
    for (here, first), (second,), bits in zip(near, far, stream_bits):
        pieces = [here, first, second, swap(first, "dp", bits[-2])]
        for bit in bits[:-2][::-1]:
            pieces = pieces + [swap(p, "dp", bit) for p in pieces]
        expert_pieces.append(pieces)
    input_grad = last_call(
        back, query_weight, key_weight, value_weight, x, gain_one, middle_grad
    )
    if copies == 1:
        full = [join_parts(held[:, at], "dp", b) for at, b in enumerate(stream_bits)]
        full, input_grad = lax.optimization_barrier((jnp.stack(full), input_grad))
        other = swap(full, "seq", 1)
        where_at = jnp.stack([turned, dp_place, chip, core]).astype(jnp.int32)
        (
            query_weight_grad,
            key_weight_grad,
            value_weight_grad,
            first_gain_grad,
            output_weight_grad,
            second_gain_grad,
        ) = dense_out_call(
            where_at, full, other, query_weight, key_weight, value_weight, gain_one, output_weight.shape
        )
        query_weight_grad, expert_pieces = lax.optimization_barrier(
            (query_weight_grad, expert_pieces)
        )
    else:
        for bit in dp_bits:
            dense = (dense.astype(f32) + swap(dense, "dp", bit).astype(f32)).astype(bf16)
        dense = lax.all_gather(dense, "seq", axis=0).astype(f32)
        output_weight_grad = dense[:, :each].reshape(output_weight.shape)
        moe_place = jnp.concatenate(places + [(1 - first_bit).astype(jnp.int32).reshape(1)])
        moe_all = moe_call(moe_place, kept[1], routed, down_weight, devices)
        moe = lax.psum_scatter(moe_all, "seq", scatter_dimension=0)
        layer_output = (middle + residual_scale * moe.astype(f32)).astype(bf16)
        second_gain_grad = dense[0, each]
        part = part.astype(bf16)
        for bit in dp_bits[::-1]:
            part = half_sum(part, "dp", bit)
        wide = lax.all_gather(part, ("dp", "seq"), axis=0)
        wide = wide.reshape(replicas, devices, features // replicas, 2 * pair)[:, ::copies]
        query_weight_grad, key_weight_grad, value_weight_grad, first_gain_grad = weights_out_call(
            wide, query_weight, key_weight, value_weight, gain_one
        )
    second_gain_grad = second_gain_grad.reshape(features)
    gate_sum, up_sum, down_sum = expert_out_call(
        part_at, *expert_pieces, gate_weight.shape, down_weight.shape
    )
    return (
        layer_output.reshape(layer_input.shape),
        input_grad.reshape(layer_input.shape),
        first_gain_grad.reshape(features),
        query_weight_grad,
        key_weight_grad,
        value_weight_grad,
        output_weight_grad,
        second_gain_grad,
        gate_sum,
        up_sum,
        down_sum,
    )


def solution(mesh):
    return jax.shard_map(
        body,
        mesh=mesh,
        in_specs=(
            P(None, "dp", "seq", None),
            P(),
            P(),
            P(),
            P(),
            P(),
            P(),
            P("seq", None, None),
            P("seq", None, None),
            P("seq", None, None),
            P(None, "dp", None, None),
            P(None, "dp", None, None),
            P(None, "dp", "seq"),
            P(None, "dp", "seq", None),
        ),
        out_specs=(
            P(None, "dp", "seq", None),
            P(None, "dp", "seq", None),
            P(),
            P(),
            P(),
            P(),
            P(),
            P(),
            P("seq", None, None),
            P("seq", None, None),
            P("seq", None, None),
        ),
        check_vma=False,
    )
```

```python
from functools import partial

import jax
import jax.numpy as jnp
from jax import lax
from jax.experimental import pallas as pl
from jax.experimental.pallas import tpu as pltpu
from jax.sharding import PartitionSpec as P

HEAD_DIM = 64

rope_theta = 10000.0
attention_scale = 0.015625
residual_scale = 0.22
norm_eps = 1e-06
masked_score = -1e30

f32 = jnp.float32
bf16 = jnp.bfloat16
NT = (((1,), (1,)), ((), ()))
TN = (((0,), (0,)), ((), ()))


def dot(a, b):
    return jnp.dot(a, b, preferred_element_type=f32)


def dot_nt(a, b):
    return lax.dot_general(a, b, NT, preferred_element_type=f32)


def params(mib, *semantics):
    return pltpu.CompilerParams(
        vmem_limit_bytes=mib * 1024 * 1024, dimension_semantics=semantics or None
    )


def cost(flops, nbytes, trans=0):
    return pl.CostEstimate(
        flops=int(flops / 8), bytes_accessed=int(nbytes / 8), transcendentals=int(trans / 8)
    )


def whole(shape):
    return pl.BlockSpec(shape, lambda *_: (0,) * len(shape))


def rope_tables(positions, width):
    half = HEAD_DIM // 2
    exponent = jnp.arange(half, dtype=f32) * (-2.0 / HEAD_DIM)
    angles = positions.astype(f32)[:, None] * (rope_theta**exponent)[None, :]
    cosine, sine = jnp.cos(angles), jnp.sin(angles)
    copies = width // HEAD_DIM
    cos_row = jnp.concatenate([cosine, cosine] * copies, axis=1)
    sin_row = jnp.concatenate([-sine, sine] * copies, axis=1)
    return cos_row, sin_row


def partner(values):
    width = values.shape[1]
    half = HEAD_DIM // 2
    lane = lax.broadcasted_iota(jnp.int32, values.shape, 1)
    ahead = pltpu.roll(values, width - half, 1)
    behind = pltpu.roll(values, half, 1)
    return jnp.where(lane % HEAD_DIM < half, ahead, behind)


def qkv_kernel(x_ref, gain_ref, cos_ref, sin_ref, w_ref, qkv_ref, low_ref):
    pair = 2 * HEAD_DIM
    x = x_ref[0].astype(f32)
    scale = lax.rsqrt(jnp.mean(x * x, axis=-1, keepdims=True) + norm_eps)
    low = (x * scale * gain_ref[...]).astype(bf16)
    low_ref[0] = low
    cosine, sine = cos_ref[...], sin_ref[...]
    made = dot(low, w_ref[...])
    q, kv = made[:, :pair], made[:, pair:]
    q = (q * cosine + partner(q) * sine) * attention_scale
    qkv_ref[0, :, :pair] = q.astype(bf16)
    lane = lax.broadcasted_iota(jnp.int32, kv.shape, 1)
    turned = kv * cosine + partner(kv) * sine
    qkv_ref[0, :, pair:] = jnp.where(lane < HEAD_DIM, turned, kv).astype(bf16)


def qkv_call(x_all, gain, cos_all, sin_all, w_own):
    blocks, rows, features = x_all.shape
    pair = 2 * HEAD_DIM
    return pl.pallas_call(
        qkv_kernel,
        grid=(blocks,),
        in_specs=[
            pl.BlockSpec((1, rows, features), lambda s: (s, 0, 0)),
            whole((1, features)),
            pl.BlockSpec((rows, pair), lambda s: (s, 0)),
            pl.BlockSpec((rows, pair), lambda s: (s, 0)),
            whole(w_own.shape),
        ],
        out_specs=[
            pl.BlockSpec((1, rows, 2 * pair), lambda s: (s, 0, 0)),
            pl.BlockSpec((1, rows, features), lambda s: (s, 0, 0)),
        ],
        out_shape=[
            jax.ShapeDtypeStruct((blocks, rows, 2 * pair), bf16),
            jax.ShapeDtypeStruct((blocks, rows, features), bf16),
        ],
        compiler_params=params(58, "arbitrary"),
        cost_estimate=cost(4 * blocks * rows * features * pair, 14e6),
        name="norm_qkv_rope",
    )(x_all, gain, cos_all, sin_all, w_own)


def split_heads(block, first):
    wide = block.astype(f32)
    lane = lax.broadcasted_iota(jnp.int32, wide.shape, 1)
    turned = pltpu.roll(wide, HEAD_DIM, 1)
    if first:
        parts = [jnp.where(lane < HEAD_DIM, wide, 0.0), jnp.where(lane < HEAD_DIM, turned, 0.0)]
    else:
        parts = [jnp.where(lane >= HEAD_DIM, turned, 0.0), jnp.where(lane >= HEAD_DIM, wide, 0.0)]
    return jnp.concatenate(parts, axis=0).astype(bf16)


def join_heads(turned):
    rows = turned.shape[1] // 2
    return jnp.transpose(jnp.concatenate([turned[:, :rows], turned[:, rows:]], axis=0))


def scores_of(kv, q2, rows):
    scores = dot_nt(kv, q2)
    count = scores.shape[0]
    own = scores[count - rows :]
    key_at = lax.broadcasted_iota(jnp.int32, own.shape, 0)
    query_at = lax.broadcasted_iota(jnp.int32, own.shape, 1) % rows
    own = jnp.where(key_at <= query_at, own, masked_score)
    if count == rows:
        return own
    return jnp.concatenate([scores[: count - rows], own], axis=0)


def attend_kernel(qkv_ref, out_ref):
    blocks, _, rows, width = qkv_ref.shape
    pair = width // 2
    kv = qkv_ref[:, 0, :, pair:].reshape(blocks * rows, pair)
    kv_t = jnp.transpose(kv)
    for at in range(blocks):
        count = (at + 1) * rows
        q2 = split_heads(qkv_ref[at, 0, :, :pair], True)
        scores = scores_of(kv[:count], q2, rows)
        top = jnp.max(scores, axis=0, keepdims=True)
        weights = jnp.exp(scores - top)
        total = jnp.sum(weights, axis=0, keepdims=True)
        out_t = dot(kv_t[:, :count], weights.astype(bf16))
        out_ref[at, 0] = join_heads(out_t[HEAD_DIM:] / total).astype(bf16)


def attend_call(qkv):
    blocks, micro, rows, width = qkv.shape
    pair = width // 2
    length = blocks * rows
    return pl.pallas_call(
        attend_kernel,
        grid=(micro,),
        in_specs=[pl.BlockSpec((blocks, 1, rows, width), lambda m: (0, m, 0, 0))],
        out_specs=pl.BlockSpec((blocks, 1, rows, pair), lambda m: (0, m, 0, 0)),
        out_shape=jax.ShapeDtypeStruct((blocks, micro, rows, pair), bf16),
        compiler_params=params(48, "arbitrary"),
        cost_estimate=cost(
            micro * length * length * 512, 3 * qkv.size, micro * length * length
        ),
        name="attention_forward",
    )(qkv)


def attend_back_kernel(qkv_ref, grad_ref, cos_ref, sin_ref, out_ref, dkv_ref):
    blocks, _, rows, width = qkv_ref.shape
    pair = width // 2
    kv = qkv_ref[:, 0, :, pair:].reshape(blocks * rows, pair)
    kv_t = jnp.transpose(kv)
    dkv_ref[...] = jnp.zeros_like(dkv_ref)
    for at in range(blocks):
        count = (at + 1) * rows
        q2 = split_heads(qkv_ref[at, 0, :, :pair], True)
        g2 = split_heads(grad_ref[at, 0], False)
        scores = scores_of(kv[:count], q2, rows)
        top = jnp.max(scores, axis=0, keepdims=True)
        weights = jnp.exp(scores - top)
        total = jnp.sum(weights, axis=0, keepdims=True)
        prob = weights * (1.0 / total)
        prob_grad = dot_nt(kv[:count], g2)
        delta = jnp.sum(prob * prob_grad, axis=0, keepdims=True)
        score_grad = (prob * (prob_grad - delta)).astype(bf16)
        dkv_ref[:count] += dot(score_grad, q2) + dot(prob.astype(bf16), g2)
        dq_t = dot(kv_t[:, :count], score_grad)
        dq = join_heads(dq_t[:HEAD_DIM] * attention_scale)
        dq = dq * cos_ref[at, 0] - partner(dq) * sin_ref[at, 0]
        out_ref[at, 0, :, :pair] = dq.astype(bf16)
    for at in range(blocks):
        dkv = dkv_ref[at * rows : (at + 1) * rows]
        lane = lax.broadcasted_iota(jnp.int32, dkv.shape, 1)
        turned = dkv * cos_ref[at, 0] - partner(dkv) * sin_ref[at, 0]
        out_ref[at, 0, :, pair:] = jnp.where(lane < HEAD_DIM, turned, dkv).astype(bf16)


def attend_back_call(qkv, grads, cos_all, sin_all):
    blocks, micro, rows, width = qkv.shape
    pair = width // 2
    length = blocks * rows
    spec = lambda lanes: pl.BlockSpec((blocks, 1, rows, lanes), lambda m: (0, m, 0, 0))
    return pl.pallas_call(
        attend_back_kernel,
        grid=(micro,),
        in_specs=[spec(width), spec(pair), spec(pair), spec(pair)],
        out_specs=spec(width),
        out_shape=jax.ShapeDtypeStruct(qkv.shape, bf16),
        scratch_shapes=[pltpu.VMEM((length, pair), f32)],
        compiler_params=params(56, "arbitrary"),
        cost_estimate=cost(
            micro * length * length * 1280, 10 * qkv.size, micro * length * length
        ),
        name="attention_backward",
    )(qkv, grads, cos_all, sin_all)


def post_kernel(mix_ref, wo_ref, x_ref, gain_ref, mixed_ref, middle_ref, low_ref):
    mixed = jnp.concatenate([mix_ref[g] for g in range(mix_ref.shape[0])], axis=1)
    mixed_ref[...] = mixed
    middle = x_ref[...].astype(f32) + residual_scale * dot(mixed, wo_ref[...])
    middle_ref[...] = middle
    scale = lax.rsqrt(jnp.mean(middle * middle, axis=-1, keepdims=True) + norm_eps)
    low_ref[...] = (middle * scale * gain_ref[...]).astype(bf16)


def post_call(mix, wo, x, gain):
    rows, features = x.shape
    return pl.pallas_call(
        post_kernel,
        out_shape=[
            jax.ShapeDtypeStruct((rows, wo.shape[0]), bf16),
            jax.ShapeDtypeStruct((rows, features), f32),
            jax.ShapeDtypeStruct((rows, features), bf16),
        ],
        compiler_params=params(32),
        cost_estimate=cost(2 * rows * wo.size, 5e6),
        name="project_norm",
    )(mix, wo, x, gain)


def expert_kernel(place_ref, a_ref, b_ref, cot_ref, w_ref, wg_ref, wu_ref, wd_ref, *refs):
    dx_ref, x_ref, ha_ref, hb_ref, dg_ref, du_ref, sa_ref, sb_ref = refs[-8:]
    step = pl.program_id(0)
    first, second = place_ref[2], place_ref[3]
    half = sa_ref.shape[2]

    @pl.when(step == 0)
    def _():
        x_ref[...] = a_ref[...]

    @pl.when(step == 1)
    def _():
        x_ref[...] = b_ref[...]

    x = x_ref[...]
    cot = cot_ref[0].astype(f32)
    weight = residual_scale * w_ref[...]
    total = None
    for e in range(wg_ref.shape[0]):
        gate = dot(x, wg_ref[e])
        up = dot(x, wu_ref[e])
        slot_grad = (weight[:, e : e + 1] * cot).astype(bf16)
        to_a, to_b = jnp.bitwise_xor(first, e), jnp.bitwise_xor(second, e)
        sa_ref[to_a] = slot_grad[:, :half]
        sb_ref[to_b] = slot_grad[:, half:]
        hidden_grad = dot_nt(slot_grad, wd_ref[e])
        sig = 0.5 * jnp.tanh(0.5 * gate) + 0.5
        silu = gate * sig
        hidden = (silu * up).astype(bf16)
        ha_ref[to_a] = hidden
        hb_ref[to_b] = hidden
        gate_grad = (hidden_grad * up * (sig + silu * (1.0 - sig))).astype(bf16)
        up_grad = (hidden_grad * silu).astype(bf16)
        dg_ref[to_a] = gate_grad
        du_ref[to_b] = up_grad
        term = dot_nt(gate_grad, wg_ref[e]) + dot_nt(up_grad, wu_ref[e])
        total = term if total is None else total + term
    dx_ref[0] = total.astype(bf16)


def expert_call(at, place, own, other, cot_all, weight, wg, wu, wd, kept):
    blocks, rows, features = cot_all.shape
    count, _, hidden = wg.shape
    tokens = blocks * rows
    inner = jax.ShapeDtypeStruct((count, tokens, hidden), bf16)
    outer = jax.ShapeDtypeStruct((count, tokens, features // 2), bf16)
    inner_spec = pl.BlockSpec((count, rows, hidden), lambda s, place: (0, 2 * at + s, 0))
    outer_spec = pl.BlockSpec((count, rows, features // 2), lambda s, place: (0, 2 * at + s, 0))
    fixed = lambda shape: pl.BlockSpec(shape, lambda s, place: (0,) * len(shape))
    any_spec = pl.BlockSpec(memory_space=pl.ANY)
    first = 8
    return pl.pallas_call(
        expert_kernel,
        grid_spec=pltpu.PrefetchScalarGridSpec(
            num_scalar_prefetch=1,
            grid=(2,),
            in_specs=[
                fixed((rows, features)),
                fixed((rows, features)),
                pl.BlockSpec((1, rows, features), lambda s, place: (place[s], 0, 0)),
                pl.BlockSpec((rows, count), lambda s, place: (place[s], 0)),
                fixed(wg.shape),
                fixed(wu.shape),
                fixed(wd.shape),
            ]
            + [any_spec] * len(kept),
            out_specs=[
                pl.BlockSpec((1, rows, features), lambda s, place: (s, 0, 0)),
                pl.BlockSpec((rows, features), lambda s, place: (2 * at + s, 0)),
            ]
            + [inner_spec] * 4
            + [outer_spec] * 2,
        ),
        out_shape=[
            jax.ShapeDtypeStruct((2, rows, features), bf16),
            jax.ShapeDtypeStruct((tokens, features), bf16),
            inner,
            inner,
            inner,
            inner,
            outer,
            outer,
        ],
        input_output_aliases={first + i: 1 + i for i in range(len(kept))},
        compiler_params=params(48, "arbitrary"),
        cost_estimate=cost(20 * rows * wg.size, 2e7, 2 * rows * hidden * count),
        name="experts",
    )(place, own, other, cot_all, weight, wg, wu, wd, *kept)


def part_sum_kernel(at_ref, *refs):
    inputs, outs = refs[:16], refs[16:]
    at = 0
    for out in outs:
        gate_came, gate_here, down_came, down_here = inputs[at : at + 4]
        rows = gate_came.shape[0]
        out[0, :rows] = (gate_came[...].astype(f32) + gate_here[...].astype(f32)).astype(bf16)
        out[0, rows:] = (down_came[...].astype(f32) + down_here[...].astype(f32)).astype(bf16)
        at += 4


def part_sum_call(at, per, came, here):
    gate_rows, down_rows = came[0].shape[0] // per, came[2].shape[0] // per
    width = came[0].shape[1]
    steps = per // 2
    specs, args, out_specs, out_shapes = [], [], [], []
    for stream in range(2):
        for sent in range(2):
            for which, rows in ((stream, gate_rows), (stream + 2, down_rows)):
                spec = pl.BlockSpec(
                    (rows, width),
                    lambda s, at, sent=sent, stream=stream: (
                        jnp.bitwise_xor(s + sent * steps, at[stream]),
                        0,
                    ),
                )
                specs += [spec, spec]
                args += [came[which], here[which]]
            out_specs.append(
                pl.BlockSpec((1, gate_rows + down_rows, width), lambda s, at: (s, 0, 0))
            )
            out_shapes.append(
                jax.ShapeDtypeStruct((steps, gate_rows + down_rows, width), bf16)
            )
    return pl.pallas_call(
        part_sum_kernel,
        grid_spec=pltpu.PrefetchScalarGridSpec(
            num_scalar_prefetch=1, grid=(steps,), in_specs=specs, out_specs=out_specs
        ),
        out_shape=out_shapes,
        compiler_params=params(48, "arbitrary"),
        cost_estimate=cost(0, 9e6),
        name="expert_part_sum",
    )(at, *args)


def joint_kernel(at_ref, *refs):
    for (part_ref, wo_ref, gain_ref), out_ref in ((refs[:3], refs[6]), (refs[3:6], refs[7])):
        rows = part_ref.shape[0]
        upto = rows + wo_ref.shape[0]
        out_ref[0, 0, :rows] = part_ref[...].astype(bf16)
        out_ref[0, 0, rows:upto] = wo_ref[...]
        out_ref[0, 0, upto:] = gain_ref[...]


def joint_call(at, part, dense, parts):
    features, width = part.shape
    pieces = 2 * parts
    rows = features // pieces
    block_cols = dense.shape[1] // width
    per_block = pieces // block_cols
    extra = 16
    wo_rows = (dense.shape[0] - extra) // per_block
    last = dense.shape[0] // extra - 1
    steps = parts // 2

    def piece(sent):
        return lambda s, p, at: s * parts + jnp.bitwise_xor(p + sent * steps, at[s])

    specs = []
    for sent in range(2):
        at_piece = piece(sent)
        specs.append(
            pl.BlockSpec((rows, width), lambda s, p, at, f=at_piece: (f(s, p, at), 0))
        )
        specs.append(
            pl.BlockSpec(
                (wo_rows, width),
                lambda s, p, at, f=at_piece: (
                    lax.rem(f(s, p, at), per_block),
                    lax.div(f(s, p, at), per_block),
                ),
            )
        )
        specs.append(
            pl.BlockSpec(
                (extra, width), lambda s, p, at, f=at_piece: (last, lax.div(f(s, p, at), per_block))
            )
        )
    out_spec = pl.BlockSpec((1, 1, rows + wo_rows + extra, width), lambda s, p, at: (s, p, 0, 0))
    out_shape = jax.ShapeDtypeStruct((2, steps, rows + wo_rows + extra, width), bf16)
    return pl.pallas_call(
        joint_kernel,
        grid_spec=pltpu.PrefetchScalarGridSpec(
            num_scalar_prefetch=1, grid=(2, steps), in_specs=specs, out_specs=[out_spec] * 2
        ),
        out_shape=[out_shape] * 2,
        compiler_params=params(32, "arbitrary", "arbitrary"),
        cost_estimate=cost(0, 2e6),
        name="dense_pieces",
    )(at, part, dense, dense, part, dense, dense)


def expert_out_kernel(at_ref, *refs):
    pieces, (gate_ref, up_ref, down_ref) = refs[:-3], refs[-3:]
    parts = len(pieces) // 2
    step = pl.program_id(0)
    rows = gate_ref.shape[1]
    half = down_ref.shape[2] // 2
    for which in range(parts):

        @pl.when(jnp.bitwise_xor(step, at_ref[0]) == which)
        def _():
            a_ref = pieces[which]
            gate_ref[0] = a_ref[:rows].astype(f32)
            down_ref[0, :, :half] = a_ref[rows:].astype(f32)

        @pl.when(jnp.bitwise_xor(step, at_ref[1]) == which)
        def _():
            b_ref = pieces[parts + which]
            up_ref[0] = b_ref[:rows].astype(f32)
            down_ref[0, :, half:] = b_ref[rows:].astype(f32)


def expert_out_call(at, a, b, gate_shape, down_shape):
    parts = len(a)
    held, width = a[0].shape
    count = gate_shape[0]
    per = parts // count
    gate_rows, down_rows = gate_shape[1] // per, down_shape[1] // per
    place = lambda r, at: (lax.div(r, per), lax.rem(r, per), 0)
    return pl.pallas_call(
        expert_out_kernel,
        grid_spec=pltpu.PrefetchScalarGridSpec(
            num_scalar_prefetch=1,
            grid=(parts,),
            in_specs=[pl.BlockSpec((held, width), lambda r, at: (0, 0))] * (2 * parts),
            out_specs=[
                pl.BlockSpec((1, gate_rows, gate_shape[2]), place),
                pl.BlockSpec((1, gate_rows, gate_shape[2]), place),
                pl.BlockSpec((1, down_rows, down_shape[2]), place),
            ],
        ),
        out_shape=[
            jax.ShapeDtypeStruct(gate_shape, f32),
            jax.ShapeDtypeStruct(gate_shape, f32),
            jax.ShapeDtypeStruct(down_shape, f32),
        ],
        compiler_params=params(40, "arbitrary"),
        cost_estimate=cost(0, 2e7),
        name="expert_weights_out",
    )(at, *a, *b)


def moe_kernel(place_ref, h_ref, w_ref, wd_ref, out_ref):
    weight = w_ref[...]
    total = None
    first = place_ref[pl.num_programs(0)]
    for e in range(wd_ref.shape[0]):
        term = weight[:, e : e + 1] * dot(h_ref[jnp.bitwise_xor(first, e)], wd_ref[e])
        total = term if total is None else total + term
    out_ref[0] = total.astype(bf16)


def moe_call(place, hidden, weight, wd, blocks):
    count, tokens, inner = hidden.shape
    features = wd.shape[2]
    rows = tokens // blocks
    return pl.pallas_call(
        moe_kernel,
        grid_spec=pltpu.PrefetchScalarGridSpec(
            num_scalar_prefetch=1,
            grid=(blocks,),
            in_specs=[
                pl.BlockSpec((count, rows, inner), lambda s, place: (0, s, 0)),
                pl.BlockSpec((rows, count), lambda s, place: (place[s], 0)),
                pl.BlockSpec(wd.shape, lambda s, place: (0, 0, 0)),
            ],
            out_specs=pl.BlockSpec((1, rows, features), lambda s, place: (place[s], 0, 0)),
        ),
        out_shape=jax.ShapeDtypeStruct((blocks, rows, features), bf16),
        compiler_params=params(32, "arbitrary"),
        cost_estimate=cost(2 * tokens * wd.size, 1.1e7),
        name="expert_outputs",
    )(place, hidden, weight, wd)


def turn_kernel(sg_ref, middle_ref, gain_ref, cot_ref, wo_ref, mg_ref, proj_ref, dmid_ref, dgain_ref):
    grad = sg_ref[...].astype(f32)
    middle = middle_ref[...]
    scale = lax.rsqrt(jnp.mean(middle * middle, axis=-1, keepdims=True) + norm_eps)
    unit = middle * scale
    dgain_ref[...] = jnp.sum(grad * unit, axis=0, keepdims=True)
    w = gain_ref[...] * grad
    dmid = cot_ref[...].astype(f32) + scale * (w - unit * jnp.mean(w * unit, axis=-1, keepdims=True))
    dmid_ref[...] = dmid
    proj = (residual_scale * dmid).astype(bf16)
    proj_ref[...] = proj
    mixed_grad = dot_nt(proj, wo_ref[...]).astype(bf16)
    groups, _, pair = mg_ref.shape
    for g in range(groups):
        mg_ref[g] = mixed_grad[:, g * pair : (g + 1) * pair]


def turn_call(sg, middle, gain, cot, wo, groups):
    rows, features = middle.shape
    pair = wo.shape[0] // groups
    return pl.pallas_call(
        turn_kernel,
        out_shape=[
            jax.ShapeDtypeStruct((groups, rows, pair), bf16),
            jax.ShapeDtypeStruct((rows, features), bf16),
            jax.ShapeDtypeStruct((rows, features), f32),
            jax.ShapeDtypeStruct((1, features), f32),
        ],
        compiler_params=params(32),
        cost_estimate=cost(2 * rows * wo.size, 6e6),
        name="norm_back_project_back",
    )(sg, middle, gain, cot, wo)


def output_weight_kernel(mixed_ref, proj_ref, dgain_ref, out_ref):
    held, each, features = out_ref.shape
    rows = mixed_ref.shape[1] // held
    part = lax.dot_general(mixed_ref[...], proj_ref[...], TN, preferred_element_type=f32)
    extra = jnp.broadcast_to(dgain_ref[...], (each - rows, features)).astype(bf16)
    for at in range(held):
        out_ref[at, :rows] = part[at * rows : (at + 1) * rows].astype(bf16)
        out_ref[at, rows:] = extra


def output_weight_call(mixed, proj, dgain, parts):
    rows, width = mixed.shape
    features = proj.shape[1]
    each = width // parts
    lanes = max(each, 2 * HEAD_DIM)
    held = lanes // each
    return pl.pallas_call(
        output_weight_kernel,
        grid=(parts // held,),
        in_specs=[
            pl.BlockSpec((rows, lanes), lambda s: (0, s)),
            whole((rows, features)),
            whole((1, features)),
        ],
        out_specs=pl.BlockSpec((held, each + 16, features), lambda s: (s, 0, 0)),
        out_shape=jax.ShapeDtypeStruct((parts, each + 16, features), bf16),
        compiler_params=params(32, "arbitrary"),
        cost_estimate=cost(2 * rows * width * features, 4e6),
        name="output_weight_part",
    )(mixed, proj, dgain)


def dense_out_kernel(
    at_ref, own_ref, other_ref, wq_ref, wk_ref, wv_ref, gain_ref, dq_ref, dk_ref, dv_ref, dg_ref, wo_ref, dg2_ref
):
    chips, _, width = own_ref.shape
    rows = dq_ref.shape[0]
    pair = width // 2
    chip, core = at_ref[2], at_ref[3]
    total = jnp.zeros((rows, pair), f32)
    for k in range(chips):
        source = lax.rem(chip - k + chips, chips)
        a = jnp.where(core == 0, own_ref[k], other_ref[k]).astype(f32)
        b = jnp.where(core == 0, other_ref[k], own_ref[k]).astype(f32)
        q = jnp.concatenate([a[:rows, :pair], b[:rows, :pair]], axis=1)
        cols = pl.ds(pl.multiple_of(source * width, width), width)
        dq_ref[:, cols] = q
        made = q * wq_ref[:, cols].astype(f32)
        total += made[:, :pair] + made[:, pair:]
        a_kv, b_kv = a[:rows, pair:], b[:rows, pair:]
        lane = lax.broadcasted_iota(jnp.int32, a_kv.shape, 1)
        key = jnp.where(lane < HEAD_DIM, a_kv, pltpu.roll(b_kv, HEAD_DIM, 1))
        val = jnp.where(lane < HEAD_DIM, pltpu.roll(a_kv, HEAD_DIM, 1), b_kv)
        cols = pl.ds(pl.multiple_of(source * pair, pair), pair)
        dk_ref[:, cols] = key
        dv_ref[:, cols] = val
        total += key * wk_ref[:, cols].astype(f32) + val * wv_ref[:, cols].astype(f32)
        wo_ref[2 * source, 0] = a[rows : rows + wo_ref.shape[2]]
        wo_ref[2 * source + 1, 0] = b[rows : rows + wo_ref.shape[2]]
        if k == 0:
            dg2_ref[...] = a[rows + wo_ref.shape[2] :][:1]
    dg_ref[...] = jnp.sum(jnp.transpose(total), axis=0, keepdims=True) / gain_ref[...]


def dense_out_call(at, own, other, wq, wk, wv, gain, wo_shape):
    streams, parts, chips, held, width = own.shape
    features = wq.shape[0]
    groups = 2 * chips
    rows = features // (streams * parts)
    block_cols = wo_shape[1] // width
    per_block = streams * parts // block_cols
    wo_rows = wo_shape[0] // groups // per_block
    by_rows = lambda w: pl.BlockSpec((rows, w.shape[1]), lambda s, r, at: (s * parts + r, 0))
    taken = pl.BlockSpec(
        (None, None, chips, held, width), lambda s, r, at: (s, jnp.bitwise_xor(r, at[s]), 0, 0, 0)
    )
    gain_spec = pl.BlockSpec((1, rows), lambda s, r, at: (0, s * parts + r))
    outs = pl.pallas_call(
        dense_out_kernel,
        grid_spec=pltpu.PrefetchScalarGridSpec(
            num_scalar_prefetch=1,
            grid=(streams, parts),
            in_specs=[taken, taken, by_rows(wq), by_rows(wk), by_rows(wv), gain_spec],
            out_specs=[
                by_rows(wq),
                by_rows(wk),
                by_rows(wv),
                gain_spec,
                pl.BlockSpec(
                    (groups, 1, wo_rows, width),
                    lambda s, r, at: (
                        0,
                        lax.rem(s * parts + r, per_block),
                        0,
                        lax.div(s * parts + r, per_block),
                    ),
                ),
                pl.BlockSpec((1, width), lambda s, r, at: (0, lax.div(s * parts + r, per_block))),
            ],
        ),
        out_shape=[
            jax.ShapeDtypeStruct(wq.shape, f32),
            jax.ShapeDtypeStruct(wk.shape, f32),
            jax.ShapeDtypeStruct(wv.shape, f32),
            jax.ShapeDtypeStruct((1, features), f32),
            jax.ShapeDtypeStruct((groups, per_block, wo_rows, wo_shape[1]), f32),
            jax.ShapeDtypeStruct((1, wo_shape[1]), f32),
        ],
        compiler_params=params(48, "arbitrary", "arbitrary"),
        cost_estimate=cost(2 * wq.size, 2.4e7),
        name="dense_weights_out",
    )(at, own, other, wq, wk, wv, gain)
    return (*outs[:4], outs[4].reshape(wo_shape), outs[5])


def weights_out_kernel(wide_ref, wq_ref, wk_ref, wv_ref, gain_ref, dq_ref, dk_ref, dv_ref, dg_ref):
    groups, rows, width = wide_ref.shape
    pair = width // 2
    total = jnp.zeros((rows, pair), f32)
    for g in range(groups):
        part = wide_ref[g, :, :pair].astype(f32)
        at = slice(g * pair, (g + 1) * pair)
        dq_ref[:, at] = part
        total += part * wq_ref[:, at].astype(f32)
    for g in range(groups // 2):
        a = wide_ref[2 * g, :, pair:].astype(f32)
        b = wide_ref[2 * g + 1, :, pair:].astype(f32)
        lane = lax.broadcasted_iota(jnp.int32, a.shape, 1)
        at = slice(g * pair, (g + 1) * pair)
        k = jnp.where(lane < HEAD_DIM, a, pltpu.roll(b, HEAD_DIM, 1))
        v = jnp.where(lane < HEAD_DIM, pltpu.roll(a, HEAD_DIM, 1), b)
        dk_ref[:, at] = k
        dv_ref[:, at] = v
        total += k * wk_ref[:, at].astype(f32) + v * wv_ref[:, at].astype(f32)
    dg_ref[...] = jnp.sum(jnp.transpose(total), axis=0, keepdims=True) / gain_ref[...]


def weights_out_call(wide, wq, wk, wv, gain):
    chunks, groups, rows, width = wide.shape
    features = chunks * rows
    by_rows = lambda w: pl.BlockSpec((rows, w.shape[1]), lambda c: (c, 0))
    return pl.pallas_call(
        weights_out_kernel,
        grid=(chunks,),
        in_specs=[
            pl.BlockSpec((None, groups, rows, width), lambda c: (c, 0, 0, 0)),
            by_rows(wq),
            by_rows(wk),
            by_rows(wv),
            pl.BlockSpec((1, rows), lambda c: (0, c)),
        ],
        out_specs=[
            by_rows(wq),
            by_rows(wk),
            by_rows(wv),
            pl.BlockSpec((1, rows), lambda c: (0, c)),
        ],
        out_shape=[
            jax.ShapeDtypeStruct(wq.shape, f32),
            jax.ShapeDtypeStruct(wk.shape, f32),
            jax.ShapeDtypeStruct(wv.shape, f32),
            jax.ShapeDtypeStruct((1, features), f32),
        ],
        compiler_params=params(32, "arbitrary"),
        cost_estimate=cost(2 * wq.size, 1.6e7),
        name="attention_weights_out",
    )(wide, wq, wk, wv, gain)


def last_kernel(d_ref, wq_ref, wk_ref, wv_ref, x_ref, gain_ref, dmid_ref, out_ref):
    groups, rows, width = d_ref.shape
    pair = width // 2
    dq = jnp.concatenate([d_ref[g, :, :pair] for g in range(groups)], axis=1)
    grad = dot_nt(dq, wq_ref[...])
    keys, vals = [], []
    for at in range(groups // 2):
        a = d_ref[2 * at, :, pair:].astype(f32)
        b = d_ref[2 * at + 1, :, pair:].astype(f32)
        lane = lax.broadcasted_iota(jnp.int32, a.shape, 1)
        keys.append(jnp.where(lane < HEAD_DIM, a, pltpu.roll(b, HEAD_DIM, 1)).astype(bf16))
        vals.append(jnp.where(lane < HEAD_DIM, pltpu.roll(a, HEAD_DIM, 1), b).astype(bf16))
    grad = grad + dot_nt(jnp.concatenate(keys, axis=1), wk_ref[...])
    grad = grad + dot_nt(jnp.concatenate(vals, axis=1), wv_ref[...])
    x = x_ref[...].astype(f32)
    scale = lax.rsqrt(jnp.mean(x * x, axis=-1, keepdims=True) + norm_eps)
    unit = x * scale
    w = gain_ref[...] * grad
    out_ref[...] = dmid_ref[...] + scale * (w - unit * jnp.mean(w * unit, axis=-1, keepdims=True))


def last_call(d, wq, wk, wv, x, gain, dmid):
    rows, features = x.shape
    return pl.pallas_call(
        last_kernel,
        out_shape=jax.ShapeDtypeStruct((rows, features), f32),
        compiler_params=params(40),
        cost_estimate=cost(4 * rows * features * features, 8e6),
        name="input_gradient",
    )(d, wq, wk, wv, x, gain, dmid)


def swap(values, axis, bit):
    return lax.ppermute(values, axis, [(i, i ^ bit) for i in range(lax.axis_size(axis))])


def half_sum(values, axis, bit):
    half = values.shape[0] // 2
    upper = ((lax.axis_index(axis) & bit) > 0).astype(jnp.int32)
    came = swap(lax.dynamic_slice_in_dim(values, (1 - upper) * half, half), axis, bit)
    mine = lax.dynamic_slice_in_dim(values, upper * half, half)
    return (mine.astype(f32) + came.astype(f32)).astype(bf16)


def relative_sum(kept, sent, axis, bits):
    while True:
        kept = (kept.astype(f32) + swap(sent, axis, bits[0]).astype(f32)).astype(bf16)
        bits = bits[1:]
        if not bits:
            return kept
        half = kept.shape[0] // 2
        kept, sent = kept[:half], kept[half:]


def join_parts(stream, axis, bits):
    shape = stream.shape
    for bit in bits[::-1]:
        stream = jnp.stack([stream, swap(stream, axis, bit)])
    return stream.reshape(-1, *shape)


def body(
    layer_input,
    first_gain,
    query_weight,
    key_weight,
    value_weight,
    output_weight,
    second_gain,
    gate_weight,
    up_weight,
    down_weight,
    expert_ids,
    gate_values,
    positions,
    cotangent,
):
    micro, _, per_device, features = layer_input.shape
    devices = lax.axis_size("seq")
    replicas = lax.axis_size("dp")
    seq_place = lax.axis_index("seq")
    rows = micro * per_device
    local_experts = gate_weight.shape[0]
    groups = key_weight.shape[1] // HEAD_DIM
    pair = query_weight.shape[1] // groups
    copies = devices // groups

    dp_bits = [1 << i for i in range(replicas.bit_length() - 1)]

    def spread(blocks):
        if copies > 1:
            blocks = jnp.repeat(blocks, copies, axis=0)
        return lax.all_to_all(blocks, "seq", 0, 0, tiled=True)

    def unspread(blocks):
        return lax.all_to_all(blocks, "seq", 0, 0, tiled=True)[::copies]

    x = layer_input.reshape(rows, features)
    cot = cotangent.reshape(rows, features)
    gain_one = first_gain.reshape(1, features)
    gain_two = second_gain.reshape(1, features)
    pos_all = lax.all_to_all(
        jnp.broadcast_to(positions.reshape(1, rows), (devices, rows)), "seq", 0, 0, tiled=True
    )
    x_all = lax.all_gather(x, "seq", axis=0)
    cos_all, sin_all = rope_tables(pos_all.reshape(-1), pair)
    mine = seq_place * local_experts + jnp.arange(local_experts, dtype=jnp.int32)
    ids = expert_ids[:, 0]
    gates = gate_values[:, 0].astype(f32)
    routed = jnp.sum(
        jnp.where(ids[..., None] == mine, gates[..., None], 0.0), axis=2
    )
    routed = routed.reshape(micro, devices, per_device, local_experts)
    routed = jnp.transpose(routed, (1, 0, 2, 3)).reshape(devices * rows, local_experts)
    group = seq_place // copies
    w_own = jnp.concatenate(
        [
            lax.dynamic_slice_in_dim(query_weight, group * pair, pair, axis=1),
            lax.dynamic_slice_in_dim(key_weight, group * HEAD_DIM, HEAD_DIM, axis=1),
            lax.dynamic_slice_in_dim(value_weight, group * HEAD_DIM, HEAD_DIM, axis=1),
        ],
        axis=1,
    )
    cos_all, sin_all, routed, w_own = lax.optimization_barrier((cos_all, sin_all, routed, w_own))
    x_all, cot_then, cos_all, sin_all, routed, w_own = lax.optimization_barrier(
        (x_all, cot, cos_all, sin_all, routed, w_own)
    )
    cot_all = lax.all_gather(cot_then, "seq", axis=0)

    qkv, first_all = qkv_call(x_all, gain_one, cos_all, sin_all, w_own)
    qkv = qkv.reshape(devices, micro, per_device, 2 * pair)
    mix = attend_call(qkv)
    mix = unspread(mix.reshape(devices, rows, pair))
    mixed, middle, second_low = post_call(mix, output_weight, x, gain_two)

    chips = devices // 2
    chip, core = seq_place // 2, seq_place % 2
    onward = [(i, (i + 2) % devices) for i in range(devices)]
    dp_place = lax.axis_index("dp")
    first_bit = dp_place & 1
    last_bit = dp_place >> (len(dp_bits) - 1)
    held, kept, running, places = second_low, (), None, []
    for hop in range(chips):
        following = lax.ppermute(held, "seq", onward) if hop < chips - 1 else None
        other = swap(held, "seq", 1)
        source = 2 * ((chip - hop) % chips)
        place = jnp.stack([source + core, source + 1 - core, 1 - first_bit, 1 - last_bit])
        place = place.astype(jnp.int32)
        places.append(place[:2])
        dx, *kept = expert_call(
            hop, place, held, other, cot_all, routed, gate_weight, up_weight, down_weight, kept
        )
        if following is not None:
            following, dx = lax.optimization_barrier((following, dx))
        part = dx[0].astype(f32) + swap(dx[1], "seq", 1).astype(f32)
        if hop == 0:
            own_part = part
        else:
            if running is not None:
                part = part + running.astype(f32)
            part = part.astype(bf16)
            if following is not None:
                part, following = lax.optimization_barrier((part, following))
            else:
                part, kept = lax.optimization_barrier((part, kept))
            running = lax.ppermute(part, "seq", onward)
        held = following
    second_grad = (own_part + running.astype(f32)).astype(bf16)
    tokens, hidden_a, hidden_b, gate_low, up_low, slot_a, slot_b = kept

    def weight_parts(at, tokens, hidden_a, hidden_b, gate_low, up_low, slot_a, slot_b):
        pairs = (
            (tokens, gate_low[at]),
            (tokens, up_low[at]),
            (hidden_a[at], slot_a[at]),
            (hidden_b[at], slot_b[at]),
        )
        return [
            lax.dot_general(a, b, TN, preferred_element_type=f32).astype(bf16) for a, b in pairs
        ]

    leaving = weight_parts(0, *kept)
    part_bits = (dp_bits[0], dp_bits[-1], dp_bits[0], dp_bits[-1])
    stream_bits = (dp_bits, dp_bits[::-1])
    came = [swap(values, "dp", bit) for values, bit in zip(leaving, part_bits)]
    leaving, second_grad = lax.optimization_barrier((leaving, second_grad))

    mg_send, proj, middle_grad, gain_two_part = turn_call(
        second_grad, middle, gain_two, cot, output_weight, groups
    )
    mg = spread(mg_send)
    kept, _ = lax.optimization_barrier((kept, mg_send))
    mixed, proj, came[2:] = lax.optimization_barrier((mixed, proj, came[2:]))
    dense = output_weight_call(mixed, proj, gain_two_part, devices)
    dense_own = dense
    staying = weight_parts(1, *kept)
    turned = sum(((dp_place >> i) & 1) << (len(dp_bits) - 1 - i) for i in range(len(dp_bits)))
    part_at = jnp.stack([turned, dp_place]).astype(jnp.int32)
    low_at = jnp.bitwise_and(part_at, replicas // 2 - 1)
    keep_a, send_a, keep_b, send_b = part_sum_call(low_at, replicas // 2, came, staying)
    mg, keep_a, send_a, keep_b, send_b = lax.optimization_barrier(
        (mg, keep_a, send_a, keep_b, send_b)
    )
    streams = [
        relative_sum(keep_a, send_a, "dp", stream_bits[0][1:]),
        relative_sum(keep_b, send_b, "dp", stream_bits[1][1:]),
    ]
    dense = dense_own
    dense = lax.psum_scatter(dense, "seq", scatter_dimension=0)
    table_shape = (devices, micro, per_device, pair)
    dqkv = attend_back_call(
        qkv,
        mg.reshape(devices, micro, per_device, pair),
        cos_all.reshape(table_shape),
        sin_all.reshape(table_shape),
    )
    dqkv, streams = lax.optimization_barrier((dqkv, streams))
    near = [
        [v[0], swap(v[0], "dp", bits[-1])] for v, bits in zip(streams, stream_bits)
    ]
    back = unspread(dqkv.reshape(devices, rows, 2 * pair))
    d_all = dqkv.reshape(devices * rows, 2 * pair)
    first_tokens = first_all.reshape(devices * rows, features)
    part = lax.dot_general(first_tokens, d_all, TN, preferred_element_type=f32)
    dense = dense.reshape(dense.shape[-2], features)
    each = output_weight.shape[0] // devices
    if copies == 1:
        width = 2 * pair
        kept_pieces, sent_pieces = joint_call(part_at, part, dense, replicas)
        first = [
            kept_pieces[at].astype(f32) + swap(sent_pieces[at], "dp", bits[0]).astype(f32)
            for at, bits in enumerate(stream_bits)
        ]
        first, near = lax.optimization_barrier(([v.astype(bf16) for v in first], near))
        own = [
            relative_sum(v[: replicas // 4], v[replicas // 4 :], "dp", bits[1:])
            for v, bits in zip(first, stream_bits)
        ]
        own = jnp.concatenate(own, axis=0)
        kept, own = lax.optimization_barrier((kept, own))
        moe_place = jnp.concatenate(places + [(1 - first_bit).astype(jnp.int32).reshape(1)])
        moe_all = moe_call(moe_place, kept[1], routed, down_weight, devices)
        own, back, here = lax.optimization_barrier((own, back, [v[0] for v in near]))
        far = [[swap(v, "dp", bits[-2])] for v, bits in zip(here, stream_bits)]
        backward = [(i, (i - 2) % devices) for i in range(devices)]
        round_ring = {0: own}
        for k in range(1, chips // 2 + 1):
            round_ring[k] = lax.ppermute(round_ring[k - 1], "seq", onward)
            if chips - k > k:
                round_ring[chips - k] = lax.ppermute(
                    round_ring[(chips - k + 1) % chips], "seq", backward
                )
        held = jnp.stack([round_ring[k] for k in range(chips)])
        held, moe_all, far = lax.optimization_barrier((held, moe_all, far))
        moe = lax.psum_scatter(moe_all, "seq", scatter_dimension=0)
        layer_output = (middle + residual_scale * moe.astype(f32)).astype(bf16)
    else:
        far = [[swap(v[0], "dp", bits[-2])] for v, bits in zip(streams, stream_bits)]
    expert_pieces = []
    for (here, first), (second,), bits in zip(near, far, stream_bits):
        pieces = [here, first, second, swap(first, "dp", bits[-2])]
        for bit in bits[:-2][::-1]:
            pieces = pieces + [swap(p, "dp", bit) for p in pieces]
        expert_pieces.append(pieces)
    input_grad = last_call(
        back, query_weight, key_weight, value_weight, x, gain_one, middle_grad
    )
    if copies == 1:
        full = [join_parts(held[:, at], "dp", b) for at, b in enumerate(stream_bits)]
        full, input_grad = lax.optimization_barrier((jnp.stack(full), input_grad))
        other = swap(full, "seq", 1)
        where_at = jnp.stack([turned, dp_place, chip, core]).astype(jnp.int32)
        (
            query_weight_grad,
            key_weight_grad,
            value_weight_grad,
            first_gain_grad,
            output_weight_grad,
            second_gain_grad,
        ) = dense_out_call(
            where_at, full, other, query_weight, key_weight, value_weight, gain_one, output_weight.shape
        )
        query_weight_grad, expert_pieces = lax.optimization_barrier(
            (query_weight_grad, expert_pieces)
        )
    else:
        for bit in dp_bits:
            dense = (dense.astype(f32) + swap(dense, "dp", bit).astype(f32)).astype(bf16)
        dense = lax.all_gather(dense, "seq", axis=0).astype(f32)
        output_weight_grad = dense[:, :each].reshape(output_weight.shape)
        moe_place = jnp.concatenate(places + [(1 - first_bit).astype(jnp.int32).reshape(1)])
        moe_all = moe_call(moe_place, kept[1], routed, down_weight, devices)
        moe = lax.psum_scatter(moe_all, "seq", scatter_dimension=0)
        layer_output = (middle + residual_scale * moe.astype(f32)).astype(bf16)
        second_gain_grad = dense[0, each]
        part = part.astype(bf16)
        for bit in dp_bits[::-1]:
            part = half_sum(part, "dp", bit)
        wide = lax.all_gather(part, ("dp", "seq"), axis=0)
        wide = wide.reshape(replicas, devices, features // replicas, 2 * pair)[:, ::copies]
        query_weight_grad, key_weight_grad, value_weight_grad, first_gain_grad = weights_out_call(
            wide, query_weight, key_weight, value_weight, gain_one
        )
    second_gain_grad = second_gain_grad.reshape(features)
    gate_sum, up_sum, down_sum = expert_out_call(
        part_at, *expert_pieces, gate_weight.shape, down_weight.shape
    )
    return (
        layer_output.reshape(layer_input.shape),
        input_grad.reshape(layer_input.shape),
        first_gain_grad.reshape(features),
        query_weight_grad,
        key_weight_grad,
        value_weight_grad,
        output_weight_grad,
        second_gain_grad,
        gate_sum,
        up_sum,
        down_sum,
    )


def solution(mesh):
    return jax.shard_map(
        body,
        mesh=mesh,
        in_specs=(
            P(None, "dp", "seq", None),
            P(),
            P(),
            P(),
            P(),
            P(),
            P(),
            P("seq", None, None),
            P("seq", None, None),
            P("seq", None, None),
            P(None, "dp", None, None),
            P(None, "dp", None, None),
            P(None, "dp", "seq"),
            P(None, "dp", "seq", None),
        ),
        out_specs=(
            P(None, "dp", "seq", None),
            P(None, "dp", "seq", None),
            P(),
            P(),
            P(),
            P(),
            P(),
            P(),
            P("seq", None, None),
            P("seq", None, None),
            P("seq", None, None),
        ),
        check_vma=False,
    )
```

```python
from functools import partial

import jax
import jax.numpy as jnp
from jax import lax
from jax.experimental import pallas as pl
from jax.experimental.pallas import tpu as pltpu
from jax.sharding import PartitionSpec as P

HEAD_DIM = 64

rope_theta = 10000.0
attention_scale = 0.015625
residual_scale = 0.22
norm_eps = 1e-06
masked_score = -1e30

f32 = jnp.float32
bf16 = jnp.bfloat16
NT = (((1,), (1,)), ((), ()))
TN = (((0,), (0,)), ((), ()))


def dot(a, b):
    return jnp.dot(a, b, preferred_element_type=f32)


def dot_nt(a, b):
    return lax.dot_general(a, b, NT, preferred_element_type=f32)


def params(mib, *semantics):
    return pltpu.CompilerParams(
        vmem_limit_bytes=mib * 1024 * 1024, dimension_semantics=semantics or None
    )


def cost(flops, nbytes, trans=0):
    return pl.CostEstimate(
        flops=int(flops / 8), bytes_accessed=int(nbytes / 8), transcendentals=int(trans / 8)
    )


def whole(shape):
    return pl.BlockSpec(shape, lambda *_: (0,) * len(shape))


def rope_tables(positions, width):
    half = HEAD_DIM // 2
    exponent = jnp.arange(half, dtype=f32) * (-2.0 / HEAD_DIM)
    angles = positions.astype(f32)[:, None] * (rope_theta**exponent)[None, :]
    cosine, sine = jnp.cos(angles), jnp.sin(angles)
    copies = width // HEAD_DIM
    cos_row = jnp.concatenate([cosine, cosine] * copies, axis=1)
    sin_row = jnp.concatenate([-sine, sine] * copies, axis=1)
    return cos_row, sin_row


def partner(values):
    width = values.shape[1]
    half = HEAD_DIM // 2
    lane = lax.broadcasted_iota(jnp.int32, values.shape, 1)
    ahead = pltpu.roll(values, width - half, 1)
    behind = pltpu.roll(values, half, 1)
    return jnp.where(lane % HEAD_DIM < half, ahead, behind)


def qkv_kernel(x_ref, gain_ref, cos_ref, sin_ref, w_ref, qkv_ref, low_ref):
    pair = 2 * HEAD_DIM
    x = x_ref[0].astype(f32)
    scale = lax.rsqrt(jnp.mean(x * x, axis=-1, keepdims=True) + norm_eps)
    low = (x * scale * gain_ref[...]).astype(bf16)
    low_ref[0] = low
    cosine, sine = cos_ref[...], sin_ref[...]
    made = dot(low, w_ref[...])
    q, kv = made[:, :pair], made[:, pair:]
    q = (q * cosine + partner(q) * sine) * attention_scale
    qkv_ref[0, :, :pair] = q.astype(bf16)
    lane = lax.broadcasted_iota(jnp.int32, kv.shape, 1)
    turned = kv * cosine + partner(kv) * sine
    qkv_ref[0, :, pair:] = jnp.where(lane < HEAD_DIM, turned, kv).astype(bf16)


def qkv_call(x_all, gain, cos_all, sin_all, w_own):
    blocks, rows, features = x_all.shape
    pair = 2 * HEAD_DIM
    return pl.pallas_call(
        qkv_kernel,
        grid=(blocks,),
        in_specs=[
            pl.BlockSpec((1, rows, features), lambda s: (s, 0, 0)),
            whole((1, features)),
            pl.BlockSpec((rows, pair), lambda s: (s, 0)),
            pl.BlockSpec((rows, pair), lambda s: (s, 0)),
            whole(w_own.shape),
        ],
        out_specs=[
            pl.BlockSpec((1, rows, 2 * pair), lambda s: (s, 0, 0)),
            pl.BlockSpec((1, rows, features), lambda s: (s, 0, 0)),
        ],
        out_shape=[
            jax.ShapeDtypeStruct((blocks, rows, 2 * pair), bf16),
            jax.ShapeDtypeStruct((blocks, rows, features), bf16),
        ],
        compiler_params=params(58, "arbitrary"),
        cost_estimate=cost(4 * blocks * rows * features * pair, 14e6),
        name="norm_qkv_rope",
    )(x_all, gain, cos_all, sin_all, w_own)


def split_heads(block, first):
    wide = block.astype(f32)
    lane = lax.broadcasted_iota(jnp.int32, wide.shape, 1)
    turned = pltpu.roll(wide, HEAD_DIM, 1)
    if first:
        parts = [jnp.where(lane < HEAD_DIM, wide, 0.0), jnp.where(lane < HEAD_DIM, turned, 0.0)]
    else:
        parts = [jnp.where(lane >= HEAD_DIM, turned, 0.0), jnp.where(lane >= HEAD_DIM, wide, 0.0)]
    return jnp.concatenate(parts, axis=0).astype(bf16)


def join_heads(turned):
    rows = turned.shape[1] // 2
    return jnp.transpose(jnp.concatenate([turned[:, :rows], turned[:, rows:]], axis=0))


def scores_of(kv, q2, rows):
    scores = dot_nt(kv, q2)
    count = scores.shape[0]
    own = scores[count - rows :]
    key_at = lax.broadcasted_iota(jnp.int32, own.shape, 0)
    query_at = lax.broadcasted_iota(jnp.int32, own.shape, 1) % rows
    own = jnp.where(key_at <= query_at, own, masked_score)
    if count == rows:
        return own
    return jnp.concatenate([scores[: count - rows], own], axis=0)


def attend_kernel(qkv_ref, out_ref, log_ref):
    blocks, _, rows, width = qkv_ref.shape
    pair = width // 2
    kv = qkv_ref[:, 0, :, pair:].reshape(blocks * rows, pair)
    kv_t = jnp.transpose(kv)
    for at in range(blocks):
        count = (at + 1) * rows
        q2 = split_heads(qkv_ref[at, 0, :, :pair], True)
        scores = scores_of(kv[:count], q2, rows)
        top = jnp.max(scores, axis=0, keepdims=True)
        weights = jnp.exp(scores - top)
        total = jnp.sum(weights, axis=0, keepdims=True)
        out_t = dot(kv_t[:, :count], weights.astype(bf16))
        out_ref[at, 0] = join_heads(out_t[HEAD_DIM:] / total).astype(bf16)
        log_ref[at, 0] = top + jnp.log(total)


def attend_call(qkv):
    blocks, micro, rows, width = qkv.shape
    pair = width // 2
    length = blocks * rows
    return pl.pallas_call(
        attend_kernel,
        grid=(micro,),
        in_specs=[pl.BlockSpec((blocks, 1, rows, width), lambda m: (0, m, 0, 0))],
        out_specs=[
            pl.BlockSpec((blocks, 1, rows, pair), lambda m: (0, m, 0, 0)),
            pl.BlockSpec((blocks, 1, 1, 2 * rows), lambda m: (0, m, 0, 0)),
        ],
        out_shape=[
            jax.ShapeDtypeStruct((blocks, micro, rows, pair), bf16),
            jax.ShapeDtypeStruct((blocks, micro, 1, 2 * rows), f32),
        ],
        compiler_params=params(48, "arbitrary"),
        cost_estimate=cost(
            micro * length * length * 512, 3 * qkv.size, micro * length * length
        ),
        name="attention_forward",
    )(qkv)


def attend_back_kernel(qkv_ref, grad_ref, log_ref, cos_ref, sin_ref, out_ref, dkv_ref):
    blocks, _, rows, width = qkv_ref.shape
    pair = width // 2
    kv = qkv_ref[:, 0, :, pair:].reshape(blocks * rows, pair)
    kv_t = jnp.transpose(kv)
    dkv_ref[...] = jnp.zeros_like(dkv_ref)
    for at in range(blocks):
        count = (at + 1) * rows
        q2 = split_heads(qkv_ref[at, 0, :, :pair], True)
        g2 = split_heads(grad_ref[at, 0], False)
        scores = scores_of(kv[:count], q2, rows)
        prob = jnp.exp(scores - log_ref[at, 0])
        prob_grad = dot_nt(kv[:count], g2)
        delta = jnp.sum(prob * prob_grad, axis=0, keepdims=True)
        score_grad = (prob * (prob_grad - delta)).astype(bf16)
        dkv_ref[:count] += dot(score_grad, q2) + dot(prob.astype(bf16), g2)
        dq_t = dot(kv_t[:, :count], score_grad)
        dq = join_heads(dq_t[:HEAD_DIM] * attention_scale)
        dq = dq * cos_ref[at, 0] - partner(dq) * sin_ref[at, 0]
        out_ref[at, 0, :, :pair] = dq.astype(bf16)
    for at in range(blocks):
        dkv = dkv_ref[at * rows : (at + 1) * rows]
        lane = lax.broadcasted_iota(jnp.int32, dkv.shape, 1)
        turned = dkv * cos_ref[at, 0] - partner(dkv) * sin_ref[at, 0]
        out_ref[at, 0, :, pair:] = jnp.where(lane < HEAD_DIM, turned, dkv).astype(bf16)


def attend_back_call(qkv, grads, log_total, cos_all, sin_all):
    blocks, micro, rows, width = qkv.shape
    pair = width // 2
    length = blocks * rows
    spec = lambda lanes: pl.BlockSpec((blocks, 1, rows, lanes), lambda m: (0, m, 0, 0))
    return pl.pallas_call(
        attend_back_kernel,
        grid=(micro,),
        in_specs=[
            spec(width),
            spec(pair),
            pl.BlockSpec((blocks, 1, 1, 2 * rows), lambda m: (0, m, 0, 0)),
            spec(pair),
            spec(pair),
        ],
        out_specs=spec(width),
        out_shape=jax.ShapeDtypeStruct(qkv.shape, bf16),
        scratch_shapes=[pltpu.VMEM((length, pair), f32)],
        compiler_params=params(56, "arbitrary"),
        cost_estimate=cost(
            micro * length * length * 1280, 10 * qkv.size, micro * length * length
        ),
        name="attention_backward",
    )(qkv, grads, log_total, cos_all, sin_all)


def post_kernel(mix_ref, wo_ref, x_ref, gain_ref, mixed_ref, middle_ref, low_ref):
    mixed = jnp.concatenate([mix_ref[g] for g in range(mix_ref.shape[0])], axis=1)
    mixed_ref[...] = mixed
    middle = x_ref[...].astype(f32) + residual_scale * dot(mixed, wo_ref[...])
    middle_ref[...] = middle
    scale = lax.rsqrt(jnp.mean(middle * middle, axis=-1, keepdims=True) + norm_eps)
    low_ref[...] = (middle * scale * gain_ref[...]).astype(bf16)


def post_call(mix, wo, x, gain):
    rows, features = x.shape
    return pl.pallas_call(
        post_kernel,
        out_shape=[
            jax.ShapeDtypeStruct((rows, wo.shape[0]), bf16),
            jax.ShapeDtypeStruct((rows, features), f32),
            jax.ShapeDtypeStruct((rows, features), bf16),
        ],
        compiler_params=params(32),
        cost_estimate=cost(2 * rows * wo.size, 5e6),
        name="project_norm",
    )(mix, wo, x, gain)


def expert_kernel(place_ref, a_ref, b_ref, cot_ref, w_ref, wg_ref, wu_ref, wd_ref, *refs):
    dx_ref, moe_ref, x_ref, ha_ref, hb_ref, dg_ref, du_ref, sa_ref, sb_ref = refs[-9:]
    step = pl.program_id(0)
    first, second = place_ref[2], place_ref[3]
    half = sa_ref.shape[2]

    @pl.when(step == 0)
    def _():
        x_ref[...] = a_ref[...]

    @pl.when(step == 1)
    def _():
        x_ref[...] = b_ref[...]

    x = x_ref[...]
    cot = cot_ref[0].astype(f32)
    weight = w_ref[...]
    total, made = None, None
    for e in range(wg_ref.shape[0]):
        gate = dot(x, wg_ref[e])
        up = dot(x, wu_ref[e])
        share = weight[:, e : e + 1]
        slot_grad = (residual_scale * share * cot).astype(bf16)
        to_a, to_b = jnp.bitwise_xor(first, e), jnp.bitwise_xor(second, e)
        sa_ref[to_a] = slot_grad[:, :half]
        sb_ref[to_b] = slot_grad[:, half:]
        hidden_grad = dot_nt(slot_grad, wd_ref[e])
        sig = 0.5 * jnp.tanh(0.5 * gate) + 0.5
        silu = gate * sig
        hidden = (silu * up).astype(bf16)
        ha_ref[to_a] = hidden
        hb_ref[to_b] = hidden
        gate_grad = (hidden_grad * up * (sig + silu * (1.0 - sig))).astype(bf16)
        up_grad = (hidden_grad * silu).astype(bf16)
        dg_ref[to_a] = gate_grad
        du_ref[to_b] = up_grad
        term = dot_nt(gate_grad, wg_ref[e]) + dot_nt(up_grad, wu_ref[e])
        out = share * dot(hidden, wd_ref[e])
        total = term if total is None else total + term
        made = out if made is None else made + out
    dx_ref[0] = total.astype(bf16)
    moe_ref[0] = made.astype(bf16)


def expert_call(at, place, own, other, cot_all, weight, wg, wu, wd, kept):
    blocks, rows, features = cot_all.shape
    count, _, hidden = wg.shape
    tokens = blocks * rows
    inner = jax.ShapeDtypeStruct((count, tokens, hidden), bf16)
    outer = jax.ShapeDtypeStruct((count, tokens, features // 2), bf16)
    inner_spec = pl.BlockSpec((count, rows, hidden), lambda s, place: (0, 2 * at + s, 0))
    outer_spec = pl.BlockSpec((count, rows, features // 2), lambda s, place: (0, 2 * at + s, 0))
    fixed = lambda shape: pl.BlockSpec(shape, lambda s, place: (0,) * len(shape))
    any_spec = pl.BlockSpec(memory_space=pl.ANY)
    first = 8
    return pl.pallas_call(
        expert_kernel,
        grid_spec=pltpu.PrefetchScalarGridSpec(
            num_scalar_prefetch=1,
            grid=(2,),
            in_specs=[
                fixed((rows, features)),
                fixed((rows, features)),
                pl.BlockSpec((1, rows, features), lambda s, place: (place[s], 0, 0)),
                pl.BlockSpec((rows, count), lambda s, place: (place[s], 0)),
                fixed(wg.shape),
                fixed(wu.shape),
                fixed(wd.shape),
            ]
            + [any_spec] * len(kept),
            out_specs=[
                pl.BlockSpec((1, rows, features), lambda s, place: (s, 0, 0)),
                pl.BlockSpec((1, rows, features), lambda s, place: (place[s], 0, 0)),
                pl.BlockSpec((rows, features), lambda s, place: (2 * at + s, 0)),
            ]
            + [inner_spec] * 4
            + [outer_spec] * 2,
        ),
        out_shape=[
            jax.ShapeDtypeStruct((2, rows, features), bf16),
            jax.ShapeDtypeStruct((blocks, rows, features), bf16),
            jax.ShapeDtypeStruct((tokens, features), bf16),
            inner,
            inner,
            inner,
            inner,
            outer,
            outer,
        ],
        input_output_aliases={first + i: 1 + i for i in range(len(kept))},
        compiler_params=params(48, "arbitrary"),
        cost_estimate=cost(24 * rows * wg.size, 2e7, 2 * rows * hidden * count),
        name="experts",
    )(place, own, other, cot_all, weight, wg, wu, wd, *kept)


def part_sum_kernel(at_ref, *refs):
    inputs, outs = refs[:16], refs[16:]
    at = 0
    for out in outs:
        gate_came, gate_here, down_came, down_here = inputs[at : at + 4]
        rows = gate_came.shape[0]
        out[0, :rows] = (gate_came[...].astype(f32) + gate_here[...].astype(f32)).astype(bf16)
        out[0, rows:] = (down_came[...].astype(f32) + down_here[...].astype(f32)).astype(bf16)
        at += 4


def part_sum_call(at, per, came, here):
    gate_rows, down_rows = came[0].shape[0] // per, came[2].shape[0] // per
    width = came[0].shape[1]
    steps = per // 2
    specs, args, out_specs, out_shapes = [], [], [], []
    for stream in range(2):
        for sent in range(2):
            for which, rows in ((stream, gate_rows), (stream + 2, down_rows)):
                spec = pl.BlockSpec(
                    (rows, width),
                    lambda s, at, sent=sent, stream=stream: (
                        jnp.bitwise_xor(s + sent * steps, at[stream]),
                        0,
                    ),
                )
                specs += [spec, spec]
                args += [came[which], here[which]]
            out_specs.append(
                pl.BlockSpec((1, gate_rows + down_rows, width), lambda s, at: (s, 0, 0))
            )
            out_shapes.append(
                jax.ShapeDtypeStruct((steps, gate_rows + down_rows, width), bf16)
            )
    return pl.pallas_call(
        part_sum_kernel,
        grid_spec=pltpu.PrefetchScalarGridSpec(
            num_scalar_prefetch=1, grid=(steps,), in_specs=specs, out_specs=out_specs
        ),
        out_shape=out_shapes,
        compiler_params=params(60, "arbitrary"),
        cost_estimate=cost(0, 9e6),
        name="expert_part_sum",
    )(at, *args)


def joint_kernel(at_ref, *refs):
    for (part_ref, wo_ref, gain_ref), out_ref in ((refs[:3], refs[6]), (refs[3:6], refs[7])):
        rows = part_ref.shape[0]
        upto = rows + wo_ref.shape[0]
        out_ref[0, 0, :rows] = part_ref[...].astype(bf16)
        out_ref[0, 0, rows:upto] = wo_ref[...]
        out_ref[0, 0, upto:] = gain_ref[...]


def joint_call(at, part, dense, parts):
    features, width = part.shape
    pieces = 2 * parts
    rows = features // pieces
    block_cols = dense.shape[1] // width
    per_block = pieces // block_cols
    extra = 16
    wo_rows = (dense.shape[0] - extra) // per_block
    last = dense.shape[0] // extra - 1
    steps = parts // 2

    def piece(sent):
        return lambda s, p, at: s * parts + jnp.bitwise_xor(p + sent * steps, at[s])

    specs = []
    for sent in range(2):
        at_piece = piece(sent)
        specs.append(
            pl.BlockSpec((rows, width), lambda s, p, at, f=at_piece: (f(s, p, at), 0))
        )
        specs.append(
            pl.BlockSpec(
                (wo_rows, width),
                lambda s, p, at, f=at_piece: (
                    lax.rem(f(s, p, at), per_block),
                    lax.div(f(s, p, at), per_block),
                ),
            )
        )
        specs.append(
            pl.BlockSpec(
                (extra, width), lambda s, p, at, f=at_piece: (last, lax.div(f(s, p, at), per_block))
            )
        )
    out_spec = pl.BlockSpec((1, 1, rows + wo_rows + extra, width), lambda s, p, at: (s, p, 0, 0))
    out_shape = jax.ShapeDtypeStruct((2, steps, rows + wo_rows + extra, width), bf16)
    return pl.pallas_call(
        joint_kernel,
        grid_spec=pltpu.PrefetchScalarGridSpec(
            num_scalar_prefetch=1, grid=(2, steps), in_specs=specs, out_specs=[out_spec] * 2
        ),
        out_shape=[out_shape] * 2,
        compiler_params=params(32, "arbitrary", "arbitrary"),
        cost_estimate=cost(0, 2e6),
        name="dense_pieces",
    )(at, part, dense, dense, part, dense, dense)


def expert_out_kernel(at_ref, *refs):
    pieces, (gate_ref, up_ref, down_ref) = refs[:-3], refs[-3:]
    parts = len(pieces) // 2
    step = pl.program_id(0)
    rows = gate_ref.shape[1]
    half = down_ref.shape[2] // 2
    for which in range(parts):

        @pl.when(jnp.bitwise_xor(step, at_ref[0]) == which)
        def _():
            a_ref = pieces[which]
            gate_ref[0] = a_ref[:rows].astype(f32)
            down_ref[0, :, :half] = a_ref[rows:].astype(f32)

        @pl.when(jnp.bitwise_xor(step, at_ref[1]) == which)
        def _():
            b_ref = pieces[parts + which]
            up_ref[0] = b_ref[:rows].astype(f32)
            down_ref[0, :, half:] = b_ref[rows:].astype(f32)


def expert_out_call(at, a, b, gate_shape, down_shape):
    parts = len(a)
    held, width = a[0].shape
    count = gate_shape[0]
    per = parts // count
    gate_rows, down_rows = gate_shape[1] // per, down_shape[1] // per
    place = lambda r, at: (lax.div(r, per), lax.rem(r, per), 0)
    return pl.pallas_call(
        expert_out_kernel,
        grid_spec=pltpu.PrefetchScalarGridSpec(
            num_scalar_prefetch=1,
            grid=(parts,),
            in_specs=[pl.BlockSpec((held, width), lambda r, at: (0, 0))] * (2 * parts),
            out_specs=[
                pl.BlockSpec((1, gate_rows, gate_shape[2]), place),
                pl.BlockSpec((1, gate_rows, gate_shape[2]), place),
                pl.BlockSpec((1, down_rows, down_shape[2]), place),
            ],
        ),
        out_shape=[
            jax.ShapeDtypeStruct(gate_shape, f32),
            jax.ShapeDtypeStruct(gate_shape, f32),
            jax.ShapeDtypeStruct(down_shape, f32),
        ],
        compiler_params=params(40, "arbitrary"),
        cost_estimate=cost(0, 2e7),
        name="expert_weights_out",
    )(at, *a, *b)


def turn_kernel(sg_ref, middle_ref, gain_ref, cot_ref, wo_ref, mg_ref, proj_ref, dmid_ref, dgain_ref):
    grad = sg_ref[...].astype(f32)
    middle = middle_ref[...]
    scale = lax.rsqrt(jnp.mean(middle * middle, axis=-1, keepdims=True) + norm_eps)
    unit = middle * scale
    dgain_ref[...] = jnp.sum(grad * unit, axis=0, keepdims=True)
    w = gain_ref[...] * grad
    dmid = cot_ref[...].astype(f32) + scale * (w - unit * jnp.mean(w * unit, axis=-1, keepdims=True))
    dmid_ref[...] = dmid
    proj = (residual_scale * dmid).astype(bf16)
    proj_ref[...] = proj
    mixed_grad = dot_nt(proj, wo_ref[...]).astype(bf16)
    groups, _, pair = mg_ref.shape
    for g in range(groups):
        mg_ref[g] = mixed_grad[:, g * pair : (g + 1) * pair]


def turn_call(sg, middle, gain, cot, wo, groups):
    rows, features = middle.shape
    pair = wo.shape[0] // groups
    return pl.pallas_call(
        turn_kernel,
        out_shape=[
            jax.ShapeDtypeStruct((groups, rows, pair), bf16),
            jax.ShapeDtypeStruct((rows, features), bf16),
            jax.ShapeDtypeStruct((rows, features), f32),
            jax.ShapeDtypeStruct((1, features), f32),
        ],
        compiler_params=params(32),
        cost_estimate=cost(2 * rows * wo.size, 6e6),
        name="norm_back_project_back",
    )(sg, middle, gain, cot, wo)


def output_weight_kernel(mixed_ref, proj_ref, dgain_ref, out_ref):
    held, each, features = out_ref.shape
    rows = mixed_ref.shape[1] // held
    part = lax.dot_general(mixed_ref[...], proj_ref[...], TN, preferred_element_type=f32)
    extra = jnp.broadcast_to(dgain_ref[...], (each - rows, features)).astype(bf16)
    for at in range(held):
        out_ref[at, :rows] = part[at * rows : (at + 1) * rows].astype(bf16)
        out_ref[at, rows:] = extra


def output_weight_call(mixed, proj, dgain, parts):
    rows, width = mixed.shape
    features = proj.shape[1]
    each = width // parts
    lanes = max(each, width // 2)
    held = lanes // each
    return pl.pallas_call(
        output_weight_kernel,
        grid=(parts // held,),
        in_specs=[
            pl.BlockSpec((rows, lanes), lambda s: (0, s)),
            whole((rows, features)),
            whole((1, features)),
        ],
        out_specs=pl.BlockSpec((held, each + 16, features), lambda s: (s, 0, 0)),
        out_shape=jax.ShapeDtypeStruct((parts, each + 16, features), bf16),
        compiler_params=params(32, "arbitrary"),
        cost_estimate=cost(2 * rows * width * features, 4e6),
        name="output_weight_part",
    )(mixed, proj, dgain)


def dense_out_kernel(
    at_ref, own_ref, other_ref, wq_ref, wk_ref, wv_ref, gain_ref, dq_ref, dk_ref, dv_ref, dg_ref, wo_ref, dg2_ref
):
    chips, _, width = own_ref.shape
    rows = dq_ref.shape[0]
    pair = width // 2
    chip, core = at_ref[2], at_ref[3]
    total = jnp.zeros((rows, pair), f32)
    for k in range(chips):
        source = lax.rem(chip - k + chips, chips)
        a = jnp.where(core == 0, own_ref[k], other_ref[k]).astype(f32)
        b = jnp.where(core == 0, other_ref[k], own_ref[k]).astype(f32)
        q = jnp.concatenate([a[:rows, :pair], b[:rows, :pair]], axis=1)
        cols = pl.ds(pl.multiple_of(source * width, width), width)
        dq_ref[:, cols] = q
        made = q * wq_ref[:, cols].astype(f32)
        total += made[:, :pair] + made[:, pair:]
        a_kv, b_kv = a[:rows, pair:], b[:rows, pair:]
        lane = lax.broadcasted_iota(jnp.int32, a_kv.shape, 1)
        key = jnp.where(lane < HEAD_DIM, a_kv, pltpu.roll(b_kv, HEAD_DIM, 1))
        val = jnp.where(lane < HEAD_DIM, pltpu.roll(a_kv, HEAD_DIM, 1), b_kv)
        cols = pl.ds(pl.multiple_of(source * pair, pair), pair)
        dk_ref[:, cols] = key
        dv_ref[:, cols] = val
        total += key * wk_ref[:, cols].astype(f32) + val * wv_ref[:, cols].astype(f32)
        wo_ref[2 * source, 0] = a[rows : rows + wo_ref.shape[2]]
        wo_ref[2 * source + 1, 0] = b[rows : rows + wo_ref.shape[2]]
        if k == 0:
            dg2_ref[...] = a[rows + wo_ref.shape[2] :][:1]
    dg_ref[...] = jnp.sum(jnp.transpose(total), axis=0, keepdims=True) / gain_ref[...]


def dense_out_call(at, own, other, wq, wk, wv, gain, wo_shape):
    streams, parts, chips, held, width = own.shape
    features = wq.shape[0]
    groups = 2 * chips
    rows = features // (streams * parts)
    block_cols = wo_shape[1] // width
    per_block = streams * parts // block_cols
    wo_rows = wo_shape[0] // groups // per_block
    by_rows = lambda w: pl.BlockSpec((rows, w.shape[1]), lambda s, r, at: (s * parts + r, 0))
    taken = pl.BlockSpec(
        (None, None, chips, held, width), lambda s, r, at: (s, jnp.bitwise_xor(r, at[s]), 0, 0, 0)
    )
    gain_spec = pl.BlockSpec((1, rows), lambda s, r, at: (0, s * parts + r))
    outs = pl.pallas_call(
        dense_out_kernel,
        grid_spec=pltpu.PrefetchScalarGridSpec(
            num_scalar_prefetch=1,
            grid=(streams, parts),
            in_specs=[taken, taken, by_rows(wq), by_rows(wk), by_rows(wv), gain_spec],
            out_specs=[
                by_rows(wq),
                by_rows(wk),
                by_rows(wv),
                gain_spec,
                pl.BlockSpec(
                    (groups, 1, wo_rows, width),
                    lambda s, r, at: (
                        0,
                        lax.rem(s * parts + r, per_block),
                        0,
                        lax.div(s * parts + r, per_block),
                    ),
                ),
                pl.BlockSpec((1, width), lambda s, r, at: (0, lax.div(s * parts + r, per_block))),
            ],
        ),
        out_shape=[
            jax.ShapeDtypeStruct(wq.shape, f32),
            jax.ShapeDtypeStruct(wk.shape, f32),
            jax.ShapeDtypeStruct(wv.shape, f32),
            jax.ShapeDtypeStruct((1, features), f32),
            jax.ShapeDtypeStruct((groups, per_block, wo_rows, wo_shape[1]), f32),
            jax.ShapeDtypeStruct((1, wo_shape[1]), f32),
        ],
        compiler_params=params(48, "arbitrary", "arbitrary"),
        cost_estimate=cost(2 * wq.size, 2.4e7),
        name="dense_weights_out",
    )(at, own, other, wq, wk, wv, gain)
    return (*outs[:4], outs[4].reshape(wo_shape), outs[5])


def weights_out_kernel(wide_ref, wq_ref, wk_ref, wv_ref, gain_ref, dq_ref, dk_ref, dv_ref, dg_ref):
    groups, rows, width = wide_ref.shape
    pair = width // 2
    total = jnp.zeros((rows, pair), f32)
    for g in range(groups):
        part = wide_ref[g, :, :pair].astype(f32)
        at = slice(g * pair, (g + 1) * pair)
        dq_ref[:, at] = part
        total += part * wq_ref[:, at].astype(f32)
    for g in range(groups // 2):
        a = wide_ref[2 * g, :, pair:].astype(f32)
        b = wide_ref[2 * g + 1, :, pair:].astype(f32)
        lane = lax.broadcasted_iota(jnp.int32, a.shape, 1)
        at = slice(g * pair, (g + 1) * pair)
        k = jnp.where(lane < HEAD_DIM, a, pltpu.roll(b, HEAD_DIM, 1))
        v = jnp.where(lane < HEAD_DIM, pltpu.roll(a, HEAD_DIM, 1), b)
        dk_ref[:, at] = k
        dv_ref[:, at] = v
        total += k * wk_ref[:, at].astype(f32) + v * wv_ref[:, at].astype(f32)
    dg_ref[...] = jnp.sum(jnp.transpose(total), axis=0, keepdims=True) / gain_ref[...]


def weights_out_call(wide, wq, wk, wv, gain):
    chunks, groups, rows, width = wide.shape
    features = chunks * rows
    by_rows = lambda w: pl.BlockSpec((rows, w.shape[1]), lambda c: (c, 0))
    return pl.pallas_call(
        weights_out_kernel,
        grid=(chunks,),
        in_specs=[
            pl.BlockSpec((None, groups, rows, width), lambda c: (c, 0, 0, 0)),
            by_rows(wq),
            by_rows(wk),
            by_rows(wv),
            pl.BlockSpec((1, rows), lambda c: (0, c)),
        ],
        out_specs=[
            by_rows(wq),
            by_rows(wk),
            by_rows(wv),
            pl.BlockSpec((1, rows), lambda c: (0, c)),
        ],
        out_shape=[
            jax.ShapeDtypeStruct(wq.shape, f32),
            jax.ShapeDtypeStruct(wk.shape, f32),
            jax.ShapeDtypeStruct(wv.shape, f32),
            jax.ShapeDtypeStruct((1, features), f32),
        ],
        compiler_params=params(32, "arbitrary"),
        cost_estimate=cost(2 * wq.size, 1.6e7),
        name="attention_weights_out",
    )(wide, wq, wk, wv, gain)


def last_kernel(d_ref, wq_ref, wk_ref, wv_ref, x_ref, gain_ref, dmid_ref, out_ref):
    groups, rows, width = d_ref.shape
    pair = width // 2
    dq = jnp.concatenate([d_ref[g, :, :pair] for g in range(groups)], axis=1)
    grad = dot_nt(dq, wq_ref[...])
    keys, vals = [], []
    for at in range(groups // 2):
        a = d_ref[2 * at, :, pair:].astype(f32)
        b = d_ref[2 * at + 1, :, pair:].astype(f32)
        lane = lax.broadcasted_iota(jnp.int32, a.shape, 1)
        keys.append(jnp.where(lane < HEAD_DIM, a, pltpu.roll(b, HEAD_DIM, 1)).astype(bf16))
        vals.append(jnp.where(lane < HEAD_DIM, pltpu.roll(a, HEAD_DIM, 1), b).astype(bf16))
    grad = grad + dot_nt(jnp.concatenate(keys, axis=1), wk_ref[...])
    grad = grad + dot_nt(jnp.concatenate(vals, axis=1), wv_ref[...])
    x = x_ref[...].astype(f32)
    scale = lax.rsqrt(jnp.mean(x * x, axis=-1, keepdims=True) + norm_eps)
    unit = x * scale
    w = gain_ref[...] * grad
    out_ref[...] = dmid_ref[...] + scale * (w - unit * jnp.mean(w * unit, axis=-1, keepdims=True))


def last_call(d, wq, wk, wv, x, gain, dmid):
    rows, features = x.shape
    return pl.pallas_call(
        last_kernel,
        out_shape=jax.ShapeDtypeStruct((rows, features), f32),
        compiler_params=params(40),
        cost_estimate=cost(4 * rows * features * features, 8e6),
        name="input_gradient",
    )(d, wq, wk, wv, x, gain, dmid)


def swap(values, axis, bit):
    return lax.ppermute(values, axis, [(i, i ^ bit) for i in range(lax.axis_size(axis))])


def half_sum(values, axis, bit):
    half = values.shape[0] // 2
    upper = ((lax.axis_index(axis) & bit) > 0).astype(jnp.int32)
    came = swap(lax.dynamic_slice_in_dim(values, (1 - upper) * half, half), axis, bit)
    mine = lax.dynamic_slice_in_dim(values, upper * half, half)
    return (mine.astype(f32) + came.astype(f32)).astype(bf16)


def relative_sum(kept, sent, axis, bits):
    while True:
        kept = (kept.astype(f32) + swap(sent, axis, bits[0]).astype(f32)).astype(bf16)
        bits = bits[1:]
        if not bits:
            return kept
        half = kept.shape[0] // 2
        kept, sent = kept[:half], kept[half:]


def join_parts(stream, axis, bits):
    shape = stream.shape
    for bit in bits[::-1]:
        stream = jnp.stack([stream, swap(stream, axis, bit)])
    return stream.reshape(-1, *shape)


def body(
    layer_input,
    first_gain,
    query_weight,
    key_weight,
    value_weight,
    output_weight,
    second_gain,
    gate_weight,
    up_weight,
    down_weight,
    expert_ids,
    gate_values,
    positions,
    cotangent,
):
    micro, _, per_device, features = layer_input.shape
    devices = lax.axis_size("seq")
    replicas = lax.axis_size("dp")
    seq_place = lax.axis_index("seq")
    rows = micro * per_device
    local_experts = gate_weight.shape[0]
    groups = key_weight.shape[1] // HEAD_DIM
    pair = query_weight.shape[1] // groups
    copies = devices // groups

    dp_bits = [1 << i for i in range(replicas.bit_length() - 1)]

    def spread(blocks):
        if copies > 1:
            blocks = jnp.repeat(blocks, copies, axis=0)
        return lax.all_to_all(blocks, "seq", 0, 0, tiled=True)

    def unspread(blocks):
        return lax.all_to_all(blocks, "seq", 0, 0, tiled=True)[::copies]

    x = layer_input.reshape(rows, features)
    cot = cotangent.reshape(rows, features)
    gain_one = first_gain.reshape(1, features)
    gain_two = second_gain.reshape(1, features)
    pos_all = lax.all_to_all(
        jnp.broadcast_to(positions.reshape(1, rows), (devices, rows)), "seq", 0, 0, tiled=True
    )
    x_all = lax.all_gather(x, "seq", axis=0)
    cos_all, sin_all = rope_tables(pos_all.reshape(-1), pair)
    mine = seq_place * local_experts + jnp.arange(local_experts, dtype=jnp.int32)
    ids = expert_ids[:, 0]
    gates = gate_values[:, 0].astype(f32)
    routed = jnp.sum(
        jnp.where(ids[..., None] == mine, gates[..., None], 0.0), axis=2
    )
    routed = routed.reshape(micro, devices, per_device, local_experts)
    routed = jnp.transpose(routed, (1, 0, 2, 3)).reshape(devices * rows, local_experts)
    group = seq_place // copies
    w_own = jnp.concatenate(
        [
            lax.dynamic_slice_in_dim(query_weight, group * pair, pair, axis=1),
            lax.dynamic_slice_in_dim(key_weight, group * HEAD_DIM, HEAD_DIM, axis=1),
            lax.dynamic_slice_in_dim(value_weight, group * HEAD_DIM, HEAD_DIM, axis=1),
        ],
        axis=1,
    )
    cos_all, sin_all, routed, w_own = lax.optimization_barrier((cos_all, sin_all, routed, w_own))
    x_all, cot_then, cos_all, sin_all, routed, w_own = lax.optimization_barrier(
        (x_all, cot, cos_all, sin_all, routed, w_own)
    )
    cot_all = lax.all_gather(cot_then, "seq", axis=0)

    qkv, first_all = qkv_call(x_all, gain_one, cos_all, sin_all, w_own)
    qkv = qkv.reshape(devices, micro, per_device, 2 * pair)
    mix, log_total = attend_call(qkv)
    mix = unspread(mix.reshape(devices, rows, pair))
    mixed, middle, second_low = post_call(mix, output_weight, x, gain_two)

    chips = devices // 2
    chip, core = seq_place // 2, seq_place % 2
    onward = [(i, (i + 2) % devices) for i in range(devices)]
    dp_place = lax.axis_index("dp")
    first_bit = dp_place & 1
    last_bit = dp_place >> (len(dp_bits) - 1)
    held, onward_from, kept, running = second_low, second_low, (), None
    for hop in range(chips):
        following = lax.ppermute(onward_from, "seq", onward) if hop < chips - 1 else None
        other = swap(held, "seq", 1)
        source = 2 * ((chip - hop) % chips)
        place = jnp.stack([source + core, source + 1 - core, 1 - first_bit, 1 - last_bit])
        place = place.astype(jnp.int32)
        dx, *kept = expert_call(
            hop, place, held, other, cot_all, routed, gate_weight, up_weight, down_weight, kept
        )
        if following is not None:
            following, dx = lax.optimization_barrier((following, dx))
        onward_from = following
        part = dx[0].astype(f32) + swap(dx[1], "seq", 1).astype(f32)
        if hop == 0:
            own_part = part
        else:
            if running is not None:
                part = part + running.astype(f32)
            part = part.astype(bf16)
            if following is not None:
                part, following = lax.optimization_barrier((part, following))
            else:
                part, kept = lax.optimization_barrier((part, kept))
            running = lax.ppermute(part, "seq", onward)
        held = following
    second_grad = (own_part + running.astype(f32)).astype(bf16)
    moe_all, *kept = kept

    def weight_parts(at, tokens, hidden_a, hidden_b, gate_low, up_low, slot_a, slot_b):
        pairs = (
            (tokens, gate_low[at]),
            (tokens, up_low[at]),
            (hidden_a[at], slot_a[at]),
            (hidden_b[at], slot_b[at]),
        )
        return [
            lax.dot_general(a, b, TN, preferred_element_type=f32).astype(bf16) for a, b in pairs
        ]

    leaving = weight_parts(0, *kept)
    part_bits = (dp_bits[0], dp_bits[-1], dp_bits[0], dp_bits[-1])
    stream_bits = (dp_bits, dp_bits[::-1])
    came = [swap(values, "dp", bit) for values, bit in zip(leaving, part_bits)]
    leaving, second_grad = lax.optimization_barrier((leaving, second_grad))

    mg_send, proj, middle_grad, gain_two_part = turn_call(
        second_grad, middle, gain_two, cot, output_weight, groups
    )
    mg = spread(mg_send)
    kept, _ = lax.optimization_barrier((kept, mg_send))
    mixed, proj, came[2:] = lax.optimization_barrier((mixed, proj, came[2:]))
    dense = output_weight_call(mixed, proj, gain_two_part, devices)
    dense_own = dense
    staying = weight_parts(1, *kept)
    turned = sum(((dp_place >> i) & 1) << (len(dp_bits) - 1 - i) for i in range(len(dp_bits)))
    part_at = jnp.stack([turned, dp_place]).astype(jnp.int32)
    low_at = jnp.bitwise_and(part_at, replicas // 2 - 1)
    keep_a, send_a, keep_b, send_b = part_sum_call(low_at, replicas // 2, came, staying)
    mg, keep_a, send_a, keep_b, send_b = lax.optimization_barrier(
        (mg, keep_a, send_a, keep_b, send_b)
    )
    streams = [
        relative_sum(keep_a, send_a, "dp", stream_bits[0][1:]),
        relative_sum(keep_b, send_b, "dp", stream_bits[1][1:]),
    ]
    dense = dense_own
    dense = lax.psum_scatter(dense, "seq", scatter_dimension=0)
    moe_all, _ = lax.optimization_barrier((moe_all, mg))
    moe = lax.psum_scatter(moe_all, "seq", scatter_dimension=0)
    layer_output = (middle + residual_scale * moe.astype(f32)).astype(bf16)
    table_shape = (devices, micro, per_device, pair)
    dqkv = attend_back_call(
        qkv,
        mg.reshape(devices, micro, per_device, pair),
        log_total,
        cos_all.reshape(table_shape),
        sin_all.reshape(table_shape),
    )
    dqkv, streams = lax.optimization_barrier((dqkv, streams))
    near = [
        [v[0], swap(v[0], "dp", bits[-1])] for v, bits in zip(streams, stream_bits)
    ]
    back = unspread(dqkv.reshape(devices, rows, 2 * pair))
    d_all = dqkv.reshape(devices * rows, 2 * pair)
    first_tokens = first_all.reshape(devices * rows, features)
    part = lax.dot_general(first_tokens, d_all, TN, preferred_element_type=f32)
    dense = dense.reshape(dense.shape[-2], features)
    each = output_weight.shape[0] // devices
    if copies == 1:
        width = 2 * pair
        kept_pieces, sent_pieces = joint_call(part_at, part, dense, replicas)
        first = [
            kept_pieces[at].astype(f32) + swap(sent_pieces[at], "dp", bits[0]).astype(f32)
            for at, bits in enumerate(stream_bits)
        ]
        first, near = lax.optimization_barrier(([v.astype(bf16) for v in first], near))
        own = [
            relative_sum(v[: replicas // 4], v[replicas // 4 :], "dp", bits[1:])
            for v, bits in zip(first, stream_bits)
        ]
        own = jnp.concatenate(own, axis=0)
        own, here = lax.optimization_barrier((own, [v[0] for v in near]))
        far = [[swap(v, "dp", bits[-2])] for v, bits in zip(here, stream_bits)]
        backward = [(i, (i - 2) % devices) for i in range(devices)]
        round_ring = {0: own}
        for k in range(1, chips // 2 + 1):
            round_ring[k] = lax.ppermute(round_ring[k - 1], "seq", onward)
            if chips - k > k:
                round_ring[chips - k] = lax.ppermute(
                    round_ring[(chips - k + 1) % chips], "seq", backward
                )
        held = jnp.stack([round_ring[k] for k in range(chips)])
        held, back, far = lax.optimization_barrier((held, back, far))
    else:
        far = [[swap(v[0], "dp", bits[-2])] for v, bits in zip(streams, stream_bits)]
    expert_pieces = []
    for (here, first), (second,), bits in zip(near, far, stream_bits):
        pieces = [here, first, second, swap(first, "dp", bits[-2])]
        for bit in bits[:-2][::-1]:
            pieces = pieces + [swap(p, "dp", bit) for p in pieces]
        expert_pieces.append(pieces)
    input_grad = last_call(
        back, query_weight, key_weight, value_weight, x, gain_one, middle_grad
    )
    if copies == 1:
        full = [join_parts(held[:, at], "dp", b) for at, b in enumerate(stream_bits)]
        full, input_grad, layer_output = lax.optimization_barrier(
            (jnp.stack(full), input_grad, layer_output)
        )
        other = swap(full, "seq", 1)
        where_at = jnp.stack([turned, dp_place, chip, core]).astype(jnp.int32)
        (
            query_weight_grad,
            key_weight_grad,
            value_weight_grad,
            first_gain_grad,
            output_weight_grad,
            second_gain_grad,
        ) = dense_out_call(
            where_at, full, other, query_weight, key_weight, value_weight, gain_one, output_weight.shape
        )
        query_weight_grad, expert_pieces = lax.optimization_barrier(
            (query_weight_grad, expert_pieces)
        )
    else:
        for bit in dp_bits:
            dense = (dense.astype(f32) + swap(dense, "dp", bit).astype(f32)).astype(bf16)
        dense = lax.all_gather(dense, "seq", axis=0).astype(f32)
        output_weight_grad = dense[:, :each].reshape(output_weight.shape)
        second_gain_grad = dense[0, each]
        part = part.astype(bf16)
        for bit in dp_bits[::-1]:
            part = half_sum(part, "dp", bit)
        wide = lax.all_gather(part, ("dp", "seq"), axis=0)
        wide = wide.reshape(replicas, devices, features // replicas, 2 * pair)[:, ::copies]
        query_weight_grad, key_weight_grad, value_weight_grad, first_gain_grad = weights_out_call(
            wide, query_weight, key_weight, value_weight, gain_one
        )
    second_gain_grad = second_gain_grad.reshape(features)
    gate_sum, up_sum, down_sum = expert_out_call(
        part_at, *expert_pieces, gate_weight.shape, down_weight.shape
    )
    return (
        layer_output.reshape(layer_input.shape),
        input_grad.reshape(layer_input.shape),
        first_gain_grad.reshape(features),
        query_weight_grad,
        key_weight_grad,
        value_weight_grad,
        output_weight_grad,
        second_gain_grad,
        gate_sum,
        up_sum,
        down_sum,
    )


def solution(mesh):
    return jax.shard_map(
        body,
        mesh=mesh,
        in_specs=(
            P(None, "dp", "seq", None),
            P(),
            P(),
            P(),
            P(),
            P(),
            P(),
            P("seq", None, None),
            P("seq", None, None),
            P("seq", None, None),
            P(None, "dp", None, None),
            P(None, "dp", None, None),
            P(None, "dp", "seq"),
            P(None, "dp", "seq", None),
        ),
        out_specs=(
            P(None, "dp", "seq", None),
            P(None, "dp", "seq", None),
            P(),
            P(),
            P(),
            P(),
            P(),
            P(),
            P("seq", None, None),
            P("seq", None, None),
            P("seq", None, None),
        ),
        check_vma=False,
    )
```

```python
from functools import partial

import jax
import jax.numpy as jnp
from jax import lax
from jax.experimental import pallas as pl
from jax.experimental.pallas import tpu as pltpu
from jax.sharding import PartitionSpec as P

HEAD_DIM = 64

rope_theta = 10000.0
attention_scale = 0.015625
residual_scale = 0.22
norm_eps = 1e-06
masked_score = -1e30

f32 = jnp.float32
bf16 = jnp.bfloat16
NT = (((1,), (1,)), ((), ()))
TN = (((0,), (0,)), ((), ()))


def dot(a, b):
    return jnp.dot(a, b, preferred_element_type=f32)


def dot_nt(a, b):
    return lax.dot_general(a, b, NT, preferred_element_type=f32)


def params(mib, *semantics):
    return pltpu.CompilerParams(
        vmem_limit_bytes=mib * 1024 * 1024, dimension_semantics=semantics or None
    )


def cost(flops, nbytes, trans=0):
    return pl.CostEstimate(
        flops=int(flops / 8), bytes_accessed=int(nbytes / 8), transcendentals=int(trans / 8)
    )


def whole(shape):
    return pl.BlockSpec(shape, lambda *_: (0,) * len(shape))


def rope_tables(positions, width):
    half = HEAD_DIM // 2
    exponent = jnp.arange(half, dtype=f32) * (-2.0 / HEAD_DIM)
    angles = positions.astype(f32)[:, None] * (rope_theta**exponent)[None, :]
    cosine, sine = jnp.cos(angles), jnp.sin(angles)
    copies = width // HEAD_DIM
    cos_row = jnp.concatenate([cosine, cosine] * copies, axis=1)
    sin_row = jnp.concatenate([-sine, sine] * copies, axis=1)
    return cos_row, sin_row


def partner(values):
    width = values.shape[1]
    half = HEAD_DIM // 2
    lane = lax.broadcasted_iota(jnp.int32, values.shape, 1)
    ahead = pltpu.roll(values, width - half, 1)
    behind = pltpu.roll(values, half, 1)
    return jnp.where(lane % HEAD_DIM < half, ahead, behind)


def qkv_kernel(x_ref, gain_ref, cos_ref, sin_ref, w_ref, qkv_ref, low_ref):
    pair = 2 * HEAD_DIM
    x = x_ref[0].astype(f32)
    scale = lax.rsqrt(jnp.mean(x * x, axis=-1, keepdims=True) + norm_eps)
    low = (x * scale * gain_ref[...]).astype(bf16)
    low_ref[0] = low
    cosine, sine = cos_ref[...], sin_ref[...]
    made = dot(low, w_ref[...])
    q, kv = made[:, :pair], made[:, pair:]
    q = (q * cosine + partner(q) * sine) * attention_scale
    qkv_ref[0, :, :pair] = q.astype(bf16)
    lane = lax.broadcasted_iota(jnp.int32, kv.shape, 1)
    turned = kv * cosine + partner(kv) * sine
    qkv_ref[0, :, pair:] = jnp.where(lane < HEAD_DIM, turned, kv).astype(bf16)


def qkv_call(x_all, gain, cos_all, sin_all, w_own):
    blocks, rows, features = x_all.shape
    pair = 2 * HEAD_DIM
    return pl.pallas_call(
        qkv_kernel,
        grid=(blocks,),
        in_specs=[
            pl.BlockSpec((1, rows, features), lambda s: (s, 0, 0)),
            whole((1, features)),
            pl.BlockSpec((rows, pair), lambda s: (s, 0)),
            pl.BlockSpec((rows, pair), lambda s: (s, 0)),
            whole(w_own.shape),
        ],
        out_specs=[
            pl.BlockSpec((1, rows, 2 * pair), lambda s: (s, 0, 0)),
            pl.BlockSpec((1, rows, features), lambda s: (s, 0, 0)),
        ],
        out_shape=[
            jax.ShapeDtypeStruct((blocks, rows, 2 * pair), bf16),
            jax.ShapeDtypeStruct((blocks, rows, features), bf16),
        ],
        compiler_params=params(58, "arbitrary"),
        cost_estimate=cost(4 * blocks * rows * features * pair, 14e6),
        name="norm_qkv_rope",
    )(x_all, gain, cos_all, sin_all, w_own)


def split_heads(block, first):
    wide = block.astype(f32)
    lane = lax.broadcasted_iota(jnp.int32, wide.shape, 1)
    turned = pltpu.roll(wide, HEAD_DIM, 1)
    if first:
        parts = [jnp.where(lane < HEAD_DIM, wide, 0.0), jnp.where(lane < HEAD_DIM, turned, 0.0)]
    else:
        parts = [jnp.where(lane >= HEAD_DIM, turned, 0.0), jnp.where(lane >= HEAD_DIM, wide, 0.0)]
    return jnp.concatenate(parts, axis=0).astype(bf16)


def join_heads(turned):
    rows = turned.shape[1] // 2
    return jnp.transpose(jnp.concatenate([turned[:, :rows], turned[:, rows:]], axis=0))


def scores_of(kv, q2, rows):
    scores = dot_nt(kv, q2)
    count = scores.shape[0]
    own = scores[count - rows :]
    key_at = lax.broadcasted_iota(jnp.int32, own.shape, 0)
    query_at = lax.broadcasted_iota(jnp.int32, own.shape, 1) % rows
    own = jnp.where(key_at <= query_at, own, masked_score)
    if count == rows:
        return own
    return jnp.concatenate([scores[: count - rows], own], axis=0)


def attend_kernel(qkv_ref, out_ref, log_ref):
    blocks, _, rows, width = qkv_ref.shape
    pair = width // 2
    kv = qkv_ref[:, 0, :, pair:].reshape(blocks * rows, pair)
    kv_t = jnp.transpose(kv)
    for at in range(blocks):
        count = (at + 1) * rows
        q2 = split_heads(qkv_ref[at, 0, :, :pair], True)
        scores = scores_of(kv[:count], q2, rows)
        top = jnp.max(scores, axis=0, keepdims=True)
        weights = jnp.exp(scores - top)
        total = jnp.sum(weights, axis=0, keepdims=True)
        out_t = dot(kv_t[:, :count], weights.astype(bf16))
        out_ref[at, 0] = join_heads(out_t[HEAD_DIM:] / total).astype(bf16)
        log_ref[at, 0] = top + jnp.log(total)


def attend_call(qkv):
    blocks, micro, rows, width = qkv.shape
    pair = width // 2
    length = blocks * rows
    return pl.pallas_call(
        attend_kernel,
        grid=(micro,),
        in_specs=[pl.BlockSpec((blocks, 1, rows, width), lambda m: (0, m, 0, 0))],
        out_specs=[
            pl.BlockSpec((blocks, 1, rows, pair), lambda m: (0, m, 0, 0)),
            pl.BlockSpec((blocks, 1, 1, 2 * rows), lambda m: (0, m, 0, 0)),
        ],
        out_shape=[
            jax.ShapeDtypeStruct((blocks, micro, rows, pair), bf16),
            jax.ShapeDtypeStruct((blocks, micro, 1, 2 * rows), f32),
        ],
        compiler_params=params(48, "arbitrary"),
        cost_estimate=cost(
            micro * length * length * 512, 3 * qkv.size, micro * length * length
        ),
        name="attention_forward",
    )(qkv)


def attend_back_kernel(qkv_ref, grad_ref, log_ref, cos_ref, sin_ref, out_ref, dkv_ref):
    blocks, _, rows, width = qkv_ref.shape
    pair = width // 2
    kv = qkv_ref[:, 0, :, pair:].reshape(blocks * rows, pair)
    kv_t = jnp.transpose(kv)
    dkv_ref[...] = jnp.zeros_like(dkv_ref)
    for at in range(blocks):
        count = (at + 1) * rows
        q2 = split_heads(qkv_ref[at, 0, :, :pair], True)
        g2 = split_heads(grad_ref[at, 0], False)
        scores = scores_of(kv[:count], q2, rows)
        prob = jnp.exp(scores - log_ref[at, 0])
        prob_grad = dot_nt(kv[:count], g2)
        delta = jnp.sum(prob * prob_grad, axis=0, keepdims=True)
        score_grad = (prob * (prob_grad - delta)).astype(bf16)
        dkv_ref[:count] += dot(score_grad, q2) + dot(prob.astype(bf16), g2)
        dq_t = dot(kv_t[:, :count], score_grad)
        dq = join_heads(dq_t[:HEAD_DIM] * attention_scale)
        dq = dq * cos_ref[at, 0] - partner(dq) * sin_ref[at, 0]
        out_ref[at, 0, :, :pair] = dq.astype(bf16)
    for at in range(blocks):
        dkv = dkv_ref[at * rows : (at + 1) * rows]
        lane = lax.broadcasted_iota(jnp.int32, dkv.shape, 1)
        turned = dkv * cos_ref[at, 0] - partner(dkv) * sin_ref[at, 0]
        out_ref[at, 0, :, pair:] = jnp.where(lane < HEAD_DIM, turned, dkv).astype(bf16)


def attend_back_call(qkv, grads, log_total, cos_all, sin_all):
    blocks, micro, rows, width = qkv.shape
    pair = width // 2
    length = blocks * rows
    spec = lambda lanes: pl.BlockSpec((blocks, 1, rows, lanes), lambda m: (0, m, 0, 0))
    return pl.pallas_call(
        attend_back_kernel,
        grid=(micro,),
        in_specs=[
            spec(width),
            spec(pair),
            pl.BlockSpec((blocks, 1, 1, 2 * rows), lambda m: (0, m, 0, 0)),
            spec(pair),
            spec(pair),
        ],
        out_specs=spec(width),
        out_shape=jax.ShapeDtypeStruct(qkv.shape, bf16),
        scratch_shapes=[pltpu.VMEM((length, pair), f32)],
        compiler_params=params(56, "arbitrary"),
        cost_estimate=cost(
            micro * length * length * 1280, 10 * qkv.size, micro * length * length
        ),
        name="attention_backward",
    )(qkv, grads, log_total, cos_all, sin_all)


def post_kernel(mix_ref, wo_ref, x_ref, gain_ref, mixed_ref, middle_ref, low_ref):
    mixed = jnp.concatenate([mix_ref[g] for g in range(mix_ref.shape[0])], axis=1)
    mixed_ref[...] = mixed
    middle = x_ref[...].astype(f32) + residual_scale * dot(mixed, wo_ref[...])
    middle_ref[...] = middle
    scale = lax.rsqrt(jnp.mean(middle * middle, axis=-1, keepdims=True) + norm_eps)
    low_ref[...] = (middle * scale * gain_ref[...]).astype(bf16)


def post_call(mix, wo, x, gain):
    rows, features = x.shape
    return pl.pallas_call(
        post_kernel,
        out_shape=[
            jax.ShapeDtypeStruct((rows, wo.shape[0]), bf16),
            jax.ShapeDtypeStruct((rows, features), f32),
            jax.ShapeDtypeStruct((rows, features), bf16),
        ],
        compiler_params=params(32),
        cost_estimate=cost(2 * rows * wo.size, 5e6),
        name="project_norm",
    )(mix, wo, x, gain)


def expert_kernel(place_ref, a_ref, b_ref, cot_ref, w_ref, wg_ref, wu_ref, wd_ref, *refs):
    dx_ref, x_ref, ha_ref, hb_ref, dg_ref, du_ref, sa_ref, sb_ref = refs[-8:]
    step = pl.program_id(0)
    first, second = place_ref[2], place_ref[3]
    half = sa_ref.shape[2]

    @pl.when(step == 0)
    def _():
        x_ref[...] = a_ref[...]

    @pl.when(step == 1)
    def _():
        x_ref[...] = b_ref[...]

    x = x_ref[...]
    cot = cot_ref[0].astype(f32)
    weight = residual_scale * w_ref[...]
    total = None
    for e in range(wg_ref.shape[0]):
        gate = dot(x, wg_ref[e])
        up = dot(x, wu_ref[e])
        slot_grad = (weight[:, e : e + 1] * cot).astype(bf16)
        to_a, to_b = jnp.bitwise_xor(first, e), jnp.bitwise_xor(second, e)
        sa_ref[to_a] = slot_grad[:, :half]
        sb_ref[to_b] = slot_grad[:, half:]
        hidden_grad = dot_nt(slot_grad, wd_ref[e])
        sig = 0.5 * jnp.tanh(0.5 * gate) + 0.5
        silu = gate * sig
        hidden = (silu * up).astype(bf16)
        ha_ref[to_a] = hidden
        hb_ref[to_b] = hidden
        gate_grad = (hidden_grad * up * (sig + silu * (1.0 - sig))).astype(bf16)
        up_grad = (hidden_grad * silu).astype(bf16)
        dg_ref[to_a] = gate_grad
        du_ref[to_b] = up_grad
        term = dot_nt(gate_grad, wg_ref[e]) + dot_nt(up_grad, wu_ref[e])
        total = term if total is None else total + term
    dx_ref[0] = total.astype(bf16)


def expert_call(at, place, own, other, cot_all, weight, wg, wu, wd, kept):
    blocks, rows, features = cot_all.shape
    count, _, hidden = wg.shape
    tokens = blocks * rows
    inner = jax.ShapeDtypeStruct((count, tokens, hidden), bf16)
    outer = jax.ShapeDtypeStruct((count, tokens, features // 2), bf16)
    inner_spec = pl.BlockSpec((count, rows, hidden), lambda s, place: (0, 2 * at + s, 0))
    outer_spec = pl.BlockSpec((count, rows, features // 2), lambda s, place: (0, 2 * at + s, 0))
    fixed = lambda shape: pl.BlockSpec(shape, lambda s, place: (0,) * len(shape))
    any_spec = pl.BlockSpec(memory_space=pl.ANY)
    first = 8
    return pl.pallas_call(
        expert_kernel,
        grid_spec=pltpu.PrefetchScalarGridSpec(
            num_scalar_prefetch=1,
            grid=(2,),
            in_specs=[
                fixed((rows, features)),
                fixed((rows, features)),
                pl.BlockSpec((1, rows, features), lambda s, place: (place[s], 0, 0)),
                pl.BlockSpec((rows, count), lambda s, place: (place[s], 0)),
                fixed(wg.shape),
                fixed(wu.shape),
                fixed(wd.shape),
            ]
            + [any_spec] * len(kept),
            out_specs=[
                pl.BlockSpec((1, rows, features), lambda s, place: (s, 0, 0)),
                pl.BlockSpec((rows, features), lambda s, place: (2 * at + s, 0)),
            ]
            + [inner_spec] * 4
            + [outer_spec] * 2,
        ),
        out_shape=[
            jax.ShapeDtypeStruct((2, rows, features), bf16),
            jax.ShapeDtypeStruct((tokens, features), bf16),
            inner,
            inner,
            inner,
            inner,
            outer,
            outer,
        ],
        input_output_aliases={first + i: 1 + i for i in range(len(kept))},
        compiler_params=params(48, "arbitrary"),
        cost_estimate=cost(20 * rows * wg.size, 2e7, 2 * rows * hidden * count),
        name="experts",
    )(place, own, other, cot_all, weight, wg, wu, wd, *kept)


def part_sum_kernel(at_ref, *refs):
    inputs, outs = refs[:16], refs[16:]
    at = 0
    for out in outs:
        gate_came, gate_here, down_came, down_here = inputs[at : at + 4]
        rows = gate_came.shape[0]
        out[0, :rows] = (gate_came[...].astype(f32) + gate_here[...].astype(f32)).astype(bf16)
        out[0, rows:] = (down_came[...].astype(f32) + down_here[...].astype(f32)).astype(bf16)
        at += 4


def part_sum_call(at, per, came, here):
    gate_rows, down_rows = came[0].shape[0] // per, came[2].shape[0] // per
    width = came[0].shape[1]
    steps = per // 2
    specs, args, out_specs, out_shapes = [], [], [], []
    for stream in range(2):
        for sent in range(2):
            for which, rows in ((stream, gate_rows), (stream + 2, down_rows)):
                spec = pl.BlockSpec(
                    (rows, width),
                    lambda s, at, sent=sent, stream=stream: (
                        jnp.bitwise_xor(s + sent * steps, at[stream]),
                        0,
                    ),
                )
                specs += [spec, spec]
                args += [came[which], here[which]]
            out_specs.append(
                pl.BlockSpec((1, gate_rows + down_rows, width), lambda s, at: (s, 0, 0))
            )
            out_shapes.append(
                jax.ShapeDtypeStruct((steps, gate_rows + down_rows, width), bf16)
            )
    return pl.pallas_call(
        part_sum_kernel,
        grid_spec=pltpu.PrefetchScalarGridSpec(
            num_scalar_prefetch=1, grid=(steps,), in_specs=specs, out_specs=out_specs
        ),
        out_shape=out_shapes,
        compiler_params=params(60, "arbitrary"),
        cost_estimate=cost(0, 9e6),
        name="expert_part_sum",
    )(at, *args)


def joint_kernel(at_ref, *refs):
    for (part_ref, wo_ref, gain_ref), out_ref in ((refs[:3], refs[6]), (refs[3:6], refs[7])):
        rows = part_ref.shape[0]
        upto = rows + wo_ref.shape[0]
        out_ref[0, 0, :rows] = part_ref[...].astype(bf16)
        out_ref[0, 0, rows:upto] = wo_ref[...]
        out_ref[0, 0, upto:] = gain_ref[...]


def joint_call(at, part, dense, parts):
    features, width = part.shape
    pieces = 2 * parts
    rows = features // pieces
    block_cols = dense.shape[1] // width
    per_block = pieces // block_cols
    extra = 16
    wo_rows = (dense.shape[0] - extra) // per_block
    last = dense.shape[0] // extra - 1
    steps = parts // 2

    def piece(sent):
        return lambda s, p, at: s * parts + jnp.bitwise_xor(p + sent * steps, at[s])

    specs = []
    for sent in range(2):
        at_piece = piece(sent)
        specs.append(
            pl.BlockSpec((rows, width), lambda s, p, at, f=at_piece: (f(s, p, at), 0))
        )
        specs.append(
            pl.BlockSpec(
                (wo_rows, width),
                lambda s, p, at, f=at_piece: (
                    lax.rem(f(s, p, at), per_block),
                    lax.div(f(s, p, at), per_block),
                ),
            )
        )
        specs.append(
            pl.BlockSpec(
                (extra, width), lambda s, p, at, f=at_piece: (last, lax.div(f(s, p, at), per_block))
            )
        )
    out_spec = pl.BlockSpec((1, 1, rows + wo_rows + extra, width), lambda s, p, at: (s, p, 0, 0))
    out_shape = jax.ShapeDtypeStruct((2, steps, rows + wo_rows + extra, width), bf16)
    return pl.pallas_call(
        joint_kernel,
        grid_spec=pltpu.PrefetchScalarGridSpec(
            num_scalar_prefetch=1, grid=(2, steps), in_specs=specs, out_specs=[out_spec] * 2
        ),
        out_shape=[out_shape] * 2,
        compiler_params=params(32, "arbitrary", "arbitrary"),
        cost_estimate=cost(0, 2e6),
        name="dense_pieces",
    )(at, part, dense, dense, part, dense, dense)


def expert_out_kernel(at_ref, *refs):
    pieces, (gate_ref, up_ref, down_ref) = refs[:-3], refs[-3:]
    parts = len(pieces) // 2
    step = pl.program_id(0)
    rows = gate_ref.shape[1]
    half = down_ref.shape[2] // 2
    for which in range(parts):

        @pl.when(jnp.bitwise_xor(step, at_ref[0]) == which)
        def _():
            a_ref = pieces[which]
            gate_ref[0] = a_ref[:rows].astype(f32)
            down_ref[0, :, :half] = a_ref[rows:].astype(f32)

        @pl.when(jnp.bitwise_xor(step, at_ref[1]) == which)
        def _():
            b_ref = pieces[parts + which]
            up_ref[0] = b_ref[:rows].astype(f32)
            down_ref[0, :, half:] = b_ref[rows:].astype(f32)


def expert_out_call(at, a, b, gate_shape, down_shape):
    parts = len(a)
    held, width = a[0].shape
    count = gate_shape[0]
    per = parts // count
    gate_rows, down_rows = gate_shape[1] // per, down_shape[1] // per
    place = lambda r, at: (lax.div(r, per), lax.rem(r, per), 0)
    return pl.pallas_call(
        expert_out_kernel,
        grid_spec=pltpu.PrefetchScalarGridSpec(
            num_scalar_prefetch=1,
            grid=(parts,),
            in_specs=[pl.BlockSpec((held, width), lambda r, at: (0, 0))] * (2 * parts),
            out_specs=[
                pl.BlockSpec((1, gate_rows, gate_shape[2]), place),
                pl.BlockSpec((1, gate_rows, gate_shape[2]), place),
                pl.BlockSpec((1, down_rows, down_shape[2]), place),
            ],
        ),
        out_shape=[
            jax.ShapeDtypeStruct(gate_shape, f32),
            jax.ShapeDtypeStruct(gate_shape, f32),
            jax.ShapeDtypeStruct(down_shape, f32),
        ],
        compiler_params=params(40, "arbitrary"),
        cost_estimate=cost(0, 2e7),
        name="expert_weights_out",
    )(at, *a, *b)


def moe_kernel(place_ref, h_ref, w_ref, wd_ref, out_ref):
    weight = w_ref[...]
    total = None
    first = place_ref[pl.num_programs(0)]
    for e in range(wd_ref.shape[0]):
        term = weight[:, e : e + 1] * dot(h_ref[jnp.bitwise_xor(first, e)], wd_ref[e])
        total = term if total is None else total + term
    out_ref[0] = total.astype(bf16)


def moe_call(place, hidden, weight, wd, blocks):
    count, tokens, inner = hidden.shape
    features = wd.shape[2]
    rows = tokens // blocks
    return pl.pallas_call(
        moe_kernel,
        grid_spec=pltpu.PrefetchScalarGridSpec(
            num_scalar_prefetch=1,
            grid=(blocks,),
            in_specs=[
                pl.BlockSpec((count, rows, inner), lambda s, place: (0, s, 0)),
                pl.BlockSpec((rows, count), lambda s, place: (place[s], 0)),
                pl.BlockSpec(wd.shape, lambda s, place: (0, 0, 0)),
            ],
            out_specs=pl.BlockSpec((1, rows, features), lambda s, place: (place[s], 0, 0)),
        ),
        out_shape=jax.ShapeDtypeStruct((blocks, rows, features), bf16),
        compiler_params=params(60, "arbitrary"),
        cost_estimate=cost(2 * tokens * wd.size, 1.1e7),
        name="expert_outputs",
    )(place, hidden, weight, wd)


def turn_kernel(sg_ref, middle_ref, gain_ref, cot_ref, wo_ref, mg_ref, proj_ref, dmid_ref, dgain_ref):
    grad = sg_ref[...].astype(f32)
    middle = middle_ref[...]
    scale = lax.rsqrt(jnp.mean(middle * middle, axis=-1, keepdims=True) + norm_eps)
    unit = middle * scale
    dgain_ref[...] = jnp.sum(grad * unit, axis=0, keepdims=True)
    w = gain_ref[...] * grad
    dmid = cot_ref[...].astype(f32) + scale * (w - unit * jnp.mean(w * unit, axis=-1, keepdims=True))
    dmid_ref[...] = dmid
    proj = (residual_scale * dmid).astype(bf16)
    proj_ref[...] = proj
    mixed_grad = dot_nt(proj, wo_ref[...]).astype(bf16)
    groups, _, pair = mg_ref.shape
    for g in range(groups):
        mg_ref[g] = mixed_grad[:, g * pair : (g + 1) * pair]


def turn_call(sg, middle, gain, cot, wo, groups):
    rows, features = middle.shape
    pair = wo.shape[0] // groups
    return pl.pallas_call(
        turn_kernel,
        out_shape=[
            jax.ShapeDtypeStruct((groups, rows, pair), bf16),
            jax.ShapeDtypeStruct((rows, features), bf16),
            jax.ShapeDtypeStruct((rows, features), f32),
            jax.ShapeDtypeStruct((1, features), f32),
        ],
        compiler_params=params(32),
        cost_estimate=cost(2 * rows * wo.size, 6e6),
        name="norm_back_project_back",
    )(sg, middle, gain, cot, wo)


def output_weight_kernel(mixed_ref, proj_ref, dgain_ref, out_ref):
    held, each, features = out_ref.shape
    rows = mixed_ref.shape[1] // held
    part = lax.dot_general(mixed_ref[...], proj_ref[...], TN, preferred_element_type=f32)
    extra = jnp.broadcast_to(dgain_ref[...], (each - rows, features)).astype(bf16)
    for at in range(held):
        out_ref[at, :rows] = part[at * rows : (at + 1) * rows].astype(bf16)
        out_ref[at, rows:] = extra


def output_weight_call(mixed, proj, dgain, parts):
    rows, width = mixed.shape
    features = proj.shape[1]
    each = width // parts
    lanes = max(each, width // 2)
    held = lanes // each
    return pl.pallas_call(
        output_weight_kernel,
        grid=(parts // held,),
        in_specs=[
            pl.BlockSpec((rows, lanes), lambda s: (0, s)),
            whole((rows, features)),
            whole((1, features)),
        ],
        out_specs=pl.BlockSpec((held, each + 16, features), lambda s: (s, 0, 0)),
        out_shape=jax.ShapeDtypeStruct((parts, each + 16, features), bf16),
        compiler_params=params(32, "arbitrary"),
        cost_estimate=cost(2 * rows * width * features, 4e6),
        name="output_weight_part",
    )(mixed, proj, dgain)


def dense_out_kernel(
    at_ref, own_ref, other_ref, wq_ref, wk_ref, wv_ref, gain_ref, dq_ref, dk_ref, dv_ref, dg_ref, wo_ref, dg2_ref
):
    chips, _, width = own_ref.shape
    rows = dq_ref.shape[0]
    pair = width // 2
    chip, core = at_ref[2], at_ref[3]
    total = jnp.zeros((rows, pair), f32)
    for k in range(chips):
        source = lax.rem(chip - k + chips, chips)
        a = jnp.where(core == 0, own_ref[k], other_ref[k]).astype(f32)
        b = jnp.where(core == 0, other_ref[k], own_ref[k]).astype(f32)
        q = jnp.concatenate([a[:rows, :pair], b[:rows, :pair]], axis=1)
        cols = pl.ds(pl.multiple_of(source * width, width), width)
        dq_ref[:, cols] = q
        made = q * wq_ref[:, cols].astype(f32)
        total += made[:, :pair] + made[:, pair:]
        a_kv, b_kv = a[:rows, pair:], b[:rows, pair:]
        lane = lax.broadcasted_iota(jnp.int32, a_kv.shape, 1)
        key = jnp.where(lane < HEAD_DIM, a_kv, pltpu.roll(b_kv, HEAD_DIM, 1))
        val = jnp.where(lane < HEAD_DIM, pltpu.roll(a_kv, HEAD_DIM, 1), b_kv)
        cols = pl.ds(pl.multiple_of(source * pair, pair), pair)
        dk_ref[:, cols] = key
        dv_ref[:, cols] = val
        total += key * wk_ref[:, cols].astype(f32) + val * wv_ref[:, cols].astype(f32)
        wo_ref[2 * source, 0] = a[rows : rows + wo_ref.shape[2]]
        wo_ref[2 * source + 1, 0] = b[rows : rows + wo_ref.shape[2]]
        if k == 0:
            dg2_ref[...] = a[rows + wo_ref.shape[2] :][:1]
    dg_ref[...] = jnp.sum(jnp.transpose(total), axis=0, keepdims=True) / gain_ref[...]


def dense_out_call(at, own, other, wq, wk, wv, gain, wo_shape):
    streams, parts, chips, held, width = own.shape
    features = wq.shape[0]
    groups = 2 * chips
    rows = features // (streams * parts)
    block_cols = wo_shape[1] // width
    per_block = streams * parts // block_cols
    wo_rows = wo_shape[0] // groups // per_block
    by_rows = lambda w: pl.BlockSpec((rows, w.shape[1]), lambda s, r, at: (s * parts + r, 0))
    taken = pl.BlockSpec(
        (None, None, chips, held, width), lambda s, r, at: (s, jnp.bitwise_xor(r, at[s]), 0, 0, 0)
    )
    gain_spec = pl.BlockSpec((1, rows), lambda s, r, at: (0, s * parts + r))
    outs = pl.pallas_call(
        dense_out_kernel,
        grid_spec=pltpu.PrefetchScalarGridSpec(
            num_scalar_prefetch=1,
            grid=(streams, parts),
            in_specs=[taken, taken, by_rows(wq), by_rows(wk), by_rows(wv), gain_spec],
            out_specs=[
                by_rows(wq),
                by_rows(wk),
                by_rows(wv),
                gain_spec,
                pl.BlockSpec(
                    (groups, 1, wo_rows, width),
                    lambda s, r, at: (
                        0,
                        lax.rem(s * parts + r, per_block),
                        0,
                        lax.div(s * parts + r, per_block),
                    ),
                ),
                pl.BlockSpec((1, width), lambda s, r, at: (0, lax.div(s * parts + r, per_block))),
            ],
        ),
        out_shape=[
            jax.ShapeDtypeStruct(wq.shape, f32),
            jax.ShapeDtypeStruct(wk.shape, f32),
            jax.ShapeDtypeStruct(wv.shape, f32),
            jax.ShapeDtypeStruct((1, features), f32),
            jax.ShapeDtypeStruct((groups, per_block, wo_rows, wo_shape[1]), f32),
            jax.ShapeDtypeStruct((1, wo_shape[1]), f32),
        ],
        compiler_params=params(48, "arbitrary", "arbitrary"),
        cost_estimate=cost(2 * wq.size, 2.4e7),
        name="dense_weights_out",
    )(at, own, other, wq, wk, wv, gain)
    return (*outs[:4], outs[4].reshape(wo_shape), outs[5])


def weights_out_kernel(wide_ref, wq_ref, wk_ref, wv_ref, gain_ref, dq_ref, dk_ref, dv_ref, dg_ref):
    groups, rows, width = wide_ref.shape
    pair = width // 2
    total = jnp.zeros((rows, pair), f32)
    for g in range(groups):
        part = wide_ref[g, :, :pair].astype(f32)
        at = slice(g * pair, (g + 1) * pair)
        dq_ref[:, at] = part
        total += part * wq_ref[:, at].astype(f32)
    for g in range(groups // 2):
        a = wide_ref[2 * g, :, pair:].astype(f32)
        b = wide_ref[2 * g + 1, :, pair:].astype(f32)
        lane = lax.broadcasted_iota(jnp.int32, a.shape, 1)
        at = slice(g * pair, (g + 1) * pair)
        k = jnp.where(lane < HEAD_DIM, a, pltpu.roll(b, HEAD_DIM, 1))
        v = jnp.where(lane < HEAD_DIM, pltpu.roll(a, HEAD_DIM, 1), b)
        dk_ref[:, at] = k
        dv_ref[:, at] = v
        total += k * wk_ref[:, at].astype(f32) + v * wv_ref[:, at].astype(f32)
    dg_ref[...] = jnp.sum(jnp.transpose(total), axis=0, keepdims=True) / gain_ref[...]


def weights_out_call(wide, wq, wk, wv, gain):
    chunks, groups, rows, width = wide.shape
    features = chunks * rows
    by_rows = lambda w: pl.BlockSpec((rows, w.shape[1]), lambda c: (c, 0))
    return pl.pallas_call(
        weights_out_kernel,
        grid=(chunks,),
        in_specs=[
            pl.BlockSpec((None, groups, rows, width), lambda c: (c, 0, 0, 0)),
            by_rows(wq),
            by_rows(wk),
            by_rows(wv),
            pl.BlockSpec((1, rows), lambda c: (0, c)),
        ],
        out_specs=[
            by_rows(wq),
            by_rows(wk),
            by_rows(wv),
            pl.BlockSpec((1, rows), lambda c: (0, c)),
        ],
        out_shape=[
            jax.ShapeDtypeStruct(wq.shape, f32),
            jax.ShapeDtypeStruct(wk.shape, f32),
            jax.ShapeDtypeStruct(wv.shape, f32),
            jax.ShapeDtypeStruct((1, features), f32),
        ],
        compiler_params=params(32, "arbitrary"),
        cost_estimate=cost(2 * wq.size, 1.6e7),
        name="attention_weights_out",
    )(wide, wq, wk, wv, gain)


def last_kernel(d_ref, wq_ref, wk_ref, wv_ref, x_ref, gain_ref, dmid_ref, out_ref):
    groups, rows, width = d_ref.shape
    pair = width // 2
    dq = jnp.concatenate([d_ref[g, :, :pair] for g in range(groups)], axis=1)
    grad = dot_nt(dq, wq_ref[...])
    keys, vals = [], []
    for at in range(groups // 2):
        a = d_ref[2 * at, :, pair:].astype(f32)
        b = d_ref[2 * at + 1, :, pair:].astype(f32)
        lane = lax.broadcasted_iota(jnp.int32, a.shape, 1)
        keys.append(jnp.where(lane < HEAD_DIM, a, pltpu.roll(b, HEAD_DIM, 1)).astype(bf16))
        vals.append(jnp.where(lane < HEAD_DIM, pltpu.roll(a, HEAD_DIM, 1), b).astype(bf16))
    grad = grad + dot_nt(jnp.concatenate(keys, axis=1), wk_ref[...])
    grad = grad + dot_nt(jnp.concatenate(vals, axis=1), wv_ref[...])
    x = x_ref[...].astype(f32)
    scale = lax.rsqrt(jnp.mean(x * x, axis=-1, keepdims=True) + norm_eps)
    unit = x * scale
    w = gain_ref[...] * grad
    out_ref[...] = dmid_ref[...] + scale * (w - unit * jnp.mean(w * unit, axis=-1, keepdims=True))


def last_call(d, wq, wk, wv, x, gain, dmid):
    rows, features = x.shape
    return pl.pallas_call(
        last_kernel,
        out_shape=jax.ShapeDtypeStruct((rows, features), f32),
        compiler_params=params(40),
        cost_estimate=cost(4 * rows * features * features, 8e6),
        name="input_gradient",
    )(d, wq, wk, wv, x, gain, dmid)


def swap(values, axis, bit):
    return lax.ppermute(values, axis, [(i, i ^ bit) for i in range(lax.axis_size(axis))])


def half_sum(values, axis, bit):
    half = values.shape[0] // 2
    upper = ((lax.axis_index(axis) & bit) > 0).astype(jnp.int32)
    came = swap(lax.dynamic_slice_in_dim(values, (1 - upper) * half, half), axis, bit)
    mine = lax.dynamic_slice_in_dim(values, upper * half, half)
    return (mine.astype(f32) + came.astype(f32)).astype(bf16)


def relative_sum(kept, sent, axis, bits):
    while True:
        kept = (kept.astype(f32) + swap(sent, axis, bits[0]).astype(f32)).astype(bf16)
        bits = bits[1:]
        if not bits:
            return kept
        half = kept.shape[0] // 2
        kept, sent = kept[:half], kept[half:]


def join_parts(stream, axis, bits):
    shape = stream.shape
    for bit in bits[::-1]:
        stream = jnp.stack([stream, swap(stream, axis, bit)])
    return stream.reshape(-1, *shape)


def body(
    layer_input,
    first_gain,
    query_weight,
    key_weight,
    value_weight,
    output_weight,
    second_gain,
    gate_weight,
    up_weight,
    down_weight,
    expert_ids,
    gate_values,
    positions,
    cotangent,
):
    micro, _, per_device, features = layer_input.shape
    devices = lax.axis_size("seq")
    replicas = lax.axis_size("dp")
    seq_place = lax.axis_index("seq")
    rows = micro * per_device
    local_experts = gate_weight.shape[0]
    groups = key_weight.shape[1] // HEAD_DIM
    pair = query_weight.shape[1] // groups
    copies = devices // groups

    dp_bits = [1 << i for i in range(replicas.bit_length() - 1)]

    def spread(blocks):
        if copies > 1:
            blocks = jnp.repeat(blocks, copies, axis=0)
        return lax.all_to_all(blocks, "seq", 0, 0, tiled=True)

    def unspread(blocks):
        return lax.all_to_all(blocks, "seq", 0, 0, tiled=True)[::copies]

    x = layer_input.reshape(rows, features)
    cot = cotangent.reshape(rows, features)
    gain_one = first_gain.reshape(1, features)
    gain_two = second_gain.reshape(1, features)
    pos_all = lax.all_to_all(
        jnp.broadcast_to(positions.reshape(1, rows), (devices, rows)), "seq", 0, 0, tiled=True
    )
    x_all = lax.all_gather(x, "seq", axis=0)
    cos_all, sin_all = rope_tables(pos_all.reshape(-1), pair)
    mine = seq_place * local_experts + jnp.arange(local_experts, dtype=jnp.int32)
    ids = expert_ids[:, 0]
    gates = gate_values[:, 0].astype(f32)
    routed = jnp.sum(
        jnp.where(ids[..., None] == mine, gates[..., None], 0.0), axis=2
    )
    routed = routed.reshape(micro, devices, per_device, local_experts)
    routed = jnp.transpose(routed, (1, 0, 2, 3)).reshape(devices * rows, local_experts)
    group = seq_place // copies
    w_own = jnp.concatenate(
        [
            lax.dynamic_slice_in_dim(query_weight, group * pair, pair, axis=1),
            lax.dynamic_slice_in_dim(key_weight, group * HEAD_DIM, HEAD_DIM, axis=1),
            lax.dynamic_slice_in_dim(value_weight, group * HEAD_DIM, HEAD_DIM, axis=1),
        ],
        axis=1,
    )
    cos_all, sin_all, routed, w_own = lax.optimization_barrier((cos_all, sin_all, routed, w_own))
    x_all, cot_then, cos_all, sin_all, routed, w_own = lax.optimization_barrier(
        (x_all, cot, cos_all, sin_all, routed, w_own)
    )
    cot_all = lax.all_gather(cot_then, "seq", axis=0)

    qkv, first_all = qkv_call(x_all, gain_one, cos_all, sin_all, w_own)
    qkv = qkv.reshape(devices, micro, per_device, 2 * pair)
    mix, log_total = attend_call(qkv)
    mix = unspread(mix.reshape(devices, rows, pair))
    mixed, middle, second_low = post_call(mix, output_weight, x, gain_two)

    chips = devices // 2
    chip, core = seq_place // 2, seq_place % 2
    onward = [(i, (i + 2) % devices) for i in range(devices)]
    dp_place = lax.axis_index("dp")
    first_bit = dp_place & 1
    last_bit = dp_place >> (len(dp_bits) - 1)
    held, kept, running, places = second_low, (), None, []
    for hop in range(chips):
        following = lax.ppermute(held, "seq", onward) if hop < chips - 1 else None
        other = swap(held, "seq", 1)
        source = 2 * ((chip - hop) % chips)
        place = jnp.stack([source + core, source + 1 - core, 1 - first_bit, 1 - last_bit])
        place = place.astype(jnp.int32)
        places.append(place[:2])
        dx, *kept = expert_call(
            hop, place, held, other, cot_all, routed, gate_weight, up_weight, down_weight, kept
        )
        if following is not None:
            following, dx = lax.optimization_barrier((following, dx))
        part = dx[0].astype(f32) + swap(dx[1], "seq", 1).astype(f32)
        if hop == 0:
            own_part = part
        else:
            if running is not None:
                part = part + running.astype(f32)
            part = part.astype(bf16)
            if following is not None:
                part, following = lax.optimization_barrier((part, following))
            else:
                part, kept = lax.optimization_barrier((part, kept))
            running = lax.ppermute(part, "seq", onward)
        held = following
    second_grad = (own_part + running.astype(f32)).astype(bf16)
    tokens, hidden_a, hidden_b, gate_low, up_low, slot_a, slot_b = kept

    def weight_parts(at, tokens, hidden_a, hidden_b, gate_low, up_low, slot_a, slot_b):
        pairs = (
            (tokens, gate_low[at]),
            (tokens, up_low[at]),
            (hidden_a[at], slot_a[at]),
            (hidden_b[at], slot_b[at]),
        )
        return [
            lax.dot_general(a, b, TN, preferred_element_type=f32).astype(bf16) for a, b in pairs
        ]

    leaving = weight_parts(0, *kept)
    part_bits = (dp_bits[0], dp_bits[-1], dp_bits[0], dp_bits[-1])
    stream_bits = (dp_bits, dp_bits[::-1])
    came = [swap(values, "dp", bit) for values, bit in zip(leaving, part_bits)]
    leaving, second_grad = lax.optimization_barrier((leaving, second_grad))

    mg_send, proj, middle_grad, gain_two_part = turn_call(
        second_grad, middle, gain_two, cot, output_weight, groups
    )
    mg = spread(mg_send)
    kept, _ = lax.optimization_barrier((kept, mg_send))
    mixed, proj, came[2:] = lax.optimization_barrier((mixed, proj, came[2:]))
    dense = output_weight_call(mixed, proj, gain_two_part, devices)
    dense_own = dense
    staying = weight_parts(1, *kept)
    turned = sum(((dp_place >> i) & 1) << (len(dp_bits) - 1 - i) for i in range(len(dp_bits)))
    part_at = jnp.stack([turned, dp_place]).astype(jnp.int32)
    low_at = jnp.bitwise_and(part_at, replicas // 2 - 1)
    keep_a, send_a, keep_b, send_b = part_sum_call(low_at, replicas // 2, came, staying)
    mg, keep_a, send_a, keep_b, send_b = lax.optimization_barrier(
        (mg, keep_a, send_a, keep_b, send_b)
    )
    streams = [
        relative_sum(keep_a, send_a, "dp", stream_bits[0][1:]),
        relative_sum(keep_b, send_b, "dp", stream_bits[1][1:]),
    ]
    dense = dense_own
    dense = lax.psum_scatter(dense, "seq", scatter_dimension=0)
    table_shape = (devices, micro, per_device, pair)
    dqkv = attend_back_call(
        qkv,
        mg.reshape(devices, micro, per_device, pair),
        log_total,
        cos_all.reshape(table_shape),
        sin_all.reshape(table_shape),
    )
    dqkv, streams = lax.optimization_barrier((dqkv, streams))
    near = [
        [v[0], swap(v[0], "dp", bits[-1])] for v, bits in zip(streams, stream_bits)
    ]
    back = unspread(dqkv.reshape(devices, rows, 2 * pair))
    d_all = dqkv.reshape(devices * rows, 2 * pair)
    first_tokens = first_all.reshape(devices * rows, features)
    part = lax.dot_general(first_tokens, d_all, TN, preferred_element_type=f32)
    dense = dense.reshape(dense.shape[-2], features)
    each = output_weight.shape[0] // devices
    if copies == 1:
        width = 2 * pair
        kept_pieces, sent_pieces = joint_call(part_at, part, dense, replicas)
        first = [
            kept_pieces[at].astype(f32) + swap(sent_pieces[at], "dp", bits[0]).astype(f32)
            for at, bits in enumerate(stream_bits)
        ]
        kept, sent_pieces = lax.optimization_barrier((kept, sent_pieces))
        moe_place = jnp.concatenate(places + [(1 - first_bit).astype(jnp.int32).reshape(1)])
        moe_all = moe_call(moe_place, kept[1], routed, down_weight, devices)
        first, near, moe_all = lax.optimization_barrier(
            ([v.astype(bf16) for v in first], near, moe_all)
        )
        own = [
            relative_sum(v[: replicas // 4], v[replicas // 4 :], "dp", bits[1:])
            for v, bits in zip(first, stream_bits)
        ]
        own = jnp.concatenate(own, axis=0)
        own, here = lax.optimization_barrier((own, [v[0] for v in near]))
        far = [[swap(v, "dp", bits[-2])] for v, bits in zip(here, stream_bits)]
        backward = [(i, (i - 2) % devices) for i in range(devices)]
        round_ring = {0: own}
        for k in range(1, chips // 2 + 1):
            round_ring[k] = lax.ppermute(round_ring[k - 1], "seq", onward)
            if chips - k > k:
                round_ring[chips - k] = lax.ppermute(
                    round_ring[(chips - k + 1) % chips], "seq", backward
                )
        held = jnp.stack([round_ring[k] for k in range(chips)])
        held, moe_all, back, far = lax.optimization_barrier((held, moe_all, back, far))
        moe = lax.psum_scatter(moe_all, "seq", scatter_dimension=0)
        layer_output = (middle + residual_scale * moe.astype(f32)).astype(bf16)
    else:
        far = [[swap(v[0], "dp", bits[-2])] for v, bits in zip(streams, stream_bits)]
    expert_pieces = []
    for (here, first), (second,), bits in zip(near, far, stream_bits):
        pieces = [here, first, second, swap(first, "dp", bits[-2])]
        for bit in bits[:-2][::-1]:
            pieces = pieces + [swap(p, "dp", bit) for p in pieces]
        expert_pieces.append(pieces)
    input_grad = last_call(
        back, query_weight, key_weight, value_weight, x, gain_one, middle_grad
    )
    if copies == 1:
        full = [join_parts(held[:, at], "dp", b) for at, b in enumerate(stream_bits)]
        full, input_grad = lax.optimization_barrier((jnp.stack(full), input_grad))
        other = swap(full, "seq", 1)
        where_at = jnp.stack([turned, dp_place, chip, core]).astype(jnp.int32)
        (
            query_weight_grad,
            key_weight_grad,
            value_weight_grad,
            first_gain_grad,
            output_weight_grad,
            second_gain_grad,
        ) = dense_out_call(
            where_at, full, other, query_weight, key_weight, value_weight, gain_one, output_weight.shape
        )
        query_weight_grad, expert_pieces = lax.optimization_barrier(
            (query_weight_grad, expert_pieces)
        )
    else:
        for bit in dp_bits:
            dense = (dense.astype(f32) + swap(dense, "dp", bit).astype(f32)).astype(bf16)
        dense = lax.all_gather(dense, "seq", axis=0).astype(f32)
        output_weight_grad = dense[:, :each].reshape(output_weight.shape)
        moe_place = jnp.concatenate(places + [(1 - first_bit).astype(jnp.int32).reshape(1)])
        moe_all = moe_call(moe_place, kept[1], routed, down_weight, devices)
        moe = lax.psum_scatter(moe_all, "seq", scatter_dimension=0)
        layer_output = (middle + residual_scale * moe.astype(f32)).astype(bf16)
        second_gain_grad = dense[0, each]
        part = part.astype(bf16)
        for bit in dp_bits[::-1]:
            part = half_sum(part, "dp", bit)
        wide = lax.all_gather(part, ("dp", "seq"), axis=0)
        wide = wide.reshape(replicas, devices, features // replicas, 2 * pair)[:, ::copies]
        query_weight_grad, key_weight_grad, value_weight_grad, first_gain_grad = weights_out_call(
            wide, query_weight, key_weight, value_weight, gain_one
        )
    second_gain_grad = second_gain_grad.reshape(features)
    gate_sum, up_sum, down_sum = expert_out_call(
        part_at, *expert_pieces, gate_weight.shape, down_weight.shape
    )
    return (
        layer_output.reshape(layer_input.shape),
        input_grad.reshape(layer_input.shape),
        first_gain_grad.reshape(features),
        query_weight_grad,
        key_weight_grad,
        value_weight_grad,
        output_weight_grad,
        second_gain_grad,
        gate_sum,
        up_sum,
        down_sum,
    )


def solution(mesh):
    return jax.shard_map(
        body,
        mesh=mesh,
        in_specs=(
            P(None, "dp", "seq", None),
            P(),
            P(),
            P(),
            P(),
            P(),
            P(),
            P("seq", None, None),
            P("seq", None, None),
            P("seq", None, None),
            P(None, "dp", None, None),
            P(None, "dp", None, None),
            P(None, "dp", "seq"),
            P(None, "dp", "seq", None),
        ),
        out_specs=(
            P(None, "dp", "seq", None),
            P(None, "dp", "seq", None),
            P(),
            P(),
            P(),
            P(),
            P(),
            P(),
            P("seq", None, None),
            P("seq", None, None),
            P("seq", None, None),
        ),
        check_vma=False,
    )
```

```python
from functools import partial

import jax
import jax.numpy as jnp
from jax import lax
from jax.experimental import pallas as pl
from jax.experimental.pallas import tpu as pltpu
from jax.sharding import PartitionSpec as P

HEAD_DIM = 64

rope_theta = 10000.0
attention_scale = 0.015625
residual_scale = 0.22
norm_eps = 1e-06
masked_score = -1e30

f32 = jnp.float32
bf16 = jnp.bfloat16
NT = (((1,), (1,)), ((), ()))
TN = (((0,), (0,)), ((), ()))


def dot(a, b):
    return jnp.dot(a, b, preferred_element_type=f32)


def dot_nt(a, b):
    return lax.dot_general(a, b, NT, preferred_element_type=f32)


def params(mib, *semantics):
    return pltpu.CompilerParams(
        vmem_limit_bytes=mib * 1024 * 1024, dimension_semantics=semantics or None
    )


def cost(flops, nbytes, trans=0):
    return pl.CostEstimate(
        flops=int(flops / 8), bytes_accessed=int(nbytes / 8), transcendentals=int(trans / 8)
    )


def whole(shape):
    return pl.BlockSpec(shape, lambda *_: (0,) * len(shape))


def rope_tables(positions, width):
    half = HEAD_DIM // 2
    exponent = jnp.arange(half, dtype=f32) * (-2.0 / HEAD_DIM)
    angles = positions.astype(f32)[:, None] * (rope_theta**exponent)[None, :]
    cosine, sine = jnp.cos(angles), jnp.sin(angles)
    copies = width // HEAD_DIM
    cos_row = jnp.concatenate([cosine, cosine] * copies, axis=1)
    sin_row = jnp.concatenate([-sine, sine] * copies, axis=1)
    return cos_row, sin_row


def partner(values):
    width = values.shape[1]
    half = HEAD_DIM // 2
    lane = lax.broadcasted_iota(jnp.int32, values.shape, 1)
    ahead = pltpu.roll(values, width - half, 1)
    behind = pltpu.roll(values, half, 1)
    return jnp.where(lane % HEAD_DIM < half, ahead, behind)


def qkv_kernel(x_ref, gain_ref, cos_ref, sin_ref, w_ref, qkv_ref, low_ref):
    pair = 2 * HEAD_DIM
    x = x_ref[0].astype(f32)
    scale = lax.rsqrt(jnp.mean(x * x, axis=-1, keepdims=True) + norm_eps)
    low = (x * scale * gain_ref[...]).astype(bf16)
    low_ref[0] = low
    cosine, sine = cos_ref[...], sin_ref[...]
    made = dot(low, w_ref[...])
    q, kv = made[:, :pair], made[:, pair:]
    q = (q * cosine + partner(q) * sine) * attention_scale
    qkv_ref[0, :, :pair] = q.astype(bf16)
    lane = lax.broadcasted_iota(jnp.int32, kv.shape, 1)
    turned = kv * cosine + partner(kv) * sine
    qkv_ref[0, :, pair:] = jnp.where(lane < HEAD_DIM, turned, kv).astype(bf16)


def qkv_call(x_all, gain, cos_all, sin_all, w_own):
    blocks, rows, features = x_all.shape
    pair = 2 * HEAD_DIM
    return pl.pallas_call(
        qkv_kernel,
        grid=(blocks,),
        in_specs=[
            pl.BlockSpec((1, rows, features), lambda s: (s, 0, 0)),
            whole((1, features)),
            pl.BlockSpec((rows, pair), lambda s: (s, 0)),
            pl.BlockSpec((rows, pair), lambda s: (s, 0)),
            whole(w_own.shape),
        ],
        out_specs=[
            pl.BlockSpec((1, rows, 2 * pair), lambda s: (s, 0, 0)),
            pl.BlockSpec((1, rows, features), lambda s: (s, 0, 0)),
        ],
        out_shape=[
            jax.ShapeDtypeStruct((blocks, rows, 2 * pair), bf16),
            jax.ShapeDtypeStruct((blocks, rows, features), bf16),
        ],
        compiler_params=params(58, "arbitrary"),
        cost_estimate=cost(4 * blocks * rows * features * pair, 14e6),
        name="norm_qkv_rope",
    )(x_all, gain, cos_all, sin_all, w_own)


def split_heads(block, first):
    wide = block.astype(f32)
    lane = lax.broadcasted_iota(jnp.int32, wide.shape, 1)
    turned = pltpu.roll(wide, HEAD_DIM, 1)
    if first:
        parts = [jnp.where(lane < HEAD_DIM, wide, 0.0), jnp.where(lane < HEAD_DIM, turned, 0.0)]
    else:
        parts = [jnp.where(lane >= HEAD_DIM, turned, 0.0), jnp.where(lane >= HEAD_DIM, wide, 0.0)]
    return jnp.concatenate(parts, axis=0).astype(bf16)


def join_heads(turned):
    rows = turned.shape[1] // 2
    return jnp.transpose(jnp.concatenate([turned[:, :rows], turned[:, rows:]], axis=0))


def scores_of(kv, q2, rows):
    scores = dot_nt(kv, q2)
    count = scores.shape[0]
    own = scores[count - rows :]
    key_at = lax.broadcasted_iota(jnp.int32, own.shape, 0)
    query_at = lax.broadcasted_iota(jnp.int32, own.shape, 1) % rows
    own = jnp.where(key_at <= query_at, own, masked_score)
    if count == rows:
        return own
    return jnp.concatenate([scores[: count - rows], own], axis=0)


def attend_kernel(qkv_ref, out_ref, log_ref):
    blocks, _, rows, width = qkv_ref.shape
    pair = width // 2
    kv = qkv_ref[:, 0, :, pair:].reshape(blocks * rows, pair)
    kv_t = jnp.transpose(kv)
    for at in range(blocks):
        count = (at + 1) * rows
        q2 = split_heads(qkv_ref[at, 0, :, :pair], True)
        scores = scores_of(kv[:count], q2, rows)
        top = jnp.max(scores, axis=0, keepdims=True)
        weights = jnp.exp(scores - top)
        total = jnp.sum(weights, axis=0, keepdims=True)
        out_t = dot(kv_t[:, :count], weights.astype(bf16))
        out_ref[at, 0] = join_heads(out_t[HEAD_DIM:] / total).astype(bf16)
        log_ref[at, 0] = top + jnp.log(total)


def attend_call(qkv):
    blocks, micro, rows, width = qkv.shape
    pair = width // 2
    length = blocks * rows
    return pl.pallas_call(
        attend_kernel,
        grid=(micro,),
        in_specs=[pl.BlockSpec((blocks, 1, rows, width), lambda m: (0, m, 0, 0))],
        out_specs=[
            pl.BlockSpec((blocks, 1, rows, pair), lambda m: (0, m, 0, 0)),
            pl.BlockSpec((blocks, 1, 1, 2 * rows), lambda m: (0, m, 0, 0)),
        ],
        out_shape=[
            jax.ShapeDtypeStruct((blocks, micro, rows, pair), bf16),
            jax.ShapeDtypeStruct((blocks, micro, 1, 2 * rows), f32),
        ],
        compiler_params=params(48, "arbitrary"),
        cost_estimate=cost(
            micro * length * length * 512, 3 * qkv.size, micro * length * length
        ),
        name="attention_forward",
    )(qkv)


def attend_back_kernel(qkv_ref, grad_ref, log_ref, cos_ref, sin_ref, out_ref, dkv_ref):
    blocks, _, rows, width = qkv_ref.shape
    pair = width // 2
    kv = qkv_ref[:, 0, :, pair:].reshape(blocks * rows, pair)
    kv_t = jnp.transpose(kv)
    dkv_ref[...] = jnp.zeros_like(dkv_ref)
    for at in range(blocks):
        count = (at + 1) * rows
        q2 = split_heads(qkv_ref[at, 0, :, :pair], True)
        g2 = split_heads(grad_ref[at, 0], False)
        scores = scores_of(kv[:count], q2, rows)
        prob = jnp.exp(scores - log_ref[at, 0])
        prob_grad = dot_nt(kv[:count], g2)
        delta = jnp.sum(prob * prob_grad, axis=0, keepdims=True)
        score_grad = (prob * (prob_grad - delta)).astype(bf16)
        dkv_ref[:count] += dot(score_grad, q2) + dot(prob.astype(bf16), g2)
        dq_t = dot(kv_t[:, :count], score_grad)
        dq = join_heads(dq_t[:HEAD_DIM] * attention_scale)
        dq = dq * cos_ref[at, 0] - partner(dq) * sin_ref[at, 0]
        out_ref[at, 0, :, :pair] = dq.astype(bf16)
    for at in range(blocks):
        dkv = dkv_ref[at * rows : (at + 1) * rows]
        lane = lax.broadcasted_iota(jnp.int32, dkv.shape, 1)
        turned = dkv * cos_ref[at, 0] - partner(dkv) * sin_ref[at, 0]
        out_ref[at, 0, :, pair:] = jnp.where(lane < HEAD_DIM, turned, dkv).astype(bf16)


def attend_back_call(qkv, grads, log_total, cos_all, sin_all):
    blocks, micro, rows, width = qkv.shape
    pair = width // 2
    length = blocks * rows
    spec = lambda lanes: pl.BlockSpec((blocks, 1, rows, lanes), lambda m: (0, m, 0, 0))
    return pl.pallas_call(
        attend_back_kernel,
        grid=(micro,),
        in_specs=[
            spec(width),
            spec(pair),
            pl.BlockSpec((blocks, 1, 1, 2 * rows), lambda m: (0, m, 0, 0)),
            spec(pair),
            spec(pair),
        ],
        out_specs=spec(width),
        out_shape=jax.ShapeDtypeStruct(qkv.shape, bf16),
        scratch_shapes=[pltpu.VMEM((length, pair), f32)],
        compiler_params=params(56, "arbitrary"),
        cost_estimate=cost(
            micro * length * length * 1280, 10 * qkv.size, micro * length * length
        ),
        name="attention_backward",
    )(qkv, grads, log_total, cos_all, sin_all)


def post_kernel(mix_ref, wo_ref, x_ref, gain_ref, mixed_ref, middle_ref, low_ref):
    mixed = jnp.concatenate([mix_ref[g] for g in range(mix_ref.shape[0])], axis=1)
    mixed_ref[...] = mixed
    middle = x_ref[...].astype(f32) + residual_scale * dot(mixed, wo_ref[...])
    middle_ref[...] = middle
    scale = lax.rsqrt(jnp.mean(middle * middle, axis=-1, keepdims=True) + norm_eps)
    low_ref[...] = (middle * scale * gain_ref[...]).astype(bf16)


def post_call(mix, wo, x, gain):
    rows, features = x.shape
    return pl.pallas_call(
        post_kernel,
        out_shape=[
            jax.ShapeDtypeStruct((rows, wo.shape[0]), bf16),
            jax.ShapeDtypeStruct((rows, features), f32),
            jax.ShapeDtypeStruct((rows, features), bf16),
        ],
        compiler_params=params(32),
        cost_estimate=cost(2 * rows * wo.size, 5e6),
        name="project_norm",
    )(mix, wo, x, gain)


def expert_kernel(place_ref, a_ref, b_ref, cot_ref, w_ref, wg_ref, wu_ref, wd_ref, *refs):
    dx_ref, x_ref, ha_ref, hb_ref, dg_ref, du_ref, sa_ref, sb_ref = refs[-8:]
    step = pl.program_id(0)
    first, second = place_ref[2], place_ref[3]
    half = sa_ref.shape[2]

    @pl.when(step == 0)
    def _():
        x_ref[...] = a_ref[...]

    @pl.when(step == 1)
    def _():
        x_ref[...] = b_ref[...]

    x = x_ref[...]
    cot = cot_ref[0].astype(f32)
    weight = residual_scale * w_ref[...]
    total = None
    for e in range(wg_ref.shape[0]):
        gate = dot(x, wg_ref[e])
        up = dot(x, wu_ref[e])
        slot_grad = (weight[:, e : e + 1] * cot).astype(bf16)
        to_a, to_b = jnp.bitwise_xor(first, e), jnp.bitwise_xor(second, e)
        sa_ref[to_a] = slot_grad[:, :half]
        sb_ref[to_b] = slot_grad[:, half:]
        hidden_grad = dot_nt(slot_grad, wd_ref[e])
        sig = 0.5 * jnp.tanh(0.5 * gate) + 0.5
        silu = gate * sig
        hidden = (silu * up).astype(bf16)
        ha_ref[to_a] = hidden
        hb_ref[to_b] = hidden
        gate_grad = (hidden_grad * up * (sig + silu * (1.0 - sig))).astype(bf16)
        up_grad = (hidden_grad * silu).astype(bf16)
        dg_ref[to_a] = gate_grad
        du_ref[to_b] = up_grad
        term = dot_nt(gate_grad, wg_ref[e]) + dot_nt(up_grad, wu_ref[e])
        total = term if total is None else total + term
    dx_ref[0] = total.astype(bf16)


def expert_call(at, place, own, other, cot_all, weight, wg, wu, wd, kept):
    blocks, rows, features = cot_all.shape
    count, _, hidden = wg.shape
    tokens = blocks * rows
    inner = jax.ShapeDtypeStruct((count, tokens, hidden), bf16)
    outer = jax.ShapeDtypeStruct((count, tokens, features // 2), bf16)
    inner_spec = pl.BlockSpec((count, rows, hidden), lambda s, place: (0, 2 * at + s, 0))
    outer_spec = pl.BlockSpec((count, rows, features // 2), lambda s, place: (0, 2 * at + s, 0))
    fixed = lambda shape: pl.BlockSpec(shape, lambda s, place: (0,) * len(shape))
    any_spec = pl.BlockSpec(memory_space=pl.ANY)
    first = 8
    return pl.pallas_call(
        expert_kernel,
        grid_spec=pltpu.PrefetchScalarGridSpec(
            num_scalar_prefetch=1,
            grid=(2,),
            in_specs=[
                fixed((rows, features)),
                fixed((rows, features)),
                pl.BlockSpec((1, rows, features), lambda s, place: (place[s], 0, 0)),
                pl.BlockSpec((rows, count), lambda s, place: (place[s], 0)),
                fixed(wg.shape),
                fixed(wu.shape),
                fixed(wd.shape),
            ]
            + [any_spec] * len(kept),
            out_specs=[
                pl.BlockSpec((1, rows, features), lambda s, place: (s, 0, 0)),
                pl.BlockSpec((rows, features), lambda s, place: (2 * at + s, 0)),
            ]
            + [inner_spec] * 4
            + [outer_spec] * 2,
        ),
        out_shape=[
            jax.ShapeDtypeStruct((2, rows, features), bf16),
            jax.ShapeDtypeStruct((tokens, features), bf16),
            inner,
            inner,
            inner,
            inner,
            outer,
            outer,
        ],
        input_output_aliases={first + i: 1 + i for i in range(len(kept))},
        compiler_params=params(48, "arbitrary"),
        cost_estimate=cost(20 * rows * wg.size, 2e7, 2 * rows * hidden * count),
        name="experts",
    )(place, own, other, cot_all, weight, wg, wu, wd, *kept)


def part_sum_kernel(at_ref, *refs):
    inputs, outs = refs[:16], refs[16:]
    at = 0
    for out in outs:
        gate_came, gate_here, down_came, down_here = inputs[at : at + 4]
        rows = gate_came.shape[0]
        out[0, :rows] = (gate_came[...].astype(f32) + gate_here[...].astype(f32)).astype(bf16)
        out[0, rows:] = (down_came[...].astype(f32) + down_here[...].astype(f32)).astype(bf16)
        at += 4


def part_sum_call(at, per, came, here):
    gate_rows, down_rows = came[0].shape[0] // per, came[2].shape[0] // per
    width = came[0].shape[1]
    steps = per // 2
    specs, args, out_specs, out_shapes = [], [], [], []
    for stream in range(2):
        for sent in range(2):
            for which, rows in ((stream, gate_rows), (stream + 2, down_rows)):
                spec = pl.BlockSpec(
                    (rows, width),
                    lambda s, at, sent=sent, stream=stream: (
                        jnp.bitwise_xor(s + sent * steps, at[stream]),
                        0,
                    ),
                )
                specs += [spec, spec]
                args += [came[which], here[which]]
            out_specs.append(
                pl.BlockSpec((1, gate_rows + down_rows, width), lambda s, at: (s, 0, 0))
            )
            out_shapes.append(
                jax.ShapeDtypeStruct((steps, gate_rows + down_rows, width), bf16)
            )
    return pl.pallas_call(
        part_sum_kernel,
        grid_spec=pltpu.PrefetchScalarGridSpec(
            num_scalar_prefetch=1, grid=(steps,), in_specs=specs, out_specs=out_specs
        ),
        out_shape=out_shapes,
        compiler_params=params(60, "arbitrary"),
        cost_estimate=cost(0, 9e6),
        name="expert_part_sum",
    )(at, *args)


def joint_kernel(at_ref, *refs):
    for (part_ref, wo_ref, gain_ref), out_ref in ((refs[:3], refs[6]), (refs[3:6], refs[7])):
        rows = part_ref.shape[0]
        upto = rows + wo_ref.shape[0]
        out_ref[0, 0, :rows] = part_ref[...].astype(bf16)
        out_ref[0, 0, rows:upto] = wo_ref[...]
        out_ref[0, 0, upto:] = gain_ref[...]


def joint_call(at, part, dense, parts):
    features, width = part.shape
    pieces = 2 * parts
    rows = features // pieces
    block_cols = dense.shape[1] // width
    per_block = pieces // block_cols
    extra = 16
    wo_rows = (dense.shape[0] - extra) // per_block
    last = dense.shape[0] // extra - 1
    steps = parts // 2

    def piece(sent):
        return lambda s, p, at: s * parts + jnp.bitwise_xor(p + sent * steps, at[s])

    specs = []
    for sent in range(2):
        at_piece = piece(sent)
        specs.append(
            pl.BlockSpec((rows, width), lambda s, p, at, f=at_piece: (f(s, p, at), 0))
        )
        specs.append(
            pl.BlockSpec(
                (wo_rows, width),
                lambda s, p, at, f=at_piece: (
                    lax.rem(f(s, p, at), per_block),
                    lax.div(f(s, p, at), per_block),
                ),
            )
        )
        specs.append(
            pl.BlockSpec(
                (extra, width), lambda s, p, at, f=at_piece: (last, lax.div(f(s, p, at), per_block))
            )
        )
    out_spec = pl.BlockSpec((1, 1, rows + wo_rows + extra, width), lambda s, p, at: (s, p, 0, 0))
    out_shape = jax.ShapeDtypeStruct((2, steps, rows + wo_rows + extra, width), bf16)
    return pl.pallas_call(
        joint_kernel,
        grid_spec=pltpu.PrefetchScalarGridSpec(
            num_scalar_prefetch=1, grid=(2, steps), in_specs=specs, out_specs=[out_spec] * 2
        ),
        out_shape=[out_shape] * 2,
        compiler_params=params(32, "arbitrary", "arbitrary"),
        cost_estimate=cost(0, 2e6),
        name="dense_pieces",
    )(at, part, dense, dense, part, dense, dense)


def expert_out_kernel(at_ref, *refs):
    pieces, (gate_ref, up_ref, down_ref) = refs[:-3], refs[-3:]
    parts = len(pieces) // 2
    step = pl.program_id(0)
    rows = gate_ref.shape[1]
    half = down_ref.shape[2] // 2
    for which in range(parts):

        @pl.when(jnp.bitwise_xor(step, at_ref[0]) == which)
        def _():
            a_ref = pieces[which]
            gate_ref[0] = a_ref[:rows].astype(f32)
            down_ref[0, :, :half] = a_ref[rows:].astype(f32)

        @pl.when(jnp.bitwise_xor(step, at_ref[1]) == which)
        def _():
            b_ref = pieces[parts + which]
            up_ref[0] = b_ref[:rows].astype(f32)
            down_ref[0, :, half:] = b_ref[rows:].astype(f32)


def expert_out_call(at, a, b, gate_shape, down_shape):
    parts = len(a)
    held, width = a[0].shape
    count = gate_shape[0]
    per = parts // count
    gate_rows, down_rows = gate_shape[1] // per, down_shape[1] // per
    place = lambda r, at: (lax.div(r, per), lax.rem(r, per), 0)
    return pl.pallas_call(
        expert_out_kernel,
        grid_spec=pltpu.PrefetchScalarGridSpec(
            num_scalar_prefetch=1,
            grid=(parts,),
            in_specs=[pl.BlockSpec((held, width), lambda r, at: (0, 0))] * (2 * parts),
            out_specs=[
                pl.BlockSpec((1, gate_rows, gate_shape[2]), place),
                pl.BlockSpec((1, gate_rows, gate_shape[2]), place),
                pl.BlockSpec((1, down_rows, down_shape[2]), place),
            ],
        ),
        out_shape=[
            jax.ShapeDtypeStruct(gate_shape, f32),
            jax.ShapeDtypeStruct(gate_shape, f32),
            jax.ShapeDtypeStruct(down_shape, f32),
        ],
        compiler_params=params(40, "arbitrary"),
        cost_estimate=cost(0, 2e7),
        name="expert_weights_out",
    )(at, *a, *b)


def moe_kernel(place_ref, h_ref, w_ref, wd_ref, out_ref):
    weight = w_ref[...]
    total = None
    first = place_ref[pl.num_programs(0)]
    for e in range(wd_ref.shape[0]):
        term = weight[:, e : e + 1] * dot(h_ref[jnp.bitwise_xor(first, e)], wd_ref[e])
        total = term if total is None else total + term
    out_ref[0] = total.astype(bf16)


def moe_call(place, hidden, weight, wd, blocks):
    count, tokens, inner = hidden.shape
    features = wd.shape[2]
    rows = tokens // blocks
    return pl.pallas_call(
        moe_kernel,
        grid_spec=pltpu.PrefetchScalarGridSpec(
            num_scalar_prefetch=1,
            grid=(blocks,),
            in_specs=[
                pl.BlockSpec((count, rows, inner), lambda s, place: (0, s, 0)),
                pl.BlockSpec((rows, count), lambda s, place: (place[s], 0)),
                pl.BlockSpec(wd.shape, lambda s, place: (0, 0, 0)),
            ],
            out_specs=pl.BlockSpec((1, rows, features), lambda s, place: (place[s], 0, 0)),
        ),
        out_shape=jax.ShapeDtypeStruct((blocks, rows, features), bf16),
        compiler_params=params(60, "arbitrary"),
        cost_estimate=cost(2 * tokens * wd.size, 1.1e7),
        name="expert_outputs",
    )(place, hidden, weight, wd)


def turn_kernel(sg_ref, middle_ref, gain_ref, cot_ref, wo_ref, mg_ref, proj_ref, dmid_ref, dgain_ref):
    grad = sg_ref[...].astype(f32)
    middle = middle_ref[...]
    scale = lax.rsqrt(jnp.mean(middle * middle, axis=-1, keepdims=True) + norm_eps)
    unit = middle * scale
    dgain_ref[...] = jnp.sum(grad * unit, axis=0, keepdims=True)
    w = gain_ref[...] * grad
    dmid = cot_ref[...].astype(f32) + scale * (w - unit * jnp.mean(w * unit, axis=-1, keepdims=True))
    dmid_ref[...] = dmid
    proj = (residual_scale * dmid).astype(bf16)
    proj_ref[...] = proj
    mixed_grad = dot_nt(proj, wo_ref[...]).astype(bf16)
    groups, _, pair = mg_ref.shape
    for g in range(groups):
        mg_ref[g] = mixed_grad[:, g * pair : (g + 1) * pair]


def turn_call(sg, middle, gain, cot, wo, groups):
    rows, features = middle.shape
    pair = wo.shape[0] // groups
    return pl.pallas_call(
        turn_kernel,
        out_shape=[
            jax.ShapeDtypeStruct((groups, rows, pair), bf16),
            jax.ShapeDtypeStruct((rows, features), bf16),
            jax.ShapeDtypeStruct((rows, features), f32),
            jax.ShapeDtypeStruct((1, features), f32),
        ],
        compiler_params=params(32),
        cost_estimate=cost(2 * rows * wo.size, 6e6),
        name="norm_back_project_back",
    )(sg, middle, gain, cot, wo)


def output_weight_kernel(mixed_ref, proj_ref, dgain_ref, out_ref):
    held, each, features = out_ref.shape
    rows = mixed_ref.shape[1] // held
    part = lax.dot_general(mixed_ref[...], proj_ref[...], TN, preferred_element_type=f32)
    extra = jnp.broadcast_to(dgain_ref[...], (each - rows, features)).astype(bf16)
    for at in range(held):
        out_ref[at, :rows] = part[at * rows : (at + 1) * rows].astype(bf16)
        out_ref[at, rows:] = extra


def output_weight_call(mixed, proj, dgain, parts):
    rows, width = mixed.shape
    features = proj.shape[1]
    each = width // parts
    lanes = max(each, width // 2)
    held = lanes // each
    return pl.pallas_call(
        output_weight_kernel,
        grid=(parts // held,),
        in_specs=[
            pl.BlockSpec((rows, lanes), lambda s: (0, s)),
            whole((rows, features)),
            whole((1, features)),
        ],
        out_specs=pl.BlockSpec((held, each + 16, features), lambda s: (s, 0, 0)),
        out_shape=jax.ShapeDtypeStruct((parts, each + 16, features), bf16),
        compiler_params=params(32, "arbitrary"),
        cost_estimate=cost(2 * rows * width * features, 4e6),
        name="output_weight_part",
    )(mixed, proj, dgain)


def dense_out_kernel(at_ref, *refs):
    held, refs = refs[:-13], refs[-13:]
    wq_ref, wk_ref, wv_ref, gain_ref, dq_ref, dk_ref, dv_ref, dg_ref, wo_ref, dg2_ref = refs[:10]
    own_ref, other_ref = refs[10:12]
    parts = len(held) // 4
    stream, step = pl.program_id(0), pl.program_id(1)
    chips, _, width = own_ref.shape
    rows = dq_ref.shape[0]
    pair = width // 2
    chip, core = at_ref[2], at_ref[3]
    for which in range(2):
        for rel in range(parts):

            @pl.when((stream == which) & (jnp.bitwise_xor(step, at_ref[which]) == rel))
            def _():
                own_ref[...] = held[which * parts + rel][...]
                other_ref[...] = held[(2 + which) * parts + rel][...]

    total = jnp.zeros((rows, pair), f32)
    for k in range(chips):
        source = lax.rem(chip - k + chips, chips)
        a = jnp.where(core == 0, own_ref[k], other_ref[k]).astype(f32)
        b = jnp.where(core == 0, other_ref[k], own_ref[k]).astype(f32)
        q = jnp.concatenate([a[:rows, :pair], b[:rows, :pair]], axis=1)
        cols = pl.ds(pl.multiple_of(source * width, width), width)
        dq_ref[:, cols] = q
        made = q * wq_ref[:, cols].astype(f32)
        total += made[:, :pair] + made[:, pair:]
        a_kv, b_kv = a[:rows, pair:], b[:rows, pair:]
        lane = lax.broadcasted_iota(jnp.int32, a_kv.shape, 1)
        key = jnp.where(lane < HEAD_DIM, a_kv, pltpu.roll(b_kv, HEAD_DIM, 1))
        val = jnp.where(lane < HEAD_DIM, pltpu.roll(a_kv, HEAD_DIM, 1), b_kv)
        cols = pl.ds(pl.multiple_of(source * pair, pair), pair)
        dk_ref[:, cols] = key
        dv_ref[:, cols] = val
        total += key * wk_ref[:, cols].astype(f32) + val * wv_ref[:, cols].astype(f32)
        wo_ref[2 * source, 0] = a[rows : rows + wo_ref.shape[2]]
        wo_ref[2 * source + 1, 0] = b[rows : rows + wo_ref.shape[2]]
        if k == 0:
            dg2_ref[...] = a[rows + wo_ref.shape[2] :][:1]
    dg_ref[...] = jnp.sum(jnp.transpose(total), axis=0, keepdims=True) / gain_ref[...]


def dense_out_call(at, own, other, wq, wk, wv, gain, wo_shape):
    held = [*own[0], *own[1], *other[0], *other[1]]
    streams, parts = 2, len(own[0])
    chips, depth, width = held[0].shape
    features = wq.shape[0]
    groups = 2 * chips
    rows = features // (streams * parts)
    block_cols = wo_shape[1] // width
    per_block = streams * parts // block_cols
    wo_rows = wo_shape[0] // groups // per_block
    by_rows = lambda w: pl.BlockSpec((rows, w.shape[1]), lambda s, r, at: (s * parts + r, 0))
    gain_spec = pl.BlockSpec((1, rows), lambda s, r, at: (0, s * parts + r))
    outs = pl.pallas_call(
        dense_out_kernel,
        grid_spec=pltpu.PrefetchScalarGridSpec(
            num_scalar_prefetch=1,
            grid=(streams, parts),
            in_specs=[pl.BlockSpec(memory_space=pltpu.VMEM)] * len(held)
            + [by_rows(wq), by_rows(wk), by_rows(wv), gain_spec],
            out_specs=[
                by_rows(wq),
                by_rows(wk),
                by_rows(wv),
                gain_spec,
                pl.BlockSpec(
                    (groups, 1, wo_rows, width),
                    lambda s, r, at: (
                        0,
                        lax.rem(s * parts + r, per_block),
                        0,
                        lax.div(s * parts + r, per_block),
                    ),
                ),
                pl.BlockSpec((1, width), lambda s, r, at: (0, lax.div(s * parts + r, per_block))),
            ],
            scratch_shapes=[pltpu.VMEM((chips, depth, width), bf16)] * 2
            + [pltpu.VMEM((8, 128), f32)],
        ),
        out_shape=[
            jax.ShapeDtypeStruct(wq.shape, f32),
            jax.ShapeDtypeStruct(wk.shape, f32),
            jax.ShapeDtypeStruct(wv.shape, f32),
            jax.ShapeDtypeStruct((1, features), f32),
            jax.ShapeDtypeStruct((groups, per_block, wo_rows, wo_shape[1]), f32),
            jax.ShapeDtypeStruct((1, wo_shape[1]), f32),
        ],
        compiler_params=params(28, "arbitrary", "arbitrary"),
        cost_estimate=cost(2 * wq.size, 2.4e7),
        name="dense_weights_out",
    )(at, *held, wq, wk, wv, gain)
    return (*outs[:4], outs[4].reshape(wo_shape), outs[5])


def weights_out_kernel(wide_ref, wq_ref, wk_ref, wv_ref, gain_ref, dq_ref, dk_ref, dv_ref, dg_ref):
    groups, rows, width = wide_ref.shape
    pair = width // 2
    total = jnp.zeros((rows, pair), f32)
    for g in range(groups):
        part = wide_ref[g, :, :pair].astype(f32)
        at = slice(g * pair, (g + 1) * pair)
        dq_ref[:, at] = part
        total += part * wq_ref[:, at].astype(f32)
    for g in range(groups // 2):
        a = wide_ref[2 * g, :, pair:].astype(f32)
        b = wide_ref[2 * g + 1, :, pair:].astype(f32)
        lane = lax.broadcasted_iota(jnp.int32, a.shape, 1)
        at = slice(g * pair, (g + 1) * pair)
        k = jnp.where(lane < HEAD_DIM, a, pltpu.roll(b, HEAD_DIM, 1))
        v = jnp.where(lane < HEAD_DIM, pltpu.roll(a, HEAD_DIM, 1), b)
        dk_ref[:, at] = k
        dv_ref[:, at] = v
        total += k * wk_ref[:, at].astype(f32) + v * wv_ref[:, at].astype(f32)
    dg_ref[...] = jnp.sum(jnp.transpose(total), axis=0, keepdims=True) / gain_ref[...]


def weights_out_call(wide, wq, wk, wv, gain):
    chunks, groups, rows, width = wide.shape
    features = chunks * rows
    by_rows = lambda w: pl.BlockSpec((rows, w.shape[1]), lambda c: (c, 0))
    return pl.pallas_call(
        weights_out_kernel,
        grid=(chunks,),
        in_specs=[
            pl.BlockSpec((None, groups, rows, width), lambda c: (c, 0, 0, 0)),
            by_rows(wq),
            by_rows(wk),
            by_rows(wv),
            pl.BlockSpec((1, rows), lambda c: (0, c)),
        ],
        out_specs=[
            by_rows(wq),
            by_rows(wk),
            by_rows(wv),
            pl.BlockSpec((1, rows), lambda c: (0, c)),
        ],
        out_shape=[
            jax.ShapeDtypeStruct(wq.shape, f32),
            jax.ShapeDtypeStruct(wk.shape, f32),
            jax.ShapeDtypeStruct(wv.shape, f32),
            jax.ShapeDtypeStruct((1, features), f32),
        ],
        compiler_params=params(32, "arbitrary"),
        cost_estimate=cost(2 * wq.size, 1.6e7),
        name="attention_weights_out",
    )(wide, wq, wk, wv, gain)


def last_kernel(d_ref, wq_ref, wk_ref, wv_ref, x_ref, gain_ref, dmid_ref, out_ref):
    groups, rows, width = d_ref.shape
    pair = width // 2
    dq = jnp.concatenate([d_ref[g, :, :pair] for g in range(groups)], axis=1)
    grad = dot_nt(dq, wq_ref[...])
    keys, vals = [], []
    for at in range(groups // 2):
        a = d_ref[2 * at, :, pair:].astype(f32)
        b = d_ref[2 * at + 1, :, pair:].astype(f32)
        lane = lax.broadcasted_iota(jnp.int32, a.shape, 1)
        keys.append(jnp.where(lane < HEAD_DIM, a, pltpu.roll(b, HEAD_DIM, 1)).astype(bf16))
        vals.append(jnp.where(lane < HEAD_DIM, pltpu.roll(a, HEAD_DIM, 1), b).astype(bf16))
    grad = grad + dot_nt(jnp.concatenate(keys, axis=1), wk_ref[...])
    grad = grad + dot_nt(jnp.concatenate(vals, axis=1), wv_ref[...])
    x = x_ref[...].astype(f32)
    scale = lax.rsqrt(jnp.mean(x * x, axis=-1, keepdims=True) + norm_eps)
    unit = x * scale
    w = gain_ref[...] * grad
    out_ref[...] = dmid_ref[...] + scale * (w - unit * jnp.mean(w * unit, axis=-1, keepdims=True))


def last_call(d, wq, wk, wv, x, gain, dmid):
    rows, features = x.shape
    return pl.pallas_call(
        last_kernel,
        out_shape=jax.ShapeDtypeStruct((rows, features), f32),
        compiler_params=params(40),
        cost_estimate=cost(4 * rows * features * features, 8e6),
        name="input_gradient",
    )(d, wq, wk, wv, x, gain, dmid)


def swap(values, axis, bit):
    return lax.ppermute(values, axis, [(i, i ^ bit) for i in range(lax.axis_size(axis))])


def half_sum(values, axis, bit):
    half = values.shape[0] // 2
    upper = ((lax.axis_index(axis) & bit) > 0).astype(jnp.int32)
    came = swap(lax.dynamic_slice_in_dim(values, (1 - upper) * half, half), axis, bit)
    mine = lax.dynamic_slice_in_dim(values, upper * half, half)
    return (mine.astype(f32) + came.astype(f32)).astype(bf16)


def relative_sum(kept, sent, axis, bits):
    while True:
        kept = (kept.astype(f32) + swap(sent, axis, bits[0]).astype(f32)).astype(bf16)
        bits = bits[1:]
        if not bits:
            return kept
        half = kept.shape[0] // 2
        kept, sent = kept[:half], kept[half:]


def join_parts(stream, axis, bits):
    shape = stream.shape
    for bit in bits[::-1]:
        stream = jnp.stack([stream, swap(stream, axis, bit)])
    return stream.reshape(-1, *shape)


def body(
    layer_input,
    first_gain,
    query_weight,
    key_weight,
    value_weight,
    output_weight,
    second_gain,
    gate_weight,
    up_weight,
    down_weight,
    expert_ids,
    gate_values,
    positions,
    cotangent,
):
    micro, _, per_device, features = layer_input.shape
    devices = lax.axis_size("seq")
    replicas = lax.axis_size("dp")
    seq_place = lax.axis_index("seq")
    rows = micro * per_device
    local_experts = gate_weight.shape[0]
    groups = key_weight.shape[1] // HEAD_DIM
    pair = query_weight.shape[1] // groups
    copies = devices // groups

    dp_bits = [1 << i for i in range(replicas.bit_length() - 1)]

    def spread(blocks):
        if copies > 1:
            blocks = jnp.repeat(blocks, copies, axis=0)
        return lax.all_to_all(blocks, "seq", 0, 0, tiled=True)

    def unspread(blocks):
        return lax.all_to_all(blocks, "seq", 0, 0, tiled=True)[::copies]

    x = layer_input.reshape(rows, features)
    cot = cotangent.reshape(rows, features)
    gain_one = first_gain.reshape(1, features)
    gain_two = second_gain.reshape(1, features)
    pos_all = lax.all_to_all(
        jnp.broadcast_to(positions.reshape(1, rows), (devices, rows)), "seq", 0, 0, tiled=True
    )
    x_all = lax.all_gather(x, "seq", axis=0)
    cos_all, sin_all = rope_tables(pos_all.reshape(-1), pair)
    mine = seq_place * local_experts + jnp.arange(local_experts, dtype=jnp.int32)
    ids = expert_ids[:, 0]
    gates = gate_values[:, 0].astype(f32)
    routed = jnp.sum(
        jnp.where(ids[..., None] == mine, gates[..., None], 0.0), axis=2
    )
    routed = routed.reshape(micro, devices, per_device, local_experts)
    routed = jnp.transpose(routed, (1, 0, 2, 3)).reshape(devices * rows, local_experts)
    group = seq_place // copies
    w_own = jnp.concatenate(
        [
            lax.dynamic_slice_in_dim(query_weight, group * pair, pair, axis=1),
            lax.dynamic_slice_in_dim(key_weight, group * HEAD_DIM, HEAD_DIM, axis=1),
            lax.dynamic_slice_in_dim(value_weight, group * HEAD_DIM, HEAD_DIM, axis=1),
        ],
        axis=1,
    )
    cos_all, sin_all, routed, w_own = lax.optimization_barrier((cos_all, sin_all, routed, w_own))
    x_all, cot_then, cos_all, sin_all, routed, w_own = lax.optimization_barrier(
        (x_all, cot, cos_all, sin_all, routed, w_own)
    )
    cot_all = lax.all_gather(cot_then, "seq", axis=0)

    qkv, first_all = qkv_call(x_all, gain_one, cos_all, sin_all, w_own)
    qkv = qkv.reshape(devices, micro, per_device, 2 * pair)
    mix, log_total = attend_call(qkv)
    mix = unspread(mix.reshape(devices, rows, pair))
    mixed, middle, second_low = post_call(mix, output_weight, x, gain_two)

    chips = devices // 2
    chip, core = seq_place // 2, seq_place % 2
    onward = [(i, (i + 2) % devices) for i in range(devices)]
    dp_place = lax.axis_index("dp")
    first_bit = dp_place & 1
    last_bit = dp_place >> (len(dp_bits) - 1)
    held, kept, running, places = second_low, (), None, []
    for hop in range(chips):
        following = lax.ppermute(held, "seq", onward) if hop < chips - 1 else None
        other = swap(held, "seq", 1)
        source = 2 * ((chip - hop) % chips)
        place = jnp.stack([source + core, source + 1 - core, 1 - first_bit, 1 - last_bit])
        place = place.astype(jnp.int32)
        places.append(place[:2])
        dx, *kept = expert_call(
            hop, place, held, other, cot_all, routed, gate_weight, up_weight, down_weight, kept
        )
        if following is not None:
            following, dx = lax.optimization_barrier((following, dx))
        part = dx[0].astype(f32) + swap(dx[1], "seq", 1).astype(f32)
        if hop == 0:
            own_part = part
        else:
            if running is not None:
                part = part + running.astype(f32)
            part = part.astype(bf16)
            if following is not None:
                part, following = lax.optimization_barrier((part, following))
            else:
                part, kept = lax.optimization_barrier((part, kept))
            running = lax.ppermute(part, "seq", onward)
        held = following
    second_grad = (own_part + running.astype(f32)).astype(bf16)
    tokens, hidden_a, hidden_b, gate_low, up_low, slot_a, slot_b = kept

    def weight_parts(at, tokens, hidden_a, hidden_b, gate_low, up_low, slot_a, slot_b):
        pairs = (
            (tokens, gate_low[at]),
            (tokens, up_low[at]),
            (hidden_a[at], slot_a[at]),
            (hidden_b[at], slot_b[at]),
        )
        return [
            lax.dot_general(a, b, TN, preferred_element_type=f32).astype(bf16) for a, b in pairs
        ]

    leaving = weight_parts(0, *kept)
    part_bits = (dp_bits[0], dp_bits[-1], dp_bits[0], dp_bits[-1])
    stream_bits = (dp_bits, dp_bits[::-1])
    came = [swap(values, "dp", bit) for values, bit in zip(leaving, part_bits)]
    leaving, second_grad = lax.optimization_barrier((leaving, second_grad))

    mg_send, proj, middle_grad, gain_two_part = turn_call(
        second_grad, middle, gain_two, cot, output_weight, groups
    )
    mg = spread(mg_send)
    kept, _ = lax.optimization_barrier((kept, mg_send))
    mixed, proj, came[2:] = lax.optimization_barrier((mixed, proj, came[2:]))
    dense = output_weight_call(mixed, proj, gain_two_part, devices)
    dense_own = dense
    staying = weight_parts(1, *kept)
    turned = sum(((dp_place >> i) & 1) << (len(dp_bits) - 1 - i) for i in range(len(dp_bits)))
    part_at = jnp.stack([turned, dp_place]).astype(jnp.int32)
    low_at = jnp.bitwise_and(part_at, replicas // 2 - 1)
    keep_a, send_a, keep_b, send_b = part_sum_call(low_at, replicas // 2, came, staying)
    mg, keep_a, send_a, keep_b, send_b = lax.optimization_barrier(
        (mg, keep_a, send_a, keep_b, send_b)
    )
    streams = [
        relative_sum(keep_a, send_a, "dp", stream_bits[0][1:]),
        relative_sum(keep_b, send_b, "dp", stream_bits[1][1:]),
    ]
    dense = dense_own
    dense = lax.psum_scatter(dense, "seq", scatter_dimension=0)
    table_shape = (devices, micro, per_device, pair)
    dqkv = attend_back_call(
        qkv,
        mg.reshape(devices, micro, per_device, pair),
        log_total,
        cos_all.reshape(table_shape),
        sin_all.reshape(table_shape),
    )
    dqkv, streams = lax.optimization_barrier((dqkv, streams))
    near = [
        [v[0], swap(v[0], "dp", bits[-1])] for v, bits in zip(streams, stream_bits)
    ]
    back = unspread(dqkv.reshape(devices, rows, 2 * pair))
    d_all = dqkv.reshape(devices * rows, 2 * pair)
    first_tokens = first_all.reshape(devices * rows, features)
    part = lax.dot_general(first_tokens, d_all, TN, preferred_element_type=f32)
    dense = dense.reshape(dense.shape[-2], features)
    each = output_weight.shape[0] // devices
    if copies == 1:
        width = 2 * pair
        kept_pieces, sent_pieces = joint_call(part_at, part, dense, replicas)
        first = [
            kept_pieces[at].astype(f32) + swap(sent_pieces[at], "dp", bits[0]).astype(f32)
            for at, bits in enumerate(stream_bits)
        ]
        kept, sent_pieces = lax.optimization_barrier((kept, sent_pieces))
        moe_place = jnp.concatenate(places + [(1 - first_bit).astype(jnp.int32).reshape(1)])
        moe_all = moe_call(moe_place, kept[1], routed, down_weight, devices)
        far = [swap(v[0], "dp", bits[-2]) for v, bits in zip(streams, stream_bits)]
        first, near = lax.optimization_barrier(([v.astype(bf16) for v in first], near))
        own = [
            relative_sum(v[: replicas // 4], v[replicas // 4 :], "dp", bits[1:])
            for v, bits in zip(first, stream_bits)
        ]
        own = jnp.concatenate(own, axis=0)
        own, far, moe_all = lax.optimization_barrier((own, far, moe_all))
        backward = [(i, (i - 2) % devices) for i in range(devices)]
        round_ring = {0: own}
        for k in range(1, chips // 2 + 1):
            round_ring[k] = lax.ppermute(round_ring[k - 1], "seq", onward)
            if chips - k > k:
                round_ring[chips - k] = lax.ppermute(
                    round_ring[(chips - k + 1) % chips], "seq", backward
                )
        held = jnp.stack([round_ring[k] for k in range(chips)])
        passed = [swap(v[1], "dp", bits[-2]) for v, bits in zip(near, stream_bits)]
        held, moe_all, back, passed = lax.optimization_barrier((held, moe_all, back, passed))
        moe = lax.psum_scatter(moe_all, "seq", scatter_dimension=0)
        layer_output = (middle + residual_scale * moe.astype(f32)).astype(bf16)
    else:
        far = [swap(v[0], "dp", bits[-2]) for v, bits in zip(streams, stream_bits)]
        passed = [swap(v[1], "dp", bits[-2]) for v, bits in zip(near, stream_bits)]
    expert_pieces = []
    for (here, first), second, third, bits in zip(near, far, passed, stream_bits):
        pieces = [here, first, second, third]
        for bit in bits[:-2][::-1]:
            pieces = pieces + [swap(p, "dp", bit) for p in pieces]
        expert_pieces.append(pieces)
    input_grad = last_call(
        back, query_weight, key_weight, value_weight, x, gain_one, middle_grad
    )
    if copies == 1:
        gate_sum, up_sum, down_sum = expert_out_call(
            part_at, *expert_pieces, gate_weight.shape, down_weight.shape
        )
        full = []
        for at, bits in enumerate(stream_bits):
            pieces = [held[:, at]]
            for bit in bits[::-1]:
                pieces = pieces + [swap(p, "dp", bit) for p in pieces]
            full.append(pieces)
        last = [pieces.pop() for pieces in full]
        last, gate_sum, up_sum, down_sum, input_grad = lax.optimization_barrier(
            (last, gate_sum, up_sum, down_sum, input_grad)
        )
        full = [pieces + [end] for pieces, end in zip(full, last)]
        other = [[swap(p, "seq", 1) for p in pieces] for pieces in full]
        where_at = jnp.stack([turned, dp_place, chip, core]).astype(jnp.int32)
        (
            query_weight_grad,
            key_weight_grad,
            value_weight_grad,
            first_gain_grad,
            output_weight_grad,
            second_gain_grad,
        ) = dense_out_call(
            where_at, full, other, query_weight, key_weight, value_weight, gain_one, output_weight.shape
        )
    else:
        gate_sum, up_sum, down_sum = expert_out_call(
            part_at, *expert_pieces, gate_weight.shape, down_weight.shape
        )
        for bit in dp_bits:
            dense = (dense.astype(f32) + swap(dense, "dp", bit).astype(f32)).astype(bf16)
        dense = lax.all_gather(dense, "seq", axis=0).astype(f32)
        output_weight_grad = dense[:, :each].reshape(output_weight.shape)
        moe_place = jnp.concatenate(places + [(1 - first_bit).astype(jnp.int32).reshape(1)])
        moe_all = moe_call(moe_place, kept[1], routed, down_weight, devices)
        moe = lax.psum_scatter(moe_all, "seq", scatter_dimension=0)
        layer_output = (middle + residual_scale * moe.astype(f32)).astype(bf16)
        second_gain_grad = dense[0, each]
        part = part.astype(bf16)
        for bit in dp_bits[::-1]:
            part = half_sum(part, "dp", bit)
        wide = lax.all_gather(part, ("dp", "seq"), axis=0)
        wide = wide.reshape(replicas, devices, features // replicas, 2 * pair)[:, ::copies]
        query_weight_grad, key_weight_grad, value_weight_grad, first_gain_grad = weights_out_call(
            wide, query_weight, key_weight, value_weight, gain_one
        )
    second_gain_grad = second_gain_grad.reshape(features)
    return (
        layer_output.reshape(layer_input.shape),
        input_grad.reshape(layer_input.shape),
        first_gain_grad.reshape(features),
        query_weight_grad,
        key_weight_grad,
        value_weight_grad,
        output_weight_grad,
        second_gain_grad,
        gate_sum,
        up_sum,
        down_sum,
    )


def solution(mesh):
    return jax.shard_map(
        body,
        mesh=mesh,
        in_specs=(
            P(None, "dp", "seq", None),
            P(),
            P(),
            P(),
            P(),
            P(),
            P(),
            P("seq", None, None),
            P("seq", None, None),
            P("seq", None, None),
            P(None, "dp", None, None),
            P(None, "dp", None, None),
            P(None, "dp", "seq"),
            P(None, "dp", "seq", None),
        ),
        out_specs=(
            P(None, "dp", "seq", None),
            P(None, "dp", "seq", None),
            P(),
            P(),
            P(),
            P(),
            P(),
            P(),
            P("seq", None, None),
            P("seq", None, None),
            P("seq", None, None),
        ),
        check_vma=False,
    )
```

```python
from functools import partial

import jax
import jax.numpy as jnp
from jax import lax
from jax.experimental import pallas as pl
from jax.experimental.pallas import tpu as pltpu
from jax.sharding import PartitionSpec as P

HEAD_DIM = 64

rope_theta = 10000.0
attention_scale = 0.015625
residual_scale = 0.22
norm_eps = 1e-06
masked_score = -1e30

f32 = jnp.float32
bf16 = jnp.bfloat16
NT = (((1,), (1,)), ((), ()))
TN = (((0,), (0,)), ((), ()))


def dot(a, b):
    return jnp.dot(a, b, preferred_element_type=f32)


def dot_nt(a, b):
    return lax.dot_general(a, b, NT, preferred_element_type=f32)


def params(mib, *semantics):
    return pltpu.CompilerParams(
        vmem_limit_bytes=mib * 1024 * 1024, dimension_semantics=semantics or None
    )


def cost(flops, nbytes, trans=0):
    return pl.CostEstimate(
        flops=int(flops / 8), bytes_accessed=int(nbytes / 8), transcendentals=int(trans / 8)
    )


def whole(shape):
    return pl.BlockSpec(shape, lambda *_: (0,) * len(shape))


def rope_tables(positions, width):
    half = HEAD_DIM // 2
    exponent = jnp.arange(half, dtype=f32) * (-2.0 / HEAD_DIM)
    angles = positions.astype(f32)[:, None] * (rope_theta**exponent)[None, :]
    cosine, sine = jnp.cos(angles), jnp.sin(angles)
    copies = width // HEAD_DIM
    cos_row = jnp.concatenate([cosine, cosine] * copies, axis=1)
    sin_row = jnp.concatenate([-sine, sine] * copies, axis=1)
    return cos_row, sin_row


def partner(values):
    width = values.shape[1]
    half = HEAD_DIM // 2
    lane = lax.broadcasted_iota(jnp.int32, values.shape, 1)
    ahead = pltpu.roll(values, width - half, 1)
    behind = pltpu.roll(values, half, 1)
    return jnp.where(lane % HEAD_DIM < half, ahead, behind)


def qkv_kernel(x_ref, gain_ref, cos_ref, sin_ref, w_ref, qkv_ref, low_ref):
    pair = 2 * HEAD_DIM
    x = x_ref[0].astype(f32)
    scale = lax.rsqrt(jnp.mean(x * x, axis=-1, keepdims=True) + norm_eps)
    low = (x * scale * gain_ref[...]).astype(bf16)
    low_ref[0] = low
    cosine, sine = cos_ref[...], sin_ref[...]
    made = dot(low, w_ref[...])
    q, kv = made[:, :pair], made[:, pair:]
    q = (q * cosine + partner(q) * sine) * attention_scale
    qkv_ref[0, :, :pair] = q.astype(bf16)
    lane = lax.broadcasted_iota(jnp.int32, kv.shape, 1)
    turned = kv * cosine + partner(kv) * sine
    qkv_ref[0, :, pair:] = jnp.where(lane < HEAD_DIM, turned, kv).astype(bf16)


def qkv_call(x_all, gain, cos_all, sin_all, w_own):
    blocks, rows, features = x_all.shape
    pair = 2 * HEAD_DIM
    return pl.pallas_call(
        qkv_kernel,
        grid=(blocks,),
        in_specs=[
            pl.BlockSpec((1, rows, features), lambda s: (s, 0, 0)),
            whole((1, features)),
            pl.BlockSpec((rows, pair), lambda s: (s, 0)),
            pl.BlockSpec((rows, pair), lambda s: (s, 0)),
            whole(w_own.shape),
        ],
        out_specs=[
            pl.BlockSpec((1, rows, 2 * pair), lambda s: (s, 0, 0)),
            pl.BlockSpec((1, rows, features), lambda s: (s, 0, 0)),
        ],
        out_shape=[
            jax.ShapeDtypeStruct((blocks, rows, 2 * pair), bf16),
            jax.ShapeDtypeStruct((blocks, rows, features), bf16),
        ],
        compiler_params=params(58, "arbitrary"),
        cost_estimate=cost(4 * blocks * rows * features * pair, 14e6),
        name="norm_qkv_rope",
    )(x_all, gain, cos_all, sin_all, w_own)


def split_heads(block, first):
    wide = block.astype(f32)
    lane = lax.broadcasted_iota(jnp.int32, wide.shape, 1)
    turned = pltpu.roll(wide, HEAD_DIM, 1)
    if first:
        parts = [jnp.where(lane < HEAD_DIM, wide, 0.0), jnp.where(lane < HEAD_DIM, turned, 0.0)]
    else:
        parts = [jnp.where(lane >= HEAD_DIM, turned, 0.0), jnp.where(lane >= HEAD_DIM, wide, 0.0)]
    return jnp.concatenate(parts, axis=0).astype(bf16)


def join_heads(turned):
    rows = turned.shape[1] // 2
    return jnp.transpose(jnp.concatenate([turned[:, :rows], turned[:, rows:]], axis=0))


def scores_of(kv, q2, rows):
    scores = dot_nt(kv, q2)
    count = scores.shape[0]
    own = scores[count - rows :]
    key_at = lax.broadcasted_iota(jnp.int32, own.shape, 0)
    query_at = lax.broadcasted_iota(jnp.int32, own.shape, 1) % rows
    own = jnp.where(key_at <= query_at, own, masked_score)
    if count == rows:
        return own
    return jnp.concatenate([scores[: count - rows], own], axis=0)


def attend_kernel(qkv_ref, out_ref, log_ref):
    blocks, _, rows, width = qkv_ref.shape
    pair = width // 2
    kv = qkv_ref[:, 0, :, pair:].reshape(blocks * rows, pair)
    kv_t = jnp.transpose(kv)
    for at in range(blocks):
        count = (at + 1) * rows
        q2 = split_heads(qkv_ref[at, 0, :, :pair], True)
        scores = scores_of(kv[:count], q2, rows)
        top = jnp.max(scores, axis=0, keepdims=True)
        weights = jnp.exp(scores - top)
        total = jnp.sum(weights, axis=0, keepdims=True)
        out_t = dot(kv_t[:, :count], weights.astype(bf16))
        out_ref[at, 0] = join_heads(out_t[HEAD_DIM:] / total).astype(bf16)
        log_ref[at, 0] = top + jnp.log(total)


def attend_call(qkv):
    blocks, micro, rows, width = qkv.shape
    pair = width // 2
    length = blocks * rows
    return pl.pallas_call(
        attend_kernel,
        grid=(micro,),
        in_specs=[pl.BlockSpec((blocks, 1, rows, width), lambda m: (0, m, 0, 0))],
        out_specs=[
            pl.BlockSpec((blocks, 1, rows, pair), lambda m: (0, m, 0, 0)),
            pl.BlockSpec((blocks, 1, 1, 2 * rows), lambda m: (0, m, 0, 0)),
        ],
        out_shape=[
            jax.ShapeDtypeStruct((blocks, micro, rows, pair), bf16),
            jax.ShapeDtypeStruct((blocks, micro, 1, 2 * rows), f32),
        ],
        compiler_params=params(48, "arbitrary"),
        cost_estimate=cost(
            micro * length * length * 512, 3 * qkv.size, micro * length * length
        ),
        name="attention_forward",
    )(qkv)


def attend_back_kernel(qkv_ref, grad_ref, log_ref, cos_ref, sin_ref, out_ref, dkv_ref):
    blocks, _, rows, width = qkv_ref.shape
    pair = width // 2
    kv = qkv_ref[:, 0, :, pair:].reshape(blocks * rows, pair)
    kv_t = jnp.transpose(kv)
    dkv_ref[...] = jnp.zeros_like(dkv_ref)
    for at in range(blocks):
        count = (at + 1) * rows
        q2 = split_heads(qkv_ref[at, 0, :, :pair], True)
        g2 = split_heads(grad_ref[at, 0], False)
        scores = scores_of(kv[:count], q2, rows)
        prob = jnp.exp(scores - log_ref[at, 0])
        prob_grad = dot_nt(kv[:count], g2)
        delta = jnp.sum(prob * prob_grad, axis=0, keepdims=True)
        score_grad = (prob * (prob_grad - delta)).astype(bf16)
        dkv_ref[:count] += dot(score_grad, q2) + dot(prob.astype(bf16), g2)
        dq_t = dot(kv_t[:, :count], score_grad)
        dq = join_heads(dq_t[:HEAD_DIM] * attention_scale)
        dq = dq * cos_ref[at, 0] - partner(dq) * sin_ref[at, 0]
        out_ref[at, 0, :, :pair] = dq.astype(bf16)
    for at in range(blocks):
        dkv = dkv_ref[at * rows : (at + 1) * rows]
        lane = lax.broadcasted_iota(jnp.int32, dkv.shape, 1)
        turned = dkv * cos_ref[at, 0] - partner(dkv) * sin_ref[at, 0]
        out_ref[at, 0, :, pair:] = jnp.where(lane < HEAD_DIM, turned, dkv).astype(bf16)


def attend_back_call(qkv, grads, log_total, cos_all, sin_all):
    blocks, micro, rows, width = qkv.shape
    pair = width // 2
    length = blocks * rows
    spec = lambda lanes: pl.BlockSpec((blocks, 1, rows, lanes), lambda m: (0, m, 0, 0))
    return pl.pallas_call(
        attend_back_kernel,
        grid=(micro,),
        in_specs=[
            spec(width),
            spec(pair),
            pl.BlockSpec((blocks, 1, 1, 2 * rows), lambda m: (0, m, 0, 0)),
            spec(pair),
            spec(pair),
        ],
        out_specs=spec(width),
        out_shape=jax.ShapeDtypeStruct(qkv.shape, bf16),
        scratch_shapes=[pltpu.VMEM((length, pair), f32)],
        compiler_params=params(56, "arbitrary"),
        cost_estimate=cost(
            micro * length * length * 1280, 10 * qkv.size, micro * length * length
        ),
        name="attention_backward",
    )(qkv, grads, log_total, cos_all, sin_all)


def post_kernel(mix_ref, wo_ref, x_ref, gain_ref, mixed_ref, middle_ref, low_ref):
    mixed = jnp.concatenate([mix_ref[g] for g in range(mix_ref.shape[0])], axis=1)
    mixed_ref[...] = mixed
    middle = x_ref[...].astype(f32) + residual_scale * dot(mixed, wo_ref[...])
    middle_ref[...] = middle
    scale = lax.rsqrt(jnp.mean(middle * middle, axis=-1, keepdims=True) + norm_eps)
    low_ref[...] = (middle * scale * gain_ref[...]).astype(bf16)


def post_call(mix, wo, x, gain):
    rows, features = x.shape
    return pl.pallas_call(
        post_kernel,
        out_shape=[
            jax.ShapeDtypeStruct((rows, wo.shape[0]), bf16),
            jax.ShapeDtypeStruct((rows, features), f32),
            jax.ShapeDtypeStruct((rows, features), bf16),
        ],
        compiler_params=params(32),
        cost_estimate=cost(2 * rows * wo.size, 5e6),
        name="project_norm",
    )(mix, wo, x, gain)


def expert_kernel(place_ref, a_ref, b_ref, cot_ref, w_ref, wg_ref, wu_ref, wd_ref, *refs):
    dx_ref, x_ref, ha_ref, hb_ref, dg_ref, du_ref, sa_ref, sb_ref = refs[-8:]
    step = pl.program_id(0)
    first, second = place_ref[2], place_ref[3]
    half = sa_ref.shape[2]

    @pl.when(step == 0)
    def _():
        x_ref[...] = a_ref[...]

    @pl.when(step == 1)
    def _():
        x_ref[...] = b_ref[...]

    x = x_ref[...]
    cot = cot_ref[0].astype(f32)
    weight = residual_scale * w_ref[...]
    total = None
    for e in range(wg_ref.shape[0]):
        gate = dot(x, wg_ref[e])
        up = dot(x, wu_ref[e])
        slot_grad = (weight[:, e : e + 1] * cot).astype(bf16)
        to_a, to_b = jnp.bitwise_xor(first, e), jnp.bitwise_xor(second, e)
        sa_ref[to_a] = slot_grad[:, :half]
        sb_ref[to_b] = slot_grad[:, half:]
        hidden_grad = dot_nt(slot_grad, wd_ref[e])
        sig = 0.5 * jnp.tanh(0.5 * gate) + 0.5
        silu = gate * sig
        hidden = (silu * up).astype(bf16)
        ha_ref[to_a] = hidden
        hb_ref[to_b] = hidden
        gate_grad = (hidden_grad * up * (sig + silu * (1.0 - sig))).astype(bf16)
        up_grad = (hidden_grad * silu).astype(bf16)
        dg_ref[to_a] = gate_grad
        du_ref[to_b] = up_grad
        term = dot_nt(gate_grad, wg_ref[e]) + dot_nt(up_grad, wu_ref[e])
        total = term if total is None else total + term
    dx_ref[0] = total.astype(bf16)


def expert_call(at, place, own, other, cot_all, weight, wg, wu, wd, kept):
    blocks, rows, features = cot_all.shape
    count, _, hidden = wg.shape
    tokens = blocks * rows
    inner = jax.ShapeDtypeStruct((count, tokens, hidden), bf16)
    outer = jax.ShapeDtypeStruct((count, tokens, features // 2), bf16)
    inner_spec = pl.BlockSpec((count, rows, hidden), lambda s, place: (0, 2 * at + s, 0))
    outer_spec = pl.BlockSpec((count, rows, features // 2), lambda s, place: (0, 2 * at + s, 0))
    fixed = lambda shape: pl.BlockSpec(shape, lambda s, place: (0,) * len(shape))
    any_spec = pl.BlockSpec(memory_space=pl.ANY)
    first = 8
    return pl.pallas_call(
        expert_kernel,
        grid_spec=pltpu.PrefetchScalarGridSpec(
            num_scalar_prefetch=1,
            grid=(2,),
            in_specs=[
                fixed((rows, features)),
                fixed((rows, features)),
                pl.BlockSpec((1, rows, features), lambda s, place: (place[s], 0, 0)),
                pl.BlockSpec((rows, count), lambda s, place: (place[s], 0)),
                fixed(wg.shape),
                fixed(wu.shape),
                fixed(wd.shape),
            ]
            + [any_spec] * len(kept),
            out_specs=[
                pl.BlockSpec((1, rows, features), lambda s, place: (s, 0, 0)),
                pl.BlockSpec((rows, features), lambda s, place: (2 * at + s, 0)),
            ]
            + [inner_spec] * 4
            + [outer_spec] * 2,
        ),
        out_shape=[
            jax.ShapeDtypeStruct((2, rows, features), bf16),
            jax.ShapeDtypeStruct((tokens, features), bf16),
            inner,
            inner,
            inner,
            inner,
            outer,
            outer,
        ],
        input_output_aliases={first + i: 1 + i for i in range(len(kept))},
        compiler_params=params(48, "arbitrary"),
        cost_estimate=cost(20 * rows * wg.size, 2e7, 2 * rows * hidden * count),
        name="experts",
    )(place, own, other, cot_all, weight, wg, wu, wd, *kept)


def part_sum_kernel(at_ref, *refs):
    inputs, outs = refs[:16], refs[16:]
    at = 0
    for out in outs:
        gate_came, gate_here, down_came, down_here = inputs[at : at + 4]
        rows = gate_came.shape[0]
        out[0, :rows] = (gate_came[...].astype(f32) + gate_here[...].astype(f32)).astype(bf16)
        out[0, rows:] = (down_came[...].astype(f32) + down_here[...].astype(f32)).astype(bf16)
        at += 4


def part_sum_call(at, per, came, here):
    gate_rows, down_rows = came[0].shape[0] // per, came[2].shape[0] // per
    width = came[0].shape[1]
    steps = per // 2
    specs, args, out_specs, out_shapes = [], [], [], []
    for stream in range(2):
        for sent in range(2):
            for which, rows in ((stream, gate_rows), (stream + 2, down_rows)):
                spec = pl.BlockSpec(
                    (rows, width),
                    lambda s, at, sent=sent, stream=stream: (
                        jnp.bitwise_xor(s + sent * steps, at[stream]),
                        0,
                    ),
                )
                specs += [spec, spec]
                args += [came[which], here[which]]
            out_specs.append(
                pl.BlockSpec((1, gate_rows + down_rows, width), lambda s, at: (s, 0, 0))
            )
            out_shapes.append(
                jax.ShapeDtypeStruct((steps, gate_rows + down_rows, width), bf16)
            )
    return pl.pallas_call(
        part_sum_kernel,
        grid_spec=pltpu.PrefetchScalarGridSpec(
            num_scalar_prefetch=1, grid=(steps,), in_specs=specs, out_specs=out_specs
        ),
        out_shape=out_shapes,
        compiler_params=params(60, "arbitrary"),
        cost_estimate=cost(0, 9e6),
        name="expert_part_sum",
    )(at, *args)


def joint_kernel(at_ref, *refs):
    for (part_ref, wo_ref, gain_ref), out_ref in ((refs[:3], refs[6]), (refs[3:6], refs[7])):
        rows = part_ref.shape[0]
        upto = rows + wo_ref.shape[0]
        out_ref[0, 0, :rows] = part_ref[...].astype(bf16)
        out_ref[0, 0, rows:upto] = wo_ref[...]
        out_ref[0, 0, upto:] = gain_ref[...]


def joint_call(at, part, dense, parts):
    features, width = part.shape
    pieces = 2 * parts
    rows = features // pieces
    block_cols = dense.shape[1] // width
    per_block = pieces // block_cols
    extra = 16
    wo_rows = (dense.shape[0] - extra) // per_block
    last = dense.shape[0] // extra - 1
    steps = parts // 2

    def piece(sent):
        return lambda s, p, at: s * parts + jnp.bitwise_xor(p + sent * steps, at[s])

    specs = []
    for sent in range(2):
        at_piece = piece(sent)
        specs.append(
            pl.BlockSpec((rows, width), lambda s, p, at, f=at_piece: (f(s, p, at), 0))
        )
        specs.append(
            pl.BlockSpec(
                (wo_rows, width),
                lambda s, p, at, f=at_piece: (
                    lax.rem(f(s, p, at), per_block),
                    lax.div(f(s, p, at), per_block),
                ),
            )
        )
        specs.append(
            pl.BlockSpec(
                (extra, width), lambda s, p, at, f=at_piece: (last, lax.div(f(s, p, at), per_block))
            )
        )
    out_spec = pl.BlockSpec((1, 1, rows + wo_rows + extra, width), lambda s, p, at: (s, p, 0, 0))
    out_shape = jax.ShapeDtypeStruct((2, steps, rows + wo_rows + extra, width), bf16)
    return pl.pallas_call(
        joint_kernel,
        grid_spec=pltpu.PrefetchScalarGridSpec(
            num_scalar_prefetch=1, grid=(2, steps), in_specs=specs, out_specs=[out_spec] * 2
        ),
        out_shape=[out_shape] * 2,
        compiler_params=params(32, "arbitrary", "arbitrary"),
        cost_estimate=cost(0, 2e6),
        name="dense_pieces",
    )(at, part, dense, dense, part, dense, dense)


def expert_out_kernel(at_ref, *refs):
    pieces, (gate_ref, up_ref, down_ref) = refs[:-3], refs[-3:]
    parts = len(pieces) // 2
    step = pl.program_id(0)
    rows = gate_ref.shape[1]
    half = down_ref.shape[2] // 2
    for which in range(parts):

        @pl.when(jnp.bitwise_xor(step, at_ref[0]) == which)
        def _():
            a_ref = pieces[which]
            gate_ref[0] = a_ref[:rows].astype(f32)
            down_ref[0, :, :half] = a_ref[rows:].astype(f32)

        @pl.when(jnp.bitwise_xor(step, at_ref[1]) == which)
        def _():
            b_ref = pieces[parts + which]
            up_ref[0] = b_ref[:rows].astype(f32)
            down_ref[0, :, half:] = b_ref[rows:].astype(f32)


def expert_out_call(at, a, b, gate_shape, down_shape):
    parts = len(a)
    held, width = a[0].shape
    count = gate_shape[0]
    per = parts // count
    gate_rows, down_rows = gate_shape[1] // per, down_shape[1] // per
    place = lambda r, at: (lax.div(r, per), lax.rem(r, per), 0)
    return pl.pallas_call(
        expert_out_kernel,
        grid_spec=pltpu.PrefetchScalarGridSpec(
            num_scalar_prefetch=1,
            grid=(parts,),
            in_specs=[pl.BlockSpec((held, width), lambda r, at: (0, 0))] * (2 * parts),
            out_specs=[
                pl.BlockSpec((1, gate_rows, gate_shape[2]), place),
                pl.BlockSpec((1, gate_rows, gate_shape[2]), place),
                pl.BlockSpec((1, down_rows, down_shape[2]), place),
            ],
        ),
        out_shape=[
            jax.ShapeDtypeStruct(gate_shape, f32),
            jax.ShapeDtypeStruct(gate_shape, f32),
            jax.ShapeDtypeStruct(down_shape, f32),
        ],
        compiler_params=params(40, "arbitrary"),
        cost_estimate=cost(0, 2e7),
        name="expert_weights_out",
    )(at, *a, *b)


def moe_kernel(place_ref, h_ref, w_ref, wd_ref, *refs):
    out_ref = refs[-1]
    weight = w_ref[...]
    total = None
    first = place_ref[pl.num_programs(0)]
    for e in range(wd_ref.shape[0]):
        term = weight[:, e : e + 1] * dot(h_ref[jnp.bitwise_xor(first, e)], wd_ref[e])
        total = term if total is None else total + term
    out_ref[0] = total.astype(bf16)


def moe_call(at, place, hidden, weight, wd, blocks, kept):
    count, tokens, inner = hidden.shape
    features = wd.shape[2]
    rows = tokens // blocks
    steps = place.shape[0] - 1
    return pl.pallas_call(
        moe_kernel,
        grid_spec=pltpu.PrefetchScalarGridSpec(
            num_scalar_prefetch=1,
            grid=(steps,),
            in_specs=[
                pl.BlockSpec((count, rows, inner), lambda s, place: (0, at + s, 0)),
                pl.BlockSpec((rows, count), lambda s, place: (place[s], 0)),
                pl.BlockSpec(wd.shape, lambda s, place: (0, 0, 0)),
            ]
            + [pl.BlockSpec(memory_space=pl.ANY)] * len(kept),
            out_specs=pl.BlockSpec((1, rows, features), lambda s, place: (place[s], 0, 0)),
        ),
        out_shape=jax.ShapeDtypeStruct((blocks, rows, features), bf16),
        input_output_aliases={4: 0} if kept else {},
        compiler_params=params(48, "arbitrary"),
        cost_estimate=cost(2 * steps * rows * wd.size, 1.1e7),
        name="expert_outputs",
    )(place, hidden, weight, wd, *kept)


def turn_kernel(sg_ref, middle_ref, gain_ref, cot_ref, wo_ref, mg_ref, proj_ref, dmid_ref, dgain_ref):
    grad = sg_ref[...].astype(f32)
    middle = middle_ref[...]
    scale = lax.rsqrt(jnp.mean(middle * middle, axis=-1, keepdims=True) + norm_eps)
    unit = middle * scale
    dgain_ref[...] = jnp.sum(grad * unit, axis=0, keepdims=True)
    w = gain_ref[...] * grad
    dmid = cot_ref[...].astype(f32) + scale * (w - unit * jnp.mean(w * unit, axis=-1, keepdims=True))
    dmid_ref[...] = dmid
    proj = (residual_scale * dmid).astype(bf16)
    proj_ref[...] = proj
    mixed_grad = dot_nt(proj, wo_ref[...]).astype(bf16)
    groups, _, pair = mg_ref.shape
    for g in range(groups):
        mg_ref[g] = mixed_grad[:, g * pair : (g + 1) * pair]


def turn_call(sg, middle, gain, cot, wo, groups):
    rows, features = middle.shape
    pair = wo.shape[0] // groups
    return pl.pallas_call(
        turn_kernel,
        out_shape=[
            jax.ShapeDtypeStruct((groups, rows, pair), bf16),
            jax.ShapeDtypeStruct((rows, features), bf16),
            jax.ShapeDtypeStruct((rows, features), f32),
            jax.ShapeDtypeStruct((1, features), f32),
        ],
        compiler_params=params(32),
        cost_estimate=cost(2 * rows * wo.size, 6e6),
        name="norm_back_project_back",
    )(sg, middle, gain, cot, wo)


def output_weight_kernel(mixed_ref, proj_ref, dgain_ref, out_ref):
    held, each, features = out_ref.shape
    rows = mixed_ref.shape[1] // held
    part = lax.dot_general(mixed_ref[...], proj_ref[...], TN, preferred_element_type=f32)
    extra = jnp.broadcast_to(dgain_ref[...], (each - rows, features)).astype(bf16)
    for at in range(held):
        out_ref[at, :rows] = part[at * rows : (at + 1) * rows].astype(bf16)
        out_ref[at, rows:] = extra


def output_weight_call(mixed, proj, dgain, parts):
    rows, width = mixed.shape
    features = proj.shape[1]
    each = width // parts
    lanes = max(each, width // 2)
    held = lanes // each
    return pl.pallas_call(
        output_weight_kernel,
        grid=(parts // held,),
        in_specs=[
            pl.BlockSpec((rows, lanes), lambda s: (0, s)),
            whole((rows, features)),
            whole((1, features)),
        ],
        out_specs=pl.BlockSpec((held, each + 16, features), lambda s: (s, 0, 0)),
        out_shape=jax.ShapeDtypeStruct((parts, each + 16, features), bf16),
        compiler_params=params(32, "arbitrary"),
        cost_estimate=cost(2 * rows * width * features, 4e6),
        name="output_weight_part",
    )(mixed, proj, dgain)


def dense_out_kernel(at_ref, *refs):
    held, refs = refs[:-13], refs[-13:]
    wq_ref, wk_ref, wv_ref, gain_ref, dq_ref, dk_ref, dv_ref, dg_ref, wo_ref, dg2_ref = refs[:10]
    own_ref, other_ref = refs[10:12]
    parts = len(held) // 4
    stream, step = pl.program_id(0), pl.program_id(1)
    chips, _, width = own_ref.shape
    rows = dq_ref.shape[0]
    pair = width // 2
    chip, core = at_ref[2], at_ref[3]
    for which in range(2):
        for rel in range(parts):

            @pl.when((stream == which) & (jnp.bitwise_xor(step, at_ref[which]) == rel))
            def _():
                own_ref[...] = held[which * parts + rel][...]
                other_ref[...] = held[(2 + which) * parts + rel][...]

    total = jnp.zeros((rows, pair), f32)
    for k in range(chips):
        source = lax.rem(chip - k + chips, chips)
        a = jnp.where(core == 0, own_ref[k], other_ref[k]).astype(f32)
        b = jnp.where(core == 0, other_ref[k], own_ref[k]).astype(f32)
        q = jnp.concatenate([a[:rows, :pair], b[:rows, :pair]], axis=1)
        cols = pl.ds(pl.multiple_of(source * width, width), width)
        dq_ref[:, cols] = q
        made = q * wq_ref[:, cols].astype(f32)
        total += made[:, :pair] + made[:, pair:]
        a_kv, b_kv = a[:rows, pair:], b[:rows, pair:]
        lane = lax.broadcasted_iota(jnp.int32, a_kv.shape, 1)
        key = jnp.where(lane < HEAD_DIM, a_kv, pltpu.roll(b_kv, HEAD_DIM, 1))
        val = jnp.where(lane < HEAD_DIM, pltpu.roll(a_kv, HEAD_DIM, 1), b_kv)
        cols = pl.ds(pl.multiple_of(source * pair, pair), pair)
        dk_ref[:, cols] = key
        dv_ref[:, cols] = val
        total += key * wk_ref[:, cols].astype(f32) + val * wv_ref[:, cols].astype(f32)
        wo_ref[2 * source, 0] = a[rows : rows + wo_ref.shape[2]]
        wo_ref[2 * source + 1, 0] = b[rows : rows + wo_ref.shape[2]]
        if k == 0:
            dg2_ref[...] = a[rows + wo_ref.shape[2] :][:1]
    dg_ref[...] = jnp.sum(jnp.transpose(total), axis=0, keepdims=True) / gain_ref[...]


def dense_out_call(at, own, other, wq, wk, wv, gain, wo_shape):
    held = [*own[0], *own[1], *other[0], *other[1]]
    streams, parts = 2, len(own[0])
    chips, depth, width = held[0].shape
    features = wq.shape[0]
    groups = 2 * chips
    rows = features // (streams * parts)
    block_cols = wo_shape[1] // width
    per_block = streams * parts // block_cols
    wo_rows = wo_shape[0] // groups // per_block
    by_rows = lambda w: pl.BlockSpec((rows, w.shape[1]), lambda s, r, at: (s * parts + r, 0))
    gain_spec = pl.BlockSpec((1, rows), lambda s, r, at: (0, s * parts + r))
    outs = pl.pallas_call(
        dense_out_kernel,
        grid_spec=pltpu.PrefetchScalarGridSpec(
            num_scalar_prefetch=1,
            grid=(streams, parts),
            in_specs=[pl.BlockSpec(memory_space=pltpu.VMEM)] * len(held)
            + [by_rows(wq), by_rows(wk), by_rows(wv), gain_spec],
            out_specs=[
                by_rows(wq),
                by_rows(wk),
                by_rows(wv),
                gain_spec,
                pl.BlockSpec(
                    (groups, 1, wo_rows, width),
                    lambda s, r, at: (
                        0,
                        lax.rem(s * parts + r, per_block),
                        0,
                        lax.div(s * parts + r, per_block),
                    ),
                ),
                pl.BlockSpec((1, width), lambda s, r, at: (0, lax.div(s * parts + r, per_block))),
            ],
            scratch_shapes=[pltpu.VMEM((chips, depth, width), bf16)] * 2
            + [pltpu.VMEM((8, 128), f32)],
        ),
        out_shape=[
            jax.ShapeDtypeStruct(wq.shape, f32),
            jax.ShapeDtypeStruct(wk.shape, f32),
            jax.ShapeDtypeStruct(wv.shape, f32),
            jax.ShapeDtypeStruct((1, features), f32),
            jax.ShapeDtypeStruct((groups, per_block, wo_rows, wo_shape[1]), f32),
            jax.ShapeDtypeStruct((1, wo_shape[1]), f32),
        ],
        compiler_params=params(28, "arbitrary", "arbitrary"),
        cost_estimate=cost(2 * wq.size, 2.4e7),
        name="dense_weights_out",
    )(at, *held, wq, wk, wv, gain)
    return (*outs[:4], outs[4].reshape(wo_shape), outs[5])


def weights_out_kernel(wide_ref, wq_ref, wk_ref, wv_ref, gain_ref, dq_ref, dk_ref, dv_ref, dg_ref):
    groups, rows, width = wide_ref.shape
    pair = width // 2
    total = jnp.zeros((rows, pair), f32)
    for g in range(groups):
        part = wide_ref[g, :, :pair].astype(f32)
        at = slice(g * pair, (g + 1) * pair)
        dq_ref[:, at] = part
        total += part * wq_ref[:, at].astype(f32)
    for g in range(groups // 2):
        a = wide_ref[2 * g, :, pair:].astype(f32)
        b = wide_ref[2 * g + 1, :, pair:].astype(f32)
        lane = lax.broadcasted_iota(jnp.int32, a.shape, 1)
        at = slice(g * pair, (g + 1) * pair)
        k = jnp.where(lane < HEAD_DIM, a, pltpu.roll(b, HEAD_DIM, 1))
        v = jnp.where(lane < HEAD_DIM, pltpu.roll(a, HEAD_DIM, 1), b)
        dk_ref[:, at] = k
        dv_ref[:, at] = v
        total += k * wk_ref[:, at].astype(f32) + v * wv_ref[:, at].astype(f32)
    dg_ref[...] = jnp.sum(jnp.transpose(total), axis=0, keepdims=True) / gain_ref[...]


def weights_out_call(wide, wq, wk, wv, gain):
    chunks, groups, rows, width = wide.shape
    features = chunks * rows
    by_rows = lambda w: pl.BlockSpec((rows, w.shape[1]), lambda c: (c, 0))
    return pl.pallas_call(
        weights_out_kernel,
        grid=(chunks,),
        in_specs=[
            pl.BlockSpec((None, groups, rows, width), lambda c: (c, 0, 0, 0)),
            by_rows(wq),
            by_rows(wk),
            by_rows(wv),
            pl.BlockSpec((1, rows), lambda c: (0, c)),
        ],
        out_specs=[
            by_rows(wq),
            by_rows(wk),
            by_rows(wv),
            pl.BlockSpec((1, rows), lambda c: (0, c)),
        ],
        out_shape=[
            jax.ShapeDtypeStruct(wq.shape, f32),
            jax.ShapeDtypeStruct(wk.shape, f32),
            jax.ShapeDtypeStruct(wv.shape, f32),
            jax.ShapeDtypeStruct((1, features), f32),
        ],
        compiler_params=params(32, "arbitrary"),
        cost_estimate=cost(2 * wq.size, 1.6e7),
        name="attention_weights_out",
    )(wide, wq, wk, wv, gain)


def last_kernel(d_ref, wq_ref, wk_ref, wv_ref, x_ref, gain_ref, dmid_ref, out_ref):
    groups, rows, width = d_ref.shape
    pair = width // 2
    dq = jnp.concatenate([d_ref[g, :, :pair] for g in range(groups)], axis=1)
    grad = dot_nt(dq, wq_ref[...])
    keys, vals = [], []
    for at in range(groups // 2):
        a = d_ref[2 * at, :, pair:].astype(f32)
        b = d_ref[2 * at + 1, :, pair:].astype(f32)
        lane = lax.broadcasted_iota(jnp.int32, a.shape, 1)
        keys.append(jnp.where(lane < HEAD_DIM, a, pltpu.roll(b, HEAD_DIM, 1)).astype(bf16))
        vals.append(jnp.where(lane < HEAD_DIM, pltpu.roll(a, HEAD_DIM, 1), b).astype(bf16))
    grad = grad + dot_nt(jnp.concatenate(keys, axis=1), wk_ref[...])
    grad = grad + dot_nt(jnp.concatenate(vals, axis=1), wv_ref[...])
    x = x_ref[...].astype(f32)
    scale = lax.rsqrt(jnp.mean(x * x, axis=-1, keepdims=True) + norm_eps)
    unit = x * scale
    w = gain_ref[...] * grad
    out_ref[...] = dmid_ref[...] + scale * (w - unit * jnp.mean(w * unit, axis=-1, keepdims=True))


def last_call(d, wq, wk, wv, x, gain, dmid):
    rows, features = x.shape
    return pl.pallas_call(
        last_kernel,
        out_shape=jax.ShapeDtypeStruct((rows, features), f32),
        compiler_params=params(40),
        cost_estimate=cost(4 * rows * features * features, 8e6),
        name="input_gradient",
    )(d, wq, wk, wv, x, gain, dmid)


def swap(values, axis, bit):
    return lax.ppermute(values, axis, [(i, i ^ bit) for i in range(lax.axis_size(axis))])


def half_sum(values, axis, bit):
    half = values.shape[0] // 2
    upper = ((lax.axis_index(axis) & bit) > 0).astype(jnp.int32)
    came = swap(lax.dynamic_slice_in_dim(values, (1 - upper) * half, half), axis, bit)
    mine = lax.dynamic_slice_in_dim(values, upper * half, half)
    return (mine.astype(f32) + came.astype(f32)).astype(bf16)


def relative_sum(kept, sent, axis, bits):
    while True:
        kept = (kept.astype(f32) + swap(sent, axis, bits[0]).astype(f32)).astype(bf16)
        bits = bits[1:]
        if not bits:
            return kept
        half = kept.shape[0] // 2
        kept, sent = kept[:half], kept[half:]


def join_parts(stream, axis, bits):
    shape = stream.shape
    for bit in bits[::-1]:
        stream = jnp.stack([stream, swap(stream, axis, bit)])
    return stream.reshape(-1, *shape)


def body(
    layer_input,
    first_gain,
    query_weight,
    key_weight,
    value_weight,
    output_weight,
    second_gain,
    gate_weight,
    up_weight,
    down_weight,
    expert_ids,
    gate_values,
    positions,
    cotangent,
):
    micro, _, per_device, features = layer_input.shape
    devices = lax.axis_size("seq")
    replicas = lax.axis_size("dp")
    seq_place = lax.axis_index("seq")
    rows = micro * per_device
    local_experts = gate_weight.shape[0]
    groups = key_weight.shape[1] // HEAD_DIM
    pair = query_weight.shape[1] // groups
    copies = devices // groups

    dp_bits = [1 << i for i in range(replicas.bit_length() - 1)]

    def spread(blocks):
        if copies > 1:
            blocks = jnp.repeat(blocks, copies, axis=0)
        return lax.all_to_all(blocks, "seq", 0, 0, tiled=True)

    def unspread(blocks):
        return lax.all_to_all(blocks, "seq", 0, 0, tiled=True)[::copies]

    x = layer_input.reshape(rows, features)
    cot = cotangent.reshape(rows, features)
    gain_one = first_gain.reshape(1, features)
    gain_two = second_gain.reshape(1, features)
    pos_all = lax.all_to_all(
        jnp.broadcast_to(positions.reshape(1, rows), (devices, rows)), "seq", 0, 0, tiled=True
    )
    x_all = lax.all_gather(x, "seq", axis=0)
    cos_all, sin_all = rope_tables(pos_all.reshape(-1), pair)
    mine = seq_place * local_experts + jnp.arange(local_experts, dtype=jnp.int32)
    ids = expert_ids[:, 0]
    gates = gate_values[:, 0].astype(f32)
    routed = jnp.sum(
        jnp.where(ids[..., None] == mine, gates[..., None], 0.0), axis=2
    )
    routed = routed.reshape(micro, devices, per_device, local_experts)
    routed = jnp.transpose(routed, (1, 0, 2, 3)).reshape(devices * rows, local_experts)
    group = seq_place // copies
    w_own = jnp.concatenate(
        [
            lax.dynamic_slice_in_dim(query_weight, group * pair, pair, axis=1),
            lax.dynamic_slice_in_dim(key_weight, group * HEAD_DIM, HEAD_DIM, axis=1),
            lax.dynamic_slice_in_dim(value_weight, group * HEAD_DIM, HEAD_DIM, axis=1),
        ],
        axis=1,
    )
    cos_all, sin_all, routed, w_own = lax.optimization_barrier((cos_all, sin_all, routed, w_own))
    x_all, cot_then, cos_all, sin_all, routed, w_own = lax.optimization_barrier(
        (x_all, cot, cos_all, sin_all, routed, w_own)
    )
    cot_all = lax.all_gather(cot_then, "seq", axis=0)

    qkv, first_all = qkv_call(x_all, gain_one, cos_all, sin_all, w_own)
    qkv = qkv.reshape(devices, micro, per_device, 2 * pair)
    mix, log_total = attend_call(qkv)
    mix = unspread(mix.reshape(devices, rows, pair))
    mixed, middle, second_low = post_call(mix, output_weight, x, gain_two)

    chips = devices // 2
    chip, core = seq_place // 2, seq_place % 2
    onward = [(i, (i + 2) % devices) for i in range(devices)]
    dp_place = lax.axis_index("dp")
    first_bit = dp_place & 1
    last_bit = dp_place >> (len(dp_bits) - 1)
    held, kept, running, places = second_low, (), None, []
    for hop in range(chips):
        following = lax.ppermute(held, "seq", onward) if hop < chips - 1 else None
        other = swap(held, "seq", 1)
        source = 2 * ((chip - hop) % chips)
        place = jnp.stack([source + core, source + 1 - core, 1 - first_bit, 1 - last_bit])
        place = place.astype(jnp.int32)
        places.append(place[:2])
        dx, *kept = expert_call(
            hop, place, held, other, cot_all, routed, gate_weight, up_weight, down_weight, kept
        )
        if following is not None:
            following, dx = lax.optimization_barrier((following, dx))
        if hop == chips - 2:
            moe_place = jnp.concatenate(places + [place[2:3]])
            moe_all = moe_call(0, moe_place, kept[1], routed, down_weight, devices, ())
            kept, moe_all, running = lax.optimization_barrier((kept, moe_all, running))
        moe_place = place[:3]
        part = dx[0].astype(f32) + swap(dx[1], "seq", 1).astype(f32)
        if hop == 0:
            own_part = part
        else:
            if running is not None:
                part = part + running.astype(f32)
            part = part.astype(bf16)
            if following is not None:
                part, following = lax.optimization_barrier((part, following))
            else:
                part, kept = lax.optimization_barrier((part, kept))
            running = lax.ppermute(part, "seq", onward)
        held = following
    second_grad = (own_part + running.astype(f32)).astype(bf16)
    tokens, hidden_a, hidden_b, gate_low, up_low, slot_a, slot_b = kept

    def weight_parts(at, tokens, hidden_a, hidden_b, gate_low, up_low, slot_a, slot_b):
        pairs = (
            (tokens, gate_low[at]),
            (tokens, up_low[at]),
            (hidden_a[at], slot_a[at]),
            (hidden_b[at], slot_b[at]),
        )
        return [
            lax.dot_general(a, b, TN, preferred_element_type=f32).astype(bf16) for a, b in pairs
        ]

    leaving = weight_parts(0, *kept)
    part_bits = (dp_bits[0], dp_bits[-1], dp_bits[0], dp_bits[-1])
    stream_bits = (dp_bits, dp_bits[::-1])
    came = [swap(values, "dp", bit) for values, bit in zip(leaving, part_bits)]
    leaving, second_grad = lax.optimization_barrier((leaving, second_grad))

    mg_send, proj, middle_grad, gain_two_part = turn_call(
        second_grad, middle, gain_two, cot, output_weight, groups
    )
    mg = spread(mg_send)
    kept, _ = lax.optimization_barrier((kept, mg_send))
    mixed, proj, came[2:] = lax.optimization_barrier((mixed, proj, came[2:]))
    dense = output_weight_call(mixed, proj, gain_two_part, devices)
    dense_own = dense
    moe_all = moe_call(
        devices - 2, moe_place, kept[1], routed, down_weight, devices, (moe_all,)
    )
    staying = weight_parts(1, *kept)
    turned = sum(((dp_place >> i) & 1) << (len(dp_bits) - 1 - i) for i in range(len(dp_bits)))
    part_at = jnp.stack([turned, dp_place]).astype(jnp.int32)
    low_at = jnp.bitwise_and(part_at, replicas // 2 - 1)
    keep_a, send_a, keep_b, send_b = part_sum_call(low_at, replicas // 2, came, staying)
    mg, keep_a, send_a, keep_b, send_b = lax.optimization_barrier(
        (mg, keep_a, send_a, keep_b, send_b)
    )
    streams = [
        relative_sum(keep_a, send_a, "dp", stream_bits[0][1:]),
        relative_sum(keep_b, send_b, "dp", stream_bits[1][1:]),
    ]
    dense = dense_own
    dense = lax.psum_scatter(dense, "seq", scatter_dimension=0)
    moe_all, mg = lax.optimization_barrier((moe_all, mg))
    moe = lax.psum_scatter(moe_all, "seq", scatter_dimension=0)
    layer_output = (middle + residual_scale * moe.astype(f32)).astype(bf16)
    table_shape = (devices, micro, per_device, pair)
    dqkv = attend_back_call(
        qkv,
        mg.reshape(devices, micro, per_device, pair),
        log_total,
        cos_all.reshape(table_shape),
        sin_all.reshape(table_shape),
    )
    dqkv, streams = lax.optimization_barrier((dqkv, streams))
    near = [
        [v[0], swap(v[0], "dp", bits[-1])] for v, bits in zip(streams, stream_bits)
    ]
    back = unspread(dqkv.reshape(devices, rows, 2 * pair))
    d_all = dqkv.reshape(devices * rows, 2 * pair)
    first_tokens = first_all.reshape(devices * rows, features)
    part = lax.dot_general(first_tokens, d_all, TN, preferred_element_type=f32)
    dense = dense.reshape(dense.shape[-2], features)
    each = output_weight.shape[0] // devices
    if copies == 1:
        width = 2 * pair
        kept_pieces, sent_pieces = joint_call(part_at, part, dense, replicas)
        first = [
            kept_pieces[at].astype(f32) + swap(sent_pieces[at], "dp", bits[0]).astype(f32)
            for at, bits in enumerate(stream_bits)
        ]
        first, near = lax.optimization_barrier(([v.astype(bf16) for v in first], near))
        own = [
            relative_sum(v[: replicas // 4], v[replicas // 4 :], "dp", bits[1:])
            for v, bits in zip(first, stream_bits)
        ]
        own = jnp.concatenate(own, axis=0)
        far = [swap(v[0], "dp", bits[-2]) for v, bits in zip(streams, stream_bits)]
        own, far = lax.optimization_barrier((own, far))
        backward = [(i, (i - 2) % devices) for i in range(devices)]
        round_ring = {0: own}
        for k in range(1, chips // 2 + 1):
            round_ring[k] = lax.ppermute(round_ring[k - 1], "seq", onward)
            if chips - k > k:
                round_ring[chips - k] = lax.ppermute(
                    round_ring[(chips - k + 1) % chips], "seq", backward
                )
        held = jnp.stack([round_ring[k] for k in range(chips)])
        passed = [swap(v[1], "dp", bits[-2]) for v, bits in zip(near, stream_bits)]
        held, back, passed = lax.optimization_barrier((held, back, passed))
    else:
        far = [swap(v[0], "dp", bits[-2]) for v, bits in zip(streams, stream_bits)]
        passed = [swap(v[1], "dp", bits[-2]) for v, bits in zip(near, stream_bits)]
    expert_pieces = []
    for (here, first), second, third, bits in zip(near, far, passed, stream_bits):
        pieces = [here, first, second, third]
        for bit in bits[:-2][::-1]:
            pieces = pieces + [swap(p, "dp", bit) for p in pieces]
        expert_pieces.append(pieces)
    input_grad = last_call(
        back, query_weight, key_weight, value_weight, x, gain_one, middle_grad
    )
    if copies == 1:
        gate_sum, up_sum, down_sum = expert_out_call(
            part_at, *expert_pieces, gate_weight.shape, down_weight.shape
        )
        full = [[held[:, at], swap(held[:, at], "dp", b[-1])] for at, b in enumerate(stream_bits)]
        beside = [swap(v[0], "dp", bits[-2]) for v, bits in zip(full, stream_bits)]
        full, gate_sum, up_sum, down_sum, input_grad = lax.optimization_barrier(
            (full, gate_sum, up_sum, down_sum, input_grad)
        )
        for at, bits in enumerate(stream_bits):
            full[at] += [beside[at], swap(full[at][1], "dp", bits[-2])]
            for bit in bits[:-2][::-1]:
                full[at] += [swap(p, "dp", bit) for p in full[at]]
        other = [[swap(p, "seq", 1) for p in pieces] for pieces in full]
        where_at = jnp.stack([turned, dp_place, chip, core]).astype(jnp.int32)
        (
            query_weight_grad,
            key_weight_grad,
            value_weight_grad,
            first_gain_grad,
            output_weight_grad,
            second_gain_grad,
        ) = dense_out_call(
            where_at, full, other, query_weight, key_weight, value_weight, gain_one, output_weight.shape
        )
    else:
        gate_sum, up_sum, down_sum = expert_out_call(
            part_at, *expert_pieces, gate_weight.shape, down_weight.shape
        )
        for bit in dp_bits:
            dense = (dense.astype(f32) + swap(dense, "dp", bit).astype(f32)).astype(bf16)
        dense = lax.all_gather(dense, "seq", axis=0).astype(f32)
        output_weight_grad = dense[:, :each].reshape(output_weight.shape)
        second_gain_grad = dense[0, each]
        part = part.astype(bf16)
        for bit in dp_bits[::-1]:
            part = half_sum(part, "dp", bit)
        wide = lax.all_gather(part, ("dp", "seq"), axis=0)
        wide = wide.reshape(replicas, devices, features // replicas, 2 * pair)[:, ::copies]
        query_weight_grad, key_weight_grad, value_weight_grad, first_gain_grad = weights_out_call(
            wide, query_weight, key_weight, value_weight, gain_one
        )
    second_gain_grad = second_gain_grad.reshape(features)
    return (
        layer_output.reshape(layer_input.shape),
        input_grad.reshape(layer_input.shape),
        first_gain_grad.reshape(features),
        query_weight_grad,
        key_weight_grad,
        value_weight_grad,
        output_weight_grad,
        second_gain_grad,
        gate_sum,
        up_sum,
        down_sum,
    )


def solution(mesh):
    return jax.shard_map(
        body,
        mesh=mesh,
        in_specs=(
            P(None, "dp", "seq", None),
            P(),
            P(),
            P(),
            P(),
            P(),
            P(),
            P("seq", None, None),
            P("seq", None, None),
            P("seq", None, None),
            P(None, "dp", None, None),
            P(None, "dp", None, None),
            P(None, "dp", "seq"),
            P(None, "dp", "seq", None),
        ),
        out_specs=(
            P(None, "dp", "seq", None),
            P(None, "dp", "seq", None),
            P(),
            P(),
            P(),
            P(),
            P(),
            P(),
            P("seq", None, None),
            P("seq", None, None),
            P("seq", None, None),
        ),
        check_vma=False,
    )
```

```python
from functools import partial

import jax
import jax.numpy as jnp
from jax import lax
from jax.experimental import pallas as pl
from jax.experimental.pallas import tpu as pltpu
from jax.sharding import PartitionSpec as P

HEAD_DIM = 64

rope_theta = 10000.0
attention_scale = 0.015625
residual_scale = 0.22
norm_eps = 1e-06
masked_score = -1e30

f32 = jnp.float32
bf16 = jnp.bfloat16
NT = (((1,), (1,)), ((), ()))
TN = (((0,), (0,)), ((), ()))


def dot(a, b):
    return jnp.dot(a, b, preferred_element_type=f32)


def dot_nt(a, b):
    return lax.dot_general(a, b, NT, preferred_element_type=f32)


def params(mib, *semantics):
    return pltpu.CompilerParams(
        vmem_limit_bytes=mib * 1024 * 1024, dimension_semantics=semantics or None
    )


def cost(flops, nbytes, trans=0):
    return pl.CostEstimate(
        flops=int(flops / 8), bytes_accessed=int(nbytes / 8), transcendentals=int(trans / 8)
    )


def whole(shape):
    return pl.BlockSpec(shape, lambda *_: (0,) * len(shape))


def rope_tables(positions, width):
    half = HEAD_DIM // 2
    exponent = jnp.arange(half, dtype=f32) * (-2.0 / HEAD_DIM)
    angles = positions.astype(f32)[:, None] * (rope_theta**exponent)[None, :]
    cosine, sine = jnp.cos(angles), jnp.sin(angles)
    copies = width // HEAD_DIM
    cos_row = jnp.concatenate([cosine, cosine] * copies, axis=1)
    sin_row = jnp.concatenate([-sine, sine] * copies, axis=1)
    return cos_row, sin_row


def partner(values):
    width = values.shape[1]
    half = HEAD_DIM // 2
    lane = lax.broadcasted_iota(jnp.int32, values.shape, 1)
    ahead = pltpu.roll(values, width - half, 1)
    behind = pltpu.roll(values, half, 1)
    return jnp.where(lane % HEAD_DIM < half, ahead, behind)


def qkv_kernel(x_ref, gain_ref, cos_ref, sin_ref, w_ref, qkv_ref, low_ref):
    pair = 2 * HEAD_DIM
    x = x_ref[0].astype(f32)
    scale = lax.rsqrt(jnp.mean(x * x, axis=-1, keepdims=True) + norm_eps)
    low = (x * scale * gain_ref[...]).astype(bf16)
    low_ref[0] = low
    cosine, sine = cos_ref[...], sin_ref[...]
    made = dot(low, w_ref[...])
    q, kv = made[:, :pair], made[:, pair:]
    q = (q * cosine + partner(q) * sine) * attention_scale
    qkv_ref[0, :, :pair] = q.astype(bf16)
    lane = lax.broadcasted_iota(jnp.int32, kv.shape, 1)
    turned = kv * cosine + partner(kv) * sine
    qkv_ref[0, :, pair:] = jnp.where(lane < HEAD_DIM, turned, kv).astype(bf16)


def qkv_call(x_all, gain, cos_all, sin_all, w_own):
    blocks, rows, features = x_all.shape
    pair = 2 * HEAD_DIM
    return pl.pallas_call(
        qkv_kernel,
        grid=(blocks,),
        in_specs=[
            pl.BlockSpec((1, rows, features), lambda s: (s, 0, 0)),
            whole((1, features)),
            pl.BlockSpec((rows, pair), lambda s: (s, 0)),
            pl.BlockSpec((rows, pair), lambda s: (s, 0)),
            whole(w_own.shape),
        ],
        out_specs=[
            pl.BlockSpec((1, rows, 2 * pair), lambda s: (s, 0, 0)),
            pl.BlockSpec((1, rows, features), lambda s: (s, 0, 0)),
        ],
        out_shape=[
            jax.ShapeDtypeStruct((blocks, rows, 2 * pair), bf16),
            jax.ShapeDtypeStruct((blocks, rows, features), bf16),
        ],
        compiler_params=params(58, "arbitrary"),
        cost_estimate=cost(4 * blocks * rows * features * pair, 14e6),
        name="norm_qkv_rope",
    )(x_all, gain, cos_all, sin_all, w_own)


def split_heads(block, first):
    wide = block.astype(f32)
    lane = lax.broadcasted_iota(jnp.int32, wide.shape, 1)
    turned = pltpu.roll(wide, HEAD_DIM, 1)
    if first:
        parts = [jnp.where(lane < HEAD_DIM, wide, 0.0), jnp.where(lane < HEAD_DIM, turned, 0.0)]
    else:
        parts = [jnp.where(lane >= HEAD_DIM, turned, 0.0), jnp.where(lane >= HEAD_DIM, wide, 0.0)]
    return jnp.concatenate(parts, axis=0).astype(bf16)


def join_heads(turned):
    rows = turned.shape[1] // 2
    return jnp.transpose(jnp.concatenate([turned[:, :rows], turned[:, rows:]], axis=0))


def scores_of(kv, q2, rows):
    scores = dot_nt(kv, q2)
    count = scores.shape[0]
    own = scores[count - rows :]
    key_at = lax.broadcasted_iota(jnp.int32, own.shape, 0)
    query_at = lax.broadcasted_iota(jnp.int32, own.shape, 1) % rows
    own = jnp.where(key_at <= query_at, own, masked_score)
    if count == rows:
        return own
    return jnp.concatenate([scores[: count - rows], own], axis=0)


def attend_kernel(qkv_ref, out_ref, log_ref):
    blocks, _, rows, width = qkv_ref.shape
    pair = width // 2
    kv = qkv_ref[:, 0, :, pair:].reshape(blocks * rows, pair)
    kv_t = jnp.transpose(kv)
    for at in range(blocks):
        count = (at + 1) * rows
        q2 = split_heads(qkv_ref[at, 0, :, :pair], True)
        scores = scores_of(kv[:count], q2, rows)
        top = jnp.max(scores, axis=0, keepdims=True)
        weights = jnp.exp(scores - top)
        total = jnp.sum(weights, axis=0, keepdims=True)
        out_t = dot(kv_t[:, :count], weights.astype(bf16))
        out_ref[at, 0] = join_heads(out_t[HEAD_DIM:] / total).astype(bf16)
        log_ref[at, 0] = top + jnp.log(total)


def attend_call(qkv):
    blocks, micro, rows, width = qkv.shape
    pair = width // 2
    length = blocks * rows
    return pl.pallas_call(
        attend_kernel,
        grid=(micro,),
        in_specs=[pl.BlockSpec((blocks, 1, rows, width), lambda m: (0, m, 0, 0))],
        out_specs=[
            pl.BlockSpec((blocks, 1, rows, pair), lambda m: (0, m, 0, 0)),
            pl.BlockSpec((blocks, 1, 1, 2 * rows), lambda m: (0, m, 0, 0)),
        ],
        out_shape=[
            jax.ShapeDtypeStruct((blocks, micro, rows, pair), bf16),
            jax.ShapeDtypeStruct((blocks, micro, 1, 2 * rows), f32),
        ],
        compiler_params=params(48, "arbitrary"),
        cost_estimate=cost(
            micro * length * length * 512, 3 * qkv.size, micro * length * length
        ),
        name="attention_forward",
    )(qkv)


def attend_back_kernel(qkv_ref, grad_ref, log_ref, cos_ref, sin_ref, out_ref, dkv_ref):
    blocks, _, rows, width = qkv_ref.shape
    pair = width // 2
    kv = qkv_ref[:, 0, :, pair:].reshape(blocks * rows, pair)
    kv_t = jnp.transpose(kv)
    dkv_ref[...] = jnp.zeros_like(dkv_ref)
    for at in range(blocks):
        count = (at + 1) * rows
        q2 = split_heads(qkv_ref[at, 0, :, :pair], True)
        g2 = split_heads(grad_ref[at, 0], False)
        scores = scores_of(kv[:count], q2, rows)
        prob = jnp.exp(scores - log_ref[at, 0])
        prob_grad = dot_nt(kv[:count], g2)
        delta = jnp.sum(prob * prob_grad, axis=0, keepdims=True)
        score_grad = (prob * (prob_grad - delta)).astype(bf16)
        dkv_ref[:count] += dot(score_grad, q2) + dot(prob.astype(bf16), g2)
        dq_t = dot(kv_t[:, :count], score_grad)
        dq = join_heads(dq_t[:HEAD_DIM] * attention_scale)
        dq = dq * cos_ref[at, 0] - partner(dq) * sin_ref[at, 0]
        out_ref[at, 0, :, :pair] = dq.astype(bf16)
    for at in range(blocks):
        dkv = dkv_ref[at * rows : (at + 1) * rows]
        lane = lax.broadcasted_iota(jnp.int32, dkv.shape, 1)
        turned = dkv * cos_ref[at, 0] - partner(dkv) * sin_ref[at, 0]
        out_ref[at, 0, :, pair:] = jnp.where(lane < HEAD_DIM, turned, dkv).astype(bf16)


def attend_back_call(qkv, grads, log_total, cos_all, sin_all):
    blocks, micro, rows, width = qkv.shape
    pair = width // 2
    length = blocks * rows
    spec = lambda lanes: pl.BlockSpec((blocks, 1, rows, lanes), lambda m: (0, m, 0, 0))
    return pl.pallas_call(
        attend_back_kernel,
        grid=(micro,),
        in_specs=[
            spec(width),
            spec(pair),
            pl.BlockSpec((blocks, 1, 1, 2 * rows), lambda m: (0, m, 0, 0)),
            spec(pair),
            spec(pair),
        ],
        out_specs=spec(width),
        out_shape=jax.ShapeDtypeStruct(qkv.shape, bf16),
        scratch_shapes=[pltpu.VMEM((length, pair), f32)],
        compiler_params=params(56, "arbitrary"),
        cost_estimate=cost(
            micro * length * length * 1280, 10 * qkv.size, micro * length * length
        ),
        name="attention_backward",
    )(qkv, grads, log_total, cos_all, sin_all)


def post_kernel(mix_ref, wo_ref, x_ref, gain_ref, mixed_ref, middle_ref, low_ref):
    mixed = jnp.concatenate([mix_ref[g] for g in range(mix_ref.shape[0])], axis=1)
    mixed_ref[...] = mixed
    middle = x_ref[...].astype(f32) + residual_scale * dot(mixed, wo_ref[...])
    middle_ref[...] = middle
    scale = lax.rsqrt(jnp.mean(middle * middle, axis=-1, keepdims=True) + norm_eps)
    low_ref[...] = (middle * scale * gain_ref[...]).astype(bf16)


def post_call(mix, wo, x, gain):
    rows, features = x.shape
    return pl.pallas_call(
        post_kernel,
        out_shape=[
            jax.ShapeDtypeStruct((rows, wo.shape[0]), bf16),
            jax.ShapeDtypeStruct((rows, features), f32),
            jax.ShapeDtypeStruct((rows, features), bf16),
        ],
        compiler_params=params(32),
        cost_estimate=cost(2 * rows * wo.size, 5e6),
        name="project_norm",
    )(mix, wo, x, gain)


def expert_kernel(place_ref, a_ref, b_ref, cot_ref, w_ref, wg_ref, wu_ref, wd_ref, *refs):
    dx_ref, x_ref, ha_ref, hb_ref, dg_ref, du_ref, sa_ref, sb_ref = refs[-8:]
    step = pl.program_id(0)
    first, second = place_ref[2], place_ref[3]
    half = sa_ref.shape[2]

    @pl.when(step == 0)
    def _():
        x_ref[...] = a_ref[...]

    @pl.when(step == 1)
    def _():
        x_ref[...] = b_ref[...]

    x = x_ref[...]
    cot = cot_ref[0].astype(f32)
    weight = residual_scale * w_ref[...]
    total = None
    for e in range(wg_ref.shape[0]):
        gate = dot(x, wg_ref[e])
        up = dot(x, wu_ref[e])
        slot_grad = (weight[:, e : e + 1] * cot).astype(bf16)
        to_a, to_b = jnp.bitwise_xor(first, e), jnp.bitwise_xor(second, e)
        sa_ref[to_a] = slot_grad[:, :half]
        sb_ref[to_b] = slot_grad[:, half:]
        hidden_grad = dot_nt(slot_grad, wd_ref[e])
        sig = 0.5 * jnp.tanh(0.5 * gate) + 0.5
        silu = gate * sig
        hidden = (silu * up).astype(bf16)
        ha_ref[to_a] = hidden
        hb_ref[to_b] = hidden
        gate_grad = (hidden_grad * up * (sig + silu * (1.0 - sig))).astype(bf16)
        up_grad = (hidden_grad * silu).astype(bf16)
        dg_ref[to_a] = gate_grad
        du_ref[to_b] = up_grad
        term = dot_nt(gate_grad, wg_ref[e]) + dot_nt(up_grad, wu_ref[e])
        total = term if total is None else total + term
    dx_ref[0] = total.astype(bf16)


def expert_call(at, place, own, other, cot_all, weight, wg, wu, wd, kept):
    blocks, rows, features = cot_all.shape
    count, _, hidden = wg.shape
    tokens = blocks * rows
    inner = jax.ShapeDtypeStruct((count, tokens, hidden), bf16)
    outer = jax.ShapeDtypeStruct((count, tokens, features // 2), bf16)
    inner_spec = pl.BlockSpec((count, rows, hidden), lambda s, place: (0, 2 * at + s, 0))
    outer_spec = pl.BlockSpec((count, rows, features // 2), lambda s, place: (0, 2 * at + s, 0))
    fixed = lambda shape: pl.BlockSpec(shape, lambda s, place: (0,) * len(shape))
    any_spec = pl.BlockSpec(memory_space=pl.ANY)
    first = 8
    return pl.pallas_call(
        expert_kernel,
        grid_spec=pltpu.PrefetchScalarGridSpec(
            num_scalar_prefetch=1,
            grid=(2,),
            in_specs=[
                fixed((rows, features)),
                fixed((rows, features)),
                pl.BlockSpec((1, rows, features), lambda s, place: (place[s], 0, 0)),
                pl.BlockSpec((rows, count), lambda s, place: (place[s], 0)),
                fixed(wg.shape),
                fixed(wu.shape),
                fixed(wd.shape),
            ]
            + [any_spec] * len(kept),
            out_specs=[
                pl.BlockSpec((1, rows, features), lambda s, place: (s, 0, 0)),
                pl.BlockSpec((rows, features), lambda s, place: (2 * at + s, 0)),
            ]
            + [inner_spec] * 4
            + [outer_spec] * 2,
        ),
        out_shape=[
            jax.ShapeDtypeStruct((2, rows, features), bf16),
            jax.ShapeDtypeStruct((tokens, features), bf16),
            inner,
            inner,
            inner,
            inner,
            outer,
            outer,
        ],
        input_output_aliases={first + i: 1 + i for i in range(len(kept))},
        compiler_params=params(48, "arbitrary"),
        cost_estimate=cost(20 * rows * wg.size, 2e7, 2 * rows * hidden * count),
        name="experts",
    )(place, own, other, cot_all, weight, wg, wu, wd, *kept)


def part_sum_kernel(at_ref, *refs):
    inputs, outs = refs[:16], refs[16:]
    at = 0
    for out in outs:
        gate_came, gate_here, down_came, down_here = inputs[at : at + 4]
        rows = gate_came.shape[0]
        out[0, :rows] = (gate_came[...].astype(f32) + gate_here[...].astype(f32)).astype(bf16)
        out[0, rows:] = (down_came[...].astype(f32) + down_here[...].astype(f32)).astype(bf16)
        at += 4


def part_sum_call(at, per, came, here):
    gate_rows, down_rows = came[0].shape[0] // per, came[2].shape[0] // per
    width = came[0].shape[1]
    steps = per // 2
    specs, args, out_specs, out_shapes = [], [], [], []
    for stream in range(2):
        for sent in range(2):
            for which, rows in ((stream, gate_rows), (stream + 2, down_rows)):
                spec = pl.BlockSpec(
                    (rows, width),
                    lambda s, at, sent=sent, stream=stream: (
                        jnp.bitwise_xor(s + sent * steps, at[stream]),
                        0,
                    ),
                )
                specs += [spec, spec]
                args += [came[which], here[which]]
            out_specs.append(
                pl.BlockSpec((1, gate_rows + down_rows, width), lambda s, at: (s, 0, 0))
            )
            out_shapes.append(
                jax.ShapeDtypeStruct((steps, gate_rows + down_rows, width), bf16)
            )
    return pl.pallas_call(
        part_sum_kernel,
        grid_spec=pltpu.PrefetchScalarGridSpec(
            num_scalar_prefetch=1, grid=(steps,), in_specs=specs, out_specs=out_specs
        ),
        out_shape=out_shapes,
        compiler_params=params(60, "arbitrary"),
        cost_estimate=cost(0, 9e6),
        name="expert_part_sum",
    )(at, *args)


def joint_kernel(at_ref, *refs):
    for (part_ref, wo_ref, gain_ref), out_ref in ((refs[:3], refs[6]), (refs[3:6], refs[7])):
        rows = part_ref.shape[0]
        upto = rows + wo_ref.shape[0]
        out_ref[0, 0, :rows] = part_ref[...].astype(bf16)
        out_ref[0, 0, rows:upto] = wo_ref[...]
        out_ref[0, 0, upto:] = gain_ref[...]


def joint_call(at, part, dense, parts):
    features, width = part.shape
    pieces = 2 * parts
    rows = features // pieces
    block_cols = dense.shape[1] // width
    per_block = pieces // block_cols
    extra = 16
    wo_rows = (dense.shape[0] - extra) // per_block
    last = dense.shape[0] // extra - 1
    steps = parts // 2

    def piece(sent):
        return lambda s, p, at: s * parts + jnp.bitwise_xor(p + sent * steps, at[s])

    specs = []
    for sent in range(2):
        at_piece = piece(sent)
        specs.append(
            pl.BlockSpec((rows, width), lambda s, p, at, f=at_piece: (f(s, p, at), 0))
        )
        specs.append(
            pl.BlockSpec(
                (wo_rows, width),
                lambda s, p, at, f=at_piece: (
                    lax.rem(f(s, p, at), per_block),
                    lax.div(f(s, p, at), per_block),
                ),
            )
        )
        specs.append(
            pl.BlockSpec(
                (extra, width), lambda s, p, at, f=at_piece: (last, lax.div(f(s, p, at), per_block))
            )
        )
    out_spec = pl.BlockSpec((1, 1, rows + wo_rows + extra, width), lambda s, p, at: (s, p, 0, 0))
    out_shape = jax.ShapeDtypeStruct((2, steps, rows + wo_rows + extra, width), bf16)
    return pl.pallas_call(
        joint_kernel,
        grid_spec=pltpu.PrefetchScalarGridSpec(
            num_scalar_prefetch=1, grid=(2, steps), in_specs=specs, out_specs=[out_spec] * 2
        ),
        out_shape=[out_shape] * 2,
        compiler_params=params(32, "arbitrary", "arbitrary"),
        cost_estimate=cost(0, 2e6),
        name="dense_pieces",
    )(at, part, dense, dense, part, dense, dense)


def expert_out_kernel(at_ref, *refs):
    pieces, (gate_ref, up_ref, down_ref) = refs[:-3], refs[-3:]
    parts = len(pieces) // 2
    step = pl.program_id(0)
    rows = gate_ref.shape[1]
    half = down_ref.shape[2] // 2
    for which in range(parts):

        @pl.when(jnp.bitwise_xor(step, at_ref[0]) == which)
        def _():
            a_ref = pieces[which]
            gate_ref[0] = a_ref[:rows].astype(f32)
            down_ref[0, :, :half] = a_ref[rows:].astype(f32)

        @pl.when(jnp.bitwise_xor(step, at_ref[1]) == which)
        def _():
            b_ref = pieces[parts + which]
            up_ref[0] = b_ref[:rows].astype(f32)
            down_ref[0, :, half:] = b_ref[rows:].astype(f32)


def expert_out_call(at, a, b, gate_shape, down_shape):
    parts = len(a)
    held, width = a[0].shape
    count = gate_shape[0]
    per = parts // count
    gate_rows, down_rows = gate_shape[1] // per, down_shape[1] // per
    place = lambda r, at: (lax.div(r, per), lax.rem(r, per), 0)
    return pl.pallas_call(
        expert_out_kernel,
        grid_spec=pltpu.PrefetchScalarGridSpec(
            num_scalar_prefetch=1,
            grid=(parts,),
            in_specs=[pl.BlockSpec((held, width), lambda r, at: (0, 0))] * (2 * parts),
            out_specs=[
                pl.BlockSpec((1, gate_rows, gate_shape[2]), place),
                pl.BlockSpec((1, gate_rows, gate_shape[2]), place),
                pl.BlockSpec((1, down_rows, down_shape[2]), place),
            ],
        ),
        out_shape=[
            jax.ShapeDtypeStruct(gate_shape, f32),
            jax.ShapeDtypeStruct(gate_shape, f32),
            jax.ShapeDtypeStruct(down_shape, f32),
        ],
        compiler_params=params(40, "arbitrary"),
        cost_estimate=cost(0, 2e7),
        name="expert_weights_out",
    )(at, *a, *b)


def moe_kernel(place_ref, h_ref, w_ref, wd_ref, out_ref):
    weight = w_ref[...]
    total = None
    first = place_ref[pl.num_programs(0)]
    for e in range(wd_ref.shape[0]):
        term = weight[:, e : e + 1] * dot(h_ref[jnp.bitwise_xor(first, e)], wd_ref[e])
        total = term if total is None else total + term
    out_ref[0] = total.astype(bf16)


def moe_call(place, hidden, weight, wd, blocks):
    count, tokens, inner = hidden.shape
    features = wd.shape[2]
    rows = tokens // blocks
    return pl.pallas_call(
        moe_kernel,
        grid_spec=pltpu.PrefetchScalarGridSpec(
            num_scalar_prefetch=1,
            grid=(blocks,),
            in_specs=[
                pl.BlockSpec((count, rows, inner), lambda s, place: (0, s, 0)),
                pl.BlockSpec((rows, count), lambda s, place: (place[s], 0)),
                pl.BlockSpec(wd.shape, lambda s, place: (0, 0, 0)),
            ],
            out_specs=pl.BlockSpec((1, rows, features), lambda s, place: (place[s], 0, 0)),
        ),
        out_shape=jax.ShapeDtypeStruct((blocks, rows, features), bf16),
        compiler_params=params(60, "arbitrary"),
        cost_estimate=cost(2 * tokens * wd.size, 1.1e7),
        name="expert_outputs",
    )(place, hidden, weight, wd)


def turn_kernel(sg_ref, middle_ref, gain_ref, cot_ref, wo_ref, mg_ref, proj_ref, dmid_ref, dgain_ref):
    grad = sg_ref[...].astype(f32)
    middle = middle_ref[...]
    scale = lax.rsqrt(jnp.mean(middle * middle, axis=-1, keepdims=True) + norm_eps)
    unit = middle * scale
    dgain_ref[...] = jnp.sum(grad * unit, axis=0, keepdims=True)
    w = gain_ref[...] * grad
    dmid = cot_ref[...].astype(f32) + scale * (w - unit * jnp.mean(w * unit, axis=-1, keepdims=True))
    dmid_ref[...] = dmid
    proj = (residual_scale * dmid).astype(bf16)
    proj_ref[...] = proj
    mixed_grad = dot_nt(proj, wo_ref[...]).astype(bf16)
    groups, _, pair = mg_ref.shape
    for g in range(groups):
        mg_ref[g] = mixed_grad[:, g * pair : (g + 1) * pair]


def turn_call(sg, middle, gain, cot, wo, groups):
    rows, features = middle.shape
    pair = wo.shape[0] // groups
    return pl.pallas_call(
        turn_kernel,
        out_shape=[
            jax.ShapeDtypeStruct((groups, rows, pair), bf16),
            jax.ShapeDtypeStruct((rows, features), bf16),
            jax.ShapeDtypeStruct((rows, features), f32),
            jax.ShapeDtypeStruct((1, features), f32),
        ],
        compiler_params=params(32),
        cost_estimate=cost(2 * rows * wo.size, 6e6),
        name="norm_back_project_back",
    )(sg, middle, gain, cot, wo)


def output_weight_kernel(mixed_ref, proj_ref, dgain_ref, out_ref):
    held, each, features = out_ref.shape
    rows = mixed_ref.shape[1] // held
    part = lax.dot_general(mixed_ref[...], proj_ref[...], TN, preferred_element_type=f32)
    extra = jnp.broadcast_to(dgain_ref[...], (each - rows, features)).astype(bf16)
    for at in range(held):
        out_ref[at, :rows] = part[at * rows : (at + 1) * rows].astype(bf16)
        out_ref[at, rows:] = extra


def output_weight_call(mixed, proj, dgain, parts):
    rows, width = mixed.shape
    features = proj.shape[1]
    each = width // parts
    lanes = max(each, width // 2)
    held = lanes // each
    return pl.pallas_call(
        output_weight_kernel,
        grid=(parts // held,),
        in_specs=[
            pl.BlockSpec((rows, lanes), lambda s: (0, s)),
            whole((rows, features)),
            whole((1, features)),
        ],
        out_specs=pl.BlockSpec((held, each + 16, features), lambda s: (s, 0, 0)),
        out_shape=jax.ShapeDtypeStruct((parts, each + 16, features), bf16),
        compiler_params=params(32, "arbitrary"),
        cost_estimate=cost(2 * rows * width * features, 4e6),
        name="output_weight_part",
    )(mixed, proj, dgain)


def dense_out_kernel(at_ref, *refs):
    held, refs = refs[:-13], refs[-13:]
    wq_ref, wk_ref, wv_ref, gain_ref, dq_ref, dk_ref, dv_ref, dg_ref, wo_ref, dg2_ref = refs[:10]
    own_ref, other_ref = refs[10:12]
    parts = len(held) // 4
    stream, step = pl.program_id(0), pl.program_id(1)
    chips, _, width = own_ref.shape
    rows = dq_ref.shape[0]
    pair = width // 2
    chip, core = at_ref[2], at_ref[3]
    for which in range(2):
        for rel in range(parts):

            @pl.when((stream == which) & (jnp.bitwise_xor(step, at_ref[which]) == rel))
            def _():
                own_ref[...] = held[which * parts + rel][...]
                other_ref[...] = held[(2 + which) * parts + rel][...]

    total = jnp.zeros((rows, pair), f32)
    for k in range(chips):
        source = lax.rem(chip - k + chips, chips)
        a = jnp.where(core == 0, own_ref[k], other_ref[k]).astype(f32)
        b = jnp.where(core == 0, other_ref[k], own_ref[k]).astype(f32)
        q = jnp.concatenate([a[:rows, :pair], b[:rows, :pair]], axis=1)
        cols = pl.ds(pl.multiple_of(source * width, width), width)
        dq_ref[:, cols] = q
        made = q * wq_ref[:, cols].astype(f32)
        total += made[:, :pair] + made[:, pair:]
        a_kv, b_kv = a[:rows, pair:], b[:rows, pair:]
        lane = lax.broadcasted_iota(jnp.int32, a_kv.shape, 1)
        key = jnp.where(lane < HEAD_DIM, a_kv, pltpu.roll(b_kv, HEAD_DIM, 1))
        val = jnp.where(lane < HEAD_DIM, pltpu.roll(a_kv, HEAD_DIM, 1), b_kv)
        cols = pl.ds(pl.multiple_of(source * pair, pair), pair)
        dk_ref[:, cols] = key
        dv_ref[:, cols] = val
        total += key * wk_ref[:, cols].astype(f32) + val * wv_ref[:, cols].astype(f32)
        wo_ref[2 * source, 0] = a[rows : rows + wo_ref.shape[2]]
        wo_ref[2 * source + 1, 0] = b[rows : rows + wo_ref.shape[2]]
        if k == 0:
            dg2_ref[...] = a[rows + wo_ref.shape[2] :][:1]
    dg_ref[...] = jnp.sum(jnp.transpose(total), axis=0, keepdims=True) / gain_ref[...]


def dense_out_call(at, own, other, wq, wk, wv, gain, wo_shape):
    held = [*own[0], *own[1], *other[0], *other[1]]
    streams, parts = 2, len(own[0])
    chips, depth, width = held[0].shape
    features = wq.shape[0]
    groups = 2 * chips
    rows = features // (streams * parts)
    block_cols = wo_shape[1] // width
    per_block = streams * parts // block_cols
    wo_rows = wo_shape[0] // groups // per_block
    by_rows = lambda w: pl.BlockSpec((rows, w.shape[1]), lambda s, r, at: (s * parts + r, 0))
    gain_spec = pl.BlockSpec((1, rows), lambda s, r, at: (0, s * parts + r))
    outs = pl.pallas_call(
        dense_out_kernel,
        grid_spec=pltpu.PrefetchScalarGridSpec(
            num_scalar_prefetch=1,
            grid=(streams, parts),
            in_specs=[pl.BlockSpec(memory_space=pltpu.VMEM)] * len(held)
            + [by_rows(wq), by_rows(wk), by_rows(wv), gain_spec],
            out_specs=[
                by_rows(wq),
                by_rows(wk),
                by_rows(wv),
                gain_spec,
                pl.BlockSpec(
                    (groups, 1, wo_rows, width),
                    lambda s, r, at: (
                        0,
                        lax.rem(s * parts + r, per_block),
                        0,
                        lax.div(s * parts + r, per_block),
                    ),
                ),
                pl.BlockSpec((1, width), lambda s, r, at: (0, lax.div(s * parts + r, per_block))),
            ],
            scratch_shapes=[pltpu.VMEM((chips, depth, width), bf16)] * 2
            + [pltpu.VMEM((8, 128), f32)],
        ),
        out_shape=[
            jax.ShapeDtypeStruct(wq.shape, f32),
            jax.ShapeDtypeStruct(wk.shape, f32),
            jax.ShapeDtypeStruct(wv.shape, f32),
            jax.ShapeDtypeStruct((1, features), f32),
            jax.ShapeDtypeStruct((groups, per_block, wo_rows, wo_shape[1]), f32),
            jax.ShapeDtypeStruct((1, wo_shape[1]), f32),
        ],
        compiler_params=params(28, "arbitrary", "arbitrary"),
        cost_estimate=cost(2 * wq.size, 2.4e7),
        name="dense_weights_out",
    )(at, *held, wq, wk, wv, gain)
    return (*outs[:4], outs[4].reshape(wo_shape), outs[5])


def weights_out_kernel(wide_ref, wq_ref, wk_ref, wv_ref, gain_ref, dq_ref, dk_ref, dv_ref, dg_ref):
    groups, rows, width = wide_ref.shape
    pair = width // 2
    total = jnp.zeros((rows, pair), f32)
    for g in range(groups):
        part = wide_ref[g, :, :pair].astype(f32)
        at = slice(g * pair, (g + 1) * pair)
        dq_ref[:, at] = part
        total += part * wq_ref[:, at].astype(f32)
    for g in range(groups // 2):
        a = wide_ref[2 * g, :, pair:].astype(f32)
        b = wide_ref[2 * g + 1, :, pair:].astype(f32)
        lane = lax.broadcasted_iota(jnp.int32, a.shape, 1)
        at = slice(g * pair, (g + 1) * pair)
        k = jnp.where(lane < HEAD_DIM, a, pltpu.roll(b, HEAD_DIM, 1))
        v = jnp.where(lane < HEAD_DIM, pltpu.roll(a, HEAD_DIM, 1), b)
        dk_ref[:, at] = k
        dv_ref[:, at] = v
        total += k * wk_ref[:, at].astype(f32) + v * wv_ref[:, at].astype(f32)
    dg_ref[...] = jnp.sum(jnp.transpose(total), axis=0, keepdims=True) / gain_ref[...]


def weights_out_call(wide, wq, wk, wv, gain):
    chunks, groups, rows, width = wide.shape
    features = chunks * rows
    by_rows = lambda w: pl.BlockSpec((rows, w.shape[1]), lambda c: (c, 0))
    return pl.pallas_call(
        weights_out_kernel,
        grid=(chunks,),
        in_specs=[
            pl.BlockSpec((None, groups, rows, width), lambda c: (c, 0, 0, 0)),
            by_rows(wq),
            by_rows(wk),
            by_rows(wv),
            pl.BlockSpec((1, rows), lambda c: (0, c)),
        ],
        out_specs=[
            by_rows(wq),
            by_rows(wk),
            by_rows(wv),
            pl.BlockSpec((1, rows), lambda c: (0, c)),
        ],
        out_shape=[
            jax.ShapeDtypeStruct(wq.shape, f32),
            jax.ShapeDtypeStruct(wk.shape, f32),
            jax.ShapeDtypeStruct(wv.shape, f32),
            jax.ShapeDtypeStruct((1, features), f32),
        ],
        compiler_params=params(32, "arbitrary"),
        cost_estimate=cost(2 * wq.size, 1.6e7),
        name="attention_weights_out",
    )(wide, wq, wk, wv, gain)


def last_kernel(d_ref, wq_ref, wk_ref, wv_ref, x_ref, gain_ref, dmid_ref, out_ref):
    groups, rows, width = d_ref.shape
    pair = width // 2
    dq = jnp.concatenate([d_ref[g, :, :pair] for g in range(groups)], axis=1)
    grad = dot_nt(dq, wq_ref[...])
    keys, vals = [], []
    for at in range(groups // 2):
        a = d_ref[2 * at, :, pair:].astype(f32)
        b = d_ref[2 * at + 1, :, pair:].astype(f32)
        lane = lax.broadcasted_iota(jnp.int32, a.shape, 1)
        keys.append(jnp.where(lane < HEAD_DIM, a, pltpu.roll(b, HEAD_DIM, 1)).astype(bf16))
        vals.append(jnp.where(lane < HEAD_DIM, pltpu.roll(a, HEAD_DIM, 1), b).astype(bf16))
    grad = grad + dot_nt(jnp.concatenate(keys, axis=1), wk_ref[...])
    grad = grad + dot_nt(jnp.concatenate(vals, axis=1), wv_ref[...])
    x = x_ref[...].astype(f32)
    scale = lax.rsqrt(jnp.mean(x * x, axis=-1, keepdims=True) + norm_eps)
    unit = x * scale
    w = gain_ref[...] * grad
    out_ref[...] = dmid_ref[...] + scale * (w - unit * jnp.mean(w * unit, axis=-1, keepdims=True))


def last_call(d, wq, wk, wv, x, gain, dmid):
    rows, features = x.shape
    return pl.pallas_call(
        last_kernel,
        out_shape=jax.ShapeDtypeStruct((rows, features), f32),
        compiler_params=params(40),
        cost_estimate=cost(4 * rows * features * features, 8e6),
        name="input_gradient",
    )(d, wq, wk, wv, x, gain, dmid)


def swap(values, axis, bit):
    return lax.ppermute(values, axis, [(i, i ^ bit) for i in range(lax.axis_size(axis))])


def half_sum(values, axis, bit):
    half = values.shape[0] // 2
    upper = ((lax.axis_index(axis) & bit) > 0).astype(jnp.int32)
    came = swap(lax.dynamic_slice_in_dim(values, (1 - upper) * half, half), axis, bit)
    mine = lax.dynamic_slice_in_dim(values, upper * half, half)
    return (mine.astype(f32) + came.astype(f32)).astype(bf16)


def relative_sum(kept, sent, axis, bits):
    while True:
        kept = (kept.astype(f32) + swap(sent, axis, bits[0]).astype(f32)).astype(bf16)
        bits = bits[1:]
        if not bits:
            return kept
        half = kept.shape[0] // 2
        kept, sent = kept[:half], kept[half:]


def join_parts(stream, axis, bits):
    shape = stream.shape
    for bit in bits[::-1]:
        stream = jnp.stack([stream, swap(stream, axis, bit)])
    return stream.reshape(-1, *shape)


def body(
    layer_input,
    first_gain,
    query_weight,
    key_weight,
    value_weight,
    output_weight,
    second_gain,
    gate_weight,
    up_weight,
    down_weight,
    expert_ids,
    gate_values,
    positions,
    cotangent,
):
    micro, _, per_device, features = layer_input.shape
    devices = lax.axis_size("seq")
    replicas = lax.axis_size("dp")
    seq_place = lax.axis_index("seq")
    rows = micro * per_device
    local_experts = gate_weight.shape[0]
    groups = key_weight.shape[1] // HEAD_DIM
    pair = query_weight.shape[1] // groups
    copies = devices // groups

    dp_bits = [1 << i for i in range(replicas.bit_length() - 1)]

    def spread(blocks):
        if copies > 1:
            blocks = jnp.repeat(blocks, copies, axis=0)
        return lax.all_to_all(blocks, "seq", 0, 0, tiled=True)

    def unspread(blocks):
        return lax.all_to_all(blocks, "seq", 0, 0, tiled=True)[::copies]

    x = layer_input.reshape(rows, features)
    cot = cotangent.reshape(rows, features)
    gain_one = first_gain.reshape(1, features)
    gain_two = second_gain.reshape(1, features)
    pos_all = lax.all_to_all(
        jnp.broadcast_to(positions.reshape(1, rows), (devices, rows)), "seq", 0, 0, tiled=True
    )
    x_all = lax.all_gather(x, "seq", axis=0)
    cos_all, sin_all = rope_tables(pos_all.reshape(-1), pair)
    mine = seq_place * local_experts + jnp.arange(local_experts, dtype=jnp.int32)
    ids = expert_ids[:, 0]
    gates = gate_values[:, 0].astype(f32)
    routed = jnp.sum(
        jnp.where(ids[..., None] == mine, gates[..., None], 0.0), axis=2
    )
    routed = routed.reshape(micro, devices, per_device, local_experts)
    routed = jnp.transpose(routed, (1, 0, 2, 3)).reshape(devices * rows, local_experts)
    group = seq_place // copies
    w_own = jnp.concatenate(
        [
            lax.dynamic_slice_in_dim(query_weight, group * pair, pair, axis=1),
            lax.dynamic_slice_in_dim(key_weight, group * HEAD_DIM, HEAD_DIM, axis=1),
            lax.dynamic_slice_in_dim(value_weight, group * HEAD_DIM, HEAD_DIM, axis=1),
        ],
        axis=1,
    )
    cos_all, sin_all, routed, w_own = lax.optimization_barrier((cos_all, sin_all, routed, w_own))
    x_all, cot_then, cos_all, sin_all, routed, w_own = lax.optimization_barrier(
        (x_all, cot, cos_all, sin_all, routed, w_own)
    )
    cot_all = lax.all_gather(cot_then, "seq", axis=0)

    qkv, first_all = qkv_call(x_all, gain_one, cos_all, sin_all, w_own)
    qkv = qkv.reshape(devices, micro, per_device, 2 * pair)
    mix, log_total = attend_call(qkv)
    mix = unspread(mix.reshape(devices, rows, pair))
    mixed, middle, second_low = post_call(mix, output_weight, x, gain_two)

    chips = devices // 2
    chip, core = seq_place // 2, seq_place % 2
    onward = [(i, (i + 2) % devices) for i in range(devices)]
    dp_place = lax.axis_index("dp")
    first_bit = dp_place & 1
    last_bit = dp_place >> (len(dp_bits) - 1)
    held, kept, running, places = second_low, (), None, []
    for hop in range(chips):
        following = lax.ppermute(held, "seq", onward) if hop < chips - 1 else None
        other = swap(held, "seq", 1)
        source = 2 * ((chip - hop) % chips)
        place = jnp.stack([source + core, source + 1 - core, 1 - first_bit, 1 - last_bit])
        place = place.astype(jnp.int32)
        places.append(place[:2])
        dx, *kept = expert_call(
            hop, place, held, other, cot_all, routed, gate_weight, up_weight, down_weight, kept
        )
        if following is not None:
            following, dx = lax.optimization_barrier((following, dx))
        part = dx[0].astype(f32) + swap(dx[1], "seq", 1).astype(f32)
        if hop == 0:
            own_part = part
        else:
            if running is not None:
                part = part + running.astype(f32)
            part = part.astype(bf16)
            if following is not None:
                part, following = lax.optimization_barrier((part, following))
            else:
                part, kept = lax.optimization_barrier((part, kept))
            running = lax.ppermute(part, "seq", onward)
        held = following
    second_grad = (own_part + running.astype(f32)).astype(bf16)
    tokens, hidden_a, hidden_b, gate_low, up_low, slot_a, slot_b = kept

    def weight_parts(at, tokens, hidden_a, hidden_b, gate_low, up_low, slot_a, slot_b):
        pairs = (
            (tokens, gate_low[at]),
            (tokens, up_low[at]),
            (hidden_a[at], slot_a[at]),
            (hidden_b[at], slot_b[at]),
        )
        return [
            lax.dot_general(a, b, TN, preferred_element_type=f32).astype(bf16) for a, b in pairs
        ]

    leaving = weight_parts(0, *kept)
    part_bits = (dp_bits[0], dp_bits[-1], dp_bits[0], dp_bits[-1])
    stream_bits = (dp_bits, dp_bits[::-1])
    came = [swap(values, "dp", bit) for values, bit in zip(leaving, part_bits)]
    leaving, second_grad = lax.optimization_barrier((leaving, second_grad))

    mg_send, proj, middle_grad, gain_two_part = turn_call(
        second_grad, middle, gain_two, cot, output_weight, groups
    )
    mg = spread(mg_send)
    kept, _ = lax.optimization_barrier((kept, mg_send))
    mixed, proj, came[2:] = lax.optimization_barrier((mixed, proj, came[2:]))
    dense = output_weight_call(mixed, proj, gain_two_part, devices)
    dense_own = dense
    staying = weight_parts(1, *kept)
    turned = sum(((dp_place >> i) & 1) << (len(dp_bits) - 1 - i) for i in range(len(dp_bits)))
    part_at = jnp.stack([turned, dp_place]).astype(jnp.int32)
    low_at = jnp.bitwise_and(part_at, replicas // 2 - 1)
    keep_a, send_a, keep_b, send_b = part_sum_call(low_at, replicas // 2, came, staying)
    mg, keep_a, send_a, keep_b, send_b = lax.optimization_barrier(
        (mg, keep_a, send_a, keep_b, send_b)
    )
    streams = [
        relative_sum(keep_a, send_a, "dp", stream_bits[0][1:]),
        relative_sum(keep_b, send_b, "dp", stream_bits[1][1:]),
    ]
    dense = dense_own
    dense = lax.psum_scatter(dense, "seq", scatter_dimension=0)
    table_shape = (devices, micro, per_device, pair)
    dqkv = attend_back_call(
        qkv,
        mg.reshape(devices, micro, per_device, pair),
        log_total,
        cos_all.reshape(table_shape),
        sin_all.reshape(table_shape),
    )
    dqkv, streams = lax.optimization_barrier((dqkv, streams))
    near = [
        [v[0], swap(v[0], "dp", bits[-1])] for v, bits in zip(streams, stream_bits)
    ]
    back = unspread(dqkv.reshape(devices, rows, 2 * pair))
    d_all = dqkv.reshape(devices * rows, 2 * pair)
    first_tokens = first_all.reshape(devices * rows, features)
    part = lax.dot_general(first_tokens, d_all, TN, preferred_element_type=f32)
    dense = dense.reshape(dense.shape[-2], features)
    each = output_weight.shape[0] // devices
    if copies == 1:
        width = 2 * pair
        kept_pieces, sent_pieces = joint_call(part_at, part, dense, replicas)
        first = [
            kept_pieces[at].astype(f32) + swap(sent_pieces[at], "dp", bits[0]).astype(f32)
            for at, bits in enumerate(stream_bits)
        ]
        kept, sent_pieces = lax.optimization_barrier((kept, sent_pieces))
        moe_place = jnp.concatenate(places + [(1 - first_bit).astype(jnp.int32).reshape(1)])
        moe_all = moe_call(moe_place, kept[1], routed, down_weight, devices)
        first, near, moe_all = lax.optimization_barrier(
            ([v.astype(bf16) for v in first], near, moe_all)
        )
        moe = lax.psum_scatter(moe_all, "seq", scatter_dimension=0)
        layer_output = (middle + residual_scale * moe.astype(f32)).astype(bf16)
        own = [
            relative_sum(v[: replicas // 4], v[replicas // 4 :], "dp", bits[1:])
            for v, bits in zip(first, stream_bits)
        ]
        own = jnp.concatenate(own, axis=0)
        own, here = lax.optimization_barrier((own, [v[0] for v in near]))
        far = [swap(v, "dp", bits[-2]) for v, bits in zip(here, stream_bits)]
        backward = [(i, (i - 2) % devices) for i in range(devices)]
        round_ring = {0: own}
        for k in range(1, chips // 2 + 1):
            round_ring[k] = lax.ppermute(round_ring[k - 1], "seq", onward)
            if chips - k > k:
                round_ring[chips - k] = lax.ppermute(
                    round_ring[(chips - k + 1) % chips], "seq", backward
                )
            if k == 1:
                round_ring[1], coming = lax.optimization_barrier(
                    (round_ring[1], [v[1] for v in near])
                )
        held = jnp.stack([round_ring[k] for k in range(chips)])
        passed = [swap(v, "dp", bits[-2]) for v, bits in zip(coming, stream_bits)]
        held, back, far, passed = lax.optimization_barrier((held, back, far, passed))
    else:
        far = [swap(v[0], "dp", bits[-2]) for v, bits in zip(streams, stream_bits)]
        passed = [swap(v[1], "dp", bits[-2]) for v, bits in zip(near, stream_bits)]
    expert_pieces = []
    for (here, first), second, third, bits in zip(near, far, passed, stream_bits):
        pieces = [here, first, second, third]
        for bit in bits[:-2][::-1]:
            pieces = pieces + [swap(p, "dp", bit) for p in pieces]
        expert_pieces.append(pieces)
    input_grad = last_call(
        back, query_weight, key_weight, value_weight, x, gain_one, middle_grad
    )
    if copies == 1:
        gate_sum, up_sum, down_sum = expert_out_call(
            part_at, *expert_pieces, gate_weight.shape, down_weight.shape
        )
        full = [[held[:, at], swap(held[:, at], "dp", b[-1])] for at, b in enumerate(stream_bits)]
        beside = [swap(v[0], "dp", bits[-2]) for v, bits in zip(full, stream_bits)]
        full, beside, gate_sum, up_sum, down_sum, input_grad = lax.optimization_barrier(
            (full, beside, gate_sum, up_sum, down_sum, input_grad)
        )
        for at, bits in enumerate(stream_bits):
            full[at] += [beside[at], swap(full[at][1], "dp", bits[-2])]
            for bit in bits[:-2][::-1]:
                full[at] += [swap(p, "dp", bit) for p in full[at]]
        ends = [pieces.pop() for pieces in full]
        ends, layer_output = lax.optimization_barrier((ends, layer_output))
        full = [pieces + [end] for pieces, end in zip(full, ends)]
        other = [[swap(p, "seq", 1) for p in pieces] for pieces in full]
        where_at = jnp.stack([turned, dp_place, chip, core]).astype(jnp.int32)
        (
            query_weight_grad,
            key_weight_grad,
            value_weight_grad,
            first_gain_grad,
            output_weight_grad,
            second_gain_grad,
        ) = dense_out_call(
            where_at, full, other, query_weight, key_weight, value_weight, gain_one, output_weight.shape
        )
    else:
        gate_sum, up_sum, down_sum = expert_out_call(
            part_at, *expert_pieces, gate_weight.shape, down_weight.shape
        )
        for bit in dp_bits:
            dense = (dense.astype(f32) + swap(dense, "dp", bit).astype(f32)).astype(bf16)
        dense = lax.all_gather(dense, "seq", axis=0).astype(f32)
        output_weight_grad = dense[:, :each].reshape(output_weight.shape)
        moe_place = jnp.concatenate(places + [(1 - first_bit).astype(jnp.int32).reshape(1)])
        moe_all = moe_call(moe_place, kept[1], routed, down_weight, devices)
        moe = lax.psum_scatter(moe_all, "seq", scatter_dimension=0)
        layer_output = (middle + residual_scale * moe.astype(f32)).astype(bf16)
        second_gain_grad = dense[0, each]
        part = part.astype(bf16)
        for bit in dp_bits[::-1]:
            part = half_sum(part, "dp", bit)
        wide = lax.all_gather(part, ("dp", "seq"), axis=0)
        wide = wide.reshape(replicas, devices, features // replicas, 2 * pair)[:, ::copies]
        query_weight_grad, key_weight_grad, value_weight_grad, first_gain_grad = weights_out_call(
            wide, query_weight, key_weight, value_weight, gain_one
        )
    second_gain_grad = second_gain_grad.reshape(features)
    return (
        layer_output.reshape(layer_input.shape),
        input_grad.reshape(layer_input.shape),
        first_gain_grad.reshape(features),
        query_weight_grad,
        key_weight_grad,
        value_weight_grad,
        output_weight_grad,
        second_gain_grad,
        gate_sum,
        up_sum,
        down_sum,
    )


def solution(mesh):
    return jax.shard_map(
        body,
        mesh=mesh,
        in_specs=(
            P(None, "dp", "seq", None),
            P(),
            P(),
            P(),
            P(),
            P(),
            P(),
            P("seq", None, None),
            P("seq", None, None),
            P("seq", None, None),
            P(None, "dp", None, None),
            P(None, "dp", None, None),
            P(None, "dp", "seq"),
            P(None, "dp", "seq", None),
        ),
        out_specs=(
            P(None, "dp", "seq", None),
            P(None, "dp", "seq", None),
            P(),
            P(),
            P(),
            P(),
            P(),
            P(),
            P("seq", None, None),
            P("seq", None, None),
            P("seq", None, None),
        ),
        check_vma=False,
    )
```

```python
from functools import partial

import jax
import jax.numpy as jnp
from jax import lax
from jax.experimental import pallas as pl
from jax.experimental.pallas import tpu as pltpu
from jax.sharding import PartitionSpec as P

HEAD_DIM = 64

rope_theta = 10000.0
attention_scale = 0.015625
residual_scale = 0.22
norm_eps = 1e-06
masked_score = -1e30

f32 = jnp.float32
bf16 = jnp.bfloat16
NT = (((1,), (1,)), ((), ()))
TN = (((0,), (0,)), ((), ()))


def dot(a, b):
    return jnp.dot(a, b, preferred_element_type=f32)


def dot_nt(a, b):
    return lax.dot_general(a, b, NT, preferred_element_type=f32)


def params(mib, *semantics):
    return pltpu.CompilerParams(
        vmem_limit_bytes=mib * 1024 * 1024, dimension_semantics=semantics or None
    )


def cost(flops, nbytes, trans=0):
    return pl.CostEstimate(
        flops=int(flops / 8), bytes_accessed=int(nbytes / 8), transcendentals=int(trans / 8)
    )


def whole(shape):
    return pl.BlockSpec(shape, lambda *_: (0,) * len(shape))


def rope_tables(positions, width):
    half = HEAD_DIM // 2
    exponent = jnp.arange(half, dtype=f32) * (-2.0 / HEAD_DIM)
    angles = positions.astype(f32)[:, None] * (rope_theta**exponent)[None, :]
    cosine, sine = jnp.cos(angles), jnp.sin(angles)
    copies = width // HEAD_DIM
    cos_row = jnp.concatenate([cosine, cosine] * copies, axis=1)
    sin_row = jnp.concatenate([-sine, sine] * copies, axis=1)
    return cos_row, sin_row


def partner(values):
    width = values.shape[1]
    half = HEAD_DIM // 2
    lane = lax.broadcasted_iota(jnp.int32, values.shape, 1)
    ahead = pltpu.roll(values, width - half, 1)
    behind = pltpu.roll(values, half, 1)
    return jnp.where(lane % HEAD_DIM < half, ahead, behind)


def qkv_kernel(x_ref, gain_ref, cos_ref, sin_ref, w_ref, qkv_ref, low_ref):
    pair = 2 * HEAD_DIM
    x = x_ref[0].astype(f32)
    scale = lax.rsqrt(jnp.mean(x * x, axis=-1, keepdims=True) + norm_eps)
    low = (x * scale * gain_ref[...]).astype(bf16)
    low_ref[0] = low
    cosine, sine = cos_ref[...], sin_ref[...]
    made = dot(low, w_ref[...])
    q, kv = made[:, :pair], made[:, pair:]
    q = (q * cosine + partner(q) * sine) * attention_scale
    qkv_ref[0, :, :pair] = q.astype(bf16)
    lane = lax.broadcasted_iota(jnp.int32, kv.shape, 1)
    turned = kv * cosine + partner(kv) * sine
    qkv_ref[0, :, pair:] = jnp.where(lane < HEAD_DIM, turned, kv).astype(bf16)


def qkv_call(x_all, gain, cos_all, sin_all, w_own):
    blocks, rows, features = x_all.shape
    pair = 2 * HEAD_DIM
    return pl.pallas_call(
        qkv_kernel,
        grid=(blocks,),
        in_specs=[
            pl.BlockSpec((1, rows, features), lambda s: (s, 0, 0)),
            whole((1, features)),
            pl.BlockSpec((rows, pair), lambda s: (s, 0)),
            pl.BlockSpec((rows, pair), lambda s: (s, 0)),
            whole(w_own.shape),
        ],
        out_specs=[
            pl.BlockSpec((1, rows, 2 * pair), lambda s: (s, 0, 0)),
            pl.BlockSpec((1, rows, features), lambda s: (s, 0, 0)),
        ],
        out_shape=[
            jax.ShapeDtypeStruct((blocks, rows, 2 * pair), bf16),
            jax.ShapeDtypeStruct((blocks, rows, features), bf16),
        ],
        compiler_params=params(58, "arbitrary"),
        cost_estimate=cost(4 * blocks * rows * features * pair, 14e6),
        name="norm_qkv_rope",
    )(x_all, gain, cos_all, sin_all, w_own)


def split_heads(block, first):
    wide = block.astype(f32)
    lane = lax.broadcasted_iota(jnp.int32, wide.shape, 1)
    turned = pltpu.roll(wide, HEAD_DIM, 1)
    if first:
        parts = [jnp.where(lane < HEAD_DIM, wide, 0.0), jnp.where(lane < HEAD_DIM, turned, 0.0)]
    else:
        parts = [jnp.where(lane >= HEAD_DIM, turned, 0.0), jnp.where(lane >= HEAD_DIM, wide, 0.0)]
    return jnp.concatenate(parts, axis=0).astype(bf16)


def join_heads(turned):
    rows = turned.shape[1] // 2
    return jnp.transpose(jnp.concatenate([turned[:, :rows], turned[:, rows:]], axis=0))


def scores_of(kv, q2, rows):
    scores = dot_nt(kv, q2)
    count = scores.shape[0]
    own = scores[count - rows :]
    key_at = lax.broadcasted_iota(jnp.int32, own.shape, 0)
    query_at = lax.broadcasted_iota(jnp.int32, own.shape, 1) % rows
    own = jnp.where(key_at <= query_at, own, masked_score)
    if count == rows:
        return own
    return jnp.concatenate([scores[: count - rows], own], axis=0)


def attend_kernel(qkv_ref, out_ref, log_ref):
    blocks, _, rows, width = qkv_ref.shape
    pair = width // 2
    kv = qkv_ref[:, 0, :, pair:].reshape(blocks * rows, pair)
    kv_t = jnp.transpose(kv)
    for at in range(blocks):
        count = (at + 1) * rows
        q2 = split_heads(qkv_ref[at, 0, :, :pair], True)
        scores = scores_of(kv[:count], q2, rows)
        top = jnp.max(scores, axis=0, keepdims=True)
        weights = jnp.exp(scores - top)
        total = jnp.sum(weights, axis=0, keepdims=True)
        out_t = dot(kv_t[:, :count], weights.astype(bf16))
        out_ref[at, 0] = join_heads(out_t[HEAD_DIM:] / total).astype(bf16)
        log_ref[at, 0] = top + jnp.log(total)


def attend_call(qkv):
    blocks, micro, rows, width = qkv.shape
    pair = width // 2
    length = blocks * rows
    return pl.pallas_call(
        attend_kernel,
        grid=(micro,),
        in_specs=[pl.BlockSpec((blocks, 1, rows, width), lambda m: (0, m, 0, 0))],
        out_specs=[
            pl.BlockSpec((blocks, 1, rows, pair), lambda m: (0, m, 0, 0)),
            pl.BlockSpec((blocks, 1, 1, 2 * rows), lambda m: (0, m, 0, 0)),
        ],
        out_shape=[
            jax.ShapeDtypeStruct((blocks, micro, rows, pair), bf16),
            jax.ShapeDtypeStruct((blocks, micro, 1, 2 * rows), f32),
        ],
        compiler_params=params(48, "arbitrary"),
        cost_estimate=cost(
            micro * length * length * 512, 3 * qkv.size, micro * length * length
        ),
        name="attention_forward",
    )(qkv)


def attend_back_kernel(qkv_ref, grad_ref, log_ref, cos_ref, sin_ref, out_ref, dkv_ref):
    blocks, _, rows, width = qkv_ref.shape
    pair = width // 2
    kv = qkv_ref[:, 0, :, pair:].reshape(blocks * rows, pair)
    kv_t = jnp.transpose(kv)
    dkv_ref[...] = jnp.zeros_like(dkv_ref)
    for at in range(blocks):
        count = (at + 1) * rows
        q2 = split_heads(qkv_ref[at, 0, :, :pair], True)
        g2 = split_heads(grad_ref[at, 0], False)
        scores = scores_of(kv[:count], q2, rows)
        prob = jnp.exp(scores - log_ref[at, 0])
        prob_grad = dot_nt(kv[:count], g2)
        delta = jnp.sum(prob * prob_grad, axis=0, keepdims=True)
        score_grad = (prob * (prob_grad - delta)).astype(bf16)
        dkv_ref[:count] += dot(score_grad, q2) + dot(prob.astype(bf16), g2)
        dq_t = dot(kv_t[:, :count], score_grad)
        dq = join_heads(dq_t[:HEAD_DIM] * attention_scale)
        dq = dq * cos_ref[at, 0] - partner(dq) * sin_ref[at, 0]
        out_ref[at, 0, :, :pair] = dq.astype(bf16)
    for at in range(blocks):
        dkv = dkv_ref[at * rows : (at + 1) * rows]
        lane = lax.broadcasted_iota(jnp.int32, dkv.shape, 1)
        turned = dkv * cos_ref[at, 0] - partner(dkv) * sin_ref[at, 0]
        out_ref[at, 0, :, pair:] = jnp.where(lane < HEAD_DIM, turned, dkv).astype(bf16)


def attend_back_call(qkv, grads, log_total, cos_all, sin_all):
    blocks, micro, rows, width = qkv.shape
    pair = width // 2
    length = blocks * rows
    spec = lambda lanes: pl.BlockSpec((blocks, 1, rows, lanes), lambda m: (0, m, 0, 0))
    return pl.pallas_call(
        attend_back_kernel,
        grid=(micro,),
        in_specs=[
            spec(width),
            spec(pair),
            pl.BlockSpec((blocks, 1, 1, 2 * rows), lambda m: (0, m, 0, 0)),
            spec(pair),
            spec(pair),
        ],
        out_specs=spec(width),
        out_shape=jax.ShapeDtypeStruct(qkv.shape, bf16),
        scratch_shapes=[pltpu.VMEM((length, pair), f32)],
        compiler_params=params(56, "arbitrary"),
        cost_estimate=cost(
            micro * length * length * 1280, 10 * qkv.size, micro * length * length
        ),
        name="attention_backward",
    )(qkv, grads, log_total, cos_all, sin_all)


def post_kernel(mix_ref, wo_ref, x_ref, gain_ref, mixed_ref, middle_ref, low_ref):
    mixed = jnp.concatenate([mix_ref[g] for g in range(mix_ref.shape[0])], axis=1)
    mixed_ref[...] = mixed
    middle = x_ref[...].astype(f32) + residual_scale * dot(mixed, wo_ref[...])
    middle_ref[...] = middle
    scale = lax.rsqrt(jnp.mean(middle * middle, axis=-1, keepdims=True) + norm_eps)
    low_ref[...] = (middle * scale * gain_ref[...]).astype(bf16)


def post_call(mix, wo, x, gain):
    rows, features = x.shape
    return pl.pallas_call(
        post_kernel,
        out_shape=[
            jax.ShapeDtypeStruct((rows, wo.shape[0]), bf16),
            jax.ShapeDtypeStruct((rows, features), f32),
            jax.ShapeDtypeStruct((rows, features), bf16),
        ],
        compiler_params=params(32),
        cost_estimate=cost(2 * rows * wo.size, 5e6),
        name="project_norm",
    )(mix, wo, x, gain)


def expert_kernel(place_ref, a_ref, b_ref, cot_ref, w_ref, wg_ref, wu_ref, wd_ref, *refs):
    dx_ref, x_ref, ha_ref, hb_ref, dg_ref, du_ref, sa_ref, sb_ref = refs[-8:]
    step = pl.program_id(0)
    first, second = place_ref[2], place_ref[3]
    half = sa_ref.shape[2]

    @pl.when(step == 0)
    def _():
        x_ref[...] = a_ref[...]

    @pl.when(step == 1)
    def _():
        x_ref[...] = b_ref[...]

    x = x_ref[...]
    cot = cot_ref[0].astype(f32)
    weight = residual_scale * w_ref[...]
    total = None
    for e in range(wg_ref.shape[0]):
        gate = dot(x, wg_ref[e])
        up = dot(x, wu_ref[e])
        slot_grad = (weight[:, e : e + 1] * cot).astype(bf16)
        to_a, to_b = jnp.bitwise_xor(first, e), jnp.bitwise_xor(second, e)
        sa_ref[to_a] = slot_grad[:, :half]
        sb_ref[to_b] = slot_grad[:, half:]
        hidden_grad = dot_nt(slot_grad, wd_ref[e])
        sig = 0.5 * jnp.tanh(0.5 * gate) + 0.5
        silu = gate * sig
        hidden = (silu * up).astype(bf16)
        ha_ref[to_a] = hidden
        hb_ref[to_b] = hidden
        gate_grad = (hidden_grad * up * (sig + silu * (1.0 - sig))).astype(bf16)
        up_grad = (hidden_grad * silu).astype(bf16)
        dg_ref[to_a] = gate_grad
        du_ref[to_b] = up_grad
        term = dot_nt(gate_grad, wg_ref[e]) + dot_nt(up_grad, wu_ref[e])
        total = term if total is None else total + term
    dx_ref[0] = total.astype(bf16)


def expert_call(at, place, own, other, cot_all, weight, wg, wu, wd, kept):
    blocks, rows, features = cot_all.shape
    count, _, hidden = wg.shape
    tokens = blocks * rows
    inner = jax.ShapeDtypeStruct((count, tokens, hidden), bf16)
    outer = jax.ShapeDtypeStruct((count, tokens, features // 2), bf16)
    inner_spec = pl.BlockSpec((count, rows, hidden), lambda s, place: (0, 2 * at + s, 0))
    outer_spec = pl.BlockSpec((count, rows, features // 2), lambda s, place: (0, 2 * at + s, 0))
    fixed = lambda shape: pl.BlockSpec(shape, lambda s, place: (0,) * len(shape))
    any_spec = pl.BlockSpec(memory_space=pl.ANY)
    first = 8
    return pl.pallas_call(
        expert_kernel,
        grid_spec=pltpu.PrefetchScalarGridSpec(
            num_scalar_prefetch=1,
            grid=(2,),
            in_specs=[
                fixed((rows, features)),
                fixed((rows, features)),
                pl.BlockSpec((1, rows, features), lambda s, place: (place[s], 0, 0)),
                pl.BlockSpec((rows, count), lambda s, place: (place[s], 0)),
                fixed(wg.shape),
                fixed(wu.shape),
                fixed(wd.shape),
            ]
            + [any_spec] * len(kept),
            out_specs=[
                pl.BlockSpec((1, rows, features), lambda s, place: (s, 0, 0)),
                pl.BlockSpec((rows, features), lambda s, place: (2 * at + s, 0)),
            ]
            + [inner_spec] * 4
            + [outer_spec] * 2,
        ),
        out_shape=[
            jax.ShapeDtypeStruct((2, rows, features), bf16),
            jax.ShapeDtypeStruct((tokens, features), bf16),
            inner,
            inner,
            inner,
            inner,
            outer,
            outer,
        ],
        input_output_aliases={first + i: 1 + i for i in range(len(kept))},
        compiler_params=params(48, "arbitrary"),
        cost_estimate=cost(20 * rows * wg.size, 2e7, 2 * rows * hidden * count),
        name="experts",
    )(place, own, other, cot_all, weight, wg, wu, wd, *kept)


def part_sum_kernel(at_ref, *refs):
    inputs, outs = refs[:16], refs[16:]
    at = 0
    for out in outs:
        gate_came, gate_here, down_came, down_here = inputs[at : at + 4]
        rows = gate_came.shape[0]
        out[0, :rows] = (gate_came[...].astype(f32) + gate_here[...].astype(f32)).astype(bf16)
        out[0, rows:] = (down_came[...].astype(f32) + down_here[...].astype(f32)).astype(bf16)
        at += 4


def part_sum_call(at, per, came, here):
    gate_rows, down_rows = came[0].shape[0] // per, came[2].shape[0] // per
    width = came[0].shape[1]
    steps = per // 2
    specs, args, out_specs, out_shapes = [], [], [], []
    for stream in range(2):
        for sent in range(2):
            for which, rows in ((stream, gate_rows), (stream + 2, down_rows)):
                spec = pl.BlockSpec(
                    (rows, width),
                    lambda s, at, sent=sent, stream=stream: (
                        jnp.bitwise_xor(s + sent * steps, at[stream]),
                        0,
                    ),
                )
                specs += [spec, spec]
                args += [came[which], here[which]]
            out_specs.append(
                pl.BlockSpec((1, gate_rows + down_rows, width), lambda s, at: (s, 0, 0))
            )
            out_shapes.append(
                jax.ShapeDtypeStruct((steps, gate_rows + down_rows, width), bf16)
            )
    return pl.pallas_call(
        part_sum_kernel,
        grid_spec=pltpu.PrefetchScalarGridSpec(
            num_scalar_prefetch=1, grid=(steps,), in_specs=specs, out_specs=out_specs
        ),
        out_shape=out_shapes,
        compiler_params=params(60, "arbitrary"),
        cost_estimate=cost(0, 9e6),
        name="expert_part_sum",
    )(at, *args)


def joint_kernel(at_ref, *refs):
    for (part_ref, wo_ref, gain_ref), out_ref in ((refs[:3], refs[6]), (refs[3:6], refs[7])):
        rows = part_ref.shape[0]
        upto = rows + wo_ref.shape[0]
        out_ref[0, 0, :rows] = part_ref[...].astype(bf16)
        out_ref[0, 0, rows:upto] = wo_ref[...]
        out_ref[0, 0, upto:] = gain_ref[...]


def joint_call(at, part, dense, parts):
    features, width = part.shape
    pieces = 2 * parts
    rows = features // pieces
    block_cols = dense.shape[1] // width
    per_block = pieces // block_cols
    extra = 16
    wo_rows = (dense.shape[0] - extra) // per_block
    last = dense.shape[0] // extra - 1
    steps = parts // 2

    def piece(sent):
        return lambda s, p, at: s * parts + jnp.bitwise_xor(p + sent * steps, at[s])

    specs = []
    for sent in range(2):
        at_piece = piece(sent)
        specs.append(
            pl.BlockSpec((rows, width), lambda s, p, at, f=at_piece: (f(s, p, at), 0))
        )
        specs.append(
            pl.BlockSpec(
                (wo_rows, width),
                lambda s, p, at, f=at_piece: (
                    lax.rem(f(s, p, at), per_block),
                    lax.div(f(s, p, at), per_block),
                ),
            )
        )
        specs.append(
            pl.BlockSpec(
                (extra, width), lambda s, p, at, f=at_piece: (last, lax.div(f(s, p, at), per_block))
            )
        )
    out_spec = pl.BlockSpec((1, 1, rows + wo_rows + extra, width), lambda s, p, at: (s, p, 0, 0))
    out_shape = jax.ShapeDtypeStruct((2, steps, rows + wo_rows + extra, width), bf16)
    return pl.pallas_call(
        joint_kernel,
        grid_spec=pltpu.PrefetchScalarGridSpec(
            num_scalar_prefetch=1, grid=(2, steps), in_specs=specs, out_specs=[out_spec] * 2
        ),
        out_shape=[out_shape] * 2,
        compiler_params=params(32, "arbitrary", "arbitrary"),
        cost_estimate=cost(0, 2e6),
        name="dense_pieces",
    )(at, part, dense, dense, part, dense, dense)


def expert_out_kernel(at_ref, *refs):
    pieces, (gate_ref, up_ref, down_ref) = refs[:-3], refs[-3:]
    parts = len(pieces) // 2
    step = pl.program_id(0)
    rows = gate_ref.shape[1]
    half = down_ref.shape[2] // 2
    for which in range(parts):

        @pl.when(jnp.bitwise_xor(step, at_ref[0]) == which)
        def _():
            a_ref = pieces[which]
            gate_ref[0] = a_ref[:rows].astype(f32)
            down_ref[0, :, :half] = a_ref[rows:].astype(f32)

        @pl.when(jnp.bitwise_xor(step, at_ref[1]) == which)
        def _():
            b_ref = pieces[parts + which]
            up_ref[0] = b_ref[:rows].astype(f32)
            down_ref[0, :, half:] = b_ref[rows:].astype(f32)


def expert_out_call(at, a, b, gate_shape, down_shape):
    parts = len(a)
    held, width = a[0].shape
    count = gate_shape[0]
    per = parts // count
    gate_rows, down_rows = gate_shape[1] // per, down_shape[1] // per
    place = lambda r, at: (lax.div(r, per), lax.rem(r, per), 0)
    return pl.pallas_call(
        expert_out_kernel,
        grid_spec=pltpu.PrefetchScalarGridSpec(
            num_scalar_prefetch=1,
            grid=(parts,),
            in_specs=[pl.BlockSpec((held, width), lambda r, at: (0, 0))] * (2 * parts),
            out_specs=[
                pl.BlockSpec((1, gate_rows, gate_shape[2]), place),
                pl.BlockSpec((1, gate_rows, gate_shape[2]), place),
                pl.BlockSpec((1, down_rows, down_shape[2]), place),
            ],
        ),
        out_shape=[
            jax.ShapeDtypeStruct(gate_shape, f32),
            jax.ShapeDtypeStruct(gate_shape, f32),
            jax.ShapeDtypeStruct(down_shape, f32),
        ],
        compiler_params=params(40, "arbitrary"),
        cost_estimate=cost(0, 2e7),
        name="expert_weights_out",
    )(at, *a, *b)


def moe_kernel(place_ref, h_ref, w_ref, wd_ref, out_ref):
    weight = w_ref[...]
    total = None
    first = place_ref[pl.num_programs(0)]
    for e in range(wd_ref.shape[0]):
        term = weight[:, e : e + 1] * dot(h_ref[jnp.bitwise_xor(first, e)], wd_ref[e])
        total = term if total is None else total + term
    out_ref[0] = total.astype(bf16)


def moe_call(place, hidden, weight, wd, blocks):
    count, tokens, inner = hidden.shape
    features = wd.shape[2]
    rows = tokens // blocks
    return pl.pallas_call(
        moe_kernel,
        grid_spec=pltpu.PrefetchScalarGridSpec(
            num_scalar_prefetch=1,
            grid=(blocks,),
            in_specs=[
                pl.BlockSpec((count, rows, inner), lambda s, place: (0, s, 0)),
                pl.BlockSpec((rows, count), lambda s, place: (place[s], 0)),
                pl.BlockSpec(wd.shape, lambda s, place: (0, 0, 0)),
            ],
            out_specs=pl.BlockSpec((1, rows, features), lambda s, place: (place[s], 0, 0)),
        ),
        out_shape=jax.ShapeDtypeStruct((blocks, rows, features), bf16),
        compiler_params=params(60, "arbitrary"),
        cost_estimate=cost(2 * tokens * wd.size, 1.1e7),
        name="expert_outputs",
    )(place, hidden, weight, wd)


def turn_kernel(sg_ref, middle_ref, gain_ref, cot_ref, wo_ref, mg_ref, proj_ref, dmid_ref, dgain_ref):
    grad = sg_ref[...].astype(f32)
    middle = middle_ref[...]
    scale = lax.rsqrt(jnp.mean(middle * middle, axis=-1, keepdims=True) + norm_eps)
    unit = middle * scale
    dgain_ref[...] = jnp.sum(grad * unit, axis=0, keepdims=True)
    w = gain_ref[...] * grad
    dmid = cot_ref[...].astype(f32) + scale * (w - unit * jnp.mean(w * unit, axis=-1, keepdims=True))
    dmid_ref[...] = dmid
    proj = (residual_scale * dmid).astype(bf16)
    proj_ref[...] = proj
    mixed_grad = dot_nt(proj, wo_ref[...]).astype(bf16)
    groups, _, pair = mg_ref.shape
    for g in range(groups):
        mg_ref[g] = mixed_grad[:, g * pair : (g + 1) * pair]


def turn_call(sg, middle, gain, cot, wo, groups):
    rows, features = middle.shape
    pair = wo.shape[0] // groups
    return pl.pallas_call(
        turn_kernel,
        out_shape=[
            jax.ShapeDtypeStruct((groups, rows, pair), bf16),
            jax.ShapeDtypeStruct((rows, features), bf16),
            jax.ShapeDtypeStruct((rows, features), f32),
            jax.ShapeDtypeStruct((1, features), f32),
        ],
        compiler_params=params(32),
        cost_estimate=cost(2 * rows * wo.size, 6e6),
        name="norm_back_project_back",
    )(sg, middle, gain, cot, wo)


def output_weight_kernel(mixed_ref, proj_ref, dgain_ref, out_ref):
    held, each, features = out_ref.shape
    rows = mixed_ref.shape[1] // held
    part = lax.dot_general(mixed_ref[...], proj_ref[...], TN, preferred_element_type=f32)
    extra = jnp.broadcast_to(dgain_ref[...], (each - rows, features)).astype(bf16)
    for at in range(held):
        out_ref[at, :rows] = part[at * rows : (at + 1) * rows].astype(bf16)
        out_ref[at, rows:] = extra


def output_weight_call(mixed, proj, dgain, parts):
    rows, width = mixed.shape
    features = proj.shape[1]
    each = width // parts
    lanes = max(each, width // 2)
    held = lanes // each
    return pl.pallas_call(
        output_weight_kernel,
        grid=(parts // held,),
        in_specs=[
            pl.BlockSpec((rows, lanes), lambda s: (0, s)),
            whole((rows, features)),
            whole((1, features)),
        ],
        out_specs=pl.BlockSpec((held, each + 16, features), lambda s: (s, 0, 0)),
        out_shape=jax.ShapeDtypeStruct((parts, each + 16, features), bf16),
        compiler_params=params(32, "arbitrary"),
        cost_estimate=cost(2 * rows * width * features, 4e6),
        name="output_weight_part",
    )(mixed, proj, dgain)


def dense_out_kernel(at_ref, *refs):
    held, refs = refs[:-13], refs[-13:]
    wq_ref, wk_ref, wv_ref, gain_ref, dq_ref, dk_ref, dv_ref, dg_ref, wo_ref, dg2_ref = refs[:10]
    own_ref, other_ref = refs[10:12]
    parts = len(held) // 4
    stream, step = pl.program_id(0), pl.program_id(1)
    chips, _, width = own_ref.shape
    rows = dq_ref.shape[0]
    pair = width // 2
    chip, core = at_ref[2], at_ref[3]
    for which in range(2):
        for rel in range(parts):

            @pl.when((stream == which) & (jnp.bitwise_xor(step, at_ref[which]) == rel))
            def _():
                own_ref[...] = held[which * parts + rel][...]
                other_ref[...] = held[(2 + which) * parts + rel][...]

    total = jnp.zeros((rows, pair), f32)
    for k in range(chips):
        source = lax.rem(chip - k + chips, chips)
        a = jnp.where(core == 0, own_ref[k], other_ref[k]).astype(f32)
        b = jnp.where(core == 0, other_ref[k], own_ref[k]).astype(f32)
        q = jnp.concatenate([a[:rows, :pair], b[:rows, :pair]], axis=1)
        cols = pl.ds(pl.multiple_of(source * width, width), width)
        dq_ref[:, cols] = q
        made = q * wq_ref[:, cols].astype(f32)
        total += made[:, :pair] + made[:, pair:]
        a_kv, b_kv = a[:rows, pair:], b[:rows, pair:]
        lane = lax.broadcasted_iota(jnp.int32, a_kv.shape, 1)
        key = jnp.where(lane < HEAD_DIM, a_kv, pltpu.roll(b_kv, HEAD_DIM, 1))
        val = jnp.where(lane < HEAD_DIM, pltpu.roll(a_kv, HEAD_DIM, 1), b_kv)
        cols = pl.ds(pl.multiple_of(source * pair, pair), pair)
        dk_ref[:, cols] = key
        dv_ref[:, cols] = val
        total += key * wk_ref[:, cols].astype(f32) + val * wv_ref[:, cols].astype(f32)
        wo_ref[2 * source, 0] = a[rows : rows + wo_ref.shape[2]]
        wo_ref[2 * source + 1, 0] = b[rows : rows + wo_ref.shape[2]]
        if k == 0:
            dg2_ref[...] = a[rows + wo_ref.shape[2] :][:1]
    dg_ref[...] = jnp.sum(jnp.transpose(total), axis=0, keepdims=True) / gain_ref[...]


def dense_out_call(at, own, other, wq, wk, wv, gain, wo_shape):
    held = [*own[0], *own[1], *other[0], *other[1]]
    streams, parts = 2, len(own[0])
    chips, depth, width = held[0].shape
    features = wq.shape[0]
    groups = 2 * chips
    rows = features // (streams * parts)
    block_cols = wo_shape[1] // width
    per_block = streams * parts // block_cols
    wo_rows = wo_shape[0] // groups // per_block
    by_rows = lambda w: pl.BlockSpec((rows, w.shape[1]), lambda s, r, at: (s * parts + r, 0))
    gain_spec = pl.BlockSpec((1, rows), lambda s, r, at: (0, s * parts + r))
    outs = pl.pallas_call(
        dense_out_kernel,
        grid_spec=pltpu.PrefetchScalarGridSpec(
            num_scalar_prefetch=1,
            grid=(streams, parts),
            in_specs=[pl.BlockSpec(memory_space=pltpu.VMEM)] * len(held)
            + [by_rows(wq), by_rows(wk), by_rows(wv), gain_spec],
            out_specs=[
                by_rows(wq),
                by_rows(wk),
                by_rows(wv),
                gain_spec,
                pl.BlockSpec(
                    (groups, 1, wo_rows, width),
                    lambda s, r, at: (
                        0,
                        lax.rem(s * parts + r, per_block),
                        0,
                        lax.div(s * parts + r, per_block),
                    ),
                ),
                pl.BlockSpec((1, width), lambda s, r, at: (0, lax.div(s * parts + r, per_block))),
            ],
            scratch_shapes=[pltpu.VMEM((chips, depth, width), bf16)] * 2
            + [pltpu.VMEM((8, 128), f32)],
        ),
        out_shape=[
            jax.ShapeDtypeStruct(wq.shape, f32),
            jax.ShapeDtypeStruct(wk.shape, f32),
            jax.ShapeDtypeStruct(wv.shape, f32),
            jax.ShapeDtypeStruct((1, features), f32),
            jax.ShapeDtypeStruct((groups, per_block, wo_rows, wo_shape[1]), f32),
            jax.ShapeDtypeStruct((1, wo_shape[1]), f32),
        ],
        compiler_params=params(28, "arbitrary", "arbitrary"),
        cost_estimate=cost(2 * wq.size, 2.4e7),
        name="dense_weights_out",
    )(at, *held, wq, wk, wv, gain)
    return (*outs[:4], outs[4].reshape(wo_shape), outs[5])


def weights_out_kernel(wide_ref, wq_ref, wk_ref, wv_ref, gain_ref, dq_ref, dk_ref, dv_ref, dg_ref):
    groups, rows, width = wide_ref.shape
    pair = width // 2
    total = jnp.zeros((rows, pair), f32)
    for g in range(groups):
        part = wide_ref[g, :, :pair].astype(f32)
        at = slice(g * pair, (g + 1) * pair)
        dq_ref[:, at] = part
        total += part * wq_ref[:, at].astype(f32)
    for g in range(groups // 2):
        a = wide_ref[2 * g, :, pair:].astype(f32)
        b = wide_ref[2 * g + 1, :, pair:].astype(f32)
        lane = lax.broadcasted_iota(jnp.int32, a.shape, 1)
        at = slice(g * pair, (g + 1) * pair)
        k = jnp.where(lane < HEAD_DIM, a, pltpu.roll(b, HEAD_DIM, 1))
        v = jnp.where(lane < HEAD_DIM, pltpu.roll(a, HEAD_DIM, 1), b)
        dk_ref[:, at] = k
        dv_ref[:, at] = v
        total += k * wk_ref[:, at].astype(f32) + v * wv_ref[:, at].astype(f32)
    dg_ref[...] = jnp.sum(jnp.transpose(total), axis=0, keepdims=True) / gain_ref[...]


def weights_out_call(wide, wq, wk, wv, gain):
    chunks, groups, rows, width = wide.shape
    features = chunks * rows
    by_rows = lambda w: pl.BlockSpec((rows, w.shape[1]), lambda c: (c, 0))
    return pl.pallas_call(
        weights_out_kernel,
        grid=(chunks,),
        in_specs=[
            pl.BlockSpec((None, groups, rows, width), lambda c: (c, 0, 0, 0)),
            by_rows(wq),
            by_rows(wk),
            by_rows(wv),
            pl.BlockSpec((1, rows), lambda c: (0, c)),
        ],
        out_specs=[
            by_rows(wq),
            by_rows(wk),
            by_rows(wv),
            pl.BlockSpec((1, rows), lambda c: (0, c)),
        ],
        out_shape=[
            jax.ShapeDtypeStruct(wq.shape, f32),
            jax.ShapeDtypeStruct(wk.shape, f32),
            jax.ShapeDtypeStruct(wv.shape, f32),
            jax.ShapeDtypeStruct((1, features), f32),
        ],
        compiler_params=params(32, "arbitrary"),
        cost_estimate=cost(2 * wq.size, 1.6e7),
        name="attention_weights_out",
    )(wide, wq, wk, wv, gain)


def last_kernel(d_ref, wq_ref, wk_ref, wv_ref, x_ref, gain_ref, dmid_ref, out_ref):
    groups, rows, width = d_ref.shape
    pair = width // 2
    dq = jnp.concatenate([d_ref[g, :, :pair] for g in range(groups)], axis=1)
    grad = dot_nt(dq, wq_ref[...])
    keys, vals = [], []
    for at in range(groups // 2):
        a = d_ref[2 * at, :, pair:].astype(f32)
        b = d_ref[2 * at + 1, :, pair:].astype(f32)
        lane = lax.broadcasted_iota(jnp.int32, a.shape, 1)
        keys.append(jnp.where(lane < HEAD_DIM, a, pltpu.roll(b, HEAD_DIM, 1)).astype(bf16))
        vals.append(jnp.where(lane < HEAD_DIM, pltpu.roll(a, HEAD_DIM, 1), b).astype(bf16))
    grad = grad + dot_nt(jnp.concatenate(keys, axis=1), wk_ref[...])
    grad = grad + dot_nt(jnp.concatenate(vals, axis=1), wv_ref[...])
    x = x_ref[...].astype(f32)
    scale = lax.rsqrt(jnp.mean(x * x, axis=-1, keepdims=True) + norm_eps)
    unit = x * scale
    w = gain_ref[...] * grad
    out_ref[...] = dmid_ref[...] + scale * (w - unit * jnp.mean(w * unit, axis=-1, keepdims=True))


def last_call(d, wq, wk, wv, x, gain, dmid):
    rows, features = x.shape
    return pl.pallas_call(
        last_kernel,
        out_shape=jax.ShapeDtypeStruct((rows, features), f32),
        compiler_params=params(40),
        cost_estimate=cost(4 * rows * features * features, 8e6),
        name="input_gradient",
    )(d, wq, wk, wv, x, gain, dmid)


def swap(values, axis, bit):
    return lax.ppermute(values, axis, [(i, i ^ bit) for i in range(lax.axis_size(axis))])


def half_sum(values, axis, bit):
    half = values.shape[0] // 2
    upper = ((lax.axis_index(axis) & bit) > 0).astype(jnp.int32)
    came = swap(lax.dynamic_slice_in_dim(values, (1 - upper) * half, half), axis, bit)
    mine = lax.dynamic_slice_in_dim(values, upper * half, half)
    return (mine.astype(f32) + came.astype(f32)).astype(bf16)


def relative_sum(kept, sent, axis, bits):
    while True:
        kept = (kept.astype(f32) + swap(sent, axis, bits[0]).astype(f32)).astype(bf16)
        bits = bits[1:]
        if not bits:
            return kept
        half = kept.shape[0] // 2
        kept, sent = kept[:half], kept[half:]


def join_parts(stream, axis, bits):
    shape = stream.shape
    for bit in bits[::-1]:
        stream = jnp.stack([stream, swap(stream, axis, bit)])
    return stream.reshape(-1, *shape)


def body(
    layer_input,
    first_gain,
    query_weight,
    key_weight,
    value_weight,
    output_weight,
    second_gain,
    gate_weight,
    up_weight,
    down_weight,
    expert_ids,
    gate_values,
    positions,
    cotangent,
):
    micro, _, per_device, features = layer_input.shape
    devices = lax.axis_size("seq")
    replicas = lax.axis_size("dp")
    seq_place = lax.axis_index("seq")
    rows = micro * per_device
    local_experts = gate_weight.shape[0]
    groups = key_weight.shape[1] // HEAD_DIM
    pair = query_weight.shape[1] // groups
    copies = devices // groups

    dp_bits = [1 << i for i in range(replicas.bit_length() - 1)]

    def spread(blocks):
        if copies > 1:
            blocks = jnp.repeat(blocks, copies, axis=0)
        return lax.all_to_all(blocks, "seq", 0, 0, tiled=True)

    def unspread(blocks):
        return lax.all_to_all(blocks, "seq", 0, 0, tiled=True)[::copies]

    x = layer_input.reshape(rows, features)
    cot = cotangent.reshape(rows, features)
    gain_one = first_gain.reshape(1, features)
    gain_two = second_gain.reshape(1, features)
    pos_all = lax.all_to_all(
        jnp.broadcast_to(positions.reshape(1, rows), (devices, rows)), "seq", 0, 0, tiled=True
    )
    x_all = lax.all_gather(x, "seq", axis=0)
    cos_all, sin_all = rope_tables(pos_all.reshape(-1), pair)
    mine = seq_place * local_experts + jnp.arange(local_experts, dtype=jnp.int32)
    ids = expert_ids[:, 0]
    gates = gate_values[:, 0].astype(f32)
    routed = jnp.sum(
        jnp.where(ids[..., None] == mine, gates[..., None], 0.0), axis=2
    )
    routed = routed.reshape(micro, devices, per_device, local_experts)
    routed = jnp.transpose(routed, (1, 0, 2, 3)).reshape(devices * rows, local_experts)
    group = seq_place // copies
    w_own = jnp.concatenate(
        [
            lax.dynamic_slice_in_dim(query_weight, group * pair, pair, axis=1),
            lax.dynamic_slice_in_dim(key_weight, group * HEAD_DIM, HEAD_DIM, axis=1),
            lax.dynamic_slice_in_dim(value_weight, group * HEAD_DIM, HEAD_DIM, axis=1),
        ],
        axis=1,
    )
    cos_all, sin_all, routed, w_own = lax.optimization_barrier((cos_all, sin_all, routed, w_own))
    x_all, cot_then, cos_all, sin_all, routed, w_own = lax.optimization_barrier(
        (x_all, cot, cos_all, sin_all, routed, w_own)
    )
    cot_all = lax.all_gather(cot_then, "seq", axis=0)

    qkv, first_all = qkv_call(x_all, gain_one, cos_all, sin_all, w_own)
    qkv = qkv.reshape(devices, micro, per_device, 2 * pair)
    mix, log_total = attend_call(qkv)
    mix = unspread(mix.reshape(devices, rows, pair))
    mixed, middle, second_low = post_call(mix, output_weight, x, gain_two)

    chips = devices // 2
    chip, core = seq_place // 2, seq_place % 2
    onward = [(i, (i + 2) % devices) for i in range(devices)]
    dp_place = lax.axis_index("dp")
    first_bit = dp_place & 1
    last_bit = dp_place >> (len(dp_bits) - 1)
    held, kept, running, places = second_low, (), None, []
    for hop in range(chips):
        following = lax.ppermute(held, "seq", onward) if hop < chips - 1 else None
        other = swap(held, "seq", 1)
        source = 2 * ((chip - hop) % chips)
        place = jnp.stack([source + core, source + 1 - core, 1 - first_bit, 1 - last_bit])
        place = place.astype(jnp.int32)
        places.append(place[:2])
        dx, *kept = expert_call(
            hop, place, held, other, cot_all, routed, gate_weight, up_weight, down_weight, kept
        )
        if following is not None:
            following, dx = lax.optimization_barrier((following, dx))
        part = dx[0].astype(f32) + swap(dx[1], "seq", 1).astype(f32)
        if hop == 0:
            own_part = part
        else:
            if running is not None:
                part = part + running.astype(f32)
            part = part.astype(bf16)
            if following is not None:
                part, following = lax.optimization_barrier((part, following))
            else:
                part, kept = lax.optimization_barrier((part, kept))
            running = lax.ppermute(part, "seq", onward)
        held = following
    second_grad = (own_part + running.astype(f32)).astype(bf16)
    tokens, hidden_a, hidden_b, gate_low, up_low, slot_a, slot_b = kept

    def weight_parts(at, tokens, hidden_a, hidden_b, gate_low, up_low, slot_a, slot_b):
        pairs = (
            (tokens, gate_low[at]),
            (tokens, up_low[at]),
            (hidden_a[at], slot_a[at]),
            (hidden_b[at], slot_b[at]),
        )
        return [
            lax.dot_general(a, b, TN, preferred_element_type=f32).astype(bf16) for a, b in pairs
        ]

    leaving = weight_parts(0, *kept)
    part_bits = (dp_bits[0], dp_bits[-1], dp_bits[0], dp_bits[-1])
    stream_bits = (dp_bits, dp_bits[::-1])
    came = [swap(values, "dp", bit) for values, bit in zip(leaving, part_bits)]
    leaving, second_grad = lax.optimization_barrier((leaving, second_grad))

    mg_send, proj, middle_grad, gain_two_part = turn_call(
        second_grad, middle, gain_two, cot, output_weight, groups
    )
    mg = spread(mg_send)
    kept, _ = lax.optimization_barrier((kept, mg_send))
    mixed, proj, came[2:] = lax.optimization_barrier((mixed, proj, came[2:]))
    dense = output_weight_call(mixed, proj, gain_two_part, devices)
    dense_own = dense
    staying = weight_parts(1, *kept)
    turned = sum(((dp_place >> i) & 1) << (len(dp_bits) - 1 - i) for i in range(len(dp_bits)))
    part_at = jnp.stack([turned, dp_place]).astype(jnp.int32)
    low_at = jnp.bitwise_and(part_at, replicas // 2 - 1)
    keep_a, send_a, keep_b, send_b = part_sum_call(low_at, replicas // 2, came, staying)
    mg, keep_a, send_a, keep_b, send_b = lax.optimization_barrier(
        (mg, keep_a, send_a, keep_b, send_b)
    )
    streams = [
        relative_sum(keep_a, send_a, "dp", stream_bits[0][1:]),
        relative_sum(keep_b, send_b, "dp", stream_bits[1][1:]),
    ]
    dense = dense_own
    dense = lax.psum_scatter(dense, "seq", scatter_dimension=0)
    table_shape = (devices, micro, per_device, pair)
    dqkv = attend_back_call(
        qkv,
        mg.reshape(devices, micro, per_device, pair),
        log_total,
        cos_all.reshape(table_shape),
        sin_all.reshape(table_shape),
    )
    dqkv, streams = lax.optimization_barrier((dqkv, streams))
    near = [
        [v[0], swap(v[0], "dp", bits[-1])] for v, bits in zip(streams, stream_bits)
    ]
    back = unspread(dqkv.reshape(devices, rows, 2 * pair))
    d_all = dqkv.reshape(devices * rows, 2 * pair)
    first_tokens = first_all.reshape(devices * rows, features)
    part = lax.dot_general(first_tokens, d_all, TN, preferred_element_type=f32)
    dense = dense.reshape(dense.shape[-2], features)
    each = output_weight.shape[0] // devices
    if copies == 1:
        width = 2 * pair
        kept_pieces, sent_pieces = joint_call(part_at, part, dense, replicas)
        first = [
            kept_pieces[at].astype(f32) + swap(sent_pieces[at], "dp", bits[0]).astype(f32)
            for at, bits in enumerate(stream_bits)
        ]
        kept, sent_pieces = lax.optimization_barrier((kept, sent_pieces))
        moe_place = jnp.concatenate(places + [(1 - first_bit).astype(jnp.int32).reshape(1)])
        moe_all = moe_call(moe_place, kept[1], routed, down_weight, devices)
        first, near, moe_all = lax.optimization_barrier(
            ([v.astype(bf16) for v in first], near, moe_all)
        )
        own = [
            relative_sum(v[: replicas // 4], v[replicas // 4 :], "dp", bits[1:])
            for v, bits in zip(first, stream_bits)
        ]
        own = jnp.concatenate(own, axis=0)
        own, back, here = lax.optimization_barrier((own, back, [v[0] for v in near]))
        far = [swap(v, "dp", bits[-2]) for v, bits in zip(here, stream_bits)]
        backward = [(i, (i - 2) % devices) for i in range(devices)]
        round_ring = {0: own}
        for k in range(1, chips // 2 + 1):
            round_ring[k] = lax.ppermute(round_ring[k - 1], "seq", onward)
            if chips - k > k:
                round_ring[chips - k] = lax.ppermute(
                    round_ring[(chips - k + 1) % chips], "seq", backward
                )
            if k == 1:
                round_ring, coming = lax.optimization_barrier(
                    (round_ring, [v[1] for v in near])
                )
        held = jnp.stack([round_ring[k] for k in range(chips)])
        passed = [swap(v, "dp", bits[-2]) for v, bits in zip(coming, stream_bits)]
        held, moe_all, far = lax.optimization_barrier((held, moe_all, far))
        moe = lax.psum_scatter(moe_all, "seq", scatter_dimension=0)
        layer_output = (middle + residual_scale * moe.astype(f32)).astype(bf16)
    else:
        far = [swap(v[0], "dp", bits[-2]) for v, bits in zip(streams, stream_bits)]
        passed = [swap(v[1], "dp", bits[-2]) for v, bits in zip(near, stream_bits)]
    expert_pieces = []
    for (here, first), second, third, bits in zip(near, far, passed, stream_bits):
        pieces = [here, first, second, third]
        for bit in bits[:-2][::-1]:
            pieces = pieces + [swap(p, "dp", bit) for p in pieces]
        expert_pieces.append(pieces)
    input_grad = last_call(
        back, query_weight, key_weight, value_weight, x, gain_one, middle_grad
    )
    if copies == 1:
        gate_sum, up_sum, down_sum = expert_out_call(
            part_at, *expert_pieces, gate_weight.shape, down_weight.shape
        )
        full = [[held[:, at], swap(held[:, at], "dp", b[-1])] for at, b in enumerate(stream_bits)]
        beside = [swap(v[0], "dp", bits[-2]) for v, bits in zip(full, stream_bits)]
        full, beside, gate_sum, up_sum, down_sum, input_grad = lax.optimization_barrier(
            (full, beside, gate_sum, up_sum, down_sum, input_grad)
        )
        for at, bits in enumerate(stream_bits):
            full[at] += [beside[at], swap(full[at][1], "dp", bits[-2])]
            for bit in bits[:-2][::-1]:
                full[at] += [swap(p, "dp", bit) for p in full[at]]
        other = [[swap(p, "seq", 1) for p in pieces] for pieces in full]
        where_at = jnp.stack([turned, dp_place, chip, core]).astype(jnp.int32)
        (
            query_weight_grad,
            key_weight_grad,
            value_weight_grad,
            first_gain_grad,
            output_weight_grad,
            second_gain_grad,
        ) = dense_out_call(
            where_at, full, other, query_weight, key_weight, value_weight, gain_one, output_weight.shape
        )
    else:
        gate_sum, up_sum, down_sum = expert_out_call(
            part_at, *expert_pieces, gate_weight.shape, down_weight.shape
        )
        for bit in dp_bits:
            dense = (dense.astype(f32) + swap(dense, "dp", bit).astype(f32)).astype(bf16)
        dense = lax.all_gather(dense, "seq", axis=0).astype(f32)
        output_weight_grad = dense[:, :each].reshape(output_weight.shape)
        moe_place = jnp.concatenate(places + [(1 - first_bit).astype(jnp.int32).reshape(1)])
        moe_all = moe_call(moe_place, kept[1], routed, down_weight, devices)
        moe = lax.psum_scatter(moe_all, "seq", scatter_dimension=0)
        layer_output = (middle + residual_scale * moe.astype(f32)).astype(bf16)
        second_gain_grad = dense[0, each]
        part = part.astype(bf16)
        for bit in dp_bits[::-1]:
            part = half_sum(part, "dp", bit)
        wide = lax.all_gather(part, ("dp", "seq"), axis=0)
        wide = wide.reshape(replicas, devices, features // replicas, 2 * pair)[:, ::copies]
        query_weight_grad, key_weight_grad, value_weight_grad, first_gain_grad = weights_out_call(
            wide, query_weight, key_weight, value_weight, gain_one
        )
    second_gain_grad = second_gain_grad.reshape(features)
    return (
        layer_output.reshape(layer_input.shape),
        input_grad.reshape(layer_input.shape),
        first_gain_grad.reshape(features),
        query_weight_grad,
        key_weight_grad,
        value_weight_grad,
        output_weight_grad,
        second_gain_grad,
        gate_sum,
        up_sum,
        down_sum,
    )


def solution(mesh):
    return jax.shard_map(
        body,
        mesh=mesh,
        in_specs=(
            P(None, "dp", "seq", None),
            P(),
            P(),
            P(),
            P(),
            P(),
            P(),
            P("seq", None, None),
            P("seq", None, None),
            P("seq", None, None),
            P(None, "dp", None, None),
            P(None, "dp", None, None),
            P(None, "dp", "seq"),
            P(None, "dp", "seq", None),
        ),
        out_specs=(
            P(None, "dp", "seq", None),
            P(None, "dp", "seq", None),
            P(),
            P(),
            P(),
            P(),
            P(),
            P(),
            P("seq", None, None),
            P("seq", None, None),
            P("seq", None, None),
        ),
        check_vma=False,
    )
```

```python
from functools import partial

import jax
import jax.numpy as jnp
from jax import lax
from jax.experimental import pallas as pl
from jax.experimental.pallas import tpu as pltpu
from jax.sharding import PartitionSpec as P

HEAD_DIM = 64

rope_theta = 10000.0
attention_scale = 0.015625
residual_scale = 0.22
norm_eps = 1e-06
masked_score = -1e30

f32 = jnp.float32
bf16 = jnp.bfloat16
NT = (((1,), (1,)), ((), ()))
TN = (((0,), (0,)), ((), ()))


def dot(a, b):
    return jnp.dot(a, b, preferred_element_type=f32)


def dot_nt(a, b):
    return lax.dot_general(a, b, NT, preferred_element_type=f32)


def params(mib, *semantics):
    return pltpu.CompilerParams(
        vmem_limit_bytes=mib * 1024 * 1024, dimension_semantics=semantics or None
    )


def cost(flops, nbytes, trans=0):
    return pl.CostEstimate(
        flops=int(flops / 8), bytes_accessed=int(nbytes / 8), transcendentals=int(trans / 8)
    )


def whole(shape):
    return pl.BlockSpec(shape, lambda *_: (0,) * len(shape))


def rope_tables(positions, width):
    half = HEAD_DIM // 2
    exponent = jnp.arange(half, dtype=f32) * (-2.0 / HEAD_DIM)
    angles = positions.astype(f32)[:, None] * (rope_theta**exponent)[None, :]
    cosine, sine = jnp.cos(angles), jnp.sin(angles)
    copies = width // HEAD_DIM
    cos_row = jnp.concatenate([cosine, cosine] * copies, axis=1)
    sin_row = jnp.concatenate([-sine, sine] * copies, axis=1)
    return cos_row, sin_row


def partner(values):
    width = values.shape[1]
    half = HEAD_DIM // 2
    lane = lax.broadcasted_iota(jnp.int32, values.shape, 1)
    ahead = pltpu.roll(values, width - half, 1)
    behind = pltpu.roll(values, half, 1)
    return jnp.where(lane % HEAD_DIM < half, ahead, behind)


def qkv_kernel(x_ref, gain_ref, cos_ref, sin_ref, w_ref, qkv_ref, low_ref):
    pair = 2 * HEAD_DIM
    x = x_ref[0].astype(f32)
    scale = lax.rsqrt(jnp.mean(x * x, axis=-1, keepdims=True) + norm_eps)
    low = (x * scale * gain_ref[...]).astype(bf16)
    low_ref[0] = low
    cosine, sine = cos_ref[...], sin_ref[...]
    made = dot(low, w_ref[...])
    q, kv = made[:, :pair], made[:, pair:]
    q = (q * cosine + partner(q) * sine) * attention_scale
    qkv_ref[0, :, :pair] = q.astype(bf16)
    lane = lax.broadcasted_iota(jnp.int32, kv.shape, 1)
    turned = kv * cosine + partner(kv) * sine
    qkv_ref[0, :, pair:] = jnp.where(lane < HEAD_DIM, turned, kv).astype(bf16)


def qkv_call(x_all, gain, cos_all, sin_all, w_own):
    blocks, rows, features = x_all.shape
    pair = 2 * HEAD_DIM
    return pl.pallas_call(
        qkv_kernel,
        grid=(blocks,),
        in_specs=[
            pl.BlockSpec((1, rows, features), lambda s: (s, 0, 0)),
            whole((1, features)),
            pl.BlockSpec((rows, pair), lambda s: (s, 0)),
            pl.BlockSpec((rows, pair), lambda s: (s, 0)),
            whole(w_own.shape),
        ],
        out_specs=[
            pl.BlockSpec((1, rows, 2 * pair), lambda s: (s, 0, 0)),
            pl.BlockSpec((1, rows, features), lambda s: (s, 0, 0)),
        ],
        out_shape=[
            jax.ShapeDtypeStruct((blocks, rows, 2 * pair), bf16),
            jax.ShapeDtypeStruct((blocks, rows, features), bf16),
        ],
        compiler_params=params(58, "arbitrary"),
        cost_estimate=cost(4 * blocks * rows * features * pair, 14e6),
        name="norm_qkv_rope",
    )(x_all, gain, cos_all, sin_all, w_own)


def split_heads(block, first):
    wide = block.astype(f32)
    lane = lax.broadcasted_iota(jnp.int32, wide.shape, 1)
    turned = pltpu.roll(wide, HEAD_DIM, 1)
    if first:
        parts = [jnp.where(lane < HEAD_DIM, wide, 0.0), jnp.where(lane < HEAD_DIM, turned, 0.0)]
    else:
        parts = [jnp.where(lane >= HEAD_DIM, turned, 0.0), jnp.where(lane >= HEAD_DIM, wide, 0.0)]
    return jnp.concatenate(parts, axis=0).astype(bf16)


def join_heads(turned):
    rows = turned.shape[1] // 2
    return jnp.transpose(jnp.concatenate([turned[:, :rows], turned[:, rows:]], axis=0))


def scores_of(kv, q2, rows):
    scores = dot_nt(kv, q2)
    count = scores.shape[0]
    own = scores[count - rows :]
    key_at = lax.broadcasted_iota(jnp.int32, own.shape, 0)
    query_at = lax.broadcasted_iota(jnp.int32, own.shape, 1) % rows
    own = jnp.where(key_at <= query_at, own, masked_score)
    if count == rows:
        return own
    return jnp.concatenate([scores[: count - rows], own], axis=0)


def attend_kernel(qkv_ref, out_ref, log_ref):
    blocks, _, rows, width = qkv_ref.shape
    pair = width // 2
    kv = qkv_ref[:, 0, :, pair:].reshape(blocks * rows, pair)
    kv_t = jnp.transpose(kv)
    for at in range(blocks):
        count = (at + 1) * rows
        q2 = split_heads(qkv_ref[at, 0, :, :pair], True)
        scores = scores_of(kv[:count], q2, rows)
        top = jnp.max(scores, axis=0, keepdims=True)
        weights = jnp.exp(scores - top)
        total = jnp.sum(weights, axis=0, keepdims=True)
        out_t = dot(kv_t[:, :count], weights.astype(bf16))
        out_ref[at, 0] = join_heads(out_t[HEAD_DIM:] / total).astype(bf16)
        log_ref[at, 0] = top + jnp.log(total)


def attend_call(qkv):
    blocks, micro, rows, width = qkv.shape
    pair = width // 2
    length = blocks * rows
    return pl.pallas_call(
        attend_kernel,
        grid=(micro,),
        in_specs=[pl.BlockSpec((blocks, 1, rows, width), lambda m: (0, m, 0, 0))],
        out_specs=[
            pl.BlockSpec((blocks, 1, rows, pair), lambda m: (0, m, 0, 0)),
            pl.BlockSpec((blocks, 1, 1, 2 * rows), lambda m: (0, m, 0, 0)),
        ],
        out_shape=[
            jax.ShapeDtypeStruct((blocks, micro, rows, pair), bf16),
            jax.ShapeDtypeStruct((blocks, micro, 1, 2 * rows), f32),
        ],
        compiler_params=params(48, "arbitrary"),
        cost_estimate=cost(
            micro * length * length * 512, 3 * qkv.size, micro * length * length
        ),
        name="attention_forward",
    )(qkv)


def attend_back_kernel(qkv_ref, grad_ref, log_ref, cos_ref, sin_ref, out_ref, dkv_ref):
    blocks, _, rows, width = qkv_ref.shape
    pair = width // 2
    kv = qkv_ref[:, 0, :, pair:].reshape(blocks * rows, pair)
    kv_t = jnp.transpose(kv)
    dkv_ref[...] = jnp.zeros_like(dkv_ref)
    for at in range(blocks):
        count = (at + 1) * rows
        q2 = split_heads(qkv_ref[at, 0, :, :pair], True)
        g2 = split_heads(grad_ref[at, 0], False)
        scores = scores_of(kv[:count], q2, rows)
        prob = jnp.exp(scores - log_ref[at, 0])
        prob_grad = dot_nt(kv[:count], g2)
        delta = jnp.sum(prob * prob_grad, axis=0, keepdims=True)
        score_grad = (prob * (prob_grad - delta)).astype(bf16)
        dkv_ref[:count] += dot(score_grad, q2) + dot(prob.astype(bf16), g2)
        dq_t = dot(kv_t[:, :count], score_grad)
        dq = join_heads(dq_t[:HEAD_DIM] * attention_scale)
        dq = dq * cos_ref[at, 0] - partner(dq) * sin_ref[at, 0]
        out_ref[at, 0, :, :pair] = dq.astype(bf16)
    for at in range(blocks):
        dkv = dkv_ref[at * rows : (at + 1) * rows]
        lane = lax.broadcasted_iota(jnp.int32, dkv.shape, 1)
        turned = dkv * cos_ref[at, 0] - partner(dkv) * sin_ref[at, 0]
        out_ref[at, 0, :, pair:] = jnp.where(lane < HEAD_DIM, turned, dkv).astype(bf16)


def attend_back_call(qkv, grads, log_total, cos_all, sin_all):
    blocks, micro, rows, width = qkv.shape
    pair = width // 2
    length = blocks * rows
    spec = lambda lanes: pl.BlockSpec((blocks, 1, rows, lanes), lambda m: (0, m, 0, 0))
    return pl.pallas_call(
        attend_back_kernel,
        grid=(micro,),
        in_specs=[
            spec(width),
            spec(pair),
            pl.BlockSpec((blocks, 1, 1, 2 * rows), lambda m: (0, m, 0, 0)),
            spec(pair),
            spec(pair),
        ],
        out_specs=spec(width),
        out_shape=jax.ShapeDtypeStruct(qkv.shape, bf16),
        scratch_shapes=[pltpu.VMEM((length, pair), f32)],
        compiler_params=params(56, "arbitrary"),
        cost_estimate=cost(
            micro * length * length * 1280, 10 * qkv.size, micro * length * length
        ),
        name="attention_backward",
    )(qkv, grads, log_total, cos_all, sin_all)


def post_kernel(mix_ref, wo_ref, x_ref, gain_ref, mixed_ref, middle_ref, low_ref):
    mixed = jnp.concatenate([mix_ref[g] for g in range(mix_ref.shape[0])], axis=1)
    mixed_ref[...] = mixed
    middle = x_ref[...].astype(f32) + residual_scale * dot(mixed, wo_ref[...])
    middle_ref[...] = middle
    scale = lax.rsqrt(jnp.mean(middle * middle, axis=-1, keepdims=True) + norm_eps)
    low_ref[...] = (middle * scale * gain_ref[...]).astype(bf16)


def post_call(mix, wo, x, gain):
    rows, features = x.shape
    return pl.pallas_call(
        post_kernel,
        out_shape=[
            jax.ShapeDtypeStruct((rows, wo.shape[0]), bf16),
            jax.ShapeDtypeStruct((rows, features), f32),
            jax.ShapeDtypeStruct((rows, features), bf16),
        ],
        compiler_params=params(32),
        cost_estimate=cost(2 * rows * wo.size, 5e6),
        name="project_norm",
    )(mix, wo, x, gain)


def expert_kernel(place_ref, a_ref, b_ref, cot_ref, w_ref, wg_ref, wu_ref, wd_ref, *refs):
    dx_ref, x_ref, ha_ref, hb_ref, dg_ref, du_ref, sa_ref, sb_ref = refs[-8:]
    step = pl.program_id(0)
    first, second = place_ref[2], place_ref[3]
    half = sa_ref.shape[2]

    @pl.when(step == 0)
    def _():
        x_ref[...] = a_ref[...]

    @pl.when(step == 1)
    def _():
        x_ref[...] = b_ref[...]

    x = x_ref[...]
    cot = cot_ref[0].astype(f32)
    weight = residual_scale * w_ref[...]
    total = None
    for e in range(wg_ref.shape[0]):
        gate = dot(x, wg_ref[e])
        up = dot(x, wu_ref[e])
        slot_grad = (weight[:, e : e + 1] * cot).astype(bf16)
        to_a, to_b = jnp.bitwise_xor(first, e), jnp.bitwise_xor(second, e)
        sa_ref[to_a] = slot_grad[:, :half]
        sb_ref[to_b] = slot_grad[:, half:]
        hidden_grad = dot_nt(slot_grad, wd_ref[e])
        sig = 0.5 * jnp.tanh(0.5 * gate) + 0.5
        silu = gate * sig
        hidden = (silu * up).astype(bf16)
        ha_ref[to_a] = hidden
        hb_ref[to_b] = hidden
        gate_grad = (hidden_grad * up * (sig + silu * (1.0 - sig))).astype(bf16)
        up_grad = (hidden_grad * silu).astype(bf16)
        dg_ref[to_a] = gate_grad
        du_ref[to_b] = up_grad
        term = dot_nt(gate_grad, wg_ref[e]) + dot_nt(up_grad, wu_ref[e])
        total = term if total is None else total + term
    dx_ref[0] = total.astype(bf16)


def expert_call(at, place, own, other, cot_all, weight, wg, wu, wd, kept):
    blocks, rows, features = cot_all.shape
    count, _, hidden = wg.shape
    tokens = blocks * rows
    inner = jax.ShapeDtypeStruct((count, tokens, hidden), bf16)
    outer = jax.ShapeDtypeStruct((count, tokens, features // 2), bf16)
    inner_spec = pl.BlockSpec((count, rows, hidden), lambda s, place: (0, 2 * at + s, 0))
    outer_spec = pl.BlockSpec((count, rows, features // 2), lambda s, place: (0, 2 * at + s, 0))
    fixed = lambda shape: pl.BlockSpec(shape, lambda s, place: (0,) * len(shape))
    any_spec = pl.BlockSpec(memory_space=pl.ANY)
    first = 8
    return pl.pallas_call(
        expert_kernel,
        grid_spec=pltpu.PrefetchScalarGridSpec(
            num_scalar_prefetch=1,
            grid=(2,),
            in_specs=[
                fixed((rows, features)),
                fixed((rows, features)),
                pl.BlockSpec((1, rows, features), lambda s, place: (place[s], 0, 0)),
                pl.BlockSpec((rows, count), lambda s, place: (place[s], 0)),
                fixed(wg.shape),
                fixed(wu.shape),
                fixed(wd.shape),
            ]
            + [any_spec] * len(kept),
            out_specs=[
                pl.BlockSpec((1, rows, features), lambda s, place: (s, 0, 0)),
                pl.BlockSpec((rows, features), lambda s, place: (2 * at + s, 0)),
            ]
            + [inner_spec] * 4
            + [outer_spec] * 2,
        ),
        out_shape=[
            jax.ShapeDtypeStruct((2, rows, features), bf16),
            jax.ShapeDtypeStruct((tokens, features), bf16),
            inner,
            inner,
            inner,
            inner,
            outer,
            outer,
        ],
        input_output_aliases={first + i: 1 + i for i in range(len(kept))},
        compiler_params=params(48, "arbitrary"),
        cost_estimate=cost(20 * rows * wg.size, 2e7, 2 * rows * hidden * count),
        name="experts",
    )(place, own, other, cot_all, weight, wg, wu, wd, *kept)


def part_sum_kernel(at_ref, *refs):
    inputs, outs = refs[:16], refs[16:]
    at = 0
    for out in outs:
        gate_came, gate_here, down_came, down_here = inputs[at : at + 4]
        rows = gate_came.shape[0]
        out[0, :rows] = (gate_came[...].astype(f32) + gate_here[...].astype(f32)).astype(bf16)
        out[0, rows:] = (down_came[...].astype(f32) + down_here[...].astype(f32)).astype(bf16)
        at += 4


def part_sum_call(at, per, came, here):
    gate_rows, down_rows = came[0].shape[0] // per, came[2].shape[0] // per
    width = came[0].shape[1]
    steps = per // 2
    specs, args, out_specs, out_shapes = [], [], [], []
    for stream in range(2):
        for sent in range(2):
            for which, rows in ((stream, gate_rows), (stream + 2, down_rows)):
                spec = pl.BlockSpec(
                    (rows, width),
                    lambda s, at, sent=sent, stream=stream: (
                        jnp.bitwise_xor(s + sent * steps, at[stream]),
                        0,
                    ),
                )
                specs += [spec, spec]
                args += [came[which], here[which]]
            out_specs.append(
                pl.BlockSpec((1, gate_rows + down_rows, width), lambda s, at: (s, 0, 0))
            )
            out_shapes.append(
                jax.ShapeDtypeStruct((steps, gate_rows + down_rows, width), bf16)
            )
    return pl.pallas_call(
        part_sum_kernel,
        grid_spec=pltpu.PrefetchScalarGridSpec(
            num_scalar_prefetch=1, grid=(steps,), in_specs=specs, out_specs=out_specs
        ),
        out_shape=out_shapes,
        compiler_params=params(60, "arbitrary"),
        cost_estimate=cost(0, 9e6),
        name="expert_part_sum",
    )(at, *args)


def joint_kernel(at_ref, *refs):
    for (part_ref, wo_ref, gain_ref), out_ref in ((refs[:3], refs[6]), (refs[3:6], refs[7])):
        rows = part_ref.shape[0]
        upto = rows + wo_ref.shape[0]
        out_ref[0, 0, :rows] = part_ref[...].astype(bf16)
        out_ref[0, 0, rows:upto] = wo_ref[...]
        out_ref[0, 0, upto:] = gain_ref[...]


def joint_call(at, part, dense, parts):
    features, width = part.shape
    pieces = 2 * parts
    rows = features // pieces
    block_cols = dense.shape[1] // width
    per_block = pieces // block_cols
    extra = 16
    wo_rows = (dense.shape[0] - extra) // per_block
    last = dense.shape[0] // extra - 1
    steps = parts // 2

    def piece(sent):
        return lambda s, p, at: s * parts + jnp.bitwise_xor(p + sent * steps, at[s])

    specs = []
    for sent in range(2):
        at_piece = piece(sent)
        specs.append(
            pl.BlockSpec((rows, width), lambda s, p, at, f=at_piece: (f(s, p, at), 0))
        )
        specs.append(
            pl.BlockSpec(
                (wo_rows, width),
                lambda s, p, at, f=at_piece: (
                    lax.rem(f(s, p, at), per_block),
                    lax.div(f(s, p, at), per_block),
                ),
            )
        )
        specs.append(
            pl.BlockSpec(
                (extra, width), lambda s, p, at, f=at_piece: (last, lax.div(f(s, p, at), per_block))
            )
        )
    out_spec = pl.BlockSpec((1, 1, rows + wo_rows + extra, width), lambda s, p, at: (s, p, 0, 0))
    out_shape = jax.ShapeDtypeStruct((2, steps, rows + wo_rows + extra, width), bf16)
    return pl.pallas_call(
        joint_kernel,
        grid_spec=pltpu.PrefetchScalarGridSpec(
            num_scalar_prefetch=1, grid=(2, steps), in_specs=specs, out_specs=[out_spec] * 2
        ),
        out_shape=[out_shape] * 2,
        compiler_params=params(32, "arbitrary", "arbitrary"),
        cost_estimate=cost(0, 2e6),
        name="dense_pieces",
    )(at, part, dense, dense, part, dense, dense)


def expert_out_kernel(at_ref, *refs):
    pieces, (gate_ref, up_ref, down_ref) = refs[:-3], refs[-3:]
    parts = len(pieces) // 2
    step = pl.program_id(0)
    rows = gate_ref.shape[1]
    half = down_ref.shape[2] // 2
    for which in range(parts):

        @pl.when(jnp.bitwise_xor(step, at_ref[0]) == which)
        def _():
            a_ref = pieces[which]
            gate_ref[0] = a_ref[:rows].astype(f32)
            down_ref[0, :, :half] = a_ref[rows:].astype(f32)

        @pl.when(jnp.bitwise_xor(step, at_ref[1]) == which)
        def _():
            b_ref = pieces[parts + which]
            up_ref[0] = b_ref[:rows].astype(f32)
            down_ref[0, :, half:] = b_ref[rows:].astype(f32)


def expert_out_call(at, a, b, gate_shape, down_shape):
    parts = len(a)
    held, width = a[0].shape
    count = gate_shape[0]
    per = parts // count
    gate_rows, down_rows = gate_shape[1] // per, down_shape[1] // per
    place = lambda r, at: (lax.div(r, per), lax.rem(r, per), 0)
    return pl.pallas_call(
        expert_out_kernel,
        grid_spec=pltpu.PrefetchScalarGridSpec(
            num_scalar_prefetch=1,
            grid=(parts,),
            in_specs=[pl.BlockSpec((held, width), lambda r, at: (0, 0))] * (2 * parts),
            out_specs=[
                pl.BlockSpec((1, gate_rows, gate_shape[2]), place),
                pl.BlockSpec((1, gate_rows, gate_shape[2]), place),
                pl.BlockSpec((1, down_rows, down_shape[2]), place),
            ],
        ),
        out_shape=[
            jax.ShapeDtypeStruct(gate_shape, f32),
            jax.ShapeDtypeStruct(gate_shape, f32),
            jax.ShapeDtypeStruct(down_shape, f32),
        ],
        compiler_params=params(40, "arbitrary"),
        cost_estimate=cost(0, 2e7),
        name="expert_weights_out",
    )(at, *a, *b)


def moe_kernel(place_ref, h_ref, w_ref, wd_ref, out_ref):
    weight = w_ref[...]
    total = None
    first = place_ref[pl.num_programs(0)]
    for e in range(wd_ref.shape[0]):
        term = weight[:, e : e + 1] * dot(h_ref[jnp.bitwise_xor(first, e)], wd_ref[e])
        total = term if total is None else total + term
    out_ref[0] = total.astype(bf16)


def moe_call(place, hidden, weight, wd, blocks):
    count, tokens, inner = hidden.shape
    features = wd.shape[2]
    rows = tokens // blocks
    return pl.pallas_call(
        moe_kernel,
        grid_spec=pltpu.PrefetchScalarGridSpec(
            num_scalar_prefetch=1,
            grid=(blocks,),
            in_specs=[
                pl.BlockSpec((count, rows, inner), lambda s, place: (0, s, 0)),
                pl.BlockSpec((rows, count), lambda s, place: (place[s], 0)),
                pl.BlockSpec(wd.shape, lambda s, place: (0, 0, 0)),
            ],
            out_specs=pl.BlockSpec((1, rows, features), lambda s, place: (place[s], 0, 0)),
        ),
        out_shape=jax.ShapeDtypeStruct((blocks, rows, features), bf16),
        compiler_params=params(60, "arbitrary"),
        cost_estimate=cost(2 * tokens * wd.size, 1.1e7),
        name="expert_outputs",
    )(place, hidden, weight, wd)


def turn_kernel(sg_ref, middle_ref, gain_ref, cot_ref, wo_ref, mg_ref, proj_ref, dmid_ref, dgain_ref):
    grad = sg_ref[...].astype(f32)
    middle = middle_ref[...]
    scale = lax.rsqrt(jnp.mean(middle * middle, axis=-1, keepdims=True) + norm_eps)
    unit = middle * scale
    dgain_ref[...] = jnp.sum(grad * unit, axis=0, keepdims=True)
    w = gain_ref[...] * grad
    dmid = cot_ref[...].astype(f32) + scale * (w - unit * jnp.mean(w * unit, axis=-1, keepdims=True))
    dmid_ref[...] = dmid
    proj = (residual_scale * dmid).astype(bf16)
    proj_ref[...] = proj
    mixed_grad = dot_nt(proj, wo_ref[...]).astype(bf16)
    groups, _, pair = mg_ref.shape
    for g in range(groups):
        mg_ref[g] = mixed_grad[:, g * pair : (g + 1) * pair]


def turn_call(sg, middle, gain, cot, wo, groups):
    rows, features = middle.shape
    pair = wo.shape[0] // groups
    return pl.pallas_call(
        turn_kernel,
        out_shape=[
            jax.ShapeDtypeStruct((groups, rows, pair), bf16),
            jax.ShapeDtypeStruct((rows, features), bf16),
            jax.ShapeDtypeStruct((rows, features), f32),
            jax.ShapeDtypeStruct((1, features), f32),
        ],
        compiler_params=params(32),
        cost_estimate=cost(2 * rows * wo.size, 6e6),
        name="norm_back_project_back",
    )(sg, middle, gain, cot, wo)


def output_weight_kernel(mixed_ref, proj_ref, dgain_ref, out_ref):
    held, each, features = out_ref.shape
    rows = mixed_ref.shape[1] // held
    part = lax.dot_general(mixed_ref[...], proj_ref[...], TN, preferred_element_type=f32)
    extra = jnp.broadcast_to(dgain_ref[...], (each - rows, features)).astype(bf16)
    for at in range(held):
        out_ref[at, :rows] = part[at * rows : (at + 1) * rows].astype(bf16)
        out_ref[at, rows:] = extra


def output_weight_call(mixed, proj, dgain, parts):
    rows, width = mixed.shape
    features = proj.shape[1]
    each = width // parts
    lanes = max(each, width // 2)
    held = lanes // each
    return pl.pallas_call(
        output_weight_kernel,
        grid=(parts // held,),
        in_specs=[
            pl.BlockSpec((rows, lanes), lambda s: (0, s)),
            whole((rows, features)),
            whole((1, features)),
        ],
        out_specs=pl.BlockSpec((held, each + 16, features), lambda s: (s, 0, 0)),
        out_shape=jax.ShapeDtypeStruct((parts, each + 16, features), bf16),
        compiler_params=params(32, "arbitrary"),
        cost_estimate=cost(2 * rows * width * features, 4e6),
        name="output_weight_part",
    )(mixed, proj, dgain)


def dense_out_kernel(at_ref, *refs):
    held, refs = refs[:-13], refs[-13:]
    wq_ref, wk_ref, wv_ref, gain_ref, dq_ref, dk_ref, dv_ref, dg_ref, wo_ref, dg2_ref = refs[:10]
    own_ref, other_ref = refs[10:12]
    parts = len(held) // 4
    stream, step = pl.program_id(0), pl.program_id(1)
    chips, _, width = own_ref.shape
    rows = dq_ref.shape[0]
    pair = width // 2
    chip, core = at_ref[2], at_ref[3]
    for which in range(2):
        for rel in range(parts):

            @pl.when((stream == which) & (jnp.bitwise_xor(step, at_ref[which]) == rel))
            def _():
                own_ref[...] = held[which * parts + rel][...]
                other_ref[...] = held[(2 + which) * parts + rel][...]

    total = jnp.zeros((rows, pair), f32)
    for k in range(chips):
        source = lax.rem(chip - k + chips, chips)
        a = jnp.where(core == 0, own_ref[k], other_ref[k]).astype(f32)
        b = jnp.where(core == 0, other_ref[k], own_ref[k]).astype(f32)
        q = jnp.concatenate([a[:rows, :pair], b[:rows, :pair]], axis=1)
        cols = pl.ds(pl.multiple_of(source * width, width), width)
        dq_ref[:, cols] = q
        made = q * wq_ref[:, cols].astype(f32)
        total += made[:, :pair] + made[:, pair:]
        a_kv, b_kv = a[:rows, pair:], b[:rows, pair:]
        lane = lax.broadcasted_iota(jnp.int32, a_kv.shape, 1)
        key = jnp.where(lane < HEAD_DIM, a_kv, pltpu.roll(b_kv, HEAD_DIM, 1))
        val = jnp.where(lane < HEAD_DIM, pltpu.roll(a_kv, HEAD_DIM, 1), b_kv)
        cols = pl.ds(pl.multiple_of(source * pair, pair), pair)
        dk_ref[:, cols] = key
        dv_ref[:, cols] = val
        total += key * wk_ref[:, cols].astype(f32) + val * wv_ref[:, cols].astype(f32)
        wo_ref[2 * source, 0] = a[rows : rows + wo_ref.shape[2]]
        wo_ref[2 * source + 1, 0] = b[rows : rows + wo_ref.shape[2]]
        if k == 0:
            dg2_ref[...] = a[rows + wo_ref.shape[2] :][:1]
    dg_ref[...] = jnp.sum(jnp.transpose(total), axis=0, keepdims=True) / gain_ref[...]


def dense_out_call(at, own, other, wq, wk, wv, gain, wo_shape):
    held = [*own[0], *own[1], *other[0], *other[1]]
    streams, parts = 2, len(own[0])
    chips, depth, width = held[0].shape
    features = wq.shape[0]
    groups = 2 * chips
    rows = features // (streams * parts)
    block_cols = wo_shape[1] // width
    per_block = streams * parts // block_cols
    wo_rows = wo_shape[0] // groups // per_block
    by_rows = lambda w: pl.BlockSpec((rows, w.shape[1]), lambda s, r, at: (s * parts + r, 0))
    gain_spec = pl.BlockSpec((1, rows), lambda s, r, at: (0, s * parts + r))
    outs = pl.pallas_call(
        dense_out_kernel,
        grid_spec=pltpu.PrefetchScalarGridSpec(
            num_scalar_prefetch=1,
            grid=(streams, parts),
            in_specs=[pl.BlockSpec(memory_space=pltpu.VMEM)] * len(held)
            + [by_rows(wq), by_rows(wk), by_rows(wv), gain_spec],
            out_specs=[
                by_rows(wq),
                by_rows(wk),
                by_rows(wv),
                gain_spec,
                pl.BlockSpec(
                    (groups, 1, wo_rows, width),
                    lambda s, r, at: (
                        0,
                        lax.rem(s * parts + r, per_block),
                        0,
                        lax.div(s * parts + r, per_block),
                    ),
                ),
                pl.BlockSpec((1, width), lambda s, r, at: (0, lax.div(s * parts + r, per_block))),
            ],
            scratch_shapes=[pltpu.VMEM((chips, depth, width), bf16)] * 2
            + [pltpu.VMEM((8, 128), f32)],
        ),
        out_shape=[
            jax.ShapeDtypeStruct(wq.shape, f32),
            jax.ShapeDtypeStruct(wk.shape, f32),
            jax.ShapeDtypeStruct(wv.shape, f32),
            jax.ShapeDtypeStruct((1, features), f32),
            jax.ShapeDtypeStruct((groups, per_block, wo_rows, wo_shape[1]), f32),
            jax.ShapeDtypeStruct((1, wo_shape[1]), f32),
        ],
        compiler_params=params(28, "arbitrary", "arbitrary"),
        cost_estimate=cost(2 * wq.size, 2.4e7),
        name="dense_weights_out",
    )(at, *held, wq, wk, wv, gain)
    return (*outs[:4], outs[4].reshape(wo_shape), outs[5])


def weights_out_kernel(wide_ref, wq_ref, wk_ref, wv_ref, gain_ref, dq_ref, dk_ref, dv_ref, dg_ref):
    groups, rows, width = wide_ref.shape
    pair = width // 2
    total = jnp.zeros((rows, pair), f32)
    for g in range(groups):
        part = wide_ref[g, :, :pair].astype(f32)
        at = slice(g * pair, (g + 1) * pair)
        dq_ref[:, at] = part
        total += part * wq_ref[:, at].astype(f32)
    for g in range(groups // 2):
        a = wide_ref[2 * g, :, pair:].astype(f32)
        b = wide_ref[2 * g + 1, :, pair:].astype(f32)
        lane = lax.broadcasted_iota(jnp.int32, a.shape, 1)
        at = slice(g * pair, (g + 1) * pair)
        k = jnp.where(lane < HEAD_DIM, a, pltpu.roll(b, HEAD_DIM, 1))
        v = jnp.where(lane < HEAD_DIM, pltpu.roll(a, HEAD_DIM, 1), b)
        dk_ref[:, at] = k
        dv_ref[:, at] = v
        total += k * wk_ref[:, at].astype(f32) + v * wv_ref[:, at].astype(f32)
    dg_ref[...] = jnp.sum(jnp.transpose(total), axis=0, keepdims=True) / gain_ref[...]


def weights_out_call(wide, wq, wk, wv, gain):
    chunks, groups, rows, width = wide.shape
    features = chunks * rows
    by_rows = lambda w: pl.BlockSpec((rows, w.shape[1]), lambda c: (c, 0))
    return pl.pallas_call(
        weights_out_kernel,
        grid=(chunks,),
        in_specs=[
            pl.BlockSpec((None, groups, rows, width), lambda c: (c, 0, 0, 0)),
            by_rows(wq),
            by_rows(wk),
            by_rows(wv),
            pl.BlockSpec((1, rows), lambda c: (0, c)),
        ],
        out_specs=[
            by_rows(wq),
            by_rows(wk),
            by_rows(wv),
            pl.BlockSpec((1, rows), lambda c: (0, c)),
        ],
        out_shape=[
            jax.ShapeDtypeStruct(wq.shape, f32),
            jax.ShapeDtypeStruct(wk.shape, f32),
            jax.ShapeDtypeStruct(wv.shape, f32),
            jax.ShapeDtypeStruct((1, features), f32),
        ],
        compiler_params=params(32, "arbitrary"),
        cost_estimate=cost(2 * wq.size, 1.6e7),
        name="attention_weights_out",
    )(wide, wq, wk, wv, gain)


def last_kernel(d_ref, wq_ref, wk_ref, wv_ref, x_ref, gain_ref, dmid_ref, out_ref):
    groups, rows, width = d_ref.shape
    pair = width // 2
    dq = jnp.concatenate([d_ref[g, :, :pair] for g in range(groups)], axis=1)
    grad = dot_nt(dq, wq_ref[...])
    keys, vals = [], []
    for at in range(groups // 2):
        a = d_ref[2 * at, :, pair:].astype(f32)
        b = d_ref[2 * at + 1, :, pair:].astype(f32)
        lane = lax.broadcasted_iota(jnp.int32, a.shape, 1)
        keys.append(jnp.where(lane < HEAD_DIM, a, pltpu.roll(b, HEAD_DIM, 1)).astype(bf16))
        vals.append(jnp.where(lane < HEAD_DIM, pltpu.roll(a, HEAD_DIM, 1), b).astype(bf16))
    grad = grad + dot_nt(jnp.concatenate(keys, axis=1), wk_ref[...])
    grad = grad + dot_nt(jnp.concatenate(vals, axis=1), wv_ref[...])
    x = x_ref[...].astype(f32)
    scale = lax.rsqrt(jnp.mean(x * x, axis=-1, keepdims=True) + norm_eps)
    unit = x * scale
    w = gain_ref[...] * grad
    out_ref[...] = dmid_ref[...] + scale * (w - unit * jnp.mean(w * unit, axis=-1, keepdims=True))


def last_call(d, wq, wk, wv, x, gain, dmid):
    rows, features = x.shape
    return pl.pallas_call(
        last_kernel,
        out_shape=jax.ShapeDtypeStruct((rows, features), f32),
        compiler_params=params(40),
        cost_estimate=cost(4 * rows * features * features, 8e6),
        name="input_gradient",
    )(d, wq, wk, wv, x, gain, dmid)


def swap(values, axis, bit):
    return lax.ppermute(values, axis, [(i, i ^ bit) for i in range(lax.axis_size(axis))])


def half_sum(values, axis, bit):
    half = values.shape[0] // 2
    upper = ((lax.axis_index(axis) & bit) > 0).astype(jnp.int32)
    came = swap(lax.dynamic_slice_in_dim(values, (1 - upper) * half, half), axis, bit)
    mine = lax.dynamic_slice_in_dim(values, upper * half, half)
    return (mine.astype(f32) + came.astype(f32)).astype(bf16)


def relative_sum(kept, sent, axis, bits):
    while True:
        kept = (kept.astype(f32) + swap(sent, axis, bits[0]).astype(f32)).astype(bf16)
        bits = bits[1:]
        if not bits:
            return kept
        half = kept.shape[0] // 2
        kept, sent = kept[:half], kept[half:]


def join_parts(stream, axis, bits):
    shape = stream.shape
    for bit in bits[::-1]:
        stream = jnp.stack([stream, swap(stream, axis, bit)])
    return stream.reshape(-1, *shape)


def body(
    layer_input,
    first_gain,
    query_weight,
    key_weight,
    value_weight,
    output_weight,
    second_gain,
    gate_weight,
    up_weight,
    down_weight,
    expert_ids,
    gate_values,
    positions,
    cotangent,
):
    micro, _, per_device, features = layer_input.shape
    devices = lax.axis_size("seq")
    replicas = lax.axis_size("dp")
    seq_place = lax.axis_index("seq")
    rows = micro * per_device
    local_experts = gate_weight.shape[0]
    groups = key_weight.shape[1] // HEAD_DIM
    pair = query_weight.shape[1] // groups
    copies = devices // groups

    dp_bits = [1 << i for i in range(replicas.bit_length() - 1)]

    def spread(blocks):
        if copies > 1:
            blocks = jnp.repeat(blocks, copies, axis=0)
        return lax.all_to_all(blocks, "seq", 0, 0, tiled=True)

    def unspread(blocks):
        return lax.all_to_all(blocks, "seq", 0, 0, tiled=True)[::copies]

    x = layer_input.reshape(rows, features)
    cot = cotangent.reshape(rows, features)
    gain_one = first_gain.reshape(1, features)
    gain_two = second_gain.reshape(1, features)
    pos_all = lax.all_to_all(
        jnp.broadcast_to(positions.reshape(1, rows), (devices, rows)), "seq", 0, 0, tiled=True
    )
    x_all = lax.all_gather(x, "seq", axis=0)
    cos_all, sin_all = rope_tables(pos_all.reshape(-1), pair)
    mine = seq_place * local_experts + jnp.arange(local_experts, dtype=jnp.int32)
    ids = expert_ids[:, 0]
    gates = gate_values[:, 0].astype(f32)
    routed = jnp.sum(
        jnp.where(ids[..., None] == mine, gates[..., None], 0.0), axis=2
    )
    routed = routed.reshape(micro, devices, per_device, local_experts)
    routed = jnp.transpose(routed, (1, 0, 2, 3)).reshape(devices * rows, local_experts)
    group = seq_place // copies
    w_own = jnp.concatenate(
        [
            lax.dynamic_slice_in_dim(query_weight, group * pair, pair, axis=1),
            lax.dynamic_slice_in_dim(key_weight, group * HEAD_DIM, HEAD_DIM, axis=1),
            lax.dynamic_slice_in_dim(value_weight, group * HEAD_DIM, HEAD_DIM, axis=1),
        ],
        axis=1,
    )
    cos_all, sin_all, routed, w_own = lax.optimization_barrier((cos_all, sin_all, routed, w_own))
    x_all, cot_then, cos_all, sin_all, routed, w_own = lax.optimization_barrier(
        (x_all, cot, cos_all, sin_all, routed, w_own)
    )
    cot_all = lax.all_gather(cot_then, "seq", axis=0)

    qkv, first_all = qkv_call(x_all, gain_one, cos_all, sin_all, w_own)
    qkv = qkv.reshape(devices, micro, per_device, 2 * pair)
    mix, log_total = attend_call(qkv)
    mix = unspread(mix.reshape(devices, rows, pair))
    mixed, middle, second_low = post_call(mix, output_weight, x, gain_two)

    chips = devices // 2
    chip, core = seq_place // 2, seq_place % 2
    onward = [(i, (i + 2) % devices) for i in range(devices)]
    dp_place = lax.axis_index("dp")
    first_bit = dp_place & 1
    last_bit = dp_place >> (len(dp_bits) - 1)
    held, kept, running, places = second_low, (), None, []
    for hop in range(chips):
        following = lax.ppermute(held, "seq", onward) if hop < chips - 1 else None
        other = swap(held, "seq", 1)
        source = 2 * ((chip - hop) % chips)
        place = jnp.stack([source + core, source + 1 - core, 1 - first_bit, 1 - last_bit])
        place = place.astype(jnp.int32)
        places.append(place[:2])
        dx, *kept = expert_call(
            hop, place, held, other, cot_all, routed, gate_weight, up_weight, down_weight, kept
        )
        if following is not None:
            following, dx = lax.optimization_barrier((following, dx))
        part = dx[0].astype(f32) + swap(dx[1], "seq", 1).astype(f32)
        if hop == 0:
            own_part = part
        else:
            if running is not None:
                part = part + running.astype(f32)
            part = part.astype(bf16)
            if following is not None:
                part, following = lax.optimization_barrier((part, following))
            else:
                part, kept = lax.optimization_barrier((part, kept))
            running = lax.ppermute(part, "seq", onward)
        held = following
    second_grad = (own_part + running.astype(f32)).astype(bf16)
    tokens, hidden_a, hidden_b, gate_low, up_low, slot_a, slot_b = kept

    def weight_parts(at, tokens, hidden_a, hidden_b, gate_low, up_low, slot_a, slot_b):
        pairs = (
            (tokens, gate_low[at]),
            (tokens, up_low[at]),
            (hidden_a[at], slot_a[at]),
            (hidden_b[at], slot_b[at]),
        )
        return [
            lax.dot_general(a, b, TN, preferred_element_type=f32).astype(bf16) for a, b in pairs
        ]

    leaving = weight_parts(0, *kept)
    part_bits = (dp_bits[0], dp_bits[-1], dp_bits[0], dp_bits[-1])
    stream_bits = (dp_bits, dp_bits[::-1])
    came = [swap(values, "dp", bit) for values, bit in zip(leaving, part_bits)]
    leaving, second_grad = lax.optimization_barrier((leaving, second_grad))

    mg_send, proj, middle_grad, gain_two_part = turn_call(
        second_grad, middle, gain_two, cot, output_weight, groups
    )
    mg = spread(mg_send)
    kept, _ = lax.optimization_barrier((kept, mg_send))
    mixed, proj, came[2:] = lax.optimization_barrier((mixed, proj, came[2:]))
    dense = output_weight_call(mixed, proj, gain_two_part, devices)
    dense_own = dense
    staying = weight_parts(1, *kept)
    turned = sum(((dp_place >> i) & 1) << (len(dp_bits) - 1 - i) for i in range(len(dp_bits)))
    part_at = jnp.stack([turned, dp_place]).astype(jnp.int32)
    low_at = jnp.bitwise_and(part_at, replicas // 2 - 1)
    keep_a, send_a, keep_b, send_b = part_sum_call(low_at, replicas // 2, came, staying)
    mg, keep_a, send_a, keep_b, send_b = lax.optimization_barrier(
        (mg, keep_a, send_a, keep_b, send_b)
    )
    streams = [
        relative_sum(keep_a, send_a, "dp", stream_bits[0][1:]),
        relative_sum(keep_b, send_b, "dp", stream_bits[1][1:]),
    ]
    dense = dense_own
    dense = lax.psum_scatter(dense, "seq", scatter_dimension=0)
    table_shape = (devices, micro, per_device, pair)
    dqkv = attend_back_call(
        qkv,
        mg.reshape(devices, micro, per_device, pair),
        log_total,
        cos_all.reshape(table_shape),
        sin_all.reshape(table_shape),
    )
    dqkv, streams = lax.optimization_barrier((dqkv, streams))
    near = [
        [v[0], swap(v[0], "dp", bits[-1])] for v, bits in zip(streams, stream_bits)
    ]
    back = unspread(dqkv.reshape(devices, rows, 2 * pair))
    d_all = dqkv.reshape(devices * rows, 2 * pair)
    first_tokens = first_all.reshape(devices * rows, features)
    part = lax.dot_general(first_tokens, d_all, TN, preferred_element_type=f32)
    dense = dense.reshape(dense.shape[-2], features)
    each = output_weight.shape[0] // devices
    if copies == 1:
        width = 2 * pair
        kept_pieces, sent_pieces = joint_call(part_at, part, dense, replicas)
        first = [
            kept_pieces[at].astype(f32) + swap(sent_pieces[at], "dp", bits[0]).astype(f32)
            for at, bits in enumerate(stream_bits)
        ]
        first, near = lax.optimization_barrier(([v.astype(bf16) for v in first], near))
        own = [
            relative_sum(v[: replicas // 4], v[replicas // 4 :], "dp", bits[1:])
            for v, bits in zip(first, stream_bits)
        ]
        own = jnp.concatenate(own, axis=0)
        own, back, here, kept = lax.optimization_barrier(
            (own, back, [v[0] for v in near], kept)
        )
        moe_place = jnp.concatenate(places + [(1 - first_bit).astype(jnp.int32).reshape(1)])
        moe_all = moe_call(moe_place, kept[1], routed, down_weight, devices)
        far = [swap(v, "dp", bits[-2]) for v, bits in zip(here, stream_bits)]
        backward = [(i, (i - 2) % devices) for i in range(devices)]
        round_ring = {0: own}
        for k in range(1, chips // 2 + 1):
            round_ring[k] = lax.ppermute(round_ring[k - 1], "seq", onward)
            if chips - k > k:
                round_ring[chips - k] = lax.ppermute(
                    round_ring[(chips - k + 1) % chips], "seq", backward
                )
            if k == 1:
                round_ring, coming = lax.optimization_barrier(
                    (round_ring, [v[1] for v in near])
                )
        round_ring, moe_all, far = lax.optimization_barrier((round_ring, moe_all, far))
        held = jnp.stack([round_ring[k] for k in range(chips)])
        passed = [swap(v, "dp", bits[-2]) for v, bits in zip(coming, stream_bits)]
        moe = lax.psum_scatter(moe_all, "seq", scatter_dimension=0)
        held, passed = lax.optimization_barrier((held, passed))
        layer_output = (middle + residual_scale * moe.astype(f32)).astype(bf16)
    else:
        far = [swap(v[0], "dp", bits[-2]) for v, bits in zip(streams, stream_bits)]
        passed = [swap(v[1], "dp", bits[-2]) for v, bits in zip(near, stream_bits)]
    expert_pieces = []
    for (here, first), second, third, bits in zip(near, far, passed, stream_bits):
        pieces = [here, first, second, third]
        for bit in bits[:-2][::-1]:
            pieces = pieces + [swap(p, "dp", bit) for p in pieces]
        expert_pieces.append(pieces)
    input_grad = last_call(
        back, query_weight, key_weight, value_weight, x, gain_one, middle_grad
    )
    if copies == 1:
        gate_sum, up_sum, down_sum = expert_out_call(
            part_at, *expert_pieces, gate_weight.shape, down_weight.shape
        )
        full = [[held[:, at], swap(held[:, at], "dp", b[-1])] for at, b in enumerate(stream_bits)]
        beside = [swap(v[0], "dp", bits[-2]) for v, bits in zip(full, stream_bits)]
        full, beside, gate_sum, up_sum, down_sum, input_grad = lax.optimization_barrier(
            (full, beside, gate_sum, up_sum, down_sum, input_grad)
        )
        for at, bits in enumerate(stream_bits):
            full[at] += [beside[at], swap(full[at][1], "dp", bits[-2])]
            for bit in bits[:-2][::-1]:
                full[at] += [swap(p, "dp", bit) for p in full[at]]
        other = [[swap(p, "seq", 1) for p in pieces] for pieces in full]
        where_at = jnp.stack([turned, dp_place, chip, core]).astype(jnp.int32)
        (
            query_weight_grad,
            key_weight_grad,
            value_weight_grad,
            first_gain_grad,
            output_weight_grad,
            second_gain_grad,
        ) = dense_out_call(
            where_at, full, other, query_weight, key_weight, value_weight, gain_one, output_weight.shape
        )
    else:
        gate_sum, up_sum, down_sum = expert_out_call(
            part_at, *expert_pieces, gate_weight.shape, down_weight.shape
        )
        for bit in dp_bits:
            dense = (dense.astype(f32) + swap(dense, "dp", bit).astype(f32)).astype(bf16)
        dense = lax.all_gather(dense, "seq", axis=0).astype(f32)
        output_weight_grad = dense[:, :each].reshape(output_weight.shape)
        moe_place = jnp.concatenate(places + [(1 - first_bit).astype(jnp.int32).reshape(1)])
        moe_all = moe_call(moe_place, kept[1], routed, down_weight, devices)
        moe = lax.psum_scatter(moe_all, "seq", scatter_dimension=0)
        layer_output = (middle + residual_scale * moe.astype(f32)).astype(bf16)
        second_gain_grad = dense[0, each]
        part = part.astype(bf16)
        for bit in dp_bits[::-1]:
            part = half_sum(part, "dp", bit)
        wide = lax.all_gather(part, ("dp", "seq"), axis=0)
        wide = wide.reshape(replicas, devices, features // replicas, 2 * pair)[:, ::copies]
        query_weight_grad, key_weight_grad, value_weight_grad, first_gain_grad = weights_out_call(
            wide, query_weight, key_weight, value_weight, gain_one
        )
    second_gain_grad = second_gain_grad.reshape(features)
    return (
        layer_output.reshape(layer_input.shape),
        input_grad.reshape(layer_input.shape),
        first_gain_grad.reshape(features),
        query_weight_grad,
        key_weight_grad,
        value_weight_grad,
        output_weight_grad,
        second_gain_grad,
        gate_sum,
        up_sum,
        down_sum,
    )


def solution(mesh):
    return jax.shard_map(
        body,
        mesh=mesh,
        in_specs=(
            P(None, "dp", "seq", None),
            P(),
            P(),
            P(),
            P(),
            P(),
            P(),
            P("seq", None, None),
            P("seq", None, None),
            P("seq", None, None),
            P(None, "dp", None, None),
            P(None, "dp", None, None),
            P(None, "dp", "seq"),
            P(None, "dp", "seq", None),
        ),
        out_specs=(
            P(None, "dp", "seq", None),
            P(None, "dp", "seq", None),
            P(),
            P(),
            P(),
            P(),
            P(),
            P(),
            P("seq", None, None),
            P("seq", None, None),
            P("seq", None, None),
        ),
        check_vma=False,
    )
```

```python
from functools import partial

import jax
import jax.numpy as jnp
from jax import lax
from jax.experimental import pallas as pl
from jax.experimental.pallas import tpu as pltpu
from jax.sharding import PartitionSpec as P

HEAD_DIM = 64

rope_theta = 10000.0
attention_scale = 0.015625
residual_scale = 0.22
norm_eps = 1e-06
masked_score = -1e30

f32 = jnp.float32
bf16 = jnp.bfloat16
NT = (((1,), (1,)), ((), ()))
TN = (((0,), (0,)), ((), ()))


def dot(a, b):
    return jnp.dot(a, b, preferred_element_type=f32)


def dot_nt(a, b):
    return lax.dot_general(a, b, NT, preferred_element_type=f32)


def params(mib, *semantics):
    return pltpu.CompilerParams(
        vmem_limit_bytes=mib * 1024 * 1024, dimension_semantics=semantics or None
    )


def cost(flops, nbytes, trans=0):
    return pl.CostEstimate(
        flops=int(flops / 8), bytes_accessed=int(nbytes / 8), transcendentals=int(trans / 8)
    )


def whole(shape):
    return pl.BlockSpec(shape, lambda *_: (0,) * len(shape))


def rope_tables(positions, width):
    half = HEAD_DIM // 2
    exponent = jnp.arange(half, dtype=f32) * (-2.0 / HEAD_DIM)
    angles = positions.astype(f32)[:, None] * (rope_theta**exponent)[None, :]
    cosine, sine = jnp.cos(angles), jnp.sin(angles)
    copies = width // HEAD_DIM
    cos_row = jnp.concatenate([cosine, cosine] * copies, axis=1)
    sin_row = jnp.concatenate([-sine, sine] * copies, axis=1)
    return cos_row, sin_row


def partner(values):
    width = values.shape[1]
    half = HEAD_DIM // 2
    lane = lax.broadcasted_iota(jnp.int32, values.shape, 1)
    ahead = pltpu.roll(values, width - half, 1)
    behind = pltpu.roll(values, half, 1)
    return jnp.where(lane % HEAD_DIM < half, ahead, behind)


def qkv_kernel(x_ref, gain_ref, cos_ref, sin_ref, w_ref, qkv_ref, low_ref):
    pair = 2 * HEAD_DIM
    x = x_ref[0].astype(f32)
    scale = lax.rsqrt(jnp.mean(x * x, axis=-1, keepdims=True) + norm_eps)
    low = (x * scale * gain_ref[...]).astype(bf16)
    low_ref[0] = low
    cosine, sine = cos_ref[...], sin_ref[...]
    made = dot(low, w_ref[...])
    q, kv = made[:, :pair], made[:, pair:]
    q = (q * cosine + partner(q) * sine) * attention_scale
    qkv_ref[0, :, :pair] = q.astype(bf16)
    lane = lax.broadcasted_iota(jnp.int32, kv.shape, 1)
    turned = kv * cosine + partner(kv) * sine
    qkv_ref[0, :, pair:] = jnp.where(lane < HEAD_DIM, turned, kv).astype(bf16)


def qkv_call(x_all, gain, cos_all, sin_all, w_own):
    blocks, rows, features = x_all.shape
    pair = 2 * HEAD_DIM
    return pl.pallas_call(
        qkv_kernel,
        grid=(blocks,),
        in_specs=[
            pl.BlockSpec((1, rows, features), lambda s: (s, 0, 0)),
            whole((1, features)),
            pl.BlockSpec((rows, pair), lambda s: (s, 0)),
            pl.BlockSpec((rows, pair), lambda s: (s, 0)),
            whole(w_own.shape),
        ],
        out_specs=[
            pl.BlockSpec((1, rows, 2 * pair), lambda s: (s, 0, 0)),
            pl.BlockSpec((1, rows, features), lambda s: (s, 0, 0)),
        ],
        out_shape=[
            jax.ShapeDtypeStruct((blocks, rows, 2 * pair), bf16),
            jax.ShapeDtypeStruct((blocks, rows, features), bf16),
        ],
        compiler_params=params(58, "arbitrary"),
        cost_estimate=cost(4 * blocks * rows * features * pair, 14e6),
        name="norm_qkv_rope",
    )(x_all, gain, cos_all, sin_all, w_own)


def split_heads(block, first):
    wide = block.astype(f32)
    lane = lax.broadcasted_iota(jnp.int32, wide.shape, 1)
    turned = pltpu.roll(wide, HEAD_DIM, 1)
    if first:
        parts = [jnp.where(lane < HEAD_DIM, wide, 0.0), jnp.where(lane < HEAD_DIM, turned, 0.0)]
    else:
        parts = [jnp.where(lane >= HEAD_DIM, turned, 0.0), jnp.where(lane >= HEAD_DIM, wide, 0.0)]
    return jnp.concatenate(parts, axis=0).astype(bf16)


def join_heads(turned):
    rows = turned.shape[1] // 2
    return jnp.transpose(jnp.concatenate([turned[:, :rows], turned[:, rows:]], axis=0))


def scores_of(kv, q2, rows):
    scores = dot_nt(kv, q2)
    count = scores.shape[0]
    own = scores[count - rows :]
    key_at = lax.broadcasted_iota(jnp.int32, own.shape, 0)
    query_at = lax.broadcasted_iota(jnp.int32, own.shape, 1) % rows
    own = jnp.where(key_at <= query_at, own, masked_score)
    if count == rows:
        return own
    return jnp.concatenate([scores[: count - rows], own], axis=0)


def attend_kernel(qkv_ref, out_ref, log_ref):
    blocks, _, rows, width = qkv_ref.shape
    pair = width // 2
    kv = qkv_ref[:, 0, :, pair:].reshape(blocks * rows, pair)
    kv_t = jnp.transpose(kv)
    for at in range(blocks):
        count = (at + 1) * rows
        q2 = split_heads(qkv_ref[at, 0, :, :pair], True)
        scores = scores_of(kv[:count], q2, rows)
        top = jnp.max(scores, axis=0, keepdims=True)
        weights = jnp.exp(scores - top)
        total = jnp.sum(weights, axis=0, keepdims=True)
        out_t = dot(kv_t[:, :count], weights.astype(bf16))
        out_ref[at, 0] = join_heads(out_t[HEAD_DIM:] / total).astype(bf16)
        log_ref[at, 0] = top + jnp.log(total)


def attend_call(qkv):
    blocks, micro, rows, width = qkv.shape
    pair = width // 2
    length = blocks * rows
    return pl.pallas_call(
        attend_kernel,
        grid=(micro,),
        in_specs=[pl.BlockSpec((blocks, 1, rows, width), lambda m: (0, m, 0, 0))],
        out_specs=[
            pl.BlockSpec((blocks, 1, rows, pair), lambda m: (0, m, 0, 0)),
            pl.BlockSpec((blocks, 1, 1, 2 * rows), lambda m: (0, m, 0, 0)),
        ],
        out_shape=[
            jax.ShapeDtypeStruct((blocks, micro, rows, pair), bf16),
            jax.ShapeDtypeStruct((blocks, micro, 1, 2 * rows), f32),
        ],
        compiler_params=params(48, "arbitrary"),
        cost_estimate=cost(
            micro * length * length * 512, 3 * qkv.size, micro * length * length
        ),
        name="attention_forward",
    )(qkv)


def attend_back_kernel(qkv_ref, grad_ref, log_ref, cos_ref, sin_ref, out_ref, dkv_ref):
    blocks, _, rows, width = qkv_ref.shape
    pair = width // 2
    kv = qkv_ref[:, 0, :, pair:].reshape(blocks * rows, pair)
    kv_t = jnp.transpose(kv)
    dkv_ref[...] = jnp.zeros_like(dkv_ref)
    for at in range(blocks):
        count = (at + 1) * rows
        q2 = split_heads(qkv_ref[at, 0, :, :pair], True)
        g2 = split_heads(grad_ref[at, 0], False)
        scores = scores_of(kv[:count], q2, rows)
        prob = jnp.exp(scores - log_ref[at, 0])
        prob_grad = dot_nt(kv[:count], g2)
        delta = jnp.sum(prob * prob_grad, axis=0, keepdims=True)
        score_grad = (prob * (prob_grad - delta)).astype(bf16)
        dkv_ref[:count] += dot(score_grad, q2) + dot(prob.astype(bf16), g2)
        dq_t = dot(kv_t[:, :count], score_grad)
        dq = join_heads(dq_t[:HEAD_DIM] * attention_scale)
        dq = dq * cos_ref[at, 0] - partner(dq) * sin_ref[at, 0]
        out_ref[at, 0, :, :pair] = dq.astype(bf16)
    for at in range(blocks):
        dkv = dkv_ref[at * rows : (at + 1) * rows]
        lane = lax.broadcasted_iota(jnp.int32, dkv.shape, 1)
        turned = dkv * cos_ref[at, 0] - partner(dkv) * sin_ref[at, 0]
        out_ref[at, 0, :, pair:] = jnp.where(lane < HEAD_DIM, turned, dkv).astype(bf16)


def attend_back_call(qkv, grads, log_total, cos_all, sin_all):
    blocks, micro, rows, width = qkv.shape
    pair = width // 2
    length = blocks * rows
    spec = lambda lanes: pl.BlockSpec((blocks, 1, rows, lanes), lambda m: (0, m, 0, 0))
    return pl.pallas_call(
        attend_back_kernel,
        grid=(micro,),
        in_specs=[
            spec(width),
            spec(pair),
            pl.BlockSpec((blocks, 1, 1, 2 * rows), lambda m: (0, m, 0, 0)),
            spec(pair),
            spec(pair),
        ],
        out_specs=spec(width),
        out_shape=jax.ShapeDtypeStruct(qkv.shape, bf16),
        scratch_shapes=[pltpu.VMEM((length, pair), f32)],
        compiler_params=params(56, "arbitrary"),
        cost_estimate=cost(
            micro * length * length * 1280, 10 * qkv.size, micro * length * length
        ),
        name="attention_backward",
    )(qkv, grads, log_total, cos_all, sin_all)


def post_kernel(mix_ref, wo_ref, x_ref, gain_ref, mixed_ref, middle_ref, low_ref):
    mixed = jnp.concatenate([mix_ref[g] for g in range(mix_ref.shape[0])], axis=1)
    mixed_ref[...] = mixed
    middle = x_ref[...].astype(f32) + residual_scale * dot(mixed, wo_ref[...])
    middle_ref[...] = middle
    scale = lax.rsqrt(jnp.mean(middle * middle, axis=-1, keepdims=True) + norm_eps)
    low_ref[...] = (middle * scale * gain_ref[...]).astype(bf16)


def post_call(mix, wo, x, gain):
    rows, features = x.shape
    return pl.pallas_call(
        post_kernel,
        out_shape=[
            jax.ShapeDtypeStruct((rows, wo.shape[0]), bf16),
            jax.ShapeDtypeStruct((rows, features), f32),
            jax.ShapeDtypeStruct((rows, features), bf16),
        ],
        compiler_params=params(32),
        cost_estimate=cost(2 * rows * wo.size, 5e6),
        name="project_norm",
    )(mix, wo, x, gain)


def expert_kernel(place_ref, a_ref, b_ref, cot_ref, w_ref, wg_ref, wu_ref, wd_ref, *refs):
    dx_ref, x_ref, ha_ref, hb_ref, dg_ref, du_ref, sa_ref, sb_ref = refs[-8:]
    step = pl.program_id(0)
    first, second = place_ref[2], place_ref[3]
    half = sa_ref.shape[2]

    @pl.when(step == 0)
    def _():
        x_ref[...] = a_ref[...]

    @pl.when(step == 1)
    def _():
        x_ref[...] = b_ref[...]

    x = x_ref[...]
    cot = cot_ref[0].astype(f32)
    weight = residual_scale * w_ref[...]
    total = None
    for e in range(wg_ref.shape[0]):
        gate = dot(x, wg_ref[e])
        up = dot(x, wu_ref[e])
        slot_grad = (weight[:, e : e + 1] * cot).astype(bf16)
        to_a, to_b = jnp.bitwise_xor(first, e), jnp.bitwise_xor(second, e)
        sa_ref[to_a] = slot_grad[:, :half]
        sb_ref[to_b] = slot_grad[:, half:]
        hidden_grad = dot_nt(slot_grad, wd_ref[e])
        sig = 0.5 * jnp.tanh(0.5 * gate) + 0.5
        silu = gate * sig
        hidden = (silu * up).astype(bf16)
        ha_ref[to_a] = hidden
        hb_ref[to_b] = hidden
        gate_grad = (hidden_grad * up * (sig + silu * (1.0 - sig))).astype(bf16)
        up_grad = (hidden_grad * silu).astype(bf16)
        dg_ref[to_a] = gate_grad
        du_ref[to_b] = up_grad
        term = dot_nt(gate_grad, wg_ref[e]) + dot_nt(up_grad, wu_ref[e])
        total = term if total is None else total + term
    dx_ref[0] = total.astype(bf16)


def expert_call(at, place, own, other, cots, weight, wg, wu, wd, kept):
    rows, features = own.shape
    count, _, hidden = wg.shape
    tokens = weight.shape[0]
    inner = jax.ShapeDtypeStruct((count, tokens, hidden), bf16)
    outer = jax.ShapeDtypeStruct((count, tokens, features // 2), bf16)
    inner_spec = pl.BlockSpec((count, rows, hidden), lambda s, place: (0, 2 * at + s, 0))
    outer_spec = pl.BlockSpec((count, rows, features // 2), lambda s, place: (0, 2 * at + s, 0))
    fixed = lambda shape: pl.BlockSpec(shape, lambda s, place: (0,) * len(shape))
    any_spec = pl.BlockSpec(memory_space=pl.ANY)
    first = 8
    return pl.pallas_call(
        expert_kernel,
        grid_spec=pltpu.PrefetchScalarGridSpec(
            num_scalar_prefetch=1,
            grid=(2,),
            in_specs=[
                fixed((rows, features)),
                fixed((rows, features)),
                pl.BlockSpec((1, rows, features), lambda s, place: (place[4 + s], 0, 0)),
                pl.BlockSpec((rows, count), lambda s, place: (place[s], 0)),
                fixed(wg.shape),
                fixed(wu.shape),
                fixed(wd.shape),
            ]
            + [any_spec] * len(kept),
            out_specs=[
                pl.BlockSpec((1, rows, features), lambda s, place: (s, 0, 0)),
                pl.BlockSpec((rows, features), lambda s, place: (2 * at + s, 0)),
            ]
            + [inner_spec] * 4
            + [outer_spec] * 2,
        ),
        out_shape=[
            jax.ShapeDtypeStruct((2, rows, features), bf16),
            jax.ShapeDtypeStruct((tokens, features), bf16),
            inner,
            inner,
            inner,
            inner,
            outer,
            outer,
        ],
        input_output_aliases={first + i: 1 + i for i in range(len(kept))},
        compiler_params=params(48, "arbitrary"),
        cost_estimate=cost(20 * rows * wg.size, 2e7, 2 * rows * hidden * count),
        name="experts",
    )(place, own, other, cots, weight, wg, wu, wd, *kept)


def part_sum_kernel(at_ref, *refs):
    inputs, outs = refs[:16], refs[16:]
    at = 0
    for out in outs:
        gate_came, gate_here, down_came, down_here = inputs[at : at + 4]
        rows = gate_came.shape[0]
        out[0, :rows] = (gate_came[...].astype(f32) + gate_here[...].astype(f32)).astype(bf16)
        out[0, rows:] = (down_came[...].astype(f32) + down_here[...].astype(f32)).astype(bf16)
        at += 4


def part_sum_call(at, per, came, here):
    gate_rows, down_rows = came[0].shape[0] // per, came[2].shape[0] // per
    width = came[0].shape[1]
    steps = per // 2
    specs, args, out_specs, out_shapes = [], [], [], []
    for stream in range(2):
        for sent in range(2):
            for which, rows in ((stream, gate_rows), (stream + 2, down_rows)):
                spec = pl.BlockSpec(
                    (rows, width),
                    lambda s, at, sent=sent, stream=stream: (
                        jnp.bitwise_xor(s + sent * steps, at[stream]),
                        0,
                    ),
                )
                specs += [spec, spec]
                args += [came[which], here[which]]
            out_specs.append(
                pl.BlockSpec((1, gate_rows + down_rows, width), lambda s, at: (s, 0, 0))
            )
            out_shapes.append(
                jax.ShapeDtypeStruct((steps, gate_rows + down_rows, width), bf16)
            )
    return pl.pallas_call(
        part_sum_kernel,
        grid_spec=pltpu.PrefetchScalarGridSpec(
            num_scalar_prefetch=1, grid=(steps,), in_specs=specs, out_specs=out_specs
        ),
        out_shape=out_shapes,
        compiler_params=params(60, "arbitrary"),
        cost_estimate=cost(0, 9e6),
        name="expert_part_sum",
    )(at, *args)


def joint_kernel(at_ref, *refs):
    for (part_ref, wo_ref, gain_ref), out_ref in ((refs[:3], refs[6]), (refs[3:6], refs[7])):
        rows = part_ref.shape[0]
        upto = rows + wo_ref.shape[0]
        out_ref[0, 0, :rows] = part_ref[...].astype(bf16)
        out_ref[0, 0, rows:upto] = wo_ref[...]
        out_ref[0, 0, upto:] = gain_ref[...]


def joint_call(at, part, dense, parts):
    features, width = part.shape
    pieces = 2 * parts
    rows = features // pieces
    block_cols = dense.shape[1] // width
    per_block = pieces // block_cols
    extra = 16
    wo_rows = (dense.shape[0] - extra) // per_block
    last = dense.shape[0] // extra - 1
    steps = parts // 2

    def piece(sent):
        return lambda s, p, at: s * parts + jnp.bitwise_xor(p + sent * steps, at[s])

    specs = []
    for sent in range(2):
        at_piece = piece(sent)
        specs.append(
            pl.BlockSpec((rows, width), lambda s, p, at, f=at_piece: (f(s, p, at), 0))
        )
        specs.append(
            pl.BlockSpec(
                (wo_rows, width),
                lambda s, p, at, f=at_piece: (
                    lax.rem(f(s, p, at), per_block),
                    lax.div(f(s, p, at), per_block),
                ),
            )
        )
        specs.append(
            pl.BlockSpec(
                (extra, width), lambda s, p, at, f=at_piece: (last, lax.div(f(s, p, at), per_block))
            )
        )
    out_spec = pl.BlockSpec((1, 1, rows + wo_rows + extra, width), lambda s, p, at: (s, p, 0, 0))
    out_shape = jax.ShapeDtypeStruct((2, steps, rows + wo_rows + extra, width), bf16)
    return pl.pallas_call(
        joint_kernel,
        grid_spec=pltpu.PrefetchScalarGridSpec(
            num_scalar_prefetch=1, grid=(2, steps), in_specs=specs, out_specs=[out_spec] * 2
        ),
        out_shape=[out_shape] * 2,
        compiler_params=params(32, "arbitrary", "arbitrary"),
        cost_estimate=cost(0, 2e6),
        name="dense_pieces",
    )(at, part, dense, dense, part, dense, dense)


def expert_out_kernel(at_ref, *refs):
    pieces, (gate_ref, up_ref, down_ref) = refs[:-3], refs[-3:]
    parts = len(pieces) // 2
    step = pl.program_id(0)
    rows = gate_ref.shape[1]
    half = down_ref.shape[2] // 2
    for which in range(parts):

        @pl.when(jnp.bitwise_xor(step, at_ref[0]) == which)
        def _():
            a_ref = pieces[which]
            gate_ref[0] = a_ref[:rows].astype(f32)
            down_ref[0, :, :half] = a_ref[rows:].astype(f32)

        @pl.when(jnp.bitwise_xor(step, at_ref[1]) == which)
        def _():
            b_ref = pieces[parts + which]
            up_ref[0] = b_ref[:rows].astype(f32)
            down_ref[0, :, half:] = b_ref[rows:].astype(f32)


def expert_out_call(at, a, b, gate_shape, down_shape):
    parts = len(a)
    held, width = a[0].shape
    count = gate_shape[0]
    per = parts // count
    gate_rows, down_rows = gate_shape[1] // per, down_shape[1] // per
    place = lambda r, at: (lax.div(r, per), lax.rem(r, per), 0)
    return pl.pallas_call(
        expert_out_kernel,
        grid_spec=pltpu.PrefetchScalarGridSpec(
            num_scalar_prefetch=1,
            grid=(parts,),
            in_specs=[pl.BlockSpec((held, width), lambda r, at: (0, 0))] * (2 * parts),
            out_specs=[
                pl.BlockSpec((1, gate_rows, gate_shape[2]), place),
                pl.BlockSpec((1, gate_rows, gate_shape[2]), place),
                pl.BlockSpec((1, down_rows, down_shape[2]), place),
            ],
        ),
        out_shape=[
            jax.ShapeDtypeStruct(gate_shape, f32),
            jax.ShapeDtypeStruct(gate_shape, f32),
            jax.ShapeDtypeStruct(down_shape, f32),
        ],
        compiler_params=params(40, "arbitrary"),
        cost_estimate=cost(0, 2e7),
        name="expert_weights_out",
    )(at, *a, *b)


def moe_kernel(place_ref, h_ref, w_ref, wd_ref, out_ref):
    weight = w_ref[...]
    total = None
    first = place_ref[pl.num_programs(0)]
    for e in range(wd_ref.shape[0]):
        term = weight[:, e : e + 1] * dot(h_ref[jnp.bitwise_xor(first, e)], wd_ref[e])
        total = term if total is None else total + term
    out_ref[0] = total.astype(bf16)


def moe_call(place, hidden, weight, wd, blocks):
    count, tokens, inner = hidden.shape
    features = wd.shape[2]
    rows = tokens // blocks
    return pl.pallas_call(
        moe_kernel,
        grid_spec=pltpu.PrefetchScalarGridSpec(
            num_scalar_prefetch=1,
            grid=(blocks,),
            in_specs=[
                pl.BlockSpec((count, rows, inner), lambda s, place: (0, s, 0)),
                pl.BlockSpec((rows, count), lambda s, place: (place[s], 0)),
                pl.BlockSpec(wd.shape, lambda s, place: (0, 0, 0)),
            ],
            out_specs=pl.BlockSpec((1, rows, features), lambda s, place: (place[s], 0, 0)),
        ),
        out_shape=jax.ShapeDtypeStruct((blocks, rows, features), bf16),
        compiler_params=params(60, "arbitrary"),
        cost_estimate=cost(2 * tokens * wd.size, 1.1e7),
        name="expert_outputs",
    )(place, hidden, weight, wd)


def turn_kernel(sg_ref, middle_ref, gain_ref, cot_ref, wo_ref, mg_ref, proj_ref, dmid_ref, dgain_ref):
    grad = sg_ref[...].astype(f32)
    middle = middle_ref[...]
    scale = lax.rsqrt(jnp.mean(middle * middle, axis=-1, keepdims=True) + norm_eps)
    unit = middle * scale
    dgain_ref[...] = jnp.sum(grad * unit, axis=0, keepdims=True)
    w = gain_ref[...] * grad
    dmid = cot_ref[...].astype(f32) + scale * (w - unit * jnp.mean(w * unit, axis=-1, keepdims=True))
    dmid_ref[...] = dmid
    proj = (residual_scale * dmid).astype(bf16)
    proj_ref[...] = proj
    mixed_grad = dot_nt(proj, wo_ref[...]).astype(bf16)
    groups, _, pair = mg_ref.shape
    for g in range(groups):
        mg_ref[g] = mixed_grad[:, g * pair : (g + 1) * pair]


def turn_call(sg, middle, gain, cot, wo, groups):
    rows, features = middle.shape
    pair = wo.shape[0] // groups
    return pl.pallas_call(
        turn_kernel,
        out_shape=[
            jax.ShapeDtypeStruct((groups, rows, pair), bf16),
            jax.ShapeDtypeStruct((rows, features), bf16),
            jax.ShapeDtypeStruct((rows, features), f32),
            jax.ShapeDtypeStruct((1, features), f32),
        ],
        compiler_params=params(32),
        cost_estimate=cost(2 * rows * wo.size, 6e6),
        name="norm_back_project_back",
    )(sg, middle, gain, cot, wo)


def output_weight_kernel(mixed_ref, proj_ref, dgain_ref, out_ref):
    held, each, features = out_ref.shape
    rows = mixed_ref.shape[1] // held
    part = lax.dot_general(mixed_ref[...], proj_ref[...], TN, preferred_element_type=f32)
    extra = jnp.broadcast_to(dgain_ref[...], (each - rows, features)).astype(bf16)
    for at in range(held):
        out_ref[at, :rows] = part[at * rows : (at + 1) * rows].astype(bf16)
        out_ref[at, rows:] = extra


def output_weight_call(mixed, proj, dgain, parts):
    rows, width = mixed.shape
    features = proj.shape[1]
    each = width // parts
    lanes = max(each, width // 2)
    held = lanes // each
    return pl.pallas_call(
        output_weight_kernel,
        grid=(parts // held,),
        in_specs=[
            pl.BlockSpec((rows, lanes), lambda s: (0, s)),
            whole((rows, features)),
            whole((1, features)),
        ],
        out_specs=pl.BlockSpec((held, each + 16, features), lambda s: (s, 0, 0)),
        out_shape=jax.ShapeDtypeStruct((parts, each + 16, features), bf16),
        compiler_params=params(32, "arbitrary"),
        cost_estimate=cost(2 * rows * width * features, 4e6),
        name="output_weight_part",
    )(mixed, proj, dgain)


def dense_out_kernel(at_ref, *refs):
    held, refs = refs[:-13], refs[-13:]
    wq_ref, wk_ref, wv_ref, gain_ref, dq_ref, dk_ref, dv_ref, dg_ref, wo_ref, dg2_ref = refs[:10]
    own_ref, other_ref = refs[10:12]
    parts = len(held) // 4
    stream, step = pl.program_id(0), pl.program_id(1)
    chips, _, width = own_ref.shape
    rows = dq_ref.shape[0]
    pair = width // 2
    chip, core = at_ref[2], at_ref[3]
    for which in range(2):
        for rel in range(parts):

            @pl.when((stream == which) & (jnp.bitwise_xor(step, at_ref[which]) == rel))
            def _():
                own_ref[...] = held[which * parts + rel][...]
                other_ref[...] = held[(2 + which) * parts + rel][...]

    total = jnp.zeros((rows, pair), f32)
    for k in range(chips):
        source = lax.rem(chip - k + chips, chips)
        a = jnp.where(core == 0, own_ref[k], other_ref[k]).astype(f32)
        b = jnp.where(core == 0, other_ref[k], own_ref[k]).astype(f32)
        q = jnp.concatenate([a[:rows, :pair], b[:rows, :pair]], axis=1)
        cols = pl.ds(pl.multiple_of(source * width, width), width)
        dq_ref[:, cols] = q
        made = q * wq_ref[:, cols].astype(f32)
        total += made[:, :pair] + made[:, pair:]
        a_kv, b_kv = a[:rows, pair:], b[:rows, pair:]
        lane = lax.broadcasted_iota(jnp.int32, a_kv.shape, 1)
        key = jnp.where(lane < HEAD_DIM, a_kv, pltpu.roll(b_kv, HEAD_DIM, 1))
        val = jnp.where(lane < HEAD_DIM, pltpu.roll(a_kv, HEAD_DIM, 1), b_kv)
        cols = pl.ds(pl.multiple_of(source * pair, pair), pair)
        dk_ref[:, cols] = key
        dv_ref[:, cols] = val
        total += key * wk_ref[:, cols].astype(f32) + val * wv_ref[:, cols].astype(f32)
        wo_ref[2 * source, 0] = a[rows : rows + wo_ref.shape[2]]
        wo_ref[2 * source + 1, 0] = b[rows : rows + wo_ref.shape[2]]
        if k == 0:
            dg2_ref[...] = a[rows + wo_ref.shape[2] :][:1]
    dg_ref[...] = jnp.sum(jnp.transpose(total), axis=0, keepdims=True) / gain_ref[...]


def dense_out_call(at, own, other, wq, wk, wv, gain, wo_shape):
    held = [*own[0], *own[1], *other[0], *other[1]]
    streams, parts = 2, len(own[0])
    chips, depth, width = held[0].shape
    features = wq.shape[0]
    groups = 2 * chips
    rows = features // (streams * parts)
    block_cols = wo_shape[1] // width
    per_block = streams * parts // block_cols
    wo_rows = wo_shape[0] // groups // per_block
    by_rows = lambda w: pl.BlockSpec((rows, w.shape[1]), lambda s, r, at: (s * parts + r, 0))
    gain_spec = pl.BlockSpec((1, rows), lambda s, r, at: (0, s * parts + r))
    outs = pl.pallas_call(
        dense_out_kernel,
        grid_spec=pltpu.PrefetchScalarGridSpec(
            num_scalar_prefetch=1,
            grid=(streams, parts),
            in_specs=[pl.BlockSpec(memory_space=pltpu.VMEM)] * len(held)
            + [by_rows(wq), by_rows(wk), by_rows(wv), gain_spec],
            out_specs=[
                by_rows(wq),
                by_rows(wk),
                by_rows(wv),
                gain_spec,
                pl.BlockSpec(
                    (groups, 1, wo_rows, width),
                    lambda s, r, at: (
                        0,
                        lax.rem(s * parts + r, per_block),
                        0,
                        lax.div(s * parts + r, per_block),
                    ),
                ),
                pl.BlockSpec((1, width), lambda s, r, at: (0, lax.div(s * parts + r, per_block))),
            ],
            scratch_shapes=[pltpu.VMEM((chips, depth, width), bf16)] * 2
            + [pltpu.VMEM((8, 128), f32)],
        ),
        out_shape=[
            jax.ShapeDtypeStruct(wq.shape, f32),
            jax.ShapeDtypeStruct(wk.shape, f32),
            jax.ShapeDtypeStruct(wv.shape, f32),
            jax.ShapeDtypeStruct((1, features), f32),
            jax.ShapeDtypeStruct((groups, per_block, wo_rows, wo_shape[1]), f32),
            jax.ShapeDtypeStruct((1, wo_shape[1]), f32),
        ],
        compiler_params=params(28, "arbitrary", "arbitrary"),
        cost_estimate=cost(2 * wq.size, 2.4e7),
        name="dense_weights_out",
    )(at, *held, wq, wk, wv, gain)
    return (*outs[:4], outs[4].reshape(wo_shape), outs[5])


def weights_out_kernel(wide_ref, wq_ref, wk_ref, wv_ref, gain_ref, dq_ref, dk_ref, dv_ref, dg_ref):
    groups, rows, width = wide_ref.shape
    pair = width // 2
    total = jnp.zeros((rows, pair), f32)
    for g in range(groups):
        part = wide_ref[g, :, :pair].astype(f32)
        at = slice(g * pair, (g + 1) * pair)
        dq_ref[:, at] = part
        total += part * wq_ref[:, at].astype(f32)
    for g in range(groups // 2):
        a = wide_ref[2 * g, :, pair:].astype(f32)
        b = wide_ref[2 * g + 1, :, pair:].astype(f32)
        lane = lax.broadcasted_iota(jnp.int32, a.shape, 1)
        at = slice(g * pair, (g + 1) * pair)
        k = jnp.where(lane < HEAD_DIM, a, pltpu.roll(b, HEAD_DIM, 1))
        v = jnp.where(lane < HEAD_DIM, pltpu.roll(a, HEAD_DIM, 1), b)
        dk_ref[:, at] = k
        dv_ref[:, at] = v
        total += k * wk_ref[:, at].astype(f32) + v * wv_ref[:, at].astype(f32)
    dg_ref[...] = jnp.sum(jnp.transpose(total), axis=0, keepdims=True) / gain_ref[...]


def weights_out_call(wide, wq, wk, wv, gain):
    chunks, groups, rows, width = wide.shape
    features = chunks * rows
    by_rows = lambda w: pl.BlockSpec((rows, w.shape[1]), lambda c: (c, 0))
    return pl.pallas_call(
        weights_out_kernel,
        grid=(chunks,),
        in_specs=[
            pl.BlockSpec((None, groups, rows, width), lambda c: (c, 0, 0, 0)),
            by_rows(wq),
            by_rows(wk),
            by_rows(wv),
            pl.BlockSpec((1, rows), lambda c: (0, c)),
        ],
        out_specs=[
            by_rows(wq),
            by_rows(wk),
            by_rows(wv),
            pl.BlockSpec((1, rows), lambda c: (0, c)),
        ],
        out_shape=[
            jax.ShapeDtypeStruct(wq.shape, f32),
            jax.ShapeDtypeStruct(wk.shape, f32),
            jax.ShapeDtypeStruct(wv.shape, f32),
            jax.ShapeDtypeStruct((1, features), f32),
        ],
        compiler_params=params(32, "arbitrary"),
        cost_estimate=cost(2 * wq.size, 1.6e7),
        name="attention_weights_out",
    )(wide, wq, wk, wv, gain)


def last_kernel(d_ref, wq_ref, wk_ref, wv_ref, x_ref, gain_ref, dmid_ref, out_ref):
    groups, rows, width = d_ref.shape
    pair = width // 2
    dq = jnp.concatenate([d_ref[g, :, :pair] for g in range(groups)], axis=1)
    grad = dot_nt(dq, wq_ref[...])
    keys, vals = [], []
    for at in range(groups // 2):
        a = d_ref[2 * at, :, pair:].astype(f32)
        b = d_ref[2 * at + 1, :, pair:].astype(f32)
        lane = lax.broadcasted_iota(jnp.int32, a.shape, 1)
        keys.append(jnp.where(lane < HEAD_DIM, a, pltpu.roll(b, HEAD_DIM, 1)).astype(bf16))
        vals.append(jnp.where(lane < HEAD_DIM, pltpu.roll(a, HEAD_DIM, 1), b).astype(bf16))
    grad = grad + dot_nt(jnp.concatenate(keys, axis=1), wk_ref[...])
    grad = grad + dot_nt(jnp.concatenate(vals, axis=1), wv_ref[...])
    x = x_ref[...].astype(f32)
    scale = lax.rsqrt(jnp.mean(x * x, axis=-1, keepdims=True) + norm_eps)
    unit = x * scale
    w = gain_ref[...] * grad
    out_ref[...] = dmid_ref[...] + scale * (w - unit * jnp.mean(w * unit, axis=-1, keepdims=True))


def last_call(d, wq, wk, wv, x, gain, dmid):
    rows, features = x.shape
    return pl.pallas_call(
        last_kernel,
        out_shape=jax.ShapeDtypeStruct((rows, features), f32),
        compiler_params=params(40),
        cost_estimate=cost(4 * rows * features * features, 8e6),
        name="input_gradient",
    )(d, wq, wk, wv, x, gain, dmid)


def swap(values, axis, bit):
    return lax.ppermute(values, axis, [(i, i ^ bit) for i in range(lax.axis_size(axis))])


def half_sum(values, axis, bit):
    half = values.shape[0] // 2
    upper = ((lax.axis_index(axis) & bit) > 0).astype(jnp.int32)
    came = swap(lax.dynamic_slice_in_dim(values, (1 - upper) * half, half), axis, bit)
    mine = lax.dynamic_slice_in_dim(values, upper * half, half)
    return (mine.astype(f32) + came.astype(f32)).astype(bf16)


def relative_sum(kept, sent, axis, bits):
    while True:
        kept = (kept.astype(f32) + swap(sent, axis, bits[0]).astype(f32)).astype(bf16)
        bits = bits[1:]
        if not bits:
            return kept
        half = kept.shape[0] // 2
        kept, sent = kept[:half], kept[half:]


def join_parts(stream, axis, bits):
    shape = stream.shape
    for bit in bits[::-1]:
        stream = jnp.stack([stream, swap(stream, axis, bit)])
    return stream.reshape(-1, *shape)


def body(
    layer_input,
    first_gain,
    query_weight,
    key_weight,
    value_weight,
    output_weight,
    second_gain,
    gate_weight,
    up_weight,
    down_weight,
    expert_ids,
    gate_values,
    positions,
    cotangent,
):
    micro, _, per_device, features = layer_input.shape
    devices = lax.axis_size("seq")
    replicas = lax.axis_size("dp")
    seq_place = lax.axis_index("seq")
    rows = micro * per_device
    local_experts = gate_weight.shape[0]
    groups = key_weight.shape[1] // HEAD_DIM
    pair = query_weight.shape[1] // groups
    copies = devices // groups

    dp_bits = [1 << i for i in range(replicas.bit_length() - 1)]

    def spread(blocks):
        if copies > 1:
            blocks = jnp.repeat(blocks, copies, axis=0)
        return lax.all_to_all(blocks, "seq", 0, 0, tiled=True)

    def unspread(blocks):
        return lax.all_to_all(blocks, "seq", 0, 0, tiled=True)[::copies]

    x = layer_input.reshape(rows, features)
    cot = cotangent.reshape(rows, features)
    gain_one = first_gain.reshape(1, features)
    gain_two = second_gain.reshape(1, features)
    pos_all = lax.all_to_all(
        jnp.broadcast_to(positions.reshape(1, rows), (devices, rows)), "seq", 0, 0, tiled=True
    )
    x_all = lax.all_gather(x, "seq", axis=0)
    cos_all, sin_all = rope_tables(pos_all.reshape(-1), pair)
    mine = seq_place * local_experts + jnp.arange(local_experts, dtype=jnp.int32)
    ids = expert_ids[:, 0]
    gates = gate_values[:, 0].astype(f32)
    routed = jnp.sum(
        jnp.where(ids[..., None] == mine, gates[..., None], 0.0), axis=2
    )
    routed = routed.reshape(micro, devices, per_device, local_experts)
    routed = jnp.transpose(routed, (1, 0, 2, 3)).reshape(devices * rows, local_experts)
    group = seq_place // copies
    w_own = jnp.concatenate(
        [
            lax.dynamic_slice_in_dim(query_weight, group * pair, pair, axis=1),
            lax.dynamic_slice_in_dim(key_weight, group * HEAD_DIM, HEAD_DIM, axis=1),
            lax.dynamic_slice_in_dim(value_weight, group * HEAD_DIM, HEAD_DIM, axis=1),
        ],
        axis=1,
    )
    cot_pair = jnp.stack([cot, swap(cot, "seq", 1)])
    cos_all, sin_all, routed, w_own, cot_pair = lax.optimization_barrier(
        (cos_all, sin_all, routed, w_own, cot_pair)
    )
    x_all, cot_then, cos_all, sin_all, routed, w_own, cot_pair = lax.optimization_barrier(
        (x_all, cot, cos_all, sin_all, routed, w_own, cot_pair)
    )
    cot_all = lax.all_gather(cot_then, "seq", axis=0)
    cots = (cot_pair, cot_all)

    qkv, first_all = qkv_call(x_all, gain_one, cos_all, sin_all, w_own)
    qkv = qkv.reshape(devices, micro, per_device, 2 * pair)
    mix, log_total = attend_call(qkv)
    mix = unspread(mix.reshape(devices, rows, pair))
    mixed, middle, second_low = post_call(mix, output_weight, x, gain_two)

    chips = devices // 2
    chip, core = seq_place // 2, seq_place % 2
    onward = [(i, (i + 2) % devices) for i in range(devices)]
    dp_place = lax.axis_index("dp")
    first_bit = dp_place & 1
    last_bit = dp_place >> (len(dp_bits) - 1)
    held, kept, running, places = second_low, (), None, []
    for hop in range(chips):
        following = lax.ppermute(held, "seq", onward) if hop < chips - 1 else None
        other = swap(held, "seq", 1)
        source = 2 * ((chip - hop) % chips)
        near_cot = [jnp.int32(0), jnp.int32(1)] if hop == 0 else [source + core, source + 1 - core]
        place = jnp.stack(
            [source + core, source + 1 - core, 1 - first_bit, 1 - last_bit, *near_cot]
        )
        place = place.astype(jnp.int32)
        places.append(place[:2])
        dx, *kept = expert_call(
            hop, place, held, other, cots[hop > 0], routed, gate_weight, up_weight, down_weight, kept
        )
        if following is not None:
            following, dx = lax.optimization_barrier((following, dx))
        part = dx[0].astype(f32) + swap(dx[1], "seq", 1).astype(f32)
        if hop == 0:
            own_part = part
        else:
            if running is not None:
                part = part + running.astype(f32)
            part = part.astype(bf16)
            if following is not None:
                part, following = lax.optimization_barrier((part, following))
            else:
                part, kept = lax.optimization_barrier((part, kept))
            running = lax.ppermute(part, "seq", onward)
        held = following
    second_grad = (own_part + running.astype(f32)).astype(bf16)
    tokens, hidden_a, hidden_b, gate_low, up_low, slot_a, slot_b = kept

    def weight_parts(at, tokens, hidden_a, hidden_b, gate_low, up_low, slot_a, slot_b):
        pairs = (
            (tokens, gate_low[at]),
            (tokens, up_low[at]),
            (hidden_a[at], slot_a[at]),
            (hidden_b[at], slot_b[at]),
        )
        return [
            lax.dot_general(a, b, TN, preferred_element_type=f32).astype(bf16) for a, b in pairs
        ]

    leaving = weight_parts(0, *kept)
    part_bits = (dp_bits[0], dp_bits[-1], dp_bits[0], dp_bits[-1])
    stream_bits = (dp_bits, dp_bits[::-1])
    came = [swap(values, "dp", bit) for values, bit in zip(leaving, part_bits)]
    leaving, second_grad = lax.optimization_barrier((leaving, second_grad))

    mg_send, proj, middle_grad, gain_two_part = turn_call(
        second_grad, middle, gain_two, cot, output_weight, groups
    )
    mg = spread(mg_send)
    kept, _ = lax.optimization_barrier((kept, mg_send))
    mixed, proj, came[2:] = lax.optimization_barrier((mixed, proj, came[2:]))
    dense = output_weight_call(mixed, proj, gain_two_part, devices)
    dense_own = dense
    staying = weight_parts(1, *kept)
    turned = sum(((dp_place >> i) & 1) << (len(dp_bits) - 1 - i) for i in range(len(dp_bits)))
    part_at = jnp.stack([turned, dp_place]).astype(jnp.int32)
    low_at = jnp.bitwise_and(part_at, replicas // 2 - 1)
    keep_a, send_a, keep_b, send_b = part_sum_call(low_at, replicas // 2, came, staying)
    mg, keep_a, send_a, keep_b, send_b = lax.optimization_barrier(
        (mg, keep_a, send_a, keep_b, send_b)
    )
    streams = [
        relative_sum(keep_a, send_a, "dp", stream_bits[0][1:]),
        relative_sum(keep_b, send_b, "dp", stream_bits[1][1:]),
    ]
    dense = dense_own
    dense = lax.psum_scatter(dense, "seq", scatter_dimension=0)
    table_shape = (devices, micro, per_device, pair)
    dqkv = attend_back_call(
        qkv,
        mg.reshape(devices, micro, per_device, pair),
        log_total,
        cos_all.reshape(table_shape),
        sin_all.reshape(table_shape),
    )
    dqkv, streams = lax.optimization_barrier((dqkv, streams))
    near = [
        [v[0], swap(v[0], "dp", bits[-1])] for v, bits in zip(streams, stream_bits)
    ]
    back = unspread(dqkv.reshape(devices, rows, 2 * pair))
    d_all = dqkv.reshape(devices * rows, 2 * pair)
    first_tokens = first_all.reshape(devices * rows, features)
    part = lax.dot_general(first_tokens, d_all, TN, preferred_element_type=f32)
    dense = dense.reshape(dense.shape[-2], features)
    each = output_weight.shape[0] // devices
    if copies == 1:
        width = 2 * pair
        kept_pieces, sent_pieces = joint_call(part_at, part, dense, replicas)
        first = [
            kept_pieces[at].astype(f32) + swap(sent_pieces[at], "dp", bits[0]).astype(f32)
            for at, bits in enumerate(stream_bits)
        ]
        kept, sent_pieces = lax.optimization_barrier((kept, sent_pieces))
        moe_place = jnp.concatenate(places + [(1 - first_bit).astype(jnp.int32).reshape(1)])
        moe_all = moe_call(moe_place, kept[1], routed, down_weight, devices)
        first, near, moe_all = lax.optimization_barrier(
            ([v.astype(bf16) for v in first], near, moe_all)
        )
        own = [
            relative_sum(v[: replicas // 4], v[replicas // 4 :], "dp", bits[1:])
            for v, bits in zip(first, stream_bits)
        ]
        own = jnp.concatenate(own, axis=0)
        own, back, here = lax.optimization_barrier((own, back, [v[0] for v in near]))
        far = [swap(v, "dp", bits[-2]) for v, bits in zip(here, stream_bits)]
        backward = [(i, (i - 2) % devices) for i in range(devices)]
        round_ring = {0: own}
        for k in range(1, chips // 2 + 1):
            round_ring[k] = lax.ppermute(round_ring[k - 1], "seq", onward)
            if chips - k > k:
                round_ring[chips - k] = lax.ppermute(
                    round_ring[(chips - k + 1) % chips], "seq", backward
                )
            if k == 1:
                round_ring, coming = lax.optimization_barrier(
                    (round_ring, [v[1] for v in near])
                )
        held = jnp.stack([round_ring[k] for k in range(chips)])
        passed = [swap(v, "dp", bits[-2]) for v, bits in zip(coming, stream_bits)]
        moe_all, far, _ = lax.optimization_barrier((moe_all, far, round_ring[chips // 2]))
        held, passed = lax.optimization_barrier((held, passed))
        moe = lax.psum_scatter(moe_all, "seq", scatter_dimension=0)
        layer_output = (middle + residual_scale * moe.astype(f32)).astype(bf16)
    else:
        far = [swap(v[0], "dp", bits[-2]) for v, bits in zip(streams, stream_bits)]
        passed = [swap(v[1], "dp", bits[-2]) for v, bits in zip(near, stream_bits)]
    expert_pieces = []
    for (here, first), second, third, bits in zip(near, far, passed, stream_bits):
        pieces = [here, first, second, third]
        for bit in bits[:-2][::-1]:
            pieces = pieces + [swap(p, "dp", bit) for p in pieces]
        expert_pieces.append(pieces)
    input_grad = last_call(
        back, query_weight, key_weight, value_weight, x, gain_one, middle_grad
    )
    if copies == 1:
        gate_sum, up_sum, down_sum = expert_out_call(
            part_at, *expert_pieces, gate_weight.shape, down_weight.shape
        )
        full = [[held[:, at], swap(held[:, at], "dp", b[-1])] for at, b in enumerate(stream_bits)]
        beside = [swap(v[0], "dp", bits[-2]) for v, bits in zip(full, stream_bits)]
        full, beside = lax.optimization_barrier((full, beside))
        for at, bits in enumerate(stream_bits):
            full[at] += [beside[at], swap(full[at][1], "dp", bits[-2])]
            for bit in bits[:-2][::-1]:
                full[at] += [swap(p, "dp", bit) for p in full[at]]
        ends = [pieces.pop() for pieces in full]
        ends, gate_sum, up_sum, down_sum, input_grad = lax.optimization_barrier(
            (ends, gate_sum, up_sum, down_sum, input_grad)
        )
        full = [pieces + [end] for pieces, end in zip(full, ends)]
        other = [[swap(p, "seq", 1) for p in pieces] for pieces in full]
        where_at = jnp.stack([turned, dp_place, chip, core]).astype(jnp.int32)
        (
            query_weight_grad,
            key_weight_grad,
            value_weight_grad,
            first_gain_grad,
            output_weight_grad,
            second_gain_grad,
        ) = dense_out_call(
            where_at, full, other, query_weight, key_weight, value_weight, gain_one, output_weight.shape
        )
    else:
        gate_sum, up_sum, down_sum = expert_out_call(
            part_at, *expert_pieces, gate_weight.shape, down_weight.shape
        )
        for bit in dp_bits:
            dense = (dense.astype(f32) + swap(dense, "dp", bit).astype(f32)).astype(bf16)
        dense = lax.all_gather(dense, "seq", axis=0).astype(f32)
        output_weight_grad = dense[:, :each].reshape(output_weight.shape)
        moe_place = jnp.concatenate(places + [(1 - first_bit).astype(jnp.int32).reshape(1)])
        moe_all = moe_call(moe_place, kept[1], routed, down_weight, devices)
        moe = lax.psum_scatter(moe_all, "seq", scatter_dimension=0)
        layer_output = (middle + residual_scale * moe.astype(f32)).astype(bf16)
        second_gain_grad = dense[0, each]
        part = part.astype(bf16)
        for bit in dp_bits[::-1]:
            part = half_sum(part, "dp", bit)
        wide = lax.all_gather(part, ("dp", "seq"), axis=0)
        wide = wide.reshape(replicas, devices, features // replicas, 2 * pair)[:, ::copies]
        query_weight_grad, key_weight_grad, value_weight_grad, first_gain_grad = weights_out_call(
            wide, query_weight, key_weight, value_weight, gain_one
        )
    second_gain_grad = second_gain_grad.reshape(features)
    return (
        layer_output.reshape(layer_input.shape),
        input_grad.reshape(layer_input.shape),
        first_gain_grad.reshape(features),
        query_weight_grad,
        key_weight_grad,
        value_weight_grad,
        output_weight_grad,
        second_gain_grad,
        gate_sum,
        up_sum,
        down_sum,
    )


def solution(mesh):
    return jax.shard_map(
        body,
        mesh=mesh,
        in_specs=(
            P(None, "dp", "seq", None),
            P(),
            P(),
            P(),
            P(),
            P(),
            P(),
            P("seq", None, None),
            P("seq", None, None),
            P("seq", None, None),
            P(None, "dp", None, None),
            P(None, "dp", None, None),
            P(None, "dp", "seq"),
            P(None, "dp", "seq", None),
        ),
        out_specs=(
            P(None, "dp", "seq", None),
            P(None, "dp", "seq", None),
            P(),
            P(),
            P(),
            P(),
            P(),
            P(),
            P("seq", None, None),
            P("seq", None, None),
            P("seq", None, None),
        ),
        check_vma=False,
    )
```

```python
from functools import partial

import jax
import jax.numpy as jnp
from jax import lax
from jax.experimental import pallas as pl
from jax.experimental.pallas import tpu as pltpu
from jax.sharding import PartitionSpec as P

HEAD_DIM = 64

rope_theta = 10000.0
attention_scale = 0.015625
residual_scale = 0.22
norm_eps = 1e-06
masked_score = -1e30

f32 = jnp.float32
bf16 = jnp.bfloat16
NT = (((1,), (1,)), ((), ()))
TN = (((0,), (0,)), ((), ()))


def dot(a, b):
    return jnp.dot(a, b, preferred_element_type=f32)


def dot_nt(a, b):
    return lax.dot_general(a, b, NT, preferred_element_type=f32)


def params(mib, *semantics):
    return pltpu.CompilerParams(
        vmem_limit_bytes=mib * 1024 * 1024, dimension_semantics=semantics or None
    )


def cost(flops, nbytes, trans=0):
    return pl.CostEstimate(
        flops=int(flops / 8), bytes_accessed=int(nbytes / 8), transcendentals=int(trans / 8)
    )


def whole(shape):
    return pl.BlockSpec(shape, lambda *_: (0,) * len(shape))


def rope_tables(positions, width):
    half = HEAD_DIM // 2
    exponent = jnp.arange(half, dtype=f32) * (-2.0 / HEAD_DIM)
    angles = positions.astype(f32)[:, None] * (rope_theta**exponent)[None, :]
    cosine, sine = jnp.cos(angles), jnp.sin(angles)
    copies = width // HEAD_DIM
    cos_row = jnp.concatenate([cosine, cosine] * copies, axis=1)
    sin_row = jnp.concatenate([-sine, sine] * copies, axis=1)
    return cos_row, sin_row


def partner(values):
    width = values.shape[1]
    half = HEAD_DIM // 2
    lane = lax.broadcasted_iota(jnp.int32, values.shape, 1)
    ahead = pltpu.roll(values, width - half, 1)
    behind = pltpu.roll(values, half, 1)
    return jnp.where(lane % HEAD_DIM < half, ahead, behind)


def qkv_kernel(x_ref, gain_ref, cos_ref, sin_ref, w_ref, qkv_ref, low_ref):
    pair = 2 * HEAD_DIM
    x = x_ref[0].astype(f32)
    scale = lax.rsqrt(jnp.mean(x * x, axis=-1, keepdims=True) + norm_eps)
    low = (x * scale * gain_ref[...]).astype(bf16)
    low_ref[0] = low
    cosine, sine = cos_ref[...], sin_ref[...]
    made = dot(low, w_ref[...])
    q, kv = made[:, :pair], made[:, pair:]
    q = (q * cosine + partner(q) * sine) * attention_scale
    qkv_ref[0, :, :pair] = q.astype(bf16)
    lane = lax.broadcasted_iota(jnp.int32, kv.shape, 1)
    turned = kv * cosine + partner(kv) * sine
    qkv_ref[0, :, pair:] = jnp.where(lane < HEAD_DIM, turned, kv).astype(bf16)


def qkv_call(x_all, gain, cos_all, sin_all, w_own):
    blocks, rows, features = x_all.shape
    pair = 2 * HEAD_DIM
    return pl.pallas_call(
        qkv_kernel,
        grid=(blocks,),
        in_specs=[
            pl.BlockSpec((1, rows, features), lambda s: (s, 0, 0)),
            whole((1, features)),
            pl.BlockSpec((rows, pair), lambda s: (s, 0)),
            pl.BlockSpec((rows, pair), lambda s: (s, 0)),
            whole(w_own.shape),
        ],
        out_specs=[
            pl.BlockSpec((1, rows, 2 * pair), lambda s: (s, 0, 0)),
            pl.BlockSpec((1, rows, features), lambda s: (s, 0, 0)),
        ],
        out_shape=[
            jax.ShapeDtypeStruct((blocks, rows, 2 * pair), bf16),
            jax.ShapeDtypeStruct((blocks, rows, features), bf16),
        ],
        compiler_params=params(58, "arbitrary"),
        cost_estimate=cost(4 * blocks * rows * features * pair, 14e6),
        name="norm_qkv_rope",
    )(x_all, gain, cos_all, sin_all, w_own)


def split_heads(block, first):
    wide = block.astype(f32)
    lane = lax.broadcasted_iota(jnp.int32, wide.shape, 1)
    turned = pltpu.roll(wide, HEAD_DIM, 1)
    if first:
        parts = [jnp.where(lane < HEAD_DIM, wide, 0.0), jnp.where(lane < HEAD_DIM, turned, 0.0)]
    else:
        parts = [jnp.where(lane >= HEAD_DIM, turned, 0.0), jnp.where(lane >= HEAD_DIM, wide, 0.0)]
    return jnp.concatenate(parts, axis=0).astype(bf16)


def join_heads(turned):
    rows = turned.shape[1] // 2
    return jnp.transpose(jnp.concatenate([turned[:, :rows], turned[:, rows:]], axis=0))


def scores_of(kv, q2, rows):
    scores = dot_nt(kv, q2)
    count = scores.shape[0]
    own = scores[count - rows :]
    key_at = lax.broadcasted_iota(jnp.int32, own.shape, 0)
    query_at = lax.broadcasted_iota(jnp.int32, own.shape, 1) % rows
    own = jnp.where(key_at <= query_at, own, masked_score)
    if count == rows:
        return own
    return jnp.concatenate([scores[: count - rows], own], axis=0)


def attend_kernel(qkv_ref, out_ref, log_ref):
    blocks, _, rows, width = qkv_ref.shape
    pair = width // 2
    kv = qkv_ref[:, 0, :, pair:].reshape(blocks * rows, pair)
    kv_t = jnp.transpose(kv)
    for at in range(blocks):
        count = (at + 1) * rows
        q2 = split_heads(qkv_ref[at, 0, :, :pair], True)
        scores = scores_of(kv[:count], q2, rows)
        top = jnp.max(scores, axis=0, keepdims=True)
        weights = jnp.exp(scores - top)
        total = jnp.sum(weights, axis=0, keepdims=True)
        out_t = dot(kv_t[:, :count], weights.astype(bf16))
        out_ref[at, 0] = join_heads(out_t[HEAD_DIM:] / total).astype(bf16)
        log_ref[at, 0] = top + jnp.log(total)


def attend_call(qkv):
    blocks, micro, rows, width = qkv.shape
    pair = width // 2
    length = blocks * rows
    return pl.pallas_call(
        attend_kernel,
        grid=(micro,),
        in_specs=[pl.BlockSpec((blocks, 1, rows, width), lambda m: (0, m, 0, 0))],
        out_specs=[
            pl.BlockSpec((blocks, 1, rows, pair), lambda m: (0, m, 0, 0)),
            pl.BlockSpec((blocks, 1, 1, 2 * rows), lambda m: (0, m, 0, 0)),
        ],
        out_shape=[
            jax.ShapeDtypeStruct((blocks, micro, rows, pair), bf16),
            jax.ShapeDtypeStruct((blocks, micro, 1, 2 * rows), f32),
        ],
        compiler_params=params(48, "arbitrary"),
        cost_estimate=cost(
            micro * length * length * 512, 3 * qkv.size, micro * length * length
        ),
        name="attention_forward",
    )(qkv)


def attend_back_kernel(qkv_ref, grad_ref, log_ref, cos_ref, sin_ref, out_ref, dkv_ref):
    blocks, _, rows, width = qkv_ref.shape
    pair = width // 2
    kv = qkv_ref[:, 0, :, pair:].reshape(blocks * rows, pair)
    kv_t = jnp.transpose(kv)
    dkv_ref[...] = jnp.zeros_like(dkv_ref)
    for at in range(blocks):
        count = (at + 1) * rows
        q2 = split_heads(qkv_ref[at, 0, :, :pair], True)
        g2 = split_heads(grad_ref[at, 0], False)
        scores = scores_of(kv[:count], q2, rows)
        prob = jnp.exp(scores - log_ref[at, 0])
        prob_grad = dot_nt(kv[:count], g2)
        delta = jnp.sum(prob * prob_grad, axis=0, keepdims=True)
        score_grad = (prob * (prob_grad - delta)).astype(bf16)
        dkv_ref[:count] += dot(score_grad, q2) + dot(prob.astype(bf16), g2)
        dq_t = dot(kv_t[:, :count], score_grad)
        dq = join_heads(dq_t[:HEAD_DIM] * attention_scale)
        dq = dq * cos_ref[at, 0] - partner(dq) * sin_ref[at, 0]
        out_ref[at, 0, :, :pair] = dq.astype(bf16)
    for at in range(blocks):
        dkv = dkv_ref[at * rows : (at + 1) * rows]
        lane = lax.broadcasted_iota(jnp.int32, dkv.shape, 1)
        turned = dkv * cos_ref[at, 0] - partner(dkv) * sin_ref[at, 0]
        out_ref[at, 0, :, pair:] = jnp.where(lane < HEAD_DIM, turned, dkv).astype(bf16)


def attend_back_call(qkv, grads, log_total, cos_all, sin_all):
    blocks, micro, rows, width = qkv.shape
    pair = width // 2
    length = blocks * rows
    spec = lambda lanes: pl.BlockSpec((blocks, 1, rows, lanes), lambda m: (0, m, 0, 0))
    return pl.pallas_call(
        attend_back_kernel,
        grid=(micro,),
        in_specs=[
            spec(width),
            spec(pair),
            pl.BlockSpec((blocks, 1, 1, 2 * rows), lambda m: (0, m, 0, 0)),
            spec(pair),
            spec(pair),
        ],
        out_specs=spec(width),
        out_shape=jax.ShapeDtypeStruct(qkv.shape, bf16),
        scratch_shapes=[pltpu.VMEM((length, pair), f32)],
        compiler_params=params(56, "arbitrary"),
        cost_estimate=cost(
            micro * length * length * 1280, 10 * qkv.size, micro * length * length
        ),
        name="attention_backward",
    )(qkv, grads, log_total, cos_all, sin_all)


def post_kernel(mix_ref, wo_ref, x_ref, gain_ref, mixed_ref, middle_ref, low_ref):
    mixed = jnp.concatenate([mix_ref[g] for g in range(mix_ref.shape[0])], axis=1)
    mixed_ref[...] = mixed
    middle = x_ref[...].astype(f32) + residual_scale * dot(mixed, wo_ref[...])
    middle_ref[...] = middle
    scale = lax.rsqrt(jnp.mean(middle * middle, axis=-1, keepdims=True) + norm_eps)
    low_ref[...] = (middle * scale * gain_ref[...]).astype(bf16)


def post_call(mix, wo, x, gain):
    rows, features = x.shape
    return pl.pallas_call(
        post_kernel,
        out_shape=[
            jax.ShapeDtypeStruct((rows, wo.shape[0]), bf16),
            jax.ShapeDtypeStruct((rows, features), f32),
            jax.ShapeDtypeStruct((rows, features), bf16),
        ],
        compiler_params=params(32),
        cost_estimate=cost(2 * rows * wo.size, 5e6),
        name="project_norm",
    )(mix, wo, x, gain)


def expert_kernel(place_ref, a_ref, b_ref, cot_ref, w_ref, wg_ref, wu_ref, wd_ref, *refs):
    dx_ref, x_ref, ha_ref, hb_ref, dg_ref, du_ref, sa_ref, sb_ref = refs[-8:]
    step = pl.program_id(0)
    first, second = place_ref[2], place_ref[3]
    half = sa_ref.shape[2]

    @pl.when(step == 0)
    def _():
        x_ref[...] = a_ref[...]

    @pl.when(step == 1)
    def _():
        x_ref[...] = b_ref[...]

    x = x_ref[...]
    cot = cot_ref[0].astype(f32)
    weight = residual_scale * w_ref[...]
    total = None
    for e in range(wg_ref.shape[0]):
        gate = dot(x, wg_ref[e])
        up = dot(x, wu_ref[e])
        slot_grad = (weight[:, e : e + 1] * cot).astype(bf16)
        to_a, to_b = jnp.bitwise_xor(first, e), jnp.bitwise_xor(second, e)
        sa_ref[to_a] = slot_grad[:, :half]
        sb_ref[to_b] = slot_grad[:, half:]
        hidden_grad = dot_nt(slot_grad, wd_ref[e])
        sig = 0.5 * jnp.tanh(0.5 * gate) + 0.5
        silu = gate * sig
        hidden = (silu * up).astype(bf16)
        ha_ref[to_a] = hidden
        hb_ref[to_b] = hidden
        gate_grad = (hidden_grad * up * (sig + silu * (1.0 - sig))).astype(bf16)
        up_grad = (hidden_grad * silu).astype(bf16)
        dg_ref[to_a] = gate_grad
        du_ref[to_b] = up_grad
        term = dot_nt(gate_grad, wg_ref[e]) + dot_nt(up_grad, wu_ref[e])
        total = term if total is None else total + term
    dx_ref[0] = total.astype(bf16)


def expert_call(at, place, own, other, cots, weight, wg, wu, wd, kept):
    rows, features = own.shape
    count, _, hidden = wg.shape
    tokens = weight.shape[0]
    inner = jax.ShapeDtypeStruct((count, tokens, hidden), bf16)
    outer = jax.ShapeDtypeStruct((count, tokens, features // 2), bf16)
    inner_spec = pl.BlockSpec((count, rows, hidden), lambda s, place: (0, 2 * at + s, 0))
    outer_spec = pl.BlockSpec((count, rows, features // 2), lambda s, place: (0, 2 * at + s, 0))
    fixed = lambda shape: pl.BlockSpec(shape, lambda s, place: (0,) * len(shape))
    any_spec = pl.BlockSpec(memory_space=pl.ANY)
    first = 8
    return pl.pallas_call(
        expert_kernel,
        grid_spec=pltpu.PrefetchScalarGridSpec(
            num_scalar_prefetch=1,
            grid=(2,),
            in_specs=[
                fixed((rows, features)),
                fixed((rows, features)),
                pl.BlockSpec((1, rows, features), lambda s, place: (place[4 + s], 0, 0)),
                pl.BlockSpec((rows, count), lambda s, place: (place[s], 0)),
                fixed(wg.shape),
                fixed(wu.shape),
                fixed(wd.shape),
            ]
            + [any_spec] * len(kept),
            out_specs=[
                pl.BlockSpec((1, rows, features), lambda s, place: (s, 0, 0)),
                pl.BlockSpec((rows, features), lambda s, place: (2 * at + s, 0)),
            ]
            + [inner_spec] * 4
            + [outer_spec] * 2,
        ),
        out_shape=[
            jax.ShapeDtypeStruct((2, rows, features), bf16),
            jax.ShapeDtypeStruct((tokens, features), bf16),
            inner,
            inner,
            inner,
            inner,
            outer,
            outer,
        ],
        input_output_aliases={first + i: 1 + i for i in range(len(kept))},
        compiler_params=params(48, "arbitrary"),
        cost_estimate=cost(20 * rows * wg.size, 2e7, 2 * rows * hidden * count),
        name="experts",
    )(place, own, other, cots, weight, wg, wu, wd, *kept)


def part_sum_kernel(at_ref, *refs):
    inputs, outs = refs[:16], refs[16:]
    at = 0
    for out in outs:
        gate_came, gate_here, down_came, down_here = inputs[at : at + 4]
        rows = gate_came.shape[0]
        out[0, :rows] = (gate_came[...].astype(f32) + gate_here[...].astype(f32)).astype(bf16)
        out[0, rows:] = (down_came[...].astype(f32) + down_here[...].astype(f32)).astype(bf16)
        at += 4


def part_sum_call(at, per, came, here):
    gate_rows, down_rows = came[0].shape[0] // per, came[2].shape[0] // per
    width = came[0].shape[1]
    steps = per // 2
    specs, args, out_specs, out_shapes = [], [], [], []
    for stream in range(2):
        for sent in range(2):
            for which, rows in ((stream, gate_rows), (stream + 2, down_rows)):
                spec = pl.BlockSpec(
                    (rows, width),
                    lambda s, at, sent=sent, stream=stream: (
                        jnp.bitwise_xor(s + sent * steps, at[stream]),
                        0,
                    ),
                )
                specs += [spec, spec]
                args += [came[which], here[which]]
            out_specs.append(
                pl.BlockSpec((1, gate_rows + down_rows, width), lambda s, at: (s, 0, 0))
            )
            out_shapes.append(
                jax.ShapeDtypeStruct((steps, gate_rows + down_rows, width), bf16)
            )
    return pl.pallas_call(
        part_sum_kernel,
        grid_spec=pltpu.PrefetchScalarGridSpec(
            num_scalar_prefetch=1, grid=(steps,), in_specs=specs, out_specs=out_specs
        ),
        out_shape=out_shapes,
        compiler_params=params(60, "arbitrary"),
        cost_estimate=cost(0, 9e6),
        name="expert_part_sum",
    )(at, *args)


def joint_kernel(at_ref, *refs):
    for (part_ref, wo_ref, gain_ref), out_ref in ((refs[:3], refs[6]), (refs[3:6], refs[7])):
        rows = part_ref.shape[0]
        upto = rows + wo_ref.shape[0]
        out_ref[0, 0, :rows] = part_ref[...].astype(bf16)
        out_ref[0, 0, rows:upto] = wo_ref[...]
        out_ref[0, 0, upto:] = gain_ref[...]


def joint_call(at, part, dense, parts):
    features, width = part.shape
    pieces = 2 * parts
    rows = features // pieces
    block_cols = dense.shape[1] // width
    per_block = pieces // block_cols
    extra = 16
    wo_rows = (dense.shape[0] - extra) // per_block
    last = dense.shape[0] // extra - 1
    steps = parts // 2

    def piece(sent):
        return lambda s, p, at: s * parts + jnp.bitwise_xor(p + sent * steps, at[s])

    specs = []
    for sent in range(2):
        at_piece = piece(sent)
        specs.append(
            pl.BlockSpec((rows, width), lambda s, p, at, f=at_piece: (f(s, p, at), 0))
        )
        specs.append(
            pl.BlockSpec(
                (wo_rows, width),
                lambda s, p, at, f=at_piece: (
                    lax.rem(f(s, p, at), per_block),
                    lax.div(f(s, p, at), per_block),
                ),
            )
        )
        specs.append(
            pl.BlockSpec(
                (extra, width), lambda s, p, at, f=at_piece: (last, lax.div(f(s, p, at), per_block))
            )
        )
    out_spec = pl.BlockSpec((1, 1, rows + wo_rows + extra, width), lambda s, p, at: (s, p, 0, 0))
    out_shape = jax.ShapeDtypeStruct((2, steps, rows + wo_rows + extra, width), bf16)
    return pl.pallas_call(
        joint_kernel,
        grid_spec=pltpu.PrefetchScalarGridSpec(
            num_scalar_prefetch=1, grid=(2, steps), in_specs=specs, out_specs=[out_spec] * 2
        ),
        out_shape=[out_shape] * 2,
        compiler_params=params(32, "arbitrary", "arbitrary"),
        cost_estimate=cost(0, 2e6),
        name="dense_pieces",
    )(at, part, dense, dense, part, dense, dense)


def expert_out_kernel(at_ref, *refs):
    pieces, (gate_ref, up_ref, down_ref) = refs[:-3], refs[-3:]
    parts = len(pieces) // 2
    step = pl.program_id(0)
    rows = gate_ref.shape[1]
    half = down_ref.shape[2] // 2
    for which in range(parts):

        @pl.when(jnp.bitwise_xor(step, at_ref[0]) == which)
        def _():
            a_ref = pieces[which]
            gate_ref[0] = a_ref[:rows].astype(f32)
            down_ref[0, :, :half] = a_ref[rows:].astype(f32)

        @pl.when(jnp.bitwise_xor(step, at_ref[1]) == which)
        def _():
            b_ref = pieces[parts + which]
            up_ref[0] = b_ref[:rows].astype(f32)
            down_ref[0, :, half:] = b_ref[rows:].astype(f32)


def expert_out_call(at, a, b, gate_shape, down_shape):
    parts = len(a)
    held, width = a[0].shape
    count = gate_shape[0]
    per = parts // count
    gate_rows, down_rows = gate_shape[1] // per, down_shape[1] // per
    place = lambda r, at: (lax.div(r, per), lax.rem(r, per), 0)
    return pl.pallas_call(
        expert_out_kernel,
        grid_spec=pltpu.PrefetchScalarGridSpec(
            num_scalar_prefetch=1,
            grid=(parts,),
            in_specs=[pl.BlockSpec((held, width), lambda r, at: (0, 0))] * (2 * parts),
            out_specs=[
                pl.BlockSpec((1, gate_rows, gate_shape[2]), place),
                pl.BlockSpec((1, gate_rows, gate_shape[2]), place),
                pl.BlockSpec((1, down_rows, down_shape[2]), place),
            ],
        ),
        out_shape=[
            jax.ShapeDtypeStruct(gate_shape, f32),
            jax.ShapeDtypeStruct(gate_shape, f32),
            jax.ShapeDtypeStruct(down_shape, f32),
        ],
        compiler_params=params(40, "arbitrary"),
        cost_estimate=cost(0, 2e7),
        name="expert_weights_out",
    )(at, *a, *b)


def moe_kernel(place_ref, h_ref, w_ref, wd_ref, out_ref):
    weight = w_ref[...]
    total = None
    first = place_ref[pl.num_programs(0)]
    for e in range(wd_ref.shape[0]):
        term = weight[:, e : e + 1] * dot(h_ref[jnp.bitwise_xor(first, e)], wd_ref[e])
        total = term if total is None else total + term
    out_ref[0] = total.astype(bf16)


def moe_call(place, hidden, weight, wd, blocks):
    count, tokens, inner = hidden.shape
    features = wd.shape[2]
    rows = tokens // blocks
    return pl.pallas_call(
        moe_kernel,
        grid_spec=pltpu.PrefetchScalarGridSpec(
            num_scalar_prefetch=1,
            grid=(blocks,),
            in_specs=[
                pl.BlockSpec((count, rows, inner), lambda s, place: (0, s, 0)),
                pl.BlockSpec((rows, count), lambda s, place: (place[s], 0)),
                pl.BlockSpec(wd.shape, lambda s, place: (0, 0, 0)),
            ],
            out_specs=pl.BlockSpec((1, rows, features), lambda s, place: (place[s], 0, 0)),
        ),
        out_shape=jax.ShapeDtypeStruct((blocks, rows, features), bf16),
        compiler_params=params(60, "arbitrary"),
        cost_estimate=cost(2 * tokens * wd.size, 1.1e7),
        name="expert_outputs",
    )(place, hidden, weight, wd)


def turn_kernel(sg_ref, middle_ref, gain_ref, cot_ref, wo_ref, mg_ref, proj_ref, dmid_ref, dgain_ref):
    grad = sg_ref[...].astype(f32)
    middle = middle_ref[...]
    scale = lax.rsqrt(jnp.mean(middle * middle, axis=-1, keepdims=True) + norm_eps)
    unit = middle * scale
    dgain_ref[...] = jnp.sum(grad * unit, axis=0, keepdims=True)
    w = gain_ref[...] * grad
    dmid = cot_ref[...].astype(f32) + scale * (w - unit * jnp.mean(w * unit, axis=-1, keepdims=True))
    dmid_ref[...] = dmid
    proj = (residual_scale * dmid).astype(bf16)
    proj_ref[...] = proj
    mixed_grad = dot_nt(proj, wo_ref[...]).astype(bf16)
    groups, _, pair = mg_ref.shape
    for g in range(groups):
        mg_ref[g] = mixed_grad[:, g * pair : (g + 1) * pair]


def turn_call(sg, middle, gain, cot, wo, groups):
    rows, features = middle.shape
    pair = wo.shape[0] // groups
    return pl.pallas_call(
        turn_kernel,
        out_shape=[
            jax.ShapeDtypeStruct((groups, rows, pair), bf16),
            jax.ShapeDtypeStruct((rows, features), bf16),
            jax.ShapeDtypeStruct((rows, features), f32),
            jax.ShapeDtypeStruct((1, features), f32),
        ],
        compiler_params=params(32),
        cost_estimate=cost(2 * rows * wo.size, 6e6),
        name="norm_back_project_back",
    )(sg, middle, gain, cot, wo)


def output_weight_kernel(mixed_ref, proj_ref, dgain_ref, out_ref):
    held, each, features = out_ref.shape
    rows = mixed_ref.shape[1] // held
    part = lax.dot_general(mixed_ref[...], proj_ref[...], TN, preferred_element_type=f32)
    extra = jnp.broadcast_to(dgain_ref[...], (each - rows, features)).astype(bf16)
    for at in range(held):
        out_ref[at, :rows] = part[at * rows : (at + 1) * rows].astype(bf16)
        out_ref[at, rows:] = extra


def output_weight_call(mixed, proj, dgain, parts):
    rows, width = mixed.shape
    features = proj.shape[1]
    each = width // parts
    lanes = max(each, width // 2)
    held = lanes // each
    return pl.pallas_call(
        output_weight_kernel,
        grid=(parts // held,),
        in_specs=[
            pl.BlockSpec((rows, lanes), lambda s: (0, s)),
            whole((rows, features)),
            whole((1, features)),
        ],
        out_specs=pl.BlockSpec((held, each + 16, features), lambda s: (s, 0, 0)),
        out_shape=jax.ShapeDtypeStruct((parts, each + 16, features), bf16),
        compiler_params=params(32, "arbitrary"),
        cost_estimate=cost(2 * rows * width * features, 4e6),
        name="output_weight_part",
    )(mixed, proj, dgain)


def dense_out_kernel(at_ref, *refs):
    held, refs = refs[:-16], refs[-16:]
    middle_ref, moe_ref, *refs = refs
    layer_ref = refs.pop(10)
    layer = middle_ref[...] + residual_scale * moe_ref[...].astype(f32)
    layer_ref[...] = layer.astype(bf16)
    wq_ref, wk_ref, wv_ref, gain_ref, dq_ref, dk_ref, dv_ref, dg_ref, wo_ref, dg2_ref = refs[:10]
    own_ref, other_ref = refs[10:12]
    parts = len(held) // 4
    stream, step = pl.program_id(0), pl.program_id(1)
    chips, _, width = own_ref.shape
    rows = dq_ref.shape[0]
    pair = width // 2
    chip, core = at_ref[2], at_ref[3]
    for which in range(2):
        for rel in range(parts):

            @pl.when((stream == which) & (jnp.bitwise_xor(step, at_ref[which]) == rel))
            def _():
                own_ref[...] = held[which * parts + rel][...]
                other_ref[...] = held[(2 + which) * parts + rel][...]

    total = jnp.zeros((rows, pair), f32)
    for k in range(chips):
        source = lax.rem(chip - k + chips, chips)
        a = jnp.where(core == 0, own_ref[k], other_ref[k]).astype(f32)
        b = jnp.where(core == 0, other_ref[k], own_ref[k]).astype(f32)
        q = jnp.concatenate([a[:rows, :pair], b[:rows, :pair]], axis=1)
        cols = pl.ds(pl.multiple_of(source * width, width), width)
        dq_ref[:, cols] = q
        made = q * wq_ref[:, cols].astype(f32)
        total += made[:, :pair] + made[:, pair:]
        a_kv, b_kv = a[:rows, pair:], b[:rows, pair:]
        lane = lax.broadcasted_iota(jnp.int32, a_kv.shape, 1)
        key = jnp.where(lane < HEAD_DIM, a_kv, pltpu.roll(b_kv, HEAD_DIM, 1))
        val = jnp.where(lane < HEAD_DIM, pltpu.roll(a_kv, HEAD_DIM, 1), b_kv)
        cols = pl.ds(pl.multiple_of(source * pair, pair), pair)
        dk_ref[:, cols] = key
        dv_ref[:, cols] = val
        total += key * wk_ref[:, cols].astype(f32) + val * wv_ref[:, cols].astype(f32)
        wo_ref[2 * source, 0] = a[rows : rows + wo_ref.shape[2]]
        wo_ref[2 * source + 1, 0] = b[rows : rows + wo_ref.shape[2]]
        if k == 0:
            dg2_ref[...] = a[rows + wo_ref.shape[2] :][:1]
    dg_ref[...] = jnp.sum(jnp.transpose(total), axis=0, keepdims=True) / gain_ref[...]


def dense_out_call(at, own, other, middle, moe, wq, wk, wv, gain, wo_shape):
    held = [*own[0], *own[1], *other[0], *other[1]]
    streams, parts = 2, len(own[0])
    chips, depth, width = held[0].shape
    features = wq.shape[0]
    groups = 2 * chips
    rows = features // (streams * parts)
    block_cols = wo_shape[1] // width
    per_block = streams * parts // block_cols
    wo_rows = wo_shape[0] // groups // per_block
    by_rows = lambda w: pl.BlockSpec((rows, w.shape[1]), lambda s, r, at: (s * parts + r, 0))
    gain_spec = pl.BlockSpec((1, rows), lambda s, r, at: (0, s * parts + r))
    tokens = middle.shape[0]
    token_spec = pl.BlockSpec(
        (tokens // (streams * parts), features), lambda s, r, at: (s * parts + r, 0)
    )
    outs = pl.pallas_call(
        dense_out_kernel,
        grid_spec=pltpu.PrefetchScalarGridSpec(
            num_scalar_prefetch=1,
            grid=(streams, parts),
            in_specs=[pl.BlockSpec(memory_space=pltpu.VMEM)] * len(held)
            + [token_spec, token_spec, by_rows(wq), by_rows(wk), by_rows(wv), gain_spec],
            out_specs=[
                by_rows(wq),
                by_rows(wk),
                by_rows(wv),
                gain_spec,
                pl.BlockSpec(
                    (groups, 1, wo_rows, width),
                    lambda s, r, at: (
                        0,
                        lax.rem(s * parts + r, per_block),
                        0,
                        lax.div(s * parts + r, per_block),
                    ),
                ),
                pl.BlockSpec((1, width), lambda s, r, at: (0, lax.div(s * parts + r, per_block))),
                token_spec,
            ],
            scratch_shapes=[pltpu.VMEM((chips, depth, width), bf16)] * 2
            + [pltpu.VMEM((8, 128), f32)],
        ),
        out_shape=[
            jax.ShapeDtypeStruct(wq.shape, f32),
            jax.ShapeDtypeStruct(wk.shape, f32),
            jax.ShapeDtypeStruct(wv.shape, f32),
            jax.ShapeDtypeStruct((1, features), f32),
            jax.ShapeDtypeStruct((groups, per_block, wo_rows, wo_shape[1]), f32),
            jax.ShapeDtypeStruct((1, wo_shape[1]), f32),
            jax.ShapeDtypeStruct((tokens, features), bf16),
        ],
        compiler_params=params(28, "arbitrary", "arbitrary"),
        cost_estimate=cost(2 * wq.size, 2.4e7),
        name="dense_weights_out",
    )(at, *held, middle, moe, wq, wk, wv, gain)
    return (*outs[:4], outs[4].reshape(wo_shape), *outs[5:])


def weights_out_kernel(wide_ref, wq_ref, wk_ref, wv_ref, gain_ref, dq_ref, dk_ref, dv_ref, dg_ref):
    groups, rows, width = wide_ref.shape
    pair = width // 2
    total = jnp.zeros((rows, pair), f32)
    for g in range(groups):
        part = wide_ref[g, :, :pair].astype(f32)
        at = slice(g * pair, (g + 1) * pair)
        dq_ref[:, at] = part
        total += part * wq_ref[:, at].astype(f32)
    for g in range(groups // 2):
        a = wide_ref[2 * g, :, pair:].astype(f32)
        b = wide_ref[2 * g + 1, :, pair:].astype(f32)
        lane = lax.broadcasted_iota(jnp.int32, a.shape, 1)
        at = slice(g * pair, (g + 1) * pair)
        k = jnp.where(lane < HEAD_DIM, a, pltpu.roll(b, HEAD_DIM, 1))
        v = jnp.where(lane < HEAD_DIM, pltpu.roll(a, HEAD_DIM, 1), b)
        dk_ref[:, at] = k
        dv_ref[:, at] = v
        total += k * wk_ref[:, at].astype(f32) + v * wv_ref[:, at].astype(f32)
    dg_ref[...] = jnp.sum(jnp.transpose(total), axis=0, keepdims=True) / gain_ref[...]


def weights_out_call(wide, wq, wk, wv, gain):
    chunks, groups, rows, width = wide.shape
    features = chunks * rows
    by_rows = lambda w: pl.BlockSpec((rows, w.shape[1]), lambda c: (c, 0))
    return pl.pallas_call(
        weights_out_kernel,
        grid=(chunks,),
        in_specs=[
            pl.BlockSpec((None, groups, rows, width), lambda c: (c, 0, 0, 0)),
            by_rows(wq),
            by_rows(wk),
            by_rows(wv),
            pl.BlockSpec((1, rows), lambda c: (0, c)),
        ],
        out_specs=[
            by_rows(wq),
            by_rows(wk),
            by_rows(wv),
            pl.BlockSpec((1, rows), lambda c: (0, c)),
        ],
        out_shape=[
            jax.ShapeDtypeStruct(wq.shape, f32),
            jax.ShapeDtypeStruct(wk.shape, f32),
            jax.ShapeDtypeStruct(wv.shape, f32),
            jax.ShapeDtypeStruct((1, features), f32),
        ],
        compiler_params=params(32, "arbitrary"),
        cost_estimate=cost(2 * wq.size, 1.6e7),
        name="attention_weights_out",
    )(wide, wq, wk, wv, gain)


def last_kernel(d_ref, wq_ref, wk_ref, wv_ref, x_ref, gain_ref, dmid_ref, out_ref):
    groups, rows, width = d_ref.shape
    pair = width // 2
    dq = jnp.concatenate([d_ref[g, :, :pair] for g in range(groups)], axis=1)
    grad = dot_nt(dq, wq_ref[...])
    keys, vals = [], []
    for at in range(groups // 2):
        a = d_ref[2 * at, :, pair:].astype(f32)
        b = d_ref[2 * at + 1, :, pair:].astype(f32)
        lane = lax.broadcasted_iota(jnp.int32, a.shape, 1)
        keys.append(jnp.where(lane < HEAD_DIM, a, pltpu.roll(b, HEAD_DIM, 1)).astype(bf16))
        vals.append(jnp.where(lane < HEAD_DIM, pltpu.roll(a, HEAD_DIM, 1), b).astype(bf16))
    grad = grad + dot_nt(jnp.concatenate(keys, axis=1), wk_ref[...])
    grad = grad + dot_nt(jnp.concatenate(vals, axis=1), wv_ref[...])
    x = x_ref[...].astype(f32)
    scale = lax.rsqrt(jnp.mean(x * x, axis=-1, keepdims=True) + norm_eps)
    unit = x * scale
    w = gain_ref[...] * grad
    out_ref[...] = dmid_ref[...] + scale * (w - unit * jnp.mean(w * unit, axis=-1, keepdims=True))


def last_call(d, wq, wk, wv, x, gain, dmid):
    rows, features = x.shape
    return pl.pallas_call(
        last_kernel,
        out_shape=jax.ShapeDtypeStruct((rows, features), f32),
        compiler_params=params(40),
        cost_estimate=cost(4 * rows * features * features, 8e6),
        name="input_gradient",
    )(d, wq, wk, wv, x, gain, dmid)


def swap(values, axis, bit):
    return lax.ppermute(values, axis, [(i, i ^ bit) for i in range(lax.axis_size(axis))])


def half_sum(values, axis, bit):
    half = values.shape[0] // 2
    upper = ((lax.axis_index(axis) & bit) > 0).astype(jnp.int32)
    came = swap(lax.dynamic_slice_in_dim(values, (1 - upper) * half, half), axis, bit)
    mine = lax.dynamic_slice_in_dim(values, upper * half, half)
    return (mine.astype(f32) + came.astype(f32)).astype(bf16)


def relative_sum(kept, sent, axis, bits):
    while True:
        kept = (kept.astype(f32) + swap(sent, axis, bits[0]).astype(f32)).astype(bf16)
        bits = bits[1:]
        if not bits:
            return kept
        half = kept.shape[0] // 2
        kept, sent = kept[:half], kept[half:]


def join_parts(stream, axis, bits):
    shape = stream.shape
    for bit in bits[::-1]:
        stream = jnp.stack([stream, swap(stream, axis, bit)])
    return stream.reshape(-1, *shape)


def body(
    layer_input,
    first_gain,
    query_weight,
    key_weight,
    value_weight,
    output_weight,
    second_gain,
    gate_weight,
    up_weight,
    down_weight,
    expert_ids,
    gate_values,
    positions,
    cotangent,
):
    micro, _, per_device, features = layer_input.shape
    devices = lax.axis_size("seq")
    replicas = lax.axis_size("dp")
    seq_place = lax.axis_index("seq")
    rows = micro * per_device
    local_experts = gate_weight.shape[0]
    groups = key_weight.shape[1] // HEAD_DIM
    pair = query_weight.shape[1] // groups
    copies = devices // groups

    dp_bits = [1 << i for i in range(replicas.bit_length() - 1)]

    def spread(blocks):
        if copies > 1:
            blocks = jnp.repeat(blocks, copies, axis=0)
        return lax.all_to_all(blocks, "seq", 0, 0, tiled=True)

    def unspread(blocks):
        return lax.all_to_all(blocks, "seq", 0, 0, tiled=True)[::copies]

    x = layer_input.reshape(rows, features)
    cot = cotangent.reshape(rows, features)
    gain_one = first_gain.reshape(1, features)
    gain_two = second_gain.reshape(1, features)
    pos_all = lax.all_to_all(
        jnp.broadcast_to(positions.reshape(1, rows), (devices, rows)), "seq", 0, 0, tiled=True
    )
    x_all = lax.all_gather(x, "seq", axis=0)
    cos_all, sin_all = rope_tables(pos_all.reshape(-1), pair)
    mine = seq_place * local_experts + jnp.arange(local_experts, dtype=jnp.int32)
    ids = expert_ids[:, 0]
    gates = gate_values[:, 0].astype(f32)
    routed = jnp.sum(
        jnp.where(ids[..., None] == mine, gates[..., None], 0.0), axis=2
    )
    routed = routed.reshape(micro, devices, per_device, local_experts)
    routed = jnp.transpose(routed, (1, 0, 2, 3)).reshape(devices * rows, local_experts)
    group = seq_place // copies
    w_own = jnp.concatenate(
        [
            lax.dynamic_slice_in_dim(query_weight, group * pair, pair, axis=1),
            lax.dynamic_slice_in_dim(key_weight, group * HEAD_DIM, HEAD_DIM, axis=1),
            lax.dynamic_slice_in_dim(value_weight, group * HEAD_DIM, HEAD_DIM, axis=1),
        ],
        axis=1,
    )
    cot_pair = jnp.stack([cot, swap(cot, "seq", 1)])
    cos_all, sin_all, routed, w_own, cot_pair = lax.optimization_barrier(
        (cos_all, sin_all, routed, w_own, cot_pair)
    )
    x_all, cot_then, cos_all, sin_all, routed, w_own, cot_pair = lax.optimization_barrier(
        (x_all, cot, cos_all, sin_all, routed, w_own, cot_pair)
    )
    cot_all = lax.all_gather(cot_then, "seq", axis=0)
    cots = (cot_pair, cot_all)

    qkv, first_all = qkv_call(x_all, gain_one, cos_all, sin_all, w_own)
    qkv = qkv.reshape(devices, micro, per_device, 2 * pair)
    mix, log_total = attend_call(qkv)
    mix = unspread(mix.reshape(devices, rows, pair))
    mixed, middle, second_low = post_call(mix, output_weight, x, gain_two)

    chips = devices // 2
    chip, core = seq_place // 2, seq_place % 2
    onward = [(i, (i + 2) % devices) for i in range(devices)]
    dp_place = lax.axis_index("dp")
    first_bit = dp_place & 1
    last_bit = dp_place >> (len(dp_bits) - 1)
    held, kept, running, places = second_low, (), None, []
    for hop in range(chips):
        following = lax.ppermute(held, "seq", onward) if hop < chips - 1 else None
        other = swap(held, "seq", 1)
        source = 2 * ((chip - hop) % chips)
        near_cot = [jnp.int32(0), jnp.int32(1)] if hop == 0 else [source + core, source + 1 - core]
        place = jnp.stack(
            [source + core, source + 1 - core, 1 - first_bit, 1 - last_bit, *near_cot]
        )
        place = place.astype(jnp.int32)
        places.append(place[:2])
        dx, *kept = expert_call(
            hop, place, held, other, cots[hop > 0], routed, gate_weight, up_weight, down_weight, kept
        )
        if following is not None:
            following, dx = lax.optimization_barrier((following, dx))
        part = dx[0].astype(f32) + swap(dx[1], "seq", 1).astype(f32)
        if hop == 0:
            own_part = part
        else:
            if running is not None:
                part = part + running.astype(f32)
            part = part.astype(bf16)
            if following is not None:
                part, following = lax.optimization_barrier((part, following))
            else:
                part, kept = lax.optimization_barrier((part, kept))
            running = lax.ppermute(part, "seq", onward)
        held = following
    second_grad = (own_part + running.astype(f32)).astype(bf16)
    tokens, hidden_a, hidden_b, gate_low, up_low, slot_a, slot_b = kept

    def weight_parts(at, tokens, hidden_a, hidden_b, gate_low, up_low, slot_a, slot_b):
        pairs = (
            (tokens, gate_low[at]),
            (tokens, up_low[at]),
            (hidden_a[at], slot_a[at]),
            (hidden_b[at], slot_b[at]),
        )
        return [
            lax.dot_general(a, b, TN, preferred_element_type=f32).astype(bf16) for a, b in pairs
        ]

    leaving = weight_parts(0, *kept)
    part_bits = (dp_bits[0], dp_bits[-1], dp_bits[0], dp_bits[-1])
    stream_bits = (dp_bits, dp_bits[::-1])
    came = [swap(values, "dp", bit) for values, bit in zip(leaving, part_bits)]
    leaving, second_grad = lax.optimization_barrier((leaving, second_grad))

    mg_send, proj, middle_grad, gain_two_part = turn_call(
        second_grad, middle, gain_two, cot, output_weight, groups
    )
    mg = spread(mg_send)
    kept, _ = lax.optimization_barrier((kept, mg_send))
    mixed, proj, came[2:] = lax.optimization_barrier((mixed, proj, came[2:]))
    dense = output_weight_call(mixed, proj, gain_two_part, devices)
    dense_own = dense
    staying = weight_parts(1, *kept)
    turned = sum(((dp_place >> i) & 1) << (len(dp_bits) - 1 - i) for i in range(len(dp_bits)))
    part_at = jnp.stack([turned, dp_place]).astype(jnp.int32)
    low_at = jnp.bitwise_and(part_at, replicas // 2 - 1)
    keep_a, send_a, keep_b, send_b = part_sum_call(low_at, replicas // 2, came, staying)
    mg, keep_a, send_a, keep_b, send_b = lax.optimization_barrier(
        (mg, keep_a, send_a, keep_b, send_b)
    )
    streams = [
        relative_sum(keep_a, send_a, "dp", stream_bits[0][1:]),
        relative_sum(keep_b, send_b, "dp", stream_bits[1][1:]),
    ]
    dense = dense_own
    dense = lax.psum_scatter(dense, "seq", scatter_dimension=0)
    table_shape = (devices, micro, per_device, pair)
    dqkv = attend_back_call(
        qkv,
        mg.reshape(devices, micro, per_device, pair),
        log_total,
        cos_all.reshape(table_shape),
        sin_all.reshape(table_shape),
    )
    dqkv, streams = lax.optimization_barrier((dqkv, streams))
    near = [
        [v[0], swap(v[0], "dp", bits[-1])] for v, bits in zip(streams, stream_bits)
    ]
    back = unspread(dqkv.reshape(devices, rows, 2 * pair))
    d_all = dqkv.reshape(devices * rows, 2 * pair)
    first_tokens = first_all.reshape(devices * rows, features)
    part = lax.dot_general(first_tokens, d_all, TN, preferred_element_type=f32)
    dense = dense.reshape(dense.shape[-2], features)
    each = output_weight.shape[0] // devices
    if copies == 1:
        width = 2 * pair
        kept_pieces, sent_pieces = joint_call(part_at, part, dense, replicas)
        first = [
            kept_pieces[at].astype(f32) + swap(sent_pieces[at], "dp", bits[0]).astype(f32)
            for at, bits in enumerate(stream_bits)
        ]
        kept, sent_pieces = lax.optimization_barrier((kept, sent_pieces))
        moe_place = jnp.concatenate(places + [(1 - first_bit).astype(jnp.int32).reshape(1)])
        moe_all = moe_call(moe_place, kept[1], routed, down_weight, devices)
        first, near, moe_all = lax.optimization_barrier(
            ([v.astype(bf16) for v in first], near, moe_all)
        )
        own = [
            relative_sum(v[: replicas // 4], v[replicas // 4 :], "dp", bits[1:])
            for v, bits in zip(first, stream_bits)
        ]
        own = jnp.concatenate(own, axis=0)
        own, back, here = lax.optimization_barrier((own, back, [v[0] for v in near]))
        far = [swap(v, "dp", bits[-2]) for v, bits in zip(here, stream_bits)]
        backward = [(i, (i - 2) % devices) for i in range(devices)]
        round_ring = {0: own}
        for k in range(1, chips // 2 + 1):
            round_ring[k] = lax.ppermute(round_ring[k - 1], "seq", onward)
            if chips - k > k:
                round_ring[chips - k] = lax.ppermute(
                    round_ring[(chips - k + 1) % chips], "seq", backward
                )
            if k == 1:
                round_ring, coming = lax.optimization_barrier(
                    (round_ring, [v[1] for v in near])
                )
        held = jnp.stack([round_ring[k] for k in range(chips)])
        passed = [swap(v, "dp", bits[-2]) for v, bits in zip(coming, stream_bits)]
        moe_all, far, _ = lax.optimization_barrier((moe_all, far, round_ring[chips // 2]))
        moe = lax.psum_scatter(moe_all, "seq", scatter_dimension=0)
    else:
        far = [swap(v[0], "dp", bits[-2]) for v, bits in zip(streams, stream_bits)]
        passed = [swap(v[1], "dp", bits[-2]) for v, bits in zip(near, stream_bits)]
    expert_pieces = []
    for (here, first), second, third, bits in zip(near, far, passed, stream_bits):
        pieces = [here, first, second, third]
        for bit in bits[:-2][::-1]:
            pieces = pieces + [swap(p, "dp", bit) for p in pieces]
        expert_pieces.append(pieces)
    input_grad = last_call(
        back, query_weight, key_weight, value_weight, x, gain_one, middle_grad
    )
    if copies == 1:
        gate_sum, up_sum, down_sum = expert_out_call(
            part_at, *expert_pieces, gate_weight.shape, down_weight.shape
        )
        full = [[held[:, at], swap(held[:, at], "dp", b[-1])] for at, b in enumerate(stream_bits)]
        beside = [swap(v[0], "dp", bits[-2]) for v, bits in zip(full, stream_bits)]
        full, beside = lax.optimization_barrier((full, beside))
        for at, bits in enumerate(stream_bits):
            full[at] += [beside[at], swap(full[at][1], "dp", bits[-2])]
            for bit in bits[:-2][::-1]:
                full[at] += [swap(p, "dp", bit) for p in full[at]]
        ends = [pieces.pop() for pieces in full]
        ends, gate_sum, up_sum, down_sum, input_grad = lax.optimization_barrier(
            (ends, gate_sum, up_sum, down_sum, input_grad)
        )
        full = [pieces + [end] for pieces, end in zip(full, ends)]
        other = [[swap(p, "seq", 1) for p in pieces] for pieces in full]
        where_at = jnp.stack([turned, dp_place, chip, core]).astype(jnp.int32)
        (
            query_weight_grad,
            key_weight_grad,
            value_weight_grad,
            first_gain_grad,
            output_weight_grad,
            second_gain_grad,
            layer_output,
        ) = dense_out_call(
            where_at,
            full,
            other,
            middle,
            moe.reshape(rows, features),
            query_weight,
            key_weight,
            value_weight,
            gain_one,
            output_weight.shape,
        )
    else:
        gate_sum, up_sum, down_sum = expert_out_call(
            part_at, *expert_pieces, gate_weight.shape, down_weight.shape
        )
        for bit in dp_bits:
            dense = (dense.astype(f32) + swap(dense, "dp", bit).astype(f32)).astype(bf16)
        dense = lax.all_gather(dense, "seq", axis=0).astype(f32)
        output_weight_grad = dense[:, :each].reshape(output_weight.shape)
        moe_place = jnp.concatenate(places + [(1 - first_bit).astype(jnp.int32).reshape(1)])
        moe_all = moe_call(moe_place, kept[1], routed, down_weight, devices)
        moe = lax.psum_scatter(moe_all, "seq", scatter_dimension=0)
        layer_output = (middle + residual_scale * moe.astype(f32)).astype(bf16)
        second_gain_grad = dense[0, each]
        part = part.astype(bf16)
        for bit in dp_bits[::-1]:
            part = half_sum(part, "dp", bit)
        wide = lax.all_gather(part, ("dp", "seq"), axis=0)
        wide = wide.reshape(replicas, devices, features // replicas, 2 * pair)[:, ::copies]
        query_weight_grad, key_weight_grad, value_weight_grad, first_gain_grad = weights_out_call(
            wide, query_weight, key_weight, value_weight, gain_one
        )
    second_gain_grad = second_gain_grad.reshape(features)
    return (
        layer_output.reshape(layer_input.shape),
        input_grad.reshape(layer_input.shape),
        first_gain_grad.reshape(features),
        query_weight_grad,
        key_weight_grad,
        value_weight_grad,
        output_weight_grad,
        second_gain_grad,
        gate_sum,
        up_sum,
        down_sum,
    )


def solution(mesh):
    return jax.shard_map(
        body,
        mesh=mesh,
        in_specs=(
            P(None, "dp", "seq", None),
            P(),
            P(),
            P(),
            P(),
            P(),
            P(),
            P("seq", None, None),
            P("seq", None, None),
            P("seq", None, None),
            P(None, "dp", None, None),
            P(None, "dp", None, None),
            P(None, "dp", "seq"),
            P(None, "dp", "seq", None),
        ),
        out_specs=(
            P(None, "dp", "seq", None),
            P(None, "dp", "seq", None),
            P(),
            P(),
            P(),
            P(),
            P(),
            P(),
            P("seq", None, None),
            P("seq", None, None),
            P("seq", None, None),
        ),
        check_vma=False,
    )
```

```python
from functools import partial

import jax
import jax.numpy as jnp
from jax import lax
from jax.experimental import pallas as pl
from jax.experimental.pallas import tpu as pltpu
from jax.sharding import PartitionSpec as P

HEAD_DIM = 64

rope_theta = 10000.0
attention_scale = 0.015625
residual_scale = 0.22
norm_eps = 1e-06
masked_score = -1e30

f32 = jnp.float32
bf16 = jnp.bfloat16
NT = (((1,), (1,)), ((), ()))
TN = (((0,), (0,)), ((), ()))


def dot(a, b):
    return jnp.dot(a, b, preferred_element_type=f32)


def dot_nt(a, b):
    return lax.dot_general(a, b, NT, preferred_element_type=f32)


def params(mib, *semantics):
    return pltpu.CompilerParams(
        vmem_limit_bytes=mib * 1024 * 1024, dimension_semantics=semantics or None
    )


def cost(flops, nbytes, trans=0):
    return pl.CostEstimate(
        flops=int(flops / 8), bytes_accessed=int(nbytes / 8), transcendentals=int(trans / 8)
    )


def whole(shape):
    return pl.BlockSpec(shape, lambda *_: (0,) * len(shape))


def rope_tables(positions, width):
    half = HEAD_DIM // 2
    exponent = jnp.arange(half, dtype=f32) * (-2.0 / HEAD_DIM)
    angles = positions.astype(f32)[:, None] * (rope_theta**exponent)[None, :]
    cosine, sine = jnp.cos(angles), jnp.sin(angles)
    copies = width // HEAD_DIM
    cos_row = jnp.concatenate([cosine, cosine] * copies, axis=1)
    sin_row = jnp.concatenate([-sine, sine] * copies, axis=1)
    return cos_row, sin_row


def partner(values):
    width = values.shape[1]
    half = HEAD_DIM // 2
    lane = lax.broadcasted_iota(jnp.int32, values.shape, 1)
    ahead = pltpu.roll(values, width - half, 1)
    behind = pltpu.roll(values, half, 1)
    return jnp.where(lane % HEAD_DIM < half, ahead, behind)


def qkv_kernel(x_ref, gain_ref, cos_ref, sin_ref, w_ref, qkv_ref, low_ref):
    pair = 2 * HEAD_DIM
    x = x_ref[0].astype(f32)
    scale = lax.rsqrt(jnp.mean(x * x, axis=-1, keepdims=True) + norm_eps)
    low = (x * scale * gain_ref[...]).astype(bf16)
    low_ref[0] = low
    cosine, sine = cos_ref[...], sin_ref[...]
    made = dot(low, w_ref[...])
    q, kv = made[:, :pair], made[:, pair:]
    q = (q * cosine + partner(q) * sine) * attention_scale
    qkv_ref[0, :, :pair] = q.astype(bf16)
    lane = lax.broadcasted_iota(jnp.int32, kv.shape, 1)
    turned = kv * cosine + partner(kv) * sine
    qkv_ref[0, :, pair:] = jnp.where(lane < HEAD_DIM, turned, kv).astype(bf16)


def qkv_call(x_all, gain, cos_all, sin_all, w_own):
    blocks, rows, features = x_all.shape
    pair = 2 * HEAD_DIM
    return pl.pallas_call(
        qkv_kernel,
        grid=(blocks,),
        in_specs=[
            pl.BlockSpec((1, rows, features), lambda s: (s, 0, 0)),
            whole((1, features)),
            pl.BlockSpec((rows, pair), lambda s: (s, 0)),
            pl.BlockSpec((rows, pair), lambda s: (s, 0)),
            whole(w_own.shape),
        ],
        out_specs=[
            pl.BlockSpec((1, rows, 2 * pair), lambda s: (s, 0, 0)),
            pl.BlockSpec((1, rows, features), lambda s: (s, 0, 0)),
        ],
        out_shape=[
            jax.ShapeDtypeStruct((blocks, rows, 2 * pair), bf16),
            jax.ShapeDtypeStruct((blocks, rows, features), bf16),
        ],
        compiler_params=params(58, "arbitrary"),
        cost_estimate=cost(4 * blocks * rows * features * pair, 14e6),
        name="norm_qkv_rope",
    )(x_all, gain, cos_all, sin_all, w_own)


def split_heads(block, first):
    wide = block.astype(f32)
    lane = lax.broadcasted_iota(jnp.int32, wide.shape, 1)
    turned = pltpu.roll(wide, HEAD_DIM, 1)
    if first:
        parts = [jnp.where(lane < HEAD_DIM, wide, 0.0), jnp.where(lane < HEAD_DIM, turned, 0.0)]
    else:
        parts = [jnp.where(lane >= HEAD_DIM, turned, 0.0), jnp.where(lane >= HEAD_DIM, wide, 0.0)]
    return jnp.concatenate(parts, axis=0).astype(bf16)


def join_heads(turned):
    rows = turned.shape[1] // 2
    return jnp.transpose(jnp.concatenate([turned[:, :rows], turned[:, rows:]], axis=0))


def scores_of(kv, q2, rows):
    scores = dot_nt(kv, q2)
    count = scores.shape[0]
    own = scores[count - rows :]
    key_at = lax.broadcasted_iota(jnp.int32, own.shape, 0)
    query_at = lax.broadcasted_iota(jnp.int32, own.shape, 1) % rows
    own = jnp.where(key_at <= query_at, own, masked_score)
    if count == rows:
        return own
    return jnp.concatenate([scores[: count - rows], own], axis=0)


def attend_kernel(qkv_ref, out_ref, log_ref):
    blocks, _, rows, width = qkv_ref.shape
    pair = width // 2
    kv = qkv_ref[:, 0, :, pair:].reshape(blocks * rows, pair)
    kv_t = jnp.transpose(kv)
    for at in range(blocks):
        count = (at + 1) * rows
        q2 = split_heads(qkv_ref[at, 0, :, :pair], True)
        scores = scores_of(kv[:count], q2, rows)
        top = jnp.max(scores, axis=0, keepdims=True)
        weights = jnp.exp(scores - top)
        total = jnp.sum(weights, axis=0, keepdims=True)
        out_t = dot(kv_t[:, :count], weights.astype(bf16))
        out_ref[at, 0] = join_heads(out_t[HEAD_DIM:] / total).astype(bf16)
        log_ref[at, 0] = top + jnp.log(total)


def attend_call(qkv):
    blocks, micro, rows, width = qkv.shape
    pair = width // 2
    length = blocks * rows
    return pl.pallas_call(
        attend_kernel,
        grid=(micro,),
        in_specs=[pl.BlockSpec((blocks, 1, rows, width), lambda m: (0, m, 0, 0))],
        out_specs=[
            pl.BlockSpec((blocks, 1, rows, pair), lambda m: (0, m, 0, 0)),
            pl.BlockSpec((blocks, 1, 1, 2 * rows), lambda m: (0, m, 0, 0)),
        ],
        out_shape=[
            jax.ShapeDtypeStruct((blocks, micro, rows, pair), bf16),
            jax.ShapeDtypeStruct((blocks, micro, 1, 2 * rows), f32),
        ],
        compiler_params=params(48, "arbitrary"),
        cost_estimate=cost(
            micro * length * length * 512, 3 * qkv.size, micro * length * length
        ),
        name="attention_forward",
    )(qkv)


def attend_back_kernel(qkv_ref, grad_ref, log_ref, cos_ref, sin_ref, out_ref, dkv_ref):
    blocks, _, rows, width = qkv_ref.shape
    pair = width // 2
    kv = qkv_ref[:, 0, :, pair:].reshape(blocks * rows, pair)
    kv_t = jnp.transpose(kv)
    dkv_ref[...] = jnp.zeros_like(dkv_ref)
    for at in range(blocks):
        count = (at + 1) * rows
        q2 = split_heads(qkv_ref[at, 0, :, :pair], True)
        g2 = split_heads(grad_ref[at, 0], False)
        scores = scores_of(kv[:count], q2, rows)
        prob = jnp.exp(scores - log_ref[at, 0])
        prob_grad = dot_nt(kv[:count], g2)
        delta = jnp.sum(prob * prob_grad, axis=0, keepdims=True)
        score_grad = (prob * (prob_grad - delta)).astype(bf16)
        dkv_ref[:count] += dot(score_grad, q2) + dot(prob.astype(bf16), g2)
        dq_t = dot(kv_t[:, :count], score_grad)
        dq = join_heads(dq_t[:HEAD_DIM] * attention_scale)
        dq = dq * cos_ref[at, 0] - partner(dq) * sin_ref[at, 0]
        out_ref[at, 0, :, :pair] = dq.astype(bf16)
    for at in range(blocks):
        dkv = dkv_ref[at * rows : (at + 1) * rows]
        lane = lax.broadcasted_iota(jnp.int32, dkv.shape, 1)
        turned = dkv * cos_ref[at, 0] - partner(dkv) * sin_ref[at, 0]
        out_ref[at, 0, :, pair:] = jnp.where(lane < HEAD_DIM, turned, dkv).astype(bf16)


def attend_back_call(qkv, grads, log_total, cos_all, sin_all):
    blocks, micro, rows, width = qkv.shape
    pair = width // 2
    length = blocks * rows
    spec = lambda lanes: pl.BlockSpec((blocks, 1, rows, lanes), lambda m: (0, m, 0, 0))
    return pl.pallas_call(
        attend_back_kernel,
        grid=(micro,),
        in_specs=[
            spec(width),
            spec(pair),
            pl.BlockSpec((blocks, 1, 1, 2 * rows), lambda m: (0, m, 0, 0)),
            spec(pair),
            spec(pair),
        ],
        out_specs=spec(width),
        out_shape=jax.ShapeDtypeStruct(qkv.shape, bf16),
        scratch_shapes=[pltpu.VMEM((length, pair), f32)],
        compiler_params=params(56, "arbitrary"),
        cost_estimate=cost(
            micro * length * length * 1280, 10 * qkv.size, micro * length * length
        ),
        name="attention_backward",
    )(qkv, grads, log_total, cos_all, sin_all)


def post_kernel(mix_ref, wo_ref, x_ref, gain_ref, mixed_ref, middle_ref, low_ref):
    mixed = jnp.concatenate([mix_ref[g] for g in range(mix_ref.shape[0])], axis=1)
    mixed_ref[...] = mixed
    middle = x_ref[...].astype(f32) + residual_scale * dot(mixed, wo_ref[...])
    middle_ref[...] = middle
    scale = lax.rsqrt(jnp.mean(middle * middle, axis=-1, keepdims=True) + norm_eps)
    low_ref[...] = (middle * scale * gain_ref[...]).astype(bf16)


def post_call(mix, wo, x, gain):
    rows, features = x.shape
    return pl.pallas_call(
        post_kernel,
        out_shape=[
            jax.ShapeDtypeStruct((rows, wo.shape[0]), bf16),
            jax.ShapeDtypeStruct((rows, features), f32),
            jax.ShapeDtypeStruct((rows, features), bf16),
        ],
        compiler_params=params(32),
        cost_estimate=cost(2 * rows * wo.size, 5e6),
        name="project_norm",
    )(mix, wo, x, gain)


def expert_kernel(place_ref, a_ref, b_ref, cot_ref, w_ref, wg_ref, wu_ref, wd_ref, *refs):
    dx_ref, x_ref, ha_ref, hb_ref, dg_ref, du_ref, sa_ref, sb_ref = refs[-8:]
    step = pl.program_id(0)
    first, second = place_ref[2], place_ref[3]
    half = sa_ref.shape[2]

    @pl.when(step == 0)
    def _():
        x_ref[...] = a_ref[...]

    @pl.when(step == 1)
    def _():
        x_ref[...] = b_ref[...]

    x = x_ref[...]
    cot = cot_ref[0].astype(f32)
    weight = residual_scale * w_ref[...]
    total = None
    for e in range(wg_ref.shape[0]):
        gate = dot(x, wg_ref[e])
        up = dot(x, wu_ref[e])
        slot_grad = (weight[:, e : e + 1] * cot).astype(bf16)
        to_a, to_b = jnp.bitwise_xor(first, e), jnp.bitwise_xor(second, e)
        sa_ref[to_a] = slot_grad[:, :half]
        sb_ref[to_b] = slot_grad[:, half:]
        hidden_grad = dot_nt(slot_grad, wd_ref[e])
        sig = 0.5 * jnp.tanh(0.5 * gate) + 0.5
        silu = gate * sig
        hidden = (silu * up).astype(bf16)
        ha_ref[to_a] = hidden
        hb_ref[to_b] = hidden
        gate_grad = (hidden_grad * up * (sig + silu * (1.0 - sig))).astype(bf16)
        up_grad = (hidden_grad * silu).astype(bf16)
        dg_ref[to_a] = gate_grad
        du_ref[to_b] = up_grad
        term = dot_nt(gate_grad, wg_ref[e]) + dot_nt(up_grad, wu_ref[e])
        total = term if total is None else total + term
    dx_ref[0] = total.astype(bf16)


def expert_call(at, place, own, other, cots, weight, wg, wu, wd, kept):
    rows, features = own.shape
    count, _, hidden = wg.shape
    tokens = weight.shape[0]
    inner = jax.ShapeDtypeStruct((count, tokens, hidden), bf16)
    outer = jax.ShapeDtypeStruct((count, tokens, features // 2), bf16)
    inner_spec = pl.BlockSpec((count, rows, hidden), lambda s, place: (0, 2 * at + s, 0))
    outer_spec = pl.BlockSpec((count, rows, features // 2), lambda s, place: (0, 2 * at + s, 0))
    fixed = lambda shape: pl.BlockSpec(shape, lambda s, place: (0,) * len(shape))
    any_spec = pl.BlockSpec(memory_space=pl.ANY)
    first = 8
    return pl.pallas_call(
        expert_kernel,
        grid_spec=pltpu.PrefetchScalarGridSpec(
            num_scalar_prefetch=1,
            grid=(2,),
            in_specs=[
                fixed((rows, features)),
                fixed((rows, features)),
                pl.BlockSpec((1, rows, features), lambda s, place: (place[4 + s], 0, 0)),
                pl.BlockSpec((rows, count), lambda s, place: (place[s], 0)),
                fixed(wg.shape),
                fixed(wu.shape),
                fixed(wd.shape),
            ]
            + [any_spec] * len(kept),
            out_specs=[
                pl.BlockSpec((1, rows, features), lambda s, place: (s, 0, 0)),
                pl.BlockSpec((rows, features), lambda s, place: (2 * at + s, 0)),
            ]
            + [inner_spec] * 4
            + [outer_spec] * 2,
        ),
        out_shape=[
            jax.ShapeDtypeStruct((2, rows, features), bf16),
            jax.ShapeDtypeStruct((tokens, features), bf16),
            inner,
            inner,
            inner,
            inner,
            outer,
            outer,
        ],
        input_output_aliases={first + i: 1 + i for i in range(len(kept))},
        compiler_params=params(48, "arbitrary"),
        cost_estimate=cost(20 * rows * wg.size, 2e7, 2 * rows * hidden * count),
        name="experts",
    )(place, own, other, cots, weight, wg, wu, wd, *kept)


def part_sum_kernel(at_ref, *refs):
    inputs, outs = refs[:16], refs[16:]
    at = 0
    for out in outs:
        gate_came, gate_here, down_came, down_here = inputs[at : at + 4]
        rows = gate_came.shape[0]
        out[0, :rows] = (gate_came[...].astype(f32) + gate_here[...].astype(f32)).astype(bf16)
        out[0, rows:] = (down_came[...].astype(f32) + down_here[...].astype(f32)).astype(bf16)
        at += 4


def part_sum_call(at, per, came, here):
    gate_rows, down_rows = came[0].shape[0] // per, came[2].shape[0] // per
    width = came[0].shape[1]
    steps = per // 2
    specs, args, out_specs, out_shapes = [], [], [], []
    for stream in range(2):
        for sent in range(2):
            for which, rows in ((stream, gate_rows), (stream + 2, down_rows)):
                spec = pl.BlockSpec(
                    (rows, width),
                    lambda s, at, sent=sent, stream=stream: (
                        jnp.bitwise_xor(s + sent * steps, at[stream]),
                        0,
                    ),
                )
                specs += [spec, spec]
                args += [came[which], here[which]]
            out_specs.append(
                pl.BlockSpec((1, gate_rows + down_rows, width), lambda s, at: (s, 0, 0))
            )
            out_shapes.append(
                jax.ShapeDtypeStruct((steps, gate_rows + down_rows, width), bf16)
            )
    return pl.pallas_call(
        part_sum_kernel,
        grid_spec=pltpu.PrefetchScalarGridSpec(
            num_scalar_prefetch=1, grid=(steps,), in_specs=specs, out_specs=out_specs
        ),
        out_shape=out_shapes,
        compiler_params=params(60, "arbitrary"),
        cost_estimate=cost(0, 9e6),
        name="expert_part_sum",
    )(at, *args)


def joint_kernel(at_ref, *refs):
    for (part_ref, wo_ref, gain_ref), out_ref in ((refs[:3], refs[6]), (refs[3:6], refs[7])):
        rows = part_ref.shape[0]
        upto = rows + wo_ref.shape[0]
        out_ref[0, 0, :rows] = part_ref[...].astype(bf16)
        out_ref[0, 0, rows:upto] = wo_ref[...]
        out_ref[0, 0, upto:] = gain_ref[...]


def joint_call(at, part, dense, parts):
    features, width = part.shape
    pieces = 2 * parts
    rows = features // pieces
    block_cols = dense.shape[1] // width
    per_block = pieces // block_cols
    extra = 16
    wo_rows = (dense.shape[0] - extra) // per_block
    last = dense.shape[0] // extra - 1
    steps = parts // 2

    def piece(sent):
        return lambda s, p, at: s * parts + jnp.bitwise_xor(p + sent * steps, at[s])

    specs = []
    for sent in range(2):
        at_piece = piece(sent)
        specs.append(
            pl.BlockSpec((rows, width), lambda s, p, at, f=at_piece: (f(s, p, at), 0))
        )
        specs.append(
            pl.BlockSpec(
                (wo_rows, width),
                lambda s, p, at, f=at_piece: (
                    lax.rem(f(s, p, at), per_block),
                    lax.div(f(s, p, at), per_block),
                ),
            )
        )
        specs.append(
            pl.BlockSpec(
                (extra, width), lambda s, p, at, f=at_piece: (last, lax.div(f(s, p, at), per_block))
            )
        )
    out_spec = pl.BlockSpec((1, 1, rows + wo_rows + extra, width), lambda s, p, at: (s, p, 0, 0))
    out_shape = jax.ShapeDtypeStruct((2, steps, rows + wo_rows + extra, width), bf16)
    return pl.pallas_call(
        joint_kernel,
        grid_spec=pltpu.PrefetchScalarGridSpec(
            num_scalar_prefetch=1, grid=(2, steps), in_specs=specs, out_specs=[out_spec] * 2
        ),
        out_shape=[out_shape] * 2,
        compiler_params=params(32, "arbitrary", "arbitrary"),
        cost_estimate=cost(0, 2e6),
        name="dense_pieces",
    )(at, part, dense, dense, part, dense, dense)


def expert_out_kernel(at_ref, *refs):
    pieces, (gate_ref, up_ref, down_ref) = refs[:-3], refs[-3:]
    parts = len(pieces) // 2
    step = pl.program_id(0)
    rows = gate_ref.shape[1]
    half = down_ref.shape[2] // 2
    for which in range(parts):

        @pl.when(jnp.bitwise_xor(step, at_ref[0]) == which)
        def _():
            a_ref = pieces[which]
            gate_ref[0] = a_ref[:rows].astype(f32)
            down_ref[0, :, :half] = a_ref[rows:].astype(f32)

        @pl.when(jnp.bitwise_xor(step, at_ref[1]) == which)
        def _():
            b_ref = pieces[parts + which]
            up_ref[0] = b_ref[:rows].astype(f32)
            down_ref[0, :, half:] = b_ref[rows:].astype(f32)


def expert_out_call(at, a, b, gate_shape, down_shape):
    parts = len(a)
    held, width = a[0].shape
    count = gate_shape[0]
    per = parts // count
    gate_rows, down_rows = gate_shape[1] // per, down_shape[1] // per
    place = lambda r, at: (lax.div(r, per), lax.rem(r, per), 0)
    return pl.pallas_call(
        expert_out_kernel,
        grid_spec=pltpu.PrefetchScalarGridSpec(
            num_scalar_prefetch=1,
            grid=(parts,),
            in_specs=[pl.BlockSpec((held, width), lambda r, at: (0, 0))] * (2 * parts),
            out_specs=[
                pl.BlockSpec((1, gate_rows, gate_shape[2]), place),
                pl.BlockSpec((1, gate_rows, gate_shape[2]), place),
                pl.BlockSpec((1, down_rows, down_shape[2]), place),
            ],
        ),
        out_shape=[
            jax.ShapeDtypeStruct(gate_shape, f32),
            jax.ShapeDtypeStruct(gate_shape, f32),
            jax.ShapeDtypeStruct(down_shape, f32),
        ],
        compiler_params=params(40, "arbitrary"),
        cost_estimate=cost(0, 2e7),
        name="expert_weights_out",
    )(at, *a, *b)


def moe_kernel(place_ref, h_ref, w_ref, wd_ref, out_ref):
    weight = w_ref[...]
    total = None
    first = place_ref[pl.num_programs(0)]
    for e in range(wd_ref.shape[0]):
        term = weight[:, e : e + 1] * dot(h_ref[jnp.bitwise_xor(first, e)], wd_ref[e])
        total = term if total is None else total + term
    out_ref[0] = total.astype(bf16)


def moe_call(place, hidden, weight, wd, blocks):
    count, tokens, inner = hidden.shape
    features = wd.shape[2]
    rows = tokens // blocks
    return pl.pallas_call(
        moe_kernel,
        grid_spec=pltpu.PrefetchScalarGridSpec(
            num_scalar_prefetch=1,
            grid=(blocks,),
            in_specs=[
                pl.BlockSpec((count, rows, inner), lambda s, place: (0, s, 0)),
                pl.BlockSpec((rows, count), lambda s, place: (place[s], 0)),
                pl.BlockSpec(wd.shape, lambda s, place: (0, 0, 0)),
            ],
            out_specs=pl.BlockSpec((1, rows, features), lambda s, place: (place[s], 0, 0)),
        ),
        out_shape=jax.ShapeDtypeStruct((blocks, rows, features), bf16),
        compiler_params=params(60, "arbitrary"),
        cost_estimate=cost(2 * tokens * wd.size, 1.1e7),
        name="expert_outputs",
    )(place, hidden, weight, wd)


def turn_kernel(sg_ref, middle_ref, gain_ref, cot_ref, wo_ref, mg_ref, proj_ref, dmid_ref, dgain_ref):
    grad = sg_ref[...].astype(f32)
    middle = middle_ref[...]
    scale = lax.rsqrt(jnp.mean(middle * middle, axis=-1, keepdims=True) + norm_eps)
    unit = middle * scale
    dgain_ref[...] = jnp.sum(grad * unit, axis=0, keepdims=True)
    w = gain_ref[...] * grad
    dmid = cot_ref[...].astype(f32) + scale * (w - unit * jnp.mean(w * unit, axis=-1, keepdims=True))
    dmid_ref[...] = dmid
    proj = (residual_scale * dmid).astype(bf16)
    proj_ref[...] = proj
    mixed_grad = dot_nt(proj, wo_ref[...]).astype(bf16)
    groups, _, pair = mg_ref.shape
    for g in range(groups):
        mg_ref[g] = mixed_grad[:, g * pair : (g + 1) * pair]


def turn_call(sg, middle, gain, cot, wo, groups):
    rows, features = middle.shape
    pair = wo.shape[0] // groups
    return pl.pallas_call(
        turn_kernel,
        out_shape=[
            jax.ShapeDtypeStruct((groups, rows, pair), bf16),
            jax.ShapeDtypeStruct((rows, features), bf16),
            jax.ShapeDtypeStruct((rows, features), f32),
            jax.ShapeDtypeStruct((1, features), f32),
        ],
        compiler_params=params(32),
        cost_estimate=cost(2 * rows * wo.size, 6e6),
        name="norm_back_project_back",
    )(sg, middle, gain, cot, wo)


def output_weight_kernel(mixed_ref, proj_ref, dgain_ref, out_ref):
    held, each, features = out_ref.shape
    rows = mixed_ref.shape[1] // held
    part = lax.dot_general(mixed_ref[...], proj_ref[...], TN, preferred_element_type=f32)
    extra = jnp.broadcast_to(dgain_ref[...], (each - rows, features)).astype(bf16)
    for at in range(held):
        out_ref[at, :rows] = part[at * rows : (at + 1) * rows].astype(bf16)
        out_ref[at, rows:] = extra


def output_weight_call(mixed, proj, dgain, parts):
    rows, width = mixed.shape
    features = proj.shape[1]
    each = width // parts
    lanes = max(each, width // 2)
    held = lanes // each
    return pl.pallas_call(
        output_weight_kernel,
        grid=(parts // held,),
        in_specs=[
            pl.BlockSpec((rows, lanes), lambda s: (0, s)),
            whole((rows, features)),
            whole((1, features)),
        ],
        out_specs=pl.BlockSpec((held, each + 16, features), lambda s: (s, 0, 0)),
        out_shape=jax.ShapeDtypeStruct((parts, each + 16, features), bf16),
        compiler_params=params(32, "arbitrary"),
        cost_estimate=cost(2 * rows * width * features, 4e6),
        name="output_weight_part",
    )(mixed, proj, dgain)


def dense_out_kernel(at_ref, *refs):
    held, refs = refs[:-13], refs[-13:]
    wq_ref, wk_ref, wv_ref, gain_ref, dq_ref, dk_ref, dv_ref, dg_ref, wo_ref, dg2_ref = refs[:10]
    own_ref, other_ref = refs[10:12]
    parts = len(held) // 4
    stream, step = pl.program_id(0), pl.program_id(1)
    chips, _, width = own_ref.shape
    rows = dq_ref.shape[0]
    pair = width // 2
    chip, core = at_ref[2], at_ref[3]
    for which in range(2):
        for rel in range(parts):

            @pl.when((stream == which) & (jnp.bitwise_xor(step, at_ref[which]) == rel))
            def _():
                own_ref[...] = held[which * parts + rel][...]
                other_ref[...] = held[(2 + which) * parts + rel][...]

    total = jnp.zeros((rows, pair), f32)
    for k in range(chips):
        source = lax.rem(chip - k + chips, chips)
        a = jnp.where(core == 0, own_ref[k], other_ref[k]).astype(f32)
        b = jnp.where(core == 0, other_ref[k], own_ref[k]).astype(f32)
        q = jnp.concatenate([a[:rows, :pair], b[:rows, :pair]], axis=1)
        cols = pl.ds(pl.multiple_of(source * width, width), width)
        dq_ref[:, cols] = q
        made = q * wq_ref[:, cols].astype(f32)
        total += made[:, :pair] + made[:, pair:]
        a_kv, b_kv = a[:rows, pair:], b[:rows, pair:]
        lane = lax.broadcasted_iota(jnp.int32, a_kv.shape, 1)
        key = jnp.where(lane < HEAD_DIM, a_kv, pltpu.roll(b_kv, HEAD_DIM, 1))
        val = jnp.where(lane < HEAD_DIM, pltpu.roll(a_kv, HEAD_DIM, 1), b_kv)
        cols = pl.ds(pl.multiple_of(source * pair, pair), pair)
        dk_ref[:, cols] = key
        dv_ref[:, cols] = val
        total += key * wk_ref[:, cols].astype(f32) + val * wv_ref[:, cols].astype(f32)
        wo_ref[2 * source, 0] = a[rows : rows + wo_ref.shape[2]]
        wo_ref[2 * source + 1, 0] = b[rows : rows + wo_ref.shape[2]]
        if k == 0:
            dg2_ref[...] = a[rows + wo_ref.shape[2] :][:1]
    dg_ref[...] = jnp.sum(jnp.transpose(total), axis=0, keepdims=True) / gain_ref[...]


def dense_out_call(at, own, other, wq, wk, wv, gain, wo_shape):
    held = [*own[0], *own[1], *other[0], *other[1]]
    streams, parts = 2, len(own[0])
    chips, depth, width = held[0].shape
    features = wq.shape[0]
    groups = 2 * chips
    rows = features // (streams * parts)
    block_cols = wo_shape[1] // width
    per_block = streams * parts // block_cols
    wo_rows = wo_shape[0] // groups // per_block
    by_rows = lambda w: pl.BlockSpec((rows, w.shape[1]), lambda s, r, at: (s * parts + r, 0))
    gain_spec = pl.BlockSpec((1, rows), lambda s, r, at: (0, s * parts + r))
    outs = pl.pallas_call(
        dense_out_kernel,
        grid_spec=pltpu.PrefetchScalarGridSpec(
            num_scalar_prefetch=1,
            grid=(streams, parts),
            in_specs=[pl.BlockSpec(memory_space=pltpu.VMEM)] * len(held)
            + [by_rows(wq), by_rows(wk), by_rows(wv), gain_spec],
            out_specs=[
                by_rows(wq),
                by_rows(wk),
                by_rows(wv),
                gain_spec,
                pl.BlockSpec(
                    (groups, 1, wo_rows, width),
                    lambda s, r, at: (
                        0,
                        lax.rem(s * parts + r, per_block),
                        0,
                        lax.div(s * parts + r, per_block),
                    ),
                ),
                pl.BlockSpec((1, width), lambda s, r, at: (0, lax.div(s * parts + r, per_block))),
            ],
            scratch_shapes=[pltpu.VMEM((chips, depth, width), bf16)] * 2
            + [pltpu.VMEM((8, 128), f32)],
        ),
        out_shape=[
            jax.ShapeDtypeStruct(wq.shape, f32),
            jax.ShapeDtypeStruct(wk.shape, f32),
            jax.ShapeDtypeStruct(wv.shape, f32),
            jax.ShapeDtypeStruct((1, features), f32),
            jax.ShapeDtypeStruct((groups, per_block, wo_rows, wo_shape[1]), f32),
            jax.ShapeDtypeStruct((1, wo_shape[1]), f32),
        ],
        compiler_params=params(28, "arbitrary", "arbitrary"),
        cost_estimate=cost(2 * wq.size, 2.4e7),
        name="dense_weights_out",
    )(at, *held, wq, wk, wv, gain)
    return (*outs[:4], outs[4].reshape(wo_shape), outs[5])


def weights_out_kernel(wide_ref, wq_ref, wk_ref, wv_ref, gain_ref, dq_ref, dk_ref, dv_ref, dg_ref):
    groups, rows, width = wide_ref.shape
    pair = width // 2
    total = jnp.zeros((rows, pair), f32)
    for g in range(groups):
        part = wide_ref[g, :, :pair].astype(f32)
        at = slice(g * pair, (g + 1) * pair)
        dq_ref[:, at] = part
        total += part * wq_ref[:, at].astype(f32)
    for g in range(groups // 2):
        a = wide_ref[2 * g, :, pair:].astype(f32)
        b = wide_ref[2 * g + 1, :, pair:].astype(f32)
        lane = lax.broadcasted_iota(jnp.int32, a.shape, 1)
        at = slice(g * pair, (g + 1) * pair)
        k = jnp.where(lane < HEAD_DIM, a, pltpu.roll(b, HEAD_DIM, 1))
        v = jnp.where(lane < HEAD_DIM, pltpu.roll(a, HEAD_DIM, 1), b)
        dk_ref[:, at] = k
        dv_ref[:, at] = v
        total += k * wk_ref[:, at].astype(f32) + v * wv_ref[:, at].astype(f32)
    dg_ref[...] = jnp.sum(jnp.transpose(total), axis=0, keepdims=True) / gain_ref[...]


def weights_out_call(wide, wq, wk, wv, gain):
    chunks, groups, rows, width = wide.shape
    features = chunks * rows
    by_rows = lambda w: pl.BlockSpec((rows, w.shape[1]), lambda c: (c, 0))
    return pl.pallas_call(
        weights_out_kernel,
        grid=(chunks,),
        in_specs=[
            pl.BlockSpec((None, groups, rows, width), lambda c: (c, 0, 0, 0)),
            by_rows(wq),
            by_rows(wk),
            by_rows(wv),
            pl.BlockSpec((1, rows), lambda c: (0, c)),
        ],
        out_specs=[
            by_rows(wq),
            by_rows(wk),
            by_rows(wv),
            pl.BlockSpec((1, rows), lambda c: (0, c)),
        ],
        out_shape=[
            jax.ShapeDtypeStruct(wq.shape, f32),
            jax.ShapeDtypeStruct(wk.shape, f32),
            jax.ShapeDtypeStruct(wv.shape, f32),
            jax.ShapeDtypeStruct((1, features), f32),
        ],
        compiler_params=params(32, "arbitrary"),
        cost_estimate=cost(2 * wq.size, 1.6e7),
        name="attention_weights_out",
    )(wide, wq, wk, wv, gain)


def last_kernel(d_ref, wq_ref, wk_ref, wv_ref, x_ref, gain_ref, dmid_ref, out_ref):
    groups, rows, width = d_ref.shape
    pair = width // 2
    dq = jnp.concatenate([d_ref[g, :, :pair] for g in range(groups)], axis=1)
    grad = dot_nt(dq, wq_ref[...])
    keys, vals = [], []
    for at in range(groups // 2):
        a = d_ref[2 * at, :, pair:].astype(f32)
        b = d_ref[2 * at + 1, :, pair:].astype(f32)
        lane = lax.broadcasted_iota(jnp.int32, a.shape, 1)
        keys.append(jnp.where(lane < HEAD_DIM, a, pltpu.roll(b, HEAD_DIM, 1)).astype(bf16))
        vals.append(jnp.where(lane < HEAD_DIM, pltpu.roll(a, HEAD_DIM, 1), b).astype(bf16))
    grad = grad + dot_nt(jnp.concatenate(keys, axis=1), wk_ref[...])
    grad = grad + dot_nt(jnp.concatenate(vals, axis=1), wv_ref[...])
    x = x_ref[...].astype(f32)
    scale = lax.rsqrt(jnp.mean(x * x, axis=-1, keepdims=True) + norm_eps)
    unit = x * scale
    w = gain_ref[...] * grad
    out_ref[...] = dmid_ref[...] + scale * (w - unit * jnp.mean(w * unit, axis=-1, keepdims=True))


def last_call(d, wq, wk, wv, x, gain, dmid):
    rows, features = x.shape
    return pl.pallas_call(
        last_kernel,
        out_shape=jax.ShapeDtypeStruct((rows, features), f32),
        compiler_params=params(40),
        cost_estimate=cost(4 * rows * features * features, 8e6),
        name="input_gradient",
    )(d, wq, wk, wv, x, gain, dmid)


def swap(values, axis, bit):
    return lax.ppermute(values, axis, [(i, i ^ bit) for i in range(lax.axis_size(axis))])


def half_sum(values, axis, bit):
    half = values.shape[0] // 2
    upper = ((lax.axis_index(axis) & bit) > 0).astype(jnp.int32)
    came = swap(lax.dynamic_slice_in_dim(values, (1 - upper) * half, half), axis, bit)
    mine = lax.dynamic_slice_in_dim(values, upper * half, half)
    return (mine.astype(f32) + came.astype(f32)).astype(bf16)


def relative_sum(kept, sent, axis, bits):
    while True:
        kept = (kept.astype(f32) + swap(sent, axis, bits[0]).astype(f32)).astype(bf16)
        bits = bits[1:]
        if not bits:
            return kept
        half = kept.shape[0] // 2
        kept, sent = kept[:half], kept[half:]


def join_parts(stream, axis, bits):
    shape = stream.shape
    for bit in bits[::-1]:
        stream = jnp.stack([stream, swap(stream, axis, bit)])
    return stream.reshape(-1, *shape)


def body(
    layer_input,
    first_gain,
    query_weight,
    key_weight,
    value_weight,
    output_weight,
    second_gain,
    gate_weight,
    up_weight,
    down_weight,
    expert_ids,
    gate_values,
    positions,
    cotangent,
):
    micro, _, per_device, features = layer_input.shape
    devices = lax.axis_size("seq")
    replicas = lax.axis_size("dp")
    seq_place = lax.axis_index("seq")
    rows = micro * per_device
    local_experts = gate_weight.shape[0]
    groups = key_weight.shape[1] // HEAD_DIM
    pair = query_weight.shape[1] // groups
    copies = devices // groups

    dp_bits = [1 << i for i in range(replicas.bit_length() - 1)]

    def spread(blocks):
        if copies > 1:
            blocks = jnp.repeat(blocks, copies, axis=0)
        return lax.all_to_all(blocks, "seq", 0, 0, tiled=True)

    def unspread(blocks):
        return lax.all_to_all(blocks, "seq", 0, 0, tiled=True)[::copies]

    x = layer_input.reshape(rows, features)
    cot = cotangent.reshape(rows, features)
    gain_one = first_gain.reshape(1, features)
    gain_two = second_gain.reshape(1, features)
    pos_all = lax.all_to_all(
        jnp.broadcast_to(positions.reshape(1, rows), (devices, rows)), "seq", 0, 0, tiled=True
    )
    x_all = lax.all_gather(x, "seq", axis=0)
    cos_all, sin_all = rope_tables(pos_all.reshape(-1), pair)
    mine = seq_place * local_experts + jnp.arange(local_experts, dtype=jnp.int32)
    ids = expert_ids[:, 0]
    gates = gate_values[:, 0].astype(f32)
    routed = jnp.sum(
        jnp.where(ids[..., None] == mine, gates[..., None], 0.0), axis=2
    )
    routed = routed.reshape(micro, devices, per_device, local_experts)
    routed = jnp.transpose(routed, (1, 0, 2, 3)).reshape(devices * rows, local_experts)
    group = seq_place // copies
    w_own = jnp.concatenate(
        [
            lax.dynamic_slice_in_dim(query_weight, group * pair, pair, axis=1),
            lax.dynamic_slice_in_dim(key_weight, group * HEAD_DIM, HEAD_DIM, axis=1),
            lax.dynamic_slice_in_dim(value_weight, group * HEAD_DIM, HEAD_DIM, axis=1),
        ],
        axis=1,
    )
    cot_pair = jnp.stack([cot, swap(cot, "seq", 1)])
    cos_all, sin_all, routed, w_own, cot_pair = lax.optimization_barrier(
        (cos_all, sin_all, routed, w_own, cot_pair)
    )
    x_all, cot_then, cos_all, sin_all, routed, w_own, cot_pair = lax.optimization_barrier(
        (x_all, cot, cos_all, sin_all, routed, w_own, cot_pair)
    )
    cot_all = lax.all_gather(cot_then, "seq", axis=0)
    cots = (cot_pair, cot_all)

    qkv, first_all = qkv_call(x_all, gain_one, cos_all, sin_all, w_own)
    qkv = qkv.reshape(devices, micro, per_device, 2 * pair)
    mix, log_total = attend_call(qkv)
    mix = unspread(mix.reshape(devices, rows, pair))
    mixed, middle, second_low = post_call(mix, output_weight, x, gain_two)

    chips = devices // 2
    chip, core = seq_place // 2, seq_place % 2
    onward = [(i, (i + 2) % devices) for i in range(devices)]
    dp_place = lax.axis_index("dp")
    first_bit = dp_place & 1
    last_bit = dp_place >> (len(dp_bits) - 1)
    held, kept, running, places = second_low, (), None, []
    for hop in range(chips):
        following = lax.ppermute(held, "seq", onward) if hop < chips - 1 else None
        other = swap(held, "seq", 1)
        source = 2 * ((chip - hop) % chips)
        near_cot = [jnp.int32(0), jnp.int32(1)] if hop == 0 else [source + core, source + 1 - core]
        place = jnp.stack(
            [source + core, source + 1 - core, 1 - first_bit, 1 - last_bit, *near_cot]
        )
        place = place.astype(jnp.int32)
        places.append(place[:2])
        dx, *kept = expert_call(
            hop, place, held, other, cots[hop > 0], routed, gate_weight, up_weight, down_weight, kept
        )
        if following is not None:
            following, dx = lax.optimization_barrier((following, dx))
        part = dx[0].astype(f32) + swap(dx[1], "seq", 1).astype(f32)
        if hop == 0:
            own_part = part
        else:
            if running is not None:
                part = part + running.astype(f32)
            part = part.astype(bf16)
            if following is not None:
                part, following = lax.optimization_barrier((part, following))
            else:
                part, kept = lax.optimization_barrier((part, kept))
            running = lax.ppermute(part, "seq", onward)
        held = following
    second_grad = (own_part + running.astype(f32)).astype(bf16)
    tokens, hidden_a, hidden_b, gate_low, up_low, slot_a, slot_b = kept

    def weight_parts(at, tokens, hidden_a, hidden_b, gate_low, up_low, slot_a, slot_b):
        pairs = (
            (tokens, gate_low[at]),
            (tokens, up_low[at]),
            (hidden_a[at], slot_a[at]),
            (hidden_b[at], slot_b[at]),
        )
        return [
            lax.dot_general(a, b, TN, preferred_element_type=f32).astype(bf16) for a, b in pairs
        ]

    leaving = weight_parts(0, *kept)
    part_bits = (dp_bits[0], dp_bits[-1], dp_bits[0], dp_bits[-1])
    stream_bits = (dp_bits, dp_bits[::-1])
    came = [swap(values, "dp", bit) for values, bit in zip(leaving, part_bits)]
    leaving, second_grad = lax.optimization_barrier((leaving, second_grad))

    mg_send, proj, middle_grad, gain_two_part = turn_call(
        second_grad, middle, gain_two, cot, output_weight, groups
    )
    mg = spread(mg_send)
    kept, _ = lax.optimization_barrier((kept, mg_send))
    mixed, proj, came[2:] = lax.optimization_barrier((mixed, proj, came[2:]))
    dense = output_weight_call(mixed, proj, gain_two_part, devices)
    dense_own = dense
    staying = weight_parts(1, *kept)
    turned = sum(((dp_place >> i) & 1) << (len(dp_bits) - 1 - i) for i in range(len(dp_bits)))
    part_at = jnp.stack([turned, dp_place]).astype(jnp.int32)
    low_at = jnp.bitwise_and(part_at, replicas // 2 - 1)
    keep_a, send_a, keep_b, send_b = part_sum_call(low_at, replicas // 2, came, staying)
    mg, keep_a, send_a, keep_b, send_b = lax.optimization_barrier(
        (mg, keep_a, send_a, keep_b, send_b)
    )
    streams = [
        relative_sum(keep_a, send_a, "dp", stream_bits[0][1:]),
        relative_sum(keep_b, send_b, "dp", stream_bits[1][1:]),
    ]
    dense = dense_own
    dense = lax.psum_scatter(dense, "seq", scatter_dimension=0)
    table_shape = (devices, micro, per_device, pair)
    dqkv = attend_back_call(
        qkv,
        mg.reshape(devices, micro, per_device, pair),
        log_total,
        cos_all.reshape(table_shape),
        sin_all.reshape(table_shape),
    )
    dqkv, streams = lax.optimization_barrier((dqkv, streams))
    near = [
        [v[0], swap(v[0], "dp", bits[-1])] for v, bits in zip(streams, stream_bits)
    ]
    back = unspread(dqkv.reshape(devices, rows, 2 * pair))
    d_all = dqkv.reshape(devices * rows, 2 * pair)
    first_tokens = first_all.reshape(devices * rows, features)
    part = lax.dot_general(first_tokens, d_all, TN, preferred_element_type=f32)
    dense = dense.reshape(dense.shape[-2], features)
    each = output_weight.shape[0] // devices
    if copies == 1:
        width = 2 * pair
        kept_pieces, sent_pieces = joint_call(part_at, part, dense, replicas)
        first = [
            kept_pieces[at].astype(f32) + swap(sent_pieces[at], "dp", bits[0]).astype(f32)
            for at, bits in enumerate(stream_bits)
        ]
        kept, sent_pieces = lax.optimization_barrier((kept, sent_pieces))
        moe_place = jnp.concatenate(places + [(1 - first_bit).astype(jnp.int32).reshape(1)])
        moe_all = moe_call(moe_place, kept[1], routed, down_weight, devices)
        far = [swap(v[0], "dp", bits[-2]) for v, bits in zip(streams, stream_bits)]
        first, near = lax.optimization_barrier(([v.astype(bf16) for v in first], near))
        own = [
            relative_sum(v[: replicas // 4], v[replicas // 4 :], "dp", bits[1:])
            for v, bits in zip(first, stream_bits)
        ]
        own = jnp.concatenate(own, axis=0)
        own, far, moe_all = lax.optimization_barrier((own, far, moe_all))
        backward = [(i, (i - 2) % devices) for i in range(devices)]
        round_ring = {0: own}
        for k in range(1, chips // 2 + 1):
            round_ring[k] = lax.ppermute(round_ring[k - 1], "seq", onward)
            if chips - k > k:
                round_ring[chips - k] = lax.ppermute(
                    round_ring[(chips - k + 1) % chips], "seq", backward
                )
        held = jnp.stack([round_ring[k] for k in range(chips)])
        passed = [swap(v[1], "dp", bits[-2]) for v, bits in zip(near, stream_bits)]
        held, moe_all, back, passed = lax.optimization_barrier((held, moe_all, back, passed))
        moe = lax.psum_scatter(moe_all, "seq", scatter_dimension=0)
        layer_output = (middle + residual_scale * moe.astype(f32)).astype(bf16)
    else:
        far = [swap(v[0], "dp", bits[-2]) for v, bits in zip(streams, stream_bits)]
        passed = [swap(v[1], "dp", bits[-2]) for v, bits in zip(near, stream_bits)]
    expert_pieces = []
    for (here, first), second, third, bits in zip(near, far, passed, stream_bits):
        pieces = [here, first, second, third]
        for bit in bits[:-2][::-1]:
            pieces = pieces + [swap(p, "dp", bit) for p in pieces]
        expert_pieces.append(pieces)
    input_grad = last_call(
        back, query_weight, key_weight, value_weight, x, gain_one, middle_grad
    )
    if copies == 1:
        gate_sum, up_sum, down_sum = expert_out_call(
            part_at, *expert_pieces, gate_weight.shape, down_weight.shape
        )
        full = []
        for at, bits in enumerate(stream_bits):
            pieces = [held[:, at]]
            for bit in bits[::-1]:
                pieces = pieces + [swap(p, "dp", bit) for p in pieces]
            full.append(pieces)
        last = [pieces.pop() for pieces in full]
        last, gate_sum, up_sum, down_sum, input_grad = lax.optimization_barrier(
            (last, gate_sum, up_sum, down_sum, input_grad)
        )
        full = [pieces + [end] for pieces, end in zip(full, last)]
        other = [[swap(p, "seq", 1) for p in pieces] for pieces in full]
        where_at = jnp.stack([turned, dp_place, chip, core]).astype(jnp.int32)
        (
            query_weight_grad,
            key_weight_grad,
            value_weight_grad,
            first_gain_grad,
            output_weight_grad,
            second_gain_grad,
        ) = dense_out_call(
            where_at, full, other, query_weight, key_weight, value_weight, gain_one, output_weight.shape
        )
    else:
        gate_sum, up_sum, down_sum = expert_out_call(
            part_at, *expert_pieces, gate_weight.shape, down_weight.shape
        )
        for bit in dp_bits:
            dense = (dense.astype(f32) + swap(dense, "dp", bit).astype(f32)).astype(bf16)
        dense = lax.all_gather(dense, "seq", axis=0).astype(f32)
        output_weight_grad = dense[:, :each].reshape(output_weight.shape)
        moe_place = jnp.concatenate(places + [(1 - first_bit).astype(jnp.int32).reshape(1)])
        moe_all = moe_call(moe_place, kept[1], routed, down_weight, devices)
        moe = lax.psum_scatter(moe_all, "seq", scatter_dimension=0)
        layer_output = (middle + residual_scale * moe.astype(f32)).astype(bf16)
        second_gain_grad = dense[0, each]
        part = part.astype(bf16)
        for bit in dp_bits[::-1]:
            part = half_sum(part, "dp", bit)
        wide = lax.all_gather(part, ("dp", "seq"), axis=0)
        wide = wide.reshape(replicas, devices, features // replicas, 2 * pair)[:, ::copies]
        query_weight_grad, key_weight_grad, value_weight_grad, first_gain_grad = weights_out_call(
            wide, query_weight, key_weight, value_weight, gain_one
        )
    second_gain_grad = second_gain_grad.reshape(features)
    return (
        layer_output.reshape(layer_input.shape),
        input_grad.reshape(layer_input.shape),
        first_gain_grad.reshape(features),
        query_weight_grad,
        key_weight_grad,
        value_weight_grad,
        output_weight_grad,
        second_gain_grad,
        gate_sum,
        up_sum,
        down_sum,
    )


def solution(mesh):
    return jax.shard_map(
        body,
        mesh=mesh,
        in_specs=(
            P(None, "dp", "seq", None),
            P(),
            P(),
            P(),
            P(),
            P(),
            P(),
            P("seq", None, None),
            P("seq", None, None),
            P("seq", None, None),
            P(None, "dp", None, None),
            P(None, "dp", None, None),
            P(None, "dp", "seq"),
            P(None, "dp", "seq", None),
        ),
        out_specs=(
            P(None, "dp", "seq", None),
            P(None, "dp", "seq", None),
            P(),
            P(),
            P(),
            P(),
            P(),
            P(),
            P("seq", None, None),
            P("seq", None, None),
            P("seq", None, None),
        ),
        check_vma=False,
    )
```

```python
from functools import partial

import jax
import jax.numpy as jnp
from jax import lax
from jax.experimental import pallas as pl
from jax.experimental.pallas import tpu as pltpu
from jax.sharding import PartitionSpec as P

HEAD_DIM = 64

rope_theta = 10000.0
attention_scale = 0.015625
residual_scale = 0.22
norm_eps = 1e-06
masked_score = -1e30

f32 = jnp.float32
bf16 = jnp.bfloat16
NT = (((1,), (1,)), ((), ()))
TN = (((0,), (0,)), ((), ()))


def dot(a, b):
    return jnp.dot(a, b, preferred_element_type=f32)


def dot_nt(a, b):
    return lax.dot_general(a, b, NT, preferred_element_type=f32)


def params(mib, *semantics):
    return pltpu.CompilerParams(
        vmem_limit_bytes=mib * 1024 * 1024, dimension_semantics=semantics or None
    )


def cost(flops, nbytes, trans=0):
    return pl.CostEstimate(
        flops=int(flops / 8), bytes_accessed=int(nbytes / 8), transcendentals=int(trans / 8)
    )


def whole(shape):
    return pl.BlockSpec(shape, lambda *_: (0,) * len(shape))


def rope_tables(positions, width):
    half = HEAD_DIM // 2
    exponent = jnp.arange(half, dtype=f32) * (-2.0 / HEAD_DIM)
    angles = positions.astype(f32)[:, None] * (rope_theta**exponent)[None, :]
    cosine, sine = jnp.cos(angles), jnp.sin(angles)
    copies = width // HEAD_DIM
    cos_row = jnp.concatenate([cosine, cosine] * copies, axis=1)
    sin_row = jnp.concatenate([-sine, sine] * copies, axis=1)
    return cos_row, sin_row


def partner(values):
    width = values.shape[1]
    half = HEAD_DIM // 2
    lane = lax.broadcasted_iota(jnp.int32, values.shape, 1)
    ahead = pltpu.roll(values, width - half, 1)
    behind = pltpu.roll(values, half, 1)
    return jnp.where(lane % HEAD_DIM < half, ahead, behind)


def qkv_kernel(x_ref, gain_ref, cos_ref, sin_ref, w_ref, qkv_ref, low_ref):
    pair = 2 * HEAD_DIM
    x = x_ref[0].astype(f32)
    scale = lax.rsqrt(jnp.mean(x * x, axis=-1, keepdims=True) + norm_eps)
    low = (x * scale * gain_ref[...]).astype(bf16)
    low_ref[0] = low
    cosine, sine = cos_ref[...], sin_ref[...]
    made = dot(low, w_ref[...])
    q, kv = made[:, :pair], made[:, pair:]
    q = (q * cosine + partner(q) * sine) * attention_scale
    qkv_ref[0, :, :pair] = q.astype(bf16)
    lane = lax.broadcasted_iota(jnp.int32, kv.shape, 1)
    turned = kv * cosine + partner(kv) * sine
    qkv_ref[0, :, pair:] = jnp.where(lane < HEAD_DIM, turned, kv).astype(bf16)


def qkv_call(x_all, gain, cos_all, sin_all, w_own):
    blocks, rows, features = x_all.shape
    pair = 2 * HEAD_DIM
    return pl.pallas_call(
        qkv_kernel,
        grid=(blocks,),
        in_specs=[
            pl.BlockSpec((1, rows, features), lambda s: (s, 0, 0)),
            whole((1, features)),
            pl.BlockSpec((rows, pair), lambda s: (s, 0)),
            pl.BlockSpec((rows, pair), lambda s: (s, 0)),
            whole(w_own.shape),
        ],
        out_specs=[
            pl.BlockSpec((1, rows, 2 * pair), lambda s: (s, 0, 0)),
            pl.BlockSpec((1, rows, features), lambda s: (s, 0, 0)),
        ],
        out_shape=[
            jax.ShapeDtypeStruct((blocks, rows, 2 * pair), bf16),
            jax.ShapeDtypeStruct((blocks, rows, features), bf16),
        ],
        compiler_params=params(58, "arbitrary"),
        cost_estimate=cost(4 * blocks * rows * features * pair, 14e6),
        name="norm_qkv_rope",
    )(x_all, gain, cos_all, sin_all, w_own)


def split_heads(block, first):
    wide = block.astype(f32)
    lane = lax.broadcasted_iota(jnp.int32, wide.shape, 1)
    turned = pltpu.roll(wide, HEAD_DIM, 1)
    if first:
        parts = [jnp.where(lane < HEAD_DIM, wide, 0.0), jnp.where(lane < HEAD_DIM, turned, 0.0)]
    else:
        parts = [jnp.where(lane >= HEAD_DIM, turned, 0.0), jnp.where(lane >= HEAD_DIM, wide, 0.0)]
    return jnp.concatenate(parts, axis=0).astype(bf16)


def join_heads(turned):
    rows = turned.shape[1] // 2
    return jnp.transpose(jnp.concatenate([turned[:, :rows], turned[:, rows:]], axis=0))


def scores_of(kv, q2, rows):
    scores = dot_nt(kv, q2)
    count = scores.shape[0]
    own = scores[count - rows :]
    key_at = lax.broadcasted_iota(jnp.int32, own.shape, 0)
    query_at = lax.broadcasted_iota(jnp.int32, own.shape, 1) % rows
    own = jnp.where(key_at <= query_at, own, masked_score)
    if count == rows:
        return own
    return jnp.concatenate([scores[: count - rows], own], axis=0)


def attend_kernel(qkv_ref, out_ref, log_ref):
    blocks, _, rows, width = qkv_ref.shape
    pair = width // 2
    kv = qkv_ref[:, 0, :, pair:].reshape(blocks * rows, pair)
    kv_t = jnp.transpose(kv)
    for at in range(blocks):
        count = (at + 1) * rows
        q2 = split_heads(qkv_ref[at, 0, :, :pair], True)
        scores = scores_of(kv[:count], q2, rows)
        top = jnp.max(scores, axis=0, keepdims=True)
        weights = jnp.exp(scores - top)
        total = jnp.sum(weights, axis=0, keepdims=True)
        out_t = dot(kv_t[:, :count], weights.astype(bf16))
        out_ref[at, 0] = join_heads(out_t[HEAD_DIM:] / total).astype(bf16)
        log_ref[at, 0] = top + jnp.log(total)


def attend_call(qkv):
    blocks, micro, rows, width = qkv.shape
    pair = width // 2
    length = blocks * rows
    return pl.pallas_call(
        attend_kernel,
        grid=(micro,),
        in_specs=[pl.BlockSpec((blocks, 1, rows, width), lambda m: (0, m, 0, 0))],
        out_specs=[
            pl.BlockSpec((blocks, 1, rows, pair), lambda m: (0, m, 0, 0)),
            pl.BlockSpec((blocks, 1, 1, 2 * rows), lambda m: (0, m, 0, 0)),
        ],
        out_shape=[
            jax.ShapeDtypeStruct((blocks, micro, rows, pair), bf16),
            jax.ShapeDtypeStruct((blocks, micro, 1, 2 * rows), f32),
        ],
        compiler_params=params(48, "arbitrary"),
        cost_estimate=cost(
            micro * length * length * 512, 3 * qkv.size, micro * length * length
        ),
        name="attention_forward",
    )(qkv)


def attend_back_kernel(qkv_ref, grad_ref, log_ref, cos_ref, sin_ref, out_ref, dkv_ref):
    blocks, _, rows, width = qkv_ref.shape
    pair = width // 2
    kv = qkv_ref[:, 0, :, pair:].reshape(blocks * rows, pair)
    kv_t = jnp.transpose(kv)
    dkv_ref[...] = jnp.zeros_like(dkv_ref)
    for at in range(blocks):
        count = (at + 1) * rows
        q2 = split_heads(qkv_ref[at, 0, :, :pair], True)
        g2 = split_heads(grad_ref[at, 0], False)
        scores = scores_of(kv[:count], q2, rows)
        prob = jnp.exp(scores - log_ref[at, 0])
        prob_grad = dot_nt(kv[:count], g2)
        delta = jnp.sum(prob * prob_grad, axis=0, keepdims=True)
        score_grad = (prob * (prob_grad - delta)).astype(bf16)
        dkv_ref[:count] += dot(score_grad, q2) + dot(prob.astype(bf16), g2)
        dq_t = dot(kv_t[:, :count], score_grad)
        dq = join_heads(dq_t[:HEAD_DIM] * attention_scale)
        dq = dq * cos_ref[at, 0] - partner(dq) * sin_ref[at, 0]
        out_ref[at, 0, :, :pair] = dq.astype(bf16)
    for at in range(blocks):
        dkv = dkv_ref[at * rows : (at + 1) * rows]
        lane = lax.broadcasted_iota(jnp.int32, dkv.shape, 1)
        turned = dkv * cos_ref[at, 0] - partner(dkv) * sin_ref[at, 0]
        out_ref[at, 0, :, pair:] = jnp.where(lane < HEAD_DIM, turned, dkv).astype(bf16)


def attend_back_call(qkv, grads, log_total, cos_all, sin_all):
    blocks, micro, rows, width = qkv.shape
    pair = width // 2
    length = blocks * rows
    spec = lambda lanes: pl.BlockSpec((blocks, 1, rows, lanes), lambda m: (0, m, 0, 0))
    return pl.pallas_call(
        attend_back_kernel,
        grid=(micro,),
        in_specs=[
            spec(width),
            spec(pair),
            pl.BlockSpec((blocks, 1, 1, 2 * rows), lambda m: (0, m, 0, 0)),
            spec(pair),
            spec(pair),
        ],
        out_specs=spec(width),
        out_shape=jax.ShapeDtypeStruct(qkv.shape, bf16),
        scratch_shapes=[pltpu.VMEM((length, pair), f32)],
        compiler_params=params(56, "arbitrary"),
        cost_estimate=cost(
            micro * length * length * 1280, 10 * qkv.size, micro * length * length
        ),
        name="attention_backward",
    )(qkv, grads, log_total, cos_all, sin_all)


def post_kernel(mix_ref, wo_ref, x_ref, gain_ref, mixed_ref, middle_ref, low_ref):
    mixed = jnp.concatenate([mix_ref[g] for g in range(mix_ref.shape[0])], axis=1)
    mixed_ref[...] = mixed
    middle = x_ref[...].astype(f32) + residual_scale * dot(mixed, wo_ref[...])
    middle_ref[...] = middle
    scale = lax.rsqrt(jnp.mean(middle * middle, axis=-1, keepdims=True) + norm_eps)
    low_ref[...] = (middle * scale * gain_ref[...]).astype(bf16)


def post_call(mix, wo, x, gain):
    rows, features = x.shape
    return pl.pallas_call(
        post_kernel,
        out_shape=[
            jax.ShapeDtypeStruct((rows, wo.shape[0]), bf16),
            jax.ShapeDtypeStruct((rows, features), f32),
            jax.ShapeDtypeStruct((rows, features), bf16),
        ],
        compiler_params=params(32),
        cost_estimate=cost(2 * rows * wo.size, 5e6),
        name="project_norm",
    )(mix, wo, x, gain)


def expert_kernel(place_ref, a_ref, b_ref, cot_ref, w_ref, wg_ref, wu_ref, wd_ref, *refs):
    dx_ref, x_ref, ha_ref, hb_ref, dg_ref, du_ref, sa_ref, sb_ref = refs[-8:]
    step = pl.program_id(0)
    first, second = place_ref[2], place_ref[3]
    half = sa_ref.shape[2]

    @pl.when(step == 0)
    def _():
        x_ref[...] = a_ref[...]

    @pl.when(step == 1)
    def _():
        x_ref[...] = b_ref[...]

    x = x_ref[...]
    cot = cot_ref[0].astype(f32)
    weight = residual_scale * w_ref[...]
    total = None
    for e in range(wg_ref.shape[0]):
        gate = dot(x, wg_ref[e])
        up = dot(x, wu_ref[e])
        slot_grad = (weight[:, e : e + 1] * cot).astype(bf16)
        to_a, to_b = jnp.bitwise_xor(first, e), jnp.bitwise_xor(second, e)
        sa_ref[to_a] = slot_grad[:, :half]
        sb_ref[to_b] = slot_grad[:, half:]
        hidden_grad = dot_nt(slot_grad, wd_ref[e])
        sig = 0.5 * jnp.tanh(0.5 * gate) + 0.5
        silu = gate * sig
        hidden = (silu * up).astype(bf16)
        ha_ref[to_a] = hidden
        hb_ref[to_b] = hidden
        gate_grad = (hidden_grad * up * (sig + silu * (1.0 - sig))).astype(bf16)
        up_grad = (hidden_grad * silu).astype(bf16)
        dg_ref[to_a] = gate_grad
        du_ref[to_b] = up_grad
        term = dot_nt(gate_grad, wg_ref[e]) + dot_nt(up_grad, wu_ref[e])
        total = term if total is None else total + term
    dx_ref[0] = total.astype(bf16)


def expert_call(at, place, own, other, cots, weight, wg, wu, wd, kept):
    rows, features = own.shape
    count, _, hidden = wg.shape
    tokens = weight.shape[0]
    inner = jax.ShapeDtypeStruct((count, tokens, hidden), bf16)
    outer = jax.ShapeDtypeStruct((count, tokens, features // 2), bf16)
    inner_spec = pl.BlockSpec((count, rows, hidden), lambda s, place: (0, 2 * at + s, 0))
    outer_spec = pl.BlockSpec((count, rows, features // 2), lambda s, place: (0, 2 * at + s, 0))
    fixed = lambda shape: pl.BlockSpec(shape, lambda s, place: (0,) * len(shape))
    any_spec = pl.BlockSpec(memory_space=pl.ANY)
    first = 8
    return pl.pallas_call(
        expert_kernel,
        grid_spec=pltpu.PrefetchScalarGridSpec(
            num_scalar_prefetch=1,
            grid=(2,),
            in_specs=[
                fixed((rows, features)),
                fixed((rows, features)),
                pl.BlockSpec((1, rows, features), lambda s, place: (place[4 + s], 0, 0)),
                pl.BlockSpec((rows, count), lambda s, place: (place[s], 0)),
                fixed(wg.shape),
                fixed(wu.shape),
                fixed(wd.shape),
            ]
            + [any_spec] * len(kept),
            out_specs=[
                pl.BlockSpec((1, rows, features), lambda s, place: (s, 0, 0)),
                pl.BlockSpec((rows, features), lambda s, place: (2 * at + s, 0)),
            ]
            + [inner_spec] * 4
            + [outer_spec] * 2,
        ),
        out_shape=[
            jax.ShapeDtypeStruct((2, rows, features), bf16),
            jax.ShapeDtypeStruct((tokens, features), bf16),
            inner,
            inner,
            inner,
            inner,
            outer,
            outer,
        ],
        input_output_aliases={first + i: 1 + i for i in range(len(kept))},
        compiler_params=params(48, "arbitrary"),
        cost_estimate=cost(20 * rows * wg.size, 2e7, 2 * rows * hidden * count),
        name="experts",
    )(place, own, other, cots, weight, wg, wu, wd, *kept)


def part_sum_kernel(at_ref, *refs):
    inputs, outs = refs[:16], refs[16:]
    at = 0
    for out in outs:
        gate_came, gate_here, down_came, down_here = inputs[at : at + 4]
        rows = gate_came.shape[0]
        out[0, :rows] = (gate_came[...].astype(f32) + gate_here[...].astype(f32)).astype(bf16)
        out[0, rows:] = (down_came[...].astype(f32) + down_here[...].astype(f32)).astype(bf16)
        at += 4


def part_sum_call(at, per, came, here):
    gate_rows, down_rows = came[0].shape[0] // per, came[2].shape[0] // per
    width = came[0].shape[1]
    steps = per // 2
    specs, args, out_specs, out_shapes = [], [], [], []
    for stream in range(2):
        for sent in range(2):
            for which, rows in ((stream, gate_rows), (stream + 2, down_rows)):
                spec = pl.BlockSpec(
                    (rows, width),
                    lambda s, at, sent=sent, stream=stream: (
                        jnp.bitwise_xor(s + sent * steps, at[stream]),
                        0,
                    ),
                )
                specs += [spec, spec]
                args += [came[which], here[which]]
            out_specs.append(
                pl.BlockSpec((1, gate_rows + down_rows, width), lambda s, at: (s, 0, 0))
            )
            out_shapes.append(
                jax.ShapeDtypeStruct((steps, gate_rows + down_rows, width), bf16)
            )
    return pl.pallas_call(
        part_sum_kernel,
        grid_spec=pltpu.PrefetchScalarGridSpec(
            num_scalar_prefetch=1, grid=(steps,), in_specs=specs, out_specs=out_specs
        ),
        out_shape=out_shapes,
        compiler_params=params(60, "arbitrary"),
        cost_estimate=cost(0, 9e6),
        name="expert_part_sum",
    )(at, *args)


def joint_kernel(at_ref, *refs):
    for (part_ref, wo_ref, gain_ref), out_ref in ((refs[:3], refs[6]), (refs[3:6], refs[7])):
        rows = part_ref.shape[0]
        upto = rows + wo_ref.shape[0]
        out_ref[0, 0, :rows] = part_ref[...].astype(bf16)
        out_ref[0, 0, rows:upto] = wo_ref[...]
        out_ref[0, 0, upto:] = gain_ref[...]


def joint_call(at, part, dense, parts):
    features, width = part.shape
    pieces = 2 * parts
    rows = features // pieces
    block_cols = dense.shape[1] // width
    per_block = pieces // block_cols
    extra = 16
    wo_rows = (dense.shape[0] - extra) // per_block
    last = dense.shape[0] // extra - 1
    steps = parts // 2

    def piece(sent):
        return lambda s, p, at: s * parts + jnp.bitwise_xor(p + sent * steps, at[s])

    specs = []
    for sent in range(2):
        at_piece = piece(sent)
        specs.append(
            pl.BlockSpec((rows, width), lambda s, p, at, f=at_piece: (f(s, p, at), 0))
        )
        specs.append(
            pl.BlockSpec(
                (wo_rows, width),
                lambda s, p, at, f=at_piece: (
                    lax.rem(f(s, p, at), per_block),
                    lax.div(f(s, p, at), per_block),
                ),
            )
        )
        specs.append(
            pl.BlockSpec(
                (extra, width), lambda s, p, at, f=at_piece: (last, lax.div(f(s, p, at), per_block))
            )
        )
    out_spec = pl.BlockSpec((1, 1, rows + wo_rows + extra, width), lambda s, p, at: (s, p, 0, 0))
    out_shape = jax.ShapeDtypeStruct((2, steps, rows + wo_rows + extra, width), bf16)
    return pl.pallas_call(
        joint_kernel,
        grid_spec=pltpu.PrefetchScalarGridSpec(
            num_scalar_prefetch=1, grid=(2, steps), in_specs=specs, out_specs=[out_spec] * 2
        ),
        out_shape=[out_shape] * 2,
        compiler_params=params(32, "arbitrary", "arbitrary"),
        cost_estimate=cost(0, 2e6),
        name="dense_pieces",
    )(at, part, dense, dense, part, dense, dense)


def expert_out_kernel(at_ref, *refs):
    pieces, (gate_ref, up_ref, down_ref) = refs[:-3], refs[-3:]
    parts = len(pieces) // 2
    step = pl.program_id(0)
    rows = gate_ref.shape[1]
    half = down_ref.shape[2] // 2
    for which in range(parts):

        @pl.when(jnp.bitwise_xor(step, at_ref[0]) == which)
        def _():
            a_ref = pieces[which]
            gate_ref[0] = a_ref[:rows].astype(f32)
            down_ref[0, :, :half] = a_ref[rows:].astype(f32)

        @pl.when(jnp.bitwise_xor(step, at_ref[1]) == which)
        def _():
            b_ref = pieces[parts + which]
            up_ref[0] = b_ref[:rows].astype(f32)
            down_ref[0, :, half:] = b_ref[rows:].astype(f32)


def expert_out_call(at, a, b, gate_shape, down_shape):
    parts = len(a)
    held, width = a[0].shape
    count = gate_shape[0]
    per = parts // count
    gate_rows, down_rows = gate_shape[1] // per, down_shape[1] // per
    place = lambda r, at: (lax.div(r, per), lax.rem(r, per), 0)
    return pl.pallas_call(
        expert_out_kernel,
        grid_spec=pltpu.PrefetchScalarGridSpec(
            num_scalar_prefetch=1,
            grid=(parts,),
            in_specs=[pl.BlockSpec((held, width), lambda r, at: (0, 0))] * (2 * parts),
            out_specs=[
                pl.BlockSpec((1, gate_rows, gate_shape[2]), place),
                pl.BlockSpec((1, gate_rows, gate_shape[2]), place),
                pl.BlockSpec((1, down_rows, down_shape[2]), place),
            ],
        ),
        out_shape=[
            jax.ShapeDtypeStruct(gate_shape, f32),
            jax.ShapeDtypeStruct(gate_shape, f32),
            jax.ShapeDtypeStruct(down_shape, f32),
        ],
        compiler_params=params(40, "arbitrary"),
        cost_estimate=cost(0, 2e7),
        name="expert_weights_out",
    )(at, *a, *b)


def moe_kernel(place_ref, h_ref, w_ref, wd_ref, out_ref):
    weight = w_ref[...]
    total = None
    first = place_ref[pl.num_programs(0)]
    for e in range(wd_ref.shape[0]):
        term = weight[:, e : e + 1] * dot(h_ref[jnp.bitwise_xor(first, e)], wd_ref[e])
        total = term if total is None else total + term
    out_ref[0] = total.astype(bf16)


def moe_call(place, hidden, weight, wd, blocks):
    count, tokens, inner = hidden.shape
    features = wd.shape[2]
    rows = tokens // blocks
    return pl.pallas_call(
        moe_kernel,
        grid_spec=pltpu.PrefetchScalarGridSpec(
            num_scalar_prefetch=1,
            grid=(blocks,),
            in_specs=[
                pl.BlockSpec((count, rows, inner), lambda s, place: (0, s, 0)),
                pl.BlockSpec((rows, count), lambda s, place: (place[s], 0)),
                pl.BlockSpec(wd.shape, lambda s, place: (0, 0, 0)),
            ],
            out_specs=pl.BlockSpec((1, rows, features), lambda s, place: (place[s], 0, 0)),
        ),
        out_shape=jax.ShapeDtypeStruct((blocks, rows, features), bf16),
        compiler_params=params(60, "arbitrary"),
        cost_estimate=cost(2 * tokens * wd.size, 1.1e7),
        name="expert_outputs",
    )(place, hidden, weight, wd)


def turn_kernel(sg_ref, middle_ref, gain_ref, cot_ref, wo_ref, mg_ref, proj_ref, dmid_ref, dgain_ref):
    grad = sg_ref[...].astype(f32)
    middle = middle_ref[...]
    scale = lax.rsqrt(jnp.mean(middle * middle, axis=-1, keepdims=True) + norm_eps)
    unit = middle * scale
    dgain_ref[...] = jnp.sum(grad * unit, axis=0, keepdims=True)
    w = gain_ref[...] * grad
    dmid = cot_ref[...].astype(f32) + scale * (w - unit * jnp.mean(w * unit, axis=-1, keepdims=True))
    dmid_ref[...] = dmid
    proj = (residual_scale * dmid).astype(bf16)
    proj_ref[...] = proj
    mixed_grad = dot_nt(proj, wo_ref[...]).astype(bf16)
    groups, _, pair = mg_ref.shape
    for g in range(groups):
        mg_ref[g] = mixed_grad[:, g * pair : (g + 1) * pair]


def turn_call(sg, middle, gain, cot, wo, groups):
    rows, features = middle.shape
    pair = wo.shape[0] // groups
    return pl.pallas_call(
        turn_kernel,
        out_shape=[
            jax.ShapeDtypeStruct((groups, rows, pair), bf16),
            jax.ShapeDtypeStruct((rows, features), bf16),
            jax.ShapeDtypeStruct((rows, features), f32),
            jax.ShapeDtypeStruct((1, features), f32),
        ],
        compiler_params=params(32),
        cost_estimate=cost(2 * rows * wo.size, 6e6),
        name="norm_back_project_back",
    )(sg, middle, gain, cot, wo)


def output_weight_kernel(mixed_ref, proj_ref, dgain_ref, out_ref):
    held, each, features = out_ref.shape
    rows = mixed_ref.shape[1] // held
    part = lax.dot_general(mixed_ref[...], proj_ref[...], TN, preferred_element_type=f32)
    extra = jnp.broadcast_to(dgain_ref[...], (each - rows, features)).astype(bf16)
    for at in range(held):
        out_ref[at, :rows] = part[at * rows : (at + 1) * rows].astype(bf16)
        out_ref[at, rows:] = extra


def output_weight_call(mixed, proj, dgain, parts):
    rows, width = mixed.shape
    features = proj.shape[1]
    each = width // parts
    lanes = max(each, width // 2)
    held = lanes // each
    return pl.pallas_call(
        output_weight_kernel,
        grid=(parts // held,),
        in_specs=[
            pl.BlockSpec((rows, lanes), lambda s: (0, s)),
            whole((rows, features)),
            whole((1, features)),
        ],
        out_specs=pl.BlockSpec((held, each + 16, features), lambda s: (s, 0, 0)),
        out_shape=jax.ShapeDtypeStruct((parts, each + 16, features), bf16),
        compiler_params=params(32, "arbitrary"),
        cost_estimate=cost(2 * rows * width * features, 4e6),
        name="output_weight_part",
    )(mixed, proj, dgain)


def dense_out_kernel(at_ref, *refs):
    held, refs = refs[:-13], refs[-13:]
    wq_ref, wk_ref, wv_ref, gain_ref, dq_ref, dk_ref, dv_ref, dg_ref, wo_ref, dg2_ref = refs[:10]
    own_ref, other_ref = refs[10:12]
    parts = len(held) // 4
    stream, step = pl.program_id(0), pl.program_id(1)
    chips, _, width = own_ref.shape
    rows = dq_ref.shape[0]
    pair = width // 2
    chip, core = at_ref[2], at_ref[3]
    for which in range(2):
        for rel in range(parts):

            @pl.when((stream == which) & (jnp.bitwise_xor(step, at_ref[which]) == rel))
            def _():
                own_ref[...] = held[which * parts + rel][...]
                other_ref[...] = held[(2 + which) * parts + rel][...]

    total = jnp.zeros((rows, pair), f32)
    for k in range(chips):
        source = lax.rem(chip - k + chips, chips)
        a = jnp.where(core == 0, own_ref[k], other_ref[k]).astype(f32)
        b = jnp.where(core == 0, other_ref[k], own_ref[k]).astype(f32)
        q = jnp.concatenate([a[:rows, :pair], b[:rows, :pair]], axis=1)
        cols = pl.ds(pl.multiple_of(source * width, width), width)
        dq_ref[:, cols] = q
        made = q * wq_ref[:, cols].astype(f32)
        total += made[:, :pair] + made[:, pair:]
        a_kv, b_kv = a[:rows, pair:], b[:rows, pair:]
        lane = lax.broadcasted_iota(jnp.int32, a_kv.shape, 1)
        key = jnp.where(lane < HEAD_DIM, a_kv, pltpu.roll(b_kv, HEAD_DIM, 1))
        val = jnp.where(lane < HEAD_DIM, pltpu.roll(a_kv, HEAD_DIM, 1), b_kv)
        cols = pl.ds(pl.multiple_of(source * pair, pair), pair)
        dk_ref[:, cols] = key
        dv_ref[:, cols] = val
        total += key * wk_ref[:, cols].astype(f32) + val * wv_ref[:, cols].astype(f32)
        wo_ref[2 * source, 0] = a[rows : rows + wo_ref.shape[2]]
        wo_ref[2 * source + 1, 0] = b[rows : rows + wo_ref.shape[2]]
        if k == 0:
            dg2_ref[...] = a[rows + wo_ref.shape[2] :][:1]
    dg_ref[...] = jnp.sum(jnp.transpose(total), axis=0, keepdims=True) / gain_ref[...]


def dense_out_call(at, own, other, wq, wk, wv, gain, wo_shape):
    held = [*own[0], *own[1], *other[0], *other[1]]
    streams, parts = 2, len(own[0])
    chips, depth, width = held[0].shape
    features = wq.shape[0]
    groups = 2 * chips
    rows = features // (streams * parts)
    block_cols = wo_shape[1] // width
    per_block = streams * parts // block_cols
    wo_rows = wo_shape[0] // groups // per_block
    by_rows = lambda w: pl.BlockSpec((rows, w.shape[1]), lambda s, r, at: (s * parts + r, 0))
    gain_spec = pl.BlockSpec((1, rows), lambda s, r, at: (0, s * parts + r))
    outs = pl.pallas_call(
        dense_out_kernel,
        grid_spec=pltpu.PrefetchScalarGridSpec(
            num_scalar_prefetch=1,
            grid=(streams, parts),
            in_specs=[pl.BlockSpec(memory_space=pltpu.VMEM)] * len(held)
            + [by_rows(wq), by_rows(wk), by_rows(wv), gain_spec],
            out_specs=[
                by_rows(wq),
                by_rows(wk),
                by_rows(wv),
                gain_spec,
                pl.BlockSpec(
                    (groups, 1, wo_rows, width),
                    lambda s, r, at: (
                        0,
                        lax.rem(s * parts + r, per_block),
                        0,
                        lax.div(s * parts + r, per_block),
                    ),
                ),
                pl.BlockSpec((1, width), lambda s, r, at: (0, lax.div(s * parts + r, per_block))),
            ],
            scratch_shapes=[pltpu.VMEM((chips, depth, width), bf16)] * 2
            + [pltpu.VMEM((8, 128), f32)],
        ),
        out_shape=[
            jax.ShapeDtypeStruct(wq.shape, f32),
            jax.ShapeDtypeStruct(wk.shape, f32),
            jax.ShapeDtypeStruct(wv.shape, f32),
            jax.ShapeDtypeStruct((1, features), f32),
            jax.ShapeDtypeStruct((groups, per_block, wo_rows, wo_shape[1]), f32),
            jax.ShapeDtypeStruct((1, wo_shape[1]), f32),
        ],
        compiler_params=params(28, "arbitrary", "arbitrary"),
        cost_estimate=cost(2 * wq.size, 2.4e7),
        name="dense_weights_out",
    )(at, *held, wq, wk, wv, gain)
    return (*outs[:4], outs[4].reshape(wo_shape), outs[5])


def weights_out_kernel(wide_ref, wq_ref, wk_ref, wv_ref, gain_ref, dq_ref, dk_ref, dv_ref, dg_ref):
    groups, rows, width = wide_ref.shape
    pair = width // 2
    total = jnp.zeros((rows, pair), f32)
    for g in range(groups):
        part = wide_ref[g, :, :pair].astype(f32)
        at = slice(g * pair, (g + 1) * pair)
        dq_ref[:, at] = part
        total += part * wq_ref[:, at].astype(f32)
    for g in range(groups // 2):
        a = wide_ref[2 * g, :, pair:].astype(f32)
        b = wide_ref[2 * g + 1, :, pair:].astype(f32)
        lane = lax.broadcasted_iota(jnp.int32, a.shape, 1)
        at = slice(g * pair, (g + 1) * pair)
        k = jnp.where(lane < HEAD_DIM, a, pltpu.roll(b, HEAD_DIM, 1))
        v = jnp.where(lane < HEAD_DIM, pltpu.roll(a, HEAD_DIM, 1), b)
        dk_ref[:, at] = k
        dv_ref[:, at] = v
        total += k * wk_ref[:, at].astype(f32) + v * wv_ref[:, at].astype(f32)
    dg_ref[...] = jnp.sum(jnp.transpose(total), axis=0, keepdims=True) / gain_ref[...]


def weights_out_call(wide, wq, wk, wv, gain):
    chunks, groups, rows, width = wide.shape
    features = chunks * rows
    by_rows = lambda w: pl.BlockSpec((rows, w.shape[1]), lambda c: (c, 0))
    return pl.pallas_call(
        weights_out_kernel,
        grid=(chunks,),
        in_specs=[
            pl.BlockSpec((None, groups, rows, width), lambda c: (c, 0, 0, 0)),
            by_rows(wq),
            by_rows(wk),
            by_rows(wv),
            pl.BlockSpec((1, rows), lambda c: (0, c)),
        ],
        out_specs=[
            by_rows(wq),
            by_rows(wk),
            by_rows(wv),
            pl.BlockSpec((1, rows), lambda c: (0, c)),
        ],
        out_shape=[
            jax.ShapeDtypeStruct(wq.shape, f32),
            jax.ShapeDtypeStruct(wk.shape, f32),
            jax.ShapeDtypeStruct(wv.shape, f32),
            jax.ShapeDtypeStruct((1, features), f32),
        ],
        compiler_params=params(32, "arbitrary"),
        cost_estimate=cost(2 * wq.size, 1.6e7),
        name="attention_weights_out",
    )(wide, wq, wk, wv, gain)


def last_kernel(d_ref, wq_ref, wk_ref, wv_ref, x_ref, gain_ref, dmid_ref, out_ref):
    groups, rows, width = d_ref.shape
    pair = width // 2
    dq = jnp.concatenate([d_ref[g, :, :pair] for g in range(groups)], axis=1)
    grad = dot_nt(dq, wq_ref[...])
    keys, vals = [], []
    for at in range(groups // 2):
        a = d_ref[2 * at, :, pair:].astype(f32)
        b = d_ref[2 * at + 1, :, pair:].astype(f32)
        lane = lax.broadcasted_iota(jnp.int32, a.shape, 1)
        keys.append(jnp.where(lane < HEAD_DIM, a, pltpu.roll(b, HEAD_DIM, 1)).astype(bf16))
        vals.append(jnp.where(lane < HEAD_DIM, pltpu.roll(a, HEAD_DIM, 1), b).astype(bf16))
    grad = grad + dot_nt(jnp.concatenate(keys, axis=1), wk_ref[...])
    grad = grad + dot_nt(jnp.concatenate(vals, axis=1), wv_ref[...])
    x = x_ref[...].astype(f32)
    scale = lax.rsqrt(jnp.mean(x * x, axis=-1, keepdims=True) + norm_eps)
    unit = x * scale
    w = gain_ref[...] * grad
    out_ref[...] = dmid_ref[...] + scale * (w - unit * jnp.mean(w * unit, axis=-1, keepdims=True))


def last_call(d, wq, wk, wv, x, gain, dmid):
    rows, features = x.shape
    return pl.pallas_call(
        last_kernel,
        out_shape=jax.ShapeDtypeStruct((rows, features), f32),
        compiler_params=params(40),
        cost_estimate=cost(4 * rows * features * features, 8e6),
        name="input_gradient",
    )(d, wq, wk, wv, x, gain, dmid)


def swap(values, axis, bit):
    return lax.ppermute(values, axis, [(i, i ^ bit) for i in range(lax.axis_size(axis))])


def half_sum(values, axis, bit):
    half = values.shape[0] // 2
    upper = ((lax.axis_index(axis) & bit) > 0).astype(jnp.int32)
    came = swap(lax.dynamic_slice_in_dim(values, (1 - upper) * half, half), axis, bit)
    mine = lax.dynamic_slice_in_dim(values, upper * half, half)
    return (mine.astype(f32) + came.astype(f32)).astype(bf16)


def relative_sum(kept, sent, axis, bits):
    while True:
        kept = (kept.astype(f32) + swap(sent, axis, bits[0]).astype(f32)).astype(bf16)
        bits = bits[1:]
        if not bits:
            return kept
        half = kept.shape[0] // 2
        kept, sent = kept[:half], kept[half:]


def join_parts(stream, axis, bits):
    shape = stream.shape
    for bit in bits[::-1]:
        stream = jnp.stack([stream, swap(stream, axis, bit)])
    return stream.reshape(-1, *shape)


def body(
    layer_input,
    first_gain,
    query_weight,
    key_weight,
    value_weight,
    output_weight,
    second_gain,
    gate_weight,
    up_weight,
    down_weight,
    expert_ids,
    gate_values,
    positions,
    cotangent,
):
    micro, _, per_device, features = layer_input.shape
    devices = lax.axis_size("seq")
    replicas = lax.axis_size("dp")
    seq_place = lax.axis_index("seq")
    rows = micro * per_device
    local_experts = gate_weight.shape[0]
    groups = key_weight.shape[1] // HEAD_DIM
    pair = query_weight.shape[1] // groups
    copies = devices // groups

    dp_bits = [1 << i for i in range(replicas.bit_length() - 1)]

    def spread(blocks):
        if copies > 1:
            blocks = jnp.repeat(blocks, copies, axis=0)
        return lax.all_to_all(blocks, "seq", 0, 0, tiled=True)

    def unspread(blocks):
        return lax.all_to_all(blocks, "seq", 0, 0, tiled=True)[::copies]

    x = layer_input.reshape(rows, features)
    cot = cotangent.reshape(rows, features)
    gain_one = first_gain.reshape(1, features)
    gain_two = second_gain.reshape(1, features)
    pos_all = lax.all_to_all(
        jnp.broadcast_to(positions.reshape(1, rows), (devices, rows)), "seq", 0, 0, tiled=True
    )
    x_all = lax.all_gather(x, "seq", axis=0)
    cos_all, sin_all = rope_tables(pos_all.reshape(-1), pair)
    mine = seq_place * local_experts + jnp.arange(local_experts, dtype=jnp.int32)
    ids = expert_ids[:, 0]
    gates = gate_values[:, 0].astype(f32)
    routed = jnp.sum(
        jnp.where(ids[..., None] == mine, gates[..., None], 0.0), axis=2
    )
    routed = routed.reshape(micro, devices, per_device, local_experts)
    routed = jnp.transpose(routed, (1, 0, 2, 3)).reshape(devices * rows, local_experts)
    group = seq_place // copies
    w_own = jnp.concatenate(
        [
            lax.dynamic_slice_in_dim(query_weight, group * pair, pair, axis=1),
            lax.dynamic_slice_in_dim(key_weight, group * HEAD_DIM, HEAD_DIM, axis=1),
            lax.dynamic_slice_in_dim(value_weight, group * HEAD_DIM, HEAD_DIM, axis=1),
        ],
        axis=1,
    )
    cot_pair = jnp.stack([cot, swap(cot, "seq", 1)])
    cos_all, sin_all, routed, w_own, cot_pair = lax.optimization_barrier(
        (cos_all, sin_all, routed, w_own, cot_pair)
    )
    x_all, cot_then, cos_all, sin_all, routed, w_own, cot_pair = lax.optimization_barrier(
        (x_all, cot, cos_all, sin_all, routed, w_own, cot_pair)
    )
    cot_all = lax.all_gather(cot_then, "seq", axis=0)
    cots = (cot_pair, cot_all)

    qkv, first_all = qkv_call(x_all, gain_one, cos_all, sin_all, w_own)
    qkv = qkv.reshape(devices, micro, per_device, 2 * pair)
    mix, log_total = attend_call(qkv)
    mix = unspread(mix.reshape(devices, rows, pair))
    mixed, middle, second_low = post_call(mix, output_weight, x, gain_two)

    chips = devices // 2
    chip, core = seq_place // 2, seq_place % 2
    onward = [(i, (i + 2) % devices) for i in range(devices)]
    dp_place = lax.axis_index("dp")
    first_bit = dp_place & 1
    last_bit = dp_place >> (len(dp_bits) - 1)
    held, kept, running, places = second_low, (), None, []
    for hop in range(chips):
        following = lax.ppermute(held, "seq", onward) if hop < chips - 1 else None
        other = swap(held, "seq", 1)
        source = 2 * ((chip - hop) % chips)
        near_cot = [jnp.int32(0), jnp.int32(1)] if hop == 0 else [source + core, source + 1 - core]
        place = jnp.stack(
            [source + core, source + 1 - core, 1 - first_bit, 1 - last_bit, *near_cot]
        )
        place = place.astype(jnp.int32)
        places.append(place[:2])
        dx, *kept = expert_call(
            hop, place, held, other, cots[hop > 0], routed, gate_weight, up_weight, down_weight, kept
        )
        if following is not None:
            following, dx = lax.optimization_barrier((following, dx))
        part = dx[0].astype(f32) + swap(dx[1], "seq", 1).astype(f32)
        if hop == 0:
            own_part = part
        else:
            if running is not None:
                part = part + running.astype(f32)
            part = part.astype(bf16)
            if following is not None:
                part, following = lax.optimization_barrier((part, following))
            else:
                part, kept = lax.optimization_barrier((part, kept))
            running = lax.ppermute(part, "seq", onward)
        held = following
    second_grad = (own_part + running.astype(f32)).astype(bf16)
    tokens, hidden_a, hidden_b, gate_low, up_low, slot_a, slot_b = kept

    def weight_parts(at, tokens, hidden_a, hidden_b, gate_low, up_low, slot_a, slot_b):
        pairs = (
            (tokens, gate_low[at]),
            (tokens, up_low[at]),
            (hidden_a[at], slot_a[at]),
            (hidden_b[at], slot_b[at]),
        )
        return [
            lax.dot_general(a, b, TN, preferred_element_type=f32).astype(bf16) for a, b in pairs
        ]

    leaving = weight_parts(0, *kept)
    part_bits = (dp_bits[0], dp_bits[-1], dp_bits[0], dp_bits[-1])
    stream_bits = (dp_bits, dp_bits[::-1])
    came = [swap(values, "dp", bit) for values, bit in zip(leaving, part_bits)]
    leaving, second_grad = lax.optimization_barrier((leaving, second_grad))

    mg_send, proj, middle_grad, gain_two_part = turn_call(
        second_grad, middle, gain_two, cot, output_weight, groups
    )
    mg = spread(mg_send)
    kept, _ = lax.optimization_barrier((kept, mg_send))
    mixed, proj, came[2:] = lax.optimization_barrier((mixed, proj, came[2:]))
    dense = output_weight_call(mixed, proj, gain_two_part, devices)
    dense_own = dense
    staying = weight_parts(1, *kept)
    turned = sum(((dp_place >> i) & 1) << (len(dp_bits) - 1 - i) for i in range(len(dp_bits)))
    part_at = jnp.stack([turned, dp_place]).astype(jnp.int32)
    low_at = jnp.bitwise_and(part_at, replicas // 2 - 1)
    keep_a, send_a, keep_b, send_b = part_sum_call(low_at, replicas // 2, came, staying)
    mg, keep_a, send_a, keep_b, send_b = lax.optimization_barrier(
        (mg, keep_a, send_a, keep_b, send_b)
    )
    streams = [
        relative_sum(keep_a, send_a, "dp", stream_bits[0][1:]),
        relative_sum(keep_b, send_b, "dp", stream_bits[1][1:]),
    ]
    dense = dense_own
    dense = lax.psum_scatter(dense, "seq", scatter_dimension=0)
    table_shape = (devices, micro, per_device, pair)
    dqkv = attend_back_call(
        qkv,
        mg.reshape(devices, micro, per_device, pair),
        log_total,
        cos_all.reshape(table_shape),
        sin_all.reshape(table_shape),
    )
    dqkv, streams = lax.optimization_barrier((dqkv, streams))
    near = [
        [v[0], swap(v[0], "dp", bits[-1])] for v, bits in zip(streams, stream_bits)
    ]
    back = unspread(dqkv.reshape(devices, rows, 2 * pair))
    d_all = dqkv.reshape(devices * rows, 2 * pair)
    first_tokens = first_all.reshape(devices * rows, features)
    part = lax.dot_general(first_tokens, d_all, TN, preferred_element_type=f32)
    dense = dense.reshape(dense.shape[-2], features)
    each = output_weight.shape[0] // devices
    if copies == 1:
        width = 2 * pair
        kept_pieces, sent_pieces = joint_call(part_at, part, dense, replicas)
        first = [
            kept_pieces[at].astype(f32) + swap(sent_pieces[at], "dp", bits[0]).astype(f32)
            for at, bits in enumerate(stream_bits)
        ]
        kept, sent_pieces = lax.optimization_barrier((kept, sent_pieces))
        moe_place = jnp.concatenate(places + [(1 - first_bit).astype(jnp.int32).reshape(1)])
        moe_all = moe_call(moe_place, kept[1], routed, down_weight, devices)
        far = [swap(v[0], "dp", bits[-2]) for v, bits in zip(streams, stream_bits)]
        first, near, moe_all = lax.optimization_barrier(
            ([v.astype(bf16) for v in first], near, moe_all)
        )
        own = [
            relative_sum(v[: replicas // 4], v[replicas // 4 :], "dp", bits[1:])
            for v, bits in zip(first, stream_bits)
        ]
        own = jnp.concatenate(own, axis=0)
        own, far = lax.optimization_barrier((own, far))
        backward = [(i, (i - 2) % devices) for i in range(devices)]
        round_ring = {0: own}
        for k in range(1, chips // 2 + 1):
            round_ring[k] = lax.ppermute(round_ring[k - 1], "seq", onward)
            if chips - k > k:
                round_ring[chips - k] = lax.ppermute(
                    round_ring[(chips - k + 1) % chips], "seq", backward
                )
        held = jnp.stack([round_ring[k] for k in range(chips)])
        passed = [swap(v[1], "dp", bits[-2]) for v, bits in zip(near, stream_bits)]
        held, moe_all, back, passed = lax.optimization_barrier((held, moe_all, back, passed))
        moe = lax.psum_scatter(moe_all, "seq", scatter_dimension=0)
        layer_output = (middle + residual_scale * moe.astype(f32)).astype(bf16)
    else:
        far = [swap(v[0], "dp", bits[-2]) for v, bits in zip(streams, stream_bits)]
        passed = [swap(v[1], "dp", bits[-2]) for v, bits in zip(near, stream_bits)]
    expert_pieces = []
    for (here, first), second, third, bits in zip(near, far, passed, stream_bits):
        pieces = [here, first, second, third]
        for bit in bits[:-2][::-1]:
            pieces = pieces + [swap(p, "dp", bit) for p in pieces]
        expert_pieces.append(pieces)
    input_grad = last_call(
        back, query_weight, key_weight, value_weight, x, gain_one, middle_grad
    )
    if copies == 1:
        gate_sum, up_sum, down_sum = expert_out_call(
            part_at, *expert_pieces, gate_weight.shape, down_weight.shape
        )
        full = [[held[:, at], swap(held[:, at], "dp", b[-1])] for at, b in enumerate(stream_bits)]
        beside = [swap(v[0], "dp", bits[-2]) for v, bits in zip(full, stream_bits)]
        full, gate_sum, up_sum, down_sum, input_grad = lax.optimization_barrier(
            (full, gate_sum, up_sum, down_sum, input_grad)
        )
        for at, bits in enumerate(stream_bits):
            full[at] += [beside[at], swap(full[at][1], "dp", bits[-2])]
            for bit in bits[:-2][::-1]:
                full[at] += [swap(p, "dp", bit) for p in full[at]]
        other = [[swap(p, "seq", 1) for p in pieces] for pieces in full]
        where_at = jnp.stack([turned, dp_place, chip, core]).astype(jnp.int32)
        (
            query_weight_grad,
            key_weight_grad,
            value_weight_grad,
            first_gain_grad,
            output_weight_grad,
            second_gain_grad,
        ) = dense_out_call(
            where_at, full, other, query_weight, key_weight, value_weight, gain_one, output_weight.shape
        )
    else:
        gate_sum, up_sum, down_sum = expert_out_call(
            part_at, *expert_pieces, gate_weight.shape, down_weight.shape
        )
        for bit in dp_bits:
            dense = (dense.astype(f32) + swap(dense, "dp", bit).astype(f32)).astype(bf16)
        dense = lax.all_gather(dense, "seq", axis=0).astype(f32)
        output_weight_grad = dense[:, :each].reshape(output_weight.shape)
        moe_place = jnp.concatenate(places + [(1 - first_bit).astype(jnp.int32).reshape(1)])
        moe_all = moe_call(moe_place, kept[1], routed, down_weight, devices)
        moe = lax.psum_scatter(moe_all, "seq", scatter_dimension=0)
        layer_output = (middle + residual_scale * moe.astype(f32)).astype(bf16)
        second_gain_grad = dense[0, each]
        part = part.astype(bf16)
        for bit in dp_bits[::-1]:
            part = half_sum(part, "dp", bit)
        wide = lax.all_gather(part, ("dp", "seq"), axis=0)
        wide = wide.reshape(replicas, devices, features // replicas, 2 * pair)[:, ::copies]
        query_weight_grad, key_weight_grad, value_weight_grad, first_gain_grad = weights_out_call(
            wide, query_weight, key_weight, value_weight, gain_one
        )
    second_gain_grad = second_gain_grad.reshape(features)
    return (
        layer_output.reshape(layer_input.shape),
        input_grad.reshape(layer_input.shape),
        first_gain_grad.reshape(features),
        query_weight_grad,
        key_weight_grad,
        value_weight_grad,
        output_weight_grad,
        second_gain_grad,
        gate_sum,
        up_sum,
        down_sum,
    )


def solution(mesh):
    return jax.shard_map(
        body,
        mesh=mesh,
        in_specs=(
            P(None, "dp", "seq", None),
            P(),
            P(),
            P(),
            P(),
            P(),
            P(),
            P("seq", None, None),
            P("seq", None, None),
            P("seq", None, None),
            P(None, "dp", None, None),
            P(None, "dp", None, None),
            P(None, "dp", "seq"),
            P(None, "dp", "seq", None),
        ),
        out_specs=(
            P(None, "dp", "seq", None),
            P(None, "dp", "seq", None),
            P(),
            P(),
            P(),
            P(),
            P(),
            P(),
            P("seq", None, None),
            P("seq", None, None),
            P("seq", None, None),
        ),
        check_vma=False,
    )
```
